32 devices in a mesh: ctx: 8 (over z, y), fsdp: 4 (over x, core).
Axes of the slice: x: 2, y: 2, z: 4, core: 2. Of those that a mesh axis runs over, the one named last changes fastest.
Arguments:
- hidden_in: bfloat16 [8192, 2048], P(('ctx', 'fsdp')), may hold values from -6 to 6
- teacher: bfloat16 [8192, 2048], P(('ctx', 'fsdp')), may hold values from -6 to 6
- blocks: int32 [8192], P(('ctx', 'fsdp')), may hold values from 0 to 15, as said below
- seq_ids: int32 [8192], P(('ctx', 'fsdp')), may hold values from 0 to 3, as said below
- valid_mask: int32 [8192], P(('ctx', 'fsdp')), may hold values from 0 to 1, as said below
- norm1_gain: bfloat16 [2048], P('fsdp'), may hold values from 0.5 to 1.5
- q_down: bfloat16 [2048, 1024], P('fsdp'), may hold values from -0.125 to 0.125
- q_gain: bfloat16 [1024], P('fsdp'), may hold values from 0.5 to 1.5
- q_up: bfloat16 [1024, 4096], P('fsdp'), may hold values from -0.1875 to 0.1875
- kv_weight: bfloat16 [2048, 512], P('fsdp'), may hold values from -0.1875 to 0.1875
- out_proj: bfloat16 [4096, 2048], P('fsdp'), may hold values from -1.5 to 1.5
- norm2_gain: bfloat16 [2048], P('fsdp'), may hold values from 0.5 to 1.5
- w_gate: bfloat16 [2048, 5632], P('fsdp'), may hold values from -0.125 to 0.125
- w_up: bfloat16 [2048, 5632], P('fsdp'), may hold values from -0.125 to 0.125
- w_down: bfloat16 [5632, 2048], P('fsdp'), may hold values from -0.078125 to 0.078125
Outputs:
- layer_out: bfloat16 [8192, 2048], P(('ctx', 'fsdp'))
- loss_value: float32 [], replicated
- input_grad: float32 [8192, 2048], P(('ctx', 'fsdp'))
- norm1_gain_grad: float32 [2048], P(('ctx', 'fsdp'))
- q_down_grad: float32 [2048, 1024], P(('ctx', 'fsdp'))
- q_gain_grad: float32 [1024], P(('ctx', 'fsdp'))
- q_up_grad: float32 [1024, 4096], P(('ctx', 'fsdp'))
- kv_weight_grad: float32 [2048, 512], P(('ctx', 'fsdp'))
- out_proj_grad: float32 [4096, 2048], P(('ctx', 'fsdp'))
- norm2_gain_grad: float32 [2048], P(('ctx', 'fsdp'))
- w_gate_grad: float32 [2048, 5632], P(('ctx', 'fsdp'))
- w_up_grad: float32 [2048, 5632], P(('ctx', 'fsdp'))
- w_down_grad: float32 [5632, 2048], P(('ctx', 'fsdp'))
The draws below stay inside these ranges and needn't reach their ends.
Inputs may be any that keep to these rules, and one draw needn't show every extreme that they name: Each device's rows form whole half-blocks of 128 tokens with one half-block number, all of one sequence, in mirrored pairs j and 15 - j; each sequence holds half-blocks 0 to 15 once each, all on devices with the same fsdp index. `seq_ids`: all tokens of one device have the same sequence. `valid_mask`: each device's first token is 1.
All inputs are finite; a program needn't handle non-finite values.
Results may differ from the reference program's by a relative error of at most 0.015.
The reference program's roundings to bfloat16 on the way count: a program that leaves them out, or rounds other values in their place, can miss the bound.
Values may be sent and summed in bfloat16 or wider, within the bound.
A program may use at most 448 MiB of HBM per device.

```python
import jax
import jax.numpy as jnp
from jax import lax

D = 2048
QR = 1024
HEADS = 16
HD = 256
FF = 5632
PAIRS_DEV = 1
PIECE = 128
SEQ_BLOCKS = 8
TOK_DEV = 256
TOKENS = 8192
N_CTX = 8
N_FSDP = 4


def slot_order(one_key):
    middle = jax.random.permutation(one_key, N_CTX - 2).astype(jnp.int32) + 1
    order = jnp.concatenate([jnp.array([0, N_CTX - 1], dtype=jnp.int32), middle])
    return jnp.argsort(order, stable=True).astype(jnp.int32)


def layout_tables(key):
    base_key = jax.random.fold_in(key, 11)
    seq_pieces = 2 * SEQ_BLOCKS
    devs_per_seq = seq_pieces // (2 * PAIRS_DEV)
    seqs_group = N_CTX // devs_per_seq
    group_keys = jax.random.split(base_key, N_FSDP)
    slot_table = jax.vmap(slot_order)(group_keys)
    slot_table = jnp.transpose(slot_table).astype(jnp.int32)
    seq_local = slot_table // devs_per_seq
    member_idx = slot_table % devs_per_seq
    group_index = jnp.arange(N_FSDP, dtype=jnp.int32)[None, :]
    seq_drawn = group_index * seqs_group + seq_local
    label_table = jax.random.permutation(jax.random.fold_in(key, 17), N_FSDP * seqs_group).astype(jnp.int32)
    seq_global = label_table[seq_drawn]
    pair_index = member_idx[:, :, None] * PAIRS_DEV + jnp.arange(PAIRS_DEV, dtype=jnp.int32)[None, None, :]
    piece_pairs = jnp.stack([pair_index, seq_pieces - 1 - pair_index], axis=-1).reshape(N_CTX, N_FSDP, 2 * PAIRS_DEV)
    token_pieces = jnp.repeat(piece_pairs, PIECE, axis=2).reshape(-1)
    token_seqs = jnp.broadcast_to(seq_global[:, :, None], (N_CTX, N_FSDP, TOK_DEV)).reshape(-1)
    return (token_pieces.astype(jnp.int32), token_seqs.astype(jnp.int32))


def draw_blocks(key, part):
    return layout_tables(key)[0]


def draw_seq_ids(key, part):
    return layout_tables(key)[1]


def draw_valid_mask(key, part):
    row_index = jnp.arange(TOKENS, dtype=jnp.int32)
    dev_index = row_index // TOK_DEV
    device_total = N_CTX * N_FSDP
    chance = 250 + 500 * dev_index // max(device_total - 1, 1)
    coins = jax.random.randint(jax.random.fold_in(key, 29), (TOKENS,), 0, 1000)
    picked = (coins < chance) | (row_index % TOK_DEV == 0)
    return picked.astype(jnp.int32)


def steps_of(own_key, extent, cuts, low, high):
    def one(dim, blocks):
        draws = jax.random.uniform(jax.random.fold_in(jax.random.fold_in(own_key, 6), dim), (blocks,), jnp.float32, low / len(cuts), high / len(cuts))
        return jnp.repeat(jnp.exp(draws), extent[dim] // blocks).reshape((-1,) + (1,) * (len(extent) - dim - 1))

    loudness = one(*cuts[0])
    for cut in cuts[1:]:
        loudness = loudness * one(*cut)
    return loudness


def centred(key, shape, scale, bound, shards=(), kind=jnp.bfloat16):
    entries = jax.random.normal(key, shape, jnp.float32) * scale
    if len(shards) > 0:
        entries = steps_of(key, shape, shards, -0.22, 0.18) * entries
    return jnp.clip(entries, min=-bound, max=bound).astype(kind)


def setup_inputs(seed: int = 0) -> dict:
    arg_keys = jax.random.split(jax.random.key(seed), 16)
    hidden_in = centred(arg_keys[0], (TOKENS, D), 1.0, 6.0, ((0, 32),))
    teacher = centred(arg_keys[1], (TOKENS, D), 1.0, 6.0, ((0, 32),))
    blocks = draw_blocks(jax.random.fold_in(arg_keys[15], 71), 0)
    seq_ids = draw_seq_ids(jax.random.fold_in(arg_keys[15], 71), 0)
    valid_mask = draw_valid_mask(jax.random.fold_in(arg_keys[15], 71), 0)
    norm1_gain = jnp.clip(1.0 + 0.1 * jax.random.normal(arg_keys[5], (D,), jnp.float32), 0.5, 1.5).astype(jnp.bfloat16)
    q_down = centred(arg_keys[6], (D, QR), D ** -0.5, 0.125, ((0, 4),))
    q_gain = jnp.clip(1.0 + 0.1 * jax.random.normal(arg_keys[7], (QR,), jnp.float32), 0.5, 1.5).astype(jnp.bfloat16)
    q_up = centred(arg_keys[8], (QR, HEADS * HD), QR ** -0.5, 0.1875, ((0, 4),))
    kv_weight = centred(arg_keys[9], (D, 2 * HD), (D // 2) ** -0.5, 0.1875, ((0, 4),))
    out_proj = centred(arg_keys[10], (HEADS * HD, D), (max(HEADS * HD // 256, 2)) ** -0.5, 1.5, ((0, 4),))
    norm2_gain = jnp.clip(1.0 + 0.1 * jax.random.normal(arg_keys[11], (D,), jnp.float32), 0.5, 1.5).astype(jnp.bfloat16)
    w_gate = centred(arg_keys[12], (D, FF), D ** -0.5, 0.125, ((0, 4),))
    w_up = centred(arg_keys[13], (D, FF), D ** -0.5, 0.125, ((0, 4),))
    w_down = centred(arg_keys[14], (FF, D), FF ** -0.5, 0.078125, ((0, 4),))
    return {"hidden_in": hidden_in, "teacher": teacher, "blocks": blocks, "seq_ids": seq_ids, "valid_mask": valid_mask, "norm1_gain": norm1_gain, "q_down": q_down, "q_gain": q_gain, "q_up": q_up, "kv_weight": kv_weight, "out_proj": out_proj, "norm2_gain": norm2_gain, "w_gate": w_gate, "w_up": w_up, "w_down": w_down}


NORM_EPS = 1e-05

@jax.custom_vjp
def low(v):
    return lax.optimization_barrier(v.astype(jnp.bfloat16)).astype(jnp.float32)

@jax.custom_vjp
def low_back(v):
    return v

def low_keep(v):
    return (low(v), None)

def low_pass(kept, grad):
    return (grad,)

def back_keep(v):
    return (v, None)

def back_low(kept, grad):
    return (low(grad),)
low.defvjp(low_keep, low_pass)
low_back.defvjp(back_keep, back_low)

def rms_apply(values, gain_vec):
    return values * lax.rsqrt(lax.optimization_barrier(jnp.mean(values * values, axis=-1, keepdims=True)) + NORM_EPS) * gain_vec

def rope_apply(values, cosine, sine):
    half_dim = values.shape[-1] // 2
    first_half = values[..., :half_dim]
    second_half = values[..., half_dim:]
    return jnp.concatenate([first_half * cosine - second_half * sine, second_half * cosine + first_half * sine], axis=-1)

def reference(hidden_in, teacher, blocks, seq_ids, valid_mask, norm1_gain, q_down, q_gain, q_up, kv_weight, out_proj, norm2_gain, w_gate, w_up, w_down):
    highest = lax.Precision.HIGHEST
    token_count = hidden_in.shape[0]
    device_count = N_CTX * N_FSDP
    half_dim = HD // 2
    positions = blocks * PIECE + jnp.arange(token_count, dtype=jnp.int32) % PIECE
    freq_table = 10000.0 ** (-(jnp.arange(half_dim, dtype=jnp.float32) * 2.0 / HD))
    angle_table = positions.astype(jnp.float32)[:, None] * freq_table[None, :]
    cosine = jnp.cos(angle_table)
    sine = jnp.sin(angle_table)
    valid_f = valid_mask.astype(jnp.float32)
    count_all = jnp.sum(valid_f)
    teacher_f = teacher.astype(jnp.float32)
    group_of = jnp.arange(device_count, dtype=jnp.int32) % N_FSDP
    score_scale = HD ** (-0.5)

    def regroup(values):
        shaped = values.reshape((N_CTX, N_FSDP, TOK_DEV) + values.shape[1:])
        return jnp.swapaxes(shaped, 0, 1).reshape((N_FSDP, N_CTX * TOK_DEV) + values.shape[1:])
    block_groups = regroup(blocks // 2)
    seq_groups = regroup(seq_ids)

    def forward(hidden_f, gain_one, w_qdown, gain_q, w_qup, w_kv, w_out, gain_two, w_gatef, w_upf, w_downf):
        normed = low(rms_apply(hidden_f, gain_one))
        q_low = low_back(jnp.dot(normed, w_qdown, precision=highest))
        q_normed = low(rms_apply(q_low, gain_q))
        q_lin = low_back(jnp.dot(q_normed, w_qup, precision=highest)).reshape(token_count, HEADS, HD)
        q_rot = low(rope_apply(q_lin, cosine[:, None, :], sine[:, None, :]))
        kv_lin = low_back(jnp.dot(normed, w_kv, precision=highest))
        key_rot = low(rope_apply(kv_lin[:, :HD], cosine, sine))
        val_rows = low(kv_lin[:, HD:])
        key_groups = regroup(key_rot)
        val_groups = regroup(val_rows)

        @jax.checkpoint
        def attend_slab(item):
            q_slab, group_idx, q_blocks, q_seqs = item
            keys_here = key_groups[group_idx]
            vals_here = val_groups[group_idx]
            allowed = (q_seqs[:, None] == seq_groups[group_idx][None, :]) & (block_groups[group_idx][None, :] <= (q_blocks // 2)[:, None])
            scores = low_back(jnp.einsum('rhd,kd->hrk', q_slab, keys_here, precision=highest) * score_scale)
            scores = jnp.where(allowed[None], scores, -1e+30)
            log_total = jax.nn.logsumexp(scores, axis=2, keepdims=True)
            probs = low(jnp.exp(scores - log_total))
            return jnp.einsum('hrk,kd->rhd', probs, vals_here, precision=highest)
        slabs = lax.map(attend_slab, (q_rot.reshape(device_count, TOK_DEV, HEADS, HD), group_of, blocks.reshape(device_count, TOK_DEV), seq_ids.reshape(device_count, TOK_DEV)))
        attn_heads = low(low_back(slabs.reshape(token_count, HEADS * HD)))
        resid = hidden_f + low_back(jnp.dot(attn_heads, w_out, precision=highest))
        normed_two = low(rms_apply(resid, gain_two))
        gate_lin = low_back(jnp.dot(normed_two, w_gatef, precision=highest))
        up_lin = low_back(jnp.dot(normed_two, w_upf, precision=highest))
        hidden_act = low(jax.nn.silu(gate_lin) * up_lin)
        result = resid + low_back(jnp.dot(hidden_act, w_downf, precision=highest))
        diff = result - teacher_f
        loss_now = jnp.sum(valid_f * lax.optimization_barrier(jnp.sum(diff * diff, axis=1))) / (D * count_all)
        return (loss_now * (token_count * D / 2.0), (result, loss_now))
    inputs_f = (hidden_in.astype(jnp.float32), norm1_gain.astype(jnp.float32), q_down.astype(jnp.float32), q_gain.astype(jnp.float32), q_up.astype(jnp.float32), kv_weight.astype(jnp.float32), out_proj.astype(jnp.float32), norm2_gain.astype(jnp.float32), w_gate.astype(jnp.float32), w_up.astype(jnp.float32), w_down.astype(jnp.float32))
    scaled_loss, vjp_fn, aux_pair = jax.vjp(forward, *inputs_f, has_aux=True)
    grads = vjp_fn(jnp.ones((), jnp.float32))
    result, loss_now = aux_pair
    return (result.astype(jnp.bfloat16), loss_now, grads[0], grads[1], grads[2], grads[3], grads[4], grads[5], grads[6], grads[7], grads[8], grads[9], grads[10])
```

```python
import jax
import jax.numpy as jnp
from jax import lax
from jax.sharding import PartitionSpec as P

PIECE = 128
SEQ_BLOCKS = 8
NORM_EPS = 1e-05
F32 = jnp.float32
BF16 = jnp.bfloat16


def rms_scale(values):
    return lax.rsqrt(jnp.mean(values * values, axis=-1, keepdims=True) + NORM_EPS)


def rms_back(values, scale, gain, grad):
    grad_gain = jnp.sum(grad * values * scale, axis=0)
    ge = gain * grad
    inner = jnp.mean(ge * values, axis=-1, keepdims=True)
    return scale * ge - values * (scale * scale * scale) * inner, grad_gain


def rope_apply(values, cosine, sine):
    half_dim = values.shape[-1] // 2
    one = values[..., :half_dim]
    two = values[..., half_dim:]
    return jnp.concatenate([one * cosine - two * sine, two * cosine + one * sine], axis=-1)


def rope_back(grads, cosine, sine):
    half_dim = grads.shape[-1] // 2
    one = grads[..., :half_dim]
    two = grads[..., half_dim:]
    return jnp.concatenate([one * cosine + two * sine, two * cosine - one * sine], axis=-1)


def dot(a, b):
    return jnp.dot(a, b, preferred_element_type=F32)


def dot_t(a, b):
    return lax.dot_general(a, b, (((1,), (1,)), ((), ())), preferred_element_type=F32)


def dot_rows(a, b):
    return lax.dot_general(a, b, (((0,), (0,)), ((), ())), preferred_element_type=F32)


def body(
    hidden_in,
    teacher,
    blocks,
    seq_ids,
    valid_mask,
    norm1_gain,
    q_down,
    q_gain,
    q_up,
    kv_weight,
    out_proj,
    norm2_gain,
    w_gate,
    w_up,
    w_down,
):
    row_count, model_width = hidden_in.shape
    head_size = kv_weight.shape[1] // 2
    heads_width = q_up.shape[1]
    head_count = heads_width // head_size
    half_dim = head_size // 2
    n_ctx = lax.axis_size("ctx")
    n_f = lax.axis_size("fsdp")
    n_z = n_ctx // 2
    token_total = row_count * n_ctx * n_f
    seq_pieces = 2 * SEQ_BLOCKS
    c_idx = lax.axis_index("ctx")
    f_idx = lax.axis_index("fsdp")
    y_idx = c_idx % 2
    z_idx = c_idx // 2
    x_idx = f_idx // 2
    k_idx = f_idx % 2

    def by_f(values, mask):
        return lax.ppermute(values, "fsdp", [(i, i ^ mask) for i in range(n_f)])

    def by_c(values, mask):
        return lax.ppermute(values, "ctx", [(i, i ^ mask) for i in range(n_ctx)])

    def all_sum(values):
        step = 1
        while step < n_f:
            values = values + by_f(values, step)
            step *= 2
        step = 1
        while step < n_ctx:
            values = values + by_c(values, step)
            step *= 2
        return values

    def cut(values, start, size, axis):
        return lax.dynamic_slice_in_dim(values, start, size, axis)

    def fetch_rows(shard):
        rows = shard.shape[0]
        half = rows // 2
        core = by_f(shard, 1)
        far = by_f(cut(shard, y_idx * half, half, 0), 2)
        far_y = by_c(far, 1)
        far_core = by_f(far, 1)
        far_y_core = by_f(far_y, 1)
        mine, other = y_idx * half, (1 - y_idx) * half
        return [
            (shard, f_idx * rows),
            (core, (f_idx ^ 1) * rows),
            (far, (f_idx ^ 2) * rows + mine),
            (far_core, (f_idx ^ 3) * rows + mine),
            (far_y, (f_idx ^ 2) * rows + other),
            (far_y_core, (f_idx ^ 3) * rows + other),
        ]

    def mul_pieces(acts, pieces):
        total = None
        for weight, start in pieces:
            term = dot(cut(acts, start, weight.shape[0], 1), weight)
            total = term if total is None else total + term
        return total

    def mul_pieces_t(grads, pieces, dtype):
        width = sum(weight.shape[0] for weight, _ in pieces)
        out = jnp.zeros((grads.shape[0], width), dtype)
        for weight, start in pieces:
            out = lax.dynamic_update_slice_in_dim(out, dot_t(grads, weight).astype(dtype), start, 1)
        return out

    def fetch_columns(shard):
        rows, columns = shard.shape
        width = columns // n_f
        half = rows // 2
        core = by_f(cut(shard, (f_idx ^ 1) * width, width, 1), 1)
        far_cut = lax.dynamic_slice(
            shard, (y_idx * half, (1 - x_idx) * 2 * width), (half, 2 * width)
        )
        far = by_f(far_cut, 2)
        far_y = by_c(far, 1)
        far_core = by_f(cut(far, (1 - k_idx) * width, width, 1), 1)
        far_y_core = by_f(cut(far_y, (1 - k_idx) * width, width, 1), 1)
        mine, other = y_idx * half, (1 - y_idx) * half
        out = jnp.zeros((rows * n_f, width), shard.dtype)
        for piece, start in (
            (cut(shard, f_idx * width, width, 1), f_idx * rows),
            (core, (f_idx ^ 1) * rows),
            (cut(far, k_idx * width, width, 1), (f_idx ^ 2) * rows + mine),
            (far_core, (f_idx ^ 3) * rows + mine),
            (cut(far_y, k_idx * width, width, 1), (f_idx ^ 2) * rows + other),
            (far_y_core, (f_idx ^ 3) * rows + other),
        ):
            out = lax.dynamic_update_slice_in_dim(out, piece, start, 0)
        return out

    def gather_tokens(values):
        core = by_f(values, 1)
        far = by_f(values, 2)
        far_core = by_f(far, 1)
        return jnp.concatenate([values, core, far, far_core], axis=0)

    def sum_tokens(partial):
        parts = partial.reshape(4, row_count, partial.shape[1])
        got = by_f(jnp.stack([parts[1], parts[3]]), 1)
        near = parts[0] + got[0]
        far = (parts[2] + got[1]).astype(BF16)
        return near + by_f(far, 2).astype(F32)

    def reduce_ctx(grad):
        rows = grad.shape[0] // n_ctx
        view = grad.reshape(n_z, 2, rows, grad.shape[1])
        give = lax.dynamic_index_in_dim(view, 1 - y_idx, 1, keepdims=False)
        keep = lax.dynamic_index_in_dim(view, y_idx, 1, keepdims=False)
        pair = (keep.astype(F32) + by_c(give.astype(BF16), 1).astype(F32)).astype(BF16)
        total = lax.dynamic_index_in_dim(pair, z_idx, 0, keepdims=False).astype(F32)
        for r in range(1, n_z):
            got = by_c(lax.dynamic_index_in_dim(pair, z_idx ^ r, 0, keepdims=False), 2 * r)
            total = total + got.astype(F32)
        return total

    def rows_to_f(values):
        return lax.all_to_all(values.astype(BF16), "fsdp", 0, 1, tiled=True)

    gains = lax.all_gather(jnp.concatenate([norm1_gain, q_gain, norm2_gain]), "fsdp", axis=0)
    d1, d2 = norm1_gain.shape[0], q_gain.shape[0]
    gain_one = gains[:, :d1].reshape(-1).astype(F32)
    gain_q = gains[:, d1 : d1 + d2].reshape(-1).astype(F32)
    gain_two = gains[:, d1 + d2 :].reshape(-1).astype(F32)
    valid_f = valid_mask.astype(F32)
    total_count = all_sum(jnp.sum(valid_f).reshape(1, 1))[0, 0]
    tags = jnp.stack([blocks.reshape(-1, PIECE)[:, 0], seq_ids.reshape(-1, PIECE)[:, 0]], axis=1)
    all_tags = lax.all_gather(tags, "ctx", axis=0, tiled=True)
    tag_piece, tag_seq = all_tags[:, 0], all_tags[:, 1]

    qkv_pieces = fetch_rows(jnp.concatenate([q_down, kv_weight], axis=1))
    up_pieces = fetch_rows(q_up)
    out_pieces = fetch_rows(out_proj)
    w_gatef = fetch_columns(w_gate)
    w_upf = fetch_columns(w_up)

    positions = blocks * PIECE + jnp.arange(row_count, dtype=jnp.int32) % PIECE
    freq_table = 10000.0 ** (-(jnp.arange(half_dim, dtype=F32) * 2.0 / head_size))
    angle_table = positions.astype(F32)[:, None] * freq_table[None, :]
    cosine = jnp.cos(angle_table)
    sine = jnp.sin(angle_table)
    hidden_f = hidden_in.astype(F32)
    scale_one = rms_scale(hidden_f)
    normed = (hidden_f * scale_one * gain_one).astype(BF16)
    q_width = q_down.shape[1]
    low_all = mul_pieces(normed, qkv_pieces)
    q_low = low_all[:, :q_width]
    kv_lin = low_all[:, q_width:]
    key_rot = rope_apply(kv_lin[:, :head_size], cosine, sine).astype(BF16)
    kv_rows = jnp.concatenate([key_rot, kv_lin[:, head_size:].astype(BF16)], axis=1)
    all_kv = lax.all_gather(kv_rows, "ctx", axis=0, tiled=True)
    scale_q = rms_scale(q_low)
    q_normed = (q_low * scale_q * gain_q).astype(BF16)
    q_lin = mul_pieces(q_normed, up_pieces).reshape(row_count, head_count, head_size)
    q_rot = rope_apply(q_lin, cosine[:, None, :], sine[:, None, :]).astype(BF16)

    piece_total = all_kv.shape[0] // PIECE
    if piece_total == seq_pieces:
        seq_kv = all_kv
        key_block = jnp.repeat(tag_piece // 2, PIECE)
    else:
        wanted = (tag_seq[None, :] == seq_ids[0]) & (
            tag_piece[None, :] == jnp.arange(seq_pieces, dtype=jnp.int32)[:, None]
        )
        pick_index = jnp.sum(
            jnp.where(wanted, jnp.arange(piece_total, dtype=jnp.int32)[None, :], 0), axis=1
        )
        seq_kv = all_kv.reshape(piece_total, PIECE, 2 * head_size)[pick_index].reshape(
            seq_pieces * PIECE, 2 * head_size
        )
        key_block = jnp.arange(seq_pieces * PIECE, dtype=jnp.int32) // (2 * PIECE)
    seq_keys = seq_kv[:, :head_size]
    seq_vals = seq_kv[:, head_size:]
    allowed = key_block[None, :] <= (blocks // 2)[:, None]
    score_scale = head_size ** (-0.5)

    def masked_scores():
        raw_scores = (
            jnp.einsum("rhd,kd->hrk", q_rot, seq_keys, preferred_element_type=F32) * score_scale
        )
        return jnp.where(allowed[None], raw_scores, -1e30)

    scores = masked_scores()
    row_peak = jnp.max(scores, axis=2, keepdims=True)
    log_total = row_peak + jnp.log(jnp.sum(jnp.exp(scores - row_peak), axis=2, keepdims=True))
    probs = jnp.exp(scores - log_total).astype(BF16)
    attn_heads = (
        jnp.einsum("hrk,kd->rhd", probs, seq_vals, preferred_element_type=F32)
        .reshape(row_count, heads_width)
        .astype(BF16)
    )
    resid = hidden_f + mul_pieces(attn_heads, out_pieces)
    scale_two = rms_scale(resid)
    normed_two = (resid * scale_two * gain_two).astype(BF16)

    group_two = gather_tokens(normed_two)
    gate_lin = dot(group_two, w_gatef)
    up_lin = dot(group_two, w_upf)
    sigma = jax.nn.sigmoid(gate_lin)
    silu_gate = gate_lin * sigma
    hidden_act = (silu_gate * up_lin).astype(BF16)
    result = resid + sum_tokens(dot(hidden_act, w_down))
    diff = result - teacher.astype(F32)
    sq_local = jnp.sum(valid_f * jnp.sum(diff * diff, axis=1))
    grad_y = diff * valid_f[:, None] * (token_total / total_count)
    group_dz = gather_tokens(grad_y.astype(BF16))
    grad_hidden = dot_t(group_dz, w_down)
    grad_gate = (grad_hidden * up_lin * sigma * (1.0 + gate_lin * (1.0 - sigma))).astype(BF16)
    grad_up = (grad_hidden * silu_gate).astype(BF16)
    grad_normed_two = sum_tokens(dot_t(grad_gate, w_gatef) + dot_t(grad_up, w_upf))
    down_part = dot_rows(hidden_act, group_dz).astype(BF16)
    gate_part = dot_rows(group_two, grad_gate).astype(BF16)
    up_part = dot_rows(group_two, grad_up).astype(BF16)

    grad_resid_norm, grad_gain_two = rms_back(resid, scale_two, gain_two, grad_normed_two)
    grad_resid = grad_y + grad_resid_norm
    grad_branch = grad_resid.astype(BF16)
    grad_attn = mul_pieces_t(grad_branch, out_pieces, BF16).reshape(
        row_count, head_count, head_size
    )
    scores_again = masked_scores()
    probs_f = jnp.exp(scores_again - log_total)
    grad_probs = jnp.einsum("rhd,kd->hrk", grad_attn, seq_vals, preferred_element_type=F32)
    row_delta = jnp.sum(probs_f * grad_probs, axis=2, keepdims=True)
    grad_scores = (probs_f * (grad_probs - row_delta)).astype(BF16)
    grad_qrot = (
        jnp.einsum("hrk,kd->rhd", grad_scores, seq_keys, preferred_element_type=F32) * score_scale
    )
    grad_seqk = (
        jnp.einsum("hrk,rhd->kd", grad_scores, q_rot, preferred_element_type=F32) * score_scale
    )
    grad_seqv = jnp.einsum("hrk,rhd->kd", probs, grad_attn, preferred_element_type=F32)
    grad_seq = jnp.concatenate([grad_seqk, grad_seqv], axis=1)
    if piece_total != seq_pieces:
        grad_seq = (
            jnp.zeros((piece_total, PIECE, 2 * head_size), F32)
            .at[pick_index]
            .set(grad_seq.reshape(seq_pieces, PIECE, 2 * head_size))
            .reshape(piece_total * PIECE, 2 * head_size)
        )
    grad_kvrows = reduce_ctx(grad_seq)
    grad_klin = rope_back(grad_kvrows[:, :head_size], cosine, sine)
    grad_kv = jnp.concatenate([grad_klin, grad_kvrows[:, head_size:]], axis=1).astype(BF16)
    grad_qlin = (
        rope_back(grad_qrot, cosine[:, None, :], sine[:, None, :])
        .reshape(row_count, heads_width)
        .astype(BF16)
    )
    grad_qnormed = mul_pieces_t(grad_qlin, up_pieces, F32)
    grad_qlow_f, grad_gain_q = rms_back(q_low, scale_q, gain_q, grad_qnormed)
    grad_qlow = grad_qlow_f.astype(BF16)
    grad_low = jnp.concatenate([grad_qlow, grad_kv], axis=1)
    grad_normed = mul_pieces_t(grad_low, qkv_pieces, F32)
    grad_input_norm, grad_gain_one = rms_back(hidden_f, scale_one, gain_one, grad_normed)
    grad_input = grad_resid + grad_input_norm

    down_rows = reduce_ctx(down_part).astype(BF16)
    order = [(c * n_f + f, f * n_ctx + c) for c in range(n_ctx) for f in range(n_f)]
    grad_down = lax.ppermute(down_rows, ("ctx", "fsdp"), order).astype(F32)
    grad_wgate = rows_to_f(reduce_ctx(gate_part)).astype(F32)
    grad_wup = rows_to_f(reduce_ctx(up_part)).astype(F32)

    def group_rows(values):
        return lax.all_gather(values, "fsdp", axis=0, tiled=True)

    out_block = heads_width // (n_ctx * n_f)
    attn_group = lax.all_to_all(
        attn_heads.reshape(row_count, n_ctx, n_f, out_block), "fsdp", 2, 0, tiled=True
    ).reshape(row_count * n_f, n_ctx * out_block)
    branch_group = group_rows(grad_branch)
    grad_wout = reduce_ctx(dot_rows(attn_group, branch_group).astype(BF16))

    qlin_group = lax.all_to_all(grad_qlin, "fsdp", 1, 0, tiled=True)
    qnorm_group = group_rows(q_normed)
    grad_wqup = rows_to_f(reduce_ctx(dot_rows(qnorm_group, qlin_group).astype(BF16))).astype(F32)

    q_cut, kv_cut = q_width // n_f, 2 * head_size // n_f
    low_mix = jnp.concatenate(
        [grad_qlow.reshape(row_count, n_f, q_cut), grad_kv.reshape(row_count, n_f, kv_cut)], axis=2
    ).reshape(row_count, n_f * (q_cut + kv_cut))
    low_group = lax.all_to_all(low_mix, "fsdp", 1, 0, tiled=True)
    normed_group = group_rows(normed)
    grad_low_w = rows_to_f(reduce_ctx(dot_rows(normed_group, low_group).astype(BF16)))
    grad_low_w = grad_low_w.astype(F32).reshape(-1, n_f, q_cut + kv_cut)
    grad_wqdown = grad_low_w[:, :, :q_cut].reshape(-1, q_width)
    grad_wkv = grad_low_w[:, :, q_cut:].reshape(-1, 2 * head_size)

    small = jnp.concatenate([grad_gain_one, grad_gain_q, grad_gain_two, sq_local.reshape(1)])
    small = lax.psum(small, ("ctx", "fsdp"))
    device = c_idx * n_f + f_idx
    q1, q2 = model_width, model_width + q_width
    n_dev = n_ctx * n_f

    def own_part(values):
        size = values.shape[0] // n_dev
        return cut(values, device * size, size, 0)

    loss_now = small[-1] / (model_width * total_count)
    return (
        result.astype(BF16),
        loss_now,
        grad_input,
        own_part(small[:q1]),
        grad_wqdown,
        own_part(small[q1:q2]),
        grad_wqup,
        grad_wkv,
        grad_wout,
        own_part(small[q2 : q2 + model_width]),
        grad_wgate,
        grad_wup,
        grad_down,
    )


def solution(mesh):
    both = ("ctx", "fsdp")
    rows = P(both, None)
    flat = P(both)
    shard = P("fsdp", None)
    gain = P("fsdp")
    return jax.shard_map(
        body,
        mesh=mesh,
        in_specs=(
            rows,
            rows,
            flat,
            flat,
            flat,
            gain,
            shard,
            gain,
            shard,
            shard,
            shard,
            gain,
            shard,
            shard,
            shard,
        ),
        out_specs=(
            rows,
            P(),
            rows,
            flat,
            rows,
            flat,
            rows,
            rows,
            rows,
            flat,
            rows,
            rows,
            rows,
        ),
        check_vma=False,
    )
```

```python
import functools
import math

import jax
import jax.numpy as jnp
from jax import lax
from jax.experimental import pallas as pl
from jax.experimental.pallas import tpu as pltpu
from jax.sharding import PartitionSpec as P

PIECE = 128
SEQ_BLOCKS = 8
NORM_EPS = 1e-05
F32 = jnp.float32
BF16 = jnp.bfloat16
LOG2E = math.log2(math.e)
HEAD_GROUP = 4


def rms_scale(values):
    return lax.rsqrt(jnp.mean(values * values, axis=-1, keepdims=True) + NORM_EPS)


def rms_back(values, scale, gain, grad):
    grad_gain = jnp.sum(grad * values * scale, axis=0)
    ge = gain * grad
    inner = jnp.mean(ge * values, axis=-1, keepdims=True)
    return scale * ge - values * (scale * scale * scale) * inner, grad_gain


def rope_apply(values, cosine, sine):
    half_dim = values.shape[-1] // 2
    one = values[..., :half_dim]
    two = values[..., half_dim:]
    return jnp.concatenate([one * cosine - two * sine, two * cosine + one * sine], axis=-1)


def rope_back(grads, cosine, sine):
    half_dim = grads.shape[-1] // 2
    one = grads[..., :half_dim]
    two = grads[..., half_dim:]
    return jnp.concatenate([one * cosine + two * sine, two * cosine - one * sine], axis=-1)


def after(values, *deps):
    return lax.optimization_barrier((values, deps))[0]


def dot(a, b):
    return jnp.dot(a, b, preferred_element_type=F32)


def dot_t(a, b):
    return lax.dot_general(a, b, (((1,), (1,)), ((), ())), preferred_element_type=F32)


def dot_rows(a, b):
    return lax.dot_general(a, b, (((0,), (0,)), ((), ())), preferred_element_type=F32)


def contract_last(a, b):
    return lax.dot_general(a, b, (((1,), (1,)), ((), ())), preferred_element_type=F32)

def find_pieces(tags_ref, own_ref, pick_ref, total):
    @pl.loop(0, total)
    def _(u):
        @pl.when(tags_ref[u, 1] == own_ref[2])
        def _():
            pick_ref[tags_ref[u, 0]] = u

def stack_heads(ref, hd):
    return jnp.concatenate([ref[:, h*hd:(h+1)*hd] for h in range(HEAD_GROUP)], axis=0)

def attn_fwd_kernel(tags_ref, own_ref, q_ref, kv_ref, o_ref, lse_ref, k_s, vt_s, acc_s, pick_s):
    half = pl.program_id(0)
    hd = k_s.shape[1]
    pieces = k_s.shape[0] // PIECE
    total = kv_ref.shape[0] // PIECE
    wide = 2 * PIECE
    coef = hd ** -0.5 * LOG2E

    @pl.when((half == 0) & (pl.program_id(1) == 0))
    def _():
        find_pieces(tags_ref, own_ref, pick_s, total)
        for i in range(pieces):
            rows = pl.ds(pl.multiple_of(pick_s[i] * PIECE, PIECE), PIECE)
            k_s[i*PIECE:(i+1)*PIECE, :] = kv_ref[rows, :hd]
            vt_s[:, i*PIECE:(i+1)*PIECE] = kv_ref[rows, hd:].T

    q = stack_heads(q_ref, hd)
    acc_s[...] = jnp.zeros_like(acc_s)
    rows = q.shape[0]
    def step(i, carry):
        peak, total_p = carry
        at = pl.ds(pl.multiple_of(i * wide, wide), wide)
        raw = contract_last(k_s[at, :], q)
        top = jnp.maximum(peak, jnp.max(raw, axis=0, keepdims=True))
        fade = jnp.exp2((peak - top) * coef)
        p = jnp.exp2((raw - top) * coef)
        acc_s[...] = acc_s[...] * fade + jnp.dot(vt_s[:, at], p.astype(BF16), preferred_element_type=F32)
        return top, total_p * fade + jnp.sum(p, axis=0, keepdims=True)
    count = own_ref[half] // 2 + 1
    peak, total_p = lax.fori_loop(0, count, step, (jnp.full((1, rows), -1e30, F32), jnp.zeros((1, rows), F32)))
    out = (acc_s[...] / total_p).astype(BF16).T
    for h in range(HEAD_GROUP):
        o_ref[:, h*hd:(h+1)*hd] = out[h*PIECE:(h+1)*PIECE, :]
    lse_ref[0] = peak * coef + jnp.log2(total_p)

def attn_fwd(tags, own, q, kv, hd, pieces):
    n_rows, width = q.shape
    groups = width // hd // HEAD_GROUP
    gw = HEAD_GROUP * hd
    halves = n_rows // PIECE
    rows = HEAD_GROUP * PIECE
    blk = pl.BlockSpec((PIECE, gw), lambda p, g, *_: (p, g))
    flops = 4 * n_rows * width * pieces * PIECE * 9 // 16
    return pl.pallas_call(
        attn_fwd_kernel,
        out_shape=(jax.ShapeDtypeStruct(q.shape, BF16), jax.ShapeDtypeStruct((halves*groups, 1, rows), F32)),
        grid_spec=pltpu.PrefetchScalarGridSpec(
            num_scalar_prefetch=2, grid=(halves, groups),
            in_specs=[blk, pl.BlockSpec(kv.shape, lambda p, g, *_: (0, 0))],
            out_specs=[blk, pl.BlockSpec((1, 1, rows), lambda p, g, *_: (p*groups+g, 0, 0))],
            scratch_shapes=[pltpu.VMEM((pieces*PIECE, hd), BF16), pltpu.VMEM((hd, pieces*PIECE), BF16),
                            pltpu.VMEM((hd, rows), F32), pltpu.SMEM((pieces,), jnp.int32)]),
        compiler_params=pltpu.CompilerParams(vmem_limit_bytes=40 << 20),
        cost_estimate=pl.CostEstimate(flops=flops, transcendentals=flops//(4*hd), bytes_accessed=2*(2*q.size+kv.size)),
        name="attn_fwd",
    )(tags, own, q, kv)

def attn_bwd_kernel(tags_ref, own_ref, q_ref, do_ref, o_ref, lse_ref, cos_ref, sin_ref, kv_ref, dq_ref, dkv_ref,
                    k_s, kt_s, v_s, dq_s, dk_s, dv_s, pick_s):
    half = pl.program_id(0)
    group = pl.program_id(1)
    hd = k_s.shape[1]
    pieces = k_s.shape[0] // PIECE
    total = kv_ref.shape[0] // PIECE
    wide = 2 * PIECE
    coef = hd ** -0.5 * LOG2E
    scale = hd ** -0.5

    @pl.when((half == 0) & (group == 0))
    def _():
        find_pieces(tags_ref, own_ref, pick_s, total)
        for i in range(pieces):
            rows = pl.ds(pl.multiple_of(pick_s[i] * PIECE, PIECE), PIECE)
            keys = kv_ref[rows, :hd]
            k_s[i*PIECE:(i+1)*PIECE, :] = keys
            kt_s[:, i*PIECE:(i+1)*PIECE] = keys.T
            v_s[i*PIECE:(i+1)*PIECE, :] = kv_ref[rows, hd:]
        dk_s[...] = jnp.zeros_like(dk_s)
        dv_s[...] = jnp.zeros_like(dv_s)

    q = stack_heads(q_ref, hd)
    do = stack_heads(do_ref, hd)
    prod = do.astype(F32) * stack_heads(o_ref, hd).astype(F32)
    delta = lax.dot_general(jnp.ones((8, hd), F32), prod, (((1,), (1,)), ((), ())),
                            preferred_element_type=F32, precision=lax.Precision.HIGHEST)[:1]
    lse = lse_ref[0]
    dq_s[...] = jnp.zeros_like(dq_s)
    def step(i, carry):
        at = pl.ds(pl.multiple_of(i * wide, wide), wide)
        p = jnp.exp2(contract_last(k_s[at, :], q) * coef - lse)
        dp = contract_last(v_s[at, :], do)
        ds = (p * (dp - delta)).astype(BF16)
        dv_s[at, :] += jnp.dot(p.astype(BF16), do, preferred_element_type=F32)
        dk_s[at, :] += jnp.dot(ds, q, preferred_element_type=F32)
        dq_s[...] += jnp.dot(kt_s[:, at], ds, preferred_element_type=F32)
        return carry
    lax.fori_loop(0, own_ref[half] // 2 + 1, step, 0)
    dq = (dq_s[...] * scale).T
    cos, sin = cos_ref[...], sin_ref[...]
    mid = hd // 2
    for h in range(HEAD_GROUP):
        one = dq[h*PIECE:(h+1)*PIECE, :mid]
        two = dq[h*PIECE:(h+1)*PIECE, mid:]
        dq_ref[:, h*hd:h*hd+mid] = (one * cos + two * sin).astype(BF16)
        dq_ref[:, h*hd+mid:(h+1)*hd] = (two * cos - one * sin).astype(BF16)

    @pl.when((half == pl.num_programs(0) - 1) & (group == pl.num_programs(1) - 1))
    def _():
        dkv_ref[:, :hd] = (dk_s[...] * scale).astype(BF16)
        dkv_ref[:, hd:] = dv_s[...].astype(BF16)

def attn_bwd(tags, own, q, do, o, lse, cos, sin, kv, hd, pieces):
    n_rows, width = q.shape
    groups = width // hd // HEAD_GROUP
    gw = HEAD_GROUP * hd
    halves = n_rows // PIECE
    rows = HEAD_GROUP * PIECE
    blk = pl.BlockSpec((PIECE, gw), lambda p, g, *_: (p, g))
    trig = pl.BlockSpec((PIECE, hd // 2), lambda p, g, *_: (p, 0))
    keys = pieces * PIECE
    flops = 10 * n_rows * width * keys * 9 // 16
    return pl.pallas_call(
        attn_bwd_kernel,
        out_shape=(jax.ShapeDtypeStruct(q.shape, BF16), jax.ShapeDtypeStruct((keys, 2*hd), BF16)),
        grid_spec=pltpu.PrefetchScalarGridSpec(
            num_scalar_prefetch=2, grid=(halves, groups),
            in_specs=[blk, blk, blk, pl.BlockSpec((1, 1, rows), lambda p, g, *_: (p*groups+g, 0, 0)), trig, trig,
                      pl.BlockSpec(kv.shape, lambda p, g, *_: (0, 0))],
            out_specs=[blk, pl.BlockSpec((keys, 2*hd), lambda p, g, *_: (0, 0))],
            scratch_shapes=[pltpu.VMEM((keys, hd), BF16), pltpu.VMEM((hd, keys), BF16), pltpu.VMEM((keys, hd), BF16),
                            pltpu.VMEM((hd, rows), F32), pltpu.VMEM((keys, hd), F32), pltpu.VMEM((keys, hd), F32),
                            pltpu.SMEM((pieces,), jnp.int32)]),
        compiler_params=pltpu.CompilerParams(vmem_limit_bytes=48 << 20),
        cost_estimate=pl.CostEstimate(flops=flops, transcendentals=flops//(10*hd), bytes_accessed=2*(4*q.size+2*kv.size)),
        name="attn_bwd",
    )(tags, own, q, do, o, lse, cos, sin, kv)

MESH = pl.DeviceIdType.MESH


def flip(index, mask):
    out = 0
    bit = 1
    while bit <= mask:
        part = (index // bit) % 2
        out = out + bit * ((1 - part) if mask & bit else part)
        bit *= 2
    return out + (index // bit) * bit


def row_loop(rows, body):
    step = 32 if rows % 32 == 0 else 16

    @pl.loop(0, rows // step)
    def _(i):
        body(pl.ds(pl.multiple_of(i * step, step), step))


def tail_kernel(kinds, n_ctx, n_f, *refs):
    count = len(kinds)
    n_z = n_ctx // 2
    refs = list(refs)
    small_ref = refs.pop(0)
    ins = [refs.pop(0) for _ in range(count)]
    small_out = refs.pop(0)
    outs = [refs.pop(0) for _ in range(count)]
    small_got = refs.pop(0)
    y_got, pairs, z_got, totals, f_got = [], [], [], [], []
    for needs_y, cut_f in kinds:
        y_got.append(refs.pop(0) if needs_y else None)
        pairs.append(refs.pop(0) if needs_y else None)
        z_got.append(refs.pop(0))
        totals.append(refs.pop(0) if cut_f else None)
        f_got.append(refs.pop(0) if cut_f else None)
    s_send, s_recv, y_send, y_recv, z_send, z_recv, f_send, f_recv = refs
    c_idx = lax.axis_index("ctx")
    f_idx = lax.axis_index("fsdp")
    y_idx = c_idx % 2
    z_idx = c_idx // 2

    def over_c(mask):
        return (flip(c_idx, mask), f_idx)

    def over_f(mask):
        return (c_idx, flip(f_idx, mask))

    peers = [over_f(m) for m in range(1, n_f)] + [over_c(1)]
    peers += [over_c(2 * r) for r in range(1, n_z)]
    barrier = pltpu.get_barrier_semaphore()
    for peer in peers:
        pl.semaphore_signal(barrier, inc=1, device_id=peer, device_id_type=MESH)
    pl.semaphore_wait(barrier, len(peers))
    started = []

    def send(src, dst, send_sem, recv_sem, peer):
        copy = pltpu.make_async_remote_copy(
            src_ref=src,
            dst_ref=dst,
            send_sem=send_sem,
            recv_sem=recv_sem,
            device_id=peer,
            device_id_type=MESH,
        )
        copy.start()
        started.append(copy)
        return copy

    steps = [over_f(1), over_f(2), over_c(1)]
    mask = 2
    while mask < n_ctx:
        steps.append(over_c(mask))
        mask *= 2
    y_copies = {}
    z_copies = {}

    def send_z(m, src, r):
        z_copies[m, r] = send(
            src.at[flip(z_idx, r)],
            z_got[m].at[r - 1],
            z_send.at[m, r - 1],
            z_recv.at[m, r - 1],
            over_c(2 * r),
        )

    order = list(range(1, n_z)) + [0]
    small_out[...] = small_ref[...]
    for s, peer in enumerate(steps):
        small_got[s, 0] = small_out[...]
        send(small_got.at[s, 0], small_got.at[s, 1], s_send.at[s], s_recv.at[s], peer).wait_recv()
        small_out[...] = small_out[...] + small_got[s, 1]
        if s == 2:
            for m, (needs_y, _) in enumerate(kinds):
                if needs_y:
                    for r in order:
                        b = flip(z_idx, r)
                        y_copies[m, r] = send(
                            ins[m].at[b, 1 - y_idx],
                            y_got[m].at[r],
                            y_send.at[m, r],
                            y_recv.at[m, r],
                            over_c(1),
                        )
    for m, (needs_y, _) in enumerate(kinds):
        if not needs_y:
            for r in range(1, n_z):
                send_z(m, ins[m], r)
    for m, (needs_y, _) in enumerate(kinds):
        if needs_y:
            for r in order:
                b = flip(z_idx, r)
                y_copies[m, r].wait_recv()

                def add_pair(at, m=m, r=r, b=b):
                    pairs[m][b, at, :] = (
                        ins[m][b, y_idx, at, :].astype(F32) + y_got[m][r, at, :].astype(F32)
                    ).astype(BF16)

                row_loop(pairs[m].shape[1], add_pair)
                if r:
                    send_z(m, pairs[m], r)
    f_copies = {}
    for m, (needs_y, cut_f) in enumerate(kinds):
        own = pairs[m] if needs_y else ins[m]
        for r in range(1, n_z):
            z_copies[m, r].wait_recv()
        rows = own.shape[1]

        def add_all(at, m=m, own=own, cut_f=cut_f):
            total = own[z_idx, at, :].astype(F32)
            for r in range(1, n_z):
                total = total + z_got[m][r - 1, at, :].astype(F32)
            if cut_f:
                totals[m][at, :] = total.astype(BF16)
            else:
                outs[m][at, :] = total

        row_loop(rows, add_all)
        if cut_f:
            part = rows // n_f
            for r in range(1, n_f):
                f_copies[m, r] = send(
                    totals[m].at[pl.ds(pl.multiple_of(flip(f_idx, r) * part, part), part), :],
                    f_got[m].at[r - 1],
                    f_send.at[m, r - 1],
                    f_recv.at[m, r - 1],
                    over_f(r),
                )
    for m, (_, cut_f) in enumerate(kinds):
        if cut_f:
            rows, width = totals[m].shape
            part = rows // n_f
            for r in range(n_f):
                if r:
                    f_copies[m, r].wait_recv()
                at = pl.ds(pl.multiple_of(flip(f_idx, r) * width, 128), width)
                if r:
                    outs[m][:, at] = f_got[m][r - 1].astype(F32)
                else:
                    mine = pl.ds(pl.multiple_of(f_idx * part, part), part)
                    outs[m][:, at] = totals[m][mine, :].astype(F32)
    for copy in started:
        copy.wait_send()


def tail_reduce(kinds, n_ctx, n_f, small, mats):
    n_z = n_ctx // 2
    steps = 2 + (n_ctx.bit_length() - 1)
    outs = [jax.ShapeDtypeStruct(small.shape, F32)]
    scratch = [pltpu.VMEM((steps, 2) + small.shape, F32)]
    for (needs_y, cut_f), mat in zip(kinds, mats):
        rows, width = mat.shape[-2:]
        if needs_y:
            scratch += [pltpu.VMEM((n_z, rows, width), BF16)] * 2
        scratch.append(pltpu.VMEM((n_z - 1, rows, width), BF16))
        if cut_f:
            scratch.append(pltpu.VMEM((rows, width), BF16))
            scratch.append(pltpu.VMEM((n_f - 1, rows // n_f, width), BF16))
            outs.append(jax.ShapeDtypeStruct((rows // n_f, width * n_f), F32))
        else:
            outs.append(jax.ShapeDtypeStruct((rows, width), F32))
    count = len(kinds)
    dma = pltpu.SemaphoreType.DMA
    scratch += [dma((steps,))] * 2 + [dma((count, n_z))] * 4 + [dma((count, n_f))] * 2
    vmem = pl.BlockSpec(memory_space=pltpu.VMEM)
    return pl.pallas_call(
        functools.partial(tail_kernel, kinds, n_ctx, n_f),
        out_shape=tuple(outs),
        in_specs=[vmem] * (1 + count),
        out_specs=tuple([vmem] * (1 + count)),
        scratch_shapes=scratch,
        compiler_params=pltpu.CompilerParams(
            collective_id=0, has_side_effects=True, vmem_limit_bytes=48 << 20
        ),
        name="tail_reduce",
    )(small, *mats)


def body(
    hidden_in,
    teacher,
    blocks,
    seq_ids,
    valid_mask,
    norm1_gain,
    q_down,
    q_gain,
    q_up,
    kv_weight,
    out_proj,
    norm2_gain,
    w_gate,
    w_up,
    w_down,
):
    row_count, model_width = hidden_in.shape
    head_size = kv_weight.shape[1] // 2
    heads_width = q_up.shape[1]
    head_count = heads_width // head_size
    half_dim = head_size // 2
    q_width = q_down.shape[1]
    n_ctx = lax.axis_size("ctx")
    n_f = lax.axis_size("fsdp")
    n_z = n_ctx // 2
    token_total = row_count * n_ctx * n_f
    seq_pieces = 2 * SEQ_BLOCKS
    c_idx = lax.axis_index("ctx")
    f_idx = lax.axis_index("fsdp")
    y_idx = c_idx % 2
    z_idx = c_idx // 2
    x_idx = f_idx // 2
    k_idx = f_idx % 2

    def by_f(values, mask):
        return lax.ppermute(values, "fsdp", [(i, i ^ mask) for i in range(n_f)])

    def by_c(values, mask):
        return lax.ppermute(values, "ctx", [(i, i ^ mask) for i in range(n_ctx)])

    def cut(values, start, size, axis):
        return lax.dynamic_slice_in_dim(values, start, size, axis)

    def gather_bit(values, got, bit):
        return jnp.concatenate(
            [jnp.where(bit == 0, values, got), jnp.where(bit == 0, got, values)], axis=0
        )

    def fetch_far(shard, mask, gate):
        half = shard.shape[0] // 2
        bit = (c_idx // mask) % 2
        return by_f(after(cut(shard, bit * half, half, 0), *gate), 2)

    def fetch_rest(shard, far, mask):
        rows = shard.shape[0]
        half = rows // 2
        bit = (c_idx // mask) % 2
        core = by_f(shard, 1)
        far_y = by_c(far, mask)
        far_core = by_f(far, 1)
        far_y_core = by_f(far_y, 1)
        mine, other = bit * half, (1 - bit) * half
        return [
            (shard, f_idx * rows),
            (core, (f_idx ^ 1) * rows),
            (far, (f_idx ^ 2) * rows + mine),
            (far_core, (f_idx ^ 3) * rows + mine),
            (far_y, (f_idx ^ 2) * rows + other),
            (far_y_core, (f_idx ^ 3) * rows + other),
        ]

    def mul_pieces(acts, pieces):
        total = None
        for weight, start in pieces:
            term = dot(cut(acts, start, weight.shape[0], 1), weight)
            total = term if total is None else total + term
        return total

    def mul_pieces_t(grads, pieces, dtype):
        width = sum(weight.shape[0] for weight, _ in pieces)
        out = jnp.zeros((grads.shape[0], width), dtype)
        for weight, start in pieces:
            out = lax.dynamic_update_slice_in_dim(out, dot_t(grads, weight).astype(dtype), start, 1)
        return out

    def columns_far(shard, gate):
        rows, columns = shard.shape
        width = columns // n_f
        half = rows // 2
        far_cut = lax.dynamic_slice(
            shard, (y_idx * half, (1 - x_idx) * 2 * width), (half, 2 * width)
        )
        return by_f(after(far_cut, *gate), 2)

    def columns_rest(shard, far):
        rows, columns = shard.shape
        width = columns // n_f
        half = rows // 2
        core = by_f(cut(shard, (f_idx ^ 1) * width, width, 1), 1)
        far_y = by_c(far, 1)
        far_core = by_f(cut(far, (1 - k_idx) * width, width, 1), 1)
        far_y_core = by_f(cut(far_y, (1 - k_idx) * width, width, 1), 1)
        mine, other = y_idx * half, (1 - y_idx) * half
        out = jnp.zeros((rows * n_f, width), shard.dtype)
        for piece, start in (
            (cut(shard, f_idx * width, width, 1), f_idx * rows),
            (core, (f_idx ^ 1) * rows),
            (cut(far, k_idx * width, width, 1), (f_idx ^ 2) * rows + mine),
            (far_core, (f_idx ^ 3) * rows + mine),
            (cut(far_y, k_idx * width, width, 1), (f_idx ^ 2) * rows + other),
            (far_y_core, (f_idx ^ 3) * rows + other),
        ):
            out = lax.dynamic_update_slice_in_dim(out, piece, start, 0)
        return out

    def gather_tokens(values):
        core = by_f(values, 1)
        far = by_f(values, 2)
        far_core = by_f(far, 1)
        return jnp.concatenate([values, core, far, far_core], axis=0)

    def sum_tokens(make_half):
        far = make_half(1).reshape(2, row_count, -1)
        far = (far[0] + by_f(far[1], 1)).astype(BF16)
        far = by_f(far, 2)
        near = make_half(0).reshape(2, row_count, -1)
        near = near[0] + by_f(near[1], 1)
        return near + far.astype(F32)

    def ctx_split(grad):
        view = grad.reshape(n_z, 2, grad.shape[0] // n_ctx, grad.shape[1])
        give = lax.dynamic_index_in_dim(view, 1 - y_idx, 1, keepdims=False)
        keep = lax.dynamic_index_in_dim(view, y_idx, 1, keepdims=False)
        return give, keep

    def ctx_pair(keep, got):
        return (keep.astype(F32) + got.astype(F32)).astype(BF16)

    def ctx_spread(pair):
        return [pair] + [
            by_c(lax.dynamic_index_in_dim(pair, z_idx ^ r, 0, keepdims=False), 2 * r)
            for r in range(1, n_z)
        ]

    def ctx_total(parts):
        total = lax.dynamic_index_in_dim(parts[0], z_idx, 0, keepdims=False).astype(F32)
        for got in parts[1:]:
            total = total + got.astype(F32)
        return total

    def rows_to_f(values):
        return lax.all_to_all(values.astype(BF16), "fsdp", 0, 1, tiled=True)

    valid_f = valid_mask.astype(F32)
    d1, d2 = norm1_gain.shape[0], q_gain.shape[0]
    qkv_shard = jnp.concatenate([q_down, kv_weight], axis=1)
    qkv_far = fetch_far(qkv_shard, 1, ())
    info = jnp.concatenate(
        [
            norm1_gain.astype(F32),
            q_gain.astype(F32),
            norm2_gain.astype(F32),
            jnp.full((128,), jnp.sum(valid_f)),
        ]
    ).reshape(1, -1)
    info = gather_bit(info, by_f(info, 1), k_idx)
    info = gather_bit(info, by_f(info, 2), x_idx)
    gain_one = info[:, :d1].reshape(-1)
    gain_q = info[:, d1 : d1 + d2].reshape(-1)
    gain_two = info[:, d1 + d2 : 2 * d1 + d2].reshape(-1)
    tag_row = jnp.concatenate(
        [
            jnp.stack([blocks.reshape(-1, PIECE)[:, 0], seq_ids.reshape(-1, PIECE)[:, 0]], axis=1)
            .astype(F32)
            .reshape(-1),
            jnp.sum(info[:, 2 * d1 + d2]).reshape(1),
        ]
    )
    tag_row = jnp.pad(tag_row, (0, 128 - tag_row.shape[0])).reshape(1, 128)
    mask = 1
    while mask < n_ctx:
        tag_row = gather_bit(tag_row, by_c(tag_row, mask), (c_idx // mask) % 2)
        mask *= 2
    own_pieces = row_count // PIECE
    tags = tag_row[:, : 2 * own_pieces].reshape(-1, 2).astype(jnp.int32)
    total_count = jnp.sum(tag_row[:, 2 * own_pieces])
    own = jnp.concatenate([blocks.reshape(-1, PIECE)[:, 0], seq_ids[:1]])

    up_far = fetch_far(q_up, 2, (info,))
    out_far = fetch_far(out_proj, 2, (qkv_far,))
    gate_far = columns_far(w_gate, (up_far,))
    upw_far = columns_far(w_up, (out_far,))
    qkv_pieces = fetch_rest(qkv_shard, qkv_far, 1)
    up_pieces = fetch_rest(q_up, up_far, 2)
    out_pieces = fetch_rest(out_proj, out_far, 2)
    w_gatef = columns_rest(w_gate, gate_far)
    w_upf = columns_rest(w_up, upw_far)

    positions = blocks * PIECE + jnp.arange(row_count, dtype=jnp.int32) % PIECE
    freq_table = 10000.0 ** (-(jnp.arange(half_dim, dtype=F32) * 2.0 / head_size))
    angle_table = positions.astype(F32)[:, None] * freq_table[None, :]
    cosine = jnp.cos(angle_table)
    sine = jnp.sin(angle_table)
    hidden_f = hidden_in.astype(F32)
    scale_one = rms_scale(hidden_f)
    normed = (hidden_f * scale_one * gain_one).astype(BF16)
    low_all = mul_pieces(normed, qkv_pieces)
    q_low = low_all[:, :q_width]
    kv_lin = low_all[:, q_width:]
    key_rot = rope_apply(kv_lin[:, :head_size], cosine, sine).astype(BF16)
    kv_rows = jnp.concatenate([key_rot, kv_lin[:, head_size:].astype(BF16)], axis=1)
    all_kv = lax.all_gather(kv_rows, "ctx", axis=0, tiled=True)
    scale_q = rms_scale(q_low)
    q_normed = (q_low * scale_q * gain_q).astype(BF16)
    q_lin = mul_pieces(q_normed, up_pieces).reshape(row_count, head_count, head_size)
    q_rot = rope_apply(q_lin, cosine[:, None, :], sine[:, None, :]).astype(BF16)
    q_rot = q_rot.reshape(row_count, heads_width)

    attn_heads, lse = attn_fwd(tags, own, q_rot, all_kv, head_size, seq_pieces)
    resid = hidden_f + mul_pieces(attn_heads, out_pieces)
    scale_two = rms_scale(resid)
    normed_two = (resid * scale_two * gain_two).astype(BF16)

    group_two = gather_tokens(normed_two)
    gate_lin = dot(group_two, w_gatef)
    up_lin = dot(group_two, w_upf)
    sigma = jax.nn.sigmoid(gate_lin)
    silu_gate = gate_lin * sigma
    hidden_act = (silu_gate * up_lin).astype(BF16)
    side = 2 * row_count

    def down_half(j):
        return dot(hidden_act[j * side : (j + 1) * side], w_down)

    result = resid + sum_tokens(down_half)
    diff = result - teacher.astype(F32)
    sq_local = jnp.sum(valid_f * jnp.sum(diff * diff, axis=1))
    grad_y = diff * valid_f[:, None] * (token_total / total_count)
    group_dz = gather_tokens(grad_y.astype(BF16))
    down_part = dot_rows(hidden_act, group_dz).astype(BF16)
    down_give, down_keep = ctx_split(down_part)
    down_got = by_c(down_give, 1)
    group_dz2 = after(group_dz, down_part)
    grad_hidden = dot_t(group_dz2, w_down)
    grad_gate = (grad_hidden * up_lin * sigma * (1.0 + gate_lin * (1.0 - sigma))).astype(BF16)
    grad_up = (grad_hidden * silu_gate).astype(BF16)
    gate_part = dot_rows(group_two, grad_gate).astype(BF16)
    gate_give, gate_keep = ctx_split(gate_part)
    gate_got = by_c(gate_give, 1)

    def back_half(j):
        rows = slice(j * side, (j + 1) * side)
        return dot_t(grad_gate[rows], w_gatef) + dot_t(grad_up[rows], w_upf)

    grad_normed_two = sum_tokens(back_half)
    up_part = dot_rows(group_two, grad_up).astype(BF16)
    up_give, up_keep = ctx_split(up_part)

    grad_resid_norm, grad_gain_two = rms_back(resid, scale_two, gain_two, grad_normed_two)
    grad_resid = grad_y + grad_resid_norm
    grad_branch = grad_resid.astype(BF16)
    grad_attn = mul_pieces_t(grad_branch, out_pieces, BF16)
    down_parts = ctx_spread(ctx_pair(down_keep, after(down_got, grad_attn)))

    grad_qlin, grad_seq = attn_bwd(
        tags, own, q_rot, grad_attn, attn_heads, lse, cosine, sine, all_kv, head_size, seq_pieces
    )
    by_piece = grad_seq.reshape(seq_pieces, PIECE, 2 * head_size)
    piece_tag = tags[:, 0].reshape(n_z, 2, own_pieces)
    piece_own = (tags[:, 1] == seq_ids[0]).reshape(n_z, 2, own_pieces)

    def kv_half(bit):
        places = lax.dynamic_index_in_dim(piece_tag, bit, 1, keepdims=False).reshape(-1)
        picked = by_piece[places]
        if n_ctx * own_pieces != seq_pieces:
            mine = lax.dynamic_index_in_dim(piece_own, bit, 1, keepdims=False).reshape(-1)
            picked = jnp.where(mine[:, None, None], picked, jnp.zeros_like(picked))
        return picked.reshape(n_z, own_pieces * PIECE, 2 * head_size)

    kv_got = by_c(kv_half(1 - y_idx), 1)
    kv_keep = kv_half(y_idx)
    up_got = by_c(after(up_give, grad_seq), 1)
    gate_parts = ctx_spread(ctx_pair(gate_keep, after(gate_got, grad_seq)))

    grad_qnormed = mul_pieces_t(grad_qlin, up_pieces, F32)
    grad_qlow_f, grad_gain_q = rms_back(q_low, scale_q, gain_q, grad_qnormed)
    grad_qlow = grad_qlow_f.astype(BF16)
    kv_total = ctx_total(ctx_spread(ctx_pair(kv_keep, after(kv_got, grad_qlow))))
    grad_klin = rope_back(kv_total[:, :head_size], cosine, sine)
    grad_kv = jnp.concatenate([grad_klin, kv_total[:, head_size:]], axis=1).astype(BF16)
    grad_low = jnp.concatenate([grad_qlow, grad_kv], axis=1)
    grad_normed = mul_pieces_t(grad_low, qkv_pieces, F32)
    grad_input_norm, grad_gain_one = rms_back(hidden_f, scale_one, gain_one, grad_normed)
    grad_input = grad_resid + grad_input_norm

    def group_rows(values):
        return lax.all_gather(values, "fsdp", axis=0, tiled=True)

    def by_ctx(grad):
        return grad.reshape(n_z, 2, grad.shape[0] // n_ctx, grad.shape[1])

    out_block = heads_width // (n_ctx * n_f)
    attn_group = lax.all_to_all(
        attn_heads.reshape(row_count, n_ctx, n_f, out_block), "fsdp", 2, 0, tiled=True
    ).reshape(row_count * n_f, n_ctx * out_block)
    branch_group = group_rows(grad_branch)
    out_part = dot_rows(attn_group, branch_group).astype(BF16)

    qlin_group = lax.all_to_all(grad_qlin, "fsdp", 1, 0, tiled=True)
    qnorm_group = group_rows(q_normed)
    qup_part = dot_rows(qnorm_group, qlin_group).astype(BF16)

    q_cut, kv_cut = q_width // n_f, 2 * head_size // n_f
    low_mix = jnp.concatenate(
        [grad_qlow.reshape(row_count, n_f, q_cut), grad_kv.reshape(row_count, n_f, kv_cut)], axis=2
    ).reshape(row_count, n_f * (q_cut + kv_cut))
    low_group = lax.all_to_all(low_mix, "fsdp", 1, 0, tiled=True)
    normed_group = group_rows(normed)
    low_part = dot_rows(normed_group, low_group).astype(BF16)
    up_pair = ctx_pair(up_keep, after(up_got, grad_input))

    order = [(c * n_f + f, f * n_ctx + c) for c in range(n_ctx) for f in range(n_f)]
    down_rows = ctx_total(down_parts).astype(BF16)
    grad_down = lax.ppermute(down_rows, ("ctx", "fsdp"), order).astype(F32)
    grad_wgate = rows_to_f(ctx_total(gate_parts)).astype(F32)

    small = jnp.concatenate([grad_gain_one, grad_gain_q, grad_gain_two, sq_local.reshape(1)])
    entries = small.shape[0]
    small = jnp.pad(small, (0, -entries % 1024)).reshape(-1, 128)
    kinds = ((False, True), (True, False), (True, True), (True, True))
    small, grad_wup, grad_wout, grad_wqup, grad_low_w = tail_reduce(
        kinds, n_ctx, n_f, small, (up_pair, by_ctx(out_part), by_ctx(qup_part), by_ctx(low_part))
    )
    small = small.reshape(-1)[:entries]
    grad_low_w = grad_low_w.reshape(-1, n_f, q_cut + kv_cut)
    grad_wqdown = grad_low_w[:, :, :q_cut].reshape(-1, q_width)
    grad_wkv = grad_low_w[:, :, q_cut:].reshape(-1, 2 * head_size)

    device = c_idx * n_f + f_idx
    q1, q2 = model_width, model_width + q_width
    n_dev = n_ctx * n_f

    def own_part(values):
        size = values.shape[0] // n_dev
        return cut(values, device * size, size, 0)

    loss_now = small[-1] / (model_width * total_count)
    return (
        result.astype(BF16),
        loss_now,
        grad_input,
        own_part(small[:q1]),
        grad_wqdown,
        own_part(small[q1:q2]),
        grad_wqup,
        grad_wkv,
        grad_wout,
        own_part(small[q2 : q2 + model_width]),
        grad_wgate,
        grad_wup,
        grad_down,
    )


def solution(mesh):
    both = ("ctx", "fsdp")
    rows = P(both, None)
    flat = P(both)
    shard = P("fsdp", None)
    gain = P("fsdp")
    return jax.shard_map(
        body,
        mesh=mesh,
        in_specs=(
            rows,
            rows,
            flat,
            flat,
            flat,
            gain,
            shard,
            gain,
            shard,
            shard,
            shard,
            gain,
            shard,
            shard,
            shard,
        ),
        out_specs=(
            rows,
            P(),
            rows,
            flat,
            rows,
            flat,
            rows,
            rows,
            rows,
            flat,
            rows,
            rows,
            rows,
        ),
        check_vma=False,
    )
```

```python
import functools
import math

import jax
import jax.numpy as jnp
from jax import lax
from jax.experimental import pallas as pl
from jax.experimental.pallas import tpu as pltpu
from jax.sharding import PartitionSpec as P

PIECE = 128
SEQ_BLOCKS = 8
NORM_EPS = 1e-05
F32 = jnp.float32
BF16 = jnp.bfloat16
LOG2E = math.log2(math.e)
HEAD_GROUP = 4


def rms_scale(values):
    return lax.rsqrt(jnp.mean(values * values, axis=-1, keepdims=True) + NORM_EPS)


def rms_back(values, scale, gain, grad):
    grad_gain = jnp.sum(grad * values * scale, axis=0)
    ge = gain * grad
    inner = jnp.mean(ge * values, axis=-1, keepdims=True)
    return scale * ge - values * (scale * scale * scale) * inner, grad_gain


def rope_apply(values, cosine, sine):
    half_dim = values.shape[-1] // 2
    one = values[..., :half_dim]
    two = values[..., half_dim:]
    return jnp.concatenate([one * cosine - two * sine, two * cosine + one * sine], axis=-1)


def rope_back(grads, cosine, sine):
    half_dim = grads.shape[-1] // 2
    one = grads[..., :half_dim]
    two = grads[..., half_dim:]
    return jnp.concatenate([one * cosine + two * sine, two * cosine - one * sine], axis=-1)


def after(values, *deps):
    return lax.optimization_barrier((values, deps))[0]


def dot(a, b):
    return jnp.dot(a, b, preferred_element_type=F32)


def dot_t(a, b):
    return lax.dot_general(a, b, (((1,), (1,)), ((), ())), preferred_element_type=F32)


def dot_rows(a, b):
    return lax.dot_general(a, b, (((0,), (0,)), ((), ())), preferred_element_type=F32)


def contract_last(a, b):
    return lax.dot_general(a, b, (((1,), (1,)), ((), ())), preferred_element_type=F32)

def find_pieces(tags_ref, own_ref, pick_ref, total):
    @pl.loop(0, total)
    def _(u):
        @pl.when(tags_ref[u, 1] == own_ref[2])
        def _():
            pick_ref[tags_ref[u, 0]] = u

def stack_heads(ref, hd):
    return jnp.concatenate([ref[:, h*hd:(h+1)*hd] for h in range(HEAD_GROUP)], axis=0)

def attn_fwd_kernel(tags_ref, own_ref, q_ref, kv_ref, o_ref, lse_ref, k_s, vt_s, acc_s, pick_s):
    half = pl.program_id(0)
    hd = k_s.shape[1]
    pieces = k_s.shape[0] // PIECE
    total = kv_ref.shape[0] // PIECE
    wide = 2 * PIECE
    coef = hd ** -0.5 * LOG2E

    @pl.when((half == 0) & (pl.program_id(1) == 0))
    def _():
        find_pieces(tags_ref, own_ref, pick_s, total)
        for i in range(pieces):
            rows = pl.ds(pl.multiple_of(pick_s[i] * PIECE, PIECE), PIECE)
            k_s[i*PIECE:(i+1)*PIECE, :] = kv_ref[rows, :hd]
            vt_s[:, i*PIECE:(i+1)*PIECE] = kv_ref[rows, hd:].T

    q = stack_heads(q_ref, hd)
    acc_s[...] = jnp.zeros_like(acc_s)
    rows = q.shape[0]
    def step(i, carry):
        peak, total_p = carry
        at = pl.ds(pl.multiple_of(i * wide, wide), wide)
        raw = contract_last(k_s[at, :], q)
        top = jnp.maximum(peak, jnp.max(raw, axis=0, keepdims=True))
        fade = jnp.exp2((peak - top) * coef)
        p = jnp.exp2((raw - top) * coef)
        acc_s[...] = acc_s[...] * fade + jnp.dot(vt_s[:, at], p.astype(BF16), preferred_element_type=F32)
        return top, total_p * fade + jnp.sum(p, axis=0, keepdims=True)
    count = own_ref[half] // 2 + 1
    peak, total_p = lax.fori_loop(0, count, step, (jnp.full((1, rows), -1e30, F32), jnp.zeros((1, rows), F32)))
    out = (acc_s[...] / total_p).astype(BF16).T
    for h in range(HEAD_GROUP):
        o_ref[:, h*hd:(h+1)*hd] = out[h*PIECE:(h+1)*PIECE, :]
    lse_ref[0] = peak * coef + jnp.log2(total_p)

def attn_fwd(tags, own, q, kv, hd, pieces):
    n_rows, width = q.shape
    groups = width // hd // HEAD_GROUP
    gw = HEAD_GROUP * hd
    halves = n_rows // PIECE
    rows = HEAD_GROUP * PIECE
    blk = pl.BlockSpec((PIECE, gw), lambda p, g, *_: (p, g))
    flops = 4 * n_rows * width * pieces * PIECE * 9 // 16
    return pl.pallas_call(
        attn_fwd_kernel,
        out_shape=(jax.ShapeDtypeStruct(q.shape, BF16), jax.ShapeDtypeStruct((halves*groups, 1, rows), F32)),
        grid_spec=pltpu.PrefetchScalarGridSpec(
            num_scalar_prefetch=2, grid=(halves, groups),
            in_specs=[blk, pl.BlockSpec(kv.shape, lambda p, g, *_: (0, 0))],
            out_specs=[blk, pl.BlockSpec((1, 1, rows), lambda p, g, *_: (p*groups+g, 0, 0))],
            scratch_shapes=[pltpu.VMEM((pieces*PIECE, hd), BF16), pltpu.VMEM((hd, pieces*PIECE), BF16),
                            pltpu.VMEM((hd, rows), F32), pltpu.SMEM((pieces,), jnp.int32)]),
        compiler_params=pltpu.CompilerParams(vmem_limit_bytes=40 << 20),
        cost_estimate=pl.CostEstimate(flops=flops, transcendentals=flops//(4*hd), bytes_accessed=2*(2*q.size+kv.size)),
        name="attn_fwd",
    )(tags, own, q, kv)

def attn_bwd_kernel(tags_ref, own_ref, q_ref, do_ref, o_ref, lse_ref, cos_ref, sin_ref, kv_ref, dq_ref, dkv_ref,
                    k_s, kt_s, v_s, dq_s, dk_s, dv_s, pick_s):
    half = pl.program_id(0)
    group = pl.program_id(1)
    hd = k_s.shape[1]
    pieces = k_s.shape[0] // PIECE
    total = kv_ref.shape[0] // PIECE
    wide = 2 * PIECE
    coef = hd ** -0.5 * LOG2E
    scale = hd ** -0.5

    @pl.when((half == 0) & (group == 0))
    def _():
        find_pieces(tags_ref, own_ref, pick_s, total)
        for i in range(pieces):
            rows = pl.ds(pl.multiple_of(pick_s[i] * PIECE, PIECE), PIECE)
            keys = kv_ref[rows, :hd]
            k_s[i*PIECE:(i+1)*PIECE, :] = keys
            kt_s[:, i*PIECE:(i+1)*PIECE] = keys.T
            v_s[i*PIECE:(i+1)*PIECE, :] = kv_ref[rows, hd:]
        dk_s[...] = jnp.zeros_like(dk_s)
        dv_s[...] = jnp.zeros_like(dv_s)

    q = stack_heads(q_ref, hd)
    do = stack_heads(do_ref, hd)
    prod = do.astype(F32) * stack_heads(o_ref, hd).astype(F32)
    delta = lax.dot_general(jnp.ones((8, hd), F32), prod, (((1,), (1,)), ((), ())),
                            preferred_element_type=F32, precision=lax.Precision.HIGHEST)[:1]
    lse = lse_ref[0]
    dq_s[...] = jnp.zeros_like(dq_s)
    def step(i, carry):
        at = pl.ds(pl.multiple_of(i * wide, wide), wide)
        p = jnp.exp2(contract_last(k_s[at, :], q) * coef - lse)
        dp = contract_last(v_s[at, :], do)
        ds = (p * (dp - delta)).astype(BF16)
        dv_s[at, :] += jnp.dot(p.astype(BF16), do, preferred_element_type=F32)
        dk_s[at, :] += jnp.dot(ds, q, preferred_element_type=F32)
        dq_s[...] += jnp.dot(kt_s[:, at], ds, preferred_element_type=F32)
        return carry
    lax.fori_loop(0, own_ref[half] // 2 + 1, step, 0)
    dq = (dq_s[...] * scale).T
    cos, sin = cos_ref[...], sin_ref[...]
    mid = hd // 2
    for h in range(HEAD_GROUP):
        one = dq[h*PIECE:(h+1)*PIECE, :mid]
        two = dq[h*PIECE:(h+1)*PIECE, mid:]
        dq_ref[:, h*hd:h*hd+mid] = (one * cos + two * sin).astype(BF16)
        dq_ref[:, h*hd+mid:(h+1)*hd] = (two * cos - one * sin).astype(BF16)

    @pl.when((half == pl.num_programs(0) - 1) & (group == pl.num_programs(1) - 1))
    def _():
        dkv_ref[:, :hd] = (dk_s[...] * scale).astype(BF16)
        dkv_ref[:, hd:] = dv_s[...].astype(BF16)

def attn_bwd(tags, own, q, do, o, lse, cos, sin, kv, hd, pieces):
    n_rows, width = q.shape
    groups = width // hd // HEAD_GROUP
    gw = HEAD_GROUP * hd
    halves = n_rows // PIECE
    rows = HEAD_GROUP * PIECE
    blk = pl.BlockSpec((PIECE, gw), lambda p, g, *_: (p, g))
    trig = pl.BlockSpec((PIECE, hd // 2), lambda p, g, *_: (p, 0))
    keys = pieces * PIECE
    flops = 10 * n_rows * width * keys * 9 // 16
    return pl.pallas_call(
        attn_bwd_kernel,
        out_shape=(jax.ShapeDtypeStruct(q.shape, BF16), jax.ShapeDtypeStruct((keys, 2*hd), BF16)),
        grid_spec=pltpu.PrefetchScalarGridSpec(
            num_scalar_prefetch=2, grid=(halves, groups),
            in_specs=[blk, blk, blk, pl.BlockSpec((1, 1, rows), lambda p, g, *_: (p*groups+g, 0, 0)), trig, trig,
                      pl.BlockSpec(kv.shape, lambda p, g, *_: (0, 0))],
            out_specs=[blk, pl.BlockSpec((keys, 2*hd), lambda p, g, *_: (0, 0))],
            scratch_shapes=[pltpu.VMEM((keys, hd), BF16), pltpu.VMEM((hd, keys), BF16), pltpu.VMEM((keys, hd), BF16),
                            pltpu.VMEM((hd, rows), F32), pltpu.VMEM((keys, hd), F32), pltpu.VMEM((keys, hd), F32),
                            pltpu.SMEM((pieces,), jnp.int32)]),
        compiler_params=pltpu.CompilerParams(vmem_limit_bytes=48 << 20),
        cost_estimate=pl.CostEstimate(flops=flops, transcendentals=flops//(10*hd), bytes_accessed=2*(4*q.size+2*kv.size)),
        name="attn_bwd",
    )(tags, own, q, do, o, lse, cos, sin, kv)

MESH = pl.DeviceIdType.MESH


def flip(index, mask):
    out = 0
    bit = 1
    while bit <= mask:
        part = (index // bit) % 2
        out = out + bit * ((1 - part) if mask & bit else part)
        bit *= 2
    return out + (index // bit) * bit


def row_loop(rows, body):
    step = 32 if rows % 32 == 0 else 16

    @pl.loop(0, rows // step)
    def _(i):
        body(pl.ds(pl.multiple_of(i * step, step), step))


def tail_kernel(kinds, n_ctx, n_f, *refs):
    count = len(kinds)
    n_z = n_ctx // 2
    refs = list(refs)
    small_ref = refs.pop(0)
    ins = [refs.pop(0) for _ in range(count)]
    small_out = refs.pop(0)
    outs = [refs.pop(0) for _ in range(count)]
    small_got = refs.pop(0)
    y_got, pairs, z_got, totals, f_got = [], [], [], [], []
    for needs_y, cut_f in kinds:
        y_got.append(refs.pop(0) if needs_y else None)
        pairs.append(refs.pop(0) if needs_y else None)
        z_got.append(refs.pop(0))
        totals.append(refs.pop(0) if cut_f else None)
        f_got.append(refs.pop(0) if cut_f else None)
    s_send, s_recv, y_send, y_recv, z_send, z_recv, f_send, f_recv = refs
    c_idx = lax.axis_index("ctx")
    f_idx = lax.axis_index("fsdp")
    y_idx = c_idx % 2
    z_idx = c_idx // 2

    def over_c(mask):
        return (flip(c_idx, mask), f_idx)

    def over_f(mask):
        return (c_idx, flip(f_idx, mask))

    peers = [over_f(m) for m in range(1, n_f)] + [over_c(1)]
    peers += [over_c(2 * r) for r in range(1, n_z)]
    barrier = pltpu.get_barrier_semaphore()
    for peer in peers:
        pl.semaphore_signal(barrier, inc=1, device_id=peer, device_id_type=MESH)
    pl.semaphore_wait(barrier, len(peers))
    started = []

    def send(src, dst, send_sem, recv_sem, peer):
        copy = pltpu.make_async_remote_copy(
            src_ref=src,
            dst_ref=dst,
            send_sem=send_sem,
            recv_sem=recv_sem,
            device_id=peer,
            device_id_type=MESH,
        )
        copy.start()
        started.append(copy)
        return copy

    steps = [over_f(1), over_f(2), over_c(1)]
    mask = 2
    while mask < n_ctx:
        steps.append(over_c(mask))
        mask *= 2
    y_copies = {}
    z_copies = {}

    def send_z(m, src, r):
        z_copies[m, r] = send(
            src.at[flip(z_idx, r)],
            z_got[m].at[r - 1],
            z_send.at[m, r - 1],
            z_recv.at[m, r - 1],
            over_c(2 * r),
        )

    order = list(range(1, n_z)) + [0]
    small_out[...] = small_ref[...]
    for s, peer in enumerate(steps):
        small_got[s, 0] = small_out[...]
        send(small_got.at[s, 0], small_got.at[s, 1], s_send.at[s], s_recv.at[s], peer).wait_recv()
        small_out[...] = small_out[...] + small_got[s, 1]
        if s == 2:
            for m, (needs_y, _) in enumerate(kinds):
                if needs_y:
                    for r in order:
                        b = flip(z_idx, r)
                        y_copies[m, r] = send(
                            ins[m].at[b, 1 - y_idx],
                            y_got[m].at[r],
                            y_send.at[m, r],
                            y_recv.at[m, r],
                            over_c(1),
                        )
    for m, (needs_y, _) in enumerate(kinds):
        if not needs_y:
            for r in range(1, n_z):
                send_z(m, ins[m], r)
    for m, (needs_y, _) in enumerate(kinds):
        if needs_y:
            for r in order:
                b = flip(z_idx, r)
                y_copies[m, r].wait_recv()

                def add_pair(at, m=m, r=r, b=b):
                    pairs[m][b, at, :] = (
                        ins[m][b, y_idx, at, :].astype(F32) + y_got[m][r, at, :].astype(F32)
                    ).astype(BF16)

                row_loop(pairs[m].shape[1], add_pair)
                if r:
                    send_z(m, pairs[m], r)
    f_copies = {}
    for m, (needs_y, cut_f) in enumerate(kinds):
        own = pairs[m] if needs_y else ins[m]
        for r in range(1, n_z):
            z_copies[m, r].wait_recv()
        rows = own.shape[1]

        def add_all(at, m=m, own=own, cut_f=cut_f):
            total = own[z_idx, at, :].astype(F32)
            for r in range(1, n_z):
                total = total + z_got[m][r - 1, at, :].astype(F32)
            if cut_f:
                totals[m][at, :] = total.astype(BF16)
            else:
                outs[m][at, :] = total

        row_loop(rows, add_all)
        if cut_f:
            part = rows // n_f
            for r in range(1, n_f):
                f_copies[m, r] = send(
                    totals[m].at[pl.ds(pl.multiple_of(flip(f_idx, r) * part, part), part), :],
                    f_got[m].at[r - 1],
                    f_send.at[m, r - 1],
                    f_recv.at[m, r - 1],
                    over_f(r),
                )
    for m, (_, cut_f) in enumerate(kinds):
        if cut_f:
            rows, width = totals[m].shape
            part = rows // n_f
            for r in range(n_f):
                if r:
                    f_copies[m, r].wait_recv()
                at = pl.ds(pl.multiple_of(flip(f_idx, r) * width, 128), width)
                if r:
                    outs[m][:, at] = f_got[m][r - 1].astype(F32)
                else:
                    mine = pl.ds(pl.multiple_of(f_idx * part, part), part)
                    outs[m][:, at] = totals[m][mine, :].astype(F32)
    for copy in started:
        copy.wait_send()


def tail_reduce(kinds, n_ctx, n_f, small, mats):
    n_z = n_ctx // 2
    steps = 2 + (n_ctx.bit_length() - 1)
    outs = [jax.ShapeDtypeStruct(small.shape, F32)]
    scratch = [pltpu.VMEM((steps, 2) + small.shape, F32)]
    for (needs_y, cut_f), mat in zip(kinds, mats):
        rows, width = mat.shape[-2:]
        if needs_y:
            scratch += [pltpu.VMEM((n_z, rows, width), BF16)] * 2
        scratch.append(pltpu.VMEM((n_z - 1, rows, width), BF16))
        if cut_f:
            scratch.append(pltpu.VMEM((rows, width), BF16))
            scratch.append(pltpu.VMEM((n_f - 1, rows // n_f, width), BF16))
            outs.append(jax.ShapeDtypeStruct((rows // n_f, width * n_f), F32))
        else:
            outs.append(jax.ShapeDtypeStruct((rows, width), F32))
    count = len(kinds)
    dma = pltpu.SemaphoreType.DMA
    scratch += [dma((steps,))] * 2 + [dma((count, n_z))] * 4 + [dma((count, n_f))] * 2
    vmem = pl.BlockSpec(memory_space=pltpu.VMEM)
    return pl.pallas_call(
        functools.partial(tail_kernel, kinds, n_ctx, n_f),
        out_shape=tuple(outs),
        in_specs=[vmem] * (1 + count),
        out_specs=tuple([vmem] * (1 + count)),
        scratch_shapes=scratch,
        compiler_params=pltpu.CompilerParams(
            collective_id=0, has_side_effects=True, vmem_limit_bytes=48 << 20
        ),
        name="tail_reduce",
    )(small, *mats)


def body(
    hidden_in,
    teacher,
    blocks,
    seq_ids,
    valid_mask,
    norm1_gain,
    q_down,
    q_gain,
    q_up,
    kv_weight,
    out_proj,
    norm2_gain,
    w_gate,
    w_up,
    w_down,
):
    row_count, model_width = hidden_in.shape
    head_size = kv_weight.shape[1] // 2
    heads_width = q_up.shape[1]
    head_count = heads_width // head_size
    half_dim = head_size // 2
    q_width = q_down.shape[1]
    n_ctx = lax.axis_size("ctx")
    n_f = lax.axis_size("fsdp")
    n_z = n_ctx // 2
    token_total = row_count * n_ctx * n_f
    seq_pieces = 2 * SEQ_BLOCKS
    c_idx = lax.axis_index("ctx")
    f_idx = lax.axis_index("fsdp")
    y_idx = c_idx % 2
    z_idx = c_idx // 2
    x_idx = f_idx // 2
    k_idx = f_idx % 2

    def by_f(values, mask):
        return lax.ppermute(values, "fsdp", [(i, i ^ mask) for i in range(n_f)])

    def by_c(values, mask):
        return lax.ppermute(values, "ctx", [(i, i ^ mask) for i in range(n_ctx)])

    def cut(values, start, size, axis):
        return lax.dynamic_slice_in_dim(values, start, size, axis)

    def gather_bit(values, got, bit):
        return jnp.concatenate(
            [jnp.where(bit == 0, values, got), jnp.where(bit == 0, got, values)], axis=0
        )

    def fetch_far(shard, mask, gate):
        half = shard.shape[0] // 2
        bit = (c_idx // mask) % 2
        return by_f(after(cut(shard, bit * half, half, 0), *gate), 2)

    def fetch_rest(shard, far, mask):
        rows = shard.shape[0]
        half = rows // 2
        bit = (c_idx // mask) % 2
        core = by_f(shard, 1)
        far_y = by_c(far, mask)
        far_core = by_f(far, 1)
        far_y_core = by_f(far_y, 1)
        mine, other = bit * half, (1 - bit) * half
        return [
            (shard, f_idx * rows),
            (core, (f_idx ^ 1) * rows),
            (far, (f_idx ^ 2) * rows + mine),
            (far_core, (f_idx ^ 3) * rows + mine),
            (far_y, (f_idx ^ 2) * rows + other),
            (far_y_core, (f_idx ^ 3) * rows + other),
        ]

    def mul_pieces(acts, pieces):
        total = None
        for weight, start in pieces:
            term = dot(cut(acts, start, weight.shape[0], 1), weight)
            total = term if total is None else total + term
        return total

    def mul_pieces_t(grads, pieces, dtype):
        width = sum(weight.shape[0] for weight, _ in pieces)
        out = jnp.zeros((grads.shape[0], width), dtype)
        for weight, start in pieces:
            out = lax.dynamic_update_slice_in_dim(out, dot_t(grads, weight).astype(dtype), start, 1)
        return out

    def columns_far(shard, gate):
        rows, columns = shard.shape
        width = columns // n_f
        half = rows // 2
        far_cut = lax.dynamic_slice(
            shard, (y_idx * half, (1 - x_idx) * 2 * width), (half, 2 * width)
        )
        return by_f(after(far_cut, *gate), 2)

    def columns_rest(shard, far):
        rows, columns = shard.shape
        width = columns // n_f
        half = rows // 2
        core = by_f(cut(shard, (f_idx ^ 1) * width, width, 1), 1)
        far_y = by_c(far, 1)
        far_core = by_f(cut(far, (1 - k_idx) * width, width, 1), 1)
        far_y_core = by_f(cut(far_y, (1 - k_idx) * width, width, 1), 1)
        mine, other = y_idx * half, (1 - y_idx) * half
        out = jnp.zeros((rows * n_f, width), shard.dtype)
        for piece, start in (
            (cut(shard, f_idx * width, width, 1), f_idx * rows),
            (core, (f_idx ^ 1) * rows),
            (cut(far, k_idx * width, width, 1), (f_idx ^ 2) * rows + mine),
            (far_core, (f_idx ^ 3) * rows + mine),
            (cut(far_y, k_idx * width, width, 1), (f_idx ^ 2) * rows + other),
            (far_y_core, (f_idx ^ 3) * rows + other),
        ):
            out = lax.dynamic_update_slice_in_dim(out, piece, start, 0)
        return out

    def gather_tokens(values):
        core = by_f(values, 1)
        far = by_f(values, 2)
        far_core = by_f(far, 1)
        return jnp.concatenate([values, core, far, far_core], axis=0)

    def sum_tokens(make_half, between=None):
        far = make_half(1).reshape(2, row_count, -1)
        far = (far[0] + by_f(far[1], 1)).astype(BF16)
        far = by_f(far, 2)
        near = make_half(0).reshape(2, row_count, -1)
        near = near[0] + by_f(near[1], 1)
        if between is not None:
            far = after(far, between(near))
        return near + far.astype(F32)

    def ctx_split(grad):
        view = grad.reshape(n_z, 2, grad.shape[0] // n_ctx, grad.shape[1])
        give = lax.dynamic_index_in_dim(view, 1 - y_idx, 1, keepdims=False)
        keep = lax.dynamic_index_in_dim(view, y_idx, 1, keepdims=False)
        return give, keep

    def ctx_pair(keep, got):
        return (keep.astype(F32) + got.astype(F32)).astype(BF16)

    def ctx_spread(pair):
        return [pair] + [
            by_c(lax.dynamic_index_in_dim(pair, z_idx ^ r, 0, keepdims=False), 2 * r)
            for r in range(1, n_z)
        ]

    def ctx_total(parts):
        total = lax.dynamic_index_in_dim(parts[0], z_idx, 0, keepdims=False).astype(F32)
        for got in parts[1:]:
            total = total + got.astype(F32)
        return total

    def group_rows(values):
        return lax.all_gather(values, "fsdp", axis=0, tiled=True)

    def rows_to_f(values):
        return lax.all_to_all(values.astype(BF16), "fsdp", 0, 1, tiled=True)

    valid_f = valid_mask.astype(F32)
    d1, d2 = norm1_gain.shape[0], q_gain.shape[0]
    qkv_shard = jnp.concatenate([q_down, kv_weight], axis=1)
    qkv_far = fetch_far(qkv_shard, 1, ())
    info = jnp.concatenate(
        [
            norm1_gain.astype(F32),
            q_gain.astype(F32),
            norm2_gain.astype(F32),
            jnp.full((128,), jnp.sum(valid_f)),
        ]
    ).reshape(1, -1)
    info = gather_bit(info, by_f(info, 1), k_idx)
    info = gather_bit(info, by_f(info, 2), x_idx)
    gain_one = info[:, :d1].reshape(-1)
    gain_q = info[:, d1 : d1 + d2].reshape(-1)
    gain_two = info[:, d1 + d2 : 2 * d1 + d2].reshape(-1)
    tag_row = jnp.concatenate(
        [
            jnp.stack([blocks.reshape(-1, PIECE)[:, 0], seq_ids.reshape(-1, PIECE)[:, 0]], axis=1)
            .astype(F32)
            .reshape(-1),
            jnp.sum(info[:, 2 * d1 + d2]).reshape(1),
        ]
    )
    tag_row = jnp.pad(tag_row, (0, 128 - tag_row.shape[0])).reshape(1, 128)
    mask = 1
    while mask < n_ctx:
        tag_row = gather_bit(tag_row, by_c(tag_row, mask), (c_idx // mask) % 2)
        mask *= 2
    own_pieces = row_count // PIECE
    tags = tag_row[:, : 2 * own_pieces].reshape(-1, 2).astype(jnp.int32)
    total_count = jnp.sum(tag_row[:, 2 * own_pieces])
    own = jnp.concatenate([blocks.reshape(-1, PIECE)[:, 0], seq_ids[:1]])

    up_far = fetch_far(q_up, 2, (info,))
    out_far = fetch_far(out_proj, 2, (qkv_far,))
    gate_far = columns_far(w_gate, (up_far,))
    upw_far = columns_far(w_up, (out_far,))
    qkv_pieces = fetch_rest(qkv_shard, qkv_far, 1)
    up_pieces = fetch_rest(q_up, up_far, 2)
    out_pieces = fetch_rest(out_proj, out_far, 2)
    w_gatef = columns_rest(w_gate, gate_far)
    w_upf = columns_rest(w_up, upw_far)

    positions = blocks * PIECE + jnp.arange(row_count, dtype=jnp.int32) % PIECE
    freq_table = 10000.0 ** (-(jnp.arange(half_dim, dtype=F32) * 2.0 / head_size))
    angle_table = positions.astype(F32)[:, None] * freq_table[None, :]
    cosine = jnp.cos(angle_table)
    sine = jnp.sin(angle_table)
    hidden_f = hidden_in.astype(F32)
    scale_one = rms_scale(hidden_f)
    normed = (hidden_f * scale_one * gain_one).astype(BF16)
    low_all = mul_pieces(normed, qkv_pieces)
    q_low = low_all[:, :q_width]
    kv_lin = low_all[:, q_width:]
    key_rot = rope_apply(kv_lin[:, :head_size], cosine, sine).astype(BF16)
    kv_rows = jnp.concatenate([key_rot, kv_lin[:, head_size:].astype(BF16)], axis=1)
    all_kv = lax.all_gather(kv_rows, "ctx", axis=0, tiled=True)
    scale_q = rms_scale(q_low)
    q_normed = (q_low * scale_q * gain_q).astype(BF16)
    q_lin = mul_pieces(q_normed, up_pieces).reshape(row_count, head_count, head_size)
    q_rot = rope_apply(q_lin, cosine[:, None, :], sine[:, None, :]).astype(BF16)
    q_rot = q_rot.reshape(row_count, heads_width)

    attn_heads, lse = attn_fwd(tags, own, q_rot, all_kv, head_size, seq_pieces)
    resid = hidden_f + mul_pieces(attn_heads, out_pieces)
    scale_two = rms_scale(resid)
    normed_two = (resid * scale_two * gain_two).astype(BF16)

    group_two = gather_tokens(normed_two)
    gate_lin = dot(group_two, w_gatef)
    up_lin = dot(group_two, w_upf)
    sigma = jax.nn.sigmoid(gate_lin)
    silu_gate = gate_lin * sigma
    hidden_act = (silu_gate * up_lin).astype(BF16)
    side = 2 * row_count

    def down_half(j):
        return dot(hidden_act[j * side : (j + 1) * side], w_down)

    result = resid + sum_tokens(down_half)
    diff = result - teacher.astype(F32)
    sq_local = jnp.sum(valid_f * jnp.sum(diff * diff, axis=1))
    grad_y = diff * valid_f[:, None] * (token_total / total_count)
    group_dz = gather_tokens(grad_y.astype(BF16))
    down_part = dot_rows(hidden_act, group_dz).astype(BF16)
    down_give, down_keep = ctx_split(down_part)
    down_got = by_c(down_give, 1)
    group_dz2 = after(group_dz, down_part)
    grad_hidden = dot_t(group_dz2, w_down)
    grad_gate = (grad_hidden * up_lin * sigma * (1.0 + gate_lin * (1.0 - sigma))).astype(BF16)
    grad_up = (grad_hidden * silu_gate).astype(BF16)
    gate_part = dot_rows(group_two, grad_gate).astype(BF16)
    gate_give, gate_keep = ctx_split(gate_part)
    gate_got = by_c(gate_give, 1)

    def back_half(j):
        rows = slice(j * side, (j + 1) * side)
        return dot_t(grad_gate[rows], w_gatef) + dot_t(grad_up[rows], w_upf)

    kept = {}

    def while_summing(near):
        up_part = dot_rows(group_two, grad_up).astype(BF16)
        kept["up"] = ctx_split(up_part)
        kept["down"] = ctx_pair(down_keep, after(down_got, near, up_part))
        return kept["down"]

    grad_normed_two = sum_tokens(back_half, while_summing)
    up_give, up_keep = kept["up"]
    down_parts = ctx_spread(kept["down"])

    grad_resid_norm, grad_gain_two = rms_back(resid, scale_two, gain_two, grad_normed_two)
    grad_resid = grad_y + grad_resid_norm
    grad_branch = grad_resid.astype(BF16)
    branch_group = group_rows(grad_branch)
    grad_attn = mul_pieces_t(grad_branch, out_pieces, BF16)
    gate_pair = ctx_pair(gate_keep, after(gate_got, grad_attn))
    gate_parts = ctx_spread(gate_pair)

    grad_qlin, grad_seq = attn_bwd(
        tags,
        own,
        q_rot,
        after(grad_attn, gate_pair),
        attn_heads,
        lse,
        cosine,
        sine,
        all_kv,
        head_size,
        seq_pieces,
    )
    by_piece = grad_seq.reshape(seq_pieces, PIECE, 2 * head_size)
    piece_tag = tags[:, 0].reshape(n_z, 2, own_pieces)
    piece_own = (tags[:, 1] == seq_ids[0]).reshape(n_z, 2, own_pieces)

    def kv_half(bit):
        places = lax.dynamic_index_in_dim(piece_tag, bit, 1, keepdims=False).reshape(-1)
        picked = by_piece[places]
        if n_ctx * own_pieces != seq_pieces:
            mine = lax.dynamic_index_in_dim(piece_own, bit, 1, keepdims=False).reshape(-1)
            picked = jnp.where(mine[:, None, None], picked, jnp.zeros_like(picked))
        return picked.reshape(n_z, own_pieces * PIECE, 2 * head_size)

    q_cut, kv_cut = q_width // n_f, 2 * head_size // n_f
    out_block = heads_width // (n_ctx * n_f)
    kv_give, kv_keep = kv_half(1 - y_idx), kv_half(y_idx)
    kv_got = by_c(kv_give, 1)
    up_got = by_c(after(up_give, kv_keep), 1)
    qlin_group = lax.all_to_all(grad_qlin, "fsdp", 1, 0, tiled=True)
    attn_group = lax.all_to_all(
        attn_heads.reshape(row_count, n_ctx, n_f, out_block), "fsdp", 2, 0, tiled=True
    ).reshape(row_count * n_f, n_ctx * out_block)

    grad_qnormed = mul_pieces_t(after(grad_qlin, kv_give), up_pieces, F32)
    grad_qlow_f, grad_gain_q = rms_back(q_low, scale_q, gain_q, grad_qnormed)
    grad_qlow = grad_qlow_f.astype(BF16)
    out_part = dot_rows(attn_group, after(branch_group, grad_qlow)).astype(BF16)
    kv_pair = ctx_pair(kv_keep, after(kv_got, out_part))
    kv_parts = ctx_spread(kv_pair)

    qnorm_group = group_rows(q_normed)
    qup_part = dot_rows(after(qnorm_group, kv_pair), qlin_group).astype(BF16)
    kv_total = ctx_total(after(kv_parts, qup_part))
    grad_klin = rope_back(kv_total[:, :head_size], cosine, sine)
    grad_kv = jnp.concatenate([grad_klin, kv_total[:, head_size:]], axis=1).astype(BF16)
    low_mix = jnp.concatenate(
        [grad_qlow.reshape(row_count, n_f, q_cut), grad_kv.reshape(row_count, n_f, kv_cut)], axis=2
    ).reshape(row_count, n_f * (q_cut + kv_cut))
    low_group = lax.all_to_all(low_mix, "fsdp", 1, 0, tiled=True)
    grad_low = jnp.concatenate([grad_qlow, grad_kv], axis=1)
    grad_normed = mul_pieces_t(grad_low, qkv_pieces, F32)
    grad_input_norm, grad_gain_one = rms_back(hidden_f, scale_one, gain_one, grad_normed)
    grad_input = grad_resid + grad_input_norm
    normed_group = group_rows(normed)
    low_part = dot_rows(normed_group, after(low_group, grad_input)).astype(BF16)
    up_pair = ctx_pair(up_keep, after(up_got, low_part))

    def by_ctx(grad):
        return grad.reshape(n_z, 2, grad.shape[0] // n_ctx, grad.shape[1])

    order = [(c * n_f + f, f * n_ctx + c) for c in range(n_ctx) for f in range(n_f)]
    down_rows = ctx_total(after(down_parts, low_part)).astype(BF16)
    down_sent = lax.ppermute(down_rows, ("ctx", "fsdp"), order)
    gate_sent = rows_to_f(ctx_total(after(gate_parts, low_part)))

    small = jnp.concatenate([grad_gain_one, grad_gain_q, grad_gain_two, sq_local.reshape(1)])
    entries = small.shape[0]
    small = jnp.pad(small, (0, -entries % 1024)).reshape(-1, 128)
    kinds = ((False, True), (True, False), (True, True), (True, True))
    small, grad_wup, grad_wout, grad_wqup, grad_low_w = tail_reduce(
        kinds, n_ctx, n_f, small, (up_pair, by_ctx(out_part), by_ctx(qup_part), by_ctx(low_part))
    )
    down_sent, gate_sent = after((down_sent, gate_sent), small)
    grad_down = down_sent.astype(F32)
    grad_wgate = gate_sent.astype(F32)
    small = small.reshape(-1)[:entries]
    grad_low_w = grad_low_w.reshape(-1, n_f, q_cut + kv_cut)
    grad_wqdown = grad_low_w[:, :, :q_cut].reshape(-1, q_width)
    grad_wkv = grad_low_w[:, :, q_cut:].reshape(-1, 2 * head_size)

    device = c_idx * n_f + f_idx
    q1, q2 = model_width, model_width + q_width
    n_dev = n_ctx * n_f

    def own_part(values):
        size = values.shape[0] // n_dev
        return cut(values, device * size, size, 0)

    loss_now = small[-1] / (model_width * total_count)
    return (
        result.astype(BF16),
        loss_now,
        grad_input,
        own_part(small[:q1]),
        grad_wqdown,
        own_part(small[q1:q2]),
        grad_wqup,
        grad_wkv,
        grad_wout,
        own_part(small[q2 : q2 + model_width]),
        grad_wgate,
        grad_wup,
        grad_down,
    )


def solution(mesh):
    both = ("ctx", "fsdp")
    rows = P(both, None)
    flat = P(both)
    shard = P("fsdp", None)
    gain = P("fsdp")
    return jax.shard_map(
        body,
        mesh=mesh,
        in_specs=(
            rows,
            rows,
            flat,
            flat,
            flat,
            gain,
            shard,
            gain,
            shard,
            shard,
            shard,
            gain,
            shard,
            shard,
            shard,
        ),
        out_specs=(
            rows,
            P(),
            rows,
            flat,
            rows,
            flat,
            rows,
            rows,
            rows,
            flat,
            rows,
            rows,
            rows,
        ),
        check_vma=False,
    )
```

```python
import functools
import math

import jax
import jax.numpy as jnp
from jax import lax
from jax.experimental import pallas as pl
from jax.experimental.pallas import tpu as pltpu
from jax.sharding import PartitionSpec as P

PIECE = 128
SEQ_BLOCKS = 8
NORM_EPS = 1e-05
F32 = jnp.float32
BF16 = jnp.bfloat16
LOG2E = math.log2(math.e)
HEAD_GROUP = 4


def rms_scale(values):
    return lax.rsqrt(jnp.mean(values * values, axis=-1, keepdims=True) + NORM_EPS)


def rms_back(values, scale, gain, grad):
    grad_gain = jnp.sum(grad * values * scale, axis=0)
    ge = gain * grad
    inner = jnp.mean(ge * values, axis=-1, keepdims=True)
    return scale * ge - values * (scale * scale * scale) * inner, grad_gain


def rope_apply(values, cosine, sine):
    half_dim = values.shape[-1] // 2
    one = values[..., :half_dim]
    two = values[..., half_dim:]
    return jnp.concatenate([one * cosine - two * sine, two * cosine + one * sine], axis=-1)


def rope_back(grads, cosine, sine):
    half_dim = grads.shape[-1] // 2
    one = grads[..., :half_dim]
    two = grads[..., half_dim:]
    return jnp.concatenate([one * cosine + two * sine, two * cosine - one * sine], axis=-1)


def after(values, *deps):
    return lax.optimization_barrier((values, deps))[0]


def dot(a, b):
    return jnp.dot(a, b, preferred_element_type=F32)


def dot_t(a, b):
    return lax.dot_general(a, b, (((1,), (1,)), ((), ())), preferred_element_type=F32)


def dot_rows(a, b):
    return lax.dot_general(a, b, (((0,), (0,)), ((), ())), preferred_element_type=F32)


def contract_last(a, b):
    return lax.dot_general(a, b, (((1,), (1,)), ((), ())), preferred_element_type=F32)

def find_pieces(tags_ref, own_ref, pick_ref, total):
    @pl.loop(0, total)
    def _(u):
        @pl.when(tags_ref[u, 1] == own_ref[2])
        def _():
            pick_ref[tags_ref[u, 0]] = u

def stack_heads(ref, hd):
    return jnp.concatenate([ref[:, h*hd:(h+1)*hd] for h in range(HEAD_GROUP)], axis=0)

def attn_fwd_kernel(tags_ref, own_ref, q_ref, kv_ref, o_ref, lse_ref, k_s, vt_s, acc_s, pick_s):
    half = pl.program_id(0)
    hd = k_s.shape[1]
    pieces = k_s.shape[0] // PIECE
    total = kv_ref.shape[0] // PIECE
    wide = 2 * PIECE
    coef = hd ** -0.5 * LOG2E

    @pl.when((half == 0) & (pl.program_id(1) == 0))
    def _():
        find_pieces(tags_ref, own_ref, pick_s, total)
        for i in range(pieces):
            rows = pl.ds(pl.multiple_of(pick_s[i] * PIECE, PIECE), PIECE)
            k_s[i*PIECE:(i+1)*PIECE, :] = kv_ref[rows, :hd]
            vt_s[:, i*PIECE:(i+1)*PIECE] = kv_ref[rows, hd:].T

    q = stack_heads(q_ref, hd)
    acc_s[...] = jnp.zeros_like(acc_s)
    rows = q.shape[0]
    def step(i, carry):
        peak, total_p = carry
        at = pl.ds(pl.multiple_of(i * wide, wide), wide)
        raw = contract_last(k_s[at, :], q)
        top = jnp.maximum(peak, jnp.max(raw, axis=0, keepdims=True))
        fade = jnp.exp2((peak - top) * coef)
        p = jnp.exp2((raw - top) * coef)
        acc_s[...] = acc_s[...] * fade + jnp.dot(vt_s[:, at], p.astype(BF16), preferred_element_type=F32)
        return top, total_p * fade + jnp.sum(p, axis=0, keepdims=True)
    count = own_ref[half] // 2 + 1
    peak, total_p = lax.fori_loop(0, count, step, (jnp.full((1, rows), -1e30, F32), jnp.zeros((1, rows), F32)))
    out = (acc_s[...] / total_p).astype(BF16).T
    for h in range(HEAD_GROUP):
        o_ref[:, h*hd:(h+1)*hd] = out[h*PIECE:(h+1)*PIECE, :]
    lse_ref[0] = peak * coef + jnp.log2(total_p)

def attn_fwd(tags, own, q, kv, hd, pieces):
    n_rows, width = q.shape
    groups = width // hd // HEAD_GROUP
    gw = HEAD_GROUP * hd
    halves = n_rows // PIECE
    rows = HEAD_GROUP * PIECE
    blk = pl.BlockSpec((PIECE, gw), lambda p, g, *_: (p, g))
    flops = 4 * n_rows * width * pieces * PIECE * 9 // 16
    return pl.pallas_call(
        attn_fwd_kernel,
        out_shape=(jax.ShapeDtypeStruct(q.shape, BF16), jax.ShapeDtypeStruct((halves*groups, 1, rows), F32)),
        grid_spec=pltpu.PrefetchScalarGridSpec(
            num_scalar_prefetch=2, grid=(halves, groups),
            in_specs=[blk, pl.BlockSpec(kv.shape, lambda p, g, *_: (0, 0))],
            out_specs=[blk, pl.BlockSpec((1, 1, rows), lambda p, g, *_: (p*groups+g, 0, 0))],
            scratch_shapes=[pltpu.VMEM((pieces*PIECE, hd), BF16), pltpu.VMEM((hd, pieces*PIECE), BF16),
                            pltpu.VMEM((hd, rows), F32), pltpu.SMEM((pieces,), jnp.int32)]),
        compiler_params=pltpu.CompilerParams(vmem_limit_bytes=40 << 20),
        cost_estimate=pl.CostEstimate(flops=flops, transcendentals=flops//(4*hd), bytes_accessed=2*(2*q.size+kv.size)),
        name="attn_fwd",
    )(tags, own, q, kv)

def attn_bwd_kernel(tags_ref, own_ref, q_ref, do_ref, o_ref, lse_ref, cos_ref, sin_ref, kv_ref, dq_ref, dkv_ref,
                    k_s, kt_s, v_s, dq_s, dk_s, dv_s, pick_s):
    half = pl.program_id(0)
    group = pl.program_id(1)
    hd = k_s.shape[1]
    pieces = k_s.shape[0] // PIECE
    total = kv_ref.shape[0] // PIECE
    wide = 2 * PIECE
    coef = hd ** -0.5 * LOG2E
    scale = hd ** -0.5

    @pl.when((half == 0) & (group == 0))
    def _():
        find_pieces(tags_ref, own_ref, pick_s, total)
        for i in range(pieces):
            rows = pl.ds(pl.multiple_of(pick_s[i] * PIECE, PIECE), PIECE)
            keys = kv_ref[rows, :hd]
            k_s[i*PIECE:(i+1)*PIECE, :] = keys
            kt_s[:, i*PIECE:(i+1)*PIECE] = keys.T
            v_s[i*PIECE:(i+1)*PIECE, :] = kv_ref[rows, hd:]
        dk_s[...] = jnp.zeros_like(dk_s)
        dv_s[...] = jnp.zeros_like(dv_s)

    q = stack_heads(q_ref, hd)
    do = stack_heads(do_ref, hd)
    prod = do.astype(F32) * stack_heads(o_ref, hd).astype(F32)
    delta = lax.dot_general(jnp.ones((8, hd), F32), prod, (((1,), (1,)), ((), ())),
                            preferred_element_type=F32, precision=lax.Precision.HIGHEST)[:1]
    lse = lse_ref[0]
    dq_s[...] = jnp.zeros_like(dq_s)
    def step(i, carry):
        at = pl.ds(pl.multiple_of(i * wide, wide), wide)
        p = jnp.exp2(contract_last(k_s[at, :], q) * coef - lse)
        dp = contract_last(v_s[at, :], do)
        ds = (p * (dp - delta)).astype(BF16)
        dv_s[at, :] += jnp.dot(p.astype(BF16), do, preferred_element_type=F32)
        dk_s[at, :] += jnp.dot(ds, q, preferred_element_type=F32)
        dq_s[...] += jnp.dot(kt_s[:, at], ds, preferred_element_type=F32)
        return carry
    lax.fori_loop(0, own_ref[half] // 2 + 1, step, 0)
    dq = (dq_s[...] * scale).T
    cos, sin = cos_ref[...], sin_ref[...]
    mid = hd // 2
    for h in range(HEAD_GROUP):
        one = dq[h*PIECE:(h+1)*PIECE, :mid]
        two = dq[h*PIECE:(h+1)*PIECE, mid:]
        dq_ref[:, h*hd:h*hd+mid] = (one * cos + two * sin).astype(BF16)
        dq_ref[:, h*hd+mid:(h+1)*hd] = (two * cos - one * sin).astype(BF16)

    @pl.when((half == pl.num_programs(0) - 1) & (group == pl.num_programs(1) - 1))
    def _():
        dkv_ref[:, :hd] = (dk_s[...] * scale).astype(BF16)
        dkv_ref[:, hd:] = dv_s[...].astype(BF16)

def attn_bwd(tags, own, q, do, o, lse, cos, sin, kv, hd, pieces):
    n_rows, width = q.shape
    groups = width // hd // HEAD_GROUP
    gw = HEAD_GROUP * hd
    halves = n_rows // PIECE
    rows = HEAD_GROUP * PIECE
    blk = pl.BlockSpec((PIECE, gw), lambda p, g, *_: (p, g))
    trig = pl.BlockSpec((PIECE, hd // 2), lambda p, g, *_: (p, 0))
    keys = pieces * PIECE
    flops = 10 * n_rows * width * keys * 9 // 16
    return pl.pallas_call(
        attn_bwd_kernel,
        out_shape=(jax.ShapeDtypeStruct(q.shape, BF16), jax.ShapeDtypeStruct((keys, 2*hd), BF16)),
        grid_spec=pltpu.PrefetchScalarGridSpec(
            num_scalar_prefetch=2, grid=(halves, groups),
            in_specs=[blk, blk, blk, pl.BlockSpec((1, 1, rows), lambda p, g, *_: (p*groups+g, 0, 0)), trig, trig,
                      pl.BlockSpec(kv.shape, lambda p, g, *_: (0, 0))],
            out_specs=[blk, pl.BlockSpec((keys, 2*hd), lambda p, g, *_: (0, 0))],
            scratch_shapes=[pltpu.VMEM((keys, hd), BF16), pltpu.VMEM((hd, keys), BF16), pltpu.VMEM((keys, hd), BF16),
                            pltpu.VMEM((hd, rows), F32), pltpu.VMEM((keys, hd), F32), pltpu.VMEM((keys, hd), F32),
                            pltpu.SMEM((pieces,), jnp.int32)]),
        compiler_params=pltpu.CompilerParams(vmem_limit_bytes=48 << 20),
        cost_estimate=pl.CostEstimate(flops=flops, transcendentals=flops//(10*hd), bytes_accessed=2*(4*q.size+2*kv.size)),
        name="attn_bwd",
    )(tags, own, q, do, o, lse, cos, sin, kv)

MESH = pl.DeviceIdType.MESH


def flip(index, mask):
    out = 0
    bit = 1
    while bit <= mask:
        part = (index // bit) % 2
        out = out + bit * ((1 - part) if mask & bit else part)
        bit *= 2
    return out + (index // bit) * bit


def row_loop(rows, body, step=32):
    if rows % step:
        step = 16

    @pl.loop(0, rows // step)
    def _(i):
        body(pl.ds(pl.multiple_of(i * step, step), step))


class Sender:
    def __init__(self):
        self.open = []

    def make(self, src, dst, send_sem, recv_sem, peer):
        return pltpu.make_async_remote_copy(
            src_ref=src,
            dst_ref=dst,
            send_sem=send_sem,
            recv_sem=recv_sem,
            device_id=peer,
            device_id_type=MESH,
        )

    def __call__(self, *args):
        copy = self.make(*args)
        copy.start()
        self.open.append(copy)
        return copy

    def finish(self):
        for copy in self.open:
            copy.wait_send()


class LineSum:
    def __init__(self, own, got, send_sem, recv_sem, c_idx, f_idx, n_z, sender):
        self.own, self.got, self.send_sem, self.recv_sem = own, got, send_sem, recv_sem
        self.n_z, self.sender = n_z, sender
        self.z = c_idx // 2
        self.left = (c_idx - 2, f_idx)
        self.right = (c_idx + 2, f_idx)

    def copy(self, b, slot, peer):
        return self.sender.make(
            self.own.at[b], self.got.at[slot], self.send_sem.at[b], self.recv_sem.at[slot], peer
        )

    def take(self, b, slot):
        self.copy(b, slot, self.left).wait_recv()

        def add(at):
            self.own[b, at, :] = (
                self.own[b, at, :].astype(F32) + self.got[slot, at, :].astype(F32)
            ).astype(BF16)

        row_loop(self.own.shape[1], add)

    def run(self):
        z, n_z = self.z, self.n_z
        for step in range(n_z - 1):
            up, down = n_z - 1 - step, step

            @pl.when(z < up)
            def _(b=up):
                @pl.when(z > 0)
                def _():
                    self.take(b, b)

                self.copy(b, b, self.right).start()

            @pl.when(z > down)
            def _(b=down):
                @pl.when(z < n_z - 1)
                def _():
                    self.take(b, b)

                @pl.when(z - 1 > b)
                def _():
                    self.copy(b, b, self.left).start()

                @pl.when(z - 1 == b)
                def _():
                    self.copy(b, n_z, self.left).start()

    def total(self, store):
        z, n_z = self.z, self.n_z

        @pl.when(z > 0)
        def _():
            self.copy(z, z, self.left).wait_recv()

        @pl.when(z < n_z - 1)
        def _():
            self.copy(z, n_z, self.left).wait_recv()

        rows = self.own.shape[1]

        @pl.when(z == 0)
        def _():
            row_loop(
                rows,
                lambda at: store(
                    at, self.own[z, at, :].astype(F32) + self.got[n_z, at, :].astype(F32)
                ),
            )

        @pl.when(z == n_z - 1)
        def _():
            row_loop(
                rows,
                lambda at: store(
                    at, self.own[z, at, :].astype(F32) + self.got[z, at, :].astype(F32)
                ),
            )

        @pl.when((z > 0) & (z < n_z - 1))
        def _():
            row_loop(
                rows,
                lambda at: store(
                    at,
                    self.own[z, at, :].astype(F32)
                    + self.got[z, at, :].astype(F32)
                    + self.got[n_z, at, :].astype(F32),
                ),
            )

    def finish(self):
        for b in range(self.n_z):

            @pl.when(self.z != b)
            def _(b=b):
                self.copy(b, b, self.left).wait_send()


TAIL_NAMES = ("gate", "kv", "up", "out", "qup", "qd", "kvw")
TAIL_CUT = ("gate", "up", "qup", "qd", "kvw")
TAIL_SENT = ("kv", "up", "out", "qup", "qd", "kvw")


def tail_kernel(n_ctx, n_f, names_in, names_out, names_scratch, *refs):
    n_z = n_ctx // 2
    names = list(names_in) + list(names_out) + list(names_scratch)
    r = dict(zip(names, refs, strict=True))
    c_idx = lax.axis_index("ctx")
    f_idx = lax.axis_index("fsdp")
    y_idx = c_idx % 2
    z_idx = c_idx // 2
    send = Sender()

    def over_c(mask):
        return (flip(c_idx, mask), f_idx)

    def over_f(mask):
        return (c_idx, flip(f_idx, mask))

    barrier = pltpu.get_barrier_semaphore()
    for mask in range(1, n_f):
        pl.semaphore_signal(barrier, inc=1, device_id=over_f(mask), device_id_type=MESH)
    for mask in range(1, n_ctx):
        pl.semaphore_signal(barrier, inc=1, device_id=over_c(mask), device_id_type=MESH)
    pl.semaphore_wait(barrier, n_f - 1 + n_ctx - 1)

    lines = {
        m: LineSum(
            r["pair_" + m],
            r["z_" + m],
            r["z_send"].at[i],
            r["z_recv"].at[i],
            c_idx,
            f_idx,
            n_z,
            send,
        )
        for i, m in enumerate(TAIL_NAMES)
    }
    order = list(range(1, n_z)) + [0]
    y_copies, keeps = {}, {}

    def start_y(m, part):
        i = TAIL_SENT.index(m)
        for s in order:
            b = flip(z_idx, s)
            y_copies[m, s] = send(
                part.at[b, 1 - y_idx],
                r["y_" + m].at[s],
                r["y_send"].at[i, s],
                r["y_recv"].at[i, s],
                over_c(1),
            )
        for s in order:
            b = flip(z_idx, s)
            keep = pltpu.make_async_copy(
                part.at[b, y_idx], r["pair_" + m].at[b], r["keep_sem"].at[i, s]
            )
            keep.start()
            keeps[m, s] = keep

    def add_pairs(m):
        for s in order:
            b = flip(z_idx, s)
            keeps[m, s].wait()
            y_copies[m, s].wait_recv()
            pair, got = r["pair_" + m], r["y_" + m]

            def add(at, s=s, b=b, pair=pair, got=got):
                pair[b, at, :] = (
                    pair[b, at, :].astype(F32) + got[s, at, :].astype(F32)
                ).astype(BF16)

            row_loop(pair.shape[1], add)

    f_copies = {}

    def finish_sum(m):
        lines[m].total(lambda at, value: store_total(m, at, value))
        if m in TAIL_CUT:
            i = TAIL_CUT.index(m)
            part = r["tot_" + m].shape[0] // n_f
            for s in range(1, n_f):
                at = pl.ds(pl.multiple_of(flip(f_idx, s) * part, part), part)
                f_copies[m, s] = send(
                    r["tot_" + m].at[at, :],
                    r["f_" + m].at[s - 1],
                    r["f_send"].at[i, s - 1],
                    r["f_recv"].at[i, s - 1],
                    over_f(s),
                )

    def store_total(m, at, value):
        if m in TAIL_CUT:
            r["tot_" + m][at, :] = value.astype(BF16)
        else:
            r["out_" + m][at, :] = value

    def put_out(m):
        total, out = r["tot_" + m], r["out_" + m]
        rows, width = total.shape
        part = rows // n_f
        for s in range(n_f):
            at = pl.ds(pl.multiple_of(flip(f_idx, s) * width, 128), width)
            if s:
                f_copies[m, s].wait_recv()
                out[:, at] = r["f_" + m][s - 1].astype(F32)
            else:
                mine = pl.ds(pl.multiple_of(f_idx * part, part), part)
                out[:, at] = total[mine, :].astype(F32)

    def cut_low(src, dst, width, index):
        rows = src.shape[0]
        mine = pl.ds(pl.multiple_of(f_idx * rows, rows), rows)
        copies = []
        for s in range(1, n_f):
            at = pl.ds(pl.multiple_of(flip(f_idx, s) * width, 128), width)
            copies.append(
                send(
                    src.at[:, at],
                    dst.at[mine, :],
                    r["low_send"].at[index, s - 1],
                    r["low_recv"].at[index, s - 1],
                    over_f(s),
                )
            )
        own = pl.ds(pl.multiple_of(f_idx * width, 128), width)
        dst[mine, :] = src[:, own]
        return copies

    start_y("kv", r["kv"])
    q_copies = cut_low(r["dqa"], r["qd_group"], r["qd_group"].shape[1], 0)
    for m in ("up", "out", "qup"):
        start_y(m, r[m])
    pair_in = pltpu.make_async_copy(r["gate"], r["pair_gate"], r["keep_sem"].at[0, n_z])
    pair_in.start()
    pair_in.wait()
    lines["gate"].run()
    add_pairs("kv")
    lines["kv"].run()
    finish_sum("gate")

    head = r["dkv"].shape[1] // 2
    mid = head // 2

    def store_kv(at, value):
        cos, sin = r["cos"][at, :], r["sin"][at, :]
        one, two = value[:, :mid], value[:, mid:head]
        r["dkv"][at, :mid] = (one * cos + two * sin).astype(BF16)
        r["dkv"][at, mid:head] = (two * cos - one * sin).astype(BF16)
        r["dkv"][at, head:] = value[:, head:].astype(BF16)

    lines["kv"].total(store_kv)
    kv_copies = cut_low(r["dkv"], r["kv_group"], r["kv_group"].shape[1], 1)

    def low_part(group, part):
        normed = r["normed_group"]
        rows = part.shape[2]
        for c in range(n_ctx):
            part[c // 2, c % 2] = lax.dot_general(
                normed[:, c * rows : (c + 1) * rows],
                group[...],
                (((0,), (0,)), ((), ())),
                preferred_element_type=F32,
            ).astype(BF16)

    for copy in q_copies:
        copy.wait_recv()
    low_part(r["qd_group"], r["part_qd"])
    start_y("qd", r["part_qd"])
    for copy in kv_copies:
        copy.wait_recv()
    low_part(r["kv_group"], r["part_kvw"])
    start_y("kvw", r["part_kvw"])

    grad_in, w_kv = r["grad_input"], r["w_kv"]
    width = grad_in.shape[1]
    tile = 256

    @pl.loop(0, width // tile)
    def _(t):
        at = pl.ds(pl.multiple_of(t * tile, tile), tile)
        grad_in[:, at] = r["da_q"][:, at] + lax.dot_general(
            r["dkv"][...],
            w_kv[at, :],
            (((1,), (1,)), ((), ())),
            preferred_element_type=F32,
        )

    r["gain_sum"][...] = jnp.zeros_like(r["gain_sum"])
    gain = r["gain_one"][...]

    def norm_rows(at):
        value = r["hidden"][at, :].astype(F32)
        grad = grad_in[at, :]
        scale = lax.rsqrt(jnp.mean(value * value, axis=-1, keepdims=True) + NORM_EPS)
        r["gain_sum"][...] += jnp.sum(grad * value * scale, axis=0, keepdims=True)
        ge = gain * grad
        inner = jnp.mean(ge * value, axis=-1, keepdims=True)
        grad_in[at, :] = (
            r["grad_resid"][at, :] + scale * ge - value * (scale * scale * scale) * inner
        )

    row_loop(grad_in.shape[0], norm_rows, step=16)

    small, small_got = r["small_out"], r["small_got"]
    small[...] = r["small"][...]
    for i in range(width // 128):
        small[i : i + 1, :] = r["gain_sum"][:, i * 128 : (i + 1) * 128]
    steps = [over_f(1), over_f(2), over_c(1)]
    mask = 2
    while mask < n_ctx:
        steps.append(over_c(mask))
        mask *= 2
    small_copies = {}

    def small_start(s):
        small_got[s, 0] = small[...]
        small_copies[s] = send(
            small_got.at[s, 0],
            small_got.at[s, 1],
            r["s_send"].at[s],
            r["s_recv"].at[s],
            steps[s],
        )

    def small_end(s):
        small_copies[s].wait_recv()
        small[...] = small[...] + small_got[s, 1]

    for s in range(2):
        small_start(s)
        small_end(s)
    small_start(2)

    put_out("gate")
    add_pairs("up")
    lines["up"].run()
    add_pairs("out")
    lines["out"].run()
    finish_sum("up")
    add_pairs("qup")
    lines["qup"].run()
    put_out("up")
    finish_sum("out")
    add_pairs("qd")
    lines["qd"].run()
    add_pairs("kvw")
    lines["kvw"].run()
    small_end(2)
    small_start(3)
    finish_sum("qup")
    for s in range(3, len(steps)):
        if s > 3:
            small_start(s)
        small_end(s)
    finish_sum("qd")
    finish_sum("kvw")
    for m in ("qup", "qd", "kvw"):
        put_out(m)
    send.finish()
    for m in TAIL_NAMES:
        lines[m].finish()


def tail_reduce(n_ctx, n_f, inputs, q_width):
    n_z = n_ctx // 2
    vmem = pl.BlockSpec(memory_space=pltpu.VMEM)
    anywhere = pl.BlockSpec(memory_space=pl.ANY)
    rows, width = inputs["hidden"].shape
    kv_width = inputs["w_kv"].shape[1]
    in_hbm = ("gate", "kv", "up", "out", "qup")
    names_in = tuple(inputs)
    in_specs = [anywhere if m in in_hbm else vmem for m in names_in]
    block = {m: inputs[m].shape[-2:] for m in in_hbm}
    block["qd"] = (width // n_ctx, q_width // n_f)
    block["kvw"] = (width // n_ctx, kv_width // n_f)
    outs = {
        "small_out": jax.ShapeDtypeStruct(inputs["small"].shape, F32),
        "grad_input": jax.ShapeDtypeStruct((rows, width), F32),
    }
    scratch = {}
    for m in TAIL_NAMES:
        high, wide = block[m]
        scratch["pair_" + m] = pltpu.VMEM((n_z, high, wide), BF16)
        scratch["z_" + m] = pltpu.VMEM((n_z + 1, high, wide), BF16)
        if m in TAIL_SENT:
            scratch["y_" + m] = pltpu.VMEM((n_z, high, wide), BF16)
        if m in TAIL_CUT:
            scratch["tot_" + m] = pltpu.VMEM((high, wide), BF16)
            scratch["f_" + m] = pltpu.VMEM((n_f - 1, high // n_f, wide), BF16)
            outs["out_" + m] = jax.ShapeDtypeStruct((high // n_f, wide * n_f), F32)
        elif m != "kv":
            outs["out_" + m] = jax.ShapeDtypeStruct((high, wide), F32)
    scratch["dkv"] = pltpu.VMEM((rows, kv_width), BF16)
    scratch["qd_group"] = pltpu.VMEM((rows * n_f, q_width // n_f), BF16)
    scratch["kv_group"] = pltpu.VMEM((rows * n_f, kv_width // n_f), BF16)
    scratch["part_qd"] = pltpu.VMEM((n_z, 2) + block["qd"], BF16)
    scratch["part_kvw"] = pltpu.VMEM((n_z, 2) + block["kvw"], BF16)
    scratch["gain_sum"] = pltpu.VMEM((1, width), F32)
    steps = 2 + (n_ctx.bit_length() - 1)
    scratch["small_got"] = pltpu.VMEM((steps, 2) + inputs["small"].shape, F32)
    dma = pltpu.SemaphoreType.DMA
    sent, cut = len(TAIL_SENT), len(TAIL_CUT)
    scratch["s_send"] = dma((steps,))
    scratch["s_recv"] = dma((steps,))
    scratch["y_send"] = dma((sent, n_z))
    scratch["y_recv"] = dma((sent, n_z))
    scratch["keep_sem"] = dma((sent, n_z + 1))
    scratch["z_send"] = dma((len(TAIL_NAMES), n_z))
    scratch["z_recv"] = dma((len(TAIL_NAMES), n_z + 1))
    scratch["f_send"] = dma((cut, n_f - 1))
    scratch["f_recv"] = dma((cut, n_f - 1))
    scratch["low_send"] = dma((2, n_f - 1))
    scratch["low_recv"] = dma((2, n_f - 1))
    values = pl.pallas_call(
        functools.partial(tail_kernel, n_ctx, n_f, names_in, tuple(outs), tuple(scratch)),
        out_shape=tuple(outs.values()),
        in_specs=in_specs,
        out_specs=tuple([vmem] * len(outs)),
        scratch_shapes=list(scratch.values()),
        compiler_params=pltpu.CompilerParams(
            collective_id=0, has_side_effects=True, vmem_limit_bytes=60 << 20
        ),
        name="tail_reduce",
    )(*inputs.values())
    return dict(zip(outs, values, strict=True))


def body(
    hidden_in,
    teacher,
    blocks,
    seq_ids,
    valid_mask,
    norm1_gain,
    q_down,
    q_gain,
    q_up,
    kv_weight,
    out_proj,
    norm2_gain,
    w_gate,
    w_up,
    w_down,
):
    row_count, model_width = hidden_in.shape
    head_size = kv_weight.shape[1] // 2
    heads_width = q_up.shape[1]
    head_count = heads_width // head_size
    half_dim = head_size // 2
    q_width = q_down.shape[1]
    n_ctx = lax.axis_size("ctx")
    n_f = lax.axis_size("fsdp")
    n_z = n_ctx // 2
    token_total = row_count * n_ctx * n_f
    seq_pieces = 2 * SEQ_BLOCKS
    c_idx = lax.axis_index("ctx")
    f_idx = lax.axis_index("fsdp")
    y_idx = c_idx % 2
    z_idx = c_idx // 2
    x_idx = f_idx // 2
    k_idx = f_idx % 2

    def by_f(values, mask):
        return lax.ppermute(values, "fsdp", [(i, i ^ mask) for i in range(n_f)])

    def by_c(values, mask):
        return lax.ppermute(values, "ctx", [(i, i ^ mask) for i in range(n_ctx)])

    def cut(values, start, size, axis):
        return lax.dynamic_slice_in_dim(values, start, size, axis)

    def gather_bit(values, got, bit):
        return jnp.concatenate(
            [jnp.where(bit == 0, values, got), jnp.where(bit == 0, got, values)], axis=0
        )

    def fetch_far(shard, mask, gate):
        half = shard.shape[0] // 2
        bit = (c_idx // mask) % 2
        return by_f(after(cut(shard, bit * half, half, 0), *gate), 2)

    def fetch_rest(shard, far, mask):
        rows = shard.shape[0]
        half = rows // 2
        bit = (c_idx // mask) % 2
        core = by_f(shard, 1)
        far_y = by_c(far, mask)
        far_core = by_f(far, 1)
        far_y_core = by_f(far_y, 1)
        mine, other = bit * half, (1 - bit) * half
        return [
            (shard, f_idx * rows),
            (core, (f_idx ^ 1) * rows),
            (far, (f_idx ^ 2) * rows + mine),
            (far_core, (f_idx ^ 3) * rows + mine),
            (far_y, (f_idx ^ 2) * rows + other),
            (far_y_core, (f_idx ^ 3) * rows + other),
        ]

    def mul_pieces(acts, pieces):
        total = None
        for weight, start in pieces:
            term = dot(cut(acts, start, weight.shape[0], 1), weight)
            total = term if total is None else total + term
        return total

    def mul_pieces_t(grads, pieces, dtype):
        width = sum(weight.shape[0] for weight, _ in pieces)
        out = jnp.zeros((grads.shape[0], width), dtype)
        for weight, start in pieces:
            out = lax.dynamic_update_slice_in_dim(out, dot_t(grads, weight).astype(dtype), start, 1)
        return out

    def columns_far(shard, gate):
        rows, columns = shard.shape
        width = columns // n_f
        half = rows // 2
        far_cut = lax.dynamic_slice(
            shard, (y_idx * half, (1 - x_idx) * 2 * width), (half, 2 * width)
        )
        return by_f(after(far_cut, *gate), 2)

    def columns_rest(shard, far):
        rows, columns = shard.shape
        width = columns // n_f
        half = rows // 2
        core = by_f(cut(shard, (f_idx ^ 1) * width, width, 1), 1)
        far_y = by_c(far, 1)
        far_core = by_f(cut(far, (1 - k_idx) * width, width, 1), 1)
        far_y_core = by_f(cut(far_y, (1 - k_idx) * width, width, 1), 1)
        mine, other = y_idx * half, (1 - y_idx) * half
        out = jnp.zeros((rows * n_f, width), shard.dtype)
        for piece, start in (
            (cut(shard, f_idx * width, width, 1), f_idx * rows),
            (core, (f_idx ^ 1) * rows),
            (cut(far, k_idx * width, width, 1), (f_idx ^ 2) * rows + mine),
            (far_core, (f_idx ^ 3) * rows + mine),
            (cut(far_y, k_idx * width, width, 1), (f_idx ^ 2) * rows + other),
            (far_y_core, (f_idx ^ 3) * rows + other),
        ):
            out = lax.dynamic_update_slice_in_dim(out, piece, start, 0)
        return out

    def gather_tokens(values):
        core = by_f(values, 1)
        far = by_f(values, 2)
        far_core = by_f(far, 1)
        return jnp.concatenate([values, core, far, far_core], axis=0)

    def sum_tokens(make_half):
        far = make_half(1).reshape(2, row_count, -1)
        far = (far[0] + by_f(far[1], 1)).astype(BF16)
        far = by_f(far, 2)
        near = make_half(0).reshape(2, row_count, -1)
        near = near[0] + by_f(near[1], 1)
        return near + far.astype(F32)

    def ctx_split(grad):
        view = grad.reshape(n_z, 2, grad.shape[0] // n_ctx, grad.shape[1])
        give = lax.dynamic_index_in_dim(view, 1 - y_idx, 1, keepdims=False)
        keep = lax.dynamic_index_in_dim(view, y_idx, 1, keepdims=False)
        return give, keep

    def ctx_pair(keep, got):
        return (keep.astype(F32) + got.astype(F32)).astype(BF16)

    def ctx_spread(pair):
        return [pair] + [
            by_c(lax.dynamic_index_in_dim(pair, z_idx ^ r, 0, keepdims=False), 2 * r)
            for r in range(1, n_z)
        ]

    def ctx_total(parts):
        total = lax.dynamic_index_in_dim(parts[0], z_idx, 0, keepdims=False).astype(F32)
        for got in parts[1:]:
            total = total + got.astype(F32)
        return total

    def group_rows(values):
        return lax.all_gather(values, "fsdp", axis=0, tiled=True)

    valid_f = valid_mask.astype(F32)
    d1, d2 = norm1_gain.shape[0], q_gain.shape[0]
    qkv_shard = jnp.concatenate([q_down, kv_weight], axis=1)
    qkv_far = fetch_far(qkv_shard, 1, ())
    info = jnp.concatenate(
        [
            norm1_gain.astype(F32),
            q_gain.astype(F32),
            norm2_gain.astype(F32),
            jnp.full((128,), jnp.sum(valid_f)),
        ]
    ).reshape(1, -1)
    info = gather_bit(info, by_f(info, 1), k_idx)
    info = gather_bit(info, by_f(info, 2), x_idx)
    gain_one = info[:, :d1].reshape(-1)
    gain_q = info[:, d1 : d1 + d2].reshape(-1)
    gain_two = info[:, d1 + d2 : 2 * d1 + d2].reshape(-1)
    tag_row = jnp.concatenate(
        [
            jnp.stack([blocks.reshape(-1, PIECE)[:, 0], seq_ids.reshape(-1, PIECE)[:, 0]], axis=1)
            .astype(F32)
            .reshape(-1),
            jnp.sum(info[:, 2 * d1 + d2]).reshape(1),
        ]
    )
    tag_row = jnp.pad(tag_row, (0, 128 - tag_row.shape[0])).reshape(1, 128)
    mask = 1
    while mask < n_ctx:
        tag_row = gather_bit(tag_row, by_c(tag_row, mask), (c_idx // mask) % 2)
        mask *= 2
    own_pieces = row_count // PIECE
    tags = tag_row[:, : 2 * own_pieces].reshape(-1, 2).astype(jnp.int32)
    total_count = jnp.sum(tag_row[:, 2 * own_pieces])
    own = jnp.concatenate([blocks.reshape(-1, PIECE)[:, 0], seq_ids[:1]])

    up_far = fetch_far(q_up, 2, (info,))
    out_far = fetch_far(out_proj, 2, (qkv_far,))
    gate_far = columns_far(w_gate, (up_far,))
    upw_far = columns_far(w_up, (out_far,))
    qkv_pieces = fetch_rest(qkv_shard, qkv_far, 1)
    up_pieces = fetch_rest(q_up, up_far, 2)
    out_pieces = fetch_rest(out_proj, out_far, 2)
    w_gatef = columns_rest(w_gate, gate_far)
    w_upf = columns_rest(w_up, upw_far)

    positions = blocks * PIECE + jnp.arange(row_count, dtype=jnp.int32) % PIECE
    freq_table = 10000.0 ** (-(jnp.arange(half_dim, dtype=F32) * 2.0 / head_size))
    angle_table = positions.astype(F32)[:, None] * freq_table[None, :]
    cosine = jnp.cos(angle_table)
    sine = jnp.sin(angle_table)
    hidden_f = hidden_in.astype(F32)
    scale_one = rms_scale(hidden_f)
    normed = (hidden_f * scale_one * gain_one).astype(BF16)
    low_all = mul_pieces(normed, qkv_pieces)
    q_low = low_all[:, :q_width]
    kv_lin = low_all[:, q_width:]
    key_rot = rope_apply(kv_lin[:, :head_size], cosine, sine).astype(BF16)
    kv_rows = jnp.concatenate([key_rot, kv_lin[:, head_size:].astype(BF16)], axis=1)
    all_kv = lax.all_gather(kv_rows, "ctx", axis=0, tiled=True)
    scale_q = rms_scale(q_low)
    q_normed = (q_low * scale_q * gain_q).astype(BF16)
    q_lin = mul_pieces(q_normed, up_pieces).reshape(row_count, head_count, head_size)
    q_rot = rope_apply(q_lin, cosine[:, None, :], sine[:, None, :]).astype(BF16)
    q_rot = q_rot.reshape(row_count, heads_width)

    attn_heads, lse = attn_fwd(tags, own, q_rot, all_kv, head_size, seq_pieces)
    resid = hidden_f + mul_pieces(attn_heads, out_pieces)
    scale_two = rms_scale(resid)
    normed_two = (resid * scale_two * gain_two).astype(BF16)

    group_two = gather_tokens(normed_two)
    gate_lin = dot(group_two, w_gatef)
    up_lin = dot(group_two, w_upf)
    sigma = jax.nn.sigmoid(gate_lin)
    silu_gate = gate_lin * sigma
    hidden_act = (silu_gate * up_lin).astype(BF16)
    side = 2 * row_count

    def down_half(j):
        return dot(hidden_act[j * side : (j + 1) * side], w_down)

    result = resid + sum_tokens(down_half)
    diff = result - teacher.astype(F32)
    sq_local = jnp.sum(valid_f * jnp.sum(diff * diff, axis=1))
    grad_y = diff * valid_f[:, None] * (token_total / total_count)
    group_dz = gather_tokens(grad_y.astype(BF16))
    down_part = dot_rows(hidden_act, group_dz).astype(BF16)
    down_give, down_keep = ctx_split(down_part)
    down_got = by_c(down_give, 1)
    group_dz2 = after(group_dz, down_part)
    grad_hidden = dot_t(group_dz2, w_down)
    grad_gate = (grad_hidden * up_lin * sigma * (1.0 + gate_lin * (1.0 - sigma))).astype(BF16)
    grad_up = (grad_hidden * silu_gate).astype(BF16)
    gate_part = dot_rows(group_two, grad_gate).astype(BF16)
    gate_give, gate_keep = ctx_split(gate_part)
    gate_got = by_c(gate_give, 1)

    def back_half(j):
        rows = slice(j * side, (j + 1) * side)
        return dot_t(grad_gate[rows], w_gatef) + dot_t(grad_up[rows], w_upf)

    grad_normed_two = sum_tokens(back_half)
    up_part = dot_rows(group_two, grad_up).astype(BF16)

    grad_resid_norm, grad_gain_two = rms_back(resid, scale_two, gain_two, grad_normed_two)
    grad_resid = grad_y + grad_resid_norm
    grad_branch = grad_resid.astype(BF16)
    grad_attn = mul_pieces_t(grad_branch, out_pieces, BF16)
    down_parts = ctx_spread(ctx_pair(down_keep, after(down_got, grad_attn)))

    grad_qlin, grad_seq = attn_bwd(
        tags, own, q_rot, grad_attn, attn_heads, lse, cosine, sine, all_kv, head_size, seq_pieces
    )
    by_piece = grad_seq.reshape(seq_pieces, PIECE, 2 * head_size)
    piece_tag = tags[:, 0].reshape(n_z, 2, own_pieces)
    piece_own = (tags[:, 1] == seq_ids[0]).reshape(n_z, 2, own_pieces)

    def kv_half(bit):
        places = lax.dynamic_index_in_dim(piece_tag, bit, 1, keepdims=False).reshape(-1)
        picked = by_piece[places]
        if n_ctx * own_pieces != seq_pieces:
            mine = lax.dynamic_index_in_dim(piece_own, bit, 1, keepdims=False).reshape(-1)
            picked = jnp.where(mine[:, None, None], picked, jnp.zeros_like(picked))
        return picked.reshape(n_z, own_pieces * PIECE, 2 * head_size)

    kv_part = jnp.stack([kv_half(0), kv_half(1)], axis=1)
    q_cut, kv_cut = q_width // n_f, 2 * head_size // n_f
    out_block = heads_width // (n_ctx * n_f)
    qlin_group = lax.all_to_all(grad_qlin, "fsdp", 1, 0, tiled=True)
    attn_group = lax.all_to_all(
        attn_heads.reshape(row_count, n_ctx, n_f, out_block), "fsdp", 2, 0, tiled=True
    ).reshape(row_count * n_f, n_ctx * out_block)
    branch_group = group_rows(grad_branch)
    qnorm_group = group_rows(q_normed)
    normed_group = group_rows(normed)

    grad_qnormed = mul_pieces_t(grad_qlin, up_pieces, F32)
    grad_qlow_f, grad_gain_q = rms_back(q_low, scale_q, gain_q, grad_qnormed)
    grad_qlow = grad_qlow_f.astype(BF16)
    da_q = mul_pieces_t(grad_qlow, [(w[:, :q_width], start) for w, start in qkv_pieces], F32)
    w_kv = jnp.zeros((model_width, 2 * head_size), BF16)
    for piece, start in qkv_pieces:
        w_kv = lax.dynamic_update_slice_in_dim(w_kv, piece[:, q_width:], start, 0)
    out_part = dot_rows(attn_group, branch_group).astype(BF16)
    qup_part = dot_rows(qnorm_group, qlin_group).astype(BF16)
    gate_pair = ctx_pair(gate_keep, after(gate_got, qup_part))

    def by_ctx(grad):
        return grad.reshape(n_z, 2, grad.shape[0] // n_ctx, grad.shape[1])

    order = [(c * n_f + f, f * n_ctx + c) for c in range(n_ctx) for f in range(n_f)]
    down_rows = ctx_total(after(down_parts, qup_part)).astype(BF16)
    down_sent = lax.ppermute(down_rows, ("ctx", "fsdp"), order)

    small = jnp.concatenate(
        [jnp.zeros_like(gain_one), grad_gain_q, grad_gain_two, sq_local.reshape(1)]
    )
    entries = small.shape[0]
    small = jnp.pad(small, (0, -entries % 1024)).reshape(-1, 128)
    ends = tail_reduce(
        n_ctx,
        n_f,
        {
            "gate": gate_pair,
            "kv": kv_part,
            "up": by_ctx(up_part),
            "out": by_ctx(out_part),
            "qup": by_ctx(qup_part),
            "dqa": grad_qlow,
            "cos": cosine,
            "sin": sine,
            "normed_group": normed_group,
            "w_kv": w_kv,
            "da_q": da_q,
            "hidden": hidden_in,
            "gain_one": gain_one.reshape(1, -1),
            "grad_resid": grad_resid,
            "small": small,
        },
        q_width,
    )
    small = ends["small_out"].reshape(-1)[:entries]
    grad_down = after(down_sent, small).astype(F32)

    device = c_idx * n_f + f_idx
    q1, q2 = model_width, model_width + q_width
    n_dev = n_ctx * n_f

    def own_part(values):
        size = values.shape[0] // n_dev
        return cut(values, device * size, size, 0)

    loss_now = small[-1] / (model_width * total_count)
    return (
        result.astype(BF16),
        loss_now,
        ends["grad_input"],
        own_part(small[:q1]),
        ends["out_qd"],
        own_part(small[q1:q2]),
        ends["out_qup"],
        ends["out_kvw"],
        ends["out_out"],
        own_part(small[q2 : q2 + model_width]),
        ends["out_gate"],
        ends["out_up"],
        grad_down,
    )


def solution(mesh):
    both = ("ctx", "fsdp")
    rows = P(both, None)
    flat = P(both)
    shard = P("fsdp", None)
    gain = P("fsdp")
    return jax.shard_map(
        body,
        mesh=mesh,
        in_specs=(
            rows,
            rows,
            flat,
            flat,
            flat,
            gain,
            shard,
            gain,
            shard,
            shard,
            shard,
            gain,
            shard,
            shard,
            shard,
        ),
        out_specs=(
            rows,
            P(),
            rows,
            flat,
            rows,
            flat,
            rows,
            rows,
            rows,
            flat,
            rows,
            rows,
            rows,
        ),
        check_vma=False,
    )
```

```python
import functools
import math

import jax
import jax.numpy as jnp
from jax import lax
from jax.experimental import pallas as pl
from jax.experimental.pallas import tpu as pltpu
from jax.sharding import PartitionSpec as P

PIECE = 128
SEQ_BLOCKS = 8
NORM_EPS = 1e-05
F32 = jnp.float32
BF16 = jnp.bfloat16
LOG2E = math.log2(math.e)
HEAD_GROUP = 4


def rms_scale(values):
    return lax.rsqrt(jnp.mean(values * values, axis=-1, keepdims=True) + NORM_EPS)


def rms_back(values, scale, gain, grad):
    grad_gain = jnp.sum(grad * values * scale, axis=0)
    ge = gain * grad
    inner = jnp.mean(ge * values, axis=-1, keepdims=True)
    return scale * ge - values * (scale * scale * scale) * inner, grad_gain


def rope_apply(values, cosine, sine):
    half_dim = values.shape[-1] // 2
    one = values[..., :half_dim]
    two = values[..., half_dim:]
    return jnp.concatenate([one * cosine - two * sine, two * cosine + one * sine], axis=-1)


def rope_back(grads, cosine, sine):
    half_dim = grads.shape[-1] // 2
    one = grads[..., :half_dim]
    two = grads[..., half_dim:]
    return jnp.concatenate([one * cosine + two * sine, two * cosine - one * sine], axis=-1)


def after(values, *deps):
    return lax.optimization_barrier((values, deps))[0]


def dot(a, b):
    return jnp.dot(a, b, preferred_element_type=F32)


def dot_t(a, b):
    return lax.dot_general(a, b, (((1,), (1,)), ((), ())), preferred_element_type=F32)


def dot_rows(a, b):
    return lax.dot_general(a, b, (((0,), (0,)), ((), ())), preferred_element_type=F32)


def contract_last(a, b):
    return lax.dot_general(a, b, (((1,), (1,)), ((), ())), preferred_element_type=F32)

def find_pieces(tags_ref, own_ref, pick_ref, total):
    @pl.loop(0, total)
    def _(u):
        @pl.when(tags_ref[u, 1] == own_ref[2])
        def _():
            pick_ref[tags_ref[u, 0]] = u

def stack_heads(ref, hd):
    return jnp.concatenate([ref[:, h*hd:(h+1)*hd] for h in range(HEAD_GROUP)], axis=0)

def attn_fwd_kernel(tags_ref, own_ref, q_ref, kv_ref, o_ref, lse_ref, k_s, vt_s, acc_s, pick_s):
    half = pl.program_id(0)
    hd = k_s.shape[1]
    pieces = k_s.shape[0] // PIECE
    total = kv_ref.shape[0] // PIECE
    wide = 2 * PIECE
    coef = hd ** -0.5 * LOG2E

    @pl.when((half == 0) & (pl.program_id(1) == 0))
    def _():
        find_pieces(tags_ref, own_ref, pick_s, total)
        for i in range(pieces):
            rows = pl.ds(pl.multiple_of(pick_s[i] * PIECE, PIECE), PIECE)
            k_s[i*PIECE:(i+1)*PIECE, :] = kv_ref[rows, :hd]
            vt_s[:, i*PIECE:(i+1)*PIECE] = kv_ref[rows, hd:].T

    q = stack_heads(q_ref, hd)
    acc_s[...] = jnp.zeros_like(acc_s)
    rows = q.shape[0]
    def step(i, carry):
        peak, total_p = carry
        at = pl.ds(pl.multiple_of(i * wide, wide), wide)
        raw = contract_last(k_s[at, :], q)
        top = jnp.maximum(peak, jnp.max(raw, axis=0, keepdims=True))
        fade = jnp.exp2((peak - top) * coef)
        p = jnp.exp2((raw - top) * coef)
        acc_s[...] = acc_s[...] * fade + jnp.dot(vt_s[:, at], p.astype(BF16), preferred_element_type=F32)
        return top, total_p * fade + jnp.sum(p, axis=0, keepdims=True)
    count = own_ref[half] // 2 + 1
    peak, total_p = lax.fori_loop(0, count, step, (jnp.full((1, rows), -1e30, F32), jnp.zeros((1, rows), F32)))
    out = (acc_s[...] / total_p).astype(BF16).T
    for h in range(HEAD_GROUP):
        o_ref[:, h*hd:(h+1)*hd] = out[h*PIECE:(h+1)*PIECE, :]
    lse_ref[0] = peak * coef + jnp.log2(total_p)

def attn_fwd(tags, own, q, kv, hd, pieces):
    n_rows, width = q.shape
    groups = width // hd // HEAD_GROUP
    gw = HEAD_GROUP * hd
    halves = n_rows // PIECE
    rows = HEAD_GROUP * PIECE
    blk = pl.BlockSpec((PIECE, gw), lambda p, g, *_: (p, g))
    flops = 4 * n_rows * width * pieces * PIECE * 9 // 16
    return pl.pallas_call(
        attn_fwd_kernel,
        out_shape=(jax.ShapeDtypeStruct(q.shape, BF16), jax.ShapeDtypeStruct((halves*groups, 1, rows), F32)),
        grid_spec=pltpu.PrefetchScalarGridSpec(
            num_scalar_prefetch=2, grid=(halves, groups),
            in_specs=[blk, pl.BlockSpec(kv.shape, lambda p, g, *_: (0, 0))],
            out_specs=[blk, pl.BlockSpec((1, 1, rows), lambda p, g, *_: (p*groups+g, 0, 0))],
            scratch_shapes=[pltpu.VMEM((pieces*PIECE, hd), BF16), pltpu.VMEM((hd, pieces*PIECE), BF16),
                            pltpu.VMEM((hd, rows), F32), pltpu.SMEM((pieces,), jnp.int32)]),
        compiler_params=pltpu.CompilerParams(vmem_limit_bytes=40 << 20),
        cost_estimate=pl.CostEstimate(flops=flops, transcendentals=flops//(4*hd), bytes_accessed=2*(2*q.size+kv.size)),
        name="attn_fwd",
    )(tags, own, q, kv)

def attn_bwd_kernel(tags_ref, own_ref, q_ref, do_ref, o_ref, lse_ref, cos_ref, sin_ref, kv_ref, dq_ref, dkv_ref,
                    k_s, kt_s, v_s, dq_s, dk_s, dv_s, pick_s):
    half = pl.program_id(0)
    group = pl.program_id(1)
    hd = k_s.shape[1]
    pieces = k_s.shape[0] // PIECE
    total = kv_ref.shape[0] // PIECE
    wide = 2 * PIECE
    coef = hd ** -0.5 * LOG2E
    scale = hd ** -0.5

    @pl.when((half == 0) & (group == 0))
    def _():
        find_pieces(tags_ref, own_ref, pick_s, total)
        for i in range(pieces):
            rows = pl.ds(pl.multiple_of(pick_s[i] * PIECE, PIECE), PIECE)
            keys = kv_ref[rows, :hd]
            k_s[i*PIECE:(i+1)*PIECE, :] = keys
            kt_s[:, i*PIECE:(i+1)*PIECE] = keys.T
            v_s[i*PIECE:(i+1)*PIECE, :] = kv_ref[rows, hd:]
        dk_s[...] = jnp.zeros_like(dk_s)
        dv_s[...] = jnp.zeros_like(dv_s)

    q = stack_heads(q_ref, hd)
    do = stack_heads(do_ref, hd)
    prod = do.astype(F32) * stack_heads(o_ref, hd).astype(F32)
    delta = lax.dot_general(jnp.ones((8, hd), F32), prod, (((1,), (1,)), ((), ())),
                            preferred_element_type=F32, precision=lax.Precision.HIGHEST)[:1]
    lse = lse_ref[0]
    dq_s[...] = jnp.zeros_like(dq_s)
    def step(i, carry):
        at = pl.ds(pl.multiple_of(i * wide, wide), wide)
        p = jnp.exp2(contract_last(k_s[at, :], q) * coef - lse)
        dp = contract_last(v_s[at, :], do)
        ds = (p * (dp - delta)).astype(BF16)
        dv_s[at, :] += jnp.dot(p.astype(BF16), do, preferred_element_type=F32)
        dk_s[at, :] += jnp.dot(ds, q, preferred_element_type=F32)
        dq_s[...] += jnp.dot(kt_s[:, at], ds, preferred_element_type=F32)
        return carry
    lax.fori_loop(0, own_ref[half] // 2 + 1, step, 0)
    dq = (dq_s[...] * scale).T
    cos, sin = cos_ref[...], sin_ref[...]
    mid = hd // 2
    for h in range(HEAD_GROUP):
        one = dq[h*PIECE:(h+1)*PIECE, :mid]
        two = dq[h*PIECE:(h+1)*PIECE, mid:]
        dq_ref[:, h*hd:h*hd+mid] = (one * cos + two * sin).astype(BF16)
        dq_ref[:, h*hd+mid:(h+1)*hd] = (two * cos - one * sin).astype(BF16)

    @pl.when((half == pl.num_programs(0) - 1) & (group == pl.num_programs(1) - 1))
    def _():
        dkv_ref[:, :hd] = (dk_s[...] * scale).astype(BF16)
        dkv_ref[:, hd:] = dv_s[...].astype(BF16)

def attn_bwd(tags, own, q, do, o, lse, cos, sin, kv, hd, pieces):
    n_rows, width = q.shape
    groups = width // hd // HEAD_GROUP
    gw = HEAD_GROUP * hd
    halves = n_rows // PIECE
    rows = HEAD_GROUP * PIECE
    blk = pl.BlockSpec((PIECE, gw), lambda p, g, *_: (p, g))
    trig = pl.BlockSpec((PIECE, hd // 2), lambda p, g, *_: (p, 0))
    keys = pieces * PIECE
    flops = 10 * n_rows * width * keys * 9 // 16
    return pl.pallas_call(
        attn_bwd_kernel,
        out_shape=(jax.ShapeDtypeStruct(q.shape, BF16), jax.ShapeDtypeStruct((keys, 2*hd), BF16)),
        grid_spec=pltpu.PrefetchScalarGridSpec(
            num_scalar_prefetch=2, grid=(halves, groups),
            in_specs=[blk, blk, blk, pl.BlockSpec((1, 1, rows), lambda p, g, *_: (p*groups+g, 0, 0)), trig, trig,
                      pl.BlockSpec(kv.shape, lambda p, g, *_: (0, 0))],
            out_specs=[blk, pl.BlockSpec((keys, 2*hd), lambda p, g, *_: (0, 0))],
            scratch_shapes=[pltpu.VMEM((keys, hd), BF16), pltpu.VMEM((hd, keys), BF16), pltpu.VMEM((keys, hd), BF16),
                            pltpu.VMEM((hd, rows), F32), pltpu.VMEM((keys, hd), F32), pltpu.VMEM((keys, hd), F32),
                            pltpu.SMEM((pieces,), jnp.int32)]),
        compiler_params=pltpu.CompilerParams(vmem_limit_bytes=48 << 20),
        cost_estimate=pl.CostEstimate(flops=flops, transcendentals=flops//(10*hd), bytes_accessed=2*(4*q.size+2*kv.size)),
        name="attn_bwd",
    )(tags, own, q, do, o, lse, cos, sin, kv)

MESH = pl.DeviceIdType.MESH


def flip(index, mask):
    out = 0
    bit = 1
    while bit <= mask:
        part = (index // bit) % 2
        out = out + bit * ((1 - part) if mask & bit else part)
        bit *= 2
    return out + (index // bit) * bit


def row_loop(rows, body, step=32):
    if rows % step:
        step = 16

    @pl.loop(0, rows // step)
    def _(i):
        body(pl.ds(pl.multiple_of(i * step, step), step))


class Sender:
    def __init__(self):
        self.open = []

    def make(self, src, dst, send_sem, recv_sem, peer):
        return pltpu.make_async_remote_copy(
            src_ref=src,
            dst_ref=dst,
            send_sem=send_sem,
            recv_sem=recv_sem,
            device_id=peer,
            device_id_type=MESH,
        )

    def __call__(self, *args):
        copy = self.make(*args)
        copy.start()
        self.open.append(copy)
        return copy

    def finish(self):
        for copy in self.open:
            copy.wait_send()


class LineSum:
    def __init__(self, own, got, send_sem, recv_sem, c_idx, f_idx, n_z, sender):
        self.own, self.got, self.send_sem, self.recv_sem = own, got, send_sem, recv_sem
        self.n_z, self.sender = n_z, sender
        self.z = c_idx // 2
        self.left = (c_idx - 2, f_idx)
        self.right = (c_idx + 2, f_idx)

    def copy(self, b, slot, peer):
        return self.sender.make(
            self.own.at[b], self.got.at[slot], self.send_sem.at[b], self.recv_sem.at[slot], peer
        )

    def take(self, b, slot):
        self.copy(b, slot, self.left).wait_recv()

        def add(at):
            self.own[b, at, :] = (
                self.own[b, at, :].astype(F32) + self.got[slot, at, :].astype(F32)
            ).astype(BF16)

        row_loop(self.own.shape[1], add)

    def run(self):
        z, n_z = self.z, self.n_z
        for step in range(n_z - 1):
            up, down = n_z - 1 - step, step

            @pl.when(z < up)
            def _(b=up):
                @pl.when(z > 0)
                def _():
                    self.take(b, b)

                self.copy(b, b, self.right).start()

            @pl.when(z > down)
            def _(b=down):
                @pl.when(z < n_z - 1)
                def _():
                    self.take(b, b)

                @pl.when(z - 1 > b)
                def _():
                    self.copy(b, b, self.left).start()

                @pl.when(z - 1 == b)
                def _():
                    self.copy(b, n_z, self.left).start()

    def total(self, store):
        z, n_z = self.z, self.n_z

        @pl.when(z > 0)
        def _():
            self.copy(z, z, self.left).wait_recv()

        @pl.when(z < n_z - 1)
        def _():
            self.copy(z, n_z, self.left).wait_recv()

        rows = self.own.shape[1]

        @pl.when(z == 0)
        def _():
            row_loop(
                rows,
                lambda at: store(
                    at, self.own[z, at, :].astype(F32) + self.got[n_z, at, :].astype(F32)
                ),
            )

        @pl.when(z == n_z - 1)
        def _():
            row_loop(
                rows,
                lambda at: store(
                    at, self.own[z, at, :].astype(F32) + self.got[z, at, :].astype(F32)
                ),
            )

        @pl.when((z > 0) & (z < n_z - 1))
        def _():
            row_loop(
                rows,
                lambda at: store(
                    at,
                    self.own[z, at, :].astype(F32)
                    + self.got[z, at, :].astype(F32)
                    + self.got[n_z, at, :].astype(F32),
                ),
            )

    def finish(self):
        for b in range(self.n_z):

            @pl.when(self.z != b)
            def _(b=b):
                self.copy(b, b, self.left).wait_send()


TAIL_NAMES = ("gate", "kv", "up", "out", "qup", "qd", "kvw")
TAIL_CUT = ("gate", "up", "qup", "qd", "kvw")
TAIL_SENT = ("kv", "up", "out", "qup", "qd", "kvw")


def tail_kernel(n_ctx, n_f, names_in, names_out, names_scratch, *refs):
    n_z = n_ctx // 2
    names = list(names_in) + list(names_out) + list(names_scratch)
    r = dict(zip(names, refs, strict=True))
    c_idx = lax.axis_index("ctx")
    f_idx = lax.axis_index("fsdp")
    y_idx = c_idx % 2
    z_idx = c_idx // 2
    send = Sender()

    def over_c(mask):
        return (flip(c_idx, mask), f_idx)

    def over_f(mask):
        return (c_idx, flip(f_idx, mask))

    barrier = pltpu.get_barrier_semaphore()
    for mask in range(1, n_f):
        pl.semaphore_signal(barrier, inc=1, device_id=over_f(mask), device_id_type=MESH)
    for mask in range(1, n_ctx):
        pl.semaphore_signal(barrier, inc=1, device_id=over_c(mask), device_id_type=MESH)
    pl.semaphore_wait(barrier, n_f - 1 + n_ctx - 1)

    lines = {
        m: LineSum(
            r["pair_" + m],
            r["z_" + m],
            r["z_send"].at[i],
            r["z_recv"].at[i],
            c_idx,
            f_idx,
            n_z,
            send,
        )
        for i, m in enumerate(TAIL_NAMES)
    }
    order = list(range(1, n_z)) + [0]
    y_copies, keeps = {}, {}

    def start_y(m, part):
        i = TAIL_SENT.index(m)
        for s in order:
            b = flip(z_idx, s)
            y_copies[m, s] = send(
                part.at[b, 1 - y_idx],
                r["y_" + m].at[s],
                r["y_send"].at[i, s],
                r["y_recv"].at[i, s],
                over_c(1),
            )
        for s in order:
            b = flip(z_idx, s)
            keep = pltpu.make_async_copy(
                part.at[b, y_idx], r["pair_" + m].at[b], r["keep_sem"].at[i, s]
            )
            keep.start()
            keeps[m, s] = keep

    def add_pairs(m):
        for s in order:
            b = flip(z_idx, s)
            keeps[m, s].wait()
            y_copies[m, s].wait_recv()
            pair, got = r["pair_" + m], r["y_" + m]

            def add(at, s=s, b=b, pair=pair, got=got):
                pair[b, at, :] = (
                    pair[b, at, :].astype(F32) + got[s, at, :].astype(F32)
                ).astype(BF16)

            row_loop(pair.shape[1], add)

    f_copies = {}

    def finish_sum(m):
        lines[m].total(lambda at, value: store_total(m, at, value))
        if m in TAIL_CUT:
            i = TAIL_CUT.index(m)
            part = r["tot_" + m].shape[0] // n_f
            for s in range(1, n_f):
                at = pl.ds(pl.multiple_of(flip(f_idx, s) * part, part), part)
                f_copies[m, s] = send(
                    r["tot_" + m].at[at, :],
                    r["f_" + m].at[s - 1],
                    r["f_send"].at[i, s - 1],
                    r["f_recv"].at[i, s - 1],
                    over_f(s),
                )

    def store_total(m, at, value):
        if m in TAIL_CUT:
            r["tot_" + m][at, :] = value.astype(BF16)
        else:
            r["out_" + m][at, :] = value

    def put_out(m):
        total, out = r["tot_" + m], r["out_" + m]
        rows, width = total.shape
        part = rows // n_f
        for s in range(n_f):
            at = pl.ds(pl.multiple_of(flip(f_idx, s) * width, 128), width)
            if s:
                f_copies[m, s].wait_recv()
                out[:, at] = r["f_" + m][s - 1].astype(F32)
            else:
                mine = pl.ds(pl.multiple_of(f_idx * part, part), part)
                out[:, at] = total[mine, :].astype(F32)

    def cut_low(src, dst, width, index):
        rows = src.shape[0]
        mine = pl.ds(pl.multiple_of(f_idx * rows, rows), rows)
        copies = []
        for s in range(1, n_f):
            at = pl.ds(pl.multiple_of(flip(f_idx, s) * width, 128), width)
            copies.append(
                send(
                    src.at[:, at],
                    dst.at[mine, :],
                    r["low_send"].at[index, s - 1],
                    r["low_recv"].at[index, s - 1],
                    over_f(s),
                )
            )
        own = pl.ds(pl.multiple_of(f_idx * width, 128), width)
        dst[mine, :] = src[:, own]
        return copies

    start_y("kv", r["kv"])
    q_copies = cut_low(r["dqa"], r["qd_group"], r["qd_group"].shape[1], 0)
    for m in ("up", "out", "qup"):
        start_y(m, r[m])
    pair_in = pltpu.make_async_copy(r["gate"], r["pair_gate"], r["keep_sem"].at[0, n_z])
    pair_in.start()
    pair_in.wait()
    lines["gate"].run()
    add_pairs("kv")
    lines["kv"].run()
    finish_sum("gate")

    head = r["dkv"].shape[1] // 2
    mid = head // 2

    def store_kv(at, value):
        cos, sin = r["cos"][at, :], r["sin"][at, :]
        one, two = value[:, :mid], value[:, mid:head]
        r["dkv"][at, :mid] = (one * cos + two * sin).astype(BF16)
        r["dkv"][at, mid:head] = (two * cos - one * sin).astype(BF16)
        r["dkv"][at, head:] = value[:, head:].astype(BF16)

    lines["kv"].total(store_kv)
    kv_copies = cut_low(r["dkv"], r["kv_group"], r["kv_group"].shape[1], 1)

    def low_part(group, part):
        normed = r["normed_group"]
        rows = part.shape[2]
        for c in range(n_ctx):
            part[c // 2, c % 2] = lax.dot_general(
                normed[:, c * rows : (c + 1) * rows],
                group[...],
                (((0,), (0,)), ((), ())),
                preferred_element_type=F32,
            ).astype(BF16)

    for copy in q_copies:
        copy.wait_recv()
    low_part(r["qd_group"], r["part_qd"])
    start_y("qd", r["part_qd"])
    for copy in kv_copies:
        copy.wait_recv()
    low_part(r["kv_group"], r["part_kvw"])
    start_y("kvw", r["part_kvw"])

    grad_in, w_kv = r["grad_input"], r["w_kv"]
    width = grad_in.shape[1]
    tile = 256

    @pl.loop(0, width // tile)
    def _(t):
        at = pl.ds(pl.multiple_of(t * tile, tile), tile)
        grad_in[:, at] = r["da_q"][:, at] + lax.dot_general(
            r["dkv"][...],
            w_kv[at, :],
            (((1,), (1,)), ((), ())),
            preferred_element_type=F32,
        )

    r["gain_sum"][...] = jnp.zeros_like(r["gain_sum"])
    gain = r["gain_one"][...]

    def norm_rows(at):
        value = r["hidden"][at, :].astype(F32)
        grad = grad_in[at, :]
        scale = lax.rsqrt(jnp.mean(value * value, axis=-1, keepdims=True) + NORM_EPS)
        r["gain_sum"][...] += jnp.sum(grad * value * scale, axis=0, keepdims=True)
        ge = gain * grad
        inner = jnp.mean(ge * value, axis=-1, keepdims=True)
        grad_in[at, :] = (
            r["grad_resid"][at, :] + scale * ge - value * (scale * scale * scale) * inner
        )

    row_loop(grad_in.shape[0], norm_rows, step=16)

    small, small_got = r["small_out"], r["small_got"]
    small[...] = r["small"][...]
    for i in range(width // 128):
        small[i : i + 1, :] = r["gain_sum"][:, i * 128 : (i + 1) * 128]
    steps = [over_f(1), over_f(2), over_c(1)]
    mask = 2
    while mask < n_ctx:
        steps.append(over_c(mask))
        mask *= 2
    small_copies = {}

    def small_start(s):
        small_got[s, 0] = small[...]
        small_copies[s] = send(
            small_got.at[s, 0],
            small_got.at[s, 1],
            r["s_send"].at[s],
            r["s_recv"].at[s],
            steps[s],
        )

    def small_end(s):
        small_copies[s].wait_recv()
        small[...] = small[...] + small_got[s, 1]

    for s in range(2):
        small_start(s)
        small_end(s)
    small_start(2)

    put_out("gate")
    add_pairs("up")
    lines["up"].run()
    add_pairs("out")
    lines["out"].run()
    finish_sum("up")
    add_pairs("qup")
    lines["qup"].run()
    put_out("up")
    finish_sum("out")
    add_pairs("qd")
    lines["qd"].run()
    add_pairs("kvw")
    lines["kvw"].run()
    small_end(2)
    small_start(3)
    finish_sum("qup")
    for s in range(3, len(steps)):
        if s > 3:
            small_start(s)
        small_end(s)
    finish_sum("qd")
    finish_sum("kvw")
    for m in ("qup", "qd", "kvw"):
        put_out(m)
    send.finish()
    for m in TAIL_NAMES:
        lines[m].finish()


def tail_reduce(n_ctx, n_f, inputs, q_width):
    n_z = n_ctx // 2
    vmem = pl.BlockSpec(memory_space=pltpu.VMEM)
    anywhere = pl.BlockSpec(memory_space=pl.ANY)
    rows, width = inputs["hidden"].shape
    kv_width = inputs["w_kv"].shape[1]
    in_hbm = ("gate", "kv", "up", "out", "qup")
    names_in = tuple(inputs)
    in_specs = [anywhere if m in in_hbm else vmem for m in names_in]
    block = {m: inputs[m].shape[-2:] for m in in_hbm}
    block["qd"] = (width // n_ctx, q_width // n_f)
    block["kvw"] = (width // n_ctx, kv_width // n_f)
    outs = {
        "small_out": jax.ShapeDtypeStruct(inputs["small"].shape, F32),
        "grad_input": jax.ShapeDtypeStruct((rows, width), F32),
    }
    scratch = {}
    for m in TAIL_NAMES:
        high, wide = block[m]
        scratch["pair_" + m] = pltpu.VMEM((n_z, high, wide), BF16)
        scratch["z_" + m] = pltpu.VMEM((n_z + 1, high, wide), BF16)
        if m in TAIL_SENT:
            scratch["y_" + m] = pltpu.VMEM((n_z, high, wide), BF16)
        if m in TAIL_CUT:
            scratch["tot_" + m] = pltpu.VMEM((high, wide), BF16)
            scratch["f_" + m] = pltpu.VMEM((n_f - 1, high // n_f, wide), BF16)
            outs["out_" + m] = jax.ShapeDtypeStruct((high // n_f, wide * n_f), F32)
        elif m != "kv":
            outs["out_" + m] = jax.ShapeDtypeStruct((high, wide), F32)
    scratch["dkv"] = pltpu.VMEM((rows, kv_width), BF16)
    scratch["qd_group"] = pltpu.VMEM((rows * n_f, q_width // n_f), BF16)
    scratch["kv_group"] = pltpu.VMEM((rows * n_f, kv_width // n_f), BF16)
    scratch["part_qd"] = pltpu.VMEM((n_z, 2) + block["qd"], BF16)
    scratch["part_kvw"] = pltpu.VMEM((n_z, 2) + block["kvw"], BF16)
    scratch["gain_sum"] = pltpu.VMEM((1, width), F32)
    steps = 2 + (n_ctx.bit_length() - 1)
    scratch["small_got"] = pltpu.VMEM((steps, 2) + inputs["small"].shape, F32)
    dma = pltpu.SemaphoreType.DMA
    sent, cut = len(TAIL_SENT), len(TAIL_CUT)
    scratch["s_send"] = dma((steps,))
    scratch["s_recv"] = dma((steps,))
    scratch["y_send"] = dma((sent, n_z))
    scratch["y_recv"] = dma((sent, n_z))
    scratch["keep_sem"] = dma((sent, n_z + 1))
    scratch["z_send"] = dma((len(TAIL_NAMES), n_z))
    scratch["z_recv"] = dma((len(TAIL_NAMES), n_z + 1))
    scratch["f_send"] = dma((cut, n_f - 1))
    scratch["f_recv"] = dma((cut, n_f - 1))
    scratch["low_send"] = dma((2, n_f - 1))
    scratch["low_recv"] = dma((2, n_f - 1))
    values = pl.pallas_call(
        functools.partial(tail_kernel, n_ctx, n_f, names_in, tuple(outs), tuple(scratch)),
        out_shape=tuple(outs.values()),
        in_specs=in_specs,
        out_specs=tuple([vmem] * len(outs)),
        scratch_shapes=list(scratch.values()),
        compiler_params=pltpu.CompilerParams(
            collective_id=0, has_side_effects=True, vmem_limit_bytes=60 << 20
        ),
        name="tail_reduce",
    )(*inputs.values())
    return dict(zip(outs, values, strict=True))


def front_kernel(n_ctx, n_f, names, *refs):
    r = dict(zip(names, refs, strict=True))
    n_z = n_ctx // 2
    c_idx = lax.axis_index("ctx")
    f_idx = lax.axis_index("fsdp")
    y_idx = c_idx % 2
    z_bit = (c_idx // 2) % 2
    x_idx = f_idx // 2
    k_idx = f_idx % 2
    far_idx = flip(f_idx, 2)
    moves = Sender()
    local = []
    at_sem = [0]

    def over_c(mask):
        return (flip(c_idx, mask), f_idx)

    def over_f(mask):
        return (c_idx, flip(f_idx, mask))

    def send(src, dst, peer):
        i = at_sem[0]
        at_sem[0] += 1
        return moves(src, dst, r["send_sem"].at[i], r["recv_sem"].at[i], peer)

    def keep(src, dst):
        copy = pltpu.make_async_copy(src, dst, r["local_sem"].at[len(local)])
        copy.start()
        local.append(copy)
        return copy

    def rows(start, size):
        return pl.ds(pl.multiple_of(start, size), size)

    barrier = pltpu.get_barrier_semaphore()
    for mask in range(1, n_f):
        pl.semaphore_signal(barrier, inc=1, device_id=over_f(mask), device_id_type=MESH)
    for mask in range(1, n_ctx):
        pl.semaphore_signal(barrier, inc=1, device_id=over_c(mask), device_id_type=MESH)
    pl.semaphore_wait(barrier, n_f - 1 + n_ctx - 1)

    infos, tags = r["infos"], r["tags"]
    infos[f_idx] = r["info"][...]
    info_copies = [
        send(infos.at[f_idx], infos.at[f_idx], over_f(mask)) for mask in range(1, n_f)
    ]

    class Rows:
        def __init__(self, shard, dest, bit, hop, chunks):
            self.dest, self.bit, self.hop = dest, bit, hop
            self.shard = shard
            self.size = shard.shape[0]
            self.half = self.size // 2
            self.step = self.half // chunks
            self.chunks = chunks
            self.far, self.next, self.cross = [], [], []

        def start(self):
            mine = self.dest.at[rows(f_idx * self.size, self.size)]
            for i in range(self.chunks):
                part = self.bit * self.half + i * self.step
                self.far.append(
                    send(
                        self.shard.at[rows(part, self.step)],
                        self.dest.at[rows(f_idx * self.size + part, self.step)],
                        over_f(2),
                    )
                )
            keep(self.shard, mine)
            self.cross.append(send(self.shard, mine, over_f(1)))

        def place(self, bit, i):
            return self.dest.at[rows(far_idx * self.size + bit * self.half + i * self.step, self.step)]

        def hop_on(self, i):
            self.far[i].wait_recv()
            here = self.place(self.bit, i)
            self.next.append(send(here, here, over_c(self.hop)))
            self.cross.append(send(here, here, over_f(1)))

        def pass_on(self, i):
            self.next[i].wait_recv()
            here = self.place(1 - self.bit, i)
            self.cross.append(send(here, here, over_f(1)))

        def end(self):
            for copy in self.cross:
                copy.wait_recv()

    class Columns:
        def __init__(self, shard, dest, box, bits, hops):
            self.shard, self.dest, self.box = shard, dest, box
            self.bits, self.hops = bits, hops
            self.size = shard.shape[0]
            self.width = dest.shape[1]
            self.quarter = self.size // 4

        def columns(self, start, count=1):
            return pl.ds(pl.multiple_of(start * self.width, 128), count * self.width)

        def start(self):
            one, two = self.bits
            at = rows((two * 2 + one) * self.quarter, self.quarter)
            self.far = send(
                self.shard.at[at, self.columns((1 - x_idx) * 2, 2)], self.box.at[at], over_f(2)
            )
            mine = self.dest.at[rows(f_idx * self.size, self.size)]
            keep(self.shard.at[:, self.columns(f_idx)], mine)
            self.cross = [send(self.shard.at[:, self.columns(flip(f_idx, 1))], mine, over_f(1))]

        def piece(self, one, two):
            return self.box.at[rows((two * 2 + one) * self.quarter, self.quarter)]

        def first(self):
            one, two = self.bits
            self.far.wait_recv()
            here = self.piece(one, two)
            self.step = send(here, here, over_c(self.hops[0]))
            self.last = [send(here, here, over_c(self.hops[1]))]

        def second(self):
            one, two = self.bits
            self.step.wait_recv()
            here = self.piece(1 - one, two)
            self.last.append(send(here, here, over_c(self.hops[1])))

        def part(self):
            for copy in self.last:
                copy.wait_recv()
            there = self.dest.at[rows(far_idx * self.size, self.size)]
            self.cross.append(send(self.box.at[:, self.columns(1 - k_idx)], there, over_f(1)))
            keep(self.box.at[:, self.columns(k_idx)], there)

        def end(self):
            for copy in self.cross:
                copy.wait_recv()

    kv = Rows(r["kv_weight"], r["kv_full"], y_idx, 1, 1)
    qd = Rows(r["q_down"], r["qd_full"], y_idx, 1, 1)
    qu = Rows(r["q_up"], r["qu_full"], y_idx, 1, 1)
    out = Rows(r["out_proj"], r["w_out"], z_bit, 2, 4)
    gate = Columns(r["w_gate"], r["gate_full"], r["gate_box"], (y_idx, z_bit), (1, 2))
    up = Columns(r["w_up"], r["up_full"], r["up_box"], (z_bit, y_idx), (2, 1))
    for part in (kv, qd, qu, gate, up, out):
        part.start()

    for copy in info_copies:
        copy.wait_recv()
    d1 = r["gain_one"].shape[1] // n_f // 128
    d2 = r["gain_q"].shape[1] // n_f // 128
    count = infos[0, 2 * d1 + d2 : 2 * d1 + d2 + 1, :]
    for f in range(n_f):
        for i in range(d1):
            col = slice((f * d1 + i) * 128, (f * d1 + i + 1) * 128)
            r["gain_one"][:, col] = infos[f, i : i + 1, :]
            r["gain_two"][:, col] = infos[f, d1 + d2 + i : d1 + d2 + i + 1, :]
        for i in range(d2):
            col = slice((f * d2 + i) * 128, (f * d2 + i + 1) * 128)
            r["gain_q"][:, col] = infos[f, d1 + i : d1 + i + 1, :]
        if f:
            count = count + infos[f, 2 * d1 + d2 : 2 * d1 + d2 + 1, :]
    tags[c_idx] = r["tag"][...]
    tags[c_idx, 1:2, :] = count
    tag_copies = [send(tags.at[c_idx], tags.at[c_idx], over_c(mask)) for mask in range(1, n_ctx)]

    normed = r["normed"]
    gain_one = r["gain_one"][...]

    def norm_rows(at):
        value = r["hidden"][at, :].astype(F32)
        scale = lax.rsqrt(jnp.mean(value * value, axis=-1, keepdims=True) + NORM_EPS)
        normed[at, :] = (value * scale * gain_one).astype(BF16)

    row_loop(normed.shape[0], norm_rows, step=16)

    kv.hop_on(0)
    qd.hop_on(0)
    kv.pass_on(0)
    qd.pass_on(0)
    kv.end()
    local[0].wait()
    head = r["kv_full"].shape[1] // 2
    mid = head // 2
    cos, sin = r["cos"], r["sin"]
    kv_rows = r["kv_rows"]
    keys = jnp.dot(normed[...], r["kv_full"][:, :head], preferred_element_type=F32)
    one, two = keys[:, :mid], keys[:, mid:]
    kv_rows[:, :mid] = (one * cos[...] - two * sin[...]).astype(BF16)
    kv_rows[:, mid:head] = (two * cos[...] + one * sin[...]).astype(BF16)
    kv_rows[:, head:] = jnp.dot(
        normed[...], r["kv_full"][:, head:], preferred_element_type=F32
    ).astype(BF16)
    all_kv = r["all_kv"]
    tokens = normed.shape[0]

    def kv_place(c):
        return all_kv.at[rows(c * tokens, tokens)]

    kv_z = [send(kv_rows, kv_place(c_idx), over_c(2 * s)) for s in range(1, n_z)]
    kv_y = [send(kv_rows, kv_place(c_idx), over_c(1))]
    keep(kv_rows, kv_place(c_idx))
    qd.end()
    local[1].wait()

    @pl.loop(0, r["q_low"].shape[1] // 256)
    def _(t):
        at = pl.ds(pl.multiple_of(t * 256, 256), 256)
        r["q_low"][:, at] = jnp.dot(
            normed[...], r["qd_full"][:, at], preferred_element_type=F32
        )

    gain_q = r["gain_q"][...]

    def norm_low(at):
        value = r["q_low"][at, :]
        scale = lax.rsqrt(jnp.mean(value * value, axis=-1, keepdims=True) + NORM_EPS)
        r["q_normed"][at, :] = (value * scale * gain_q).astype(BF16)

    row_loop(tokens, norm_low, step=16)
    qu.hop_on(0)
    gate.first()
    for s in range(1, n_z):
        kv_z[s - 1].wait_recv()
        here = kv_place(flip(c_idx, 2 * s))
        kv_y.append(send(here, here, over_c(1)))
    qu.pass_on(0)
    up.first()
    qu.end()
    local[2].wait()

    @pl.loop(0, r["q_rot"].shape[1] // head)
    def _(h):
        start = pl.multiple_of(h * head, head)
        value = jnp.dot(
            r["q_normed"][...],
            r["qu_full"][:, pl.ds(start, head)],
            preferred_element_type=F32,
        )
        one, two = value[:, :mid], value[:, mid:]
        r["q_rot"][:, pl.ds(start, mid)] = (one * cos[...] - two * sin[...]).astype(BF16)
        late = pl.multiple_of(h * head + mid, mid)
        r["q_rot"][:, pl.ds(late, mid)] = (two * cos[...] + one * sin[...]).astype(BF16)

    for m in ("kv", "qd", "qu"):
        keep(r[m + "_full"], r["w_" + m])
    gate.second()
    out.hop_on(0)
    up.second()
    for i in range(1, out.chunks):
        out.hop_on(i)
    gate.part()
    for i in range(out.chunks):
        out.pass_on(i)
    up.part()
    for copy in kv_y + tag_copies:
        copy.wait_recv()
    for part in (gate, up, out):
        part.end()
    for copy in local[3:]:
        copy.wait()
    moves.finish()


def front(n_ctx, n_f, inputs, head_size):
    tokens, width = inputs["hidden"].shape
    shape = jax.ShapeDtypeStruct
    q_width = inputs["q_down"].shape[1]
    heads_width = inputs["q_up"].shape[1]
    part = inputs["w_gate"].shape[1] // n_f

    def whole(m):
        return (inputs[m].shape[0] * n_f, inputs[m].shape[1])

    in_hbm = ("q_down", "kv_weight", "q_up", "out_proj", "w_gate", "w_up")
    outs = {
        "w_qd": shape(whole("q_down"), BF16),
        "w_kv": shape(whole("kv_weight"), BF16),
        "w_qu": shape(whole("q_up"), BF16),
        "w_out": shape(whole("out_proj"), BF16),
        "gate_full": shape((width, part), BF16),
        "up_full": shape((width, part), BF16),
        "all_kv": shape((tokens * n_ctx, 2 * head_size), BF16),
        "normed": shape((tokens, width), BF16),
        "q_low": shape((tokens, q_width), F32),
        "q_normed": shape((tokens, q_width), BF16),
        "q_rot": shape((tokens, heads_width), BF16),
        "gain_one": shape((1, width), F32),
        "gain_q": shape((1, q_width), F32),
        "gain_two": shape((1, width), F32),
        "tags": shape((n_ctx, 8, 128), F32),
    }
    out_hbm = ("w_qd", "w_kv", "w_qu", "w_out", "gate_full", "up_full", "all_kv")
    box = (inputs["w_gate"].shape[0], 2 * part)
    dma = pltpu.SemaphoreType.DMA
    scratch = {
        "infos": pltpu.VMEM((n_f,) + inputs["info"].shape, F32),
        "qd_full": pltpu.VMEM(whole("q_down"), BF16),
        "kv_full": pltpu.VMEM(whole("kv_weight"), BF16),
        "qu_full": pltpu.VMEM(whole("q_up"), BF16),
        "gate_box": pltpu.VMEM(box, BF16),
        "up_box": pltpu.VMEM(box, BF16),
        "kv_rows": pltpu.VMEM((tokens, 2 * head_size), BF16),
        "send_sem": dma((64 + 2 * n_ctx,)),
        "recv_sem": dma((64 + 2 * n_ctx,)),
        "local_sem": dma((16,)),
    }
    vmem = pl.BlockSpec(memory_space=pltpu.VMEM)
    anywhere = pl.BlockSpec(memory_space=pl.ANY)
    names = tuple(inputs) + tuple(outs) + tuple(scratch)
    values = pl.pallas_call(
        functools.partial(front_kernel, n_ctx, n_f, names),
        out_shape=tuple(outs.values()),
        in_specs=[anywhere if m in in_hbm else vmem for m in inputs],
        out_specs=tuple([anywhere if m in out_hbm else vmem for m in outs]),
        scratch_shapes=list(scratch.values()),
        compiler_params=pltpu.CompilerParams(
            collective_id=1, has_side_effects=True, vmem_limit_bytes=48 << 20
        ),
        name="front",
    )(*inputs.values())
    return dict(zip(outs, values, strict=True))


def body(
    hidden_in,
    teacher,
    blocks,
    seq_ids,
    valid_mask,
    norm1_gain,
    q_down,
    q_gain,
    q_up,
    kv_weight,
    out_proj,
    norm2_gain,
    w_gate,
    w_up,
    w_down,
):
    row_count, model_width = hidden_in.shape
    head_size = kv_weight.shape[1] // 2
    heads_width = q_up.shape[1]
    head_count = heads_width // head_size
    half_dim = head_size // 2
    q_width = q_down.shape[1]
    n_ctx = lax.axis_size("ctx")
    n_f = lax.axis_size("fsdp")
    n_z = n_ctx // 2
    token_total = row_count * n_ctx * n_f
    seq_pieces = 2 * SEQ_BLOCKS
    c_idx = lax.axis_index("ctx")
    f_idx = lax.axis_index("fsdp")
    y_idx = c_idx % 2
    z_idx = c_idx // 2
    x_idx = f_idx // 2
    k_idx = f_idx % 2

    def by_f(values, mask):
        return lax.ppermute(values, "fsdp", [(i, i ^ mask) for i in range(n_f)])

    def by_c(values, mask):
        return lax.ppermute(values, "ctx", [(i, i ^ mask) for i in range(n_ctx)])

    def cut(values, start, size, axis):
        return lax.dynamic_slice_in_dim(values, start, size, axis)

    def gather_tokens(values):
        core = by_f(values, 1)
        far = by_f(values, 2)
        far_core = by_f(far, 1)
        return jnp.concatenate([values, core, far, far_core], axis=0)

    def sum_tokens(make_half):
        far = make_half(1).reshape(2, row_count, -1)
        far = (far[0] + by_f(far[1], 1)).astype(BF16)
        far = by_f(far, 2)
        near = make_half(0).reshape(2, row_count, -1)
        near = near[0] + by_f(near[1], 1)
        return near + far.astype(F32)

    def ctx_split(grad):
        view = grad.reshape(n_z, 2, grad.shape[0] // n_ctx, grad.shape[1])
        give = lax.dynamic_index_in_dim(view, 1 - y_idx, 1, keepdims=False)
        keep = lax.dynamic_index_in_dim(view, y_idx, 1, keepdims=False)
        return give, keep

    def ctx_pair(keep, got):
        return (keep.astype(F32) + got.astype(F32)).astype(BF16)

    def ctx_spread(pair):
        return [pair] + [
            by_c(lax.dynamic_index_in_dim(pair, z_idx ^ r, 0, keepdims=False), 2 * r)
            for r in range(1, n_z)
        ]

    def ctx_total(parts):
        total = lax.dynamic_index_in_dim(parts[0], z_idx, 0, keepdims=False).astype(F32)
        for got in parts[1:]:
            total = total + got.astype(F32)
        return total

    def group_rows(values):
        return lax.all_gather(values, "fsdp", axis=0, tiled=True)

    valid_f = valid_mask.astype(F32)
    own_pieces = row_count // PIECE
    info = jnp.concatenate(
        [
            norm1_gain.astype(F32),
            q_gain.astype(F32),
            norm2_gain.astype(F32),
            jnp.full((128,), jnp.sum(valid_f)),
        ]
    )
    info = jnp.pad(info, (0, -info.shape[0] % 1024)).reshape(-1, 128)
    own_tags = jnp.stack([blocks.reshape(-1, PIECE)[:, 0], seq_ids.reshape(-1, PIECE)[:, 0]], 1)
    tag = jnp.pad(own_tags.astype(F32).reshape(1, -1), ((0, 7), (0, 128 - 2 * own_pieces)))
    own = jnp.concatenate([blocks.reshape(-1, PIECE)[:, 0], seq_ids[:1]])

    positions = blocks * PIECE + jnp.arange(row_count, dtype=jnp.int32) % PIECE
    freq_table = 10000.0 ** (-(jnp.arange(half_dim, dtype=F32) * 2.0 / head_size))
    angle_table = positions.astype(F32)[:, None] * freq_table[None, :]
    cosine = jnp.cos(angle_table)
    sine = jnp.sin(angle_table)
    fetched = front(
        n_ctx,
        n_f,
        {
            "q_down": q_down,
            "kv_weight": kv_weight,
            "q_up": q_up,
            "out_proj": out_proj,
            "w_gate": w_gate,
            "w_up": w_up,
            "hidden": hidden_in,
            "info": info,
            "tag": tag,
            "cos": cosine,
            "sin": sine,
        },
        head_size,
    )
    w_gatef, w_upf, w_out = fetched["gate_full"], fetched["up_full"], fetched["w_out"]
    all_kv, q_rot = fetched["all_kv"], fetched["q_rot"]
    normed, q_low, q_normed = fetched["normed"], fetched["q_low"], fetched["q_normed"]
    gain_one, gain_q, gain_two = fetched["gain_one"], fetched["gain_q"], fetched["gain_two"]
    tags = fetched["tags"][:, 0, : 2 * own_pieces].reshape(-1, 2).astype(jnp.int32)
    total_count = jnp.sum(fetched["tags"][:, 1, 0])
    hidden_f = hidden_in.astype(F32)
    scale_q = rms_scale(q_low)

    attn_heads, lse = attn_fwd(tags, own, q_rot, all_kv, head_size, seq_pieces)
    resid = hidden_f + dot(attn_heads, w_out)
    scale_two = rms_scale(resid)
    normed_two = (resid * scale_two * gain_two).astype(BF16)

    group_two = gather_tokens(normed_two)
    gate_lin = dot(group_two, w_gatef)
    up_lin = dot(group_two, w_upf)
    sigma = jax.nn.sigmoid(gate_lin)
    silu_gate = gate_lin * sigma
    hidden_act = (silu_gate * up_lin).astype(BF16)
    side = 2 * row_count

    def down_half(j):
        return dot(hidden_act[j * side : (j + 1) * side], w_down)

    result = resid + sum_tokens(down_half)
    diff = result - teacher.astype(F32)
    sq_local = jnp.sum(valid_f * jnp.sum(diff * diff, axis=1))
    grad_y = diff * valid_f[:, None] * (token_total / total_count)
    group_dz = gather_tokens(grad_y.astype(BF16))
    down_part = dot_rows(hidden_act, group_dz).astype(BF16)
    down_give, down_keep = ctx_split(down_part)
    down_got = by_c(down_give, 1)
    group_dz2 = after(group_dz, down_part)
    grad_hidden = dot_t(group_dz2, w_down)
    grad_gate = (grad_hidden * up_lin * sigma * (1.0 + gate_lin * (1.0 - sigma))).astype(BF16)
    grad_up = (grad_hidden * silu_gate).astype(BF16)
    gate_part = dot_rows(group_two, grad_gate).astype(BF16)
    gate_give, gate_keep = ctx_split(gate_part)
    gate_got = by_c(gate_give, 1)

    def back_half(j):
        rows = slice(j * side, (j + 1) * side)
        return dot_t(grad_gate[rows], w_gatef) + dot_t(grad_up[rows], w_upf)

    grad_normed_two = sum_tokens(back_half)
    up_part = dot_rows(group_two, grad_up).astype(BF16)

    grad_resid_norm, grad_gain_two = rms_back(resid, scale_two, gain_two, grad_normed_two)
    grad_resid = grad_y + grad_resid_norm
    grad_branch = grad_resid.astype(BF16)
    grad_attn = dot_t(grad_branch, w_out).astype(BF16)
    down_parts = ctx_spread(ctx_pair(down_keep, after(down_got, grad_attn)))

    grad_qlin, grad_seq = attn_bwd(
        tags, own, q_rot, grad_attn, attn_heads, lse, cosine, sine, all_kv, head_size, seq_pieces
    )
    by_piece = grad_seq.reshape(seq_pieces, PIECE, 2 * head_size)
    piece_tag = tags[:, 0].reshape(n_z, 2, own_pieces)
    piece_own = (tags[:, 1] == seq_ids[0]).reshape(n_z, 2, own_pieces)

    def kv_half(bit):
        places = lax.dynamic_index_in_dim(piece_tag, bit, 1, keepdims=False).reshape(-1)
        picked = by_piece[places]
        if n_ctx * own_pieces != seq_pieces:
            mine = lax.dynamic_index_in_dim(piece_own, bit, 1, keepdims=False).reshape(-1)
            picked = jnp.where(mine[:, None, None], picked, jnp.zeros_like(picked))
        return picked.reshape(n_z, own_pieces * PIECE, 2 * head_size)

    kv_part = jnp.stack([kv_half(0), kv_half(1)], axis=1)
    q_cut, kv_cut = q_width // n_f, 2 * head_size // n_f
    out_block = heads_width // (n_ctx * n_f)
    qlin_group = lax.all_to_all(grad_qlin, "fsdp", 1, 0, tiled=True)
    attn_group = lax.all_to_all(
        attn_heads.reshape(row_count, n_ctx, n_f, out_block), "fsdp", 2, 0, tiled=True
    ).reshape(row_count * n_f, n_ctx * out_block)
    branch_group = group_rows(grad_branch)
    qnorm_group = group_rows(q_normed)
    normed_group = group_rows(normed)

    grad_qnormed = dot_t(grad_qlin, fetched["w_qu"])
    grad_qlow_f, grad_gain_q = rms_back(q_low, scale_q, gain_q, grad_qnormed)
    grad_qlow = grad_qlow_f.astype(BF16)
    da_q = dot_t(grad_qlow, fetched["w_qd"])
    out_part = dot_rows(attn_group, branch_group).astype(BF16)
    qup_part = dot_rows(qnorm_group, qlin_group).astype(BF16)
    gate_pair = ctx_pair(gate_keep, after(gate_got, qup_part))

    def by_ctx(grad):
        return grad.reshape(n_z, 2, grad.shape[0] // n_ctx, grad.shape[1])

    order = [(c * n_f + f, f * n_ctx + c) for c in range(n_ctx) for f in range(n_f)]
    down_rows = ctx_total(after(down_parts, qup_part)).astype(BF16)
    down_sent = lax.ppermute(down_rows, ("ctx", "fsdp"), order)

    small = jnp.concatenate(
        [jnp.zeros((model_width,), F32), grad_gain_q, grad_gain_two, sq_local.reshape(1)]
    )
    entries = small.shape[0]
    small = jnp.pad(small, (0, -entries % 1024)).reshape(-1, 128)
    ends = tail_reduce(
        n_ctx,
        n_f,
        {
            "gate": gate_pair,
            "kv": kv_part,
            "up": by_ctx(up_part),
            "out": by_ctx(out_part),
            "qup": by_ctx(qup_part),
            "dqa": grad_qlow,
            "cos": cosine,
            "sin": sine,
            "normed_group": normed_group,
            "w_kv": fetched["w_kv"],
            "da_q": da_q,
            "hidden": hidden_in,
            "gain_one": gain_one,
            "grad_resid": grad_resid,
            "small": small,
        },
        q_width,
    )
    small = ends["small_out"].reshape(-1)[:entries]
    grad_down = after(down_sent, small).astype(F32)

    device = c_idx * n_f + f_idx
    q1, q2 = model_width, model_width + q_width
    n_dev = n_ctx * n_f

    def own_part(values):
        size = values.shape[0] // n_dev
        return cut(values, device * size, size, 0)

    loss_now = small[-1] / (model_width * total_count)
    return (
        result.astype(BF16),
        loss_now,
        ends["grad_input"],
        own_part(small[:q1]),
        ends["out_qd"],
        own_part(small[q1:q2]),
        ends["out_qup"],
        ends["out_kvw"],
        ends["out_out"],
        own_part(small[q2 : q2 + model_width]),
        ends["out_gate"],
        ends["out_up"],
        grad_down,
    )


def solution(mesh):
    both = ("ctx", "fsdp")
    rows = P(both, None)
    flat = P(both)
    shard = P("fsdp", None)
    gain = P("fsdp")
    return jax.shard_map(
        body,
        mesh=mesh,
        in_specs=(
            rows,
            rows,
            flat,
            flat,
            flat,
            gain,
            shard,
            gain,
            shard,
            shard,
            shard,
            gain,
            shard,
            shard,
            shard,
        ),
        out_specs=(
            rows,
            P(),
            rows,
            flat,
            rows,
            flat,
            rows,
            rows,
            rows,
            flat,
            rows,
            rows,
            rows,
        ),
        check_vma=False,
    )
```

```python
import functools
import math

import jax
import jax.numpy as jnp
from jax import lax
from jax.experimental import pallas as pl
from jax.experimental.pallas import tpu as pltpu
from jax.sharding import PartitionSpec as P

PIECE = 128
SEQ_BLOCKS = 8
NORM_EPS = 1e-05
F32 = jnp.float32
BF16 = jnp.bfloat16
LOG2E = math.log2(math.e)
HEAD_GROUP = 4


def rms_scale(values):
    return lax.rsqrt(jnp.mean(values * values, axis=-1, keepdims=True) + NORM_EPS)


def rms_back(values, scale, gain, grad):
    grad_gain = jnp.sum(grad * values * scale, axis=0)
    ge = gain * grad
    inner = jnp.mean(ge * values, axis=-1, keepdims=True)
    return scale * ge - values * (scale * scale * scale) * inner, grad_gain


def rope_apply(values, cosine, sine):
    half_dim = values.shape[-1] // 2
    one = values[..., :half_dim]
    two = values[..., half_dim:]
    return jnp.concatenate([one * cosine - two * sine, two * cosine + one * sine], axis=-1)


def rope_back(grads, cosine, sine):
    half_dim = grads.shape[-1] // 2
    one = grads[..., :half_dim]
    two = grads[..., half_dim:]
    return jnp.concatenate([one * cosine + two * sine, two * cosine - one * sine], axis=-1)


def after(values, *deps):
    return lax.optimization_barrier((values, deps))[0]


def dot(a, b):
    return jnp.dot(a, b, preferred_element_type=F32)


def dot_t(a, b):
    return lax.dot_general(a, b, (((1,), (1,)), ((), ())), preferred_element_type=F32)


def dot_rows(a, b):
    return lax.dot_general(a, b, (((0,), (0,)), ((), ())), preferred_element_type=F32)


def contract_last(a, b):
    return lax.dot_general(a, b, (((1,), (1,)), ((), ())), preferred_element_type=F32)

def find_pieces(tags_ref, own_ref, pick_ref, total):
    @pl.loop(0, total)
    def _(u):
        @pl.when(tags_ref[u, 1] == own_ref[2])
        def _():
            pick_ref[tags_ref[u, 0]] = u

def stack_heads(ref, hd):
    return jnp.concatenate([ref[:, h*hd:(h+1)*hd] for h in range(HEAD_GROUP)], axis=0)

def attn_fwd_kernel(tags_ref, own_ref, q_ref, kv_ref, o_ref, lse_ref, k_s, vt_s, acc_s, pick_s):
    half = pl.program_id(0)
    hd = k_s.shape[1]
    pieces = k_s.shape[0] // PIECE
    total = kv_ref.shape[0] // PIECE
    wide = 2 * PIECE
    coef = hd ** -0.5 * LOG2E

    @pl.when((half == 0) & (pl.program_id(1) == 0))
    def _():
        find_pieces(tags_ref, own_ref, pick_s, total)
        for i in range(pieces):
            rows = pl.ds(pl.multiple_of(pick_s[i] * PIECE, PIECE), PIECE)
            k_s[i*PIECE:(i+1)*PIECE, :] = kv_ref[rows, :hd]
            vt_s[:, i*PIECE:(i+1)*PIECE] = kv_ref[rows, hd:].T

    q = stack_heads(q_ref, hd)
    acc_s[...] = jnp.zeros_like(acc_s)
    rows = q.shape[0]
    def step(i, carry):
        peak, total_p = carry
        at = pl.ds(pl.multiple_of(i * wide, wide), wide)
        raw = contract_last(k_s[at, :], q)
        top = jnp.maximum(peak, jnp.max(raw, axis=0, keepdims=True))
        fade = jnp.exp2((peak - top) * coef)
        p = jnp.exp2((raw - top) * coef)
        acc_s[...] = acc_s[...] * fade + jnp.dot(vt_s[:, at], p.astype(BF16), preferred_element_type=F32)
        return top, total_p * fade + jnp.sum(p, axis=0, keepdims=True)
    count = own_ref[half] // 2 + 1
    peak, total_p = lax.fori_loop(0, count, step, (jnp.full((1, rows), -1e30, F32), jnp.zeros((1, rows), F32)))
    out = (acc_s[...] / total_p).astype(BF16).T
    for h in range(HEAD_GROUP):
        o_ref[:, h*hd:(h+1)*hd] = out[h*PIECE:(h+1)*PIECE, :]
    lse_ref[0] = peak * coef + jnp.log2(total_p)

def attn_fwd(tags, own, q, kv, hd, pieces):
    n_rows, width = q.shape
    groups = width // hd // HEAD_GROUP
    gw = HEAD_GROUP * hd
    halves = n_rows // PIECE
    rows = HEAD_GROUP * PIECE
    blk = pl.BlockSpec((PIECE, gw), lambda p, g, *_: (p, g))
    flops = 4 * n_rows * width * pieces * PIECE * 9 // 16
    return pl.pallas_call(
        attn_fwd_kernel,
        out_shape=(jax.ShapeDtypeStruct(q.shape, BF16), jax.ShapeDtypeStruct((halves*groups, 1, rows), F32)),
        grid_spec=pltpu.PrefetchScalarGridSpec(
            num_scalar_prefetch=2, grid=(halves, groups),
            in_specs=[blk, pl.BlockSpec(kv.shape, lambda p, g, *_: (0, 0))],
            out_specs=[blk, pl.BlockSpec((1, 1, rows), lambda p, g, *_: (p*groups+g, 0, 0))],
            scratch_shapes=[pltpu.VMEM((pieces*PIECE, hd), BF16), pltpu.VMEM((hd, pieces*PIECE), BF16),
                            pltpu.VMEM((hd, rows), F32), pltpu.SMEM((pieces,), jnp.int32)]),
        compiler_params=pltpu.CompilerParams(vmem_limit_bytes=40 << 20),
        cost_estimate=pl.CostEstimate(flops=flops, transcendentals=flops//(4*hd), bytes_accessed=2*(2*q.size+kv.size)),
        name="attn_fwd",
    )(tags, own, q, kv)

def attn_bwd_kernel(tags_ref, own_ref, q_ref, do_ref, o_ref, lse_ref, cos_ref, sin_ref, kv_ref, dq_ref, dkv_ref,
                    k_s, kt_s, v_s, dq_s, dk_s, dv_s, pick_s):
    half = pl.program_id(0)
    group = pl.program_id(1)
    hd = k_s.shape[1]
    pieces = k_s.shape[0] // PIECE
    total = kv_ref.shape[0] // PIECE
    wide = 2 * PIECE
    coef = hd ** -0.5 * LOG2E
    scale = hd ** -0.5

    @pl.when((half == 0) & (group == 0))
    def _():
        find_pieces(tags_ref, own_ref, pick_s, total)
        for i in range(pieces):
            rows = pl.ds(pl.multiple_of(pick_s[i] * PIECE, PIECE), PIECE)
            keys = kv_ref[rows, :hd]
            k_s[i*PIECE:(i+1)*PIECE, :] = keys
            kt_s[:, i*PIECE:(i+1)*PIECE] = keys.T
            v_s[i*PIECE:(i+1)*PIECE, :] = kv_ref[rows, hd:]
        dk_s[...] = jnp.zeros_like(dk_s)
        dv_s[...] = jnp.zeros_like(dv_s)

    q = stack_heads(q_ref, hd)
    do = stack_heads(do_ref, hd)
    prod = do.astype(F32) * stack_heads(o_ref, hd).astype(F32)
    delta = lax.dot_general(jnp.ones((8, hd), F32), prod, (((1,), (1,)), ((), ())),
                            preferred_element_type=F32, precision=lax.Precision.HIGHEST)[:1]
    lse = lse_ref[0]
    dq_s[...] = jnp.zeros_like(dq_s)
    def step(i, carry):
        at = pl.ds(pl.multiple_of(i * wide, wide), wide)
        p = jnp.exp2(contract_last(k_s[at, :], q) * coef - lse)
        dp = contract_last(v_s[at, :], do)
        ds = (p * (dp - delta)).astype(BF16)
        dv_s[at, :] += jnp.dot(p.astype(BF16), do, preferred_element_type=F32)
        dk_s[at, :] += jnp.dot(ds, q, preferred_element_type=F32)
        dq_s[...] += jnp.dot(kt_s[:, at], ds, preferred_element_type=F32)
        return carry
    lax.fori_loop(0, own_ref[half] // 2 + 1, step, 0)
    dq = (dq_s[...] * scale).T
    cos, sin = cos_ref[...], sin_ref[...]
    mid = hd // 2
    for h in range(HEAD_GROUP):
        one = dq[h*PIECE:(h+1)*PIECE, :mid]
        two = dq[h*PIECE:(h+1)*PIECE, mid:]
        dq_ref[:, h*hd:h*hd+mid] = (one * cos + two * sin).astype(BF16)
        dq_ref[:, h*hd+mid:(h+1)*hd] = (two * cos - one * sin).astype(BF16)

    @pl.when((half == pl.num_programs(0) - 1) & (group == pl.num_programs(1) - 1))
    def _():
        dkv_ref[:, :hd] = (dk_s[...] * scale).astype(BF16)
        dkv_ref[:, hd:] = dv_s[...].astype(BF16)

def attn_bwd(tags, own, q, do, o, lse, cos, sin, kv, hd, pieces):
    n_rows, width = q.shape
    groups = width // hd // HEAD_GROUP
    gw = HEAD_GROUP * hd
    halves = n_rows // PIECE
    rows = HEAD_GROUP * PIECE
    blk = pl.BlockSpec((PIECE, gw), lambda p, g, *_: (p, g))
    trig = pl.BlockSpec((PIECE, hd // 2), lambda p, g, *_: (p, 0))
    keys = pieces * PIECE
    flops = 10 * n_rows * width * keys * 9 // 16
    return pl.pallas_call(
        attn_bwd_kernel,
        out_shape=(jax.ShapeDtypeStruct(q.shape, BF16), jax.ShapeDtypeStruct((keys, 2*hd), BF16)),
        grid_spec=pltpu.PrefetchScalarGridSpec(
            num_scalar_prefetch=2, grid=(halves, groups),
            in_specs=[blk, blk, blk, pl.BlockSpec((1, 1, rows), lambda p, g, *_: (p*groups+g, 0, 0)), trig, trig,
                      pl.BlockSpec(kv.shape, lambda p, g, *_: (0, 0))],
            out_specs=[blk, pl.BlockSpec((keys, 2*hd), lambda p, g, *_: (0, 0))],
            scratch_shapes=[pltpu.VMEM((keys, hd), BF16), pltpu.VMEM((hd, keys), BF16), pltpu.VMEM((keys, hd), BF16),
                            pltpu.VMEM((hd, rows), F32), pltpu.VMEM((keys, hd), F32), pltpu.VMEM((keys, hd), F32),
                            pltpu.SMEM((pieces,), jnp.int32)]),
        compiler_params=pltpu.CompilerParams(vmem_limit_bytes=48 << 20),
        cost_estimate=pl.CostEstimate(flops=flops, transcendentals=flops//(10*hd), bytes_accessed=2*(4*q.size+2*kv.size)),
        name="attn_bwd",
    )(tags, own, q, do, o, lse, cos, sin, kv)

MESH = pl.DeviceIdType.MESH


def flip(index, mask):
    out = 0
    bit = 1
    while bit <= mask:
        part = (index // bit) % 2
        out = out + bit * ((1 - part) if mask & bit else part)
        bit *= 2
    return out + (index // bit) * bit


def row_loop(rows, body, step=32):
    if rows % step:
        step = 16

    @pl.loop(0, rows // step)
    def _(i):
        body(pl.ds(pl.multiple_of(i * step, step), step))


class Sender:
    def __init__(self):
        self.open = []

    def make(self, src, dst, send_sem, recv_sem, peer):
        return pltpu.make_async_remote_copy(
            src_ref=src,
            dst_ref=dst,
            send_sem=send_sem,
            recv_sem=recv_sem,
            device_id=peer,
            device_id_type=MESH,
        )

    def __call__(self, *args):
        copy = self.make(*args)
        copy.start()
        self.open.append(copy)
        return copy

    def finish(self):
        for copy in self.open:
            copy.wait_send()


class LineSum:
    def __init__(self, own, got, send_sem, recv_sem, c_idx, f_idx, n_z, sender):
        self.own, self.got, self.send_sem, self.recv_sem = own, got, send_sem, recv_sem
        self.n_z, self.sender = n_z, sender
        self.z = c_idx // 2
        self.left = (c_idx - 2, f_idx)
        self.right = (c_idx + 2, f_idx)

    def copy(self, b, slot, peer):
        return self.sender.make(
            self.own.at[b], self.got.at[slot], self.send_sem.at[b], self.recv_sem.at[slot], peer
        )

    def take(self, b, slot):
        self.copy(b, slot, self.left).wait_recv()

        def add(at):
            self.own[b, at, :] = (
                self.own[b, at, :].astype(F32) + self.got[slot, at, :].astype(F32)
            ).astype(BF16)

        row_loop(self.own.shape[1], add)

    def step(self, i):
        z, n_z = self.z, self.n_z
        up, down = n_z - 1 - i, i

        @pl.when(z < up)
        def _():
            @pl.when(z > 0)
            def _():
                self.take(up, up)

            self.copy(up, up, self.right).start()

        @pl.when(z > down)
        def _():
            @pl.when(z < n_z - 1)
            def _():
                self.take(down, down)

            @pl.when(z - 1 > down)
            def _():
                self.copy(down, down, self.left).start()

            @pl.when(z - 1 == down)
            def _():
                self.copy(down, n_z, self.left).start()

    def total(self, store):
        z, n_z = self.z, self.n_z

        @pl.when(z > 0)
        def _():
            self.copy(z, z, self.left).wait_recv()

        @pl.when(z < n_z - 1)
        def _():
            self.copy(z, n_z, self.left).wait_recv()

        rows = self.own.shape[1]

        @pl.when(z == 0)
        def _():
            row_loop(
                rows,
                lambda at: store(
                    at, self.own[z, at, :].astype(F32) + self.got[n_z, at, :].astype(F32)
                ),
            )

        @pl.when(z == n_z - 1)
        def _():
            row_loop(
                rows,
                lambda at: store(
                    at, self.own[z, at, :].astype(F32) + self.got[z, at, :].astype(F32)
                ),
            )

        @pl.when((z > 0) & (z < n_z - 1))
        def _():
            row_loop(
                rows,
                lambda at: store(
                    at,
                    self.own[z, at, :].astype(F32)
                    + self.got[z, at, :].astype(F32)
                    + self.got[n_z, at, :].astype(F32),
                ),
            )

    def finish(self):
        for b in range(self.n_z):

            @pl.when(self.z != b)
            def _(b=b):
                self.copy(b, b, self.left).wait_send()


WINDOW = 3
TAIL_NAMES = ("gate", "kv", "up", "out", "qup", "qd", "kvw")
TAIL_CUT = ("gate", "up", "qup", "qd", "kvw")
TAIL_SENT = ("kv", "up", "out", "qup", "qd", "kvw")


def tail_kernel(n_ctx, n_f, names_in, names_out, names_scratch, *refs):
    n_z = n_ctx // 2
    names = list(names_in) + list(names_out) + list(names_scratch)
    r = dict(zip(names, refs, strict=True))
    c_idx = lax.axis_index("ctx")
    f_idx = lax.axis_index("fsdp")
    y_idx = c_idx % 2
    z_idx = c_idx // 2
    send = Sender()

    def over_c(mask):
        return (flip(c_idx, mask), f_idx)

    def over_f(mask):
        return (c_idx, flip(f_idx, mask))

    barrier = pltpu.get_barrier_semaphore()
    for mask in range(1, n_f):
        pl.semaphore_signal(barrier, inc=1, device_id=over_f(mask), device_id_type=MESH)
    for mask in range(1, n_ctx):
        pl.semaphore_signal(barrier, inc=1, device_id=over_c(mask), device_id_type=MESH)
    pl.semaphore_wait(barrier, n_f - 1 + n_ctx - 1)

    lines = {
        m: LineSum(
            r["pair_" + m],
            r["z_" + m],
            r["z_send"].at[i],
            r["z_recv"].at[i],
            c_idx,
            f_idx,
            n_z,
            send,
        )
        for i, m in enumerate(TAIL_NAMES)
    }
    order = list(range(1, n_z)) + [0]
    y_copies, keeps = {}, {}

    parts = {m: r[m] for m in ("kv", "up", "out", "qup")}
    parts["qd"], parts["kvw"] = r["part_qd"], r["part_kvw"]
    queue = [(m, s) for m in TAIL_SENT for s in order]

    def next_y():
        if queue:
            m, s = queue.pop(0)
            i = TAIL_SENT.index(m)
            b = flip(z_idx, s)
            y_copies[m, s] = send(
                parts[m].at[b, 1 - y_idx],
                r["y_" + m].at[s],
                r["y_send"].at[i, s],
                r["y_recv"].at[i, s],
                over_c(1),
            )
            keep = pltpu.make_async_copy(
                parts[m].at[b, y_idx], r["pair_" + m].at[b], r["keep_sem"].at[i, s]
            )
            keep.start()
            keeps[m, s] = keep

    def add_pair(m, s):
        b = flip(z_idx, s)
        y_copies[m, s].wait_recv()
        next_y()
        keeps[m, s].wait()
        pair, got = r["pair_" + m], r["y_" + m]

        def add(at):
            pair[b, at, :] = (pair[b, at, :].astype(F32) + got[s, at, :].astype(F32)).astype(BF16)

        row_loop(pair.shape[1], add)

    def advance(pair, line):
        for i, s in enumerate(order):
            if pair is not None:
                add_pair(pair, s)
            if line is not None and i < n_z - 1:
                lines[line].step(i)

    f_copies = {}

    def finish_sum(m):
        lines[m].total(lambda at, value: store_total(m, at, value))
        if m in TAIL_CUT:
            i = TAIL_CUT.index(m)
            part = r["tot_" + m].shape[0] // n_f
            for s in range(1, n_f):
                at = pl.ds(pl.multiple_of(flip(f_idx, s) * part, part), part)
                f_copies[m, s] = send(
                    r["tot_" + m].at[at, :],
                    r["f_" + m].at[s - 1],
                    r["f_send"].at[i, s - 1],
                    r["f_recv"].at[i, s - 1],
                    over_f(s),
                )

    def store_total(m, at, value):
        if m in TAIL_CUT:
            r["tot_" + m][at, :] = value.astype(BF16)
        else:
            r["out_" + m][at, :] = value

    def put_out(m):
        total, out = r["tot_" + m], r["out_" + m]
        rows, width = total.shape
        part = rows // n_f
        for s in range(n_f):
            at = pl.ds(pl.multiple_of(flip(f_idx, s) * width, 128), width)
            if s:
                f_copies[m, s].wait_recv()
                out[:, at] = r["f_" + m][s - 1].astype(F32)
            else:
                mine = pl.ds(pl.multiple_of(f_idx * part, part), part)
                out[:, at] = total[mine, :].astype(F32)

    def cut_low(src, dst, width, index):
        rows = src.shape[0]
        mine = pl.ds(pl.multiple_of(f_idx * rows, rows), rows)
        copies = []
        for s in range(1, n_f):
            at = pl.ds(pl.multiple_of(flip(f_idx, s) * width, 128), width)
            copies.append(
                send(
                    src.at[:, at],
                    dst.at[mine, :],
                    r["low_send"].at[index, s - 1],
                    r["low_recv"].at[index, s - 1],
                    over_f(s),
                )
            )
        own = pl.ds(pl.multiple_of(f_idx * width, 128), width)
        dst[mine, :] = src[:, own]
        return copies

    for _ in range(WINDOW):
        next_y()
    q_copies = cut_low(r["dqa"], r["qd_group"], r["qd_group"].shape[1], 0)
    pair_in = pltpu.make_async_copy(r["gate"], r["pair_gate"], r["keep_sem"].at[0, n_z])
    pair_in.start()
    pair_in.wait()
    advance("kv", "gate")
    advance("up", "kv")
    finish_sum("gate")

    head = r["dkv"].shape[1] // 2
    mid = head // 2

    def store_kv(at, value):
        cos, sin = r["cos"][at, :], r["sin"][at, :]
        one, two = value[:, :mid], value[:, mid:head]
        r["dkv"][at, :mid] = (one * cos + two * sin).astype(BF16)
        r["dkv"][at, mid:head] = (two * cos - one * sin).astype(BF16)
        r["dkv"][at, head:] = value[:, head:].astype(BF16)

    lines["kv"].total(store_kv)
    kv_copies = cut_low(r["dkv"], r["kv_group"], r["kv_group"].shape[1], 1)

    def low_part(group, part):
        normed = r["normed_group"]
        rows = part.shape[2]
        for c in range(n_ctx):
            part[c // 2, c % 2] = lax.dot_general(
                normed[:, c * rows : (c + 1) * rows],
                group[...],
                (((0,), (0,)), ((), ())),
                preferred_element_type=F32,
            ).astype(BF16)

    for copy in q_copies:
        copy.wait_recv()
    low_part(r["qd_group"], r["part_qd"])
    advance("out", "up")
    for copy in kv_copies:
        copy.wait_recv()
    low_part(r["kv_group"], r["part_kvw"])

    grad_in, w_kv = r["grad_input"], r["w_kv"]
    width = grad_in.shape[1]
    tile = 256

    @pl.loop(0, width // tile)
    def _(t):
        at = pl.ds(pl.multiple_of(t * tile, tile), tile)
        grad_in[:, at] = r["da_q"][:, at] + lax.dot_general(
            r["dkv"][...],
            w_kv[at, :],
            (((1,), (1,)), ((), ())),
            preferred_element_type=F32,
        )

    r["gain_sum"][...] = jnp.zeros_like(r["gain_sum"])
    gain = r["gain_one"][...]

    def norm_rows(at):
        value = r["hidden"][at, :].astype(F32)
        grad = grad_in[at, :]
        scale = lax.rsqrt(jnp.mean(value * value, axis=-1, keepdims=True) + NORM_EPS)
        r["gain_sum"][...] += jnp.sum(grad * value * scale, axis=0, keepdims=True)
        ge = gain * grad
        inner = jnp.mean(ge * value, axis=-1, keepdims=True)
        grad_in[at, :] = (
            r["grad_resid"][at, :] + scale * ge - value * (scale * scale * scale) * inner
        )

    row_loop(grad_in.shape[0], norm_rows, step=16)

    small, small_got = r["small_out"], r["small_got"]
    small[...] = r["small"][...]
    for i in range(width // 128):
        small[i : i + 1, :] = r["gain_sum"][:, i * 128 : (i + 1) * 128]
    steps = [over_f(1), over_f(2), over_c(1)]
    mask = 2
    while mask < n_ctx:
        steps.append(over_c(mask))
        mask *= 2
    small_copies = {}

    def small_start(s):
        small_got[s, 0] = small[...]
        small_copies[s] = send(
            small_got.at[s, 0],
            small_got.at[s, 1],
            r["s_send"].at[s],
            r["s_recv"].at[s],
            steps[s],
        )

    def small_end(s):
        small_copies[s].wait_recv()
        small[...] = small[...] + small_got[s, 1]

    for s in range(2):
        small_start(s)
        small_end(s)
    small_start(2)

    put_out("gate")
    advance("qup", "out")
    finish_sum("up")
    advance("qd", "qup")
    finish_sum("out")
    small_end(2)
    small_start(3)
    advance("kvw", "qd")
    put_out("up")
    finish_sum("qup")
    advance(None, "kvw")
    for s in range(3, len(steps)):
        if s > 3:
            small_start(s)
        small_end(s)
    finish_sum("qd")
    finish_sum("kvw")
    for m in ("qup", "qd", "kvw"):
        put_out(m)
    send.finish()
    for m in TAIL_NAMES:
        lines[m].finish()


def tail_reduce(n_ctx, n_f, inputs, q_width):
    n_z = n_ctx // 2
    vmem = pl.BlockSpec(memory_space=pltpu.VMEM)
    anywhere = pl.BlockSpec(memory_space=pl.ANY)
    rows, width = inputs["hidden"].shape
    kv_width = inputs["w_kv"].shape[1]
    in_hbm = ("gate", "kv", "up", "out", "qup")
    names_in = tuple(inputs)
    in_specs = [anywhere if m in in_hbm else vmem for m in names_in]
    block = {m: inputs[m].shape[-2:] for m in in_hbm}
    block["qd"] = (width // n_ctx, q_width // n_f)
    block["kvw"] = (width // n_ctx, kv_width // n_f)
    outs = {
        "small_out": jax.ShapeDtypeStruct(inputs["small"].shape, F32),
        "grad_input": jax.ShapeDtypeStruct((rows, width), F32),
    }
    scratch = {}
    for m in TAIL_NAMES:
        high, wide = block[m]
        scratch["pair_" + m] = pltpu.VMEM((n_z, high, wide), BF16)
        scratch["z_" + m] = pltpu.VMEM((n_z + 1, high, wide), BF16)
        if m in TAIL_SENT:
            scratch["y_" + m] = pltpu.VMEM((n_z, high, wide), BF16)
        if m in TAIL_CUT:
            scratch["tot_" + m] = pltpu.VMEM((high, wide), BF16)
            scratch["f_" + m] = pltpu.VMEM((n_f - 1, high // n_f, wide), BF16)
            outs["out_" + m] = jax.ShapeDtypeStruct((high // n_f, wide * n_f), F32)
        elif m != "kv":
            outs["out_" + m] = jax.ShapeDtypeStruct((high, wide), F32)
    scratch["dkv"] = pltpu.VMEM((rows, kv_width), BF16)
    scratch["qd_group"] = pltpu.VMEM((rows * n_f, q_width // n_f), BF16)
    scratch["kv_group"] = pltpu.VMEM((rows * n_f, kv_width // n_f), BF16)
    scratch["part_qd"] = pltpu.VMEM((n_z, 2) + block["qd"], BF16)
    scratch["part_kvw"] = pltpu.VMEM((n_z, 2) + block["kvw"], BF16)
    scratch["gain_sum"] = pltpu.VMEM((1, width), F32)
    steps = 2 + (n_ctx.bit_length() - 1)
    scratch["small_got"] = pltpu.VMEM((steps, 2) + inputs["small"].shape, F32)
    dma = pltpu.SemaphoreType.DMA
    sent, cut = len(TAIL_SENT), len(TAIL_CUT)
    scratch["s_send"] = dma((steps,))
    scratch["s_recv"] = dma((steps,))
    scratch["y_send"] = dma((sent, n_z))
    scratch["y_recv"] = dma((sent, n_z))
    scratch["keep_sem"] = dma((sent, n_z + 1))
    scratch["z_send"] = dma((len(TAIL_NAMES), n_z))
    scratch["z_recv"] = dma((len(TAIL_NAMES), n_z + 1))
    scratch["f_send"] = dma((cut, n_f - 1))
    scratch["f_recv"] = dma((cut, n_f - 1))
    scratch["low_send"] = dma((2, n_f - 1))
    scratch["low_recv"] = dma((2, n_f - 1))
    values = pl.pallas_call(
        functools.partial(tail_kernel, n_ctx, n_f, names_in, tuple(outs), tuple(scratch)),
        out_shape=tuple(outs.values()),
        in_specs=in_specs,
        out_specs=tuple([vmem] * len(outs)),
        scratch_shapes=list(scratch.values()),
        compiler_params=pltpu.CompilerParams(
            collective_id=0, has_side_effects=True, vmem_limit_bytes=60 << 20
        ),
        name="tail_reduce",
    )(*inputs.values())
    return dict(zip(outs, values, strict=True))


def front_kernel(n_ctx, n_f, names, *refs):
    r = dict(zip(names, refs, strict=True))
    n_z = n_ctx // 2
    c_idx = lax.axis_index("ctx")
    f_idx = lax.axis_index("fsdp")
    y_idx = c_idx % 2
    z_bit = (c_idx // 2) % 2
    x_idx = f_idx // 2
    k_idx = f_idx % 2
    far_idx = flip(f_idx, 2)
    moves = Sender()
    local = []
    at_sem = [0]

    def over_c(mask):
        return (flip(c_idx, mask), f_idx)

    def over_f(mask):
        return (c_idx, flip(f_idx, mask))

    def send(src, dst, peer):
        i = at_sem[0]
        at_sem[0] += 1
        return moves(src, dst, r["send_sem"].at[i], r["recv_sem"].at[i], peer)

    def keep(src, dst):
        copy = pltpu.make_async_copy(src, dst, r["local_sem"].at[len(local)])
        copy.start()
        local.append(copy)
        return copy

    def rows(start, size):
        return pl.ds(pl.multiple_of(start, size), size)

    barrier = pltpu.get_barrier_semaphore()
    for mask in range(1, n_f):
        pl.semaphore_signal(barrier, inc=1, device_id=over_f(mask), device_id_type=MESH)
    for mask in range(1, n_ctx):
        pl.semaphore_signal(barrier, inc=1, device_id=over_c(mask), device_id_type=MESH)
    pl.semaphore_wait(barrier, n_f - 1 + n_ctx - 1)

    infos, tags = r["infos"], r["tags"]
    infos[f_idx] = r["info"][...]
    info_copies = [
        send(infos.at[f_idx], infos.at[f_idx], over_f(mask)) for mask in range(1, n_f)
    ]

    class Rows:
        def __init__(self, shard, dest, bit, hop, chunks):
            self.dest, self.bit, self.hop = dest, bit, hop
            self.shard = shard
            self.size = shard.shape[0]
            self.half = self.size // 2
            self.step = self.half // chunks
            self.chunks = chunks
            self.far, self.next, self.cross = [], [], []

        def start(self):
            mine = self.dest.at[rows(f_idx * self.size, self.size)]
            self.kept = keep(self.shard, mine)
            self.cross.append(send(self.shard, mine, over_f(1)))

        def reach(self, i):
            part = self.bit * self.half + i * self.step
            self.far.append(
                send(
                    self.shard.at[rows(part, self.step)],
                    self.dest.at[rows(f_idx * self.size + part, self.step)],
                    over_f(2),
                )
            )

        def place(self, bit, i):
            return self.dest.at[rows(far_idx * self.size + bit * self.half + i * self.step, self.step)]

        def hop_on(self, i):
            self.far[i].wait_recv()
            reach_next()
            here = self.place(self.bit, i)
            self.next.append(send(here, here, over_c(self.hop)))
            self.cross.append(send(here, here, over_f(1)))

        def pass_on(self, i):
            self.next[i].wait_recv()
            here = self.place(1 - self.bit, i)
            self.cross.append(send(here, here, over_f(1)))

        def end(self):
            for copy in self.cross:
                copy.wait_recv()

    class Columns:
        def __init__(self, shard, dest, box, bits, hops):
            self.shard, self.dest, self.box = shard, dest, box
            self.bits, self.hops = bits, hops
            self.size = shard.shape[0]
            self.width = dest.shape[1]
            self.quarter = self.size // 4

        def columns(self, start, count=1):
            return pl.ds(pl.multiple_of(start * self.width, 128), count * self.width)

        def start(self):
            mine = self.dest.at[rows(f_idx * self.size, self.size)]
            keep(self.shard.at[:, self.columns(f_idx)], mine)
            self.cross = [send(self.shard.at[:, self.columns(flip(f_idx, 1))], mine, over_f(1))]

        def reach(self, i):
            one, two = self.bits
            at = rows((two * 2 + one) * self.quarter, self.quarter)
            self.far = send(
                self.shard.at[at, self.columns((1 - x_idx) * 2, 2)], self.box.at[at], over_f(2)
            )

        def piece(self, one, two):
            return self.box.at[rows((two * 2 + one) * self.quarter, self.quarter)]

        def first(self):
            one, two = self.bits
            self.far.wait_recv()
            reach_next()
            here = self.piece(one, two)
            self.step = send(here, here, over_c(self.hops[0]))
            self.last = [send(here, here, over_c(self.hops[1]))]

        def second(self):
            one, two = self.bits
            self.step.wait_recv()
            here = self.piece(1 - one, two)
            self.last.append(send(here, here, over_c(self.hops[1])))

        def part(self):
            for copy in self.last:
                copy.wait_recv()
            there = self.dest.at[rows(far_idx * self.size, self.size)]
            self.cross.append(send(self.box.at[:, self.columns(1 - k_idx)], there, over_f(1)))
            keep(self.box.at[:, self.columns(k_idx)], there)

        def end(self):
            for copy in self.cross:
                copy.wait_recv()

    kv = Rows(r["kv_weight"], r["kv_full"], y_idx, 1, 1)
    qd = Rows(r["q_down"], r["qd_full"], y_idx, 1, 1)
    qu = Rows(r["q_up"], r["qu_full"], y_idx, 1, 2)
    out = Rows(r["out_proj"], r["w_out"], z_bit, 2, 4)
    gate = Columns(r["w_gate"], r["gate_full"], r["gate_box"], (y_idx, z_bit), (1, 2))
    up = Columns(r["w_up"], r["up_full"], r["up_box"], (z_bit, y_idx), (2, 1))
    queue = [(kv, 0), (qd, 0), (qu, 0), (qu, 1), (gate, 0), (up, 0)]
    queue += [(out, i) for i in range(out.chunks)]

    def reach_next():
        if queue:
            part, i = queue.pop(0)
            part.reach(i)

    reach_next()
    reach_next()
    kv.start()
    qd.start()

    for copy in info_copies:
        copy.wait_recv()
    d1 = r["gain_one"].shape[1] // n_f // 128
    d2 = r["gain_q"].shape[1] // n_f // 128
    count = infos[0, 2 * d1 + d2 : 2 * d1 + d2 + 1, :]
    for f in range(n_f):
        for i in range(d1):
            col = slice((f * d1 + i) * 128, (f * d1 + i + 1) * 128)
            r["gain_one"][:, col] = infos[f, i : i + 1, :]
            r["gain_two"][:, col] = infos[f, d1 + d2 + i : d1 + d2 + i + 1, :]
        for i in range(d2):
            col = slice((f * d2 + i) * 128, (f * d2 + i + 1) * 128)
            r["gain_q"][:, col] = infos[f, d1 + i : d1 + i + 1, :]
        if f:
            count = count + infos[f, 2 * d1 + d2 : 2 * d1 + d2 + 1, :]
    tags[c_idx] = r["tag"][...]
    tags[c_idx, 1:2, :] = count
    tag_copies = [send(tags.at[c_idx], tags.at[c_idx], over_c(mask)) for mask in range(1, n_ctx)]

    normed = r["normed"]
    gain_one = r["gain_one"][...]

    def norm_rows(at):
        value = r["hidden"][at, :].astype(F32)
        scale = lax.rsqrt(jnp.mean(value * value, axis=-1, keepdims=True) + NORM_EPS)
        normed[at, :] = (value * scale * gain_one).astype(BF16)

    row_loop(normed.shape[0], norm_rows, step=16)

    kv.hop_on(0)
    qd.hop_on(0)
    qu.start()
    kv.pass_on(0)
    qd.pass_on(0)
    kv.end()
    kv.kept.wait()
    head = r["kv_full"].shape[1] // 2
    mid = head // 2
    cos, sin = r["cos"], r["sin"]
    kv_rows = r["kv_rows"]
    keys = jnp.dot(normed[...], r["kv_full"][:, :head], preferred_element_type=F32)
    one, two = keys[:, :mid], keys[:, mid:]
    kv_rows[:, :mid] = (one * cos[...] - two * sin[...]).astype(BF16)
    kv_rows[:, mid:head] = (two * cos[...] + one * sin[...]).astype(BF16)
    kv_rows[:, head:] = jnp.dot(
        normed[...], r["kv_full"][:, head:], preferred_element_type=F32
    ).astype(BF16)
    all_kv = r["all_kv"]
    tokens = normed.shape[0]

    def kv_place(c):
        return all_kv.at[rows(c * tokens, tokens)]

    kv_z = [send(kv_rows, kv_place(c_idx), over_c(2 * s)) for s in range(1, n_z)]
    kv_y = [send(kv_rows, kv_place(c_idx), over_c(1))]
    keep(kv_rows, kv_place(c_idx))
    qu.hop_on(0)
    qd.end()
    qd.kept.wait()

    @pl.loop(0, r["q_low"].shape[1] // 256)
    def _(t):
        at = pl.ds(pl.multiple_of(t * 256, 256), 256)
        r["q_low"][:, at] = jnp.dot(
            normed[...], r["qd_full"][:, at], preferred_element_type=F32
        )

    gain_q = r["gain_q"][...]

    def norm_low(at):
        value = r["q_low"][at, :]
        scale = lax.rsqrt(jnp.mean(value * value, axis=-1, keepdims=True) + NORM_EPS)
        r["q_normed"][at, :] = (value * scale * gain_q).astype(BF16)

    row_loop(tokens, norm_low, step=16)
    qu.hop_on(1)
    for s in range(1, n_z):
        kv_z[s - 1].wait_recv()
        here = kv_place(flip(c_idx, 2 * s))
        kv_y.append(send(here, here, over_c(1)))
    qu.pass_on(0)
    qu.pass_on(1)
    gate.first()
    qu.end()
    for part in (gate, up, out):
        part.start()
    qu.kept.wait()

    @pl.loop(0, r["q_rot"].shape[1] // head)
    def _(h):
        start = pl.multiple_of(h * head, head)
        value = jnp.dot(
            r["q_normed"][...],
            r["qu_full"][:, pl.ds(start, head)],
            preferred_element_type=F32,
        )
        one, two = value[:, :mid], value[:, mid:]
        r["q_rot"][:, pl.ds(start, mid)] = (one * cos[...] - two * sin[...]).astype(BF16)
        late = pl.multiple_of(h * head + mid, mid)
        r["q_rot"][:, pl.ds(late, mid)] = (two * cos[...] + one * sin[...]).astype(BF16)

    up.first()
    for m in ("kv", "qd", "qu"):
        keep(r[m + "_full"], r["w_" + m])
    gate.second()
    out.hop_on(0)
    up.second()
    for i in range(1, out.chunks):
        out.hop_on(i)
    gate.part()
    for i in range(out.chunks):
        out.pass_on(i)
    up.part()
    for copy in kv_y + tag_copies:
        copy.wait_recv()
    for part in (gate, up, out):
        part.end()
    for copy in local:
        if not any(copy is part.kept for part in (kv, qd, qu)):
            copy.wait()
    moves.finish()


def front(n_ctx, n_f, inputs, head_size):
    tokens, width = inputs["hidden"].shape
    shape = jax.ShapeDtypeStruct
    q_width = inputs["q_down"].shape[1]
    heads_width = inputs["q_up"].shape[1]
    part = inputs["w_gate"].shape[1] // n_f

    def whole(m):
        return (inputs[m].shape[0] * n_f, inputs[m].shape[1])

    in_hbm = ("q_down", "kv_weight", "q_up", "out_proj", "w_gate", "w_up")
    outs = {
        "w_qd": shape(whole("q_down"), BF16),
        "w_kv": shape(whole("kv_weight"), BF16),
        "w_qu": shape(whole("q_up"), BF16),
        "w_out": shape(whole("out_proj"), BF16),
        "gate_full": shape((width, part), BF16),
        "up_full": shape((width, part), BF16),
        "all_kv": shape((tokens * n_ctx, 2 * head_size), BF16),
        "normed": shape((tokens, width), BF16),
        "q_low": shape((tokens, q_width), F32),
        "q_normed": shape((tokens, q_width), BF16),
        "q_rot": shape((tokens, heads_width), BF16),
        "gain_one": shape((1, width), F32),
        "gain_q": shape((1, q_width), F32),
        "gain_two": shape((1, width), F32),
        "tags": shape((n_ctx, 8, 128), F32),
    }
    out_hbm = ("w_qd", "w_kv", "w_qu", "w_out", "gate_full", "up_full", "all_kv")
    box = (inputs["w_gate"].shape[0], 2 * part)
    dma = pltpu.SemaphoreType.DMA
    scratch = {
        "infos": pltpu.VMEM((n_f,) + inputs["info"].shape, F32),
        "qd_full": pltpu.VMEM(whole("q_down"), BF16),
        "kv_full": pltpu.VMEM(whole("kv_weight"), BF16),
        "qu_full": pltpu.VMEM(whole("q_up"), BF16),
        "gate_box": pltpu.VMEM(box, BF16),
        "up_box": pltpu.VMEM(box, BF16),
        "kv_rows": pltpu.VMEM((tokens, 2 * head_size), BF16),
        "send_sem": dma((64 + 2 * n_ctx,)),
        "recv_sem": dma((64 + 2 * n_ctx,)),
        "local_sem": dma((16,)),
    }
    vmem = pl.BlockSpec(memory_space=pltpu.VMEM)
    anywhere = pl.BlockSpec(memory_space=pl.ANY)
    names = tuple(inputs) + tuple(outs) + tuple(scratch)
    values = pl.pallas_call(
        functools.partial(front_kernel, n_ctx, n_f, names),
        out_shape=tuple(outs.values()),
        in_specs=[anywhere if m in in_hbm else vmem for m in inputs],
        out_specs=tuple([anywhere if m in out_hbm else vmem for m in outs]),
        scratch_shapes=list(scratch.values()),
        compiler_params=pltpu.CompilerParams(
            collective_id=1, has_side_effects=True, vmem_limit_bytes=48 << 20
        ),
        name="front",
    )(*inputs.values())
    return dict(zip(outs, values, strict=True))


def body(
    hidden_in,
    teacher,
    blocks,
    seq_ids,
    valid_mask,
    norm1_gain,
    q_down,
    q_gain,
    q_up,
    kv_weight,
    out_proj,
    norm2_gain,
    w_gate,
    w_up,
    w_down,
):
    row_count, model_width = hidden_in.shape
    head_size = kv_weight.shape[1] // 2
    heads_width = q_up.shape[1]
    head_count = heads_width // head_size
    half_dim = head_size // 2
    q_width = q_down.shape[1]
    n_ctx = lax.axis_size("ctx")
    n_f = lax.axis_size("fsdp")
    n_z = n_ctx // 2
    token_total = row_count * n_ctx * n_f
    seq_pieces = 2 * SEQ_BLOCKS
    c_idx = lax.axis_index("ctx")
    f_idx = lax.axis_index("fsdp")
    y_idx = c_idx % 2
    z_idx = c_idx // 2
    x_idx = f_idx // 2
    k_idx = f_idx % 2

    def by_f(values, mask):
        return lax.ppermute(values, "fsdp", [(i, i ^ mask) for i in range(n_f)])

    def by_c(values, mask):
        return lax.ppermute(values, "ctx", [(i, i ^ mask) for i in range(n_ctx)])

    def cut(values, start, size, axis):
        return lax.dynamic_slice_in_dim(values, start, size, axis)

    def gather_tokens(values):
        core = by_f(values, 1)
        far = by_f(values, 2)
        far_core = by_f(far, 1)
        return jnp.concatenate([values, core, far, far_core], axis=0)

    def sum_tokens(make_half):
        far = make_half(1).reshape(2, row_count, -1)
        far = (far[0] + by_f(far[1], 1)).astype(BF16)
        far = by_f(far, 2)
        near = make_half(0).reshape(2, row_count, -1)
        near = near[0] + by_f(near[1], 1)
        return near + far.astype(F32)

    def ctx_split(grad):
        view = grad.reshape(n_z, 2, grad.shape[0] // n_ctx, grad.shape[1])
        give = lax.dynamic_index_in_dim(view, 1 - y_idx, 1, keepdims=False)
        keep = lax.dynamic_index_in_dim(view, y_idx, 1, keepdims=False)
        return give, keep

    def ctx_pair(keep, got):
        return (keep.astype(F32) + got.astype(F32)).astype(BF16)

    def ctx_spread(pair):
        return [pair] + [
            by_c(lax.dynamic_index_in_dim(pair, z_idx ^ r, 0, keepdims=False), 2 * r)
            for r in range(1, n_z)
        ]

    def ctx_total(parts):
        total = lax.dynamic_index_in_dim(parts[0], z_idx, 0, keepdims=False).astype(F32)
        for got in parts[1:]:
            total = total + got.astype(F32)
        return total

    def group_rows(values):
        return lax.all_gather(values, "fsdp", axis=0, tiled=True)

    valid_f = valid_mask.astype(F32)
    own_pieces = row_count // PIECE
    info = jnp.concatenate(
        [
            norm1_gain.astype(F32),
            q_gain.astype(F32),
            norm2_gain.astype(F32),
            jnp.full((128,), jnp.sum(valid_f)),
        ]
    )
    info = jnp.pad(info, (0, -info.shape[0] % 1024)).reshape(-1, 128)
    own_tags = jnp.stack([blocks.reshape(-1, PIECE)[:, 0], seq_ids.reshape(-1, PIECE)[:, 0]], 1)
    tag = jnp.pad(own_tags.astype(F32).reshape(1, -1), ((0, 7), (0, 128 - 2 * own_pieces)))
    own = jnp.concatenate([blocks.reshape(-1, PIECE)[:, 0], seq_ids[:1]])

    positions = blocks * PIECE + jnp.arange(row_count, dtype=jnp.int32) % PIECE
    freq_table = 10000.0 ** (-(jnp.arange(half_dim, dtype=F32) * 2.0 / head_size))
    angle_table = positions.astype(F32)[:, None] * freq_table[None, :]
    cosine = jnp.cos(angle_table)
    sine = jnp.sin(angle_table)
    fetched = front(
        n_ctx,
        n_f,
        {
            "q_down": q_down,
            "kv_weight": kv_weight,
            "q_up": q_up,
            "out_proj": out_proj,
            "w_gate": w_gate,
            "w_up": w_up,
            "hidden": hidden_in,
            "info": info,
            "tag": tag,
            "cos": cosine,
            "sin": sine,
        },
        head_size,
    )
    w_gatef, w_upf, w_out = fetched["gate_full"], fetched["up_full"], fetched["w_out"]
    all_kv, q_rot = fetched["all_kv"], fetched["q_rot"]
    normed, q_low, q_normed = fetched["normed"], fetched["q_low"], fetched["q_normed"]
    gain_one, gain_q, gain_two = fetched["gain_one"], fetched["gain_q"], fetched["gain_two"]
    tags = fetched["tags"][:, 0, : 2 * own_pieces].reshape(-1, 2).astype(jnp.int32)
    total_count = jnp.sum(fetched["tags"][:, 1, 0])
    hidden_f = hidden_in.astype(F32)
    scale_q = rms_scale(q_low)

    attn_heads, lse = attn_fwd(tags, own, q_rot, all_kv, head_size, seq_pieces)
    resid = hidden_f + dot(attn_heads, w_out)
    scale_two = rms_scale(resid)
    normed_two = (resid * scale_two * gain_two).astype(BF16)

    group_two = gather_tokens(normed_two)
    gate_lin = dot(group_two, w_gatef)
    up_lin = dot(group_two, w_upf)
    sigma = jax.nn.sigmoid(gate_lin)
    silu_gate = gate_lin * sigma
    hidden_act = (silu_gate * up_lin).astype(BF16)
    side = 2 * row_count

    def down_half(j):
        return dot(hidden_act[j * side : (j + 1) * side], w_down)

    result = resid + sum_tokens(down_half)
    diff = result - teacher.astype(F32)
    sq_local = jnp.sum(valid_f * jnp.sum(diff * diff, axis=1))
    grad_y = diff * valid_f[:, None] * (token_total / total_count)
    group_dz = gather_tokens(grad_y.astype(BF16))
    down_part = dot_rows(hidden_act, group_dz).astype(BF16)
    down_give, down_keep = ctx_split(down_part)
    down_got = by_c(down_give, 1)
    group_dz2 = after(group_dz, down_part)
    grad_hidden = dot_t(group_dz2, w_down)
    grad_gate = (grad_hidden * up_lin * sigma * (1.0 + gate_lin * (1.0 - sigma))).astype(BF16)
    grad_up = (grad_hidden * silu_gate).astype(BF16)
    gate_part = dot_rows(group_two, grad_gate).astype(BF16)
    gate_give, gate_keep = ctx_split(gate_part)
    gate_got = by_c(gate_give, 1)

    def back_half(j):
        rows = slice(j * side, (j + 1) * side)
        return dot_t(grad_gate[rows], w_gatef) + dot_t(grad_up[rows], w_upf)

    grad_normed_two = sum_tokens(back_half)
    up_part = dot_rows(group_two, grad_up).astype(BF16)

    grad_resid_norm, grad_gain_two = rms_back(resid, scale_two, gain_two, grad_normed_two)
    grad_resid = grad_y + grad_resid_norm
    grad_branch = grad_resid.astype(BF16)
    grad_attn = dot_t(grad_branch, w_out).astype(BF16)
    down_parts = ctx_spread(ctx_pair(down_keep, after(down_got, grad_attn)))

    grad_qlin, grad_seq = attn_bwd(
        tags, own, q_rot, grad_attn, attn_heads, lse, cosine, sine, all_kv, head_size, seq_pieces
    )
    by_piece = grad_seq.reshape(seq_pieces, PIECE, 2 * head_size)
    piece_tag = tags[:, 0].reshape(n_z, 2, own_pieces)
    piece_own = (tags[:, 1] == seq_ids[0]).reshape(n_z, 2, own_pieces)

    def kv_half(bit):
        places = lax.dynamic_index_in_dim(piece_tag, bit, 1, keepdims=False).reshape(-1)
        picked = by_piece[places]
        if n_ctx * own_pieces != seq_pieces:
            mine = lax.dynamic_index_in_dim(piece_own, bit, 1, keepdims=False).reshape(-1)
            picked = jnp.where(mine[:, None, None], picked, jnp.zeros_like(picked))
        return picked.reshape(n_z, own_pieces * PIECE, 2 * head_size)

    kv_part = jnp.stack([kv_half(0), kv_half(1)], axis=1)
    q_cut, kv_cut = q_width // n_f, 2 * head_size // n_f
    out_block = heads_width // (n_ctx * n_f)
    qlin_group = lax.all_to_all(grad_qlin, "fsdp", 1, 0, tiled=True)
    attn_group = lax.all_to_all(
        attn_heads.reshape(row_count, n_ctx, n_f, out_block), "fsdp", 2, 0, tiled=True
    ).reshape(row_count * n_f, n_ctx * out_block)
    branch_group = group_rows(grad_branch)
    qnorm_group = group_rows(q_normed)
    normed_group = group_rows(normed)

    grad_qnormed = dot_t(grad_qlin, fetched["w_qu"])
    grad_qlow_f, grad_gain_q = rms_back(q_low, scale_q, gain_q, grad_qnormed)
    grad_qlow = grad_qlow_f.astype(BF16)
    da_q = dot_t(grad_qlow, fetched["w_qd"])
    out_part = dot_rows(attn_group, branch_group).astype(BF16)
    qup_part = dot_rows(qnorm_group, qlin_group).astype(BF16)
    gate_pair = ctx_pair(gate_keep, after(gate_got, qup_part))

    def by_ctx(grad):
        return grad.reshape(n_z, 2, grad.shape[0] // n_ctx, grad.shape[1])

    order = [(c * n_f + f, f * n_ctx + c) for c in range(n_ctx) for f in range(n_f)]
    down_rows = ctx_total(after(down_parts, qup_part)).astype(BF16)
    down_sent = lax.ppermute(down_rows, ("ctx", "fsdp"), order)

    small = jnp.concatenate(
        [jnp.zeros((model_width,), F32), grad_gain_q, grad_gain_two, sq_local.reshape(1)]
    )
    entries = small.shape[0]
    small = jnp.pad(small, (0, -entries % 1024)).reshape(-1, 128)
    ends = tail_reduce(
        n_ctx,
        n_f,
        {
            "gate": gate_pair,
            "kv": kv_part,
            "up": by_ctx(up_part),
            "out": by_ctx(out_part),
            "qup": by_ctx(qup_part),
            "dqa": grad_qlow,
            "cos": cosine,
            "sin": sine,
            "normed_group": normed_group,
            "w_kv": fetched["w_kv"],
            "da_q": da_q,
            "hidden": hidden_in,
            "gain_one": gain_one,
            "grad_resid": grad_resid,
            "small": small,
        },
        q_width,
    )
    small = ends["small_out"].reshape(-1)[:entries]
    grad_down = after(down_sent, small).astype(F32)

    device = c_idx * n_f + f_idx
    q1, q2 = model_width, model_width + q_width
    n_dev = n_ctx * n_f

    def own_part(values):
        size = values.shape[0] // n_dev
        return cut(values, device * size, size, 0)

    loss_now = small[-1] / (model_width * total_count)
    return (
        result.astype(BF16),
        loss_now,
        ends["grad_input"],
        own_part(small[:q1]),
        ends["out_qd"],
        own_part(small[q1:q2]),
        ends["out_qup"],
        ends["out_kvw"],
        ends["out_out"],
        own_part(small[q2 : q2 + model_width]),
        ends["out_gate"],
        ends["out_up"],
        grad_down,
    )


def solution(mesh):
    both = ("ctx", "fsdp")
    rows = P(both, None)
    flat = P(both)
    shard = P("fsdp", None)
    gain = P("fsdp")
    return jax.shard_map(
        body,
        mesh=mesh,
        in_specs=(
            rows,
            rows,
            flat,
            flat,
            flat,
            gain,
            shard,
            gain,
            shard,
            shard,
            shard,
            gain,
            shard,
            shard,
            shard,
        ),
        out_specs=(
            rows,
            P(),
            rows,
            flat,
            rows,
            flat,
            rows,
            rows,
            rows,
            flat,
            rows,
            rows,
            rows,
        ),
        check_vma=False,
    )
```

```python
import functools
import math

import jax
import jax.numpy as jnp
from jax import lax
from jax.experimental import pallas as pl
from jax.experimental.pallas import tpu as pltpu
from jax.sharding import PartitionSpec as P

PIECE = 128
SEQ_BLOCKS = 8
NORM_EPS = 1e-05
F32 = jnp.float32
BF16 = jnp.bfloat16
LOG2E = math.log2(math.e)
HEAD_GROUP = 4


def rms_scale(values):
    return lax.rsqrt(jnp.mean(values * values, axis=-1, keepdims=True) + NORM_EPS)


def rms_back(values, scale, gain, grad):
    grad_gain = jnp.sum(grad * values * scale, axis=0)
    ge = gain * grad
    inner = jnp.mean(ge * values, axis=-1, keepdims=True)
    return scale * ge - values * (scale * scale * scale) * inner, grad_gain


def rope_apply(values, cosine, sine):
    half_dim = values.shape[-1] // 2
    one = values[..., :half_dim]
    two = values[..., half_dim:]
    return jnp.concatenate([one * cosine - two * sine, two * cosine + one * sine], axis=-1)


def rope_back(grads, cosine, sine):
    half_dim = grads.shape[-1] // 2
    one = grads[..., :half_dim]
    two = grads[..., half_dim:]
    return jnp.concatenate([one * cosine + two * sine, two * cosine - one * sine], axis=-1)


def after(values, *deps):
    return lax.optimization_barrier((values, deps))[0]


def dot(a, b):
    return jnp.dot(a, b, preferred_element_type=F32)


def dot_t(a, b):
    return lax.dot_general(a, b, (((1,), (1,)), ((), ())), preferred_element_type=F32)


def dot_rows(a, b):
    return lax.dot_general(a, b, (((0,), (0,)), ((), ())), preferred_element_type=F32)


def contract_last(a, b):
    return lax.dot_general(a, b, (((1,), (1,)), ((), ())), preferred_element_type=F32)

def find_pieces(tags_ref, own_ref, pick_ref, total):
    @pl.loop(0, total)
    def _(u):
        @pl.when(tags_ref[u, 1] == own_ref[2])
        def _():
            pick_ref[tags_ref[u, 0]] = u

def stack_heads(ref, hd):
    return jnp.concatenate([ref[:, h*hd:(h+1)*hd] for h in range(HEAD_GROUP)], axis=0)

def attn_fwd_kernel(tags_ref, own_ref, q_ref, kv_ref, o_ref, lse_ref, k_s, vt_s, acc_s, pick_s):
    half = pl.program_id(0)
    hd = k_s.shape[1]
    pieces = k_s.shape[0] // PIECE
    total = kv_ref.shape[0] // PIECE
    wide = 2 * PIECE
    coef = hd ** -0.5 * LOG2E

    @pl.when((half == 0) & (pl.program_id(1) == 0))
    def _():
        find_pieces(tags_ref, own_ref, pick_s, total)
        for i in range(pieces):
            rows = pl.ds(pl.multiple_of(pick_s[i] * PIECE, PIECE), PIECE)
            k_s[i*PIECE:(i+1)*PIECE, :] = kv_ref[rows, :hd]
            vt_s[:, i*PIECE:(i+1)*PIECE] = kv_ref[rows, hd:].T

    q = stack_heads(q_ref, hd)
    acc_s[...] = jnp.zeros_like(acc_s)
    rows = q.shape[0]
    def step(i, carry):
        peak, total_p = carry
        at = pl.ds(pl.multiple_of(i * wide, wide), wide)
        raw = contract_last(k_s[at, :], q)
        top = jnp.maximum(peak, jnp.max(raw, axis=0, keepdims=True))
        fade = jnp.exp2((peak - top) * coef)
        p = jnp.exp2((raw - top) * coef)
        acc_s[...] = acc_s[...] * fade + jnp.dot(vt_s[:, at], p.astype(BF16), preferred_element_type=F32)
        return top, total_p * fade + jnp.sum(p, axis=0, keepdims=True)
    count = own_ref[half] // 2 + 1
    peak, total_p = lax.fori_loop(0, count, step, (jnp.full((1, rows), -1e30, F32), jnp.zeros((1, rows), F32)))
    out = (acc_s[...] / total_p).astype(BF16).T
    for h in range(HEAD_GROUP):
        o_ref[:, h*hd:(h+1)*hd] = out[h*PIECE:(h+1)*PIECE, :]
    lse_ref[0] = peak * coef + jnp.log2(total_p)

def attn_fwd(tags, own, q, kv, hd, pieces):
    n_rows, width = q.shape
    groups = width // hd // HEAD_GROUP
    gw = HEAD_GROUP * hd
    halves = n_rows // PIECE
    rows = HEAD_GROUP * PIECE
    blk = pl.BlockSpec((PIECE, gw), lambda p, g, *_: (p, g))
    flops = 4 * n_rows * width * pieces * PIECE * 9 // 16
    return pl.pallas_call(
        attn_fwd_kernel,
        out_shape=(jax.ShapeDtypeStruct(q.shape, BF16), jax.ShapeDtypeStruct((halves*groups, 1, rows), F32)),
        grid_spec=pltpu.PrefetchScalarGridSpec(
            num_scalar_prefetch=2, grid=(halves, groups),
            in_specs=[blk, pl.BlockSpec(kv.shape, lambda p, g, *_: (0, 0))],
            out_specs=[blk, pl.BlockSpec((1, 1, rows), lambda p, g, *_: (p*groups+g, 0, 0))],
            scratch_shapes=[pltpu.VMEM((pieces*PIECE, hd), BF16), pltpu.VMEM((hd, pieces*PIECE), BF16),
                            pltpu.VMEM((hd, rows), F32), pltpu.SMEM((pieces,), jnp.int32)]),
        compiler_params=pltpu.CompilerParams(vmem_limit_bytes=40 << 20),
        cost_estimate=pl.CostEstimate(flops=flops, transcendentals=flops//(4*hd), bytes_accessed=2*(2*q.size+kv.size)),
        name="attn_fwd",
    )(tags, own, q, kv)

def attn_bwd_kernel(tags_ref, own_ref, q_ref, do_ref, o_ref, lse_ref, cos_ref, sin_ref, kv_ref, dq_ref, dkv_ref,
                    k_s, kt_s, v_s, dq_s, dk_s, dv_s, pick_s):
    half = pl.program_id(0)
    group = pl.program_id(1)
    hd = k_s.shape[1]
    pieces = k_s.shape[0] // PIECE
    total = kv_ref.shape[0] // PIECE
    wide = 2 * PIECE
    coef = hd ** -0.5 * LOG2E
    scale = hd ** -0.5

    @pl.when((half == 0) & (group == 0))
    def _():
        find_pieces(tags_ref, own_ref, pick_s, total)
        for i in range(pieces):
            rows = pl.ds(pl.multiple_of(pick_s[i] * PIECE, PIECE), PIECE)
            keys = kv_ref[rows, :hd]
            k_s[i*PIECE:(i+1)*PIECE, :] = keys
            kt_s[:, i*PIECE:(i+1)*PIECE] = keys.T
            v_s[i*PIECE:(i+1)*PIECE, :] = kv_ref[rows, hd:]
        dk_s[...] = jnp.zeros_like(dk_s)
        dv_s[...] = jnp.zeros_like(dv_s)

    q = stack_heads(q_ref, hd)
    do = stack_heads(do_ref, hd)
    prod = do.astype(F32) * stack_heads(o_ref, hd).astype(F32)
    delta = lax.dot_general(jnp.ones((8, hd), F32), prod, (((1,), (1,)), ((), ())),
                            preferred_element_type=F32, precision=lax.Precision.HIGHEST)[:1]
    lse = lse_ref[0]
    dq_s[...] = jnp.zeros_like(dq_s)
    def step(i, carry):
        at = pl.ds(pl.multiple_of(i * wide, wide), wide)
        p = jnp.exp2(contract_last(k_s[at, :], q) * coef - lse)
        dp = contract_last(v_s[at, :], do)
        ds = (p * (dp - delta)).astype(BF16)
        dv_s[at, :] += jnp.dot(p.astype(BF16), do, preferred_element_type=F32)
        dk_s[at, :] += jnp.dot(ds, q, preferred_element_type=F32)
        dq_s[...] += jnp.dot(kt_s[:, at], ds, preferred_element_type=F32)
        return carry
    lax.fori_loop(0, own_ref[half] // 2 + 1, step, 0)
    dq = (dq_s[...] * scale).T
    cos, sin = cos_ref[...], sin_ref[...]
    mid = hd // 2
    for h in range(HEAD_GROUP):
        one = dq[h*PIECE:(h+1)*PIECE, :mid]
        two = dq[h*PIECE:(h+1)*PIECE, mid:]
        dq_ref[:, h*hd:h*hd+mid] = (one * cos + two * sin).astype(BF16)
        dq_ref[:, h*hd+mid:(h+1)*hd] = (two * cos - one * sin).astype(BF16)

    @pl.when((half == pl.num_programs(0) - 1) & (group == pl.num_programs(1) - 1))
    def _():
        dkv_ref[:, :hd] = (dk_s[...] * scale).astype(BF16)
        dkv_ref[:, hd:] = dv_s[...].astype(BF16)

def attn_bwd(tags, own, q, do, o, lse, cos, sin, kv, hd, pieces):
    n_rows, width = q.shape
    groups = width // hd // HEAD_GROUP
    gw = HEAD_GROUP * hd
    halves = n_rows // PIECE
    rows = HEAD_GROUP * PIECE
    blk = pl.BlockSpec((PIECE, gw), lambda p, g, *_: (p, g))
    trig = pl.BlockSpec((PIECE, hd // 2), lambda p, g, *_: (p, 0))
    keys = pieces * PIECE
    flops = 10 * n_rows * width * keys * 9 // 16
    return pl.pallas_call(
        attn_bwd_kernel,
        out_shape=(jax.ShapeDtypeStruct(q.shape, BF16), jax.ShapeDtypeStruct((keys, 2*hd), BF16)),
        grid_spec=pltpu.PrefetchScalarGridSpec(
            num_scalar_prefetch=2, grid=(halves, groups),
            in_specs=[blk, blk, blk, pl.BlockSpec((1, 1, rows), lambda p, g, *_: (p*groups+g, 0, 0)), trig, trig,
                      pl.BlockSpec(kv.shape, lambda p, g, *_: (0, 0))],
            out_specs=[blk, pl.BlockSpec((keys, 2*hd), lambda p, g, *_: (0, 0))],
            scratch_shapes=[pltpu.VMEM((keys, hd), BF16), pltpu.VMEM((hd, keys), BF16), pltpu.VMEM((keys, hd), BF16),
                            pltpu.VMEM((hd, rows), F32), pltpu.VMEM((keys, hd), F32), pltpu.VMEM((keys, hd), F32),
                            pltpu.SMEM((pieces,), jnp.int32)]),
        compiler_params=pltpu.CompilerParams(vmem_limit_bytes=48 << 20),
        cost_estimate=pl.CostEstimate(flops=flops, transcendentals=flops//(10*hd), bytes_accessed=2*(4*q.size+2*kv.size)),
        name="attn_bwd",
    )(tags, own, q, do, o, lse, cos, sin, kv)

MESH = pl.DeviceIdType.MESH


def flip(index, mask):
    out = 0
    bit = 1
    while bit <= mask:
        part = (index // bit) % 2
        out = out + bit * ((1 - part) if mask & bit else part)
        bit *= 2
    return out + (index // bit) * bit


def row_loop(rows, body, step=32):
    if rows % step:
        step = 16

    @pl.loop(0, rows // step)
    def _(i):
        body(pl.ds(pl.multiple_of(i * step, step), step))


class Sender:
    def __init__(self):
        self.open = []

    def make(self, src, dst, send_sem, recv_sem, peer):
        return pltpu.make_async_remote_copy(
            src_ref=src,
            dst_ref=dst,
            send_sem=send_sem,
            recv_sem=recv_sem,
            device_id=peer,
            device_id_type=MESH,
        )

    def __call__(self, *args):
        copy = self.make(*args)
        copy.start()
        self.open.append(copy)
        return copy

    def finish(self):
        for copy in self.open:
            copy.wait_send()


class LineSum:
    def __init__(self, own, got, send_sem, recv_sem, c_idx, f_idx, n_z, sender):
        self.own, self.got, self.send_sem, self.recv_sem = own, got, send_sem, recv_sem
        self.n_z, self.sender = n_z, sender
        self.z = c_idx // 2
        self.left = (c_idx - 2, f_idx)
        self.right = (c_idx + 2, f_idx)

    def copy(self, b, slot, peer):
        return self.sender.make(
            self.own.at[b], self.got.at[slot], self.send_sem.at[b], self.recv_sem.at[slot], peer
        )

    def take(self, b, slot):
        self.copy(b, slot, self.left).wait_recv()

        def add(at):
            self.own[b, at, :] = (
                self.own[b, at, :].astype(F32) + self.got[slot, at, :].astype(F32)
            ).astype(BF16)

        row_loop(self.own.shape[1], add)

    def go_right(self, b):
        z = self.z

        @pl.when(z < b)
        def _():
            @pl.when(z > 0)
            def _():
                self.take(b, b)

            self.copy(b, b, self.right).start()

    def go_left(self, b):
        z, n_z = self.z, self.n_z

        @pl.when(z > b)
        def _():
            @pl.when(z < n_z - 1)
            def _():
                self.take(b, b)

            @pl.when(z - 1 > b)
            def _():
                self.copy(b, b, self.left).start()

            @pl.when(z - 1 == b)
            def _():
                self.copy(b, n_z, self.left).start()

    def step(self, i):
        @pl.when(2 * self.z < self.n_z)
        def _():
            self.go_right(self.n_z - 1 - i)
            self.go_left(i)

        @pl.when(2 * self.z >= self.n_z)
        def _():
            self.go_left(i)
            self.go_right(self.n_z - 1 - i)

    def total(self, store):
        z, n_z = self.z, self.n_z

        @pl.when(z > 0)
        def _():
            self.copy(z, z, self.left).wait_recv()

        @pl.when(z < n_z - 1)
        def _():
            self.copy(z, n_z, self.left).wait_recv()

        rows = self.own.shape[1]

        @pl.when(z == 0)
        def _():
            row_loop(
                rows,
                lambda at: store(
                    at, self.own[z, at, :].astype(F32) + self.got[n_z, at, :].astype(F32)
                ),
            )

        @pl.when(z == n_z - 1)
        def _():
            row_loop(
                rows,
                lambda at: store(
                    at, self.own[z, at, :].astype(F32) + self.got[z, at, :].astype(F32)
                ),
            )

        @pl.when((z > 0) & (z < n_z - 1))
        def _():
            row_loop(
                rows,
                lambda at: store(
                    at,
                    self.own[z, at, :].astype(F32)
                    + self.got[z, at, :].astype(F32)
                    + self.got[n_z, at, :].astype(F32),
                ),
            )

    def finish(self):
        for b in range(self.n_z):

            @pl.when(self.z != b)
            def _(b=b):
                self.copy(b, b, self.left).wait_send()


WINDOW = 3
TAIL_NAMES = ("gate", "kv", "up", "out", "qup", "qd", "kvw")
TAIL_CUT = ("gate", "up", "qup", "qd", "kvw")
TAIL_SENT = ("kv", "up", "out", "qup", "qd", "kvw")


def tail_kernel(n_ctx, n_f, names_in, names_out, names_scratch, *refs):
    n_z = n_ctx // 2
    names = list(names_in) + list(names_out) + list(names_scratch)
    r = dict(zip(names, refs, strict=True))
    c_idx = lax.axis_index("ctx")
    f_idx = lax.axis_index("fsdp")
    y_idx = c_idx % 2
    z_idx = c_idx // 2
    send = Sender()

    def over_c(mask):
        return (flip(c_idx, mask), f_idx)

    def over_f(mask):
        return (c_idx, flip(f_idx, mask))

    barrier = pltpu.get_barrier_semaphore()
    for mask in range(1, n_f):
        pl.semaphore_signal(barrier, inc=1, device_id=over_f(mask), device_id_type=MESH)
    for mask in range(1, n_ctx):
        pl.semaphore_signal(barrier, inc=1, device_id=over_c(mask), device_id_type=MESH)
    pl.semaphore_wait(barrier, n_f - 1 + n_ctx - 1)

    lines = {
        m: LineSum(
            r["pair_" + m],
            r["z_" + m],
            r["z_send"].at[i],
            r["z_recv"].at[i],
            c_idx,
            f_idx,
            n_z,
            send,
        )
        for i, m in enumerate(TAIL_NAMES)
    }
    order = list(range(1, n_z)) + [0]
    y_copies, keeps = {}, {}

    parts = {m: r[m] for m in ("kv", "up", "out", "qup")}
    parts["qd"], parts["kvw"] = r["part_qd"], r["part_kvw"]
    queue = [(m, s) for m in TAIL_SENT for s in order]

    def next_y():
        if queue:
            m, s = queue.pop(0)
            i = TAIL_SENT.index(m)
            b = flip(z_idx, s)
            y_copies[m, s] = send(
                parts[m].at[b, 1 - y_idx],
                r["y_" + m].at[s],
                r["y_send"].at[i, s],
                r["y_recv"].at[i, s],
                over_c(1),
            )
            keep = pltpu.make_async_copy(
                parts[m].at[b, y_idx], r["pair_" + m].at[b], r["keep_sem"].at[i, s]
            )
            keep.start()
            keeps[m, s] = keep

    def add_pair(m, s):
        b = flip(z_idx, s)
        y_copies[m, s].wait_recv()
        next_y()
        keeps[m, s].wait()
        pair, got = r["pair_" + m], r["y_" + m]

        def add(at):
            pair[b, at, :] = (pair[b, at, :].astype(F32) + got[s, at, :].astype(F32)).astype(BF16)

        row_loop(pair.shape[1], add)

    def advance(pair, line):
        for i, s in enumerate(order):
            if pair is not None:
                add_pair(pair, s)
            if line is not None and i < n_z - 1:
                lines[line].step(i)

    f_copies = {}

    def finish_sum(m):
        lines[m].total(lambda at, value: store_total(m, at, value))
        if m in TAIL_CUT:
            i = TAIL_CUT.index(m)
            part = r["tot_" + m].shape[0] // n_f
            for s in range(1, n_f):
                at = pl.ds(pl.multiple_of(flip(f_idx, s) * part, part), part)
                f_copies[m, s] = send(
                    r["tot_" + m].at[at, :],
                    r["f_" + m].at[s - 1],
                    r["f_send"].at[i, s - 1],
                    r["f_recv"].at[i, s - 1],
                    over_f(s),
                )

    def store_total(m, at, value):
        if m in TAIL_CUT:
            r["tot_" + m][at, :] = value.astype(BF16)
        else:
            r["out_" + m][at, :] = value

    def put_out(m):
        total, out = r["tot_" + m], r["out_" + m]
        rows, width = total.shape
        part = rows // n_f
        for s in range(n_f):
            at = pl.ds(pl.multiple_of(flip(f_idx, s) * width, 128), width)
            if s:
                f_copies[m, s].wait_recv()
                out[:, at] = r["f_" + m][s - 1].astype(F32)
            else:
                mine = pl.ds(pl.multiple_of(f_idx * part, part), part)
                out[:, at] = total[mine, :].astype(F32)

    def cut_low(src, dst, width, index):
        rows = src.shape[0]
        mine = pl.ds(pl.multiple_of(f_idx * rows, rows), rows)
        copies = []
        for s in range(1, n_f):
            at = pl.ds(pl.multiple_of(flip(f_idx, s) * width, 128), width)
            copies.append(
                send(
                    src.at[:, at],
                    dst.at[mine, :],
                    r["low_send"].at[index, s - 1],
                    r["low_recv"].at[index, s - 1],
                    over_f(s),
                )
            )
        own = pl.ds(pl.multiple_of(f_idx * width, 128), width)
        dst[mine, :] = src[:, own]
        return copies

    for _ in range(WINDOW):
        next_y()
    q_copies = cut_low(r["dqa"], r["qd_group"], r["qd_group"].shape[1], 0)
    pair_in = pltpu.make_async_copy(r["gate"], r["pair_gate"], r["keep_sem"].at[0, n_z])
    pair_in.start()
    pair_in.wait()
    advance("kv", "gate")
    advance("up", "kv")
    finish_sum("gate")

    head = r["dkv"].shape[1] // 2
    mid = head // 2

    def store_kv(at, value):
        cos, sin = r["cos"][at, :], r["sin"][at, :]
        one, two = value[:, :mid], value[:, mid:head]
        r["dkv"][at, :mid] = (one * cos + two * sin).astype(BF16)
        r["dkv"][at, mid:head] = (two * cos - one * sin).astype(BF16)
        r["dkv"][at, head:] = value[:, head:].astype(BF16)

    lines["kv"].total(store_kv)
    kv_copies = cut_low(r["dkv"], r["kv_group"], r["kv_group"].shape[1], 1)

    def low_part(group, part):
        normed = r["normed_group"]
        rows = part.shape[2]
        for c in range(n_ctx):
            part[c // 2, c % 2] = lax.dot_general(
                normed[:, c * rows : (c + 1) * rows],
                group[...],
                (((0,), (0,)), ((), ())),
                preferred_element_type=F32,
            ).astype(BF16)

    for copy in q_copies:
        copy.wait_recv()
    low_part(r["qd_group"], r["part_qd"])
    advance("out", "up")
    for copy in kv_copies:
        copy.wait_recv()
    low_part(r["kv_group"], r["part_kvw"])

    grad_in, w_kv = r["grad_input"], r["w_kv"]
    width = grad_in.shape[1]
    tile = 256

    @pl.loop(0, width // tile)
    def _(t):
        at = pl.ds(pl.multiple_of(t * tile, tile), tile)
        grad_in[:, at] = r["da_q"][:, at] + lax.dot_general(
            r["dkv"][...],
            w_kv[at, :],
            (((1,), (1,)), ((), ())),
            preferred_element_type=F32,
        )

    r["gain_sum"][...] = jnp.zeros_like(r["gain_sum"])
    gain = r["gain_one"][...]

    def norm_rows(at):
        value = r["hidden"][at, :].astype(F32)
        grad = grad_in[at, :]
        scale = lax.rsqrt(jnp.mean(value * value, axis=-1, keepdims=True) + NORM_EPS)
        r["gain_sum"][...] += jnp.sum(grad * value * scale, axis=0, keepdims=True)
        ge = gain * grad
        inner = jnp.mean(ge * value, axis=-1, keepdims=True)
        grad_in[at, :] = (
            r["grad_resid"][at, :] + scale * ge - value * (scale * scale * scale) * inner
        )

    row_loop(grad_in.shape[0], norm_rows, step=16)

    small, small_got = r["small_out"], r["small_got"]
    small[...] = r["small"][...]
    for i in range(width // 128):
        small[i : i + 1, :] = r["gain_sum"][:, i * 128 : (i + 1) * 128]
    steps = [over_f(1), over_f(2), over_c(1)]
    mask = 2
    while mask < n_ctx:
        steps.append(over_c(mask))
        mask *= 2
    small_copies = {}

    def small_start(s):
        small_got[s, 0] = small[...]
        small_copies[s] = send(
            small_got.at[s, 0],
            small_got.at[s, 1],
            r["s_send"].at[s],
            r["s_recv"].at[s],
            steps[s],
        )

    def small_end(s):
        small_copies[s].wait_recv()
        small[...] = small[...] + small_got[s, 1]

    for s in range(2):
        small_start(s)
        small_end(s)
    small_start(2)

    put_out("gate")
    advance("qup", "out")
    finish_sum("up")
    advance("qd", "qup")
    finish_sum("out")
    small_end(2)
    small_start(3)
    advance("kvw", "qd")
    put_out("up")
    finish_sum("qup")
    advance(None, "kvw")
    for s in range(3, len(steps)):
        if s > 3:
            small_start(s)
        small_end(s)
    finish_sum("qd")
    finish_sum("kvw")
    for m in ("qup", "qd", "kvw"):
        put_out(m)
    send.finish()
    for m in TAIL_NAMES:
        lines[m].finish()


def tail_reduce(n_ctx, n_f, inputs, q_width):
    n_z = n_ctx // 2
    vmem = pl.BlockSpec(memory_space=pltpu.VMEM)
    anywhere = pl.BlockSpec(memory_space=pl.ANY)
    rows, width = inputs["hidden"].shape
    kv_width = inputs["w_kv"].shape[1]
    in_hbm = ("gate", "kv", "up", "out", "qup")
    names_in = tuple(inputs)
    in_specs = [anywhere if m in in_hbm else vmem for m in names_in]
    block = {m: inputs[m].shape[-2:] for m in in_hbm}
    block["qd"] = (width // n_ctx, q_width // n_f)
    block["kvw"] = (width // n_ctx, kv_width // n_f)
    outs = {
        "small_out": jax.ShapeDtypeStruct(inputs["small"].shape, F32),
        "grad_input": jax.ShapeDtypeStruct((rows, width), F32),
    }
    scratch = {}
    for m in TAIL_NAMES:
        high, wide = block[m]
        scratch["pair_" + m] = pltpu.VMEM((n_z, high, wide), BF16)
        scratch["z_" + m] = pltpu.VMEM((n_z + 1, high, wide), BF16)
        if m in TAIL_SENT:
            scratch["y_" + m] = pltpu.VMEM((n_z, high, wide), BF16)
        if m in TAIL_CUT:
            scratch["tot_" + m] = pltpu.VMEM((high, wide), BF16)
            scratch["f_" + m] = pltpu.VMEM((n_f - 1, high // n_f, wide), BF16)
            outs["out_" + m] = jax.ShapeDtypeStruct((high // n_f, wide * n_f), F32)
        elif m != "kv":
            outs["out_" + m] = jax.ShapeDtypeStruct((high, wide), F32)
    scratch["dkv"] = pltpu.VMEM((rows, kv_width), BF16)
    scratch["qd_group"] = pltpu.VMEM((rows * n_f, q_width // n_f), BF16)
    scratch["kv_group"] = pltpu.VMEM((rows * n_f, kv_width // n_f), BF16)
    scratch["part_qd"] = pltpu.VMEM((n_z, 2) + block["qd"], BF16)
    scratch["part_kvw"] = pltpu.VMEM((n_z, 2) + block["kvw"], BF16)
    scratch["gain_sum"] = pltpu.VMEM((1, width), F32)
    steps = 2 + (n_ctx.bit_length() - 1)
    scratch["small_got"] = pltpu.VMEM((steps, 2) + inputs["small"].shape, F32)
    dma = pltpu.SemaphoreType.DMA
    sent, cut = len(TAIL_SENT), len(TAIL_CUT)
    scratch["s_send"] = dma((steps,))
    scratch["s_recv"] = dma((steps,))
    scratch["y_send"] = dma((sent, n_z))
    scratch["y_recv"] = dma((sent, n_z))
    scratch["keep_sem"] = dma((sent, n_z + 1))
    scratch["z_send"] = dma((len(TAIL_NAMES), n_z))
    scratch["z_recv"] = dma((len(TAIL_NAMES), n_z + 1))
    scratch["f_send"] = dma((cut, n_f - 1))
    scratch["f_recv"] = dma((cut, n_f - 1))
    scratch["low_send"] = dma((2, n_f - 1))
    scratch["low_recv"] = dma((2, n_f - 1))
    values = pl.pallas_call(
        functools.partial(tail_kernel, n_ctx, n_f, names_in, tuple(outs), tuple(scratch)),
        out_shape=tuple(outs.values()),
        in_specs=in_specs,
        out_specs=tuple([vmem] * len(outs)),
        scratch_shapes=list(scratch.values()),
        compiler_params=pltpu.CompilerParams(
            collective_id=0, has_side_effects=True, vmem_limit_bytes=60 << 20
        ),
        name="tail_reduce",
    )(*inputs.values())
    return dict(zip(outs, values, strict=True))


def front_kernel(n_ctx, n_f, names, *refs):
    r = dict(zip(names, refs, strict=True))
    n_z = n_ctx // 2
    c_idx = lax.axis_index("ctx")
    f_idx = lax.axis_index("fsdp")
    y_idx = c_idx % 2
    z_bit = (c_idx // 2) % 2
    x_idx = f_idx // 2
    k_idx = f_idx % 2
    far_idx = flip(f_idx, 2)
    moves = Sender()
    local = []
    at_sem = [0]

    def over_c(mask):
        return (flip(c_idx, mask), f_idx)

    def over_f(mask):
        return (c_idx, flip(f_idx, mask))

    def send(src, dst, peer):
        i = at_sem[0]
        at_sem[0] += 1
        return moves(src, dst, r["send_sem"].at[i], r["recv_sem"].at[i], peer)

    def keep(src, dst):
        copy = pltpu.make_async_copy(src, dst, r["local_sem"].at[len(local)])
        copy.start()
        local.append(copy)
        return copy

    def rows(start, size):
        return pl.ds(pl.multiple_of(start, size), size)

    barrier = pltpu.get_barrier_semaphore()
    for mask in range(1, n_f):
        pl.semaphore_signal(barrier, inc=1, device_id=over_f(mask), device_id_type=MESH)
    for mask in range(1, n_ctx):
        pl.semaphore_signal(barrier, inc=1, device_id=over_c(mask), device_id_type=MESH)
    pl.semaphore_wait(barrier, n_f - 1 + n_ctx - 1)

    infos, tags = r["infos"], r["tags"]
    infos[f_idx] = r["info"][...]
    info_copies = [
        send(infos.at[f_idx], infos.at[f_idx], over_f(mask)) for mask in range(1, n_f)
    ]

    class Rows:
        def __init__(self, shard, dest, bit, hop, chunks):
            self.dest, self.bit, self.hop = dest, bit, hop
            self.shard = shard
            self.size = shard.shape[0]
            self.half = self.size // 2
            self.step = self.half // chunks
            self.chunks = chunks
            self.far, self.next, self.cross = [], [], []

        def start(self, spare=None):
            mine = self.dest.at[rows(f_idx * self.size, self.size)]
            if spare is None:
                self.kept = keep(self.shard, mine)
            else:
                self.spare, self.kept = spare, keep(self.shard, spare)
            self.cross.append(send(self.shard, mine, over_f(1)))

        def settle(self):
            self.kept.wait()
            keep(self.spare, self.dest.at[rows(f_idx * self.size, self.size)])

        def reach(self, i):
            part = self.bit * self.half + i * self.step
            self.far.append(
                send(
                    self.shard.at[rows(part, self.step)],
                    self.dest.at[rows(f_idx * self.size + part, self.step)],
                    over_f(2),
                )
            )

        def place(self, bit, i):
            return self.dest.at[rows(far_idx * self.size + bit * self.half + i * self.step, self.step)]

        def hop_on(self, i):
            self.far[i].wait_recv()
            reach_next()
            here = self.place(self.bit, i)
            self.next.append(send(here, here, over_c(self.hop)))
            self.cross.append(send(here, here, over_f(1)))

        def pass_on(self, i):
            self.next[i].wait_recv()
            here = self.place(1 - self.bit, i)
            self.cross.append(send(here, here, over_f(1)))

        def end(self):
            for copy in self.cross:
                copy.wait_recv()

    class Columns:
        def __init__(self, shard, dest, box, bits, hops):
            self.shard, self.dest, self.box = shard, dest, box
            self.bits, self.hops = bits, hops
            self.size = shard.shape[0]
            self.width = dest.shape[1]
            self.quarter = self.size // 4

        def columns(self, start, count=1):
            return pl.ds(pl.multiple_of(start * self.width, 128), count * self.width)

        def start(self, spare):
            mine = self.dest.at[rows(f_idx * self.size, self.size)]
            self.spare, self.kept = spare, keep(self.shard.at[:, self.columns(f_idx)], spare)
            self.cross = [send(self.shard.at[:, self.columns(flip(f_idx, 1))], mine, over_f(1))]

        def settle(self):
            self.kept.wait()
            keep(self.spare, self.dest.at[rows(f_idx * self.size, self.size)])

        def reach(self, i):
            one, two = self.bits
            at = rows((two * 2 + one) * self.quarter, self.quarter)
            self.far = send(
                self.shard.at[at, self.columns((1 - x_idx) * 2, 2)], self.box.at[at], over_f(2)
            )

        def piece(self, one, two):
            return self.box.at[rows((two * 2 + one) * self.quarter, self.quarter)]

        def first(self):
            one, two = self.bits
            self.far.wait_recv()
            reach_next()
            here = self.piece(one, two)
            self.step = send(here, here, over_c(self.hops[0]))
            self.last = [send(here, here, over_c(self.hops[1]))]

        def second(self):
            one, two = self.bits
            self.step.wait_recv()
            here = self.piece(1 - one, two)
            self.last.append(send(here, here, over_c(self.hops[1])))

        def part(self):
            for copy in self.last:
                copy.wait_recv()
            there = self.dest.at[rows(far_idx * self.size, self.size)]
            self.cross.append(send(self.box.at[:, self.columns(1 - k_idx)], there, over_f(1)))
            keep(self.box.at[:, self.columns(k_idx)], there)

        def end(self):
            for copy in self.cross:
                copy.wait_recv()

    kv = Rows(r["kv_weight"], r["kv_full"], y_idx, 1, 1)
    qd = Rows(r["q_down"], r["qd_full"], y_idx, 1, 1)
    qu = Rows(r["q_up"], r["qu_full"], y_idx, 1, 2)
    out = Rows(r["out_proj"], r["w_out"], z_bit, 2, 4)
    gate = Columns(r["w_gate"], r["gate_full"], r["gate_box"], (y_idx, z_bit), (1, 2))
    up = Columns(r["w_up"], r["up_full"], r["up_box"], (z_bit, y_idx), (2, 1))
    queue = [(kv, 0), (qd, 0), (qu, 0), (qu, 1), (gate, 0), (up, 0)]
    queue += [(out, i) for i in range(out.chunks)]

    def reach_next():
        if queue:
            part, i = queue.pop(0)
            part.reach(i)

    reach_next()
    reach_next()
    kv.start()
    qd.start()

    for copy in info_copies:
        copy.wait_recv()
    d1 = r["gain_one"].shape[1] // n_f // 128
    d2 = r["gain_q"].shape[1] // n_f // 128
    count = infos[0, 2 * d1 + d2 : 2 * d1 + d2 + 1, :]
    for f in range(n_f):
        for i in range(d1):
            col = slice((f * d1 + i) * 128, (f * d1 + i + 1) * 128)
            r["gain_one"][:, col] = infos[f, i : i + 1, :]
            r["gain_two"][:, col] = infos[f, d1 + d2 + i : d1 + d2 + i + 1, :]
        for i in range(d2):
            col = slice((f * d2 + i) * 128, (f * d2 + i + 1) * 128)
            r["gain_q"][:, col] = infos[f, d1 + i : d1 + i + 1, :]
        if f:
            count = count + infos[f, 2 * d1 + d2 : 2 * d1 + d2 + 1, :]
    tags[c_idx] = r["tag"][...]
    tags[c_idx, 1:2, :] = count
    tag_copies = [send(tags.at[c_idx], tags.at[c_idx], over_c(mask)) for mask in range(1, n_ctx)]

    normed = r["normed"]
    gain_one = r["gain_one"][...]

    def norm_rows(at):
        value = r["hidden"][at, :].astype(F32)
        scale = lax.rsqrt(jnp.mean(value * value, axis=-1, keepdims=True) + NORM_EPS)
        normed[at, :] = (value * scale * gain_one).astype(BF16)

    row_loop(normed.shape[0], norm_rows, step=16)

    kv.hop_on(0)
    qd.hop_on(0)
    qu.start()
    kv.pass_on(0)
    qd.pass_on(0)
    kv.end()
    kv.kept.wait()
    head = r["kv_full"].shape[1] // 2
    mid = head // 2
    cos, sin = r["cos"], r["sin"]
    kv_rows = r["kv_rows"]
    keys = jnp.dot(normed[...], r["kv_full"][:, :head], preferred_element_type=F32)
    one, two = keys[:, :mid], keys[:, mid:]
    kv_rows[:, :mid] = (one * cos[...] - two * sin[...]).astype(BF16)
    kv_rows[:, mid:head] = (two * cos[...] + one * sin[...]).astype(BF16)
    kv_rows[:, head:] = jnp.dot(
        normed[...], r["kv_full"][:, head:], preferred_element_type=F32
    ).astype(BF16)
    all_kv = r["all_kv"]
    tokens = normed.shape[0]

    def kv_place(c):
        return all_kv.at[rows(c * tokens, tokens)]

    kv_z = [send(kv_rows, kv_place(c_idx), over_c(2 * s)) for s in range(1, n_z)]
    kv_y = [send(kv_rows, kv_place(c_idx), over_c(1))]
    keep(kv_rows, kv_place(c_idx))
    qu.hop_on(0)
    qd.end()
    qd.kept.wait()

    @pl.loop(0, r["q_low"].shape[1] // 256)
    def _(t):
        at = pl.ds(pl.multiple_of(t * 256, 256), 256)
        r["q_low"][:, at] = jnp.dot(
            normed[...], r["qd_full"][:, at], preferred_element_type=F32
        )

    gain_q = r["gain_q"][...]

    def norm_low(at):
        value = r["q_low"][at, :]
        scale = lax.rsqrt(jnp.mean(value * value, axis=-1, keepdims=True) + NORM_EPS)
        r["q_normed"][at, :] = (value * scale * gain_q).astype(BF16)

    row_loop(tokens, norm_low, step=16)
    qu.hop_on(1)
    for s in range(1, n_z):
        kv_z[s - 1].wait_recv()
        here = kv_place(flip(c_idx, 2 * s))
        kv_y.append(send(here, here, over_c(1)))
    qu.pass_on(0)
    qu.pass_on(1)
    gate.first()
    qu.end()
    for m, part in (("gate", gate), ("up", up), ("out", out)):
        part.start(r[m + "_spare"])
    qu.kept.wait()

    @pl.loop(0, r["q_rot"].shape[1] // head)
    def _(h):
        start = pl.multiple_of(h * head, head)
        value = jnp.dot(
            r["q_normed"][...],
            r["qu_full"][:, pl.ds(start, head)],
            preferred_element_type=F32,
        )
        one, two = value[:, :mid], value[:, mid:]
        r["q_rot"][:, pl.ds(start, mid)] = (one * cos[...] - two * sin[...]).astype(BF16)
        late = pl.multiple_of(h * head + mid, mid)
        r["q_rot"][:, pl.ds(late, mid)] = (two * cos[...] + one * sin[...]).astype(BF16)

    up.first()
    for part in (gate, up, out):
        part.settle()
    for m in ("kv", "qd", "qu"):
        keep(r[m + "_full"], r["w_" + m])
    gate.second()
    out.hop_on(0)
    up.second()
    for i in range(1, out.chunks):
        out.hop_on(i)
    gate.part()
    for i in range(out.chunks):
        out.pass_on(i)
    up.part()
    for copy in kv_y + tag_copies:
        copy.wait_recv()
    for part in (gate, up, out):
        part.end()
    for copy in local:
        if not any(copy is part.kept for part in (kv, qd, qu, gate, up, out)):
            copy.wait()
    moves.finish()


def front(n_ctx, n_f, inputs, head_size):
    tokens, width = inputs["hidden"].shape
    shape = jax.ShapeDtypeStruct
    q_width = inputs["q_down"].shape[1]
    heads_width = inputs["q_up"].shape[1]
    part = inputs["w_gate"].shape[1] // n_f

    def whole(m):
        return (inputs[m].shape[0] * n_f, inputs[m].shape[1])

    in_hbm = ("q_down", "kv_weight", "q_up", "out_proj", "w_gate", "w_up")
    outs = {
        "w_qd": shape(whole("q_down"), BF16),
        "w_kv": shape(whole("kv_weight"), BF16),
        "w_qu": shape(whole("q_up"), BF16),
        "w_out": shape(whole("out_proj"), BF16),
        "gate_full": shape((width, part), BF16),
        "up_full": shape((width, part), BF16),
        "all_kv": shape((tokens * n_ctx, 2 * head_size), BF16),
        "normed": shape((tokens, width), BF16),
        "q_low": shape((tokens, q_width), F32),
        "q_normed": shape((tokens, q_width), BF16),
        "q_rot": shape((tokens, heads_width), BF16),
        "gain_one": shape((1, width), F32),
        "gain_q": shape((1, q_width), F32),
        "gain_two": shape((1, width), F32),
        "tags": shape((n_ctx, 8, 128), F32),
    }
    out_hbm = ("w_qd", "w_kv", "w_qu", "w_out", "gate_full", "up_full", "all_kv")
    box = (inputs["w_gate"].shape[0], 2 * part)
    dma = pltpu.SemaphoreType.DMA
    scratch = {
        "infos": pltpu.VMEM((n_f,) + inputs["info"].shape, F32),
        "qd_full": pltpu.VMEM(whole("q_down"), BF16),
        "kv_full": pltpu.VMEM(whole("kv_weight"), BF16),
        "qu_full": pltpu.VMEM(whole("q_up"), BF16),
        "gate_box": pltpu.VMEM(box, BF16),
        "up_box": pltpu.VMEM(box, BF16),
        "gate_spare": pltpu.VMEM((box[0], part), BF16),
        "up_spare": pltpu.VMEM((box[0], part), BF16),
        "out_spare": pltpu.VMEM(inputs["out_proj"].shape, BF16),
        "kv_rows": pltpu.VMEM((tokens, 2 * head_size), BF16),
        "send_sem": dma((64 + 2 * n_ctx,)),
        "recv_sem": dma((64 + 2 * n_ctx,)),
        "local_sem": dma((16,)),
    }
    vmem = pl.BlockSpec(memory_space=pltpu.VMEM)
    anywhere = pl.BlockSpec(memory_space=pl.ANY)
    names = tuple(inputs) + tuple(outs) + tuple(scratch)
    values = pl.pallas_call(
        functools.partial(front_kernel, n_ctx, n_f, names),
        out_shape=tuple(outs.values()),
        in_specs=[anywhere if m in in_hbm else vmem for m in inputs],
        out_specs=tuple([anywhere if m in out_hbm else vmem for m in outs]),
        scratch_shapes=list(scratch.values()),
        compiler_params=pltpu.CompilerParams(
            collective_id=1, has_side_effects=True, vmem_limit_bytes=48 << 20
        ),
        name="front",
    )(*inputs.values())
    return dict(zip(outs, values, strict=True))


def tiles(total, wide, body):
    whole = total // wide

    @pl.loop(0, whole)
    def _(t):
        body(pl.multiple_of(t * wide, wide), wide)

    if total % wide:
        body(whole * wide, total % wide)


def contract_first(a, b):
    return jnp.dot(a.T, b, preferred_element_type=F32)


def ffn_kernel(n_f, names, *refs):
    r = dict(zip(names, refs, strict=True))
    c_idx = lax.axis_index("ctx")
    f_idx = lax.axis_index("fsdp")
    moves = Sender()
    at_sem = [0]
    core, far = (c_idx, flip(f_idx, 1)), (c_idx, flip(f_idx, 2))

    def send(src, dst, peer):
        i = at_sem[0]
        at_sem[0] += 1
        return moves(src, dst, r["send_sem"].at[i], r["recv_sem"].at[i], peer)

    barrier = pltpu.get_barrier_semaphore()
    for peer in (core, far):
        pl.semaphore_signal(barrier, inc=1, device_id=peer, device_id_type=MESH)
    pl.semaphore_wait(barrier, 2)

    tokens, width = r["normed"].shape
    units = r["w_down"].shape[0]
    group, dz = r["group"], r["dz"]
    block = [slice(i * tokens, (i + 1) * tokens) for i in range(4)]
    pair = [slice(0, 2 * tokens), slice(2 * tokens, 4 * tokens)]

    def gather(buf):
        to_core = send(buf.at[block[0]], buf.at[block[1]], core)
        to_far = send(buf.at[block[0]], buf.at[block[2]], far)
        return to_core, to_far

    def gather_far(buf, to_far):
        to_far.wait_recv()
        send(buf.at[block[2]], buf.at[block[3]], core).wait_recv()

    group[block[0], :] = r["normed"][...]
    to_core, to_far = gather(group)
    loads = []
    for i, m in enumerate(("gate", "up", "down")):
        load = pltpu.make_async_copy(r["w_" + m], r["v_" + m], r["load_sem"].at[i])
        load.start()
        loads.append(load)
    loads[0].wait()
    loads[1].wait()

    def hidden_part(rows):
        def one(start, wide):
            at = pl.ds(start, wide)
            both = jnp.concatenate([r["v_gate"][:, at], r["v_up"][:, at]], axis=1)
            out = jnp.dot(group[rows, :], both, preferred_element_type=F32)
            gate, up = out[:, :wide], out[:, wide:]
            r["gate"][rows, at] = gate.astype(BF16)
            r["up"][rows, at] = up.astype(BF16)
            r["hid"][rows, at] = (gate / (1.0 + jnp.exp(-gate)) * up).astype(BF16)

        tiles(units, 128, one)

    to_core.wait_recv()
    hidden_part(pair[0])
    gather_far(group, to_far)
    hidden_part(pair[1])
    loads[2].wait()

    def down_block(i, dest):
        def one(start, wide):
            at = pl.ds(start, wide)
            dest[:, at] = jnp.dot(
                r["hid"][block[i], :], r["v_down"][:, at], preferred_element_type=F32
            ).astype(dest.dtype)

        tiles(width, 256, one)

    def back_block(i, dest):
        def one(start, wide):
            at = pl.ds(start, wide)
            dest[:, at] = (
                contract_last(r["gate"][block[i], :], r["v_gate"][at, :])
                + contract_last(r["up"][block[i], :], r["v_up"][at, :])
            ).astype(dest.dtype)

        tiles(width, 256, one)

    def add_rows(dest, one, two):
        def add(at):
            dest[at, :] = (one[at, :].astype(F32) + two[at, :].astype(F32)).astype(dest.dtype)

        row_loop(tokens, add)

    def far_sum(k, make):
        make(3, r["give"].at[2 * k])
        step = send(r["give"].at[2 * k], r["got"].at[2 * k], core)
        make(2, r["far_sum"])
        step.wait_recv()
        add_rows(r["far_give"].at[k], r["far_sum"], r["got"].at[2 * k])
        return send(r["far_give"].at[k], r["far_got"].at[k], far)

    def near_sum(k, make):
        make(1, r["give"].at[2 * k + 1])
        step = send(r["give"].at[2 * k + 1], r["got"].at[2 * k + 1], core)
        make(0, r["near_sum"])
        return step

    def near_end(k, step):
        step.wait_recv()
        add_rows(r["near_sum"], r["near_sum"], r["got"].at[2 * k + 1])

    far_step = far_sum(0, down_block)
    near_end(0, near_sum(0, down_block))
    far_step.wait_recv()
    r["sq"][...] = jnp.zeros_like(r["sq"])

    def loss_rows(at):
        value = r["resid"][at, :] + r["near_sum"][at, :] + r["far_got"][0, at, :].astype(F32)
        r["result"][at, :] = value.astype(BF16)
        diff = value - r["teacher"][at, :].astype(F32)
        squares = jnp.sum(diff * diff, axis=1, keepdims=True) * r["valid"][at, :]
        r["sq"][:1, :] += jnp.sum(squares, axis=0, keepdims=True)
        grad = diff * r["valid_scale"][at, :1]
        r["grad_resid"][at, :] = grad
        dz[at, :] = grad.astype(BF16)

    row_loop(tokens, loss_rows, step=16)
    to_core, to_far = gather(dz)

    def back_hidden(rows):
        def one(start, wide):
            at = pl.ds(start, wide)
            grad = contract_last(dz[rows, :], r["v_down"][at, :])
            gate = r["gate"][rows, at].astype(F32)
            up = r["up"][rows, at].astype(F32)
            sigma = 1.0 / (1.0 + jnp.exp(-gate))
            r["gate"][rows, at] = (grad * up * sigma * (1.0 + gate * (1.0 - sigma))).astype(BF16)
            r["up"][rows, at] = (grad * (gate * sigma)).astype(BF16)

        tiles(units, 256, one)

    to_core.wait_recv()
    back_hidden(pair[0])
    near_step = near_sum(1, back_block)
    gather_far(dz, to_far)
    back_hidden(pair[1])
    far_step = far_sum(1, back_block)
    near_end(1, near_step)

    saves = []

    def save(src, dst, i):
        copy = pltpu.make_async_copy(src, dst, r["save_sem"].at[i])
        copy.start()
        return copy

    def down_tile(start, wide):
        at = pl.ds(start, wide)
        spot = r["tile"].at[pl.ds(0, wide)]
        spot[...] = contract_first(r["hid"][:, at], dz[...]).astype(BF16)
        save(spot, r["down_part"].at[at], 0).wait()

    tiles(units, 128, down_tile)

    def gate_tile(start, wide):
        at = pl.ds(start, wide)
        left = group[:, at].T
        for i, m in enumerate(("gate", "up")):
            spot = r["wide_tile"].at[i]
            spot[...] = jnp.dot(left, r[m][...], preferred_element_type=F32).astype(BF16)
            saves.append(save(spot, r[m + "_part"].at[at], 1 + i))
        saves.pop().wait()
        saves.pop().wait()

    tiles(width, 256, gate_tile)
    far_step.wait_recv()
    gain = r["gain_two"][...]
    r["gain_sum"][...] = jnp.zeros_like(r["gain_sum"])

    def norm_rows(at):
        grad = r["near_sum"][at, :] + r["far_got"][1, at, :].astype(F32)
        value = r["resid"][at, :]
        scale = lax.rsqrt(jnp.mean(value * value, axis=-1, keepdims=True) + NORM_EPS)
        r["gain_sum"][...] += jnp.sum(grad * value * scale, axis=0, keepdims=True)
        ge = gain * grad
        inner = jnp.mean(ge * value, axis=-1, keepdims=True)
        total = r["grad_resid"][at, :] + scale * ge - value * (scale * scale * scale) * inner
        r["grad_resid"][at, :] = total
        r["grad_branch"][at, :] = total.astype(BF16)

    row_loop(tokens, norm_rows, step=16)
    moves.finish()


def feed_forward(n_f, inputs):
    tokens, width = inputs["normed"].shape
    units = inputs["w_down"].shape[0]
    shape = jax.ShapeDtypeStruct
    outs = {
        "result": shape((tokens, width), BF16),
        "grad_resid": shape((tokens, width), F32),
        "grad_branch": shape((tokens, width), BF16),
        "down_part": shape((units, width), BF16),
        "gate_part": shape((width, units), BF16),
        "up_part": shape((width, units), BF16),
        "gain_sum": shape((1, width), F32),
        "sq": shape((8, 128), F32),
    }
    hbm = ("w_gate", "w_up", "w_down", "down_part", "gate_part", "up_part")
    dma = pltpu.SemaphoreType.DMA
    many = tokens * n_f
    scratch = {
        "v_gate": pltpu.VMEM((width, units), BF16),
        "v_up": pltpu.VMEM((width, units), BF16),
        "v_down": pltpu.VMEM((units, width), BF16),
        "group": pltpu.VMEM((many, width), BF16),
        "dz": pltpu.VMEM((many, width), BF16),
        "gate": pltpu.VMEM((many, units), BF16),
        "up": pltpu.VMEM((many, units), BF16),
        "hid": pltpu.VMEM((many, units), BF16),
        "give": pltpu.VMEM((4, tokens, width), BF16),
        "got": pltpu.VMEM((4, tokens, width), BF16),
        "far_sum": pltpu.VMEM((tokens, width), F32),
        "near_sum": pltpu.VMEM((tokens, width), F32),
        "far_give": pltpu.VMEM((2, tokens, width), BF16),
        "far_got": pltpu.VMEM((2, tokens, width), BF16),
        "tile": pltpu.VMEM((128, width), BF16),
        "wide_tile": pltpu.VMEM((2, 256, units), BF16),
        "send_sem": dma((16,)),
        "recv_sem": dma((16,)),
        "load_sem": dma((3,)),
        "save_sem": dma((3,)),
    }
    vmem = pl.BlockSpec(memory_space=pltpu.VMEM)
    anywhere = pl.BlockSpec(memory_space=pl.ANY)
    names = tuple(inputs) + tuple(outs) + tuple(scratch)
    values = pl.pallas_call(
        functools.partial(ffn_kernel, n_f, names),
        out_shape=tuple(outs.values()),
        in_specs=[anywhere if m in hbm else vmem for m in inputs],
        out_specs=tuple([anywhere if m in hbm else vmem for m in outs]),
        scratch_shapes=list(scratch.values()),
        compiler_params=pltpu.CompilerParams(
            collective_id=2, has_side_effects=True, vmem_limit_bytes=60 << 20
        ),
        name="feed_forward",
    )(*inputs.values())
    return dict(zip(outs, values, strict=True))


def body(
    hidden_in,
    teacher,
    blocks,
    seq_ids,
    valid_mask,
    norm1_gain,
    q_down,
    q_gain,
    q_up,
    kv_weight,
    out_proj,
    norm2_gain,
    w_gate,
    w_up,
    w_down,
):
    row_count, model_width = hidden_in.shape
    head_size = kv_weight.shape[1] // 2
    heads_width = q_up.shape[1]
    head_count = heads_width // head_size
    half_dim = head_size // 2
    q_width = q_down.shape[1]
    n_ctx = lax.axis_size("ctx")
    n_f = lax.axis_size("fsdp")
    n_z = n_ctx // 2
    token_total = row_count * n_ctx * n_f
    seq_pieces = 2 * SEQ_BLOCKS
    c_idx = lax.axis_index("ctx")
    f_idx = lax.axis_index("fsdp")
    y_idx = c_idx % 2
    z_idx = c_idx // 2
    x_idx = f_idx // 2
    k_idx = f_idx % 2

    def by_f(values, mask):
        return lax.ppermute(values, "fsdp", [(i, i ^ mask) for i in range(n_f)])

    def by_c(values, mask):
        return lax.ppermute(values, "ctx", [(i, i ^ mask) for i in range(n_ctx)])

    def cut(values, start, size, axis):
        return lax.dynamic_slice_in_dim(values, start, size, axis)

    def ctx_split(grad):
        view = grad.reshape(n_z, 2, grad.shape[0] // n_ctx, grad.shape[1])
        give = lax.dynamic_index_in_dim(view, 1 - y_idx, 1, keepdims=False)
        keep = lax.dynamic_index_in_dim(view, y_idx, 1, keepdims=False)
        return give, keep

    def ctx_pair(keep, got):
        return (keep.astype(F32) + got.astype(F32)).astype(BF16)

    def ctx_spread(pair):
        return [pair] + [
            by_c(lax.dynamic_index_in_dim(pair, z_idx ^ r, 0, keepdims=False), 2 * r)
            for r in range(1, n_z)
        ]

    def ctx_total(parts):
        total = lax.dynamic_index_in_dim(parts[0], z_idx, 0, keepdims=False).astype(F32)
        for got in parts[1:]:
            total = total + got.astype(F32)
        return total

    def group_rows(values):
        return lax.all_gather(values, "fsdp", axis=0, tiled=True)

    valid_f = valid_mask.astype(F32)
    own_pieces = row_count // PIECE
    info = jnp.concatenate(
        [
            norm1_gain.astype(F32),
            q_gain.astype(F32),
            norm2_gain.astype(F32),
            jnp.full((128,), jnp.sum(valid_f)),
        ]
    )
    info = jnp.pad(info, (0, -info.shape[0] % 1024)).reshape(-1, 128)
    own_tags = jnp.stack([blocks.reshape(-1, PIECE)[:, 0], seq_ids.reshape(-1, PIECE)[:, 0]], 1)
    tag = jnp.pad(own_tags.astype(F32).reshape(1, -1), ((0, 7), (0, 128 - 2 * own_pieces)))
    own = jnp.concatenate([blocks.reshape(-1, PIECE)[:, 0], seq_ids[:1]])

    positions = blocks * PIECE + jnp.arange(row_count, dtype=jnp.int32) % PIECE
    freq_table = 10000.0 ** (-(jnp.arange(half_dim, dtype=F32) * 2.0 / head_size))
    angle_table = positions.astype(F32)[:, None] * freq_table[None, :]
    cosine = jnp.cos(angle_table)
    sine = jnp.sin(angle_table)
    fetched = front(
        n_ctx,
        n_f,
        {
            "q_down": q_down,
            "kv_weight": kv_weight,
            "q_up": q_up,
            "out_proj": out_proj,
            "w_gate": w_gate,
            "w_up": w_up,
            "hidden": hidden_in,
            "info": info,
            "tag": tag,
            "cos": cosine,
            "sin": sine,
        },
        head_size,
    )
    w_out = fetched["w_out"]
    all_kv, q_rot = fetched["all_kv"], fetched["q_rot"]
    normed, q_low, q_normed = fetched["normed"], fetched["q_low"], fetched["q_normed"]
    gain_one, gain_q, gain_two = fetched["gain_one"], fetched["gain_q"], fetched["gain_two"]
    tags = fetched["tags"][:, 0, : 2 * own_pieces].reshape(-1, 2).astype(jnp.int32)
    total_count = jnp.sum(fetched["tags"][:, 1, 0])
    hidden_f = hidden_in.astype(F32)
    scale_q = rms_scale(q_low)

    attn_heads, lse = attn_fwd(tags, own, q_rot, all_kv, head_size, seq_pieces)
    resid = hidden_f + dot(attn_heads, w_out)
    scale_two = rms_scale(resid)
    normed_two = (resid * scale_two * gain_two).astype(BF16)

    wide_valid = jnp.broadcast_to(valid_f[:, None], (row_count, 128))
    ffn = feed_forward(
        n_f,
        {
            "normed": normed_two,
            "resid": resid,
            "teacher": teacher,
            "valid": wide_valid,
            "valid_scale": wide_valid * (token_total / total_count),
            "gain_two": gain_two,
            "w_gate": fetched["gate_full"],
            "w_up": fetched["up_full"],
            "w_down": w_down,
        },
    )
    grad_resid, grad_branch = ffn["grad_resid"], ffn["grad_branch"]
    grad_gain_two = ffn["gain_sum"].reshape(-1)
    sq_local = ffn["sq"][0, 0]
    down_give, down_keep = ctx_split(ffn["down_part"])
    down_got = by_c(down_give, 1)
    gate_give, gate_keep = ctx_split(ffn["gate_part"])
    gate_got = by_c(gate_give, 1)
    up_part = ffn["up_part"]
    branch_group = group_rows(grad_branch)
    grad_attn = dot_t(grad_branch, w_out).astype(BF16)
    out_block = heads_width // (n_ctx * n_f)
    attn_group = lax.all_to_all(
        attn_heads.reshape(row_count, n_ctx, n_f, out_block), "fsdp", 2, 0, tiled=True
    ).reshape(row_count * n_f, n_ctx * out_block)
    grad_attn = after(grad_attn, attn_group)

    grad_qlin, grad_seq = attn_bwd(
        tags, own, q_rot, grad_attn, attn_heads, lse, cosine, sine, all_kv, head_size, seq_pieces
    )
    by_piece = grad_seq.reshape(seq_pieces, PIECE, 2 * head_size)
    piece_tag = tags[:, 0].reshape(n_z, 2, own_pieces)
    piece_own = (tags[:, 1] == seq_ids[0]).reshape(n_z, 2, own_pieces)

    def kv_half(bit):
        places = lax.dynamic_index_in_dim(piece_tag, bit, 1, keepdims=False).reshape(-1)
        picked = by_piece[places]
        if n_ctx * own_pieces != seq_pieces:
            mine = lax.dynamic_index_in_dim(piece_own, bit, 1, keepdims=False).reshape(-1)
            picked = jnp.where(mine[:, None, None], picked, jnp.zeros_like(picked))
        return picked.reshape(n_z, own_pieces * PIECE, 2 * head_size)

    kv_part = jnp.stack([kv_half(0), kv_half(1)], axis=1)
    q_cut, kv_cut = q_width // n_f, 2 * head_size // n_f
    qlin_group = lax.all_to_all(grad_qlin, "fsdp", 1, 0, tiled=True)
    down_parts = ctx_spread(ctx_pair(down_keep, after(down_got, kv_part)))
    qnorm_group = group_rows(q_normed)
    normed_group = group_rows(normed)

    grad_qnormed = dot_t(grad_qlin, fetched["w_qu"])
    grad_qlow_f, grad_gain_q = rms_back(q_low, scale_q, gain_q, grad_qnormed)
    grad_qlow = grad_qlow_f.astype(BF16)
    da_q = dot_t(grad_qlow, fetched["w_qd"])
    out_part = dot_rows(attn_group, branch_group).astype(BF16)
    qup_part = dot_rows(qnorm_group, qlin_group).astype(BF16)
    gate_pair = ctx_pair(gate_keep, after(gate_got, qup_part))

    def by_ctx(grad):
        return grad.reshape(n_z, 2, grad.shape[0] // n_ctx, grad.shape[1])

    order = [(c * n_f + f, f * n_ctx + c) for c in range(n_ctx) for f in range(n_f)]
    down_rows = ctx_total(after(down_parts, qup_part)).astype(BF16)
    down_sent = lax.ppermute(down_rows, ("ctx", "fsdp"), order)

    small = jnp.concatenate(
        [jnp.zeros((model_width,), F32), grad_gain_q, grad_gain_two, sq_local.reshape(1)]
    )
    entries = small.shape[0]
    small = jnp.pad(small, (0, -entries % 1024)).reshape(-1, 128)
    ends = tail_reduce(
        n_ctx,
        n_f,
        {
            "gate": gate_pair,
            "kv": kv_part,
            "up": by_ctx(up_part),
            "out": by_ctx(out_part),
            "qup": by_ctx(qup_part),
            "dqa": grad_qlow,
            "cos": cosine,
            "sin": sine,
            "normed_group": normed_group,
            "w_kv": fetched["w_kv"],
            "da_q": da_q,
            "hidden": hidden_in,
            "gain_one": gain_one,
            "grad_resid": grad_resid,
            "small": small,
        },
        q_width,
    )
    small = ends["small_out"].reshape(-1)[:entries]
    grad_down = after(down_sent, small).astype(F32)

    device = c_idx * n_f + f_idx
    q1, q2 = model_width, model_width + q_width
    n_dev = n_ctx * n_f

    def own_part(values):
        size = values.shape[0] // n_dev
        return cut(values, device * size, size, 0)

    loss_now = small[-1] / (model_width * total_count)
    return (
        ffn["result"],
        loss_now,
        ends["grad_input"],
        own_part(small[:q1]),
        ends["out_qd"],
        own_part(small[q1:q2]),
        ends["out_qup"],
        ends["out_kvw"],
        ends["out_out"],
        own_part(small[q2 : q2 + model_width]),
        ends["out_gate"],
        ends["out_up"],
        grad_down,
    )


def solution(mesh):
    both = ("ctx", "fsdp")
    rows = P(both, None)
    flat = P(both)
    shard = P("fsdp", None)
    gain = P("fsdp")
    return jax.shard_map(
        body,
        mesh=mesh,
        in_specs=(
            rows,
            rows,
            flat,
            flat,
            flat,
            gain,
            shard,
            gain,
            shard,
            shard,
            shard,
            gain,
            shard,
            shard,
            shard,
        ),
        out_specs=(
            rows,
            P(),
            rows,
            flat,
            rows,
            flat,
            rows,
            rows,
            rows,
            flat,
            rows,
            rows,
            rows,
        ),
        check_vma=False,
    )
```

```python
import functools
import math

import jax
import jax.numpy as jnp
from jax import lax
from jax.experimental import pallas as pl
from jax.experimental.pallas import tpu as pltpu
from jax.sharding import PartitionSpec as P

PIECE = 128
SEQ_BLOCKS = 8
NORM_EPS = 1e-05
F32 = jnp.float32
BF16 = jnp.bfloat16
LOG2E = math.log2(math.e)
HEAD_GROUP = 4


def rms_scale(values):
    return lax.rsqrt(jnp.mean(values * values, axis=-1, keepdims=True) + NORM_EPS)


def rms_back(values, scale, gain, grad):
    grad_gain = jnp.sum(grad * values * scale, axis=0)
    ge = gain * grad
    inner = jnp.mean(ge * values, axis=-1, keepdims=True)
    return scale * ge - values * (scale * scale * scale) * inner, grad_gain


def rope_apply(values, cosine, sine):
    half_dim = values.shape[-1] // 2
    one = values[..., :half_dim]
    two = values[..., half_dim:]
    return jnp.concatenate([one * cosine - two * sine, two * cosine + one * sine], axis=-1)


def rope_back(grads, cosine, sine):
    half_dim = grads.shape[-1] // 2
    one = grads[..., :half_dim]
    two = grads[..., half_dim:]
    return jnp.concatenate([one * cosine + two * sine, two * cosine - one * sine], axis=-1)


def together(*values):
    return lax.optimization_barrier(values)


def dot(a, b):
    return jnp.dot(a, b, preferred_element_type=F32)


def dot_t(a, b):
    return lax.dot_general(a, b, (((1,), (1,)), ((), ())), preferred_element_type=F32)


def dot_rows(a, b):
    return lax.dot_general(a, b, (((0,), (0,)), ((), ())), preferred_element_type=F32)


def contract_last(a, b):
    return lax.dot_general(a, b, (((1,), (1,)), ((), ())), preferred_element_type=F32)

def find_pieces(tags_ref, own_ref, pick_ref, total):
    @pl.loop(0, total)
    def _(u):
        @pl.when(tags_ref[u, 1] == own_ref[2])
        def _():
            pick_ref[tags_ref[u, 0]] = u

def stack_heads(ref, hd):
    return jnp.concatenate([ref[:, h*hd:(h+1)*hd] for h in range(HEAD_GROUP)], axis=0)

def attn_fwd_kernel(tags_ref, own_ref, q_ref, kv_ref, o_ref, lse_ref, k_s, vt_s, acc_s, pick_s):
    half = pl.program_id(0)
    hd = k_s.shape[1]
    pieces = k_s.shape[0] // PIECE
    total = kv_ref.shape[0] // PIECE
    wide = 2 * PIECE
    coef = hd ** -0.5 * LOG2E

    @pl.when((half == 0) & (pl.program_id(1) == 0))
    def _():
        find_pieces(tags_ref, own_ref, pick_s, total)
        for i in range(pieces):
            rows = pl.ds(pl.multiple_of(pick_s[i] * PIECE, PIECE), PIECE)
            k_s[i*PIECE:(i+1)*PIECE, :] = kv_ref[rows, :hd]
            vt_s[:, i*PIECE:(i+1)*PIECE] = kv_ref[rows, hd:].T

    q = stack_heads(q_ref, hd)
    acc_s[...] = jnp.zeros_like(acc_s)
    rows = q.shape[0]
    def step(i, carry):
        peak, total_p = carry
        at = pl.ds(pl.multiple_of(i * wide, wide), wide)
        raw = contract_last(k_s[at, :], q)
        top = jnp.maximum(peak, jnp.max(raw, axis=0, keepdims=True))
        fade = jnp.exp2((peak - top) * coef)
        p = jnp.exp2((raw - top) * coef)
        acc_s[...] = acc_s[...] * fade + jnp.dot(vt_s[:, at], p.astype(BF16), preferred_element_type=F32)
        return top, total_p * fade + jnp.sum(p, axis=0, keepdims=True)
    count = own_ref[half] // 2 + 1
    peak, total_p = lax.fori_loop(0, count, step, (jnp.full((1, rows), -1e30, F32), jnp.zeros((1, rows), F32)))
    out = (acc_s[...] / total_p).astype(BF16).T
    for h in range(HEAD_GROUP):
        o_ref[:, h*hd:(h+1)*hd] = out[h*PIECE:(h+1)*PIECE, :]
    lse_ref[0] = peak * coef + jnp.log2(total_p)

def attn_fwd(tags, own, q, kv, hd, pieces):
    n_rows, width = q.shape
    groups = width // hd // HEAD_GROUP
    gw = HEAD_GROUP * hd
    halves = n_rows // PIECE
    rows = HEAD_GROUP * PIECE
    blk = pl.BlockSpec((PIECE, gw), lambda p, g, *_: (p, g))
    flops = 4 * n_rows * width * pieces * PIECE * 9 // 16
    return pl.pallas_call(
        attn_fwd_kernel,
        out_shape=(jax.ShapeDtypeStruct(q.shape, BF16), jax.ShapeDtypeStruct((halves*groups, 1, rows), F32)),
        grid_spec=pltpu.PrefetchScalarGridSpec(
            num_scalar_prefetch=2, grid=(halves, groups),
            in_specs=[blk, pl.BlockSpec(kv.shape, lambda p, g, *_: (0, 0))],
            out_specs=[blk, pl.BlockSpec((1, 1, rows), lambda p, g, *_: (p*groups+g, 0, 0))],
            scratch_shapes=[pltpu.VMEM((pieces*PIECE, hd), BF16), pltpu.VMEM((hd, pieces*PIECE), BF16),
                            pltpu.VMEM((hd, rows), F32), pltpu.SMEM((pieces,), jnp.int32)]),
        compiler_params=pltpu.CompilerParams(vmem_limit_bytes=40 << 20),
        cost_estimate=pl.CostEstimate(flops=flops, transcendentals=flops//(4*hd), bytes_accessed=2*(2*q.size+kv.size)),
        name="attn_fwd",
    )(tags, own, q, kv)

def attn_bwd_kernel(tags_ref, own_ref, q_ref, do_ref, o_ref, lse_ref, cos_ref, sin_ref, kv_ref, dq_ref, dkv_ref,
                    k_s, kt_s, v_s, dq_s, dk_s, dv_s, pick_s):
    half = pl.program_id(0)
    group = pl.program_id(1)
    hd = k_s.shape[1]
    pieces = k_s.shape[0] // PIECE
    total = kv_ref.shape[0] // PIECE
    wide = 2 * PIECE
    coef = hd ** -0.5 * LOG2E
    scale = hd ** -0.5

    @pl.when((half == 0) & (group == 0))
    def _():
        find_pieces(tags_ref, own_ref, pick_s, total)
        for i in range(pieces):
            rows = pl.ds(pl.multiple_of(pick_s[i] * PIECE, PIECE), PIECE)
            keys = kv_ref[rows, :hd]
            k_s[i*PIECE:(i+1)*PIECE, :] = keys
            kt_s[:, i*PIECE:(i+1)*PIECE] = keys.T
            v_s[i*PIECE:(i+1)*PIECE, :] = kv_ref[rows, hd:]
        dk_s[...] = jnp.zeros_like(dk_s)
        dv_s[...] = jnp.zeros_like(dv_s)

    q = stack_heads(q_ref, hd)
    do = stack_heads(do_ref, hd)
    prod = do.astype(F32) * stack_heads(o_ref, hd).astype(F32)
    delta = lax.dot_general(jnp.ones((8, hd), F32), prod, (((1,), (1,)), ((), ())),
                            preferred_element_type=F32, precision=lax.Precision.HIGHEST)[:1]
    lse = lse_ref[0]
    dq_s[...] = jnp.zeros_like(dq_s)
    def step(i, carry):
        at = pl.ds(pl.multiple_of(i * wide, wide), wide)
        p = jnp.exp2(contract_last(k_s[at, :], q) * coef - lse)
        dp = contract_last(v_s[at, :], do)
        ds = (p * (dp - delta)).astype(BF16)
        dv_s[at, :] += jnp.dot(p.astype(BF16), do, preferred_element_type=F32)
        dk_s[at, :] += jnp.dot(ds, q, preferred_element_type=F32)
        dq_s[...] += jnp.dot(kt_s[:, at], ds, preferred_element_type=F32)
        return carry
    lax.fori_loop(0, own_ref[half] // 2 + 1, step, 0)
    dq = (dq_s[...] * scale).T
    cos, sin = cos_ref[...], sin_ref[...]
    mid = hd // 2
    for h in range(HEAD_GROUP):
        one = dq[h*PIECE:(h+1)*PIECE, :mid]
        two = dq[h*PIECE:(h+1)*PIECE, mid:]
        dq_ref[:, h*hd:h*hd+mid] = (one * cos + two * sin).astype(BF16)
        dq_ref[:, h*hd+mid:(h+1)*hd] = (two * cos - one * sin).astype(BF16)

    @pl.when((half == pl.num_programs(0) - 1) & (group == pl.num_programs(1) - 1))
    def _():
        dkv_ref[:, :hd] = (dk_s[...] * scale).astype(BF16)
        dkv_ref[:, hd:] = dv_s[...].astype(BF16)

def attn_bwd(tags, own, q, do, o, lse, cos, sin, kv, hd, pieces):
    n_rows, width = q.shape
    groups = width // hd // HEAD_GROUP
    gw = HEAD_GROUP * hd
    halves = n_rows // PIECE
    rows = HEAD_GROUP * PIECE
    blk = pl.BlockSpec((PIECE, gw), lambda p, g, *_: (p, g))
    trig = pl.BlockSpec((PIECE, hd // 2), lambda p, g, *_: (p, 0))
    keys = pieces * PIECE
    flops = 10 * n_rows * width * keys * 9 // 16
    return pl.pallas_call(
        attn_bwd_kernel,
        out_shape=(jax.ShapeDtypeStruct(q.shape, BF16), jax.ShapeDtypeStruct((keys, 2*hd), BF16)),
        grid_spec=pltpu.PrefetchScalarGridSpec(
            num_scalar_prefetch=2, grid=(halves, groups),
            in_specs=[blk, blk, blk, pl.BlockSpec((1, 1, rows), lambda p, g, *_: (p*groups+g, 0, 0)), trig, trig,
                      pl.BlockSpec(kv.shape, lambda p, g, *_: (0, 0))],
            out_specs=[blk, pl.BlockSpec((keys, 2*hd), lambda p, g, *_: (0, 0))],
            scratch_shapes=[pltpu.VMEM((keys, hd), BF16), pltpu.VMEM((hd, keys), BF16), pltpu.VMEM((keys, hd), BF16),
                            pltpu.VMEM((hd, rows), F32), pltpu.VMEM((keys, hd), F32), pltpu.VMEM((keys, hd), F32),
                            pltpu.SMEM((pieces,), jnp.int32)]),
        compiler_params=pltpu.CompilerParams(vmem_limit_bytes=48 << 20),
        cost_estimate=pl.CostEstimate(flops=flops, transcendentals=flops//(10*hd), bytes_accessed=2*(4*q.size+2*kv.size)),
        name="attn_bwd",
    )(tags, own, q, do, o, lse, cos, sin, kv)

MESH = pl.DeviceIdType.MESH


def flip(index, mask):
    out = 0
    bit = 1
    while bit <= mask:
        part = (index // bit) % 2
        out = out + bit * ((1 - part) if mask & bit else part)
        bit *= 2
    return out + (index // bit) * bit


def row_loop(rows, body, step=32):
    if rows % step:
        step = 16

    @pl.loop(0, rows // step)
    def _(i):
        body(pl.ds(pl.multiple_of(i * step, step), step))


class Sender:
    def __init__(self):
        self.open = []

    def make(self, src, dst, send_sem, recv_sem, peer):
        return pltpu.make_async_remote_copy(
            src_ref=src,
            dst_ref=dst,
            send_sem=send_sem,
            recv_sem=recv_sem,
            device_id=peer,
            device_id_type=MESH,
        )

    def __call__(self, *args):
        copy = self.make(*args)
        copy.start()
        self.open.append(copy)
        return copy

    def finish(self):
        for copy in self.open:
            copy.wait_send()


class LineSum:
    def __init__(self, own, got, send_sem, recv_sem, c_idx, f_idx, n_z, sender):
        self.own, self.got, self.send_sem, self.recv_sem = own, got, send_sem, recv_sem
        self.n_z, self.sender = n_z, sender
        self.z = c_idx // 2
        self.left = (c_idx - 2, f_idx)
        self.right = (c_idx + 2, f_idx)

    def copy(self, b, slot, peer):
        return self.sender.make(
            self.own.at[b], self.got.at[slot], self.send_sem.at[b], self.recv_sem.at[slot], peer
        )

    def take(self, b, slot):
        self.copy(b, slot, self.left).wait_recv()

        def add(at):
            self.own[b, at, :] = (
                self.own[b, at, :].astype(F32) + self.got[slot, at, :].astype(F32)
            ).astype(BF16)

        row_loop(self.own.shape[1], add)

    def go_right(self, b):
        z = self.z

        @pl.when(z < b)
        def _():
            @pl.when(z > 0)
            def _():
                self.take(b, b)

            self.copy(b, b, self.right).start()

    def go_left(self, b):
        z, n_z = self.z, self.n_z

        @pl.when(z > b)
        def _():
            @pl.when(z < n_z - 1)
            def _():
                self.take(b, b)

            @pl.when(z - 1 > b)
            def _():
                self.copy(b, b, self.left).start()

            @pl.when(z - 1 == b)
            def _():
                self.copy(b, n_z, self.left).start()

    def step(self, i):
        @pl.when(2 * self.z < self.n_z)
        def _():
            self.go_right(self.n_z - 1 - i)
            self.go_left(i)

        @pl.when(2 * self.z >= self.n_z)
        def _():
            self.go_left(i)
            self.go_right(self.n_z - 1 - i)

    def total(self, store):
        z, n_z = self.z, self.n_z

        @pl.when(z > 0)
        def _():
            self.copy(z, z, self.left).wait_recv()

        @pl.when(z < n_z - 1)
        def _():
            self.copy(z, n_z, self.left).wait_recv()

        rows = self.own.shape[1]

        @pl.when(z == 0)
        def _():
            row_loop(
                rows,
                lambda at: store(
                    at, self.own[z, at, :].astype(F32) + self.got[n_z, at, :].astype(F32)
                ),
            )

        @pl.when(z == n_z - 1)
        def _():
            row_loop(
                rows,
                lambda at: store(
                    at, self.own[z, at, :].astype(F32) + self.got[z, at, :].astype(F32)
                ),
            )

        @pl.when((z > 0) & (z < n_z - 1))
        def _():
            row_loop(
                rows,
                lambda at: store(
                    at,
                    self.own[z, at, :].astype(F32)
                    + self.got[z, at, :].astype(F32)
                    + self.got[n_z, at, :].astype(F32),
                ),
            )

    def finish(self):
        for b in range(self.n_z):

            @pl.when(self.z != b)
            def _(b=b):
                self.copy(b, b, self.left).wait_send()


WINDOW = 3
TAIL_NAMES = ("gate", "kv", "up", "out", "qup", "qd", "kvw")
TAIL_CUT = ("gate", "up", "qup", "qd", "kvw")
TAIL_SENT = ("kv", "up", "out", "qup", "qd", "kvw")


def tail_kernel(n_ctx, n_f, names_in, names_out, names_scratch, *refs):
    n_z = n_ctx // 2
    names = list(names_in) + list(names_out) + list(names_scratch)
    r = dict(zip(names, refs, strict=True))
    c_idx = lax.axis_index("ctx")
    f_idx = lax.axis_index("fsdp")
    y_idx = c_idx % 2
    z_idx = c_idx // 2
    send = Sender()

    def over_c(mask):
        return (flip(c_idx, mask), f_idx)

    def over_f(mask):
        return (c_idx, flip(f_idx, mask))

    barrier = pltpu.get_barrier_semaphore()
    for mask in range(1, n_f):
        pl.semaphore_signal(barrier, inc=1, device_id=over_f(mask), device_id_type=MESH)
    for mask in range(1, n_ctx):
        pl.semaphore_signal(barrier, inc=1, device_id=over_c(mask), device_id_type=MESH)
    pl.semaphore_wait(barrier, n_f - 1 + n_ctx - 1)

    lines = {
        m: LineSum(
            r["pair_" + m],
            r["z_" + m],
            r["z_send"].at[i],
            r["z_recv"].at[i],
            c_idx,
            f_idx,
            n_z,
            send,
        )
        for i, m in enumerate(TAIL_NAMES)
    }
    order = list(range(1, n_z)) + [0]
    y_copies, keeps = {}, {}

    parts = {m: r[m] for m in ("kv", "up", "out", "qup")}
    parts["qd"], parts["kvw"] = r["part_qd"], r["part_kvw"]
    queue = [(m, s) for m in TAIL_SENT for s in order]

    def next_y():
        if queue:
            m, s = queue.pop(0)
            i = TAIL_SENT.index(m)
            b = flip(z_idx, s)
            y_copies[m, s] = send(
                parts[m].at[b, 1 - y_idx],
                r["y_" + m].at[s],
                r["y_send"].at[i, s],
                r["y_recv"].at[i, s],
                over_c(1),
            )
            keep = pltpu.make_async_copy(
                parts[m].at[b, y_idx], r["pair_" + m].at[b], r["keep_sem"].at[i, s]
            )
            keep.start()
            keeps[m, s] = keep

    def add_pair(m, s):
        b = flip(z_idx, s)
        y_copies[m, s].wait_recv()
        next_y()
        keeps[m, s].wait()
        pair, got = r["pair_" + m], r["y_" + m]

        def add(at):
            pair[b, at, :] = (pair[b, at, :].astype(F32) + got[s, at, :].astype(F32)).astype(BF16)

        row_loop(pair.shape[1], add)

    def advance(pair, line):
        for i, s in enumerate(order):
            if pair is not None:
                add_pair(pair, s)
            if line is not None and i < n_z - 1:
                lines[line].step(i)

    f_copies = {}

    def finish_sum(m):
        lines[m].total(lambda at, value: store_total(m, at, value))
        if m in TAIL_CUT:
            i = TAIL_CUT.index(m)
            part = r["tot_" + m].shape[0] // n_f
            for s in range(1, n_f):
                at = pl.ds(pl.multiple_of(flip(f_idx, s) * part, part), part)
                f_copies[m, s] = send(
                    r["tot_" + m].at[at, :],
                    r["f_" + m].at[s - 1],
                    r["f_send"].at[i, s - 1],
                    r["f_recv"].at[i, s - 1],
                    over_f(s),
                )

    def store_total(m, at, value):
        if m in TAIL_CUT:
            r["tot_" + m][at, :] = value.astype(BF16)
        else:
            r["out_" + m][at, :] = value

    def put_out(m):
        total, out = r["tot_" + m], r["out_" + m]
        rows, width = total.shape
        part = rows // n_f
        for s in range(n_f):
            at = pl.ds(pl.multiple_of(flip(f_idx, s) * width, 128), width)
            if s:
                f_copies[m, s].wait_recv()
                out[:, at] = r["f_" + m][s - 1].astype(F32)
            else:
                mine = pl.ds(pl.multiple_of(f_idx * part, part), part)
                out[:, at] = total[mine, :].astype(F32)

    def cut_low(src, dst, width, index):
        rows = src.shape[0]
        mine = pl.ds(pl.multiple_of(f_idx * rows, rows), rows)
        copies = []
        for s in range(1, n_f):
            at = pl.ds(pl.multiple_of(flip(f_idx, s) * width, 128), width)
            copies.append(
                send(
                    src.at[:, at],
                    dst.at[mine, :],
                    r["low_send"].at[index, s - 1],
                    r["low_recv"].at[index, s - 1],
                    over_f(s),
                )
            )
        own = pl.ds(pl.multiple_of(f_idx * width, 128), width)
        dst[mine, :] = src[:, own]
        return copies

    for _ in range(WINDOW):
        next_y()
    q_copies = cut_low(r["dqa"], r["qd_group"], r["qd_group"].shape[1], 0)
    pair_in = pltpu.make_async_copy(r["gate"], r["pair_gate"], r["keep_sem"].at[0, n_z])
    pair_in.start()
    pair_in.wait()
    advance("kv", "gate")
    advance("up", "kv")
    finish_sum("gate")

    head = r["dkv"].shape[1] // 2
    mid = head // 2

    def store_kv(at, value):
        cos, sin = r["cos"][at, :], r["sin"][at, :]
        one, two = value[:, :mid], value[:, mid:head]
        r["dkv"][at, :mid] = (one * cos + two * sin).astype(BF16)
        r["dkv"][at, mid:head] = (two * cos - one * sin).astype(BF16)
        r["dkv"][at, head:] = value[:, head:].astype(BF16)

    lines["kv"].total(store_kv)
    kv_copies = cut_low(r["dkv"], r["kv_group"], r["kv_group"].shape[1], 1)

    def low_part(group, part):
        normed = r["normed_group"]
        rows = part.shape[2]
        for c in range(n_ctx):
            part[c // 2, c % 2] = lax.dot_general(
                normed[:, c * rows : (c + 1) * rows],
                group[...],
                (((0,), (0,)), ((), ())),
                preferred_element_type=F32,
            ).astype(BF16)

    for copy in q_copies:
        copy.wait_recv()
    low_part(r["qd_group"], r["part_qd"])
    advance("out", "up")
    for copy in kv_copies:
        copy.wait_recv()
    low_part(r["kv_group"], r["part_kvw"])

    grad_in, w_kv = r["grad_input"], r["w_kv"]
    width = grad_in.shape[1]
    tile = 256

    @pl.loop(0, width // tile)
    def _(t):
        at = pl.ds(pl.multiple_of(t * tile, tile), tile)
        grad_in[:, at] = r["da_q"][:, at] + lax.dot_general(
            r["dkv"][...],
            w_kv[at, :],
            (((1,), (1,)), ((), ())),
            preferred_element_type=F32,
        )

    r["gain_sum"][...] = jnp.zeros_like(r["gain_sum"])
    gain = r["gain_one"][...]

    def norm_rows(at):
        value = r["hidden"][at, :].astype(F32)
        grad = grad_in[at, :]
        scale = lax.rsqrt(jnp.mean(value * value, axis=-1, keepdims=True) + NORM_EPS)
        r["gain_sum"][...] += jnp.sum(grad * value * scale, axis=0, keepdims=True)
        ge = gain * grad
        inner = jnp.mean(ge * value, axis=-1, keepdims=True)
        grad_in[at, :] = (
            r["grad_resid"][at, :] + scale * ge - value * (scale * scale * scale) * inner
        )

    row_loop(grad_in.shape[0], norm_rows, step=16)

    small, small_got = r["small_out"], r["small_got"]
    small[...] = r["small"][...]
    for i in range(width // 128):
        small[i : i + 1, :] = r["gain_sum"][:, i * 128 : (i + 1) * 128]
    steps = [over_f(1), over_f(2), over_c(1)]
    mask = 2
    while mask < n_ctx:
        steps.append(over_c(mask))
        mask *= 2
    small_copies = {}

    def small_start(s):
        small_got[s, 0] = small[...]
        small_copies[s] = send(
            small_got.at[s, 0],
            small_got.at[s, 1],
            r["s_send"].at[s],
            r["s_recv"].at[s],
            steps[s],
        )

    def small_end(s):
        small_copies[s].wait_recv()
        small[...] = small[...] + small_got[s, 1]

    for s in range(2):
        small_start(s)
        small_end(s)
    small_start(2)

    put_out("gate")
    advance("qup", "out")
    finish_sum("up")
    advance("qd", "qup")
    finish_sum("out")
    small_end(2)
    small_start(3)
    advance("kvw", "qd")
    put_out("up")
    finish_sum("qup")
    advance(None, "kvw")
    for s in range(3, len(steps)):
        if s > 3:
            small_start(s)
        small_end(s)
    finish_sum("qd")
    finish_sum("kvw")
    for m in ("qup", "qd", "kvw"):
        put_out(m)
    send.finish()
    for m in TAIL_NAMES:
        lines[m].finish()


def tail_reduce(n_ctx, n_f, inputs, q_width):
    n_z = n_ctx // 2
    vmem = pl.BlockSpec(memory_space=pltpu.VMEM)
    anywhere = pl.BlockSpec(memory_space=pl.ANY)
    rows, width = inputs["hidden"].shape
    kv_width = inputs["w_kv"].shape[1]
    in_hbm = ("gate", "kv", "up", "out", "qup")
    names_in = tuple(inputs)
    in_specs = [anywhere if m in in_hbm else vmem for m in names_in]
    block = {m: inputs[m].shape[-2:] for m in in_hbm}
    block["qd"] = (width // n_ctx, q_width // n_f)
    block["kvw"] = (width // n_ctx, kv_width // n_f)
    outs = {
        "small_out": jax.ShapeDtypeStruct(inputs["small"].shape, F32),
        "grad_input": jax.ShapeDtypeStruct((rows, width), F32),
    }
    scratch = {}
    for m in TAIL_NAMES:
        high, wide = block[m]
        scratch["pair_" + m] = pltpu.VMEM((n_z, high, wide), BF16)
        scratch["z_" + m] = pltpu.VMEM((n_z + 1, high, wide), BF16)
        if m in TAIL_SENT:
            scratch["y_" + m] = pltpu.VMEM((n_z, high, wide), BF16)
        if m in TAIL_CUT:
            scratch["tot_" + m] = pltpu.VMEM((high, wide), BF16)
            scratch["f_" + m] = pltpu.VMEM((n_f - 1, high // n_f, wide), BF16)
            outs["out_" + m] = jax.ShapeDtypeStruct((high // n_f, wide * n_f), F32)
        elif m != "kv":
            outs["out_" + m] = jax.ShapeDtypeStruct((high, wide), F32)
    scratch["dkv"] = pltpu.VMEM((rows, kv_width), BF16)
    scratch["qd_group"] = pltpu.VMEM((rows * n_f, q_width // n_f), BF16)
    scratch["kv_group"] = pltpu.VMEM((rows * n_f, kv_width // n_f), BF16)
    scratch["part_qd"] = pltpu.VMEM((n_z, 2) + block["qd"], BF16)
    scratch["part_kvw"] = pltpu.VMEM((n_z, 2) + block["kvw"], BF16)
    scratch["gain_sum"] = pltpu.VMEM((1, width), F32)
    steps = 2 + (n_ctx.bit_length() - 1)
    scratch["small_got"] = pltpu.VMEM((steps, 2) + inputs["small"].shape, F32)
    dma = pltpu.SemaphoreType.DMA
    sent, cut = len(TAIL_SENT), len(TAIL_CUT)
    scratch["s_send"] = dma((steps,))
    scratch["s_recv"] = dma((steps,))
    scratch["y_send"] = dma((sent, n_z))
    scratch["y_recv"] = dma((sent, n_z))
    scratch["keep_sem"] = dma((sent, n_z + 1))
    scratch["z_send"] = dma((len(TAIL_NAMES), n_z))
    scratch["z_recv"] = dma((len(TAIL_NAMES), n_z + 1))
    scratch["f_send"] = dma((cut, n_f - 1))
    scratch["f_recv"] = dma((cut, n_f - 1))
    scratch["low_send"] = dma((2, n_f - 1))
    scratch["low_recv"] = dma((2, n_f - 1))
    values = pl.pallas_call(
        functools.partial(tail_kernel, n_ctx, n_f, names_in, tuple(outs), tuple(scratch)),
        out_shape=tuple(outs.values()),
        in_specs=in_specs,
        out_specs=tuple([vmem] * len(outs)),
        scratch_shapes=list(scratch.values()),
        compiler_params=pltpu.CompilerParams(
            collective_id=0, has_side_effects=True, vmem_limit_bytes=60 << 20
        ),
        name="tail_reduce",
    )(*inputs.values())
    return dict(zip(outs, values, strict=True))


def front_kernel(n_ctx, n_f, names, *refs):
    r = dict(zip(names, refs, strict=True))
    n_z = n_ctx // 2
    c_idx = lax.axis_index("ctx")
    f_idx = lax.axis_index("fsdp")
    y_idx = c_idx % 2
    z_bit = (c_idx // 2) % 2
    x_idx = f_idx // 2
    k_idx = f_idx % 2
    far_idx = flip(f_idx, 2)
    moves = Sender()
    local = []
    at_sem = [0]

    def over_c(mask):
        return (flip(c_idx, mask), f_idx)

    def over_f(mask):
        return (c_idx, flip(f_idx, mask))

    def send(src, dst, peer):
        i = at_sem[0]
        at_sem[0] += 1
        return moves(src, dst, r["send_sem"].at[i], r["recv_sem"].at[i], peer)

    def keep(src, dst):
        copy = pltpu.make_async_copy(src, dst, r["local_sem"].at[len(local)])
        copy.start()
        local.append(copy)
        return copy

    def rows(start, size):
        return pl.ds(pl.multiple_of(start, size), size)

    barrier = pltpu.get_barrier_semaphore()
    for mask in range(1, n_f):
        pl.semaphore_signal(barrier, inc=1, device_id=over_f(mask), device_id_type=MESH)
    for mask in range(1, n_ctx):
        pl.semaphore_signal(barrier, inc=1, device_id=over_c(mask), device_id_type=MESH)
    pl.semaphore_wait(barrier, n_f - 1 + n_ctx - 1)

    infos, tags = r["infos"], r["tags"]
    infos[f_idx] = r["info"][...]
    info_copies = [
        send(infos.at[f_idx], infos.at[f_idx], over_f(mask)) for mask in range(1, n_f)
    ]

    class Rows:
        def __init__(self, shard, dest, bit, hop, chunks):
            self.dest, self.bit, self.hop = dest, bit, hop
            self.shard = shard
            self.size = shard.shape[0]
            self.half = self.size // 2
            self.step = self.half // chunks
            self.chunks = chunks
            self.far, self.next, self.cross = [], [], []

        def start(self, spare=None):
            mine = self.dest.at[rows(f_idx * self.size, self.size)]
            if spare is None:
                self.kept = keep(self.shard, mine)
            else:
                self.spare, self.kept = spare, keep(self.shard, spare)
            self.cross.append(send(self.shard, mine, over_f(1)))

        def settle(self):
            self.kept.wait()
            keep(self.spare, self.dest.at[rows(f_idx * self.size, self.size)])

        def reach(self, i):
            part = self.bit * self.half + i * self.step
            self.far.append(
                send(
                    self.shard.at[rows(part, self.step)],
                    self.dest.at[rows(f_idx * self.size + part, self.step)],
                    over_f(2),
                )
            )

        def place(self, bit, i):
            return self.dest.at[rows(far_idx * self.size + bit * self.half + i * self.step, self.step)]

        def hop_on(self, i):
            self.far[i].wait_recv()
            reach_next()
            here = self.place(self.bit, i)
            self.next.append(send(here, here, over_c(self.hop)))
            self.cross.append(send(here, here, over_f(1)))

        def pass_on(self, i):
            self.next[i].wait_recv()
            here = self.place(1 - self.bit, i)
            self.cross.append(send(here, here, over_f(1)))

        def end(self):
            for copy in self.cross:
                copy.wait_recv()

    class Columns:
        def __init__(self, shard, dest, box, bits, hops):
            self.shard, self.dest, self.box = shard, dest, box
            self.bits, self.hops = bits, hops
            self.size = shard.shape[0]
            self.width = dest.shape[1]
            self.quarter = self.size // 4

        def columns(self, start, count=1):
            return pl.ds(pl.multiple_of(start * self.width, 128), count * self.width)

        def start(self, spare):
            mine = self.dest.at[rows(f_idx * self.size, self.size)]
            self.spare, self.kept = spare, keep(self.shard.at[:, self.columns(f_idx)], spare)
            self.cross = [send(self.shard.at[:, self.columns(flip(f_idx, 1))], mine, over_f(1))]

        def settle(self):
            self.kept.wait()
            keep(self.spare, self.dest.at[rows(f_idx * self.size, self.size)])

        def reach(self, i):
            one, two = self.bits
            at = rows((two * 2 + one) * self.quarter, self.quarter)
            self.far = send(
                self.shard.at[at, self.columns((1 - x_idx) * 2, 2)], self.box.at[at], over_f(2)
            )

        def piece(self, one, two):
            return self.box.at[rows((two * 2 + one) * self.quarter, self.quarter)]

        def first(self):
            one, two = self.bits
            self.far.wait_recv()
            reach_next()
            here = self.piece(one, two)
            self.step = send(here, here, over_c(self.hops[0]))
            self.last = [send(here, here, over_c(self.hops[1]))]

        def second(self):
            one, two = self.bits
            self.step.wait_recv()
            here = self.piece(1 - one, two)
            self.last.append(send(here, here, over_c(self.hops[1])))

        def part(self):
            for copy in self.last:
                copy.wait_recv()
            there = self.dest.at[rows(far_idx * self.size, self.size)]
            self.cross.append(send(self.box.at[:, self.columns(1 - k_idx)], there, over_f(1)))
            keep(self.box.at[:, self.columns(k_idx)], there)

        def end(self):
            for copy in self.cross:
                copy.wait_recv()

    kv = Rows(r["kv_weight"], r["kv_full"], y_idx, 1, 1)
    qd = Rows(r["q_down"], r["qd_full"], y_idx, 1, 1)
    qu = Rows(r["q_up"], r["qu_full"], y_idx, 1, 2)
    out = Rows(r["out_proj"], r["w_out"], z_bit, 2, 4)
    gate = Columns(r["w_gate"], r["gate_full"], r["gate_box"], (y_idx, z_bit), (1, 2))
    up = Columns(r["w_up"], r["up_full"], r["up_box"], (z_bit, y_idx), (2, 1))
    queue = [(kv, 0), (qd, 0), (qu, 0), (qu, 1), (gate, 0), (up, 0)]
    queue += [(out, i) for i in range(out.chunks)]

    def reach_next():
        if queue:
            part, i = queue.pop(0)
            part.reach(i)

    reach_next()
    reach_next()
    kv.start()
    qd.start()

    for copy in info_copies:
        copy.wait_recv()
    d1 = r["gain_one"].shape[1] // n_f // 128
    d2 = r["gain_q"].shape[1] // n_f // 128
    count = infos[0, 2 * d1 + d2 : 2 * d1 + d2 + 1, :]
    for f in range(n_f):
        for i in range(d1):
            col = slice((f * d1 + i) * 128, (f * d1 + i + 1) * 128)
            r["gain_one"][:, col] = infos[f, i : i + 1, :]
            r["gain_two"][:, col] = infos[f, d1 + d2 + i : d1 + d2 + i + 1, :]
        for i in range(d2):
            col = slice((f * d2 + i) * 128, (f * d2 + i + 1) * 128)
            r["gain_q"][:, col] = infos[f, d1 + i : d1 + i + 1, :]
        if f:
            count = count + infos[f, 2 * d1 + d2 : 2 * d1 + d2 + 1, :]
    tags[c_idx] = r["tag"][...]
    tags[c_idx, 1:2, :] = count
    tag_copies = [send(tags.at[c_idx], tags.at[c_idx], over_c(mask)) for mask in range(1, n_ctx)]

    normed = r["normed"]
    gain_one = r["gain_one"][...]

    def norm_rows(at):
        value = r["hidden"][at, :].astype(F32)
        scale = lax.rsqrt(jnp.mean(value * value, axis=-1, keepdims=True) + NORM_EPS)
        normed[at, :] = (value * scale * gain_one).astype(BF16)

    row_loop(normed.shape[0], norm_rows, step=16)

    kv.hop_on(0)
    qd.hop_on(0)
    qu.start()
    kv.pass_on(0)
    qd.pass_on(0)
    kv.end()
    kv.kept.wait()
    head = r["kv_full"].shape[1] // 2
    mid = head // 2
    cos, sin = r["cos"], r["sin"]
    kv_rows = r["kv_rows"]
    keys = jnp.dot(normed[...], r["kv_full"][:, :head], preferred_element_type=F32)
    one, two = keys[:, :mid], keys[:, mid:]
    kv_rows[:, :mid] = (one * cos[...] - two * sin[...]).astype(BF16)
    kv_rows[:, mid:head] = (two * cos[...] + one * sin[...]).astype(BF16)
    kv_rows[:, head:] = jnp.dot(
        normed[...], r["kv_full"][:, head:], preferred_element_type=F32
    ).astype(BF16)
    all_kv = r["all_kv"]
    tokens = normed.shape[0]

    def kv_place(c):
        return all_kv.at[rows(c * tokens, tokens)]

    kv_z = [send(kv_rows, kv_place(c_idx), over_c(2 * s)) for s in range(1, n_z)]
    kv_y = [send(kv_rows, kv_place(c_idx), over_c(1))]
    keep(kv_rows, kv_place(c_idx))
    qu.hop_on(0)
    qd.end()
    qd.kept.wait()

    @pl.loop(0, r["q_low"].shape[1] // 256)
    def _(t):
        at = pl.ds(pl.multiple_of(t * 256, 256), 256)
        r["q_low"][:, at] = jnp.dot(
            normed[...], r["qd_full"][:, at], preferred_element_type=F32
        )

    gain_q = r["gain_q"][...]

    def norm_low(at):
        value = r["q_low"][at, :]
        scale = lax.rsqrt(jnp.mean(value * value, axis=-1, keepdims=True) + NORM_EPS)
        r["q_normed"][at, :] = (value * scale * gain_q).astype(BF16)

    row_loop(tokens, norm_low, step=16)
    qu.hop_on(1)
    for s in range(1, n_z):
        kv_z[s - 1].wait_recv()
        here = kv_place(flip(c_idx, 2 * s))
        kv_y.append(send(here, here, over_c(1)))
    qu.pass_on(0)
    qu.pass_on(1)
    gate.first()
    qu.end()
    for m, part in (("gate", gate), ("up", up), ("out", out)):
        part.start(r[m + "_spare"])
    qu.kept.wait()

    @pl.loop(0, r["q_rot"].shape[1] // head)
    def _(h):
        start = pl.multiple_of(h * head, head)
        value = jnp.dot(
            r["q_normed"][...],
            r["qu_full"][:, pl.ds(start, head)],
            preferred_element_type=F32,
        )
        one, two = value[:, :mid], value[:, mid:]
        r["q_rot"][:, pl.ds(start, mid)] = (one * cos[...] - two * sin[...]).astype(BF16)
        late = pl.multiple_of(h * head + mid, mid)
        r["q_rot"][:, pl.ds(late, mid)] = (two * cos[...] + one * sin[...]).astype(BF16)

    up.first()
    for part in (gate, up, out):
        part.settle()
    for m in ("kv", "qd", "qu"):
        keep(r[m + "_full"], r["w_" + m])
    gate.second()
    out.hop_on(0)
    up.second()
    for i in range(1, out.chunks):
        out.hop_on(i)
    gate.part()
    for i in range(out.chunks):
        out.pass_on(i)
    up.part()
    for copy in kv_y + tag_copies:
        copy.wait_recv()
    for part in (gate, up, out):
        part.end()
    for copy in local:
        if not any(copy is part.kept for part in (kv, qd, qu, gate, up, out)):
            copy.wait()
    moves.finish()


def front(n_ctx, n_f, inputs, head_size):
    tokens, width = inputs["hidden"].shape
    shape = jax.ShapeDtypeStruct
    q_width = inputs["q_down"].shape[1]
    heads_width = inputs["q_up"].shape[1]
    part = inputs["w_gate"].shape[1] // n_f

    def whole(m):
        return (inputs[m].shape[0] * n_f, inputs[m].shape[1])

    in_hbm = ("q_down", "kv_weight", "q_up", "out_proj", "w_gate", "w_up")
    outs = {
        "w_qd": shape(whole("q_down"), BF16),
        "w_kv": shape(whole("kv_weight"), BF16),
        "w_qu": shape(whole("q_up"), BF16),
        "w_out": shape(whole("out_proj"), BF16),
        "gate_full": shape((width, part), BF16),
        "up_full": shape((width, part), BF16),
        "all_kv": shape((tokens * n_ctx, 2 * head_size), BF16),
        "normed": shape((tokens, width), BF16),
        "q_low": shape((tokens, q_width), F32),
        "q_normed": shape((tokens, q_width), BF16),
        "q_rot": shape((tokens, heads_width), BF16),
        "gain_one": shape((1, width), F32),
        "gain_q": shape((1, q_width), F32),
        "gain_two": shape((1, width), F32),
        "tags": shape((n_ctx, 8, 128), F32),
    }
    out_hbm = ("w_qd", "w_kv", "w_qu", "w_out", "gate_full", "up_full", "all_kv")
    box = (inputs["w_gate"].shape[0], 2 * part)
    dma = pltpu.SemaphoreType.DMA
    scratch = {
        "infos": pltpu.VMEM((n_f,) + inputs["info"].shape, F32),
        "qd_full": pltpu.VMEM(whole("q_down"), BF16),
        "kv_full": pltpu.VMEM(whole("kv_weight"), BF16),
        "qu_full": pltpu.VMEM(whole("q_up"), BF16),
        "gate_box": pltpu.VMEM(box, BF16),
        "up_box": pltpu.VMEM(box, BF16),
        "gate_spare": pltpu.VMEM((box[0], part), BF16),
        "up_spare": pltpu.VMEM((box[0], part), BF16),
        "out_spare": pltpu.VMEM(inputs["out_proj"].shape, BF16),
        "kv_rows": pltpu.VMEM((tokens, 2 * head_size), BF16),
        "send_sem": dma((64 + 2 * n_ctx,)),
        "recv_sem": dma((64 + 2 * n_ctx,)),
        "local_sem": dma((16,)),
    }
    vmem = pl.BlockSpec(memory_space=pltpu.VMEM)
    anywhere = pl.BlockSpec(memory_space=pl.ANY)
    names = tuple(inputs) + tuple(outs) + tuple(scratch)
    values = pl.pallas_call(
        functools.partial(front_kernel, n_ctx, n_f, names),
        out_shape=tuple(outs.values()),
        in_specs=[anywhere if m in in_hbm else vmem for m in inputs],
        out_specs=tuple([anywhere if m in out_hbm else vmem for m in outs]),
        scratch_shapes=list(scratch.values()),
        compiler_params=pltpu.CompilerParams(
            collective_id=1, has_side_effects=True, vmem_limit_bytes=48 << 20
        ),
        name="front",
    )(*inputs.values())
    return dict(zip(outs, values, strict=True))


def tiles(total, wide, body):
    whole = total // wide

    @pl.loop(0, whole)
    def _(t):
        body(pl.multiple_of(t * wide, wide), wide)

    if total % wide:
        body(whole * wide, total % wide)


def contract_first(a, b):
    return jnp.dot(a.T, b, preferred_element_type=F32)


def ffn_kernel(n_f, names, *refs):
    r = dict(zip(names, refs, strict=True))
    c_idx = lax.axis_index("ctx")
    f_idx = lax.axis_index("fsdp")
    moves = Sender()
    at_sem = [0]
    core, far = (c_idx, flip(f_idx, 1)), (c_idx, flip(f_idx, 2))

    def send(src, dst, peer):
        i = at_sem[0]
        at_sem[0] += 1
        return moves(src, dst, r["send_sem"].at[i], r["recv_sem"].at[i], peer)

    barrier = pltpu.get_barrier_semaphore()
    for peer in (core, far):
        pl.semaphore_signal(barrier, inc=1, device_id=peer, device_id_type=MESH)
    pl.semaphore_wait(barrier, 2)

    tokens, width = r["normed"].shape
    units = r["w_down"].shape[0]
    group, dz = r["group"], r["dz"]
    block = [slice(i * tokens, (i + 1) * tokens) for i in range(4)]
    pair = [slice(0, 2 * tokens), slice(2 * tokens, 4 * tokens)]

    def gather(buf):
        to_core = send(buf.at[block[0]], buf.at[block[1]], core)
        to_far = send(buf.at[block[0]], buf.at[block[2]], far)
        return to_core, to_far

    def gather_far(buf, to_far):
        to_far.wait_recv()
        send(buf.at[block[2]], buf.at[block[3]], core).wait_recv()

    group[block[0], :] = r["normed"][...]
    to_core, to_far = gather(group)
    loads = []
    for i, m in enumerate(("gate", "up", "down")):
        load = pltpu.make_async_copy(r["w_" + m], r["v_" + m], r["load_sem"].at[i])
        load.start()
        loads.append(load)
    loads[0].wait()
    loads[1].wait()

    def hidden_part(rows):
        def one(start, wide):
            at = pl.ds(start, wide)
            both = jnp.concatenate([r["v_gate"][:, at], r["v_up"][:, at]], axis=1)
            out = jnp.dot(group[rows, :], both, preferred_element_type=F32)
            gate, up = out[:, :wide], out[:, wide:]
            r["gate"][rows, at] = gate.astype(BF16)
            r["up"][rows, at] = up.astype(BF16)
            r["hid"][rows, at] = (gate / (1.0 + jnp.exp(-gate)) * up).astype(BF16)

        tiles(units, 128, one)

    to_core.wait_recv()
    hidden_part(pair[0])
    gather_far(group, to_far)
    hidden_part(pair[1])
    loads[2].wait()

    def down_block(i, dest):
        def one(start, wide):
            at = pl.ds(start, wide)
            dest[:, at] = jnp.dot(
                r["hid"][block[i], :], r["v_down"][:, at], preferred_element_type=F32
            ).astype(dest.dtype)

        tiles(width, 256, one)

    def back_block(i, dest):
        def one(start, wide):
            at = pl.ds(start, wide)
            dest[:, at] = (
                contract_last(r["gate"][block[i], :], r["v_gate"][at, :])
                + contract_last(r["up"][block[i], :], r["v_up"][at, :])
            ).astype(dest.dtype)

        tiles(width, 256, one)

    def add_rows(dest, one, two):
        def add(at):
            dest[at, :] = (one[at, :].astype(F32) + two[at, :].astype(F32)).astype(dest.dtype)

        row_loop(tokens, add)

    def far_sum(k, make):
        make(3, r["give"].at[2 * k])
        step = send(r["give"].at[2 * k], r["got"].at[2 * k], core)
        make(2, r["far_sum"])
        step.wait_recv()
        add_rows(r["far_give"].at[k], r["far_sum"], r["got"].at[2 * k])
        return send(r["far_give"].at[k], r["far_got"].at[k], far)

    def near_sum(k, make):
        make(1, r["give"].at[2 * k + 1])
        step = send(r["give"].at[2 * k + 1], r["got"].at[2 * k + 1], core)
        make(0, r["near_sum"])
        return step

    def near_end(k, step):
        step.wait_recv()
        add_rows(r["near_sum"], r["near_sum"], r["got"].at[2 * k + 1])

    far_step = far_sum(0, down_block)
    near_end(0, near_sum(0, down_block))
    far_step.wait_recv()
    r["sq"][...] = jnp.zeros_like(r["sq"])

    def loss_rows(at):
        value = r["resid"][at, :] + r["near_sum"][at, :] + r["far_got"][0, at, :].astype(F32)
        r["result"][at, :] = value.astype(BF16)
        diff = value - r["teacher"][at, :].astype(F32)
        squares = jnp.sum(diff * diff, axis=1, keepdims=True) * r["valid"][at, :]
        r["sq"][:1, :] += jnp.sum(squares, axis=0, keepdims=True)
        grad = diff * r["valid_scale"][at, :1]
        r["grad_resid"][at, :] = grad
        dz[at, :] = grad.astype(BF16)

    row_loop(tokens, loss_rows, step=16)
    to_core, to_far = gather(dz)

    def back_hidden(rows):
        def one(start, wide):
            at = pl.ds(start, wide)
            grad = contract_last(dz[rows, :], r["v_down"][at, :])
            gate = r["gate"][rows, at].astype(F32)
            up = r["up"][rows, at].astype(F32)
            sigma = 1.0 / (1.0 + jnp.exp(-gate))
            r["gate"][rows, at] = (grad * up * sigma * (1.0 + gate * (1.0 - sigma))).astype(BF16)
            r["up"][rows, at] = (grad * (gate * sigma)).astype(BF16)

        tiles(units, 256, one)

    to_core.wait_recv()
    back_hidden(pair[0])
    near_step = near_sum(1, back_block)
    gather_far(dz, to_far)
    back_hidden(pair[1])
    far_step = far_sum(1, back_block)
    near_end(1, near_step)

    saves = []

    def save(src, dst, i):
        copy = pltpu.make_async_copy(src, dst, r["save_sem"].at[i])
        copy.start()
        return copy

    def down_tile(start, wide):
        at = pl.ds(start, wide)
        spot = r["tile"].at[pl.ds(0, wide)]
        spot[...] = contract_first(r["hid"][:, at], dz[...]).astype(BF16)
        save(spot, r["down_part"].at[at], 0).wait()

    tiles(units, 128, down_tile)

    def gate_tile(start, wide):
        at = pl.ds(start, wide)
        left = group[:, at].T
        for i, m in enumerate(("gate", "up")):
            spot = r["wide_tile"].at[i]
            spot[...] = jnp.dot(left, r[m][...], preferred_element_type=F32).astype(BF16)
            saves.append(save(spot, r[m + "_part"].at[at], 1 + i))
        saves.pop().wait()
        saves.pop().wait()

    tiles(width, 256, gate_tile)
    far_step.wait_recv()
    gain = r["gain_two"][...]
    r["gain_sum"][...] = jnp.zeros_like(r["gain_sum"])

    def norm_rows(at):
        grad = r["near_sum"][at, :] + r["far_got"][1, at, :].astype(F32)
        value = r["resid"][at, :]
        scale = lax.rsqrt(jnp.mean(value * value, axis=-1, keepdims=True) + NORM_EPS)
        r["gain_sum"][...] += jnp.sum(grad * value * scale, axis=0, keepdims=True)
        ge = gain * grad
        inner = jnp.mean(ge * value, axis=-1, keepdims=True)
        total = r["grad_resid"][at, :] + scale * ge - value * (scale * scale * scale) * inner
        r["grad_resid"][at, :] = total
        r["grad_branch"][at, :] = total.astype(BF16)

    row_loop(tokens, norm_rows, step=16)
    moves.finish()


def feed_forward(n_f, inputs):
    tokens, width = inputs["normed"].shape
    units = inputs["w_down"].shape[0]
    shape = jax.ShapeDtypeStruct
    outs = {
        "result": shape((tokens, width), BF16),
        "grad_resid": shape((tokens, width), F32),
        "grad_branch": shape((tokens, width), BF16),
        "down_part": shape((units, width), BF16),
        "gate_part": shape((width, units), BF16),
        "up_part": shape((width, units), BF16),
        "gain_sum": shape((1, width), F32),
        "sq": shape((8, 128), F32),
    }
    hbm = ("w_gate", "w_up", "w_down", "down_part", "gate_part", "up_part")
    dma = pltpu.SemaphoreType.DMA
    many = tokens * n_f
    scratch = {
        "v_gate": pltpu.VMEM((width, units), BF16),
        "v_up": pltpu.VMEM((width, units), BF16),
        "v_down": pltpu.VMEM((units, width), BF16),
        "group": pltpu.VMEM((many, width), BF16),
        "dz": pltpu.VMEM((many, width), BF16),
        "gate": pltpu.VMEM((many, units), BF16),
        "up": pltpu.VMEM((many, units), BF16),
        "hid": pltpu.VMEM((many, units), BF16),
        "give": pltpu.VMEM((4, tokens, width), BF16),
        "got": pltpu.VMEM((4, tokens, width), BF16),
        "far_sum": pltpu.VMEM((tokens, width), F32),
        "near_sum": pltpu.VMEM((tokens, width), F32),
        "far_give": pltpu.VMEM((2, tokens, width), BF16),
        "far_got": pltpu.VMEM((2, tokens, width), BF16),
        "tile": pltpu.VMEM((128, width), BF16),
        "wide_tile": pltpu.VMEM((2, 256, units), BF16),
        "send_sem": dma((16,)),
        "recv_sem": dma((16,)),
        "load_sem": dma((3,)),
        "save_sem": dma((3,)),
    }
    vmem = pl.BlockSpec(memory_space=pltpu.VMEM)
    anywhere = pl.BlockSpec(memory_space=pl.ANY)
    names = tuple(inputs) + tuple(outs) + tuple(scratch)
    values = pl.pallas_call(
        functools.partial(ffn_kernel, n_f, names),
        out_shape=tuple(outs.values()),
        in_specs=[anywhere if m in hbm else vmem for m in inputs],
        out_specs=tuple([anywhere if m in hbm else vmem for m in outs]),
        scratch_shapes=list(scratch.values()),
        compiler_params=pltpu.CompilerParams(
            collective_id=2, has_side_effects=True, vmem_limit_bytes=60 << 20
        ),
        name="feed_forward",
    )(*inputs.values())
    return dict(zip(outs, values, strict=True))


def body(
    hidden_in,
    teacher,
    blocks,
    seq_ids,
    valid_mask,
    norm1_gain,
    q_down,
    q_gain,
    q_up,
    kv_weight,
    out_proj,
    norm2_gain,
    w_gate,
    w_up,
    w_down,
):
    row_count, model_width = hidden_in.shape
    head_size = kv_weight.shape[1] // 2
    heads_width = q_up.shape[1]
    head_count = heads_width // head_size
    half_dim = head_size // 2
    q_width = q_down.shape[1]
    n_ctx = lax.axis_size("ctx")
    n_f = lax.axis_size("fsdp")
    n_z = n_ctx // 2
    token_total = row_count * n_ctx * n_f
    seq_pieces = 2 * SEQ_BLOCKS
    c_idx = lax.axis_index("ctx")
    f_idx = lax.axis_index("fsdp")
    y_idx = c_idx % 2
    z_idx = c_idx // 2
    x_idx = f_idx // 2
    k_idx = f_idx % 2

    def by_f(values, mask):
        return lax.ppermute(values, "fsdp", [(i, i ^ mask) for i in range(n_f)])

    def by_c(values, mask):
        return lax.ppermute(values, "ctx", [(i, i ^ mask) for i in range(n_ctx)])

    def cut(values, start, size, axis):
        return lax.dynamic_slice_in_dim(values, start, size, axis)

    def ctx_split(grad):
        view = grad.reshape(n_z, 2, grad.shape[0] // n_ctx, grad.shape[1])
        give = lax.dynamic_index_in_dim(view, 1 - y_idx, 1, keepdims=False)
        keep = lax.dynamic_index_in_dim(view, y_idx, 1, keepdims=False)
        return give, keep

    def ctx_pair(keep, got):
        return (keep.astype(F32) + got.astype(F32)).astype(BF16)

    def ctx_spread(pair):
        return [pair] + [
            by_c(lax.dynamic_index_in_dim(pair, z_idx ^ r, 0, keepdims=False), 2 * r)
            for r in range(1, n_z)
        ]

    def ctx_total(parts):
        total = lax.dynamic_index_in_dim(parts[0], z_idx, 0, keepdims=False).astype(F32)
        for got in parts[1:]:
            total = total + got.astype(F32)
        return total

    def group_rows(values):
        return lax.all_gather(values, "fsdp", axis=0, tiled=True)

    valid_f = valid_mask.astype(F32)
    own_pieces = row_count // PIECE
    info = jnp.concatenate(
        [
            norm1_gain.astype(F32),
            q_gain.astype(F32),
            norm2_gain.astype(F32),
            jnp.full((128,), jnp.sum(valid_f)),
        ]
    )
    info = jnp.pad(info, (0, -info.shape[0] % 1024)).reshape(-1, 128)
    own_tags = jnp.stack([blocks.reshape(-1, PIECE)[:, 0], seq_ids.reshape(-1, PIECE)[:, 0]], 1)
    tag = jnp.pad(own_tags.astype(F32).reshape(1, -1), ((0, 7), (0, 128 - 2 * own_pieces)))
    own = jnp.concatenate([blocks.reshape(-1, PIECE)[:, 0], seq_ids[:1]])

    positions = blocks * PIECE + jnp.arange(row_count, dtype=jnp.int32) % PIECE
    freq_table = 10000.0 ** (-(jnp.arange(half_dim, dtype=F32) * 2.0 / head_size))
    angle_table = positions.astype(F32)[:, None] * freq_table[None, :]
    cosine = jnp.cos(angle_table)
    sine = jnp.sin(angle_table)
    fetched = front(
        n_ctx,
        n_f,
        {
            "q_down": q_down,
            "kv_weight": kv_weight,
            "q_up": q_up,
            "out_proj": out_proj,
            "w_gate": w_gate,
            "w_up": w_up,
            "hidden": hidden_in,
            "info": info,
            "tag": tag,
            "cos": cosine,
            "sin": sine,
        },
        head_size,
    )
    w_out = fetched["w_out"]
    all_kv, q_rot = fetched["all_kv"], fetched["q_rot"]
    normed, q_low, q_normed = fetched["normed"], fetched["q_low"], fetched["q_normed"]
    gain_one, gain_q, gain_two = fetched["gain_one"], fetched["gain_q"], fetched["gain_two"]
    tags = fetched["tags"][:, 0, : 2 * own_pieces].reshape(-1, 2).astype(jnp.int32)
    total_count = jnp.sum(fetched["tags"][:, 1, 0])
    hidden_f = hidden_in.astype(F32)
    scale_q = rms_scale(q_low)

    attn_heads, lse = attn_fwd(tags, own, q_rot, all_kv, head_size, seq_pieces)
    resid = hidden_f + dot(attn_heads, w_out)
    scale_two = rms_scale(resid)
    normed_two = (resid * scale_two * gain_two).astype(BF16)

    wide_valid = jnp.broadcast_to(valid_f[:, None], (row_count, 128))
    ffn = feed_forward(
        n_f,
        {
            "normed": normed_two,
            "resid": resid,
            "teacher": teacher,
            "valid": wide_valid,
            "valid_scale": wide_valid * (token_total / total_count),
            "gain_two": gain_two,
            "w_gate": fetched["gate_full"],
            "w_up": fetched["up_full"],
            "w_down": w_down,
        },
    )
    grad_resid, grad_branch = ffn["grad_resid"], ffn["grad_branch"]
    grad_gain_two = ffn["gain_sum"].reshape(-1)
    sq_local = ffn["sq"][0, 0]
    down_give, down_keep = ctx_split(ffn["down_part"])
    down_got = by_c(down_give, 1)
    gate_give, gate_keep = ctx_split(ffn["gate_part"])
    gate_got = by_c(gate_give, 1)
    up_part = ffn["up_part"]
    branch_group = group_rows(grad_branch)
    grad_attn = dot_t(grad_branch, w_out).astype(BF16)
    out_block = heads_width // (n_ctx * n_f)
    attn_group = lax.all_to_all(
        attn_heads.reshape(row_count, n_ctx, n_f, out_block), "fsdp", 2, 0, tiled=True
    ).reshape(row_count * n_f, n_ctx * out_block)
    grad_attn, attn_group = together(grad_attn, attn_group)
    grad_qlin, grad_seq = attn_bwd(
        tags, own, q_rot, grad_attn, attn_heads, lse, cosine, sine, all_kv, head_size, seq_pieces
    )
    down_got, grad_qlin, grad_seq = together(down_got, grad_qlin, grad_seq)
    qlin_group = lax.all_to_all(grad_qlin, "fsdp", 1, 0, tiled=True)
    down_pair, grad_qlin, grad_seq = together(
        ctx_pair(down_keep, down_got), grad_qlin, grad_seq
    )
    down_parts = ctx_spread(down_pair)
    by_piece = grad_seq.reshape(seq_pieces, PIECE, 2 * head_size)
    piece_tag = tags[:, 0].reshape(n_z, 2, own_pieces)
    piece_own = (tags[:, 1] == seq_ids[0]).reshape(n_z, 2, own_pieces)

    def kv_half(bit):
        places = lax.dynamic_index_in_dim(piece_tag, bit, 1, keepdims=False).reshape(-1)
        picked = by_piece[places]
        if n_ctx * own_pieces != seq_pieces:
            mine = lax.dynamic_index_in_dim(piece_own, bit, 1, keepdims=False).reshape(-1)
            picked = jnp.where(mine[:, None, None], picked, jnp.zeros_like(picked))
        return picked.reshape(n_z, own_pieces * PIECE, 2 * head_size)

    kv_part = jnp.stack([kv_half(0), kv_half(1)], axis=1)
    q_cut, kv_cut = q_width // n_f, 2 * head_size // n_f
    qnorm_group = group_rows(q_normed)
    normed_group = group_rows(normed)

    grad_qnormed = dot_t(grad_qlin, fetched["w_qu"])
    grad_qlow_f, grad_gain_q = rms_back(q_low, scale_q, gain_q, grad_qnormed)
    grad_qlow = grad_qlow_f.astype(BF16)
    da_q = dot_t(grad_qlow, fetched["w_qd"])
    out_part = dot_rows(attn_group, branch_group).astype(BF16)
    qup_part = dot_rows(qnorm_group, qlin_group).astype(BF16)
    down_parts, gate_got, qup_part, out_part = together(down_parts, gate_got, qup_part, out_part)
    gate_pair = ctx_pair(gate_keep, gate_got)

    def by_ctx(grad):
        return grad.reshape(n_z, 2, grad.shape[0] // n_ctx, grad.shape[1])

    order = [(c * n_f + f, f * n_ctx + c) for c in range(n_ctx) for f in range(n_f)]
    down_rows = ctx_total(down_parts).astype(BF16)
    down_sent = lax.ppermute(down_rows, ("ctx", "fsdp"), order)

    small = jnp.concatenate(
        [jnp.zeros((model_width,), F32), grad_gain_q, grad_gain_two, sq_local.reshape(1)]
    )
    entries = small.shape[0]
    small = jnp.pad(small, (0, -entries % 1024)).reshape(-1, 128)
    ends = tail_reduce(
        n_ctx,
        n_f,
        {
            "gate": gate_pair,
            "kv": kv_part,
            "up": by_ctx(up_part),
            "out": by_ctx(out_part),
            "qup": by_ctx(qup_part),
            "dqa": grad_qlow,
            "cos": cosine,
            "sin": sine,
            "normed_group": normed_group,
            "w_kv": fetched["w_kv"],
            "da_q": da_q,
            "hidden": hidden_in,
            "gain_one": gain_one,
            "grad_resid": grad_resid,
            "small": small,
        },
        q_width,
    )
    small, down_sent = together(ends["small_out"], down_sent)
    small = small.reshape(-1)[:entries]
    grad_down = down_sent.astype(F32)

    device = c_idx * n_f + f_idx
    q1, q2 = model_width, model_width + q_width
    n_dev = n_ctx * n_f

    def own_part(values):
        size = values.shape[0] // n_dev
        return cut(values, device * size, size, 0)

    loss_now = small[-1] / (model_width * total_count)
    return (
        ffn["result"],
        loss_now,
        ends["grad_input"],
        own_part(small[:q1]),
        ends["out_qd"],
        own_part(small[q1:q2]),
        ends["out_qup"],
        ends["out_kvw"],
        ends["out_out"],
        own_part(small[q2 : q2 + model_width]),
        ends["out_gate"],
        ends["out_up"],
        grad_down,
    )


def solution(mesh):
    both = ("ctx", "fsdp")
    rows = P(both, None)
    flat = P(both)
    shard = P("fsdp", None)
    gain = P("fsdp")
    return jax.shard_map(
        body,
        mesh=mesh,
        in_specs=(
            rows,
            rows,
            flat,
            flat,
            flat,
            gain,
            shard,
            gain,
            shard,
            shard,
            shard,
            gain,
            shard,
            shard,
            shard,
        ),
        out_specs=(
            rows,
            P(),
            rows,
            flat,
            rows,
            flat,
            rows,
            rows,
            rows,
            flat,
            rows,
            rows,
            rows,
        ),
        check_vma=False,
    )
```

```python
import functools
import math

import jax
import jax.numpy as jnp
from jax import lax
from jax.experimental import pallas as pl
from jax.experimental.pallas import tpu as pltpu
from jax.sharding import PartitionSpec as P

PIECE = 128
SEQ_BLOCKS = 8
NORM_EPS = 1e-05
F32 = jnp.float32
BF16 = jnp.bfloat16
LOG2E = math.log2(math.e)
HEAD_GROUP = 4


def rms_scale(values):
    return lax.rsqrt(jnp.mean(values * values, axis=-1, keepdims=True) + NORM_EPS)


def rms_back(values, scale, gain, grad):
    grad_gain = jnp.sum(grad * values * scale, axis=0)
    ge = gain * grad
    inner = jnp.mean(ge * values, axis=-1, keepdims=True)
    return scale * ge - values * (scale * scale * scale) * inner, grad_gain


def rope_apply(values, cosine, sine):
    half_dim = values.shape[-1] // 2
    one = values[..., :half_dim]
    two = values[..., half_dim:]
    return jnp.concatenate([one * cosine - two * sine, two * cosine + one * sine], axis=-1)


def rope_back(grads, cosine, sine):
    half_dim = grads.shape[-1] // 2
    one = grads[..., :half_dim]
    two = grads[..., half_dim:]
    return jnp.concatenate([one * cosine + two * sine, two * cosine - one * sine], axis=-1)


def together(*values):
    return lax.optimization_barrier(values)


def dot(a, b):
    return jnp.dot(a, b, preferred_element_type=F32)


def dot_t(a, b):
    return lax.dot_general(a, b, (((1,), (1,)), ((), ())), preferred_element_type=F32)


def dot_rows(a, b):
    return lax.dot_general(a, b, (((0,), (0,)), ((), ())), preferred_element_type=F32)


def contract_last(a, b):
    return lax.dot_general(a, b, (((1,), (1,)), ((), ())), preferred_element_type=F32)

def find_pieces(tags_ref, own_ref, pick_ref, total):
    @pl.loop(0, total)
    def _(u):
        @pl.when(tags_ref[u, 1] == own_ref[2])
        def _():
            pick_ref[tags_ref[u, 0]] = u

def stack_heads(ref, hd):
    return jnp.concatenate([ref[:, h*hd:(h+1)*hd] for h in range(HEAD_GROUP)], axis=0)

def attn_fwd_kernel(n_f, tags_ref, own_ref, q_ref, kv_ref, o_ref, lse_ref, *rest):
    k_s, vt_s, acc_s, pick_s = rest[-4:]
    half = pl.program_id(0)
    hd = k_s.shape[1]
    pieces = k_s.shape[0] // PIECE
    total = kv_ref.shape[0] // PIECE
    wide = 2 * PIECE
    coef = hd ** -0.5 * LOG2E

    @pl.when((half == 0) & (pl.program_id(1) == 0))
    def _():
        find_pieces(tags_ref, own_ref, pick_s, total)
        for i in range(pieces):
            rows = pl.ds(pl.multiple_of(pick_s[i] * PIECE, PIECE), PIECE)
            k_s[i*PIECE:(i+1)*PIECE, :] = kv_ref[rows, :hd]
            vt_s[:, i*PIECE:(i+1)*PIECE] = kv_ref[rows, hd:].T

    q = stack_heads(q_ref, hd)
    acc_s[...] = jnp.zeros_like(acc_s)
    rows = q.shape[0]
    def step(i, carry):
        peak, total_p = carry
        at = pl.ds(pl.multiple_of(i * wide, wide), wide)
        raw = contract_last(k_s[at, :], q)
        top = jnp.maximum(peak, jnp.max(raw, axis=0, keepdims=True))
        fade = jnp.exp2((peak - top) * coef)
        p = jnp.exp2((raw - top) * coef)
        acc_s[...] = acc_s[...] * fade + jnp.dot(vt_s[:, at], p.astype(BF16), preferred_element_type=F32)
        return top, total_p * fade + jnp.sum(p, axis=0, keepdims=True)
    count = own_ref[half] // 2 + 1
    peak, total_p = lax.fori_loop(0, count, step, (jnp.full((1, rows), -1e30, F32), jnp.zeros((1, rows), F32)))
    out = (acc_s[...] / total_p).astype(BF16).T
    for h in range(HEAD_GROUP):
        o_ref[:, h*hd:(h+1)*hd] = out[h*PIECE:(h+1)*PIECE, :]
    if len(rest) > 4:
        for b in range(HEAD_GROUP * hd // 128):
            head, part = b * 128 // hd, b * 128 % hd
            rest[0][b % n_f, :, b // n_f * 128:(b // n_f + 1) * 128] = out[
                head*PIECE:(head+1)*PIECE, part:part+128
            ]
    lse_ref[0] = peak * coef + jnp.log2(total_p)

def attn_fwd(tags, own, q, kv, hd, pieces, n_f, cut):
    n_rows, width = q.shape
    groups = width // hd // HEAD_GROUP
    gw = HEAD_GROUP * hd
    halves = n_rows // PIECE
    rows = HEAD_GROUP * PIECE
    blk = pl.BlockSpec((PIECE, gw), lambda p, g, *_: (p, g))
    flops = 4 * n_rows * width * pieces * PIECE * 9 // 16
    shapes = [jax.ShapeDtypeStruct(q.shape, BF16), jax.ShapeDtypeStruct((halves*groups, 1, rows), F32)]
    specs = [blk, pl.BlockSpec((1, 1, rows), lambda p, g, *_: (p*groups+g, 0, 0))]
    if cut:
        shapes.append(jax.ShapeDtypeStruct((n_f, n_rows, width // n_f), BF16))
        specs.append(pl.BlockSpec((n_f, PIECE, gw // n_f), lambda p, g, *_: (0, p, g)))
    return pl.pallas_call(
        functools.partial(attn_fwd_kernel, n_f),
        out_shape=tuple(shapes),
        grid_spec=pltpu.PrefetchScalarGridSpec(
            num_scalar_prefetch=2, grid=(halves, groups),
            in_specs=[blk, pl.BlockSpec(kv.shape, lambda p, g, *_: (0, 0))],
            out_specs=tuple(specs),
            scratch_shapes=[pltpu.VMEM((pieces*PIECE, hd), BF16), pltpu.VMEM((hd, pieces*PIECE), BF16),
                            pltpu.VMEM((hd, rows), F32), pltpu.SMEM((pieces,), jnp.int32)]),
        compiler_params=pltpu.CompilerParams(vmem_limit_bytes=40 << 20),
        cost_estimate=pl.CostEstimate(flops=flops, transcendentals=flops//(4*hd), bytes_accessed=2*(2*q.size+kv.size)),
        name="attn_fwd",
    )(tags, own, q, kv)

def attn_bwd_kernel(tags_ref, own_ref, q_ref, do_ref, o_ref, lse_ref, cos_ref, sin_ref, kv_ref, dq_ref, dkv_ref,
                    k_s, kt_s, v_s, dq_s, dk_s, dv_s, pick_s):
    half = pl.program_id(0)
    group = pl.program_id(1)
    hd = k_s.shape[1]
    pieces = k_s.shape[0] // PIECE
    total = kv_ref.shape[0] // PIECE
    wide = 2 * PIECE
    coef = hd ** -0.5 * LOG2E
    scale = hd ** -0.5

    @pl.when((half == 0) & (group == 0))
    def _():
        find_pieces(tags_ref, own_ref, pick_s, total)
        for i in range(pieces):
            rows = pl.ds(pl.multiple_of(pick_s[i] * PIECE, PIECE), PIECE)
            keys = kv_ref[rows, :hd]
            k_s[i*PIECE:(i+1)*PIECE, :] = keys
            kt_s[:, i*PIECE:(i+1)*PIECE] = keys.T
            v_s[i*PIECE:(i+1)*PIECE, :] = kv_ref[rows, hd:]
        dk_s[...] = jnp.zeros_like(dk_s)
        dv_s[...] = jnp.zeros_like(dv_s)

    q = stack_heads(q_ref, hd)
    do = stack_heads(do_ref, hd)
    prod = do.astype(F32) * stack_heads(o_ref, hd).astype(F32)
    delta = lax.dot_general(jnp.ones((8, hd), F32), prod, (((1,), (1,)), ((), ())),
                            preferred_element_type=F32, precision=lax.Precision.HIGHEST)[:1]
    lse = lse_ref[0]
    dq_s[...] = jnp.zeros_like(dq_s)
    def step(i, carry):
        at = pl.ds(pl.multiple_of(i * wide, wide), wide)
        p = jnp.exp2(contract_last(k_s[at, :], q) * coef - lse)
        dp = contract_last(v_s[at, :], do)
        ds = (p * (dp - delta)).astype(BF16)
        dv_s[at, :] += jnp.dot(p.astype(BF16), do, preferred_element_type=F32)
        dk_s[at, :] += jnp.dot(ds, q, preferred_element_type=F32)
        dq_s[...] += jnp.dot(kt_s[:, at], ds, preferred_element_type=F32)
        return carry
    lax.fori_loop(0, own_ref[half] // 2 + 1, step, 0)
    dq = (dq_s[...] * scale).T
    cos, sin = cos_ref[...], sin_ref[...]
    mid = hd // 2
    for h in range(HEAD_GROUP):
        one = dq[h*PIECE:(h+1)*PIECE, :mid]
        two = dq[h*PIECE:(h+1)*PIECE, mid:]
        dq_ref[:, h*hd:h*hd+mid] = (one * cos + two * sin).astype(BF16)
        dq_ref[:, h*hd+mid:(h+1)*hd] = (two * cos - one * sin).astype(BF16)

    @pl.when((half == pl.num_programs(0) - 1) & (group == pl.num_programs(1) - 1))
    def _():
        dkv_ref[:, :hd] = (dk_s[...] * scale).astype(BF16)
        dkv_ref[:, hd:] = dv_s[...].astype(BF16)

def attn_bwd(tags, own, q, do, o, lse, cos, sin, kv, hd, pieces):
    n_rows, width = q.shape
    groups = width // hd // HEAD_GROUP
    gw = HEAD_GROUP * hd
    halves = n_rows // PIECE
    rows = HEAD_GROUP * PIECE
    blk = pl.BlockSpec((PIECE, gw), lambda p, g, *_: (p, g))
    trig = pl.BlockSpec((PIECE, hd // 2), lambda p, g, *_: (p, 0))
    keys = pieces * PIECE
    flops = 10 * n_rows * width * keys * 9 // 16
    return pl.pallas_call(
        attn_bwd_kernel,
        out_shape=(jax.ShapeDtypeStruct(q.shape, BF16), jax.ShapeDtypeStruct((keys, 2*hd), BF16)),
        grid_spec=pltpu.PrefetchScalarGridSpec(
            num_scalar_prefetch=2, grid=(halves, groups),
            in_specs=[blk, blk, blk, pl.BlockSpec((1, 1, rows), lambda p, g, *_: (p*groups+g, 0, 0)), trig, trig,
                      pl.BlockSpec(kv.shape, lambda p, g, *_: (0, 0))],
            out_specs=[blk, pl.BlockSpec((keys, 2*hd), lambda p, g, *_: (0, 0))],
            scratch_shapes=[pltpu.VMEM((keys, hd), BF16), pltpu.VMEM((hd, keys), BF16), pltpu.VMEM((keys, hd), BF16),
                            pltpu.VMEM((hd, rows), F32), pltpu.VMEM((keys, hd), F32), pltpu.VMEM((keys, hd), F32),
                            pltpu.SMEM((pieces,), jnp.int32)]),
        compiler_params=pltpu.CompilerParams(vmem_limit_bytes=48 << 20),
        cost_estimate=pl.CostEstimate(flops=flops, transcendentals=flops//(10*hd), bytes_accessed=2*(4*q.size+2*kv.size)),
        name="attn_bwd",
    )(tags, own, q, do, o, lse, cos, sin, kv)

MESH = pl.DeviceIdType.MESH


def flip(index, mask):
    out = 0
    bit = 1
    while bit <= mask:
        part = (index // bit) % 2
        out = out + bit * ((1 - part) if mask & bit else part)
        bit *= 2
    return out + (index // bit) * bit


def row_loop(rows, body, step=32):
    if rows % step:
        step = 16

    @pl.loop(0, rows // step)
    def _(i):
        body(pl.ds(pl.multiple_of(i * step, step), step))


class Sender:
    def __init__(self):
        self.open = []

    def make(self, src, dst, send_sem, recv_sem, peer):
        return pltpu.make_async_remote_copy(
            src_ref=src,
            dst_ref=dst,
            send_sem=send_sem,
            recv_sem=recv_sem,
            device_id=peer,
            device_id_type=MESH,
        )

    def __call__(self, *args):
        copy = self.make(*args)
        copy.start()
        self.open.append(copy)
        return copy

    def finish(self):
        for copy in self.open:
            copy.wait_send()


class LineSum:
    def __init__(self, own, got, send_sem, recv_sem, c_idx, f_idx, n_z, sender):
        self.own, self.got, self.send_sem, self.recv_sem = own, got, send_sem, recv_sem
        self.n_z, self.sender = n_z, sender
        self.z = c_idx // 2
        self.left = (c_idx - 2, f_idx)
        self.right = (c_idx + 2, f_idx)

    def copy(self, b, slot, peer):
        return self.sender.make(
            self.own.at[b], self.got.at[slot], self.send_sem.at[b], self.recv_sem.at[slot], peer
        )

    def take(self, b, slot):
        self.copy(b, slot, self.left).wait_recv()

        def add(at):
            self.own[b, at, :] = (
                self.own[b, at, :].astype(F32) + self.got[slot, at, :].astype(F32)
            ).astype(BF16)

        row_loop(self.own.shape[1], add)

    def go_right(self, b):
        z = self.z

        @pl.when(z < b)
        def _():
            @pl.when(z > 0)
            def _():
                self.take(b, b)

            self.copy(b, b, self.right).start()

    def go_left(self, b):
        z, n_z = self.z, self.n_z

        @pl.when(z > b)
        def _():
            @pl.when(z < n_z - 1)
            def _():
                self.take(b, b)

            @pl.when(z - 1 > b)
            def _():
                self.copy(b, b, self.left).start()

            @pl.when(z - 1 == b)
            def _():
                self.copy(b, n_z, self.left).start()

    def step(self, i):
        @pl.when(2 * self.z < self.n_z)
        def _():
            self.go_right(self.n_z - 1 - i)
            self.go_left(i)

        @pl.when(2 * self.z >= self.n_z)
        def _():
            self.go_left(i)
            self.go_right(self.n_z - 1 - i)

    def total(self, store):
        z, n_z = self.z, self.n_z

        @pl.when(z > 0)
        def _():
            self.copy(z, z, self.left).wait_recv()

        @pl.when(z < n_z - 1)
        def _():
            self.copy(z, n_z, self.left).wait_recv()

        rows = self.own.shape[1]

        @pl.when(z == 0)
        def _():
            row_loop(
                rows,
                lambda at: store(
                    at, self.own[z, at, :].astype(F32) + self.got[n_z, at, :].astype(F32)
                ),
            )

        @pl.when(z == n_z - 1)
        def _():
            row_loop(
                rows,
                lambda at: store(
                    at, self.own[z, at, :].astype(F32) + self.got[z, at, :].astype(F32)
                ),
            )

        @pl.when((z > 0) & (z < n_z - 1))
        def _():
            row_loop(
                rows,
                lambda at: store(
                    at,
                    self.own[z, at, :].astype(F32)
                    + self.got[z, at, :].astype(F32)
                    + self.got[n_z, at, :].astype(F32),
                ),
            )

    def finish(self):
        for b in range(self.n_z):

            @pl.when(self.z != b)
            def _(b=b):
                self.copy(b, b, self.left).wait_send()


WINDOW = 3
TAIL_NAMES = ("gate", "kv", "up", "out", "qup", "qd", "kvw")
TAIL_CUT = ("gate", "up", "qup", "qd", "kvw")
TAIL_SENT = ("kv", "up", "out", "qup", "qd", "kvw")


def tail_kernel(n_ctx, n_f, names_in, names_out, names_scratch, *refs):
    n_z = n_ctx // 2
    names = list(names_in) + list(names_out) + list(names_scratch)
    r = dict(zip(names, refs, strict=True))
    c_idx = lax.axis_index("ctx")
    f_idx = lax.axis_index("fsdp")
    y_idx = c_idx % 2
    z_idx = c_idx // 2
    send = Sender()

    def over_c(mask):
        return (flip(c_idx, mask), f_idx)

    def over_f(mask):
        return (c_idx, flip(f_idx, mask))

    barrier = pltpu.get_barrier_semaphore()
    for mask in range(1, n_f):
        pl.semaphore_signal(barrier, inc=1, device_id=over_f(mask), device_id_type=MESH)
    for mask in range(1, n_ctx):
        pl.semaphore_signal(barrier, inc=1, device_id=over_c(mask), device_id_type=MESH)
    pl.semaphore_wait(barrier, n_f - 1 + n_ctx - 1)

    lines = {
        m: LineSum(
            r["pair_" + m],
            r["z_" + m],
            r["z_send"].at[i],
            r["z_recv"].at[i],
            c_idx,
            f_idx,
            n_z,
            send,
        )
        for i, m in enumerate(TAIL_NAMES)
    }
    order = list(range(1, n_z)) + [0]
    y_copies, keeps = {}, {}

    parts = {m: r[m] for m in ("kv", "up", "out", "qup")}
    parts["qd"], parts["kvw"] = r["part_qd"], r["part_kvw"]
    queue = [(m, s) for m in TAIL_SENT for s in order]

    def next_y():
        if queue:
            m, s = queue.pop(0)
            i = TAIL_SENT.index(m)
            b = flip(z_idx, s)
            y_copies[m, s] = send(
                parts[m].at[b, 1 - y_idx],
                r["y_" + m].at[s],
                r["y_send"].at[i, s],
                r["y_recv"].at[i, s],
                over_c(1),
            )
            keep = pltpu.make_async_copy(
                parts[m].at[b, y_idx], r["pair_" + m].at[b], r["keep_sem"].at[i, s]
            )
            keep.start()
            keeps[m, s] = keep

    def add_pair(m, s):
        b = flip(z_idx, s)
        y_copies[m, s].wait_recv()
        next_y()
        keeps[m, s].wait()
        pair, got = r["pair_" + m], r["y_" + m]

        def add(at):
            pair[b, at, :] = (pair[b, at, :].astype(F32) + got[s, at, :].astype(F32)).astype(BF16)

        row_loop(pair.shape[1], add)

    def advance(pair, line):
        for i, s in enumerate(order):
            if pair is not None:
                add_pair(pair, s)
            if line is not None and i < n_z - 1:
                lines[line].step(i)

    f_copies = {}

    def finish_sum(m):
        lines[m].total(lambda at, value: store_total(m, at, value))
        if m in TAIL_CUT:
            i = TAIL_CUT.index(m)
            part = r["tot_" + m].shape[0] // n_f
            for s in range(1, n_f):
                at = pl.ds(pl.multiple_of(flip(f_idx, s) * part, part), part)
                f_copies[m, s] = send(
                    r["tot_" + m].at[at, :],
                    r["f_" + m].at[s - 1],
                    r["f_send"].at[i, s - 1],
                    r["f_recv"].at[i, s - 1],
                    over_f(s),
                )

    def store_total(m, at, value):
        if m in TAIL_CUT:
            r["tot_" + m][at, :] = value.astype(BF16)
        else:
            r["out_" + m][at, :] = value

    def put_out(m):
        total, out = r["tot_" + m], r["out_" + m]
        rows, width = total.shape
        part = rows // n_f
        for s in range(n_f):
            at = pl.ds(pl.multiple_of(flip(f_idx, s) * width, 128), width)
            if s:
                f_copies[m, s].wait_recv()
                out[:, at] = r["f_" + m][s - 1].astype(F32)
            else:
                mine = pl.ds(pl.multiple_of(f_idx * part, part), part)
                out[:, at] = total[mine, :].astype(F32)

    def cut_low(src, dst, width, index):
        rows = src.shape[0]
        mine = pl.ds(pl.multiple_of(f_idx * rows, rows), rows)
        copies = []
        for s in range(1, n_f):
            at = pl.ds(pl.multiple_of(flip(f_idx, s) * width, 128), width)
            copies.append(
                send(
                    src.at[:, at],
                    dst.at[mine, :],
                    r["low_send"].at[index, s - 1],
                    r["low_recv"].at[index, s - 1],
                    over_f(s),
                )
            )
        own = pl.ds(pl.multiple_of(f_idx * width, 128), width)
        dst[mine, :] = src[:, own]
        return copies

    for _ in range(WINDOW):
        next_y()
    q_copies = cut_low(r["dqa"], r["qd_group"], r["qd_group"].shape[1], 0)
    pair_in = pltpu.make_async_copy(r["gate"], r["pair_gate"], r["keep_sem"].at[0, n_z])
    pair_in.start()
    pair_in.wait()
    advance("kv", "gate")
    advance("up", "kv")
    finish_sum("gate")

    head = r["dkv"].shape[1] // 2
    mid = head // 2

    def store_kv(at, value):
        cos, sin = r["cos"][at, :], r["sin"][at, :]
        one, two = value[:, :mid], value[:, mid:head]
        r["dkv"][at, :mid] = (one * cos + two * sin).astype(BF16)
        r["dkv"][at, mid:head] = (two * cos - one * sin).astype(BF16)
        r["dkv"][at, head:] = value[:, head:].astype(BF16)

    lines["kv"].total(store_kv)
    kv_copies = cut_low(r["dkv"], r["kv_group"], r["kv_group"].shape[1], 1)

    def low_part(group, part):
        normed = r["normed_group"]
        rows = part.shape[2]
        for c in range(n_ctx):
            part[c // 2, c % 2] = lax.dot_general(
                normed[:, c * rows : (c + 1) * rows],
                group[...],
                (((0,), (0,)), ((), ())),
                preferred_element_type=F32,
            ).astype(BF16)

    for copy in q_copies:
        copy.wait_recv()
    low_part(r["qd_group"], r["part_qd"])
    advance("out", "up")
    for copy in kv_copies:
        copy.wait_recv()
    low_part(r["kv_group"], r["part_kvw"])

    grad_in, w_kv = r["grad_input"], r["w_kv"]
    width = grad_in.shape[1]
    tile = 256

    @pl.loop(0, width // tile)
    def _(t):
        at = pl.ds(pl.multiple_of(t * tile, tile), tile)
        grad_in[:, at] = r["da_q"][:, at] + lax.dot_general(
            r["dkv"][...],
            w_kv[at, :],
            (((1,), (1,)), ((), ())),
            preferred_element_type=F32,
        )

    r["gain_sum"][...] = jnp.zeros_like(r["gain_sum"])
    gain = r["gain_one"][...]

    def norm_rows(at):
        value = r["hidden"][at, :].astype(F32)
        grad = grad_in[at, :]
        scale = lax.rsqrt(jnp.mean(value * value, axis=-1, keepdims=True) + NORM_EPS)
        r["gain_sum"][...] += jnp.sum(grad * value * scale, axis=0, keepdims=True)
        ge = gain * grad
        inner = jnp.mean(ge * value, axis=-1, keepdims=True)
        grad_in[at, :] = (
            r["grad_resid"][at, :] + scale * ge - value * (scale * scale * scale) * inner
        )

    row_loop(grad_in.shape[0], norm_rows, step=16)

    small, small_got = r["small_out"], r["small_got"]
    small[...] = r["small"][...]
    for i in range(width // 128):
        small[i : i + 1, :] = r["gain_sum"][:, i * 128 : (i + 1) * 128]
    steps = [over_f(1), over_f(2), over_c(1)]
    mask = 2
    while mask < n_ctx:
        steps.append(over_c(mask))
        mask *= 2
    small_copies = {}

    def small_start(s):
        small_got[s, 0] = small[...]
        small_copies[s] = send(
            small_got.at[s, 0],
            small_got.at[s, 1],
            r["s_send"].at[s],
            r["s_recv"].at[s],
            steps[s],
        )

    def small_end(s):
        small_copies[s].wait_recv()
        small[...] = small[...] + small_got[s, 1]

    for s in range(2):
        small_start(s)
        small_end(s)
    small_start(2)

    put_out("gate")
    advance("qup", "out")
    finish_sum("up")
    advance("qd", "qup")
    finish_sum("out")
    small_end(2)
    small_start(3)
    advance("kvw", "qd")
    put_out("up")
    finish_sum("qup")
    advance(None, "kvw")
    for s in range(3, len(steps)):
        if s > 3:
            small_start(s)
        small_end(s)
    finish_sum("qd")
    finish_sum("kvw")
    for m in ("qup", "qd", "kvw"):
        put_out(m)
    send.finish()
    for m in TAIL_NAMES:
        lines[m].finish()


def tail_reduce(n_ctx, n_f, inputs, q_width):
    n_z = n_ctx // 2
    vmem = pl.BlockSpec(memory_space=pltpu.VMEM)
    anywhere = pl.BlockSpec(memory_space=pl.ANY)
    rows, width = inputs["hidden"].shape
    kv_width = inputs["w_kv"].shape[1]
    in_hbm = ("gate", "kv", "up", "out", "qup")
    names_in = tuple(inputs)
    in_specs = [anywhere if m in in_hbm else vmem for m in names_in]
    block = {m: inputs[m].shape[-2:] for m in in_hbm}
    block["qd"] = (width // n_ctx, q_width // n_f)
    block["kvw"] = (width // n_ctx, kv_width // n_f)
    outs = {
        "small_out": jax.ShapeDtypeStruct(inputs["small"].shape, F32),
        "grad_input": jax.ShapeDtypeStruct((rows, width), F32),
    }
    scratch = {}
    for m in TAIL_NAMES:
        high, wide = block[m]
        scratch["pair_" + m] = pltpu.VMEM((n_z, high, wide), BF16)
        scratch["z_" + m] = pltpu.VMEM((n_z + 1, high, wide), BF16)
        if m in TAIL_SENT:
            scratch["y_" + m] = pltpu.VMEM((n_z, high, wide), BF16)
        if m in TAIL_CUT:
            scratch["tot_" + m] = pltpu.VMEM((high, wide), BF16)
            scratch["f_" + m] = pltpu.VMEM((n_f - 1, high // n_f, wide), BF16)
            outs["out_" + m] = jax.ShapeDtypeStruct((high // n_f, wide * n_f), F32)
        elif m != "kv":
            outs["out_" + m] = jax.ShapeDtypeStruct((high, wide), F32)
    scratch["dkv"] = pltpu.VMEM((rows, kv_width), BF16)
    scratch["qd_group"] = pltpu.VMEM((rows * n_f, q_width // n_f), BF16)
    scratch["kv_group"] = pltpu.VMEM((rows * n_f, kv_width // n_f), BF16)
    scratch["part_qd"] = pltpu.VMEM((n_z, 2) + block["qd"], BF16)
    scratch["part_kvw"] = pltpu.VMEM((n_z, 2) + block["kvw"], BF16)
    scratch["gain_sum"] = pltpu.VMEM((1, width), F32)
    steps = 2 + (n_ctx.bit_length() - 1)
    scratch["small_got"] = pltpu.VMEM((steps, 2) + inputs["small"].shape, F32)
    dma = pltpu.SemaphoreType.DMA
    sent, cut = len(TAIL_SENT), len(TAIL_CUT)
    scratch["s_send"] = dma((steps,))
    scratch["s_recv"] = dma((steps,))
    scratch["y_send"] = dma((sent, n_z))
    scratch["y_recv"] = dma((sent, n_z))
    scratch["keep_sem"] = dma((sent, n_z + 1))
    scratch["z_send"] = dma((len(TAIL_NAMES), n_z))
    scratch["z_recv"] = dma((len(TAIL_NAMES), n_z + 1))
    scratch["f_send"] = dma((cut, n_f - 1))
    scratch["f_recv"] = dma((cut, n_f - 1))
    scratch["low_send"] = dma((2, n_f - 1))
    scratch["low_recv"] = dma((2, n_f - 1))
    values = pl.pallas_call(
        functools.partial(tail_kernel, n_ctx, n_f, names_in, tuple(outs), tuple(scratch)),
        out_shape=tuple(outs.values()),
        in_specs=in_specs,
        out_specs=tuple([vmem] * len(outs)),
        scratch_shapes=list(scratch.values()),
        compiler_params=pltpu.CompilerParams(
            collective_id=0, has_side_effects=True, vmem_limit_bytes=60 << 20
        ),
        name="tail_reduce",
    )(*inputs.values())
    return dict(zip(outs, values, strict=True))


def front_kernel(n_ctx, n_f, names, *refs):
    r = dict(zip(names, refs, strict=True))
    n_z = n_ctx // 2
    c_idx = lax.axis_index("ctx")
    f_idx = lax.axis_index("fsdp")
    y_idx = c_idx % 2
    z_bit = (c_idx // 2) % 2
    x_idx = f_idx // 2
    k_idx = f_idx % 2
    far_idx = flip(f_idx, 2)
    moves = Sender()
    local = []
    at_sem = [0]

    def over_c(mask):
        return (flip(c_idx, mask), f_idx)

    def over_f(mask):
        return (c_idx, flip(f_idx, mask))

    def send(src, dst, peer):
        i = at_sem[0]
        at_sem[0] += 1
        return moves(src, dst, r["send_sem"].at[i], r["recv_sem"].at[i], peer)

    def keep(src, dst):
        copy = pltpu.make_async_copy(src, dst, r["local_sem"].at[len(local)])
        copy.start()
        local.append(copy)
        return copy

    def rows(start, size):
        return pl.ds(pl.multiple_of(start, size), size)

    barrier = pltpu.get_barrier_semaphore()
    for mask in range(1, n_f):
        pl.semaphore_signal(barrier, inc=1, device_id=over_f(mask), device_id_type=MESH)
    for mask in range(1, n_ctx):
        pl.semaphore_signal(barrier, inc=1, device_id=over_c(mask), device_id_type=MESH)
    pl.semaphore_wait(barrier, n_f - 1 + n_ctx - 1)

    infos, tags = r["infos"], r["tags"]
    infos[f_idx] = r["info"][...]
    info_copies = [
        send(infos.at[f_idx], infos.at[f_idx], over_f(mask)) for mask in range(1, n_f)
    ]

    class Rows:
        def __init__(self, shard, dest, bit, hop, chunks):
            self.dest, self.bit, self.hop = dest, bit, hop
            self.shard = shard
            self.size = shard.shape[0]
            self.half = self.size // 2
            self.step = self.half // chunks
            self.chunks = chunks
            self.far, self.next, self.cross = [], [], []

        def start(self, spare=None):
            mine = self.dest.at[rows(f_idx * self.size, self.size)]
            if spare is None:
                self.kept = keep(self.shard, mine)
            else:
                self.spare, self.kept = spare, keep(self.shard, spare)
            self.cross.append(send(self.shard, mine, over_f(1)))

        def settle(self):
            self.kept.wait()
            keep(self.spare, self.dest.at[rows(f_idx * self.size, self.size)])

        def reach(self, i):
            part = self.bit * self.half + i * self.step
            self.far.append(
                send(
                    self.shard.at[rows(part, self.step)],
                    self.dest.at[rows(f_idx * self.size + part, self.step)],
                    over_f(2),
                )
            )

        def place(self, bit, i):
            return self.dest.at[rows(far_idx * self.size + bit * self.half + i * self.step, self.step)]

        def hop_on(self, i):
            self.far[i].wait_recv()
            reach_next()
            here = self.place(self.bit, i)
            self.next.append(send(here, here, over_c(self.hop)))
            self.cross.append(send(here, here, over_f(1)))

        def pass_on(self, i):
            self.next[i].wait_recv()
            here = self.place(1 - self.bit, i)
            self.cross.append(send(here, here, over_f(1)))

        def end(self):
            for copy in self.cross:
                copy.wait_recv()

    class Columns:
        def __init__(self, shard, dest, box, bits, hops):
            self.shard, self.dest, self.box = shard, dest, box
            self.bits, self.hops = bits, hops
            self.size = shard.shape[0]
            self.width = dest.shape[1]
            self.quarter = self.size // 4

        def columns(self, start, count=1):
            return pl.ds(pl.multiple_of(start * self.width, 128), count * self.width)

        def start(self, spare):
            mine = self.dest.at[rows(f_idx * self.size, self.size)]
            self.spare, self.kept = spare, keep(self.shard.at[:, self.columns(f_idx)], spare)
            self.cross = [send(self.shard.at[:, self.columns(flip(f_idx, 1))], mine, over_f(1))]

        def settle(self):
            self.kept.wait()
            keep(self.spare, self.dest.at[rows(f_idx * self.size, self.size)])

        def reach(self, i):
            one, two = self.bits
            at = rows((two * 2 + one) * self.quarter, self.quarter)
            self.far = send(
                self.shard.at[at, self.columns((1 - x_idx) * 2, 2)], self.box.at[at], over_f(2)
            )

        def piece(self, one, two):
            return self.box.at[rows((two * 2 + one) * self.quarter, self.quarter)]

        def first(self):
            one, two = self.bits
            self.far.wait_recv()
            reach_next()
            here = self.piece(one, two)
            self.step = send(here, here, over_c(self.hops[0]))
            self.last = [send(here, here, over_c(self.hops[1]))]

        def second(self):
            one, two = self.bits
            self.step.wait_recv()
            here = self.piece(1 - one, two)
            self.last.append(send(here, here, over_c(self.hops[1])))

        def part(self):
            for copy in self.last:
                copy.wait_recv()
            there = self.dest.at[rows(far_idx * self.size, self.size)]
            self.cross.append(send(self.box.at[:, self.columns(1 - k_idx)], there, over_f(1)))
            keep(self.box.at[:, self.columns(k_idx)], there)

        def end(self):
            for copy in self.cross:
                copy.wait_recv()

    kv = Rows(r["kv_weight"], r["kv_full"], y_idx, 1, 1)
    qd = Rows(r["q_down"], r["qd_full"], y_idx, 1, 1)
    qu = Rows(r["q_up"], r["qu_full"], y_idx, 1, 2)
    out = Rows(r["out_proj"], r["w_out"], z_bit, 2, 4)
    gate = Columns(r["w_gate"], r["gate_full"], r["gate_box"], (y_idx, z_bit), (1, 2))
    up = Columns(r["w_up"], r["up_full"], r["up_box"], (z_bit, y_idx), (2, 1))
    queue = [(kv, 0), (qd, 0), (qu, 0), (qu, 1), (gate, 0), (up, 0)]
    queue += [(out, i) for i in range(out.chunks)]

    def reach_next():
        if queue:
            part, i = queue.pop(0)
            part.reach(i)

    reach_next()
    reach_next()
    kv.start()
    qd.start()

    for copy in info_copies:
        copy.wait_recv()
    d1 = r["gain_one"].shape[1] // n_f // 128
    d2 = r["gain_q"].shape[1] // n_f // 128
    count = infos[0, 2 * d1 + d2 : 2 * d1 + d2 + 1, :]
    for f in range(n_f):
        for i in range(d1):
            col = slice((f * d1 + i) * 128, (f * d1 + i + 1) * 128)
            r["gain_one"][:, col] = infos[f, i : i + 1, :]
            r["gain_two"][:, col] = infos[f, d1 + d2 + i : d1 + d2 + i + 1, :]
        for i in range(d2):
            col = slice((f * d2 + i) * 128, (f * d2 + i + 1) * 128)
            r["gain_q"][:, col] = infos[f, d1 + i : d1 + i + 1, :]
        if f:
            count = count + infos[f, 2 * d1 + d2 : 2 * d1 + d2 + 1, :]
    tags[c_idx] = r["tag"][...]
    tags[c_idx, 1:2, :] = count
    tag_copies = [send(tags.at[c_idx], tags.at[c_idx], over_c(mask)) for mask in range(1, n_ctx)]

    normed = r["normed"]
    gain_one = r["gain_one"][...]

    def norm_rows(at):
        value = r["hidden"][at, :].astype(F32)
        scale = lax.rsqrt(jnp.mean(value * value, axis=-1, keepdims=True) + NORM_EPS)
        normed[at, :] = (value * scale * gain_one).astype(BF16)

    row_loop(normed.shape[0], norm_rows, step=16)

    kv.hop_on(0)
    qd.hop_on(0)
    qu.start()
    kv.pass_on(0)
    qd.pass_on(0)
    kv.end()
    kv.kept.wait()
    head = r["kv_full"].shape[1] // 2
    mid = head // 2
    cos, sin = r["cos"], r["sin"]
    kv_rows = r["kv_rows"]
    keys = jnp.dot(normed[...], r["kv_full"][:, :head], preferred_element_type=F32)
    one, two = keys[:, :mid], keys[:, mid:]
    kv_rows[:, :mid] = (one * cos[...] - two * sin[...]).astype(BF16)
    kv_rows[:, mid:head] = (two * cos[...] + one * sin[...]).astype(BF16)
    kv_rows[:, head:] = jnp.dot(
        normed[...], r["kv_full"][:, head:], preferred_element_type=F32
    ).astype(BF16)
    all_kv = r["all_kv"]
    tokens = normed.shape[0]

    def kv_place(c):
        return all_kv.at[rows(c * tokens, tokens)]

    kv_z = [send(kv_rows, kv_place(c_idx), over_c(2 * s)) for s in range(1, n_z)]
    kv_y = [send(kv_rows, kv_place(c_idx), over_c(1))]
    keep(kv_rows, kv_place(c_idx))
    qu.hop_on(0)
    qd.end()
    qd.kept.wait()

    @pl.loop(0, r["q_low"].shape[1] // 256)
    def _(t):
        at = pl.ds(pl.multiple_of(t * 256, 256), 256)
        r["q_low"][:, at] = jnp.dot(
            normed[...], r["qd_full"][:, at], preferred_element_type=F32
        )

    gain_q = r["gain_q"][...]

    def norm_low(at):
        value = r["q_low"][at, :]
        scale = lax.rsqrt(jnp.mean(value * value, axis=-1, keepdims=True) + NORM_EPS)
        r["q_normed"][at, :] = (value * scale * gain_q).astype(BF16)

    row_loop(tokens, norm_low, step=16)
    qu.hop_on(1)
    for s in range(1, n_z):
        kv_z[s - 1].wait_recv()
        here = kv_place(flip(c_idx, 2 * s))
        kv_y.append(send(here, here, over_c(1)))
    qu.pass_on(0)
    qu.pass_on(1)
    gate.first()
    qu.end()
    for m, part in (("gate", gate), ("up", up), ("out", out)):
        part.start(r[m + "_spare"])
    qu.kept.wait()

    @pl.loop(0, r["q_rot"].shape[1] // head)
    def _(h):
        start = pl.multiple_of(h * head, head)
        value = jnp.dot(
            r["q_normed"][...],
            r["qu_full"][:, pl.ds(start, head)],
            preferred_element_type=F32,
        )
        one, two = value[:, :mid], value[:, mid:]
        r["q_rot"][:, pl.ds(start, mid)] = (one * cos[...] - two * sin[...]).astype(BF16)
        late = pl.multiple_of(h * head + mid, mid)
        r["q_rot"][:, pl.ds(late, mid)] = (two * cos[...] + one * sin[...]).astype(BF16)

    up.first()
    for part in (gate, up, out):
        part.settle()
    for m in ("kv", "qd", "qu"):
        keep(r[m + "_full"], r["w_" + m])
    gate.second()
    out.hop_on(0)
    up.second()
    for i in range(1, out.chunks):
        out.hop_on(i)
    gate.part()
    for i in range(out.chunks):
        out.pass_on(i)
    up.part()
    for copy in kv_y + tag_copies:
        copy.wait_recv()
    for part in (gate, up, out):
        part.end()
    for copy in local:
        if not any(copy is part.kept for part in (kv, qd, qu, gate, up, out)):
            copy.wait()
    moves.finish()


def front(n_ctx, n_f, inputs, head_size):
    tokens, width = inputs["hidden"].shape
    shape = jax.ShapeDtypeStruct
    q_width = inputs["q_down"].shape[1]
    heads_width = inputs["q_up"].shape[1]
    part = inputs["w_gate"].shape[1] // n_f

    def whole(m):
        return (inputs[m].shape[0] * n_f, inputs[m].shape[1])

    in_hbm = ("q_down", "kv_weight", "q_up", "out_proj", "w_gate", "w_up")
    outs = {
        "w_qd": shape(whole("q_down"), BF16),
        "w_kv": shape(whole("kv_weight"), BF16),
        "w_qu": shape(whole("q_up"), BF16),
        "w_out": shape(whole("out_proj"), BF16),
        "gate_full": shape((width, part), BF16),
        "up_full": shape((width, part), BF16),
        "all_kv": shape((tokens * n_ctx, 2 * head_size), BF16),
        "normed": shape((tokens, width), BF16),
        "q_low": shape((tokens, q_width), F32),
        "q_normed": shape((tokens, q_width), BF16),
        "q_rot": shape((tokens, heads_width), BF16),
        "gain_one": shape((1, width), F32),
        "gain_q": shape((1, q_width), F32),
        "gain_two": shape((1, width), F32),
        "tags": shape((n_ctx, 8, 128), F32),
    }
    out_hbm = ("w_qd", "w_kv", "w_qu", "w_out", "gate_full", "up_full", "all_kv")
    box = (inputs["w_gate"].shape[0], 2 * part)
    dma = pltpu.SemaphoreType.DMA
    scratch = {
        "infos": pltpu.VMEM((n_f,) + inputs["info"].shape, F32),
        "qd_full": pltpu.VMEM(whole("q_down"), BF16),
        "kv_full": pltpu.VMEM(whole("kv_weight"), BF16),
        "qu_full": pltpu.VMEM(whole("q_up"), BF16),
        "gate_box": pltpu.VMEM(box, BF16),
        "up_box": pltpu.VMEM(box, BF16),
        "gate_spare": pltpu.VMEM((box[0], part), BF16),
        "up_spare": pltpu.VMEM((box[0], part), BF16),
        "out_spare": pltpu.VMEM(inputs["out_proj"].shape, BF16),
        "kv_rows": pltpu.VMEM((tokens, 2 * head_size), BF16),
        "send_sem": dma((64 + 2 * n_ctx,)),
        "recv_sem": dma((64 + 2 * n_ctx,)),
        "local_sem": dma((16,)),
    }
    vmem = pl.BlockSpec(memory_space=pltpu.VMEM)
    anywhere = pl.BlockSpec(memory_space=pl.ANY)
    names = tuple(inputs) + tuple(outs) + tuple(scratch)
    values = pl.pallas_call(
        functools.partial(front_kernel, n_ctx, n_f, names),
        out_shape=tuple(outs.values()),
        in_specs=[anywhere if m in in_hbm else vmem for m in inputs],
        out_specs=tuple([anywhere if m in out_hbm else vmem for m in outs]),
        scratch_shapes=list(scratch.values()),
        compiler_params=pltpu.CompilerParams(
            collective_id=1, has_side_effects=True, vmem_limit_bytes=48 << 20
        ),
        name="front",
    )(*inputs.values())
    return dict(zip(outs, values, strict=True))


def tiles(total, wide, body):
    whole = total // wide

    @pl.loop(0, whole)
    def _(t):
        body(pl.multiple_of(t * wide, wide), wide)

    if total % wide:
        body(whole * wide, total % wide)


def contract_first(a, b):
    return jnp.dot(a.T, b, preferred_element_type=F32)


def ffn_kernel(n_f, names, *refs):
    r = dict(zip(names, refs, strict=True))
    c_idx = lax.axis_index("ctx")
    f_idx = lax.axis_index("fsdp")
    moves = Sender()
    at_sem = [0]
    core, far = (c_idx, flip(f_idx, 1)), (c_idx, flip(f_idx, 2))
    beside = (flip(c_idx, 1), f_idx)
    y_idx = c_idx % 2

    def send(src, dst, peer):
        i = at_sem[0]
        at_sem[0] += 1
        return moves(src, dst, r["send_sem"].at[i], r["recv_sem"].at[i], peer)

    barrier = pltpu.get_barrier_semaphore()
    for peer in (core, far, (c_idx, flip(f_idx, 3)), beside):
        pl.semaphore_signal(barrier, inc=1, device_id=peer, device_id_type=MESH)
    pl.semaphore_wait(barrier, 4)

    tokens, width = r["normed"].shape
    mine = r["attn_group"].at[pl.ds(pl.multiple_of(f_idx * tokens, tokens), tokens)]
    own_attn = pltpu.make_async_copy(r["attn_cut"].at[f_idx], mine, r["load_sem"].at[3])
    own_attn.start()

    def send_attn(mask):
        return send(r["attn_cut"].at[flip(f_idx, mask)], mine, (c_idx, flip(f_idx, mask)))

    units = r["w_down"].shape[0]
    group, dz = r["group"], r["dz"]
    block = [slice(i * tokens, (i + 1) * tokens) for i in range(4)]
    pair = [slice(0, 2 * tokens), slice(2 * tokens, 4 * tokens)]

    def gather(buf):
        to_core = send(buf.at[block[0]], buf.at[block[1]], core)
        to_far = send(buf.at[block[0]], buf.at[block[2]], far)
        return to_core, to_far

    def gather_far(buf, to_far):
        to_far.wait_recv()
        send(buf.at[block[2]], buf.at[block[3]], core).wait_recv()

    group[block[0], :] = r["normed"][...]
    to_core, to_far = gather(group)
    loads = []
    for i, m in enumerate(("gate", "up", "down")):
        load = pltpu.make_async_copy(r["w_" + m], r["v_" + m], r["load_sem"].at[i])
        load.start()
        loads.append(load)
    loads[0].wait()
    loads[1].wait()

    def hidden_part(rows):
        def one(start, wide):
            at = pl.ds(start, wide)
            both = jnp.concatenate([r["v_gate"][:, at], r["v_up"][:, at]], axis=1)
            out = jnp.dot(group[rows, :], both, preferred_element_type=F32)
            gate, up = out[:, :wide], out[:, wide:]
            r["gate"][rows, at] = gate.astype(BF16)
            r["up"][rows, at] = up.astype(BF16)
            r["hid"][rows, at] = (gate / (1.0 + jnp.exp(-gate)) * up).astype(BF16)

        tiles(units, 128, one)

    to_core.wait_recv()
    hidden_part(pair[0])
    gather_far(group, to_far)
    attn_copies = [send_attn(1), send_attn(2)]
    hidden_part(pair[1])
    loads[2].wait()

    def down_block(i, dest):
        def one(start, wide):
            at = pl.ds(start, wide)
            dest[:, at] = jnp.dot(
                r["hid"][block[i], :], r["v_down"][:, at], preferred_element_type=F32
            ).astype(dest.dtype)

        tiles(width, 256, one)

    def back_block(i, dest):
        def one(start, wide):
            at = pl.ds(start, wide)
            dest[:, at] = (
                contract_last(r["gate"][block[i], :], r["v_gate"][at, :])
                + contract_last(r["up"][block[i], :], r["v_up"][at, :])
            ).astype(dest.dtype)

        tiles(width, 256, one)

    def add_rows(dest, one, two):
        def add(at):
            dest[at, :] = (one[at, :].astype(F32) + two[at, :].astype(F32)).astype(dest.dtype)

        row_loop(tokens, add)

    def far_sum(k, make):
        make(3, r["give"].at[2 * k])
        step = send(r["give"].at[2 * k], r["got"].at[2 * k], core)
        make(2, r["far_sum"])
        step.wait_recv()
        add_rows(r["far_give"].at[k], r["far_sum"], r["got"].at[2 * k])
        return send(r["far_give"].at[k], r["far_got"].at[k], far)

    def near_sum(k, make):
        make(1, r["give"].at[2 * k + 1])
        step = send(r["give"].at[2 * k + 1], r["got"].at[2 * k + 1], core)
        make(0, r["near_sum"])
        return step

    def near_end(k, step):
        step.wait_recv()
        add_rows(r["near_sum"], r["near_sum"], r["got"].at[2 * k + 1])

    far_step = far_sum(0, down_block)
    near_end(0, near_sum(0, down_block))
    far_step.wait_recv()
    r["sq"][...] = jnp.zeros_like(r["sq"])

    def loss_rows(at):
        value = r["resid"][at, :] + r["near_sum"][at, :] + r["far_got"][0, at, :].astype(F32)
        r["result"][at, :] = value.astype(BF16)
        diff = value - r["teacher"][at, :].astype(F32)
        squares = jnp.sum(diff * diff, axis=1, keepdims=True) * r["valid"][at, :]
        r["sq"][:1, :] += jnp.sum(squares, axis=0, keepdims=True)
        grad = diff * r["valid_scale"][at, :1]
        r["grad_resid"][at, :] = grad
        dz[at, :] = grad.astype(BF16)

    row_loop(tokens, loss_rows, step=16)
    to_core, to_far = gather(dz)

    def back_hidden(rows):
        def one(start, wide):
            at = pl.ds(start, wide)
            grad = contract_last(dz[rows, :], r["v_down"][at, :])
            gate = r["gate"][rows, at].astype(F32)
            up = r["up"][rows, at].astype(F32)
            sigma = 1.0 / (1.0 + jnp.exp(-gate))
            r["gate"][rows, at] = (grad * up * sigma * (1.0 + gate * (1.0 - sigma))).astype(BF16)
            r["up"][rows, at] = (grad * (gate * sigma)).astype(BF16)

        tiles(units, 256, one)

    to_core.wait_recv()
    back_hidden(pair[0])
    near_step = near_sum(1, back_block)
    gather_far(dz, to_far)
    saves = []

    def save(src, dst, i):
        copy = pltpu.make_async_copy(src, dst, r["save_sem"].at[i])
        copy.start()
        return copy

    def down_tile(start, wide):
        at = pl.ds(start, wide)
        spot = r["tile"].at[pl.ds(0, wide)]
        spot[...] = contract_first(r["hid"][:, at], dz[...]).astype(BF16)
        save(spot, r["down_part"].at[at], 0).wait()

    tiles(units, 128, down_tile)
    half = units // 2
    give = pl.ds(pl.multiple_of((1 - y_idx) * half, half), half)
    down_step = send(r["down_part"].at[give], r["down_got"], beside)
    attn_copies.append(send_attn(3))
    back_hidden(pair[1])
    far_step = far_sum(1, back_block)
    near_end(1, near_step)

    def gate_tile(start, wide):
        at = pl.ds(start, wide)
        left = group[:, at].T
        for i, m in enumerate(("gate", "up")):
            spot = r["wide_tile"].at[i]
            spot[...] = jnp.dot(left, r[m][...], preferred_element_type=F32).astype(BF16)
            saves.append(save(spot, r[m + "_part"].at[at], 1 + i))
        saves.pop().wait()
        saves.pop().wait()

    tiles(width, 256, gate_tile)
    far_step.wait_recv()
    gain = r["gain_two"][...]
    r["gain_sum"][...] = jnp.zeros_like(r["gain_sum"])

    def norm_rows(at):
        grad = r["near_sum"][at, :] + r["far_got"][1, at, :].astype(F32)
        value = r["resid"][at, :]
        scale = lax.rsqrt(jnp.mean(value * value, axis=-1, keepdims=True) + NORM_EPS)
        r["gain_sum"][...] += jnp.sum(grad * value * scale, axis=0, keepdims=True)
        ge = gain * grad
        inner = jnp.mean(ge * value, axis=-1, keepdims=True)
        total = r["grad_resid"][at, :] + scale * ge - value * (scale * scale * scale) * inner
        r["grad_resid"][at, :] = total
        r["grad_branch"][at, :] = total.astype(BF16)

    row_loop(tokens, norm_rows, step=16)
    for copy in attn_copies + [down_step]:
        copy.wait_recv()
    own_attn.wait()
    moves.finish()


def feed_forward(n_f, inputs):
    tokens, width = inputs["normed"].shape
    units = inputs["w_down"].shape[0]
    shape = jax.ShapeDtypeStruct
    outs = {
        "result": shape((tokens, width), BF16),
        "grad_resid": shape((tokens, width), F32),
        "grad_branch": shape((tokens, width), BF16),
        "down_part": shape((units, width), BF16),
        "down_got": shape((units // 2, width), BF16),
        "gate_part": shape((width, units), BF16),
        "up_part": shape((width, units), BF16),
        "attn_group": shape((tokens * n_f, inputs["attn_cut"].shape[2]), BF16),
        "gain_sum": shape((1, width), F32),
        "sq": shape((8, 128), F32),
    }
    hbm = ("w_gate", "w_up", "w_down", "attn_cut", "attn_group")
    hbm += ("down_part", "down_got", "gate_part", "up_part")
    dma = pltpu.SemaphoreType.DMA
    many = tokens * n_f
    scratch = {
        "v_gate": pltpu.VMEM((width, units), BF16),
        "v_up": pltpu.VMEM((width, units), BF16),
        "v_down": pltpu.VMEM((units, width), BF16),
        "group": pltpu.VMEM((many, width), BF16),
        "dz": pltpu.VMEM((many, width), BF16),
        "gate": pltpu.VMEM((many, units), BF16),
        "up": pltpu.VMEM((many, units), BF16),
        "hid": pltpu.VMEM((many, units), BF16),
        "give": pltpu.VMEM((4, tokens, width), BF16),
        "got": pltpu.VMEM((4, tokens, width), BF16),
        "far_sum": pltpu.VMEM((tokens, width), F32),
        "near_sum": pltpu.VMEM((tokens, width), F32),
        "far_give": pltpu.VMEM((2, tokens, width), BF16),
        "far_got": pltpu.VMEM((2, tokens, width), BF16),
        "tile": pltpu.VMEM((128, width), BF16),
        "wide_tile": pltpu.VMEM((2, 256, units), BF16),
        "send_sem": dma((16,)),
        "recv_sem": dma((16,)),
        "load_sem": dma((4,)),
        "save_sem": dma((3,)),
    }
    vmem = pl.BlockSpec(memory_space=pltpu.VMEM)
    anywhere = pl.BlockSpec(memory_space=pl.ANY)
    names = tuple(inputs) + tuple(outs) + tuple(scratch)
    values = pl.pallas_call(
        functools.partial(ffn_kernel, n_f, names),
        out_shape=tuple(outs.values()),
        in_specs=[anywhere if m in hbm else vmem for m in inputs],
        out_specs=tuple([anywhere if m in hbm else vmem for m in outs]),
        scratch_shapes=list(scratch.values()),
        compiler_params=pltpu.CompilerParams(
            collective_id=2, has_side_effects=True, vmem_limit_bytes=60 << 20
        ),
        name="feed_forward",
    )(*inputs.values())
    return dict(zip(outs, values, strict=True))


def body(
    hidden_in,
    teacher,
    blocks,
    seq_ids,
    valid_mask,
    norm1_gain,
    q_down,
    q_gain,
    q_up,
    kv_weight,
    out_proj,
    norm2_gain,
    w_gate,
    w_up,
    w_down,
):
    row_count, model_width = hidden_in.shape
    head_size = kv_weight.shape[1] // 2
    heads_width = q_up.shape[1]
    head_count = heads_width // head_size
    half_dim = head_size // 2
    q_width = q_down.shape[1]
    n_ctx = lax.axis_size("ctx")
    n_f = lax.axis_size("fsdp")
    n_z = n_ctx // 2
    token_total = row_count * n_ctx * n_f
    seq_pieces = 2 * SEQ_BLOCKS
    c_idx = lax.axis_index("ctx")
    f_idx = lax.axis_index("fsdp")
    y_idx = c_idx % 2
    z_idx = c_idx // 2
    x_idx = f_idx // 2
    k_idx = f_idx % 2

    def by_f(values, mask):
        return lax.ppermute(values, "fsdp", [(i, i ^ mask) for i in range(n_f)])

    def by_c(values, mask):
        return lax.ppermute(values, "ctx", [(i, i ^ mask) for i in range(n_ctx)])

    def cut(values, start, size, axis):
        return lax.dynamic_slice_in_dim(values, start, size, axis)

    def ctx_split(grad):
        view = grad.reshape(n_z, 2, grad.shape[0] // n_ctx, grad.shape[1])
        give = lax.dynamic_index_in_dim(view, 1 - y_idx, 1, keepdims=False)
        keep = lax.dynamic_index_in_dim(view, y_idx, 1, keepdims=False)
        return give, keep

    def ctx_pair(keep, got):
        return (keep.astype(F32) + got.astype(F32)).astype(BF16)

    def ctx_spread(pair):
        return [pair] + [
            by_c(lax.dynamic_index_in_dim(pair, z_idx ^ r, 0, keepdims=False), 2 * r)
            for r in range(1, n_z)
        ]

    def ctx_total(parts):
        total = lax.dynamic_index_in_dim(parts[0], z_idx, 0, keepdims=False).astype(F32)
        for got in parts[1:]:
            total = total + got.astype(F32)
        return total

    def group_rows(values):
        return lax.all_gather(values, "fsdp", axis=0, tiled=True)

    valid_f = valid_mask.astype(F32)
    own_pieces = row_count // PIECE
    info = jnp.concatenate(
        [
            norm1_gain.astype(F32),
            q_gain.astype(F32),
            norm2_gain.astype(F32),
            jnp.full((128,), jnp.sum(valid_f)),
        ]
    )
    info = jnp.pad(info, (0, -info.shape[0] % 1024)).reshape(-1, 128)
    own_tags = jnp.stack([blocks.reshape(-1, PIECE)[:, 0], seq_ids.reshape(-1, PIECE)[:, 0]], 1)
    tag = jnp.pad(own_tags.astype(F32).reshape(1, -1), ((0, 7), (0, 128 - 2 * own_pieces)))
    own = jnp.concatenate([blocks.reshape(-1, PIECE)[:, 0], seq_ids[:1]])

    positions = blocks * PIECE + jnp.arange(row_count, dtype=jnp.int32) % PIECE
    freq_table = 10000.0 ** (-(jnp.arange(half_dim, dtype=F32) * 2.0 / head_size))
    angle_table = positions.astype(F32)[:, None] * freq_table[None, :]
    cosine = jnp.cos(angle_table)
    sine = jnp.sin(angle_table)
    fetched = front(
        n_ctx,
        n_f,
        {
            "q_down": q_down,
            "kv_weight": kv_weight,
            "q_up": q_up,
            "out_proj": out_proj,
            "w_gate": w_gate,
            "w_up": w_up,
            "hidden": hidden_in,
            "info": info,
            "tag": tag,
            "cos": cosine,
            "sin": sine,
        },
        head_size,
    )
    w_out = fetched["w_out"]
    all_kv, q_rot = fetched["all_kv"], fetched["q_rot"]
    normed, q_low, q_normed = fetched["normed"], fetched["q_low"], fetched["q_normed"]
    gain_one, gain_q, gain_two = fetched["gain_one"], fetched["gain_q"], fetched["gain_two"]
    tags = fetched["tags"][:, 0, : 2 * own_pieces].reshape(-1, 2).astype(jnp.int32)
    total_count = jnp.sum(fetched["tags"][:, 1, 0])
    hidden_f = hidden_in.astype(F32)
    scale_q = rms_scale(q_low)

    out_block = heads_width // (n_ctx * n_f)
    if out_block == 128:
        attn_heads, lse, attn_cut = attn_fwd(
            tags, own, q_rot, all_kv, head_size, seq_pieces, n_f, True
        )
    else:
        attn_heads, lse = attn_fwd(tags, own, q_rot, all_kv, head_size, seq_pieces, n_f, False)
        attn_cut = attn_heads.reshape(row_count, n_ctx, n_f, out_block).transpose(2, 0, 1, 3)
        attn_cut = attn_cut.reshape(n_f, row_count, n_ctx * out_block)
    resid = hidden_f + dot(attn_heads, w_out)
    scale_two = rms_scale(resid)
    normed_two = (resid * scale_two * gain_two).astype(BF16)

    wide_valid = jnp.broadcast_to(valid_f[:, None], (row_count, 128))
    ffn = feed_forward(
        n_f,
        {
            "normed": normed_two,
            "resid": resid,
            "teacher": teacher,
            "valid": wide_valid,
            "valid_scale": wide_valid * (token_total / total_count),
            "gain_two": gain_two,
            "w_gate": fetched["gate_full"],
            "w_up": fetched["up_full"],
            "w_down": w_down,
            "attn_cut": attn_cut,
        },
    )
    grad_resid, grad_branch = ffn["grad_resid"], ffn["grad_branch"]
    grad_gain_two = ffn["gain_sum"].reshape(-1)
    sq_local = ffn["sq"][0, 0]
    half_units = w_down.shape[0] // 2
    down_pair = ctx_pair(cut(ffn["down_part"], y_idx * half_units, half_units, 0), ffn["down_got"])
    down_parts = ctx_spread(down_pair.reshape(n_z, -1, model_width))
    gate_give, gate_keep = ctx_split(ffn["gate_part"])
    gate_got = by_c(gate_give, 1)
    up_part = ffn["up_part"]
    branch_group = group_rows(grad_branch)
    grad_attn = dot_t(grad_branch, w_out).astype(BF16)
    grad_qlin, grad_seq = attn_bwd(
        tags, own, q_rot, grad_attn, attn_heads, lse, cosine, sine, all_kv, head_size, seq_pieces
    )
    qlin_group = lax.all_to_all(grad_qlin, "fsdp", 1, 0, tiled=True)

    by_piece = grad_seq.reshape(seq_pieces, PIECE, 2 * head_size)
    piece_tag = tags[:, 0].reshape(n_z, 2, own_pieces)
    piece_own = (tags[:, 1] == seq_ids[0]).reshape(n_z, 2, own_pieces)

    def kv_half(bit):
        places = lax.dynamic_index_in_dim(piece_tag, bit, 1, keepdims=False).reshape(-1)
        picked = by_piece[places]
        if n_ctx * own_pieces != seq_pieces:
            mine = lax.dynamic_index_in_dim(piece_own, bit, 1, keepdims=False).reshape(-1)
            picked = jnp.where(mine[:, None, None], picked, jnp.zeros_like(picked))
        return picked.reshape(n_z, own_pieces * PIECE, 2 * head_size)

    kv_part = jnp.stack([kv_half(0), kv_half(1)], axis=1)
    q_cut, kv_cut = q_width // n_f, 2 * head_size // n_f
    qnorm_group = group_rows(q_normed)
    normed_group = group_rows(normed)

    grad_qnormed = dot_t(grad_qlin, fetched["w_qu"])
    grad_qlow_f, grad_gain_q = rms_back(q_low, scale_q, gain_q, grad_qnormed)
    grad_qlow = grad_qlow_f.astype(BF16)
    da_q = dot_t(grad_qlow, fetched["w_qd"])
    out_part = dot_rows(ffn["attn_group"], branch_group).astype(BF16)
    qup_part = dot_rows(qnorm_group, qlin_group).astype(BF16)
    down_parts, gate_got, qup_part, out_part = together(down_parts, gate_got, qup_part, out_part)
    gate_pair = ctx_pair(gate_keep, gate_got)

    def by_ctx(grad):
        return grad.reshape(n_z, 2, grad.shape[0] // n_ctx, grad.shape[1])

    order = [
        (c * n_f + f, f * n_ctx + c % 2 * n_z + c // 2) for c in range(n_ctx) for f in range(n_f)
    ]
    down_rows = ctx_total(down_parts).astype(BF16)
    down_sent = lax.ppermute(down_rows, ("ctx", "fsdp"), order)

    small = jnp.concatenate(
        [jnp.zeros((model_width,), F32), grad_gain_q, grad_gain_two, sq_local.reshape(1)]
    )
    entries = small.shape[0]
    small = jnp.pad(small, (0, -entries % 1024)).reshape(-1, 128)
    ends = tail_reduce(
        n_ctx,
        n_f,
        {
            "gate": gate_pair,
            "kv": kv_part,
            "up": by_ctx(up_part),
            "out": by_ctx(out_part),
            "qup": by_ctx(qup_part),
            "dqa": grad_qlow,
            "cos": cosine,
            "sin": sine,
            "normed_group": normed_group,
            "w_kv": fetched["w_kv"],
            "da_q": da_q,
            "hidden": hidden_in,
            "gain_one": gain_one,
            "grad_resid": grad_resid,
            "small": small,
        },
        q_width,
    )
    small, down_sent = together(ends["small_out"], down_sent)
    small = small.reshape(-1)[:entries]
    grad_down = down_sent.astype(F32)

    device = c_idx * n_f + f_idx
    q1, q2 = model_width, model_width + q_width
    n_dev = n_ctx * n_f

    def own_part(values):
        size = values.shape[0] // n_dev
        return cut(values, device * size, size, 0)

    loss_now = small[-1] / (model_width * total_count)
    return (
        ffn["result"],
        loss_now,
        ends["grad_input"],
        own_part(small[:q1]),
        ends["out_qd"],
        own_part(small[q1:q2]),
        ends["out_qup"],
        ends["out_kvw"],
        ends["out_out"],
        own_part(small[q2 : q2 + model_width]),
        ends["out_gate"],
        ends["out_up"],
        grad_down,
    )


def solution(mesh):
    both = ("ctx", "fsdp")
    rows = P(both, None)
    flat = P(both)
    shard = P("fsdp", None)
    gain = P("fsdp")
    return jax.shard_map(
        body,
        mesh=mesh,
        in_specs=(
            rows,
            rows,
            flat,
            flat,
            flat,
            gain,
            shard,
            gain,
            shard,
            shard,
            shard,
            gain,
            shard,
            shard,
            shard,
        ),
        out_specs=(
            rows,
            P(),
            rows,
            flat,
            rows,
            flat,
            rows,
            rows,
            rows,
            flat,
            rows,
            rows,
            rows,
        ),
        check_vma=False,
    )
```

```python
import functools
import math

import jax
import jax.numpy as jnp
from jax import lax
from jax.experimental import pallas as pl
from jax.experimental.pallas import tpu as pltpu
from jax.sharding import PartitionSpec as P

PIECE = 128
SEQ_BLOCKS = 8
NORM_EPS = 1e-05
F32 = jnp.float32
BF16 = jnp.bfloat16
LOG2E = math.log2(math.e)
HEAD_GROUP = 4


def rms_scale(values):
    return lax.rsqrt(jnp.mean(values * values, axis=-1, keepdims=True) + NORM_EPS)


def rms_back(values, scale, gain, grad):
    grad_gain = jnp.sum(grad * values * scale, axis=0)
    ge = gain * grad
    inner = jnp.mean(ge * values, axis=-1, keepdims=True)
    return scale * ge - values * (scale * scale * scale) * inner, grad_gain


def rope_apply(values, cosine, sine):
    half_dim = values.shape[-1] // 2
    one = values[..., :half_dim]
    two = values[..., half_dim:]
    return jnp.concatenate([one * cosine - two * sine, two * cosine + one * sine], axis=-1)


def rope_back(grads, cosine, sine):
    half_dim = grads.shape[-1] // 2
    one = grads[..., :half_dim]
    two = grads[..., half_dim:]
    return jnp.concatenate([one * cosine + two * sine, two * cosine - one * sine], axis=-1)


def together(*values):
    return lax.optimization_barrier(values)


def dot(a, b):
    return jnp.dot(a, b, preferred_element_type=F32)


def dot_t(a, b):
    return lax.dot_general(a, b, (((1,), (1,)), ((), ())), preferred_element_type=F32)


def dot_rows(a, b):
    return lax.dot_general(a, b, (((0,), (0,)), ((), ())), preferred_element_type=F32)


def contract_last(a, b):
    return lax.dot_general(a, b, (((1,), (1,)), ((), ())), preferred_element_type=F32)

def find_pieces(tags_ref, own_ref, pick_ref, total):
    @pl.loop(0, total)
    def _(u):
        @pl.when(tags_ref[u, 1] == own_ref[2])
        def _():
            pick_ref[tags_ref[u, 0]] = u

def stack_heads(ref, hd):
    return jnp.concatenate([ref[:, h*hd:(h+1)*hd] for h in range(HEAD_GROUP)], axis=0)

def attn_fwd_kernel(n_f, tags_ref, own_ref, q_ref, kv_ref, o_ref, lse_ref, *rest):
    k_s, vt_s, acc_s, pick_s = rest[-4:]
    half = pl.program_id(0)
    hd = k_s.shape[1]
    pieces = k_s.shape[0] // PIECE
    total = kv_ref.shape[0] // PIECE
    wide = 2 * PIECE
    coef = hd ** -0.5 * LOG2E

    @pl.when((half == 0) & (pl.program_id(1) == 0))
    def _():
        find_pieces(tags_ref, own_ref, pick_s, total)
        for i in range(pieces):
            rows = pl.ds(pl.multiple_of(pick_s[i] * PIECE, PIECE), PIECE)
            k_s[i*PIECE:(i+1)*PIECE, :] = kv_ref[rows, :hd]
            vt_s[:, i*PIECE:(i+1)*PIECE] = kv_ref[rows, hd:].T

    q = stack_heads(q_ref, hd)
    acc_s[...] = jnp.zeros_like(acc_s)
    rows = q.shape[0]
    def step(i, carry):
        peak, total_p = carry
        at = pl.ds(pl.multiple_of(i * wide, wide), wide)
        raw = contract_last(k_s[at, :], q)
        top = jnp.maximum(peak, jnp.max(raw, axis=0, keepdims=True))
        fade = jnp.exp2((peak - top) * coef)
        p = jnp.exp2((raw - top) * coef)
        acc_s[...] = acc_s[...] * fade + jnp.dot(vt_s[:, at], p.astype(BF16), preferred_element_type=F32)
        return top, total_p * fade + jnp.sum(p, axis=0, keepdims=True)
    count = own_ref[half] // 2 + 1
    peak, total_p = lax.fori_loop(0, count, step, (jnp.full((1, rows), -1e30, F32), jnp.zeros((1, rows), F32)))
    out = (acc_s[...] / total_p).astype(BF16).T
    for h in range(HEAD_GROUP):
        o_ref[:, h*hd:(h+1)*hd] = out[h*PIECE:(h+1)*PIECE, :]
    if len(rest) > 4:
        for b in range(HEAD_GROUP * hd // 128):
            head, part = b * 128 // hd, b * 128 % hd
            rest[0][b % n_f, :, b // n_f * 128:(b // n_f + 1) * 128] = out[
                head*PIECE:(head+1)*PIECE, part:part+128
            ]
    lse_ref[0] = peak * coef + jnp.log2(total_p)

def attn_fwd(tags, own, q, kv, hd, pieces, n_f, cut):
    n_rows, width = q.shape
    groups = width // hd // HEAD_GROUP
    gw = HEAD_GROUP * hd
    halves = n_rows // PIECE
    rows = HEAD_GROUP * PIECE
    blk = pl.BlockSpec((PIECE, gw), lambda p, g, *_: (p, g))
    flops = 4 * n_rows * width * pieces * PIECE * 9 // 16
    shapes = [jax.ShapeDtypeStruct(q.shape, BF16), jax.ShapeDtypeStruct((halves*groups, 1, rows), F32)]
    specs = [blk, pl.BlockSpec((1, 1, rows), lambda p, g, *_: (p*groups+g, 0, 0))]
    if cut:
        shapes.append(jax.ShapeDtypeStruct((n_f, n_rows, width // n_f), BF16))
        specs.append(pl.BlockSpec((n_f, PIECE, gw // n_f), lambda p, g, *_: (0, p, g)))
    return pl.pallas_call(
        functools.partial(attn_fwd_kernel, n_f),
        out_shape=tuple(shapes),
        grid_spec=pltpu.PrefetchScalarGridSpec(
            num_scalar_prefetch=2, grid=(halves, groups),
            in_specs=[blk, pl.BlockSpec(kv.shape, lambda p, g, *_: (0, 0))],
            out_specs=tuple(specs),
            scratch_shapes=[pltpu.VMEM((pieces*PIECE, hd), BF16), pltpu.VMEM((hd, pieces*PIECE), BF16),
                            pltpu.VMEM((hd, rows), F32), pltpu.SMEM((pieces,), jnp.int32)]),
        compiler_params=pltpu.CompilerParams(vmem_limit_bytes=40 << 20),
        cost_estimate=pl.CostEstimate(flops=flops, transcendentals=flops//(4*hd), bytes_accessed=2*(2*q.size+kv.size)),
        name="attn_fwd",
    )(tags, own, q, kv)

def attn_bwd_kernel(tags_ref, own_ref, q_ref, do_ref, o_ref, lse_ref, cos_ref, sin_ref, kv_ref, dq_ref, dkv_ref,
                    k_s, kt_s, v_s, dq_s, dk_s, dv_s, pick_s):
    half = pl.program_id(0)
    group = pl.program_id(1)
    hd = k_s.shape[1]
    pieces = k_s.shape[0] // PIECE
    total = kv_ref.shape[0] // PIECE
    wide = 2 * PIECE
    coef = hd ** -0.5 * LOG2E
    scale = hd ** -0.5

    @pl.when((half == 0) & (group == 0))
    def _():
        find_pieces(tags_ref, own_ref, pick_s, total)
        for i in range(pieces):
            rows = pl.ds(pl.multiple_of(pick_s[i] * PIECE, PIECE), PIECE)
            keys = kv_ref[rows, :hd]
            k_s[i*PIECE:(i+1)*PIECE, :] = keys
            kt_s[:, i*PIECE:(i+1)*PIECE] = keys.T
            v_s[i*PIECE:(i+1)*PIECE, :] = kv_ref[rows, hd:]
        dk_s[...] = jnp.zeros_like(dk_s)
        dv_s[...] = jnp.zeros_like(dv_s)

    q = stack_heads(q_ref, hd)
    do = stack_heads(do_ref, hd)
    prod = do.astype(F32) * stack_heads(o_ref, hd).astype(F32)
    delta = lax.dot_general(jnp.ones((8, hd), F32), prod, (((1,), (1,)), ((), ())),
                            preferred_element_type=F32, precision=lax.Precision.HIGHEST)[:1]
    lse = lse_ref[0]
    dq_s[...] = jnp.zeros_like(dq_s)
    def step(i, carry):
        at = pl.ds(pl.multiple_of(i * wide, wide), wide)
        p = jnp.exp2(contract_last(k_s[at, :], q) * coef - lse)
        dp = contract_last(v_s[at, :], do)
        ds = (p * (dp - delta)).astype(BF16)
        dv_s[at, :] += jnp.dot(p.astype(BF16), do, preferred_element_type=F32)
        dk_s[at, :] += jnp.dot(ds, q, preferred_element_type=F32)
        dq_s[...] += jnp.dot(kt_s[:, at], ds, preferred_element_type=F32)
        return carry
    lax.fori_loop(0, own_ref[half] // 2 + 1, step, 0)
    dq = (dq_s[...] * scale).T
    cos, sin = cos_ref[...], sin_ref[...]
    mid = hd // 2
    for h in range(HEAD_GROUP):
        one = dq[h*PIECE:(h+1)*PIECE, :mid]
        two = dq[h*PIECE:(h+1)*PIECE, mid:]
        dq_ref[:, h*hd:h*hd+mid] = (one * cos + two * sin).astype(BF16)
        dq_ref[:, h*hd+mid:(h+1)*hd] = (two * cos - one * sin).astype(BF16)

    @pl.when((half == pl.num_programs(0) - 1) & (group == pl.num_programs(1) - 1))
    def _():
        dkv_ref[:, :hd] = (dk_s[...] * scale).astype(BF16)
        dkv_ref[:, hd:] = dv_s[...].astype(BF16)

def attn_bwd(tags, own, q, do, o, lse, cos, sin, kv, hd, pieces):
    n_rows, width = q.shape
    groups = width // hd // HEAD_GROUP
    gw = HEAD_GROUP * hd
    halves = n_rows // PIECE
    rows = HEAD_GROUP * PIECE
    blk = pl.BlockSpec((PIECE, gw), lambda p, g, *_: (p, g))
    trig = pl.BlockSpec((PIECE, hd // 2), lambda p, g, *_: (p, 0))
    keys = pieces * PIECE
    flops = 10 * n_rows * width * keys * 9 // 16
    return pl.pallas_call(
        attn_bwd_kernel,
        out_shape=(jax.ShapeDtypeStruct(q.shape, BF16), jax.ShapeDtypeStruct((keys, 2*hd), BF16)),
        grid_spec=pltpu.PrefetchScalarGridSpec(
            num_scalar_prefetch=2, grid=(halves, groups),
            in_specs=[blk, blk, blk, pl.BlockSpec((1, 1, rows), lambda p, g, *_: (p*groups+g, 0, 0)), trig, trig,
                      pl.BlockSpec(kv.shape, lambda p, g, *_: (0, 0))],
            out_specs=[blk, pl.BlockSpec((keys, 2*hd), lambda p, g, *_: (0, 0))],
            scratch_shapes=[pltpu.VMEM((keys, hd), BF16), pltpu.VMEM((hd, keys), BF16), pltpu.VMEM((keys, hd), BF16),
                            pltpu.VMEM((hd, rows), F32), pltpu.VMEM((keys, hd), F32), pltpu.VMEM((keys, hd), F32),
                            pltpu.SMEM((pieces,), jnp.int32)]),
        compiler_params=pltpu.CompilerParams(vmem_limit_bytes=48 << 20),
        cost_estimate=pl.CostEstimate(flops=flops, transcendentals=flops//(10*hd), bytes_accessed=2*(4*q.size+2*kv.size)),
        name="attn_bwd",
    )(tags, own, q, do, o, lse, cos, sin, kv)

MESH = pl.DeviceIdType.MESH


def flip(index, mask):
    out = 0
    bit = 1
    while bit <= mask:
        part = (index // bit) % 2
        out = out + bit * ((1 - part) if mask & bit else part)
        bit *= 2
    return out + (index // bit) * bit


def row_loop(rows, body, step=32):
    if rows % step:
        step = 16

    @pl.loop(0, rows // step)
    def _(i):
        body(pl.ds(pl.multiple_of(i * step, step), step))


class Sender:
    def __init__(self):
        self.open = []

    def make(self, src, dst, send_sem, recv_sem, peer):
        return pltpu.make_async_remote_copy(
            src_ref=src,
            dst_ref=dst,
            send_sem=send_sem,
            recv_sem=recv_sem,
            device_id=peer,
            device_id_type=MESH,
        )

    def __call__(self, *args):
        copy = self.make(*args)
        copy.start()
        self.open.append(copy)
        return copy

    def finish(self):
        for copy in self.open:
            copy.wait_send()


class LineSum:
    def __init__(self, own, got, send_sem, recv_sem, c_idx, f_idx, n_z, sender):
        self.own, self.got, self.send_sem, self.recv_sem = own, got, send_sem, recv_sem
        self.n_z, self.sender = n_z, sender
        self.z = c_idx // 2
        self.left = (c_idx - 2, f_idx)
        self.right = (c_idx + 2, f_idx)

    def copy(self, b, slot, peer):
        return self.sender.make(
            self.own.at[b], self.got.at[slot], self.send_sem.at[b], self.recv_sem.at[slot], peer
        )

    def take(self, b, slot):
        self.copy(b, slot, self.left).wait_recv()

        def add(at):
            self.own[b, at, :] = (
                self.own[b, at, :].astype(F32) + self.got[slot, at, :].astype(F32)
            ).astype(BF16)

        row_loop(self.own.shape[1], add)

    def go_right(self, b):
        z = self.z

        @pl.when(z < b)
        def _():
            @pl.when(z > 0)
            def _():
                self.take(b, b)

            self.copy(b, b, self.right).start()

    def go_left(self, b):
        z, n_z = self.z, self.n_z

        @pl.when(z > b)
        def _():
            @pl.when(z < n_z - 1)
            def _():
                self.take(b, b)

            @pl.when(z - 1 > b)
            def _():
                self.copy(b, b, self.left).start()

            @pl.when(z - 1 == b)
            def _():
                self.copy(b, n_z, self.left).start()

    def step(self, i):
        @pl.when(2 * self.z < self.n_z)
        def _():
            self.go_right(self.n_z - 1 - i)
            self.go_left(i)

        @pl.when(2 * self.z >= self.n_z)
        def _():
            self.go_left(i)
            self.go_right(self.n_z - 1 - i)

    def total(self, store):
        z, n_z = self.z, self.n_z

        @pl.when(z > 0)
        def _():
            self.copy(z, z, self.left).wait_recv()

        @pl.when(z < n_z - 1)
        def _():
            self.copy(z, n_z, self.left).wait_recv()

        rows = self.own.shape[1]

        @pl.when(z == 0)
        def _():
            row_loop(
                rows,
                lambda at: store(
                    at, self.own[z, at, :].astype(F32) + self.got[n_z, at, :].astype(F32)
                ),
            )

        @pl.when(z == n_z - 1)
        def _():
            row_loop(
                rows,
                lambda at: store(
                    at, self.own[z, at, :].astype(F32) + self.got[z, at, :].astype(F32)
                ),
            )

        @pl.when((z > 0) & (z < n_z - 1))
        def _():
            row_loop(
                rows,
                lambda at: store(
                    at,
                    self.own[z, at, :].astype(F32)
                    + self.got[z, at, :].astype(F32)
                    + self.got[n_z, at, :].astype(F32),
                ),
            )

    def finish(self):
        for b in range(self.n_z):

            @pl.when(self.z != b)
            def _(b=b):
                self.copy(b, b, self.left).wait_send()


WINDOW = 3
TAIL_NAMES = ("gate", "kv", "up", "out", "qup", "low")
TAIL_CUT = ("gate", "up", "qup", "low")
TAIL_SENT = ("kv", "up", "out", "qup", "low")


def tail_kernel(n_ctx, n_f, names_in, names_out, names_scratch, *refs):
    n_z = n_ctx // 2
    names = list(names_in) + list(names_out) + list(names_scratch)
    r = dict(zip(names, refs, strict=True))
    c_idx = lax.axis_index("ctx")
    f_idx = lax.axis_index("fsdp")
    y_idx = c_idx % 2
    z_idx = c_idx // 2
    send = Sender()

    def over_c(mask):
        return (flip(c_idx, mask), f_idx)

    def over_f(mask):
        return (c_idx, flip(f_idx, mask))

    barrier = pltpu.get_barrier_semaphore()
    for mask in range(1, n_f):
        pl.semaphore_signal(barrier, inc=1, device_id=over_f(mask), device_id_type=MESH)
    for mask in range(1, n_ctx):
        pl.semaphore_signal(barrier, inc=1, device_id=over_c(mask), device_id_type=MESH)
    pl.semaphore_wait(barrier, n_f - 1 + n_ctx - 1)

    lines = {
        m: LineSum(
            r["pair_" + m],
            r["z_" + m],
            r["z_send"].at[i],
            r["z_recv"].at[i],
            c_idx,
            f_idx,
            n_z,
            send,
        )
        for i, m in enumerate(TAIL_NAMES)
    }
    y_copies, keeps = {}, {}
    early = r["up_got"].shape[0]

    parts = {m: r[m] for m in ("kv", "up", "out", "qup")}
    parts["low"] = r["part_low"]
    queue = [
        (m, b) for m in TAIL_SENT for b in range(n_z) if m != "up" or b >= early
    ]
    owed = tuple(queue)

    def next_y():
        if queue:
            m, b = queue.pop(0)
            i = TAIL_SENT.index(m)
            y_copies[m, b] = send(
                parts[m].at[b, 1 - y_idx],
                r["y_" + m].at[b],
                r["y_send"].at[i, b],
                r["y_recv"].at[i, b],
                over_c(1),
            )
            take_own(m, b)

    def take_own(m, b):
        keep = pltpu.make_async_copy(
            parts[m].at[b, y_idx],
            r["pair_" + m].at[b],
            r["keep_sem"].at[TAIL_SENT.index(m), b],
        )
        keep.start()
        keeps[m, b] = keep

    def add_pair(m, b):
        y_copies[m, b].wait_recv()
        next_y()
        add_ready(m, b)

    def add_ready(m, b):
        keeps[m, b].wait()
        pair, got = r["pair_" + m], r["y_" + m]

        def add(at):
            pair[b, at, :] = (pair[b, at, :].astype(F32) + got[b, at, :].astype(F32)).astype(BF16)

        row_loop(pair.shape[1], add)

    def advance(pair, line):
        if pair == "up":
            here.wait()
            for b in range(early):
                add_ready(pair, b)
        for b in range(n_z):
            if pair is not None and (pair, b) in owed:
                add_pair(pair, b)
            if line is not None and b < n_z - 1:
                lines[line].step(b)

    f_copies = {}

    def finish_sum(m):
        lines[m].total(lambda at, value: store_total(m, at, value))
        if m in TAIL_CUT:
            i = TAIL_CUT.index(m)
            part = r["tot_" + m].shape[0] // n_f
            for s in range(1, n_f):
                at = pl.ds(pl.multiple_of(flip(f_idx, s) * part, part), part)
                f_copies[m, s] = send(
                    r["tot_" + m].at[at, :],
                    r["f_" + m].at[s - 1],
                    r["f_send"].at[i, s - 1],
                    r["f_recv"].at[i, s - 1],
                    over_f(s),
                )

    def store_total(m, at, value):
        if m in TAIL_CUT:
            r["tot_" + m][at, :] = value.astype(BF16)
        else:
            r["out_" + m][at, :] = value

    def put_out(m):
        total = r["tot_" + m]
        rows, width = total.shape
        part = rows // n_f
        cuts = {"out_" + m: (0, width)}
        if m == "low":
            split = r["qd_group"].shape[1]
            cuts = {"out_qd": (0, split), "out_kvw": (split, width - split)}
        for s in range(n_f):
            source = flip(f_idx, s)
            if s:
                f_copies[m, s].wait_recv()
                got = r["f_" + m].at[s - 1]
            else:
                got = total.at[pl.ds(pl.multiple_of(f_idx * part, part), part)]
            for name, (start, wide) in cuts.items():
                at = pl.ds(pl.multiple_of(source * wide, 128), wide)
                r[name][:, at] = got[:, start : start + wide].astype(F32)

    def cut_low(src, dst, width, index):
        rows = src.shape[0]
        mine = pl.ds(pl.multiple_of(f_idx * rows, rows), rows)
        copies = []
        for s in range(1, n_f):
            at = pl.ds(pl.multiple_of(flip(f_idx, s) * width, 128), width)
            copies.append(
                send(
                    src.at[:, at],
                    dst.at[mine, :],
                    r["low_send"].at[index, s - 1],
                    r["low_recv"].at[index, s - 1],
                    over_f(s),
                )
            )
        own = pl.ds(pl.multiple_of(f_idx * width, 128), width)
        dst[mine, :] = src[:, own]
        return copies

    for _ in range(WINDOW):
        next_y()
    q_copies = cut_low(r["dqa"], r["qd_group"], r["qd_group"].shape[1], 0)
    pair_in = pltpu.make_async_copy(r["gate"], r["pair_gate"], r["keep_sem"].at[0, n_z])
    pair_in.start()
    here = pltpu.make_async_copy(
        r["up_got"], r["y_up"].at[pl.ds(0, early)], r["keep_sem"].at[1, n_z]
    )
    here.start()
    for b in range(early):
        take_own("up", b)
    pair_in.wait()
    advance("kv", "gate")
    advance("up", "kv")
    finish_sum("gate")

    head = r["dkv"].shape[1] // 2
    mid = head // 2

    def store_kv(at, value):
        cos, sin = r["cos"][at, :], r["sin"][at, :]
        one, two = value[:, :mid], value[:, mid:head]
        r["dkv"][at, :mid] = (one * cos + two * sin).astype(BF16)
        r["dkv"][at, mid:head] = (two * cos - one * sin).astype(BF16)
        r["dkv"][at, head:] = value[:, head:].astype(BF16)

    lines["kv"].total(store_kv)
    kv_copies = cut_low(r["dkv"], r["kv_group"], r["kv_group"].shape[1], 1)

    def low_part(group, start):
        normed, part = r["normed_group"], r["part_low"]
        rows = part.shape[2]
        for c in range(n_ctx):
            part[c // 2, c % 2, :, start : start + group.shape[1]] = lax.dot_general(
                normed[:, c * rows : (c + 1) * rows],
                group[...],
                (((0,), (0,)), ((), ())),
                preferred_element_type=F32,
            ).astype(BF16)

    for copy in q_copies:
        copy.wait_recv()
    low_part(r["qd_group"], 0)
    advance("out", "up")
    for copy in kv_copies:
        copy.wait_recv()
    low_part(r["kv_group"], r["qd_group"].shape[1])

    grad_in, w_kv = r["grad_input"], r["w_kv"]
    width = grad_in.shape[1]
    tile = 256

    @pl.loop(0, width // tile)
    def _(t):
        at = pl.ds(pl.multiple_of(t * tile, tile), tile)
        grad_in[:, at] = r["da_q"][:, at] + lax.dot_general(
            r["dkv"][...],
            w_kv[at, :],
            (((1,), (1,)), ((), ())),
            preferred_element_type=F32,
        )

    r["gain_sum"][...] = jnp.zeros_like(r["gain_sum"])
    gain = r["gain_one"][...]

    def norm_rows(at):
        value = r["hidden"][at, :].astype(F32)
        grad = grad_in[at, :]
        scale = lax.rsqrt(jnp.mean(value * value, axis=-1, keepdims=True) + NORM_EPS)
        r["gain_sum"][...] += jnp.sum(grad * value * scale, axis=0, keepdims=True)
        ge = gain * grad
        inner = jnp.mean(ge * value, axis=-1, keepdims=True)
        grad_in[at, :] = (
            r["grad_resid"][at, :] + scale * ge - value * (scale * scale * scale) * inner
        )

    row_loop(grad_in.shape[0], norm_rows, step=16)

    small, small_got = r["small_out"], r["small_got"]
    small[...] = r["small"][...]
    for i in range(width // 128):
        small[i : i + 1, :] = r["gain_sum"][:, i * 128 : (i + 1) * 128]
    steps = [over_f(1), over_f(2), over_c(1)]
    mask = 2
    while mask < n_ctx:
        steps.append(over_c(mask))
        mask *= 2
    small_copies = {}

    def small_start(s):
        small_got[s, 0] = small[...]
        small_copies[s] = send(
            small_got.at[s, 0],
            small_got.at[s, 1],
            r["s_send"].at[s],
            r["s_recv"].at[s],
            steps[s],
        )

    def small_end(s):
        small_copies[s].wait_recv()
        small[...] = small[...] + small_got[s, 1]

    for s in range(2):
        small_start(s)
        small_end(s)
    small_start(2)

    put_out("gate")
    advance("qup", "out")
    finish_sum("up")
    advance("low", "qup")
    finish_sum("out")
    small_end(2)
    small_start(3)
    put_out("up")
    finish_sum("qup")
    advance(None, "low")
    for s in range(3, len(steps)):
        if s > 3:
            small_start(s)
        small_end(s)
    finish_sum("low")
    put_out("qup")
    put_out("low")
    send.finish()
    for m in TAIL_NAMES:
        lines[m].finish()


def tail_reduce(n_ctx, n_f, inputs, q_width):
    n_z = n_ctx // 2
    vmem = pl.BlockSpec(memory_space=pltpu.VMEM)
    anywhere = pl.BlockSpec(memory_space=pl.ANY)
    rows, width = inputs["hidden"].shape
    kv_width = inputs["w_kv"].shape[1]
    in_hbm = ("gate", "kv", "up", "up_got", "out", "qup")
    names_in = tuple(inputs)
    in_specs = [anywhere if m in in_hbm else vmem for m in names_in]
    block = {m: inputs[m].shape[-2:] for m in in_hbm}
    cut_q, cut_kv, high = q_width // n_f, kv_width // n_f, width // n_ctx
    block["low"] = (high, cut_q + cut_kv)
    outs = {
        "small_out": jax.ShapeDtypeStruct(inputs["small"].shape, F32),
        "grad_input": jax.ShapeDtypeStruct((rows, width), F32),
        "out_qd": jax.ShapeDtypeStruct((high // n_f, q_width), F32),
        "out_kvw": jax.ShapeDtypeStruct((high // n_f, kv_width), F32),
    }
    scratch = {}
    for m in TAIL_NAMES:
        high, wide = block[m]
        scratch["pair_" + m] = pltpu.VMEM((n_z, high, wide), BF16)
        scratch["z_" + m] = pltpu.VMEM((n_z + 1, high, wide), BF16)
        if m in TAIL_SENT:
            scratch["y_" + m] = pltpu.VMEM((n_z, high, wide), BF16)
        if m in TAIL_CUT:
            scratch["tot_" + m] = pltpu.VMEM((high, wide), BF16)
            scratch["f_" + m] = pltpu.VMEM((n_f - 1, high // n_f, wide), BF16)
            if m != "low":
                outs["out_" + m] = jax.ShapeDtypeStruct((high // n_f, wide * n_f), F32)
        elif m != "kv":
            outs["out_" + m] = jax.ShapeDtypeStruct((high, wide), F32)
    scratch["dkv"] = pltpu.VMEM((rows, kv_width), BF16)
    scratch["qd_group"] = pltpu.VMEM((rows * n_f, q_width // n_f), BF16)
    scratch["kv_group"] = pltpu.VMEM((rows * n_f, kv_width // n_f), BF16)
    scratch["part_low"] = pltpu.VMEM((n_z, 2) + block["low"], BF16)
    scratch["gain_sum"] = pltpu.VMEM((1, width), F32)
    steps = 2 + (n_ctx.bit_length() - 1)
    scratch["small_got"] = pltpu.VMEM((steps, 2) + inputs["small"].shape, F32)
    dma = pltpu.SemaphoreType.DMA
    sent, cut = len(TAIL_SENT), len(TAIL_CUT)
    scratch["s_send"] = dma((steps,))
    scratch["s_recv"] = dma((steps,))
    scratch["y_send"] = dma((sent, n_z))
    scratch["y_recv"] = dma((sent, n_z))
    scratch["keep_sem"] = dma((sent, n_z + 1))
    scratch["z_send"] = dma((len(TAIL_NAMES), n_z))
    scratch["z_recv"] = dma((len(TAIL_NAMES), n_z + 1))
    scratch["f_send"] = dma((cut, n_f - 1))
    scratch["f_recv"] = dma((cut, n_f - 1))
    scratch["low_send"] = dma((2, n_f - 1))
    scratch["low_recv"] = dma((2, n_f - 1))
    values = pl.pallas_call(
        functools.partial(tail_kernel, n_ctx, n_f, names_in, tuple(outs), tuple(scratch)),
        out_shape=tuple(outs.values()),
        in_specs=in_specs,
        out_specs=tuple([vmem] * len(outs)),
        scratch_shapes=list(scratch.values()),
        compiler_params=pltpu.CompilerParams(
            collective_id=0, has_side_effects=True, vmem_limit_bytes=60 << 20
        ),
        name="tail_reduce",
    )(*inputs.values())
    return dict(zip(outs, values, strict=True))


def front_kernel(n_ctx, n_f, names, *refs):
    r = dict(zip(names, refs, strict=True))
    n_z = n_ctx // 2
    c_idx = lax.axis_index("ctx")
    f_idx = lax.axis_index("fsdp")
    y_idx = c_idx % 2
    z_bit = (c_idx // 2) % 2
    x_idx = f_idx // 2
    k_idx = f_idx % 2
    far_idx = flip(f_idx, 2)
    moves = Sender()
    local = []
    at_sem = [0]

    def over_c(mask):
        return (flip(c_idx, mask), f_idx)

    def over_f(mask):
        return (c_idx, flip(f_idx, mask))

    def send(src, dst, peer):
        i = at_sem[0]
        at_sem[0] += 1
        return moves(src, dst, r["send_sem"].at[i], r["recv_sem"].at[i], peer)

    def keep(src, dst):
        copy = pltpu.make_async_copy(src, dst, r["local_sem"].at[len(local)])
        copy.start()
        local.append(copy)
        return copy

    def rows(start, size):
        return pl.ds(pl.multiple_of(start, size), size)

    barrier = pltpu.get_barrier_semaphore()
    for mask in range(1, n_f):
        pl.semaphore_signal(barrier, inc=1, device_id=over_f(mask), device_id_type=MESH)
    for mask in range(1, n_ctx):
        pl.semaphore_signal(barrier, inc=1, device_id=over_c(mask), device_id_type=MESH)
    pl.semaphore_wait(barrier, n_f - 1 + n_ctx - 1)

    infos, tags = r["infos"], r["tags"]
    infos[f_idx] = r["info"][...]
    info_copies = [
        send(infos.at[f_idx], infos.at[f_idx], over_f(mask)) for mask in range(1, n_f)
    ]

    class Rows:
        def __init__(self, shard, dest, bit, hop, chunks):
            self.dest, self.bit, self.hop = dest, bit, hop
            self.shard = shard
            self.size = shard.shape[0]
            self.half = self.size // 2
            self.step = self.half // chunks
            self.chunks = chunks
            self.far, self.next, self.cross = [], [], []

        def start(self, spare=None):
            mine = self.dest.at[rows(f_idx * self.size, self.size)]
            if spare is None:
                self.kept = keep(self.shard, mine)
            else:
                self.spare, self.kept = spare, keep(self.shard, spare)
            self.cross.append(send(self.shard, mine, over_f(1)))

        def settle(self):
            self.kept.wait()
            keep(self.spare, self.dest.at[rows(f_idx * self.size, self.size)])

        def reach(self, i):
            part = self.bit * self.half + i * self.step
            self.far.append(
                send(
                    self.shard.at[rows(part, self.step)],
                    self.dest.at[rows(f_idx * self.size + part, self.step)],
                    over_f(2),
                )
            )

        def place(self, bit, i):
            return self.dest.at[rows(far_idx * self.size + bit * self.half + i * self.step, self.step)]

        def hop_on(self, i):
            self.far[i].wait_recv()
            reach_next()
            here = self.place(self.bit, i)
            self.next.append(send(here, here, over_c(self.hop)))
            self.cross.append(send(here, here, over_f(1)))

        def pass_on(self, i):
            self.next[i].wait_recv()
            here = self.place(1 - self.bit, i)
            self.cross.append(send(here, here, over_f(1)))

        def end(self):
            for copy in self.cross:
                copy.wait_recv()

    class Columns:
        def __init__(self, shard, dest, box, bits, hops):
            self.shard, self.dest, self.box = shard, dest, box
            self.bits, self.hops = bits, hops
            self.size = shard.shape[0]
            self.width = dest.shape[1]
            self.quarter = self.size // 4

        def columns(self, start, count=1):
            return pl.ds(pl.multiple_of(start * self.width, 128), count * self.width)

        def start(self, spare):
            mine = self.dest.at[rows(f_idx * self.size, self.size)]
            self.spare, self.kept = spare, keep(self.shard.at[:, self.columns(f_idx)], spare)
            self.cross = [send(self.shard.at[:, self.columns(flip(f_idx, 1))], mine, over_f(1))]

        def settle(self):
            self.kept.wait()
            keep(self.spare, self.dest.at[rows(f_idx * self.size, self.size)])

        def reach(self, i):
            one, two = self.bits
            at = rows((two * 2 + one) * self.quarter, self.quarter)
            self.far = send(
                self.shard.at[at, self.columns((1 - x_idx) * 2, 2)], self.box.at[at], over_f(2)
            )

        def piece(self, one, two):
            return self.box.at[rows((two * 2 + one) * self.quarter, self.quarter)]

        def first(self):
            one, two = self.bits
            self.far.wait_recv()
            reach_next()
            here = self.piece(one, two)
            self.step = send(here, here, over_c(self.hops[0]))
            self.last = [send(here, here, over_c(self.hops[1]))]

        def second(self):
            one, two = self.bits
            self.step.wait_recv()
            here = self.piece(1 - one, two)
            self.last.append(send(here, here, over_c(self.hops[1])))

        def part(self):
            for copy in self.last:
                copy.wait_recv()
            there = self.dest.at[rows(far_idx * self.size, self.size)]
            self.cross.append(send(self.box.at[:, self.columns(1 - k_idx)], there, over_f(1)))
            keep(self.box.at[:, self.columns(k_idx)], there)

        def end(self):
            for copy in self.cross:
                copy.wait_recv()

    kv = Rows(r["kv_weight"], r["kv_full"], y_idx, 1, 1)
    qd = Rows(r["q_down"], r["qd_full"], y_idx, 1, 1)
    qu = Rows(r["q_up"], r["qu_full"], y_idx, 1, 2)
    out = Rows(r["out_proj"], r["w_out"], z_bit, 2, 4)
    gate = Columns(r["w_gate"], r["gate_full"], r["gate_box"], (y_idx, z_bit), (1, 2))
    up = Columns(r["w_up"], r["up_full"], r["up_box"], (z_bit, y_idx), (2, 1))
    queue = [(kv, 0), (qd, 0), (qu, 0), (qu, 1), (gate, 0), (up, 0)]
    queue += [(out, i) for i in range(out.chunks)]

    def reach_next():
        if queue:
            part, i = queue.pop(0)
            part.reach(i)

    reach_next()
    reach_next()
    kv.start()
    qd.start()

    for copy in info_copies:
        copy.wait_recv()
    d1 = r["gain_one"].shape[1] // n_f // 128
    d2 = r["gain_q"].shape[1] // n_f // 128
    count = infos[0, 2 * d1 + d2 : 2 * d1 + d2 + 1, :]
    for f in range(n_f):
        for i in range(d1):
            col = slice((f * d1 + i) * 128, (f * d1 + i + 1) * 128)
            r["gain_one"][:, col] = infos[f, i : i + 1, :]
            r["gain_two"][:, col] = infos[f, d1 + d2 + i : d1 + d2 + i + 1, :]
        for i in range(d2):
            col = slice((f * d2 + i) * 128, (f * d2 + i + 1) * 128)
            r["gain_q"][:, col] = infos[f, d1 + i : d1 + i + 1, :]
        if f:
            count = count + infos[f, 2 * d1 + d2 : 2 * d1 + d2 + 1, :]
    tags[c_idx] = r["tag"][...]
    tags[c_idx, 1:2, :] = count
    tag_copies = [send(tags.at[c_idx], tags.at[c_idx], over_c(mask)) for mask in range(1, n_ctx)]

    normed = r["normed"]
    gain_one = r["gain_one"][...]

    def norm_rows(at):
        value = r["hidden"][at, :].astype(F32)
        scale = lax.rsqrt(jnp.mean(value * value, axis=-1, keepdims=True) + NORM_EPS)
        normed[at, :] = (value * scale * gain_one).astype(BF16)

    row_loop(normed.shape[0], norm_rows, step=16)

    kv.hop_on(0)
    qd.hop_on(0)
    qu.start()
    kv.pass_on(0)
    qd.pass_on(0)
    kv.end()
    kv.kept.wait()
    head = r["kv_full"].shape[1] // 2
    mid = head // 2
    cos, sin = r["cos"], r["sin"]
    kv_rows = r["kv_rows"]
    keys = jnp.dot(normed[...], r["kv_full"][:, :head], preferred_element_type=F32)
    one, two = keys[:, :mid], keys[:, mid:]
    kv_rows[:, :mid] = (one * cos[...] - two * sin[...]).astype(BF16)
    kv_rows[:, mid:head] = (two * cos[...] + one * sin[...]).astype(BF16)
    kv_rows[:, head:] = jnp.dot(
        normed[...], r["kv_full"][:, head:], preferred_element_type=F32
    ).astype(BF16)
    all_kv = r["all_kv"]
    tokens = normed.shape[0]

    def kv_place(c):
        return all_kv.at[rows(c * tokens, tokens)]

    kv_z = [send(kv_rows, kv_place(c_idx), over_c(2 * s)) for s in range(1, n_z)]
    kv_y = [send(kv_rows, kv_place(c_idx), over_c(1))]
    keep(kv_rows, kv_place(c_idx))
    qu.hop_on(0)
    qd.end()
    qd.kept.wait()

    @pl.loop(0, r["q_low"].shape[1] // 256)
    def _(t):
        at = pl.ds(pl.multiple_of(t * 256, 256), 256)
        r["q_low"][:, at] = jnp.dot(
            normed[...], r["qd_full"][:, at], preferred_element_type=F32
        )

    gain_q = r["gain_q"][...]

    def norm_low(at):
        value = r["q_low"][at, :]
        scale = lax.rsqrt(jnp.mean(value * value, axis=-1, keepdims=True) + NORM_EPS)
        r["q_normed"][at, :] = (value * scale * gain_q).astype(BF16)

    row_loop(tokens, norm_low, step=16)
    qu.hop_on(1)
    for s in range(1, n_z):
        kv_z[s - 1].wait_recv()
        here = kv_place(flip(c_idx, 2 * s))
        kv_y.append(send(here, here, over_c(1)))
    qu.pass_on(0)
    qu.pass_on(1)
    gate.first()
    qu.end()
    for m, part in (("gate", gate), ("up", up), ("out", out)):
        part.start(r[m + "_spare"])
    qu.kept.wait()

    @pl.loop(0, r["q_rot"].shape[1] // head)
    def _(h):
        start = pl.multiple_of(h * head, head)
        value = jnp.dot(
            r["q_normed"][...],
            r["qu_full"][:, pl.ds(start, head)],
            preferred_element_type=F32,
        )
        one, two = value[:, :mid], value[:, mid:]
        r["q_rot"][:, pl.ds(start, mid)] = (one * cos[...] - two * sin[...]).astype(BF16)
        late = pl.multiple_of(h * head + mid, mid)
        r["q_rot"][:, pl.ds(late, mid)] = (two * cos[...] + one * sin[...]).astype(BF16)

    up.first()
    for part in (gate, up, out):
        part.settle()
    for m in ("kv", "qd", "qu"):
        keep(r[m + "_full"], r["w_" + m])
    gate.second()
    out.hop_on(0)
    up.second()
    for i in range(1, out.chunks):
        out.hop_on(i)
    gate.part()
    for i in range(out.chunks):
        out.pass_on(i)
    up.part()
    for copy in kv_y + tag_copies:
        copy.wait_recv()
    for part in (gate, up, out):
        part.end()
    for copy in local:
        if not any(copy is part.kept for part in (kv, qd, qu, gate, up, out)):
            copy.wait()
    moves.finish()


def front(n_ctx, n_f, inputs, head_size):
    tokens, width = inputs["hidden"].shape
    shape = jax.ShapeDtypeStruct
    q_width = inputs["q_down"].shape[1]
    heads_width = inputs["q_up"].shape[1]
    part = inputs["w_gate"].shape[1] // n_f

    def whole(m):
        return (inputs[m].shape[0] * n_f, inputs[m].shape[1])

    in_hbm = ("q_down", "kv_weight", "q_up", "out_proj", "w_gate", "w_up")
    outs = {
        "w_qd": shape(whole("q_down"), BF16),
        "w_kv": shape(whole("kv_weight"), BF16),
        "w_qu": shape(whole("q_up"), BF16),
        "w_out": shape(whole("out_proj"), BF16),
        "gate_full": shape((width, part), BF16),
        "up_full": shape((width, part), BF16),
        "all_kv": shape((tokens * n_ctx, 2 * head_size), BF16),
        "normed": shape((tokens, width), BF16),
        "q_low": shape((tokens, q_width), F32),
        "q_normed": shape((tokens, q_width), BF16),
        "q_rot": shape((tokens, heads_width), BF16),
        "gain_one": shape((1, width), F32),
        "gain_q": shape((1, q_width), F32),
        "gain_two": shape((1, width), F32),
        "tags": shape((n_ctx, 8, 128), F32),
    }
    out_hbm = ("w_qd", "w_kv", "w_qu", "w_out", "gate_full", "up_full", "all_kv")
    box = (inputs["w_gate"].shape[0], 2 * part)
    dma = pltpu.SemaphoreType.DMA
    scratch = {
        "infos": pltpu.VMEM((n_f,) + inputs["info"].shape, F32),
        "qd_full": pltpu.VMEM(whole("q_down"), BF16),
        "kv_full": pltpu.VMEM(whole("kv_weight"), BF16),
        "qu_full": pltpu.VMEM(whole("q_up"), BF16),
        "gate_box": pltpu.VMEM(box, BF16),
        "up_box": pltpu.VMEM(box, BF16),
        "gate_spare": pltpu.VMEM((box[0], part), BF16),
        "up_spare": pltpu.VMEM((box[0], part), BF16),
        "out_spare": pltpu.VMEM(inputs["out_proj"].shape, BF16),
        "kv_rows": pltpu.VMEM((tokens, 2 * head_size), BF16),
        "send_sem": dma((64 + 2 * n_ctx,)),
        "recv_sem": dma((64 + 2 * n_ctx,)),
        "local_sem": dma((16,)),
    }
    vmem = pl.BlockSpec(memory_space=pltpu.VMEM)
    anywhere = pl.BlockSpec(memory_space=pl.ANY)
    names = tuple(inputs) + tuple(outs) + tuple(scratch)
    values = pl.pallas_call(
        functools.partial(front_kernel, n_ctx, n_f, names),
        out_shape=tuple(outs.values()),
        in_specs=[anywhere if m in in_hbm else vmem for m in inputs],
        out_specs=tuple([anywhere if m in out_hbm else vmem for m in outs]),
        scratch_shapes=list(scratch.values()),
        compiler_params=pltpu.CompilerParams(
            collective_id=1, has_side_effects=True, vmem_limit_bytes=48 << 20
        ),
        name="front",
    )(*inputs.values())
    return dict(zip(outs, values, strict=True))


def tiles(total, wide, body):
    whole = total // wide

    @pl.loop(0, whole)
    def _(t):
        body(pl.multiple_of(t * wide, wide), wide)

    if total % wide:
        body(whole * wide, total % wide)


def contract_first(a, b):
    return jnp.dot(a.T, b, preferred_element_type=F32)


def ffn_kernel(n_f, names, *refs):
    r = dict(zip(names, refs, strict=True))
    c_idx = lax.axis_index("ctx")
    f_idx = lax.axis_index("fsdp")
    moves = Sender()
    at_sem = [0]
    core, far = (c_idx, flip(f_idx, 1)), (c_idx, flip(f_idx, 2))
    beside = (flip(c_idx, 1), f_idx)
    y_idx = c_idx % 2

    def send(src, dst, peer):
        i = at_sem[0]
        at_sem[0] += 1
        return moves(src, dst, r["send_sem"].at[i], r["recv_sem"].at[i], peer)

    barrier = pltpu.get_barrier_semaphore()
    for peer in (core, far, (c_idx, flip(f_idx, 3)), beside):
        pl.semaphore_signal(barrier, inc=1, device_id=peer, device_id_type=MESH)
    pl.semaphore_wait(barrier, 4)

    tokens, width = r["normed"].shape
    mine = r["attn_group"].at[pl.ds(pl.multiple_of(f_idx * tokens, tokens), tokens)]
    own_attn = pltpu.make_async_copy(r["attn_cut"].at[f_idx], mine, r["load_sem"].at[3])
    own_attn.start()

    def send_attn(mask):
        return send(r["attn_cut"].at[flip(f_idx, mask)], mine, (c_idx, flip(f_idx, mask)))

    units = r["w_down"].shape[0]
    group, dz = r["group"], r["dz"]
    block = [slice(i * tokens, (i + 1) * tokens) for i in range(4)]
    pair = [slice(0, 2 * tokens), slice(2 * tokens, 4 * tokens)]

    def gather(buf):
        to_core = send(buf.at[block[0]], buf.at[block[1]], core)
        to_far = send(buf.at[block[0]], buf.at[block[2]], far)
        return to_core, to_far

    def gather_far(buf, to_far):
        to_far.wait_recv()
        send(buf.at[block[2]], buf.at[block[3]], core).wait_recv()

    group[block[0], :] = r["normed"][...]
    to_core, to_far = gather(group)
    loads = []
    for i, m in enumerate(("gate", "up", "down")):
        load = pltpu.make_async_copy(r["w_" + m], r["v_" + m], r["load_sem"].at[i])
        load.start()
        loads.append(load)
    loads[0].wait()
    loads[1].wait()

    def hidden_part(rows):
        def one(start, wide):
            at = pl.ds(start, wide)
            both = jnp.concatenate([r["v_gate"][:, at], r["v_up"][:, at]], axis=1)
            out = jnp.dot(group[rows, :], both, preferred_element_type=F32)
            gate, up = out[:, :wide], out[:, wide:]
            r["gate"][rows, at] = gate.astype(BF16)
            r["up"][rows, at] = up.astype(BF16)
            r["hid"][rows, at] = (gate / (1.0 + jnp.exp(-gate)) * up).astype(BF16)

        tiles(units, 128, one)

    to_core.wait_recv()
    hidden_part(pair[0])
    gather_far(group, to_far)
    attn_copies = [send_attn(1), send_attn(2)]
    hidden_part(pair[1])
    loads[2].wait()

    def down_block(i, dest):
        def one(start, wide):
            at = pl.ds(start, wide)
            dest[:, at] = jnp.dot(
                r["hid"][block[i], :], r["v_down"][:, at], preferred_element_type=F32
            ).astype(dest.dtype)

        tiles(width, 256, one)

    def back_block(i, dest):
        def one(start, wide):
            at = pl.ds(start, wide)
            dest[:, at] = (
                contract_last(r["gate"][block[i], :], r["v_gate"][at, :])
                + contract_last(r["up"][block[i], :], r["v_up"][at, :])
            ).astype(dest.dtype)

        tiles(width, 256, one)

    def add_rows(dest, one, two):
        def add(at):
            dest[at, :] = (one[at, :].astype(F32) + two[at, :].astype(F32)).astype(dest.dtype)

        row_loop(tokens, add)

    def far_sum(k, make):
        make(3, r["give"].at[2 * k])
        step = send(r["give"].at[2 * k], r["got"].at[2 * k], core)
        make(2, r["far_sum"])
        step.wait_recv()
        add_rows(r["far_give"].at[k], r["far_sum"], r["got"].at[2 * k])
        return send(r["far_give"].at[k], r["far_got"].at[k], far)

    def near_sum(k, make):
        make(1, r["give"].at[2 * k + 1])
        step = send(r["give"].at[2 * k + 1], r["got"].at[2 * k + 1], core)
        make(0, r["near_sum"])
        return step

    def near_end(k, step):
        step.wait_recv()
        add_rows(r["near_sum"], r["near_sum"], r["got"].at[2 * k + 1])

    far_step = far_sum(0, down_block)
    near_end(0, near_sum(0, down_block))
    far_step.wait_recv()
    r["sq"][...] = jnp.zeros_like(r["sq"])

    def loss_rows(at):
        value = r["resid"][at, :] + r["near_sum"][at, :] + r["far_got"][0, at, :].astype(F32)
        r["result"][at, :] = value.astype(BF16)
        diff = value - r["teacher"][at, :].astype(F32)
        squares = jnp.sum(diff * diff, axis=1, keepdims=True) * r["valid"][at, :]
        r["sq"][:1, :] += jnp.sum(squares, axis=0, keepdims=True)
        grad = diff * r["valid_scale"][at, :1]
        r["grad_resid"][at, :] = grad
        dz[at, :] = grad.astype(BF16)

    row_loop(tokens, loss_rows, step=16)
    to_core, to_far = gather(dz)

    def back_hidden(rows):
        def one(start, wide):
            at = pl.ds(start, wide)
            grad = contract_last(dz[rows, :], r["v_down"][at, :])
            gate = r["gate"][rows, at].astype(F32)
            up = r["up"][rows, at].astype(F32)
            sigma = 1.0 / (1.0 + jnp.exp(-gate))
            r["gate"][rows, at] = (grad * up * sigma * (1.0 + gate * (1.0 - sigma))).astype(BF16)
            r["up"][rows, at] = (grad * (gate * sigma)).astype(BF16)

        tiles(units, 256, one)

    to_core.wait_recv()
    back_hidden(pair[0])
    near_step = near_sum(1, back_block)
    gather_far(dz, to_far)
    saves = []

    def save(src, dst, i):
        copy = pltpu.make_async_copy(src, dst, r["save_sem"].at[i])
        copy.start()
        return copy

    def down_tile(start, wide):
        at = pl.ds(start, wide)
        spot = r["tile"].at[pl.ds(0, wide)]
        spot[...] = contract_first(r["hid"][:, at], dz[...]).astype(BF16)
        save(spot, r["down_part"].at[at], 0).wait()

    tiles(units, 128, down_tile)
    half = units // 2
    give = pl.ds(pl.multiple_of((1 - y_idx) * half, half), half)
    down_step = send(r["down_part"].at[give], r["down_got"], beside)
    attn_copies.append(send_attn(3))
    back_hidden(pair[1])
    far_step = far_sum(1, back_block)
    near_end(1, near_step)

    def gate_tile(start, wide):
        at = pl.ds(start, wide)
        left = group[:, at].T
        for i, m in enumerate(("gate", "up")):
            spot = r["wide_tile"].at[i]
            spot[...] = jnp.dot(left, r[m][...], preferred_element_type=F32).astype(BF16)
            saves.append(save(spot, r[m + "_part"].at[at], 1 + i))
        saves.pop().wait()
        saves.pop().wait()

    tiles(width, 256, gate_tile)
    far_step.wait_recv()
    gain = r["gain_two"][...]
    r["gain_sum"][...] = jnp.zeros_like(r["gain_sum"])

    def norm_rows(at):
        grad = r["near_sum"][at, :] + r["far_got"][1, at, :].astype(F32)
        value = r["resid"][at, :]
        scale = lax.rsqrt(jnp.mean(value * value, axis=-1, keepdims=True) + NORM_EPS)
        r["gain_sum"][...] += jnp.sum(grad * value * scale, axis=0, keepdims=True)
        ge = gain * grad
        inner = jnp.mean(ge * value, axis=-1, keepdims=True)
        total = r["grad_resid"][at, :] + scale * ge - value * (scale * scale * scale) * inner
        r["grad_resid"][at, :] = total
        r["grad_branch"][at, :] = total.astype(BF16)

    row_loop(tokens, norm_rows, step=16)
    for copy in attn_copies + [down_step]:
        copy.wait_recv()
    own_attn.wait()
    moves.finish()


def feed_forward(n_f, inputs):
    tokens, width = inputs["normed"].shape
    units = inputs["w_down"].shape[0]
    shape = jax.ShapeDtypeStruct
    outs = {
        "result": shape((tokens, width), BF16),
        "grad_resid": shape((tokens, width), F32),
        "grad_branch": shape((tokens, width), BF16),
        "down_part": shape((units, width), BF16),
        "down_got": shape((units // 2, width), BF16),
        "gate_part": shape((width, units), BF16),
        "up_part": shape((width, units), BF16),
        "attn_group": shape((tokens * n_f, inputs["attn_cut"].shape[2]), BF16),
        "gain_sum": shape((1, width), F32),
        "sq": shape((8, 128), F32),
    }
    hbm = ("w_gate", "w_up", "w_down", "attn_cut", "attn_group")
    hbm += ("down_part", "down_got", "gate_part", "up_part")
    dma = pltpu.SemaphoreType.DMA
    many = tokens * n_f
    scratch = {
        "v_gate": pltpu.VMEM((width, units), BF16),
        "v_up": pltpu.VMEM((width, units), BF16),
        "v_down": pltpu.VMEM((units, width), BF16),
        "group": pltpu.VMEM((many, width), BF16),
        "dz": pltpu.VMEM((many, width), BF16),
        "gate": pltpu.VMEM((many, units), BF16),
        "up": pltpu.VMEM((many, units), BF16),
        "hid": pltpu.VMEM((many, units), BF16),
        "give": pltpu.VMEM((4, tokens, width), BF16),
        "got": pltpu.VMEM((4, tokens, width), BF16),
        "far_sum": pltpu.VMEM((tokens, width), F32),
        "near_sum": pltpu.VMEM((tokens, width), F32),
        "far_give": pltpu.VMEM((2, tokens, width), BF16),
        "far_got": pltpu.VMEM((2, tokens, width), BF16),
        "tile": pltpu.VMEM((128, width), BF16),
        "wide_tile": pltpu.VMEM((2, 256, units), BF16),
        "send_sem": dma((16,)),
        "recv_sem": dma((16,)),
        "load_sem": dma((4,)),
        "save_sem": dma((3,)),
    }
    vmem = pl.BlockSpec(memory_space=pltpu.VMEM)
    anywhere = pl.BlockSpec(memory_space=pl.ANY)
    names = tuple(inputs) + tuple(outs) + tuple(scratch)
    values = pl.pallas_call(
        functools.partial(ffn_kernel, n_f, names),
        out_shape=tuple(outs.values()),
        in_specs=[anywhere if m in hbm else vmem for m in inputs],
        out_specs=tuple([anywhere if m in hbm else vmem for m in outs]),
        scratch_shapes=list(scratch.values()),
        compiler_params=pltpu.CompilerParams(
            collective_id=2, has_side_effects=True, vmem_limit_bytes=60 << 20
        ),
        name="feed_forward",
    )(*inputs.values())
    return dict(zip(outs, values, strict=True))


def body(
    hidden_in,
    teacher,
    blocks,
    seq_ids,
    valid_mask,
    norm1_gain,
    q_down,
    q_gain,
    q_up,
    kv_weight,
    out_proj,
    norm2_gain,
    w_gate,
    w_up,
    w_down,
):
    row_count, model_width = hidden_in.shape
    head_size = kv_weight.shape[1] // 2
    heads_width = q_up.shape[1]
    head_count = heads_width // head_size
    half_dim = head_size // 2
    q_width = q_down.shape[1]
    n_ctx = lax.axis_size("ctx")
    n_f = lax.axis_size("fsdp")
    n_z = n_ctx // 2
    token_total = row_count * n_ctx * n_f
    seq_pieces = 2 * SEQ_BLOCKS
    c_idx = lax.axis_index("ctx")
    f_idx = lax.axis_index("fsdp")
    y_idx = c_idx % 2
    z_idx = c_idx // 2
    x_idx = f_idx // 2
    k_idx = f_idx % 2

    def by_f(values, mask):
        return lax.ppermute(values, "fsdp", [(i, i ^ mask) for i in range(n_f)])

    def by_c(values, mask):
        return lax.ppermute(values, "ctx", [(i, i ^ mask) for i in range(n_ctx)])

    def cut(values, start, size, axis):
        return lax.dynamic_slice_in_dim(values, start, size, axis)

    def ctx_split(grad):
        view = grad.reshape(n_z, 2, grad.shape[0] // n_ctx, grad.shape[1])
        give = lax.dynamic_index_in_dim(view, 1 - y_idx, 1, keepdims=False)
        keep = lax.dynamic_index_in_dim(view, y_idx, 1, keepdims=False)
        return give, keep

    def ctx_pair(keep, got):
        return (keep.astype(F32) + got.astype(F32)).astype(BF16)

    def ctx_spread(pair):
        return [pair] + [
            by_c(lax.dynamic_index_in_dim(pair, z_idx ^ r, 0, keepdims=False), 2 * r)
            for r in range(1, n_z)
        ]

    def ctx_total(parts):
        total = lax.dynamic_index_in_dim(parts[0], z_idx, 0, keepdims=False).astype(F32)
        for got in parts[1:]:
            total = total + got.astype(F32)
        return total

    def group_rows(values):
        return lax.all_gather(values, "fsdp", axis=0, tiled=True)

    valid_f = valid_mask.astype(F32)
    own_pieces = row_count // PIECE
    info = jnp.concatenate(
        [
            norm1_gain.astype(F32),
            q_gain.astype(F32),
            norm2_gain.astype(F32),
            jnp.full((128,), jnp.sum(valid_f)),
        ]
    )
    info = jnp.pad(info, (0, -info.shape[0] % 1024)).reshape(-1, 128)
    own_tags = jnp.stack([blocks.reshape(-1, PIECE)[:, 0], seq_ids.reshape(-1, PIECE)[:, 0]], 1)
    tag = jnp.pad(own_tags.astype(F32).reshape(1, -1), ((0, 7), (0, 128 - 2 * own_pieces)))
    own = jnp.concatenate([blocks.reshape(-1, PIECE)[:, 0], seq_ids[:1]])

    positions = blocks * PIECE + jnp.arange(row_count, dtype=jnp.int32) % PIECE
    freq_table = 10000.0 ** (-(jnp.arange(half_dim, dtype=F32) * 2.0 / head_size))
    angle_table = positions.astype(F32)[:, None] * freq_table[None, :]
    cosine = jnp.cos(angle_table)
    sine = jnp.sin(angle_table)
    fetched = front(
        n_ctx,
        n_f,
        {
            "q_down": q_down,
            "kv_weight": kv_weight,
            "q_up": q_up,
            "out_proj": out_proj,
            "w_gate": w_gate,
            "w_up": w_up,
            "hidden": hidden_in,
            "info": info,
            "tag": tag,
            "cos": cosine,
            "sin": sine,
        },
        head_size,
    )
    w_out = fetched["w_out"]
    all_kv, q_rot = fetched["all_kv"], fetched["q_rot"]
    normed, q_low, q_normed = fetched["normed"], fetched["q_low"], fetched["q_normed"]
    gain_one, gain_q, gain_two = fetched["gain_one"], fetched["gain_q"], fetched["gain_two"]
    tags = fetched["tags"][:, 0, : 2 * own_pieces].reshape(-1, 2).astype(jnp.int32)
    total_count = jnp.sum(fetched["tags"][:, 1, 0])
    hidden_f = hidden_in.astype(F32)
    scale_q = rms_scale(q_low)

    out_block = heads_width // (n_ctx * n_f)
    if out_block == 128:
        attn_heads, lse, attn_cut = attn_fwd(
            tags, own, q_rot, all_kv, head_size, seq_pieces, n_f, True
        )
    else:
        attn_heads, lse = attn_fwd(tags, own, q_rot, all_kv, head_size, seq_pieces, n_f, False)
        attn_cut = attn_heads.reshape(row_count, n_ctx, n_f, out_block).transpose(2, 0, 1, 3)
        attn_cut = attn_cut.reshape(n_f, row_count, n_ctx * out_block)
    resid = hidden_f + dot(attn_heads, w_out)
    scale_two = rms_scale(resid)
    normed_two = (resid * scale_two * gain_two).astype(BF16)

    wide_valid = jnp.broadcast_to(valid_f[:, None], (row_count, 128))
    ffn = feed_forward(
        n_f,
        {
            "normed": normed_two,
            "resid": resid,
            "teacher": teacher,
            "valid": wide_valid,
            "valid_scale": wide_valid * (token_total / total_count),
            "gain_two": gain_two,
            "w_gate": fetched["gate_full"],
            "w_up": fetched["up_full"],
            "w_down": w_down,
            "attn_cut": attn_cut,
        },
    )
    grad_resid, grad_branch = ffn["grad_resid"], ffn["grad_branch"]
    grad_gain_two = ffn["gain_sum"].reshape(-1)
    sq_local = ffn["sq"][0, 0]
    half_units = w_down.shape[0] // 2
    down_pair = ctx_pair(cut(ffn["down_part"], y_idx * half_units, half_units, 0), ffn["down_got"])
    down_parts = ctx_spread(down_pair.reshape(n_z, -1, model_width))
    gate_give, gate_keep = ctx_split(ffn["gate_part"])
    gate_got = by_c(gate_give, 1)
    early = n_z // 2
    up_blocks = ffn["up_part"].reshape(n_z, 2, model_width // n_ctx, -1)
    up_got = by_c(
        lax.dynamic_index_in_dim(up_blocks[:early], 1 - y_idx, 1, keepdims=False), 1
    )
    branch_group = group_rows(grad_branch)
    grad_attn = dot_t(grad_branch, w_out).astype(BF16)
    grad_qlin, grad_seq = attn_bwd(
        tags, own, q_rot, grad_attn, attn_heads, lse, cosine, sine, all_kv, head_size, seq_pieces
    )
    qlin_group = lax.all_to_all(grad_qlin, "fsdp", 1, 0, tiled=True)

    by_piece = grad_seq.reshape(seq_pieces, PIECE, 2 * head_size)
    piece_tag = tags[:, 0].reshape(n_z, 2, own_pieces)
    piece_own = (tags[:, 1] == seq_ids[0]).reshape(n_z, 2, own_pieces)

    def kv_half(bit):
        places = lax.dynamic_index_in_dim(piece_tag, bit, 1, keepdims=False).reshape(-1)
        picked = by_piece[places]
        if n_ctx * own_pieces != seq_pieces:
            mine = lax.dynamic_index_in_dim(piece_own, bit, 1, keepdims=False).reshape(-1)
            picked = jnp.where(mine[:, None, None], picked, jnp.zeros_like(picked))
        return picked.reshape(n_z, own_pieces * PIECE, 2 * head_size)

    kv_part = jnp.stack([kv_half(0), kv_half(1)], axis=1)
    q_cut, kv_cut = q_width // n_f, 2 * head_size // n_f
    qnorm_group = group_rows(q_normed)
    normed_group = group_rows(normed)

    grad_qnormed = dot_t(grad_qlin, fetched["w_qu"])
    grad_qlow_f, grad_gain_q = rms_back(q_low, scale_q, gain_q, grad_qnormed)
    grad_qlow = grad_qlow_f.astype(BF16)
    down_parts, gate_got, grad_qlow, qlin_group, kv_part, attn_group = together(
        down_parts, gate_got, grad_qlow, qlin_group, kv_part, ffn["attn_group"]
    )
    da_q = dot_t(grad_qlow, fetched["w_qd"])
    gate_pair = ctx_pair(gate_keep, gate_got)
    out_part = dot_rows(attn_group, branch_group).astype(BF16)
    qup_part = dot_rows(qnorm_group, qlin_group).astype(BF16)

    def by_ctx(grad):
        return grad.reshape(n_z, 2, grad.shape[0] // n_ctx, grad.shape[1])

    order = [
        (c * n_f + f, f * n_ctx + c % 2 * n_z + c // 2) for c in range(n_ctx) for f in range(n_f)
    ]
    down_rows = ctx_total(down_parts).astype(BF16)
    down_sent = lax.ppermute(down_rows, ("ctx", "fsdp"), order)

    up_got, out_part, qup_part = together(up_got, out_part, qup_part)

    small = jnp.concatenate(
        [jnp.zeros((model_width,), F32), grad_gain_q, grad_gain_two, sq_local.reshape(1)]
    )
    entries = small.shape[0]
    small = jnp.pad(small, (0, -entries % 1024)).reshape(-1, 128)
    ends = tail_reduce(
        n_ctx,
        n_f,
        {
            "gate": gate_pair,
            "kv": kv_part,
            "up": up_blocks,
            "up_got": up_got,
            "out": by_ctx(out_part),
            "qup": by_ctx(qup_part),
            "dqa": grad_qlow,
            "cos": cosine,
            "sin": sine,
            "normed_group": normed_group,
            "w_kv": fetched["w_kv"],
            "da_q": da_q,
            "hidden": hidden_in,
            "gain_one": gain_one,
            "grad_resid": grad_resid,
            "small": small,
        },
        q_width,
    )
    small, down_sent = together(ends["small_out"], down_sent)
    small = small.reshape(-1)[:entries]
    grad_down = down_sent.astype(F32)

    device = c_idx * n_f + f_idx
    q1, q2 = model_width, model_width + q_width
    n_dev = n_ctx * n_f

    def own_part(values):
        size = values.shape[0] // n_dev
        return cut(values, device * size, size, 0)

    loss_now = small[-1] / (model_width * total_count)
    return (
        ffn["result"],
        loss_now,
        ends["grad_input"],
        own_part(small[:q1]),
        ends["out_qd"],
        own_part(small[q1:q2]),
        ends["out_qup"],
        ends["out_kvw"],
        ends["out_out"],
        own_part(small[q2 : q2 + model_width]),
        ends["out_gate"],
        ends["out_up"],
        grad_down,
    )


def solution(mesh):
    both = ("ctx", "fsdp")
    rows = P(both, None)
    flat = P(both)
    shard = P("fsdp", None)
    gain = P("fsdp")
    return jax.shard_map(
        body,
        mesh=mesh,
        in_specs=(
            rows,
            rows,
            flat,
            flat,
            flat,
            gain,
            shard,
            gain,
            shard,
            shard,
            shard,
            gain,
            shard,
            shard,
            shard,
        ),
        out_specs=(
            rows,
            P(),
            rows,
            flat,
            rows,
            flat,
            rows,
            rows,
            rows,
            flat,
            rows,
            rows,
            rows,
        ),
        check_vma=False,
    )
```

```python
import functools
import math

import jax
import jax.numpy as jnp
from jax import lax
from jax.experimental import pallas as pl
from jax.experimental.pallas import tpu as pltpu
from jax.sharding import PartitionSpec as P

PIECE = 128
SEQ_BLOCKS = 8
NORM_EPS = 1e-05
F32 = jnp.float32
BF16 = jnp.bfloat16
LOG2E = math.log2(math.e)
HEAD_GROUP = 4


def rms_scale(values):
    return lax.rsqrt(jnp.mean(values * values, axis=-1, keepdims=True) + NORM_EPS)


def rms_back(values, scale, gain, grad):
    grad_gain = jnp.sum(grad * values * scale, axis=0)
    ge = gain * grad
    inner = jnp.mean(ge * values, axis=-1, keepdims=True)
    return scale * ge - values * (scale * scale * scale) * inner, grad_gain


def rope_apply(values, cosine, sine):
    half_dim = values.shape[-1] // 2
    one = values[..., :half_dim]
    two = values[..., half_dim:]
    return jnp.concatenate([one * cosine - two * sine, two * cosine + one * sine], axis=-1)


def rope_back(grads, cosine, sine):
    half_dim = grads.shape[-1] // 2
    one = grads[..., :half_dim]
    two = grads[..., half_dim:]
    return jnp.concatenate([one * cosine + two * sine, two * cosine - one * sine], axis=-1)


def together(*values):
    return lax.optimization_barrier(values)


def dot(a, b):
    return jnp.dot(a, b, preferred_element_type=F32)


def dot_t(a, b):
    return lax.dot_general(a, b, (((1,), (1,)), ((), ())), preferred_element_type=F32)


def dot_rows(a, b):
    return lax.dot_general(a, b, (((0,), (0,)), ((), ())), preferred_element_type=F32)


def contract_last(a, b):
    return lax.dot_general(a, b, (((1,), (1,)), ((), ())), preferred_element_type=F32)

def find_pieces(tags_ref, own_ref, pick_ref, total):
    @pl.loop(0, total)
    def _(u):
        @pl.when(tags_ref[u, 1] == own_ref[2])
        def _():
            pick_ref[tags_ref[u, 0]] = u

def stack_heads(ref, hd):
    return jnp.concatenate([ref[:, h*hd:(h+1)*hd] for h in range(HEAD_GROUP)], axis=0)

def attn_fwd_kernel(n_f, tags_ref, own_ref, q_ref, kv_ref, o_ref, lse_ref, *rest):
    k_s, vt_s, acc_s, pick_s = rest[-4:]
    half = pl.program_id(0)
    hd = k_s.shape[1]
    pieces = k_s.shape[0] // PIECE
    total = kv_ref.shape[0] // PIECE
    wide = 2 * PIECE
    coef = hd ** -0.5 * LOG2E

    @pl.when((half == 0) & (pl.program_id(1) == 0))
    def _():
        find_pieces(tags_ref, own_ref, pick_s, total)
        for i in range(pieces):
            rows = pl.ds(pl.multiple_of(pick_s[i] * PIECE, PIECE), PIECE)
            k_s[i*PIECE:(i+1)*PIECE, :] = kv_ref[rows, :hd]
            vt_s[:, i*PIECE:(i+1)*PIECE] = kv_ref[rows, hd:].T

    q = stack_heads(q_ref, hd)
    acc_s[...] = jnp.zeros_like(acc_s)
    rows = q.shape[0]
    def step(i, carry):
        peak, total_p = carry
        at = pl.ds(pl.multiple_of(i * wide, wide), wide)
        raw = contract_last(k_s[at, :], q)
        top = jnp.maximum(peak, jnp.max(raw, axis=0, keepdims=True))
        fade = jnp.exp2((peak - top) * coef)
        p = jnp.exp2((raw - top) * coef)
        acc_s[...] = acc_s[...] * fade + jnp.dot(vt_s[:, at], p.astype(BF16), preferred_element_type=F32)
        return top, total_p * fade + jnp.sum(p, axis=0, keepdims=True)
    count = own_ref[half] // 2 + 1
    peak, total_p = lax.fori_loop(0, count, step, (jnp.full((1, rows), -1e30, F32), jnp.zeros((1, rows), F32)))
    out = (acc_s[...] / total_p).astype(BF16).T
    for h in range(HEAD_GROUP):
        o_ref[:, h*hd:(h+1)*hd] = out[h*PIECE:(h+1)*PIECE, :]
    if len(rest) > 4:
        for b in range(HEAD_GROUP * hd // 128):
            head, part = b * 128 // hd, b * 128 % hd
            rest[0][b % n_f, :, b // n_f * 128:(b // n_f + 1) * 128] = out[
                head*PIECE:(head+1)*PIECE, part:part+128
            ]
    lse_ref[0] = peak * coef + jnp.log2(total_p)

def attn_fwd(tags, own, q, kv, hd, pieces, n_f, cut):
    n_rows, width = q.shape
    groups = width // hd // HEAD_GROUP
    gw = HEAD_GROUP * hd
    halves = n_rows // PIECE
    rows = HEAD_GROUP * PIECE
    blk = pl.BlockSpec((PIECE, gw), lambda p, g, *_: (p, g))
    flops = 4 * n_rows * width * pieces * PIECE * 9 // 16
    shapes = [jax.ShapeDtypeStruct(q.shape, BF16), jax.ShapeDtypeStruct((halves*groups, 1, rows), F32)]
    specs = [blk, pl.BlockSpec((1, 1, rows), lambda p, g, *_: (p*groups+g, 0, 0))]
    if cut:
        shapes.append(jax.ShapeDtypeStruct((n_f, n_rows, width // n_f), BF16))
        specs.append(pl.BlockSpec((n_f, PIECE, gw // n_f), lambda p, g, *_: (0, p, g)))
    return pl.pallas_call(
        functools.partial(attn_fwd_kernel, n_f),
        out_shape=tuple(shapes),
        grid_spec=pltpu.PrefetchScalarGridSpec(
            num_scalar_prefetch=2, grid=(halves, groups),
            in_specs=[blk, pl.BlockSpec(kv.shape, lambda p, g, *_: (0, 0))],
            out_specs=tuple(specs),
            scratch_shapes=[pltpu.VMEM((pieces*PIECE, hd), BF16), pltpu.VMEM((hd, pieces*PIECE), BF16),
                            pltpu.VMEM((hd, rows), F32), pltpu.SMEM((pieces,), jnp.int32)]),
        compiler_params=pltpu.CompilerParams(vmem_limit_bytes=40 << 20),
        cost_estimate=pl.CostEstimate(flops=flops, transcendentals=flops//(4*hd), bytes_accessed=2*(2*q.size+kv.size)),
        name="attn_fwd",
    )(tags, own, q, kv)

def attn_bwd_kernel(tags_ref, own_ref, q_ref, do_ref, o_ref, lse_ref, cos_ref, sin_ref, kv_ref, dq_ref, dkv_ref,
                    k_s, kt_s, v_s, dq_s, dk_s, dv_s, pick_s):
    half = pl.program_id(0)
    group = pl.program_id(1)
    hd = k_s.shape[1]
    pieces = k_s.shape[0] // PIECE
    total = kv_ref.shape[0] // PIECE
    wide = 2 * PIECE
    coef = hd ** -0.5 * LOG2E
    scale = hd ** -0.5

    @pl.when((half == 0) & (group == 0))
    def _():
        find_pieces(tags_ref, own_ref, pick_s, total)
        for i in range(pieces):
            rows = pl.ds(pl.multiple_of(pick_s[i] * PIECE, PIECE), PIECE)
            keys = kv_ref[rows, :hd]
            k_s[i*PIECE:(i+1)*PIECE, :] = keys
            kt_s[:, i*PIECE:(i+1)*PIECE] = keys.T
            v_s[i*PIECE:(i+1)*PIECE, :] = kv_ref[rows, hd:]
        dk_s[...] = jnp.zeros_like(dk_s)
        dv_s[...] = jnp.zeros_like(dv_s)

    q = stack_heads(q_ref, hd)
    do = stack_heads(do_ref, hd)
    prod = do.astype(F32) * stack_heads(o_ref, hd).astype(F32)
    delta = lax.dot_general(jnp.ones((8, hd), F32), prod, (((1,), (1,)), ((), ())),
                            preferred_element_type=F32, precision=lax.Precision.HIGHEST)[:1]
    lse = lse_ref[0]
    dq_s[...] = jnp.zeros_like(dq_s)
    def step(i, carry):
        at = pl.ds(pl.multiple_of(i * wide, wide), wide)
        p = jnp.exp2(contract_last(k_s[at, :], q) * coef - lse)
        dp = contract_last(v_s[at, :], do)
        ds = (p * (dp - delta)).astype(BF16)
        dv_s[at, :] += jnp.dot(p.astype(BF16), do, preferred_element_type=F32)
        dk_s[at, :] += jnp.dot(ds, q, preferred_element_type=F32)
        dq_s[...] += jnp.dot(kt_s[:, at], ds, preferred_element_type=F32)
        return carry
    lax.fori_loop(0, own_ref[half] // 2 + 1, step, 0)
    dq = (dq_s[...] * scale).T
    cos, sin = cos_ref[...], sin_ref[...]
    mid = hd // 2
    for h in range(HEAD_GROUP):
        one = dq[h*PIECE:(h+1)*PIECE, :mid]
        two = dq[h*PIECE:(h+1)*PIECE, mid:]
        dq_ref[:, h*hd:h*hd+mid] = (one * cos + two * sin).astype(BF16)
        dq_ref[:, h*hd+mid:(h+1)*hd] = (two * cos - one * sin).astype(BF16)

    @pl.when((half == pl.num_programs(0) - 1) & (group == pl.num_programs(1) - 1))
    def _():
        dkv_ref[:, :hd] = (dk_s[...] * scale).astype(BF16)
        dkv_ref[:, hd:] = dv_s[...].astype(BF16)

def attn_bwd(tags, own, q, do, o, lse, cos, sin, kv, hd, pieces):
    n_rows, width = q.shape
    groups = width // hd // HEAD_GROUP
    gw = HEAD_GROUP * hd
    halves = n_rows // PIECE
    rows = HEAD_GROUP * PIECE
    blk = pl.BlockSpec((PIECE, gw), lambda p, g, *_: (p, g))
    trig = pl.BlockSpec((PIECE, hd // 2), lambda p, g, *_: (p, 0))
    keys = pieces * PIECE
    return pl.pallas_call(
        attn_bwd_kernel,
        out_shape=(jax.ShapeDtypeStruct(q.shape, BF16), jax.ShapeDtypeStruct((keys, 2*hd), BF16)),
        grid_spec=pltpu.PrefetchScalarGridSpec(
            num_scalar_prefetch=2, grid=(halves, groups),
            in_specs=[blk, blk, blk, pl.BlockSpec((1, 1, rows), lambda p, g, *_: (p*groups+g, 0, 0)), trig, trig,
                      pl.BlockSpec(kv.shape, lambda p, g, *_: (0, 0))],
            out_specs=[blk, pl.BlockSpec((keys, 2*hd), lambda p, g, *_: (0, 0))],
            scratch_shapes=[pltpu.VMEM((keys, hd), BF16), pltpu.VMEM((hd, keys), BF16), pltpu.VMEM((keys, hd), BF16),
                            pltpu.VMEM((hd, rows), F32), pltpu.VMEM((keys, hd), F32), pltpu.VMEM((keys, hd), F32),
                            pltpu.SMEM((pieces,), jnp.int32)]),
        compiler_params=pltpu.CompilerParams(vmem_limit_bytes=48 << 20),
        name="attn_bwd",
    )(tags, own, q, do, o, lse, cos, sin, kv)

MESH = pl.DeviceIdType.MESH


def flip(index, mask):
    out = 0
    bit = 1
    while bit <= mask:
        part = (index // bit) % 2
        out = out + bit * ((1 - part) if mask & bit else part)
        bit *= 2
    return out + (index // bit) * bit


def row_loop(rows, body, step=32):
    if rows % step:
        step = 16

    @pl.loop(0, rows // step)
    def _(i):
        body(pl.ds(pl.multiple_of(i * step, step), step))


class Sender:
    def __init__(self):
        self.open = []

    def make(self, src, dst, send_sem, recv_sem, peer):
        return pltpu.make_async_remote_copy(
            src_ref=src,
            dst_ref=dst,
            send_sem=send_sem,
            recv_sem=recv_sem,
            device_id=peer,
            device_id_type=MESH,
        )

    def __call__(self, *args):
        copy = self.make(*args)
        copy.start()
        self.open.append(copy)
        return copy

    def finish(self):
        for copy in self.open:
            copy.wait_send()


class LineSum:
    def __init__(self, own, got, send_sem, recv_sem, c_idx, f_idx, n_z, sender):
        self.own, self.got, self.send_sem, self.recv_sem = own, got, send_sem, recv_sem
        self.n_z, self.sender = n_z, sender
        self.z = c_idx // 2
        self.left = (c_idx - 2, f_idx)
        self.right = (c_idx + 2, f_idx)

    def copy(self, b, slot, peer):
        return self.sender.make(
            self.own.at[b], self.got.at[slot], self.send_sem.at[b], self.recv_sem.at[slot], peer
        )

    def take(self, b, slot):
        self.copy(b, slot, self.left).wait_recv()

        def add(at):
            self.own[b, at, :] = (
                self.own[b, at, :].astype(F32) + self.got[slot, at, :].astype(F32)
            ).astype(BF16)

        row_loop(self.own.shape[1], add)

    def go_right(self, b):
        z = self.z

        @pl.when(z < b)
        def _():
            @pl.when(z > 0)
            def _():
                self.take(b, b)

            self.copy(b, b, self.right).start()

    def go_left(self, b):
        z, n_z = self.z, self.n_z

        @pl.when(z > b)
        def _():
            @pl.when(z < n_z - 1)
            def _():
                self.take(b, b)

            @pl.when(z - 1 > b)
            def _():
                self.copy(b, b, self.left).start()

            @pl.when(z - 1 == b)
            def _():
                self.copy(b, n_z, self.left).start()

    def step(self, i):
        @pl.when(2 * self.z < self.n_z)
        def _():
            self.go_right(self.n_z - 1 - i)
            self.go_left(i)

        @pl.when(2 * self.z >= self.n_z)
        def _():
            self.go_left(i)
            self.go_right(self.n_z - 1 - i)

    def total(self, store):
        z, n_z = self.z, self.n_z

        @pl.when(z > 0)
        def _():
            self.copy(z, z, self.left).wait_recv()

        @pl.when(z < n_z - 1)
        def _():
            self.copy(z, n_z, self.left).wait_recv()

        rows = self.own.shape[1]

        @pl.when(z == 0)
        def _():
            row_loop(
                rows,
                lambda at: store(
                    at, self.own[z, at, :].astype(F32) + self.got[n_z, at, :].astype(F32)
                ),
            )

        @pl.when(z == n_z - 1)
        def _():
            row_loop(
                rows,
                lambda at: store(
                    at, self.own[z, at, :].astype(F32) + self.got[z, at, :].astype(F32)
                ),
            )

        @pl.when((z > 0) & (z < n_z - 1))
        def _():
            row_loop(
                rows,
                lambda at: store(
                    at,
                    self.own[z, at, :].astype(F32)
                    + self.got[z, at, :].astype(F32)
                    + self.got[n_z, at, :].astype(F32),
                ),
            )

    def finish(self):
        for b in range(self.n_z):

            @pl.when(self.z != b)
            def _(b=b):
                self.copy(b, b, self.left).wait_send()


WINDOW = 3
TAIL_NAMES = ("kv", "up", "out", "qup", "low")
TAIL_CUT = ("up", "qup", "low")
TAIL_SENT = ("kv", "up", "out", "qup", "low")


def tail_kernel(n_ctx, n_f, names_in, names_out, names_scratch, *refs):
    n_z = n_ctx // 2
    names = list(names_in) + list(names_out) + list(names_scratch)
    r = dict(zip(names, refs, strict=True))
    c_idx = lax.axis_index("ctx")
    f_idx = lax.axis_index("fsdp")
    y_idx = c_idx % 2
    z_idx = c_idx // 2
    send = Sender()

    def over_c(mask):
        return (flip(c_idx, mask), f_idx)

    def over_f(mask):
        return (c_idx, flip(f_idx, mask))

    barrier = pltpu.get_barrier_semaphore()
    for mask in range(1, n_f):
        pl.semaphore_signal(barrier, inc=1, device_id=over_f(mask), device_id_type=MESH)
    for mask in range(1, n_ctx):
        pl.semaphore_signal(barrier, inc=1, device_id=over_c(mask), device_id_type=MESH)
    pl.semaphore_wait(barrier, n_f - 1 + n_ctx - 1)

    lines = {
        m: LineSum(
            r["pair_" + m],
            r["z_" + m],
            r["z_send"].at[i],
            r["z_recv"].at[i],
            c_idx,
            f_idx,
            n_z,
            send,
        )
        for i, m in enumerate(TAIL_NAMES)
    }
    y_copies, keeps = {}, {}
    early = r["up_got"].shape[0]

    parts = {m: r[m] for m in ("kv", "up", "out", "qup")}
    parts["low"] = r["part_low"]
    queue = [
        (m, b) for m in TAIL_SENT for b in range(n_z) if m != "up" or b >= early
    ]
    owed = tuple(queue)

    def next_y():
        if queue:
            m, b = queue.pop(0)
            i = TAIL_SENT.index(m)
            y_copies[m, b] = send(
                parts[m].at[b, 1 - y_idx],
                r["y_" + m].at[b],
                r["y_send"].at[i, b],
                r["y_recv"].at[i, b],
                over_c(1),
            )
            take_own(m, b)

    def take_own(m, b):
        keep = pltpu.make_async_copy(
            parts[m].at[b, y_idx],
            r["pair_" + m].at[b],
            r["keep_sem"].at[TAIL_SENT.index(m), b],
        )
        keep.start()
        keeps[m, b] = keep

    def add_pair(m, b):
        y_copies[m, b].wait_recv()
        next_y()
        add_ready(m, b)

    def add_ready(m, b):
        keeps[m, b].wait()
        pair, got = r["pair_" + m], r["y_" + m]

        def add(at):
            pair[b, at, :] = (pair[b, at, :].astype(F32) + got[b, at, :].astype(F32)).astype(BF16)

        row_loop(pair.shape[1], add)

    def advance(pair, line):
        if pair == "up":
            here.wait()
            for b in range(early):
                add_ready(pair, b)
        for b in range(n_z):
            if pair is not None and (pair, b) in owed:
                add_pair(pair, b)
            if line is not None and b < n_z - 1:
                lines[line].step(b)

    f_copies = {}

    def finish_sum(m):
        lines[m].total(lambda at, value: store_total(m, at, value))
        if m in TAIL_CUT:
            i = TAIL_CUT.index(m)
            part = r["tot_" + m].shape[0] // n_f
            for s in range(1, n_f):
                at = pl.ds(pl.multiple_of(flip(f_idx, s) * part, part), part)
                f_copies[m, s] = send(
                    r["tot_" + m].at[at, :],
                    r["f_" + m].at[s - 1],
                    r["f_send"].at[i, s - 1],
                    r["f_recv"].at[i, s - 1],
                    over_f(s),
                )

    def store_total(m, at, value):
        if m in TAIL_CUT:
            r["tot_" + m][at, :] = value.astype(BF16)
        else:
            r["out_" + m][at, :] = value

    def put_out(m):
        total = r["tot_" + m]
        rows, width = total.shape
        part = rows // n_f
        cuts = {"out_" + m: (0, width)}
        if m == "low":
            split = r["qd_group"].shape[1]
            cuts = {"out_qd": (0, split), "out_kvw": (split, width - split)}
        for s in range(n_f):
            source = flip(f_idx, s)
            if s:
                f_copies[m, s].wait_recv()
                got = r["f_" + m].at[s - 1]
            else:
                got = total.at[pl.ds(pl.multiple_of(f_idx * part, part), part)]
            for name, (start, wide) in cuts.items():
                at = pl.ds(pl.multiple_of(source * wide, 128), wide)
                r[name][:, at] = got[:, start : start + wide].astype(F32)

    def cut_low(src, dst, width, index):
        rows = src.shape[0]
        mine = pl.ds(pl.multiple_of(f_idx * rows, rows), rows)
        copies = []
        for s in range(1, n_f):
            at = pl.ds(pl.multiple_of(flip(f_idx, s) * width, 128), width)
            copies.append(
                send(
                    src.at[:, at],
                    dst.at[mine, :],
                    r["low_send"].at[index, s - 1],
                    r["low_recv"].at[index, s - 1],
                    over_f(s),
                )
            )
        own = pl.ds(pl.multiple_of(f_idx * width, 128), width)
        dst[mine, :] = src[:, own]
        return copies

    for _ in range(WINDOW):
        next_y()
    q_copies = cut_low(r["dqa"], r["qd_group"], r["qd_group"].shape[1], 0)
    here = pltpu.make_async_copy(
        r["up_got"], r["y_up"].at[pl.ds(0, early)], r["keep_sem"].at[1, n_z]
    )
    here.start()
    for b in range(early):
        take_own("up", b)
    advance("up", None)
    advance("kv", "up")
    advance(None, "kv")

    head = r["dkv"].shape[1] // 2
    mid = head // 2

    def store_kv(at, value):
        cos, sin = r["cos"][at, :], r["sin"][at, :]
        one, two = value[:, :mid], value[:, mid:head]
        r["dkv"][at, :mid] = (one * cos + two * sin).astype(BF16)
        r["dkv"][at, mid:head] = (two * cos - one * sin).astype(BF16)
        r["dkv"][at, head:] = value[:, head:].astype(BF16)

    lines["kv"].total(store_kv)
    kv_copies = cut_low(r["dkv"], r["kv_group"], r["kv_group"].shape[1], 1)

    def low_part(group, start):
        normed, part = r["normed_group"], r["part_low"]
        rows = part.shape[2]
        for c in range(n_ctx):
            part[c // 2, c % 2, :, start : start + group.shape[1]] = lax.dot_general(
                normed[:, c * rows : (c + 1) * rows],
                group[...],
                (((0,), (0,)), ((), ())),
                preferred_element_type=F32,
            ).astype(BF16)

    for copy in q_copies:
        copy.wait_recv()
    low_part(r["qd_group"], 0)
    advance("out", None)
    for copy in kv_copies:
        copy.wait_recv()
    low_part(r["kv_group"], r["qd_group"].shape[1])

    grad_in, w_kv = r["grad_input"], r["w_kv"]
    width = grad_in.shape[1]
    tile = 256

    @pl.loop(0, width // tile)
    def _(t):
        at = pl.ds(pl.multiple_of(t * tile, tile), tile)
        grad_in[:, at] = r["da_q"][:, at] + lax.dot_general(
            r["dkv"][...],
            w_kv[at, :],
            (((1,), (1,)), ((), ())),
            preferred_element_type=F32,
        )

    r["gain_sum"][...] = jnp.zeros_like(r["gain_sum"])
    gain = r["gain_one"][...]

    def norm_rows(at):
        value = r["hidden"][at, :].astype(F32)
        grad = grad_in[at, :]
        scale = lax.rsqrt(jnp.mean(value * value, axis=-1, keepdims=True) + NORM_EPS)
        r["gain_sum"][...] += jnp.sum(grad * value * scale, axis=0, keepdims=True)
        ge = gain * grad
        inner = jnp.mean(ge * value, axis=-1, keepdims=True)
        grad_in[at, :] = (
            r["grad_resid"][at, :] + scale * ge - value * (scale * scale * scale) * inner
        )

    row_loop(grad_in.shape[0], norm_rows, step=16)

    small, small_got = r["small_out"], r["small_got"]
    small[...] = r["small"][...]
    for i in range(width // 128):
        small[i : i + 1, :] = r["gain_sum"][:, i * 128 : (i + 1) * 128]
    steps = [over_f(1), over_f(2), over_c(1)]
    mask = 2
    while mask < n_ctx:
        steps.append(over_c(mask))
        mask *= 2
    small_copies = {}

    def small_start(s):
        small_got[s, 0] = small[...]
        small_copies[s] = send(
            small_got.at[s, 0],
            small_got.at[s, 1],
            r["s_send"].at[s],
            r["s_recv"].at[s],
            steps[s],
        )

    def small_end(s):
        small_copies[s].wait_recv()
        small[...] = small[...] + small_got[s, 1]

    for s in range(2):
        small_start(s)
        small_end(s)
    small_start(2)

    advance("qup", "out")
    finish_sum("up")
    advance("low", "qup")
    finish_sum("out")
    small_end(2)
    small_start(3)
    put_out("up")
    finish_sum("qup")
    advance(None, "low")
    for s in range(3, len(steps)):
        if s > 3:
            small_start(s)
        small_end(s)
    finish_sum("low")
    put_out("qup")
    put_out("low")
    send.finish()
    for m in TAIL_NAMES:
        lines[m].finish()


def tail_reduce(n_ctx, n_f, inputs, q_width):
    n_z = n_ctx // 2
    vmem = pl.BlockSpec(memory_space=pltpu.VMEM)
    anywhere = pl.BlockSpec(memory_space=pl.ANY)
    rows, width = inputs["hidden"].shape
    kv_width = inputs["w_kv"].shape[1]
    in_hbm = ("kv", "up", "up_got", "out", "qup")
    names_in = tuple(inputs)
    in_specs = [anywhere if m in in_hbm else vmem for m in names_in]
    block = {m: inputs[m].shape[-2:] for m in in_hbm}
    cut_q, cut_kv, high = q_width // n_f, kv_width // n_f, width // n_ctx
    block["low"] = (high, cut_q + cut_kv)
    outs = {
        "small_out": jax.ShapeDtypeStruct(inputs["small"].shape, F32),
        "grad_input": jax.ShapeDtypeStruct((rows, width), F32),
        "out_qd": jax.ShapeDtypeStruct((high // n_f, q_width), F32),
        "out_kvw": jax.ShapeDtypeStruct((high // n_f, kv_width), F32),
    }
    scratch = {}
    for m in TAIL_NAMES:
        high, wide = block[m]
        scratch["pair_" + m] = pltpu.VMEM((n_z, high, wide), BF16)
        scratch["z_" + m] = pltpu.VMEM((n_z + 1, high, wide), BF16)
        if m in TAIL_SENT:
            scratch["y_" + m] = pltpu.VMEM((n_z, high, wide), BF16)
        if m in TAIL_CUT:
            scratch["tot_" + m] = pltpu.VMEM((high, wide), BF16)
            scratch["f_" + m] = pltpu.VMEM((n_f - 1, high // n_f, wide), BF16)
            if m != "low":
                outs["out_" + m] = jax.ShapeDtypeStruct((high // n_f, wide * n_f), F32)
        elif m != "kv":
            outs["out_" + m] = jax.ShapeDtypeStruct((high, wide), F32)
    scratch["dkv"] = pltpu.VMEM((rows, kv_width), BF16)
    scratch["qd_group"] = pltpu.VMEM((rows * n_f, q_width // n_f), BF16)
    scratch["kv_group"] = pltpu.VMEM((rows * n_f, kv_width // n_f), BF16)
    scratch["part_low"] = pltpu.VMEM((n_z, 2) + block["low"], BF16)
    scratch["gain_sum"] = pltpu.VMEM((1, width), F32)
    steps = 2 + (n_ctx.bit_length() - 1)
    scratch["small_got"] = pltpu.VMEM((steps, 2) + inputs["small"].shape, F32)
    dma = pltpu.SemaphoreType.DMA
    sent, cut = len(TAIL_SENT), len(TAIL_CUT)
    scratch["s_send"] = dma((steps,))
    scratch["s_recv"] = dma((steps,))
    scratch["y_send"] = dma((sent, n_z))
    scratch["y_recv"] = dma((sent, n_z))
    scratch["keep_sem"] = dma((sent, n_z + 1))
    scratch["z_send"] = dma((len(TAIL_NAMES), n_z))
    scratch["z_recv"] = dma((len(TAIL_NAMES), n_z + 1))
    scratch["f_send"] = dma((cut, n_f - 1))
    scratch["f_recv"] = dma((cut, n_f - 1))
    scratch["low_send"] = dma((2, n_f - 1))
    scratch["low_recv"] = dma((2, n_f - 1))
    values = pl.pallas_call(
        functools.partial(tail_kernel, n_ctx, n_f, names_in, tuple(outs), tuple(scratch)),
        out_shape=tuple(outs.values()),
        in_specs=in_specs,
        out_specs=tuple([vmem] * len(outs)),
        scratch_shapes=list(scratch.values()),
        compiler_params=pltpu.CompilerParams(
            collective_id=0, has_side_effects=True, vmem_limit_bytes=60 << 20
        ),
        name="tail_reduce",
    )(*inputs.values())
    return dict(zip(outs, values, strict=True))


def front_kernel(n_ctx, n_f, names, *refs):
    r = dict(zip(names, refs, strict=True))
    n_z = n_ctx // 2
    c_idx = lax.axis_index("ctx")
    f_idx = lax.axis_index("fsdp")
    y_idx = c_idx % 2
    z_bit = (c_idx // 2) % 2
    x_idx = f_idx // 2
    k_idx = f_idx % 2
    far_idx = flip(f_idx, 2)
    moves = Sender()
    local = []
    at_sem = [0]

    def over_c(mask):
        return (flip(c_idx, mask), f_idx)

    def over_f(mask):
        return (c_idx, flip(f_idx, mask))

    def send(src, dst, peer):
        i = at_sem[0]
        at_sem[0] += 1
        return moves(src, dst, r["send_sem"].at[i], r["recv_sem"].at[i], peer)

    def keep(src, dst):
        copy = pltpu.make_async_copy(src, dst, r["local_sem"].at[len(local)])
        copy.start()
        local.append(copy)
        return copy

    def rows(start, size):
        return pl.ds(pl.multiple_of(start, size), size)

    barrier = pltpu.get_barrier_semaphore()
    for mask in range(1, n_f):
        pl.semaphore_signal(barrier, inc=1, device_id=over_f(mask), device_id_type=MESH)
    for mask in range(1, n_ctx):
        pl.semaphore_signal(barrier, inc=1, device_id=over_c(mask), device_id_type=MESH)
    pl.semaphore_wait(barrier, n_f - 1 + n_ctx - 1)

    infos, tags = r["infos"], r["tags"]
    infos[f_idx] = r["info"][...]
    info_copies = [
        send(infos.at[f_idx], infos.at[f_idx], over_f(mask)) for mask in range(1, n_f)
    ]

    class Rows:
        def __init__(self, shard, dest, bit, hop, chunks):
            self.dest, self.bit, self.hop = dest, bit, hop
            self.shard = shard
            self.size = shard.shape[0]
            self.half = self.size // 2
            self.step = self.half // chunks
            self.chunks = chunks
            self.far, self.next, self.cross = [], [], []

        def start(self, spare=None):
            mine = self.dest.at[rows(f_idx * self.size, self.size)]
            if spare is None:
                self.kept = keep(self.shard, mine)
            else:
                self.spare, self.kept = spare, keep(self.shard, spare)
            self.cross.append(send(self.shard, mine, over_f(1)))

        def settle(self):
            self.kept.wait()
            keep(self.spare, self.dest.at[rows(f_idx * self.size, self.size)])

        def reach(self, i):
            part = self.bit * self.half + i * self.step
            self.far.append(
                send(
                    self.shard.at[rows(part, self.step)],
                    self.dest.at[rows(f_idx * self.size + part, self.step)],
                    over_f(2),
                )
            )

        def place(self, bit, i):
            return self.dest.at[rows(far_idx * self.size + bit * self.half + i * self.step, self.step)]

        def hop_on(self, i):
            self.far[i].wait_recv()
            reach_next()
            here = self.place(self.bit, i)
            self.next.append(send(here, here, over_c(self.hop)))
            self.cross.append(send(here, here, over_f(1)))

        def pass_on(self, i):
            self.next[i].wait_recv()
            here = self.place(1 - self.bit, i)
            self.cross.append(send(here, here, over_f(1)))

        def end(self):
            for copy in self.cross:
                copy.wait_recv()

    class Columns:
        def __init__(self, shard, dest, box, bits, hops):
            self.shard, self.dest, self.box = shard, dest, box
            self.bits, self.hops = bits, hops
            self.size = shard.shape[0]
            self.width = dest.shape[1]
            self.quarter = self.size // 4

        def columns(self, start, count=1):
            return pl.ds(pl.multiple_of(start * self.width, 128), count * self.width)

        def start(self, spare):
            mine = self.dest.at[rows(f_idx * self.size, self.size)]
            self.spare, self.kept = spare, keep(self.shard.at[:, self.columns(f_idx)], spare)
            self.cross = [send(self.shard.at[:, self.columns(flip(f_idx, 1))], mine, over_f(1))]

        def settle(self):
            self.kept.wait()
            keep(self.spare, self.dest.at[rows(f_idx * self.size, self.size)])

        def reach(self, i):
            one, two = self.bits
            at = rows((two * 2 + one) * self.quarter, self.quarter)
            self.far = send(
                self.shard.at[at, self.columns((1 - x_idx) * 2, 2)], self.box.at[at], over_f(2)
            )

        def piece(self, one, two):
            return self.box.at[rows((two * 2 + one) * self.quarter, self.quarter)]

        def first(self):
            one, two = self.bits
            self.far.wait_recv()
            reach_next()
            here = self.piece(one, two)
            self.step = send(here, here, over_c(self.hops[0]))
            self.last = [send(here, here, over_c(self.hops[1]))]

        def second(self):
            one, two = self.bits
            self.step.wait_recv()
            here = self.piece(1 - one, two)
            self.last.append(send(here, here, over_c(self.hops[1])))

        def part(self):
            for copy in self.last:
                copy.wait_recv()
            there = self.dest.at[rows(far_idx * self.size, self.size)]
            self.cross.append(send(self.box.at[:, self.columns(1 - k_idx)], there, over_f(1)))
            keep(self.box.at[:, self.columns(k_idx)], there)

        def end(self):
            for copy in self.cross:
                copy.wait_recv()

    kv = Rows(r["kv_weight"], r["kv_full"], y_idx, 1, 1)
    qd = Rows(r["q_down"], r["qd_full"], y_idx, 1, 1)
    qu = Rows(r["q_up"], r["qu_full"], y_idx, 1, 2)
    out = Rows(r["out_proj"], r["w_out"], z_bit, 2, 4)
    gate = Columns(r["w_gate"], r["gate_full"], r["gate_box"], (y_idx, z_bit), (1, 2))
    up = Columns(r["w_up"], r["up_full"], r["up_box"], (z_bit, y_idx), (2, 1))
    queue = [(kv, 0), (qd, 0), (qu, 0), (qu, 1), (gate, 0), (up, 0)]
    queue += [(out, i) for i in range(out.chunks)]

    def reach_next():
        if queue:
            part, i = queue.pop(0)
            part.reach(i)

    reach_next()
    reach_next()
    kv.start()
    qd.start()

    for copy in info_copies:
        copy.wait_recv()
    d1 = r["gain_one"].shape[1] // n_f // 128
    d2 = r["gain_q"].shape[1] // n_f // 128
    count = infos[0, 2 * d1 + d2 : 2 * d1 + d2 + 1, :]
    for f in range(n_f):
        for i in range(d1):
            col = slice((f * d1 + i) * 128, (f * d1 + i + 1) * 128)
            r["gain_one"][:, col] = infos[f, i : i + 1, :]
            r["gain_two"][:, col] = infos[f, d1 + d2 + i : d1 + d2 + i + 1, :]
        for i in range(d2):
            col = slice((f * d2 + i) * 128, (f * d2 + i + 1) * 128)
            r["gain_q"][:, col] = infos[f, d1 + i : d1 + i + 1, :]
        if f:
            count = count + infos[f, 2 * d1 + d2 : 2 * d1 + d2 + 1, :]
    tags[c_idx] = r["tag"][...]
    tags[c_idx, 1:2, :] = count
    tag_copies = [send(tags.at[c_idx], tags.at[c_idx], over_c(mask)) for mask in range(1, n_ctx)]

    normed = r["normed"]
    gain_one = r["gain_one"][...]

    def norm_rows(at):
        value = r["hidden"][at, :].astype(F32)
        scale = lax.rsqrt(jnp.mean(value * value, axis=-1, keepdims=True) + NORM_EPS)
        normed[at, :] = (value * scale * gain_one).astype(BF16)

    row_loop(normed.shape[0], norm_rows, step=16)

    kv.hop_on(0)
    qd.hop_on(0)
    qu.start()
    kv.pass_on(0)
    qd.pass_on(0)
    kv.end()
    kv.kept.wait()
    head = r["kv_full"].shape[1] // 2
    mid = head // 2
    cos, sin = r["cos"], r["sin"]
    kv_rows = r["kv_rows"]
    keys = jnp.dot(normed[...], r["kv_full"][:, :head], preferred_element_type=F32)
    one, two = keys[:, :mid], keys[:, mid:]
    kv_rows[:, :mid] = (one * cos[...] - two * sin[...]).astype(BF16)
    kv_rows[:, mid:head] = (two * cos[...] + one * sin[...]).astype(BF16)
    kv_rows[:, head:] = jnp.dot(
        normed[...], r["kv_full"][:, head:], preferred_element_type=F32
    ).astype(BF16)
    all_kv = r["all_kv"]
    tokens = normed.shape[0]

    def kv_place(c):
        return all_kv.at[rows(c * tokens, tokens)]

    kv_z = [send(kv_rows, kv_place(c_idx), over_c(2 * s)) for s in range(1, n_z)]
    kv_y = [send(kv_rows, kv_place(c_idx), over_c(1))]
    keep(kv_rows, kv_place(c_idx))
    qu.hop_on(0)
    qd.end()
    qd.kept.wait()

    @pl.loop(0, r["q_low"].shape[1] // 256)
    def _(t):
        at = pl.ds(pl.multiple_of(t * 256, 256), 256)
        r["q_low"][:, at] = jnp.dot(
            normed[...], r["qd_full"][:, at], preferred_element_type=F32
        )

    gain_q = r["gain_q"][...]

    def norm_low(at):
        value = r["q_low"][at, :]
        scale = lax.rsqrt(jnp.mean(value * value, axis=-1, keepdims=True) + NORM_EPS)
        r["q_normed"][at, :] = (value * scale * gain_q).astype(BF16)

    row_loop(tokens, norm_low, step=16)
    qu.hop_on(1)
    for s in range(1, n_z):
        kv_z[s - 1].wait_recv()
        here = kv_place(flip(c_idx, 2 * s))
        kv_y.append(send(here, here, over_c(1)))
    qu.pass_on(0)
    qu.pass_on(1)
    gate.first()
    qu.end()
    for m, part in (("gate", gate), ("up", up), ("out", out)):
        part.start(r[m + "_spare"])
    qu.kept.wait()

    @pl.loop(0, r["q_rot"].shape[1] // head)
    def _(h):
        start = pl.multiple_of(h * head, head)
        value = jnp.dot(
            r["q_normed"][...],
            r["qu_full"][:, pl.ds(start, head)],
            preferred_element_type=F32,
        )
        one, two = value[:, :mid], value[:, mid:]
        r["q_rot"][:, pl.ds(start, mid)] = (one * cos[...] - two * sin[...]).astype(BF16)
        late = pl.multiple_of(h * head + mid, mid)
        r["q_rot"][:, pl.ds(late, mid)] = (two * cos[...] + one * sin[...]).astype(BF16)

    up.first()
    for part in (gate, up, out):
        part.settle()
    for m in ("kv", "qd", "qu"):
        keep(r[m + "_full"], r["w_" + m])
    gate.second()
    out.hop_on(0)
    up.second()
    for i in range(1, out.chunks):
        out.hop_on(i)
    gate.part()
    for i in range(out.chunks):
        out.pass_on(i)
    up.part()
    for copy in kv_y + tag_copies:
        copy.wait_recv()
    for part in (gate, up, out):
        part.end()
    for copy in local:
        if not any(copy is part.kept for part in (kv, qd, qu, gate, up, out)):
            copy.wait()
    moves.finish()


def front(n_ctx, n_f, inputs, head_size):
    tokens, width = inputs["hidden"].shape
    shape = jax.ShapeDtypeStruct
    q_width = inputs["q_down"].shape[1]
    heads_width = inputs["q_up"].shape[1]
    part = inputs["w_gate"].shape[1] // n_f

    def whole(m):
        return (inputs[m].shape[0] * n_f, inputs[m].shape[1])

    in_hbm = ("q_down", "kv_weight", "q_up", "out_proj", "w_gate", "w_up")
    outs = {
        "w_qd": shape(whole("q_down"), BF16),
        "w_kv": shape(whole("kv_weight"), BF16),
        "w_qu": shape(whole("q_up"), BF16),
        "w_out": shape(whole("out_proj"), BF16),
        "gate_full": shape((width, part), BF16),
        "up_full": shape((width, part), BF16),
        "all_kv": shape((tokens * n_ctx, 2 * head_size), BF16),
        "normed": shape((tokens, width), BF16),
        "q_low": shape((tokens, q_width), F32),
        "q_normed": shape((tokens, q_width), BF16),
        "q_rot": shape((tokens, heads_width), BF16),
        "gain_one": shape((1, width), F32),
        "gain_q": shape((1, q_width), F32),
        "gain_two": shape((1, width), F32),
        "tags": shape((n_ctx, 8, 128), F32),
    }
    out_hbm = ("w_qd", "w_kv", "w_qu", "w_out", "gate_full", "up_full", "all_kv")
    box = (inputs["w_gate"].shape[0], 2 * part)
    dma = pltpu.SemaphoreType.DMA
    scratch = {
        "infos": pltpu.VMEM((n_f,) + inputs["info"].shape, F32),
        "qd_full": pltpu.VMEM(whole("q_down"), BF16),
        "kv_full": pltpu.VMEM(whole("kv_weight"), BF16),
        "qu_full": pltpu.VMEM(whole("q_up"), BF16),
        "gate_box": pltpu.VMEM(box, BF16),
        "up_box": pltpu.VMEM(box, BF16),
        "gate_spare": pltpu.VMEM((box[0], part), BF16),
        "up_spare": pltpu.VMEM((box[0], part), BF16),
        "out_spare": pltpu.VMEM(inputs["out_proj"].shape, BF16),
        "kv_rows": pltpu.VMEM((tokens, 2 * head_size), BF16),
        "send_sem": dma((64 + 2 * n_ctx,)),
        "recv_sem": dma((64 + 2 * n_ctx,)),
        "local_sem": dma((16,)),
    }
    vmem = pl.BlockSpec(memory_space=pltpu.VMEM)
    anywhere = pl.BlockSpec(memory_space=pl.ANY)
    names = tuple(inputs) + tuple(outs) + tuple(scratch)
    values = pl.pallas_call(
        functools.partial(front_kernel, n_ctx, n_f, names),
        out_shape=tuple(outs.values()),
        in_specs=[anywhere if m in in_hbm else vmem for m in inputs],
        out_specs=tuple([anywhere if m in out_hbm else vmem for m in outs]),
        scratch_shapes=list(scratch.values()),
        compiler_params=pltpu.CompilerParams(
            collective_id=1, has_side_effects=True, vmem_limit_bytes=48 << 20
        ),
        name="front",
    )(*inputs.values())
    return dict(zip(outs, values, strict=True))


def tiles(total, wide, body):
    whole = total // wide

    @pl.loop(0, whole)
    def _(t):
        body(pl.multiple_of(t * wide, wide), wide)

    if total % wide:
        body(whole * wide, total % wide)


def contract_first(a, b):
    return jnp.dot(a.T, b, preferred_element_type=F32)


def ffn_kernel(n_f, names, *refs):
    r = dict(zip(names, refs, strict=True))
    c_idx = lax.axis_index("ctx")
    f_idx = lax.axis_index("fsdp")
    moves = Sender()
    at_sem = [0]
    core, far = (c_idx, flip(f_idx, 1)), (c_idx, flip(f_idx, 2))
    beside = (flip(c_idx, 1), f_idx)
    y_idx = c_idx % 2

    def send(src, dst, peer):
        i = at_sem[0]
        at_sem[0] += 1
        return moves(src, dst, r["send_sem"].at[i], r["recv_sem"].at[i], peer)

    barrier = pltpu.get_barrier_semaphore()
    for peer in (core, far, (c_idx, flip(f_idx, 3)), beside):
        pl.semaphore_signal(barrier, inc=1, device_id=peer, device_id_type=MESH)
    pl.semaphore_wait(barrier, 4)

    tokens, width = r["normed"].shape
    mine = r["attn_group"].at[pl.ds(pl.multiple_of(f_idx * tokens, tokens), tokens)]
    own_attn = pltpu.make_async_copy(r["attn_cut"].at[f_idx], mine, r["load_sem"].at[3])
    own_attn.start()

    def send_attn(mask):
        return send(r["attn_cut"].at[flip(f_idx, mask)], mine, (c_idx, flip(f_idx, mask)))

    units = r["w_down"].shape[0]
    group, dz = r["group"], r["dz"]
    block = [slice(i * tokens, (i + 1) * tokens) for i in range(4)]
    pair = [slice(0, 2 * tokens), slice(2 * tokens, 4 * tokens)]

    def gather(buf):
        to_core = send(buf.at[block[0]], buf.at[block[1]], core)
        to_far = send(buf.at[block[0]], buf.at[block[2]], far)
        return to_core, to_far

    def gather_far(buf, to_far):
        to_far.wait_recv()
        send(buf.at[block[2]], buf.at[block[3]], core).wait_recv()

    group[block[0], :] = r["normed"][...]
    to_core, to_far = gather(group)
    loads = []
    for i, m in enumerate(("gate", "up", "down")):
        load = pltpu.make_async_copy(r["w_" + m], r["v_" + m], r["load_sem"].at[i])
        load.start()
        loads.append(load)
    loads[0].wait()
    loads[1].wait()

    def hidden_part(rows):
        def one(start, wide):
            at = pl.ds(start, wide)
            both = jnp.concatenate([r["v_gate"][:, at], r["v_up"][:, at]], axis=1)
            out = jnp.dot(group[rows, :], both, preferred_element_type=F32)
            gate, up = out[:, :wide], out[:, wide:]
            r["gate"][rows, at] = gate.astype(BF16)
            r["up"][rows, at] = up.astype(BF16)
            r["hid"][rows, at] = (gate / (1.0 + jnp.exp(-gate)) * up).astype(BF16)

        tiles(units, 128, one)

    to_core.wait_recv()
    hidden_part(pair[0])
    gather_far(group, to_far)
    attn_copies = [send_attn(1), send_attn(2)]
    hidden_part(pair[1])
    loads[2].wait()

    def down_block(i, dest):
        def one(start, wide):
            at = pl.ds(start, wide)
            dest[:, at] = jnp.dot(
                r["hid"][block[i], :], r["v_down"][:, at], preferred_element_type=F32
            ).astype(dest.dtype)

        tiles(width, 256, one)

    def back_block(i, dest):
        def one(start, wide):
            at = pl.ds(start, wide)
            dest[:, at] = (
                contract_last(r["gate"][block[i], :], r["v_gate"][at, :])
                + contract_last(r["up"][block[i], :], r["v_up"][at, :])
            ).astype(dest.dtype)

        tiles(width, 256, one)

    def add_rows(dest, one, two):
        def add(at):
            dest[at, :] = (one[at, :].astype(F32) + two[at, :].astype(F32)).astype(dest.dtype)

        row_loop(tokens, add)

    def far_sum(k, make):
        make(3, r["give"].at[2 * k])
        step = send(r["give"].at[2 * k], r["got"].at[2 * k], core)
        make(2, r["far_sum"])
        step.wait_recv()
        add_rows(r["far_give"].at[k], r["far_sum"], r["got"].at[2 * k])
        return send(r["far_give"].at[k], r["far_got"].at[k], far)

    def near_sum(k, make):
        make(1, r["give"].at[2 * k + 1])
        step = send(r["give"].at[2 * k + 1], r["got"].at[2 * k + 1], core)
        make(0, r["near_sum"])
        return step

    def near_end(k, step):
        step.wait_recv()
        add_rows(r["near_sum"], r["near_sum"], r["got"].at[2 * k + 1])

    far_step = far_sum(0, down_block)
    near_end(0, near_sum(0, down_block))
    far_step.wait_recv()
    r["sq"][...] = jnp.zeros_like(r["sq"])

    def loss_rows(at):
        value = r["resid"][at, :] + r["near_sum"][at, :] + r["far_got"][0, at, :].astype(F32)
        r["result"][at, :] = value.astype(BF16)
        diff = value - r["teacher"][at, :].astype(F32)
        squares = jnp.sum(diff * diff, axis=1, keepdims=True) * r["valid"][at, :]
        r["sq"][:1, :] += jnp.sum(squares, axis=0, keepdims=True)
        grad = diff * r["valid_scale"][at, :1]
        r["grad_resid"][at, :] = grad
        dz[at, :] = grad.astype(BF16)

    row_loop(tokens, loss_rows, step=16)
    to_core, to_far = gather(dz)

    def back_hidden(rows):
        def one(start, wide):
            at = pl.ds(start, wide)
            grad = contract_last(dz[rows, :], r["v_down"][at, :])
            gate = r["gate"][rows, at].astype(F32)
            up = r["up"][rows, at].astype(F32)
            sigma = 1.0 / (1.0 + jnp.exp(-gate))
            r["gate"][rows, at] = (grad * up * sigma * (1.0 + gate * (1.0 - sigma))).astype(BF16)
            r["up"][rows, at] = (grad * (gate * sigma)).astype(BF16)

        tiles(units, 256, one)

    to_core.wait_recv()
    back_hidden(pair[0])
    near_step = near_sum(1, back_block)
    gather_far(dz, to_far)
    saves = []

    def save(src, dst, i):
        copy = pltpu.make_async_copy(src, dst, r["save_sem"].at[i])
        copy.start()
        return copy

    def down_tile(start, wide):
        at = pl.ds(start, wide)
        spot = r["tile"].at[pl.ds(0, wide)]
        spot[...] = contract_first(r["hid"][:, at], dz[...]).astype(BF16)
        save(spot, r["down_part"].at[at], 0).wait()

    tiles(units, 128, down_tile)
    half = units // 2
    give = pl.ds(pl.multiple_of((1 - y_idx) * half, half), half)
    down_step = send(r["down_part"].at[give], r["down_got"], beside)
    attn_copies.append(send_attn(3))
    back_hidden(pair[1])
    far_step = far_sum(1, back_block)
    near_end(1, near_step)

    def gate_tile(start, wide):
        at = pl.ds(start, wide)
        left = group[:, at].T
        for i, m in enumerate(("gate", "up")):
            spot = r["wide_tile"].at[i]
            spot[...] = jnp.dot(left, r[m][...], preferred_element_type=F32).astype(BF16)
            saves.append(save(spot, r[m + "_part"].at[at], 1 + i))
        saves.pop().wait()
        saves.pop().wait()

    tiles(width, 256, gate_tile)
    far_step.wait_recv()
    gain = r["gain_two"][...]
    r["gain_sum"][...] = jnp.zeros_like(r["gain_sum"])

    def norm_rows(at):
        grad = r["near_sum"][at, :] + r["far_got"][1, at, :].astype(F32)
        value = r["resid"][at, :]
        scale = lax.rsqrt(jnp.mean(value * value, axis=-1, keepdims=True) + NORM_EPS)
        r["gain_sum"][...] += jnp.sum(grad * value * scale, axis=0, keepdims=True)
        ge = gain * grad
        inner = jnp.mean(ge * value, axis=-1, keepdims=True)
        total = r["grad_resid"][at, :] + scale * ge - value * (scale * scale * scale) * inner
        r["grad_resid"][at, :] = total
        r["grad_branch"][at, :] = total.astype(BF16)

    row_loop(tokens, norm_rows, step=16)
    for copy in attn_copies + [down_step]:
        copy.wait_recv()
    own_attn.wait()
    moves.finish()


def feed_forward(n_f, inputs):
    tokens, width = inputs["normed"].shape
    units = inputs["w_down"].shape[0]
    shape = jax.ShapeDtypeStruct
    outs = {
        "result": shape((tokens, width), BF16),
        "grad_resid": shape((tokens, width), F32),
        "grad_branch": shape((tokens, width), BF16),
        "down_part": shape((units, width), BF16),
        "down_got": shape((units // 2, width), BF16),
        "gate_part": shape((width, units), BF16),
        "up_part": shape((width, units), BF16),
        "attn_group": shape((tokens * n_f, inputs["attn_cut"].shape[2]), BF16),
        "gain_sum": shape((1, width), F32),
        "sq": shape((8, 128), F32),
    }
    hbm = ("w_gate", "w_up", "w_down", "attn_cut", "attn_group")
    hbm += ("down_part", "down_got", "gate_part", "up_part")
    dma = pltpu.SemaphoreType.DMA
    many = tokens * n_f
    scratch = {
        "v_gate": pltpu.VMEM((width, units), BF16),
        "v_up": pltpu.VMEM((width, units), BF16),
        "v_down": pltpu.VMEM((units, width), BF16),
        "group": pltpu.VMEM((many, width), BF16),
        "dz": pltpu.VMEM((many, width), BF16),
        "gate": pltpu.VMEM((many, units), BF16),
        "up": pltpu.VMEM((many, units), BF16),
        "hid": pltpu.VMEM((many, units), BF16),
        "give": pltpu.VMEM((4, tokens, width), BF16),
        "got": pltpu.VMEM((4, tokens, width), BF16),
        "far_sum": pltpu.VMEM((tokens, width), F32),
        "near_sum": pltpu.VMEM((tokens, width), F32),
        "far_give": pltpu.VMEM((2, tokens, width), BF16),
        "far_got": pltpu.VMEM((2, tokens, width), BF16),
        "tile": pltpu.VMEM((128, width), BF16),
        "wide_tile": pltpu.VMEM((2, 256, units), BF16),
        "send_sem": dma((16,)),
        "recv_sem": dma((16,)),
        "load_sem": dma((4,)),
        "save_sem": dma((3,)),
    }
    vmem = pl.BlockSpec(memory_space=pltpu.VMEM)
    anywhere = pl.BlockSpec(memory_space=pl.ANY)
    names = tuple(inputs) + tuple(outs) + tuple(scratch)
    values = pl.pallas_call(
        functools.partial(ffn_kernel, n_f, names),
        out_shape=tuple(outs.values()),
        in_specs=[anywhere if m in hbm else vmem for m in inputs],
        out_specs=tuple([anywhere if m in hbm else vmem for m in outs]),
        scratch_shapes=list(scratch.values()),
        compiler_params=pltpu.CompilerParams(
            collective_id=2, has_side_effects=True, vmem_limit_bytes=60 << 20
        ),
        name="feed_forward",
    )(*inputs.values())
    return dict(zip(outs, values, strict=True))


def body(
    hidden_in,
    teacher,
    blocks,
    seq_ids,
    valid_mask,
    norm1_gain,
    q_down,
    q_gain,
    q_up,
    kv_weight,
    out_proj,
    norm2_gain,
    w_gate,
    w_up,
    w_down,
):
    row_count, model_width = hidden_in.shape
    head_size = kv_weight.shape[1] // 2
    heads_width = q_up.shape[1]
    head_count = heads_width // head_size
    half_dim = head_size // 2
    q_width = q_down.shape[1]
    n_ctx = lax.axis_size("ctx")
    n_f = lax.axis_size("fsdp")
    n_z = n_ctx // 2
    token_total = row_count * n_ctx * n_f
    seq_pieces = 2 * SEQ_BLOCKS
    c_idx = lax.axis_index("ctx")
    f_idx = lax.axis_index("fsdp")
    y_idx = c_idx % 2
    z_idx = c_idx // 2
    x_idx = f_idx // 2
    k_idx = f_idx % 2

    def by_f(values, mask):
        return lax.ppermute(values, "fsdp", [(i, i ^ mask) for i in range(n_f)])

    def by_c(values, mask):
        return lax.ppermute(values, "ctx", [(i, i ^ mask) for i in range(n_ctx)])

    def cut(values, start, size, axis):
        return lax.dynamic_slice_in_dim(values, start, size, axis)

    def ctx_split(grad):
        view = grad.reshape(n_z, 2, grad.shape[0] // n_ctx, grad.shape[1])
        give = lax.dynamic_index_in_dim(view, 1 - y_idx, 1, keepdims=False)
        keep = lax.dynamic_index_in_dim(view, y_idx, 1, keepdims=False)
        return give, keep

    def ctx_pair(keep, got):
        return (keep.astype(F32) + got.astype(F32)).astype(BF16)

    def ctx_spread(pair):
        return [pair] + [
            by_c(lax.dynamic_index_in_dim(pair, z_idx ^ r, 0, keepdims=False), 2 * r)
            for r in range(1, n_z)
        ]

    def ctx_total(parts):
        total = lax.dynamic_index_in_dim(parts[0], z_idx, 0, keepdims=False).astype(F32)
        for got in parts[1:]:
            total = total + got.astype(F32)
        return total

    def group_rows(values):
        return lax.all_gather(values, "fsdp", axis=0, tiled=True)

    valid_f = valid_mask.astype(F32)
    own_pieces = row_count // PIECE
    info = jnp.concatenate(
        [
            norm1_gain.astype(F32),
            q_gain.astype(F32),
            norm2_gain.astype(F32),
            jnp.full((128,), jnp.sum(valid_f)),
        ]
    )
    info = jnp.pad(info, (0, -info.shape[0] % 1024)).reshape(-1, 128)
    own_tags = jnp.stack([blocks.reshape(-1, PIECE)[:, 0], seq_ids.reshape(-1, PIECE)[:, 0]], 1)
    tag = jnp.pad(own_tags.astype(F32).reshape(1, -1), ((0, 7), (0, 128 - 2 * own_pieces)))
    own = jnp.concatenate([blocks.reshape(-1, PIECE)[:, 0], seq_ids[:1]])

    positions = blocks * PIECE + jnp.arange(row_count, dtype=jnp.int32) % PIECE
    freq_table = 10000.0 ** (-(jnp.arange(half_dim, dtype=F32) * 2.0 / head_size))
    angle_table = positions.astype(F32)[:, None] * freq_table[None, :]
    cosine = jnp.cos(angle_table)
    sine = jnp.sin(angle_table)
    fetched = front(
        n_ctx,
        n_f,
        {
            "q_down": q_down,
            "kv_weight": kv_weight,
            "q_up": q_up,
            "out_proj": out_proj,
            "w_gate": w_gate,
            "w_up": w_up,
            "hidden": hidden_in,
            "info": info,
            "tag": tag,
            "cos": cosine,
            "sin": sine,
        },
        head_size,
    )
    w_out = fetched["w_out"]
    all_kv, q_rot = fetched["all_kv"], fetched["q_rot"]
    normed, q_low, q_normed = fetched["normed"], fetched["q_low"], fetched["q_normed"]
    gain_one, gain_q, gain_two = fetched["gain_one"], fetched["gain_q"], fetched["gain_two"]
    tags = fetched["tags"][:, 0, : 2 * own_pieces].reshape(-1, 2).astype(jnp.int32)
    total_count = jnp.sum(fetched["tags"][:, 1, 0])
    hidden_f = hidden_in.astype(F32)
    scale_q = rms_scale(q_low)

    out_block = heads_width // (n_ctx * n_f)
    if out_block == 128:
        attn_heads, lse, attn_cut = attn_fwd(
            tags, own, q_rot, all_kv, head_size, seq_pieces, n_f, True
        )
    else:
        attn_heads, lse = attn_fwd(tags, own, q_rot, all_kv, head_size, seq_pieces, n_f, False)
        attn_cut = attn_heads.reshape(row_count, n_ctx, n_f, out_block).transpose(2, 0, 1, 3)
        attn_cut = attn_cut.reshape(n_f, row_count, n_ctx * out_block)
    resid = hidden_f + dot(attn_heads, w_out)
    scale_two = rms_scale(resid)
    normed_two = (resid * scale_two * gain_two).astype(BF16)

    wide_valid = jnp.broadcast_to(valid_f[:, None], (row_count, 128))
    ffn = feed_forward(
        n_f,
        {
            "normed": normed_two,
            "resid": resid,
            "teacher": teacher,
            "valid": wide_valid,
            "valid_scale": wide_valid * (token_total / total_count),
            "gain_two": gain_two,
            "w_gate": fetched["gate_full"],
            "w_up": fetched["up_full"],
            "w_down": w_down,
            "attn_cut": attn_cut,
        },
    )
    grad_resid, grad_branch = ffn["grad_resid"], ffn["grad_branch"]
    grad_gain_two = ffn["gain_sum"].reshape(-1)
    sq_local = ffn["sq"][0, 0]
    half_units = w_down.shape[0] // 2
    down_pair = ctx_pair(cut(ffn["down_part"], y_idx * half_units, half_units, 0), ffn["down_got"])
    down_parts = ctx_spread(down_pair.reshape(n_z, -1, model_width))
    gate_give, gate_keep = ctx_split(ffn["gate_part"])
    gate_got = by_c(gate_give, 1)
    early = n_z
    up_blocks = ffn["up_part"].reshape(n_z, 2, model_width // n_ctx, -1)
    up_got = by_c(
        lax.dynamic_index_in_dim(up_blocks[:early], 1 - y_idx, 1, keepdims=False), 1
    )
    branch_group = group_rows(grad_branch)
    grad_attn = dot_t(grad_branch, w_out).astype(BF16)
    grad_qlin, grad_seq = attn_bwd(
        tags, own, q_rot, grad_attn, attn_heads, lse, cosine, sine, all_kv, head_size, seq_pieces
    )
    qlin_group = lax.all_to_all(grad_qlin, "fsdp", 1, 0, tiled=True)
    down_parts, gate_got, grad_seq = together(down_parts, gate_got, grad_seq)

    by_piece = grad_seq.reshape(seq_pieces, PIECE, 2 * head_size)
    piece_tag = tags[:, 0].reshape(n_z, 2, own_pieces)
    piece_own = (tags[:, 1] == seq_ids[0]).reshape(n_z, 2, own_pieces)

    def kv_half(bit):
        places = lax.dynamic_index_in_dim(piece_tag, bit, 1, keepdims=False).reshape(-1)
        picked = by_piece[places]
        if n_ctx * own_pieces != seq_pieces:
            mine = lax.dynamic_index_in_dim(piece_own, bit, 1, keepdims=False).reshape(-1)
            picked = jnp.where(mine[:, None, None], picked, jnp.zeros_like(picked))
        return picked.reshape(n_z, own_pieces * PIECE, 2 * head_size)

    kv_part = jnp.stack([kv_half(0), kv_half(1)], axis=1)
    q_cut, kv_cut = q_width // n_f, 2 * head_size // n_f
    qnorm_group = group_rows(q_normed)
    normed_group = group_rows(normed)

    grad_qnormed = dot_t(grad_qlin, fetched["w_qu"])
    grad_qlow_f, grad_gain_q = rms_back(q_low, scale_q, gain_q, grad_qnormed)
    grad_qlow = grad_qlow_f.astype(BF16)
    attn_group = ffn["attn_group"]
    da_q = dot_t(grad_qlow, fetched["w_qd"])
    gate_parts = ctx_spread(ctx_pair(gate_keep, gate_got))
    out_part = dot_rows(attn_group, branch_group).astype(BF16)
    qup_part = dot_rows(qnorm_group, qlin_group).astype(BF16)

    def by_ctx(grad):
        return grad.reshape(n_z, 2, grad.shape[0] // n_ctx, grad.shape[1])

    order = [
        (c * n_f + f, f * n_ctx + c % 2 * n_z + c // 2) for c in range(n_ctx) for f in range(n_f)
    ]
    down_rows = ctx_total(down_parts).astype(BF16)
    down_sent = lax.ppermute(down_rows, ("ctx", "fsdp"), order)

    gate_parts, up_got, out_part, qup_part, kv_part, da_q = together(
        gate_parts, up_got, out_part, qup_part, kv_part, da_q
    )
    gate_sent = lax.all_to_all(
        ctx_total(gate_parts).astype(BF16), "fsdp", 0, 1, tiled=True
    )

    small = jnp.concatenate(
        [jnp.zeros((model_width,), F32), grad_gain_q, grad_gain_two, sq_local.reshape(1)]
    )
    entries = small.shape[0]
    small = jnp.pad(small, (0, -entries % 1024)).reshape(-1, 128)
    ends = tail_reduce(
        n_ctx,
        n_f,
        {
            "kv": kv_part,
            "up": up_blocks,
            "up_got": up_got,
            "out": by_ctx(out_part),
            "qup": by_ctx(qup_part),
            "dqa": grad_qlow,
            "cos": cosine,
            "sin": sine,
            "normed_group": normed_group,
            "w_kv": fetched["w_kv"],
            "da_q": da_q,
            "hidden": hidden_in,
            "gain_one": gain_one,
            "grad_resid": grad_resid,
            "small": small,
        },
        q_width,
    )
    small, down_sent, gate_sent = together(ends["small_out"], down_sent, gate_sent)
    small = small.reshape(-1)[:entries]
    grad_down = down_sent.astype(F32)

    device = c_idx * n_f + f_idx
    q1, q2 = model_width, model_width + q_width
    n_dev = n_ctx * n_f

    def own_part(values):
        size = values.shape[0] // n_dev
        return cut(values, device * size, size, 0)

    loss_now = small[-1] / (model_width * total_count)
    return (
        ffn["result"],
        loss_now,
        ends["grad_input"],
        own_part(small[:q1]),
        ends["out_qd"],
        own_part(small[q1:q2]),
        ends["out_qup"],
        ends["out_kvw"],
        ends["out_out"],
        own_part(small[q2 : q2 + model_width]),
        gate_sent.astype(F32),
        ends["out_up"],
        grad_down,
    )


def solution(mesh):
    both = ("ctx", "fsdp")
    rows = P(both, None)
    flat = P(both)
    shard = P("fsdp", None)
    gain = P("fsdp")
    return jax.shard_map(
        body,
        mesh=mesh,
        in_specs=(
            rows,
            rows,
            flat,
            flat,
            flat,
            gain,
            shard,
            gain,
            shard,
            shard,
            shard,
            gain,
            shard,
            shard,
            shard,
        ),
        out_specs=(
            rows,
            P(),
            rows,
            flat,
            rows,
            flat,
            rows,
            rows,
            rows,
            flat,
            rows,
            rows,
            rows,
        ),
        check_vma=False,
    )
```

```python
import functools
import math

import jax
import jax.numpy as jnp
from jax import lax
from jax.experimental import pallas as pl
from jax.experimental.pallas import tpu as pltpu
from jax.sharding import PartitionSpec as P

PIECE = 128
SEQ_BLOCKS = 8
NORM_EPS = 1e-05
F32 = jnp.float32
BF16 = jnp.bfloat16
LOG2E = math.log2(math.e)
HEAD_GROUP = 4


def rms_scale(values):
    return lax.rsqrt(jnp.mean(values * values, axis=-1, keepdims=True) + NORM_EPS)


def rms_back(values, scale, gain, grad):
    grad_gain = jnp.sum(grad * values * scale, axis=0)
    ge = gain * grad
    inner = jnp.mean(ge * values, axis=-1, keepdims=True)
    return scale * ge - values * (scale * scale * scale) * inner, grad_gain


def rope_apply(values, cosine, sine):
    half_dim = values.shape[-1] // 2
    one = values[..., :half_dim]
    two = values[..., half_dim:]
    return jnp.concatenate([one * cosine - two * sine, two * cosine + one * sine], axis=-1)


def rope_back(grads, cosine, sine):
    half_dim = grads.shape[-1] // 2
    one = grads[..., :half_dim]
    two = grads[..., half_dim:]
    return jnp.concatenate([one * cosine + two * sine, two * cosine - one * sine], axis=-1)


def together(*values):
    return lax.optimization_barrier(values)


def dot(a, b):
    return jnp.dot(a, b, preferred_element_type=F32)


def dot_t(a, b):
    return lax.dot_general(a, b, (((1,), (1,)), ((), ())), preferred_element_type=F32)


def dot_rows(a, b):
    return lax.dot_general(a, b, (((0,), (0,)), ((), ())), preferred_element_type=F32)


def contract_last(a, b):
    return lax.dot_general(a, b, (((1,), (1,)), ((), ())), preferred_element_type=F32)

def find_pieces(tags_ref, own_ref, pick_ref, total):
    @pl.loop(0, total)
    def _(u):
        @pl.when(tags_ref[u, 1] == own_ref[2])
        def _():
            pick_ref[tags_ref[u, 0]] = u

def stack_heads(ref, hd):
    return jnp.concatenate([ref[:, h*hd:(h+1)*hd] for h in range(HEAD_GROUP)], axis=0)

def attn_fwd_kernel(n_f, tags_ref, own_ref, q_ref, kv_ref, o_ref, lse_ref, *rest):
    k_s, vt_s, acc_s, pick_s = rest[-4:]
    half = pl.program_id(0)
    hd = k_s.shape[1]
    pieces = k_s.shape[0] // PIECE
    total = kv_ref.shape[0] // PIECE
    wide = 2 * PIECE
    coef = hd ** -0.5 * LOG2E

    @pl.when((half == 0) & (pl.program_id(1) == 0))
    def _():
        find_pieces(tags_ref, own_ref, pick_s, total)
        for i in range(pieces):
            rows = pl.ds(pl.multiple_of(pick_s[i] * PIECE, PIECE), PIECE)
            k_s[i*PIECE:(i+1)*PIECE, :] = kv_ref[rows, :hd]
            vt_s[:, i*PIECE:(i+1)*PIECE] = kv_ref[rows, hd:].T

    q = stack_heads(q_ref, hd)
    acc_s[...] = jnp.zeros_like(acc_s)
    rows = q.shape[0]
    def step(i, carry):
        peak, total_p = carry
        at = pl.ds(pl.multiple_of(i * wide, wide), wide)
        raw = contract_last(k_s[at, :], q)
        top = jnp.maximum(peak, jnp.max(raw, axis=0, keepdims=True))
        fade = jnp.exp2((peak - top) * coef)
        p = jnp.exp2((raw - top) * coef)
        acc_s[...] = acc_s[...] * fade + jnp.dot(vt_s[:, at], p.astype(BF16), preferred_element_type=F32)
        return top, total_p * fade + jnp.sum(p, axis=0, keepdims=True)
    count = own_ref[half] // 2 + 1
    peak, total_p = lax.fori_loop(0, count, step, (jnp.full((1, rows), -1e30, F32), jnp.zeros((1, rows), F32)))
    out = (acc_s[...] / total_p).astype(BF16).T
    for h in range(HEAD_GROUP):
        o_ref[:, h*hd:(h+1)*hd] = out[h*PIECE:(h+1)*PIECE, :]
    if len(rest) > 4:
        for b in range(HEAD_GROUP * hd // 128):
            head, part = b * 128 // hd, b * 128 % hd
            rest[0][b % n_f, :, b // n_f * 128:(b // n_f + 1) * 128] = out[
                head*PIECE:(head+1)*PIECE, part:part+128
            ]
    lse_ref[0] = peak * coef + jnp.log2(total_p)

def attn_fwd(tags, own, q, kv, hd, pieces, n_f, cut):
    n_rows, width = q.shape
    groups = width // hd // HEAD_GROUP
    gw = HEAD_GROUP * hd
    halves = n_rows // PIECE
    rows = HEAD_GROUP * PIECE
    blk = pl.BlockSpec((PIECE, gw), lambda p, g, *_: (p, g))
    flops = 4 * n_rows * width * pieces * PIECE * 9 // 16
    shapes = [jax.ShapeDtypeStruct(q.shape, BF16), jax.ShapeDtypeStruct((halves*groups, 1, rows), F32)]
    specs = [blk, pl.BlockSpec((1, 1, rows), lambda p, g, *_: (p*groups+g, 0, 0))]
    if cut:
        shapes.append(jax.ShapeDtypeStruct((n_f, n_rows, width // n_f), BF16))
        specs.append(pl.BlockSpec((n_f, PIECE, gw // n_f), lambda p, g, *_: (0, p, g)))
    return pl.pallas_call(
        functools.partial(attn_fwd_kernel, n_f),
        out_shape=tuple(shapes),
        grid_spec=pltpu.PrefetchScalarGridSpec(
            num_scalar_prefetch=2, grid=(halves, groups),
            in_specs=[blk, pl.BlockSpec(kv.shape, lambda p, g, *_: (0, 0))],
            out_specs=tuple(specs),
            scratch_shapes=[pltpu.VMEM((pieces*PIECE, hd), BF16), pltpu.VMEM((hd, pieces*PIECE), BF16),
                            pltpu.VMEM((hd, rows), F32), pltpu.SMEM((pieces,), jnp.int32)]),
        compiler_params=pltpu.CompilerParams(vmem_limit_bytes=40 << 20),
        cost_estimate=pl.CostEstimate(flops=flops, transcendentals=flops//(4*hd), bytes_accessed=2*(2*q.size+kv.size)),
        name="attn_fwd",
    )(tags, own, q, kv)

def attn_bwd_kernel(tags_ref, own_ref, q_ref, do_ref, o_ref, lse_ref, cos_ref, sin_ref, kv_ref, dq_ref, dkv_ref,
                    k_s, kt_s, v_s, dq_s, dk_s, dv_s, pick_s):
    half = pl.program_id(0)
    group = pl.program_id(1)
    hd = k_s.shape[1]
    pieces = k_s.shape[0] // PIECE
    total = kv_ref.shape[0] // PIECE
    wide = 2 * PIECE
    coef = hd ** -0.5 * LOG2E
    scale = hd ** -0.5

    @pl.when((half == 0) & (group == 0))
    def _():
        find_pieces(tags_ref, own_ref, pick_s, total)
        for i in range(pieces):
            rows = pl.ds(pl.multiple_of(pick_s[i] * PIECE, PIECE), PIECE)
            keys = kv_ref[rows, :hd]
            k_s[i*PIECE:(i+1)*PIECE, :] = keys
            kt_s[:, i*PIECE:(i+1)*PIECE] = keys.T
            v_s[i*PIECE:(i+1)*PIECE, :] = kv_ref[rows, hd:]
        dk_s[...] = jnp.zeros_like(dk_s)
        dv_s[...] = jnp.zeros_like(dv_s)

    q = stack_heads(q_ref, hd)
    do = stack_heads(do_ref, hd)
    prod = do.astype(F32) * stack_heads(o_ref, hd).astype(F32)
    delta = lax.dot_general(jnp.ones((8, hd), F32), prod, (((1,), (1,)), ((), ())),
                            preferred_element_type=F32, precision=lax.Precision.HIGHEST)[:1]
    lse = lse_ref[0]
    dq_s[...] = jnp.zeros_like(dq_s)
    def step(i, carry):
        at = pl.ds(pl.multiple_of(i * wide, wide), wide)
        p = jnp.exp2(contract_last(k_s[at, :], q) * coef - lse)
        dp = contract_last(v_s[at, :], do)
        ds = (p * (dp - delta)).astype(BF16)
        dv_s[at, :] += jnp.dot(p.astype(BF16), do, preferred_element_type=F32)
        dk_s[at, :] += jnp.dot(ds, q, preferred_element_type=F32)
        dq_s[...] += jnp.dot(kt_s[:, at], ds, preferred_element_type=F32)
        return carry
    lax.fori_loop(0, own_ref[half] // 2 + 1, step, 0)
    dq = (dq_s[...] * scale).T
    cos, sin = cos_ref[...], sin_ref[...]
    mid = hd // 2
    for h in range(HEAD_GROUP):
        one = dq[h*PIECE:(h+1)*PIECE, :mid]
        two = dq[h*PIECE:(h+1)*PIECE, mid:]
        dq_ref[:, h*hd:h*hd+mid] = (one * cos + two * sin).astype(BF16)
        dq_ref[:, h*hd+mid:(h+1)*hd] = (two * cos - one * sin).astype(BF16)

    @pl.when((half == pl.num_programs(0) - 1) & (group == pl.num_programs(1) - 1))
    def _():
        dkv_ref[:, :hd] = (dk_s[...] * scale).astype(BF16)
        dkv_ref[:, hd:] = dv_s[...].astype(BF16)

def attn_bwd(tags, own, q, do, o, lse, cos, sin, kv, hd, pieces):
    n_rows, width = q.shape
    groups = width // hd // HEAD_GROUP
    gw = HEAD_GROUP * hd
    halves = n_rows // PIECE
    rows = HEAD_GROUP * PIECE
    blk = pl.BlockSpec((PIECE, gw), lambda p, g, *_: (p, g))
    trig = pl.BlockSpec((PIECE, hd // 2), lambda p, g, *_: (p, 0))
    keys = pieces * PIECE
    return pl.pallas_call(
        attn_bwd_kernel,
        out_shape=(jax.ShapeDtypeStruct(q.shape, BF16), jax.ShapeDtypeStruct((keys, 2*hd), BF16)),
        grid_spec=pltpu.PrefetchScalarGridSpec(
            num_scalar_prefetch=2, grid=(halves, groups),
            in_specs=[blk, blk, blk, pl.BlockSpec((1, 1, rows), lambda p, g, *_: (p*groups+g, 0, 0)), trig, trig,
                      pl.BlockSpec(kv.shape, lambda p, g, *_: (0, 0))],
            out_specs=[blk, pl.BlockSpec((keys, 2*hd), lambda p, g, *_: (0, 0))],
            scratch_shapes=[pltpu.VMEM((keys, hd), BF16), pltpu.VMEM((hd, keys), BF16), pltpu.VMEM((keys, hd), BF16),
                            pltpu.VMEM((hd, rows), F32), pltpu.VMEM((keys, hd), F32), pltpu.VMEM((keys, hd), F32),
                            pltpu.SMEM((pieces,), jnp.int32)]),
        compiler_params=pltpu.CompilerParams(vmem_limit_bytes=48 << 20),
        name="attn_bwd",
    )(tags, own, q, do, o, lse, cos, sin, kv)

MESH = pl.DeviceIdType.MESH


def flip(index, mask):
    out = 0
    bit = 1
    while bit <= mask:
        part = (index // bit) % 2
        out = out + bit * ((1 - part) if mask & bit else part)
        bit *= 2
    return out + (index // bit) * bit


def row_loop(rows, body, step=32):
    if rows % step:
        step = 16

    @pl.loop(0, rows // step)
    def _(i):
        body(pl.ds(pl.multiple_of(i * step, step), step))


class Sender:
    def __init__(self):
        self.open = []

    def make(self, src, dst, send_sem, recv_sem, peer):
        return pltpu.make_async_remote_copy(
            src_ref=src,
            dst_ref=dst,
            send_sem=send_sem,
            recv_sem=recv_sem,
            device_id=peer,
            device_id_type=MESH,
        )

    def __call__(self, *args):
        copy = self.make(*args)
        copy.start()
        self.open.append(copy)
        return copy

    def finish(self):
        for copy in self.open:
            copy.wait_send()


class LineSum:
    def __init__(self, own, got, send_sem, recv_sem, c_idx, f_idx, n_z, sender):
        self.own, self.got, self.send_sem, self.recv_sem = own, got, send_sem, recv_sem
        self.n_z, self.sender = n_z, sender
        self.z = c_idx // 2
        self.left = (c_idx - 2, f_idx)
        self.right = (c_idx + 2, f_idx)

    def copy(self, b, slot, peer):
        return self.sender.make(
            self.own.at[b], self.got.at[slot], self.send_sem.at[b], self.recv_sem.at[slot], peer
        )

    def take(self, b, slot):
        self.copy(b, slot, self.left).wait_recv()

        def add(at):
            self.own[b, at, :] = (
                self.own[b, at, :].astype(F32) + self.got[slot, at, :].astype(F32)
            ).astype(BF16)

        row_loop(self.own.shape[1], add)

    def go_right(self, b):
        z = self.z

        @pl.when(z < b)
        def _():
            @pl.when(z > 0)
            def _():
                self.take(b, b)

            self.copy(b, b, self.right).start()

    def go_left(self, b):
        z, n_z = self.z, self.n_z

        @pl.when(z > b)
        def _():
            @pl.when(z < n_z - 1)
            def _():
                self.take(b, b)

            @pl.when(z - 1 > b)
            def _():
                self.copy(b, b, self.left).start()

            @pl.when(z - 1 == b)
            def _():
                self.copy(b, n_z, self.left).start()

    def step(self, i):
        @pl.when(2 * self.z < self.n_z)
        def _():
            self.go_right(self.n_z - 1 - i)
            self.go_left(i)

        @pl.when(2 * self.z >= self.n_z)
        def _():
            self.go_left(i)
            self.go_right(self.n_z - 1 - i)

    def total(self, store):
        z, n_z = self.z, self.n_z

        @pl.when(z > 0)
        def _():
            self.copy(z, z, self.left).wait_recv()

        @pl.when(z < n_z - 1)
        def _():
            self.copy(z, n_z, self.left).wait_recv()

        rows = self.own.shape[1]

        @pl.when(z == 0)
        def _():
            row_loop(
                rows,
                lambda at: store(
                    at, self.own[z, at, :].astype(F32) + self.got[n_z, at, :].astype(F32)
                ),
            )

        @pl.when(z == n_z - 1)
        def _():
            row_loop(
                rows,
                lambda at: store(
                    at, self.own[z, at, :].astype(F32) + self.got[z, at, :].astype(F32)
                ),
            )

        @pl.when((z > 0) & (z < n_z - 1))
        def _():
            row_loop(
                rows,
                lambda at: store(
                    at,
                    self.own[z, at, :].astype(F32)
                    + self.got[z, at, :].astype(F32)
                    + self.got[n_z, at, :].astype(F32),
                ),
            )

    def finish(self):
        for b in range(self.n_z):

            @pl.when(self.z != b)
            def _(b=b):
                self.copy(b, b, self.left).wait_send()


WINDOW = 3
TAIL_NAMES = ("gate", "kv", "up", "out", "qup", "low")
TAIL_CUT = ("gate", "up", "qup", "low")
TAIL_SENT = ("kv", "up", "out", "qup", "low")


def tail_kernel(n_ctx, n_f, names_in, names_out, names_scratch, *refs):
    n_z = n_ctx // 2
    names = list(names_in) + list(names_out) + list(names_scratch)
    r = dict(zip(names, refs, strict=True))
    c_idx = lax.axis_index("ctx")
    f_idx = lax.axis_index("fsdp")
    y_idx = c_idx % 2
    z_idx = c_idx // 2
    send = Sender()

    def over_c(mask):
        return (flip(c_idx, mask), f_idx)

    def over_f(mask):
        return (c_idx, flip(f_idx, mask))

    barrier = pltpu.get_barrier_semaphore()
    for mask in range(1, n_f):
        pl.semaphore_signal(barrier, inc=1, device_id=over_f(mask), device_id_type=MESH)
    for mask in range(1, n_ctx):
        pl.semaphore_signal(barrier, inc=1, device_id=over_c(mask), device_id_type=MESH)
    pl.semaphore_wait(barrier, n_f - 1 + n_ctx - 1)

    lines = {
        m: LineSum(
            r["pair_" + m],
            r["z_" + m],
            r["z_send"].at[i],
            r["z_recv"].at[i],
            c_idx,
            f_idx,
            n_z,
            send,
        )
        for i, m in enumerate(TAIL_NAMES)
    }
    y_copies, keeps = {}, {}
    early = r["up_got"].shape[0]

    parts = {m: r[m] for m in ("kv", "up", "out", "qup")}
    parts["low"] = r["part_low"]
    queue = [
        (m, b) for m in TAIL_SENT for b in range(n_z) if m != "up" or b >= early
    ]
    owed = tuple(queue)

    def next_y():
        if queue:
            m, b = queue.pop(0)
            i = TAIL_SENT.index(m)
            y_copies[m, b] = send(
                parts[m].at[b, 1 - y_idx],
                r["y_" + m].at[b],
                r["y_send"].at[i, b],
                r["y_recv"].at[i, b],
                over_c(1),
            )
            take_own(m, b)

    def take_own(m, b):
        keep = pltpu.make_async_copy(
            parts[m].at[b, y_idx],
            r["pair_" + m].at[b],
            r["keep_sem"].at[TAIL_SENT.index(m), b],
        )
        keep.start()
        keeps[m, b] = keep

    def add_pair(m, b):
        y_copies[m, b].wait_recv()
        next_y()
        add_ready(m, b)

    def add_ready(m, b):
        keeps[m, b].wait()
        pair, got = r["pair_" + m], r["y_" + m]

        def add(at):
            pair[b, at, :] = (pair[b, at, :].astype(F32) + got[b, at, :].astype(F32)).astype(BF16)

        row_loop(pair.shape[1], add)

    def advance(pair, line):
        if pair == "up":
            here.wait()
            for b in range(early):
                add_ready(pair, b)
        for b in range(n_z):
            if pair is not None and (pair, b) in owed:
                add_pair(pair, b)
            if line is not None and b < n_z - 1:
                lines[line].step(b)

    f_copies = {}

    def finish_sum(m):
        lines[m].total(lambda at, value: store_total(m, at, value))
        if m in TAIL_CUT:
            i = TAIL_CUT.index(m)
            part = r["tot_" + m].shape[0] // n_f
            for s in range(1, n_f):
                at = pl.ds(pl.multiple_of(flip(f_idx, s) * part, part), part)
                f_copies[m, s] = send(
                    r["tot_" + m].at[at, :],
                    r["f_" + m].at[s - 1],
                    r["f_send"].at[i, s - 1],
                    r["f_recv"].at[i, s - 1],
                    over_f(s),
                )

    def store_total(m, at, value):
        if m in TAIL_CUT:
            r["tot_" + m][at, :] = value.astype(BF16)
        else:
            r["out_" + m][at, :] = value

    def put_out(m):
        total = r["tot_" + m]
        rows, width = total.shape
        part = rows // n_f
        cuts = {"out_" + m: (0, width)}
        if m == "low":
            split = r["qd_group"].shape[1]
            cuts = {"out_qd": (0, split), "out_kvw": (split, width - split)}
        for s in range(n_f):
            source = flip(f_idx, s)
            if s:
                f_copies[m, s].wait_recv()
                got = r["f_" + m].at[s - 1]
            else:
                got = total.at[pl.ds(pl.multiple_of(f_idx * part, part), part)]
            for name, (start, wide) in cuts.items():
                at = pl.ds(pl.multiple_of(source * wide, 128), wide)
                r[name][:, at] = got[:, start : start + wide].astype(F32)

    def cut_low(src, dst, width, index):
        rows = src.shape[0]
        mine = pl.ds(pl.multiple_of(f_idx * rows, rows), rows)
        copies = []
        for s in range(1, n_f):
            at = pl.ds(pl.multiple_of(flip(f_idx, s) * width, 128), width)
            copies.append(
                send(
                    src.at[:, at],
                    dst.at[mine, :],
                    r["low_send"].at[index, s - 1],
                    r["low_recv"].at[index, s - 1],
                    over_f(s),
                )
            )
        own = pl.ds(pl.multiple_of(f_idx * width, 128), width)
        dst[mine, :] = src[:, own]
        return copies

    for _ in range(WINDOW):
        next_y()
    q_copies = cut_low(r["dqa"], r["qd_group"], r["qd_group"].shape[1], 0)
    pair_in = pltpu.make_async_copy(r["gate"], r["pair_gate"], r["keep_sem"].at[0, n_z])
    pair_in.start()
    here = pltpu.make_async_copy(
        r["up_got"], r["y_up"].at[pl.ds(0, early)], r["keep_sem"].at[1, n_z]
    )
    here.start()
    for b in range(early):
        take_own("up", b)
    pair_in.wait()
    advance("kv", "gate")
    advance("up", "kv")
    finish_sum("gate")

    head = r["dkv"].shape[1] // 2
    mid = head // 2

    def store_kv(at, value):
        cos, sin = r["cos"][at, :], r["sin"][at, :]
        one, two = value[:, :mid], value[:, mid:head]
        r["dkv"][at, :mid] = (one * cos + two * sin).astype(BF16)
        r["dkv"][at, mid:head] = (two * cos - one * sin).astype(BF16)
        r["dkv"][at, head:] = value[:, head:].astype(BF16)

    lines["kv"].total(store_kv)
    kv_copies = cut_low(r["dkv"], r["kv_group"], r["kv_group"].shape[1], 1)

    def low_part(group, start):
        normed, part = r["normed_group"], r["part_low"]
        rows = part.shape[2]

        def one(z, y, at):
            part[z, y, :, start : start + group.shape[1]] = lax.dot_general(
                normed[:, at],
                group[...],
                (((0,), (0,)), ((), ())),
                preferred_element_type=F32,
            ).astype(BF16)

        if rows % 128:
            for c in range(n_ctx):
                one(c // 2, c % 2, slice(c * rows, (c + 1) * rows))
        else:

            @pl.loop(0, n_ctx)
            def _(c):
                one(c // 2, c % 2, pl.ds(pl.multiple_of(c * rows, rows), rows))

    for copy in q_copies:
        copy.wait_recv()
    low_part(r["qd_group"], 0)
    advance("out", "up")
    for copy in kv_copies:
        copy.wait_recv()
    low_part(r["kv_group"], r["qd_group"].shape[1])

    grad_in, w_kv = r["grad_input"], r["w_kv"]
    width = grad_in.shape[1]
    tile = 256

    @pl.loop(0, width // tile)
    def _(t):
        at = pl.ds(pl.multiple_of(t * tile, tile), tile)
        grad_in[:, at] = r["da_q"][:, at] + lax.dot_general(
            r["dkv"][...],
            w_kv[at, :],
            (((1,), (1,)), ((), ())),
            preferred_element_type=F32,
        )

    r["gain_sum"][...] = jnp.zeros_like(r["gain_sum"])
    gain = r["gain_one"][...]

    def norm_rows(at):
        value = r["hidden"][at, :].astype(F32)
        grad = grad_in[at, :]
        scale = lax.rsqrt(jnp.mean(value * value, axis=-1, keepdims=True) + NORM_EPS)
        r["gain_sum"][...] += jnp.sum(grad * value * scale, axis=0, keepdims=True)
        ge = gain * grad
        inner = jnp.mean(ge * value, axis=-1, keepdims=True)
        grad_in[at, :] = (
            r["grad_resid"][at, :] + scale * ge - value * (scale * scale * scale) * inner
        )

    row_loop(grad_in.shape[0], norm_rows, step=16)

    small, small_got = r["small_out"], r["small_got"]
    small[...] = r["small"][...]
    for i in range(width // 128):
        small[i : i + 1, :] = r["gain_sum"][:, i * 128 : (i + 1) * 128]
    steps = [over_f(1), over_f(2), over_c(1)]
    mask = 2
    while mask < n_ctx:
        steps.append(over_c(mask))
        mask *= 2
    small_copies = {}

    def small_start(s):
        small_got[s, 0] = small[...]
        small_copies[s] = send(
            small_got.at[s, 0],
            small_got.at[s, 1],
            r["s_send"].at[s],
            r["s_recv"].at[s],
            steps[s],
        )

    def small_end(s):
        small_copies[s].wait_recv()
        small[...] = small[...] + small_got[s, 1]

    for s in range(2):
        small_start(s)
        small_end(s)
    small_start(2)

    put_out("gate")
    advance("qup", "out")
    finish_sum("up")
    advance("low", "qup")
    finish_sum("out")
    small_end(2)
    small_start(3)
    put_out("up")
    finish_sum("qup")
    advance(None, "low")
    for s in range(3, len(steps)):
        if s > 3:
            small_start(s)
        small_end(s)
    finish_sum("low")
    put_out("qup")
    put_out("low")
    send.finish()
    for m in TAIL_NAMES:
        lines[m].finish()


def tail_reduce(n_ctx, n_f, inputs, q_width):
    n_z = n_ctx // 2
    vmem = pl.BlockSpec(memory_space=pltpu.VMEM)
    anywhere = pl.BlockSpec(memory_space=pl.ANY)
    rows, width = inputs["hidden"].shape
    kv_width = inputs["w_kv"].shape[1]
    in_hbm = ("gate", "kv", "up", "up_got", "out", "qup")
    names_in = tuple(inputs)
    in_specs = [anywhere if m in in_hbm else vmem for m in names_in]
    block = {m: inputs[m].shape[-2:] for m in in_hbm}
    cut_q, cut_kv, high = q_width // n_f, kv_width // n_f, width // n_ctx
    block["low"] = (high, cut_q + cut_kv)
    outs = {
        "small_out": jax.ShapeDtypeStruct(inputs["small"].shape, F32),
        "grad_input": jax.ShapeDtypeStruct((rows, width), F32),
        "out_qd": jax.ShapeDtypeStruct((high // n_f, q_width), F32),
        "out_kvw": jax.ShapeDtypeStruct((high // n_f, kv_width), F32),
    }
    scratch = {}
    for m in TAIL_NAMES:
        high, wide = block[m]
        scratch["pair_" + m] = pltpu.VMEM((n_z, high, wide), BF16)
        scratch["z_" + m] = pltpu.VMEM((n_z + 1, high, wide), BF16)
        if m in TAIL_SENT:
            scratch["y_" + m] = pltpu.VMEM((n_z, high, wide), BF16)
        if m in TAIL_CUT:
            scratch["tot_" + m] = pltpu.VMEM((high, wide), BF16)
            scratch["f_" + m] = pltpu.VMEM((n_f - 1, high // n_f, wide), BF16)
            if m != "low":
                outs["out_" + m] = jax.ShapeDtypeStruct((high // n_f, wide * n_f), F32)
        elif m != "kv":
            outs["out_" + m] = jax.ShapeDtypeStruct((high, wide), F32)
    scratch["dkv"] = pltpu.VMEM((rows, kv_width), BF16)
    scratch["qd_group"] = pltpu.VMEM((rows * n_f, q_width // n_f), BF16)
    scratch["kv_group"] = pltpu.VMEM((rows * n_f, kv_width // n_f), BF16)
    scratch["part_low"] = pltpu.VMEM((n_z, 2) + block["low"], BF16)
    scratch["gain_sum"] = pltpu.VMEM((1, width), F32)
    steps = 2 + (n_ctx.bit_length() - 1)
    scratch["small_got"] = pltpu.VMEM((steps, 2) + inputs["small"].shape, F32)
    dma = pltpu.SemaphoreType.DMA
    sent, cut = len(TAIL_SENT), len(TAIL_CUT)
    scratch["s_send"] = dma((steps,))
    scratch["s_recv"] = dma((steps,))
    scratch["y_send"] = dma((sent, n_z))
    scratch["y_recv"] = dma((sent, n_z))
    scratch["keep_sem"] = dma((sent, n_z + 1))
    scratch["z_send"] = dma((len(TAIL_NAMES), n_z))
    scratch["z_recv"] = dma((len(TAIL_NAMES), n_z + 1))
    scratch["f_send"] = dma((cut, n_f - 1))
    scratch["f_recv"] = dma((cut, n_f - 1))
    scratch["low_send"] = dma((2, n_f - 1))
    scratch["low_recv"] = dma((2, n_f - 1))
    values = pl.pallas_call(
        functools.partial(tail_kernel, n_ctx, n_f, names_in, tuple(outs), tuple(scratch)),
        out_shape=tuple(outs.values()),
        in_specs=in_specs,
        out_specs=tuple([vmem] * len(outs)),
        scratch_shapes=list(scratch.values()),
        compiler_params=pltpu.CompilerParams(
            collective_id=0, has_side_effects=True, vmem_limit_bytes=60 << 20
        ),
        name="tail_reduce",
    )(*inputs.values())
    return dict(zip(outs, values, strict=True))


def split_columns(width):
    return slice(0, width // 2), slice(width // 2, width)


def front_kernel(n_ctx, n_f, names, *refs):
    r = dict(zip(names, refs, strict=True))
    n_z = n_ctx // 2
    c_idx = lax.axis_index("ctx")
    f_idx = lax.axis_index("fsdp")
    y_idx = c_idx % 2
    z_bit = (c_idx // 2) % 2
    x_idx = f_idx // 2
    k_idx = f_idx % 2
    far_idx = flip(f_idx, 2)
    moves = Sender()
    local = []
    at_sem = [0]

    def over_c(mask):
        return (flip(c_idx, mask), f_idx)

    def over_f(mask):
        return (c_idx, flip(f_idx, mask))

    def send(src, dst, peer):
        i = at_sem[0]
        at_sem[0] += 1
        return moves(src, dst, r["send_sem"].at[i], r["recv_sem"].at[i], peer)

    def keep(src, dst):
        copy = pltpu.make_async_copy(src, dst, r["local_sem"].at[len(local)])
        copy.start()
        local.append(copy)
        return copy

    def rows(start, size):
        return pl.ds(pl.multiple_of(start, size), size)

    barrier = pltpu.get_barrier_semaphore()
    for mask in range(1, n_f):
        pl.semaphore_signal(barrier, inc=1, device_id=over_f(mask), device_id_type=MESH)
    for mask in range(1, n_ctx):
        pl.semaphore_signal(barrier, inc=1, device_id=over_c(mask), device_id_type=MESH)
    pl.semaphore_wait(barrier, n_f - 1 + n_ctx - 1)

    infos, tags = r["infos"], r["tags"]
    infos[f_idx] = r["info"][...]
    info_copies = [
        send(infos.at[f_idx], infos.at[f_idx], over_f(mask)) for mask in range(1, n_f)
    ]

    class Rows:
        def __init__(self, shard, dest, bit, hop, chunks):
            self.dest, self.bit, self.hop = dest, bit, hop
            self.shard = shard
            self.size = shard.shape[0]
            self.half = self.size // 2
            self.step = self.half // chunks
            self.chunks = chunks
            self.far, self.next, self.cross = [], [], []

        def start(self, spare=None):
            mine = self.dest.at[rows(f_idx * self.size, self.size)]
            if spare is None:
                self.kept = keep(self.shard, mine)
            else:
                self.spare, self.kept = spare, keep(self.shard, spare)
            self.cross.append(send(self.shard, mine, over_f(1)))

        def settle(self):
            self.kept.wait()
            keep(self.spare, self.dest.at[rows(f_idx * self.size, self.size)])

        def reach(self, i):
            part = self.bit * self.half + i * self.step
            self.far.append(
                send(
                    self.shard.at[rows(part, self.step)],
                    self.dest.at[rows(f_idx * self.size + part, self.step)],
                    over_f(2),
                )
            )

        def place(self, bit, i):
            return self.dest.at[rows(far_idx * self.size + bit * self.half + i * self.step, self.step)]

        def hop_on(self, i):
            self.far[i].wait_recv()
            reach_next()
            here = self.place(self.bit, i)
            self.next.append(send(here, here, over_c(self.hop)))
            self.cross.append(send(here, here, over_f(1)))

        def pass_on(self, i):
            self.next[i].wait_recv()
            here = self.place(1 - self.bit, i)
            self.cross.append(send(here, here, over_f(1)))

        def end(self):
            for copy in self.cross:
                copy.wait_recv()

    class Columns:
        def __init__(self, shard, dest, box, bits, hops):
            self.shard, self.dest, self.box = shard, dest, box
            self.bits, self.hops = bits, hops
            self.size = shard.shape[0]
            self.width = dest.shape[1]
            self.quarter = self.size // 4

        def columns(self, start, count=1):
            return pl.ds(pl.multiple_of(start * self.width, 128), count * self.width)

        def start(self, spare):
            mine = self.dest.at[rows(f_idx * self.size, self.size)]
            self.spare, self.kept = spare, keep(self.shard.at[:, self.columns(f_idx)], spare)
            self.cross = [send(self.shard.at[:, self.columns(flip(f_idx, 1))], mine, over_f(1))]

        def settle(self):
            self.kept.wait()
            keep(self.spare, self.dest.at[rows(f_idx * self.size, self.size)])

        def reach(self, i):
            one, two = self.bits
            at = rows((two * 2 + one) * self.quarter, self.quarter)
            self.far = send(
                self.shard.at[at, self.columns((1 - x_idx) * 2, 2)], self.box.at[at], over_f(2)
            )

        def piece(self, one, two):
            return self.box.at[rows((two * 2 + one) * self.quarter, self.quarter)]

        def first(self):
            one, two = self.bits
            self.far.wait_recv()
            reach_next()
            here = self.piece(one, two)
            self.step = send(here, here, over_c(self.hops[0]))
            self.last = [send(here, here, over_c(self.hops[1]))]

        def second(self):
            one, two = self.bits
            self.step.wait_recv()
            here = self.piece(1 - one, two)
            self.last.append(send(here, here, over_c(self.hops[1])))

        def part(self):
            for copy in self.last:
                copy.wait_recv()
            there = self.dest.at[rows(far_idx * self.size, self.size)]
            self.cross.append(send(self.box.at[:, self.columns(1 - k_idx)], there, over_f(1)))
            keep(self.box.at[:, self.columns(k_idx)], there)

        def end(self):
            for copy in self.cross:
                copy.wait_recv()

    kv = Rows(r["kv_weight"], r["kv_full"], y_idx, 1, 1)
    qd = Rows(r["q_down"], r["qd_full"], y_idx, 1, 1)
    qu = Rows(r["q_up"], r["qu_full"], z_bit, 2, 2)
    left, right = split_columns(r["out_proj"].shape[1])
    outs = [
        Rows(r["out_proj"].at[:, left], r["w_out"].at[:, left], y_idx, 1, 2),
        Rows(r["out_proj"].at[:, right], r["w_out"].at[:, right], z_bit, 2, 2),
    ]
    gate = Columns(r["w_gate"], r["gate_full"], r["gate_box"], (y_idx, z_bit), (1, 2))
    up = Columns(r["w_up"], r["up_full"], r["up_box"], (z_bit, y_idx), (2, 1))
    queue = [(kv, 0), (qd, 0), (qu, 0), (qu, 1), (gate, 0), (up, 0)]
    queue += [(out, i) for i in range(2) for out in outs]

    def reach_next():
        if queue:
            part, i = queue.pop(0)
            part.reach(i)

    reach_next()
    reach_next()
    reach_next()
    kv.start()
    qd.start()

    for copy in info_copies:
        copy.wait_recv()
    d1 = r["gain_one"].shape[1] // n_f // 128
    d2 = r["gain_q"].shape[1] // n_f // 128
    count = infos[0, 2 * d1 + d2 : 2 * d1 + d2 + 1, :]
    for f in range(n_f):
        for i in range(d1):
            col = slice((f * d1 + i) * 128, (f * d1 + i + 1) * 128)
            r["gain_one"][:, col] = infos[f, i : i + 1, :]
            r["gain_two"][:, col] = infos[f, d1 + d2 + i : d1 + d2 + i + 1, :]
        for i in range(d2):
            col = slice((f * d2 + i) * 128, (f * d2 + i + 1) * 128)
            r["gain_q"][:, col] = infos[f, d1 + i : d1 + i + 1, :]
        if f:
            count = count + infos[f, 2 * d1 + d2 : 2 * d1 + d2 + 1, :]
    tags[c_idx] = r["tag"][...]
    tags[c_idx, 1:2, :] = count
    tag_copies = [send(tags.at[c_idx], tags.at[c_idx], over_c(mask)) for mask in range(1, n_ctx)]

    normed = r["normed"]
    gain_one = r["gain_one"][...]

    def norm_rows(at):
        value = r["hidden"][at, :].astype(F32)
        scale = lax.rsqrt(jnp.mean(value * value, axis=-1, keepdims=True) + NORM_EPS)
        normed[at, :] = (value * scale * gain_one).astype(BF16)

    row_loop(normed.shape[0], norm_rows, step=16)

    kv.hop_on(0)
    qd.hop_on(0)
    qu.start()
    kv.pass_on(0)
    qd.pass_on(0)
    kv.end()
    kv.kept.wait()
    head = r["kv_full"].shape[1] // 2
    mid = head // 2
    cos, sin = r["cos"], r["sin"]
    kv_rows = r["kv_rows"]
    keys = jnp.dot(normed[...], r["kv_full"][:, :head], preferred_element_type=F32)
    one, two = keys[:, :mid], keys[:, mid:]
    kv_rows[:, :mid] = (one * cos[...] - two * sin[...]).astype(BF16)
    kv_rows[:, mid:head] = (two * cos[...] + one * sin[...]).astype(BF16)
    kv_rows[:, head:] = jnp.dot(
        normed[...], r["kv_full"][:, head:], preferred_element_type=F32
    ).astype(BF16)
    all_kv = r["all_kv"]
    tokens = normed.shape[0]

    def kv_place(c):
        return all_kv.at[rows(c * tokens, tokens)]

    kv_z = [send(kv_rows, kv_place(c_idx), over_c(2 * s)) for s in range(1, n_z)]
    kv_y = [send(kv_rows, kv_place(c_idx), over_c(1))]
    keep(kv_rows, kv_place(c_idx))
    qu.hop_on(0)
    qd.end()
    qd.kept.wait()

    @pl.loop(0, r["q_low"].shape[1] // 256)
    def _(t):
        at = pl.ds(pl.multiple_of(t * 256, 256), 256)
        r["q_low"][:, at] = jnp.dot(
            normed[...], r["qd_full"][:, at], preferred_element_type=F32
        )

    gain_q = r["gain_q"][...]

    def norm_low(at):
        value = r["q_low"][at, :]
        scale = lax.rsqrt(jnp.mean(value * value, axis=-1, keepdims=True) + NORM_EPS)
        r["q_normed"][at, :] = (value * scale * gain_q).astype(BF16)

    row_loop(tokens, norm_low, step=16)
    qu.hop_on(1)
    gate.first()
    for s in range(1, n_z):
        kv_z[s - 1].wait_recv()
        here = kv_place(flip(c_idx, 2 * s))
        kv_y.append(send(here, here, over_c(1)))
    qu.pass_on(0)
    qu.pass_on(1)
    up.first()
    qu.end()
    gate.start(r["gate_spare"])
    up.start(r["up_spare"])
    outs[0].start(r["out_spare"].at[:, left])
    outs[1].start(r["out_spare"].at[:, right])
    qu.kept.wait()

    @pl.loop(0, r["q_rot"].shape[1] // head)
    def _(h):
        start = pl.multiple_of(h * head, head)
        value = jnp.dot(
            r["q_normed"][...],
            r["qu_full"][:, pl.ds(start, head)],
            preferred_element_type=F32,
        )
        one, two = value[:, :mid], value[:, mid:]
        r["q_rot"][:, pl.ds(start, mid)] = (one * cos[...] - two * sin[...]).astype(BF16)
        late = pl.multiple_of(h * head + mid, mid)
        r["q_rot"][:, pl.ds(late, mid)] = (two * cos[...] + one * sin[...]).astype(BF16)

    for part in [gate, up] + outs:
        part.settle()
    for m in ("kv", "qd", "qu"):
        keep(r[m + "_full"], r["w_" + m])
    gate.second()
    for out in outs:
        out.hop_on(0)
    up.second()
    for out in outs:
        out.hop_on(1)
    gate.part()
    for i in range(2):
        for out in outs:
            out.pass_on(i)
    up.part()
    for copy in kv_y + tag_copies:
        copy.wait_recv()
    for part in [gate, up] + outs:
        part.end()
    for copy in local:
        if not any(copy is part.kept for part in [kv, qd, qu, gate, up] + outs):
            copy.wait()
    moves.finish()


def front(n_ctx, n_f, inputs, head_size):
    tokens, width = inputs["hidden"].shape
    shape = jax.ShapeDtypeStruct
    q_width = inputs["q_down"].shape[1]
    heads_width = inputs["q_up"].shape[1]
    part = inputs["w_gate"].shape[1] // n_f

    def whole(m):
        return (inputs[m].shape[0] * n_f, inputs[m].shape[1])

    in_hbm = ("q_down", "kv_weight", "q_up", "out_proj", "w_gate", "w_up")
    outs = {
        "w_qd": shape(whole("q_down"), BF16),
        "w_kv": shape(whole("kv_weight"), BF16),
        "w_qu": shape(whole("q_up"), BF16),
        "w_out": shape(whole("out_proj"), BF16),
        "gate_full": shape((width, part), BF16),
        "up_full": shape((width, part), BF16),
        "all_kv": shape((tokens * n_ctx, 2 * head_size), BF16),
        "normed": shape((tokens, width), BF16),
        "q_low": shape((tokens, q_width), F32),
        "q_normed": shape((tokens, q_width), BF16),
        "q_rot": shape((tokens, heads_width), BF16),
        "gain_one": shape((1, width), F32),
        "gain_q": shape((1, q_width), F32),
        "gain_two": shape((1, width), F32),
        "tags": shape((n_ctx, 8, 128), F32),
    }
    out_hbm = ("w_qd", "w_kv", "w_qu", "w_out", "gate_full", "up_full", "all_kv")
    box = (inputs["w_gate"].shape[0], 2 * part)
    dma = pltpu.SemaphoreType.DMA
    scratch = {
        "infos": pltpu.VMEM((n_f,) + inputs["info"].shape, F32),
        "qd_full": pltpu.VMEM(whole("q_down"), BF16),
        "kv_full": pltpu.VMEM(whole("kv_weight"), BF16),
        "qu_full": pltpu.VMEM(whole("q_up"), BF16),
        "gate_box": pltpu.VMEM(box, BF16),
        "up_box": pltpu.VMEM(box, BF16),
        "gate_spare": pltpu.VMEM((box[0], part), BF16),
        "up_spare": pltpu.VMEM((box[0], part), BF16),
        "out_spare": pltpu.VMEM(inputs["out_proj"].shape, BF16),
        "kv_rows": pltpu.VMEM((tokens, 2 * head_size), BF16),
        "send_sem": dma((64 + 2 * n_ctx,)),
        "recv_sem": dma((64 + 2 * n_ctx,)),
        "local_sem": dma((24,)),
    }
    vmem = pl.BlockSpec(memory_space=pltpu.VMEM)
    anywhere = pl.BlockSpec(memory_space=pl.ANY)
    names = tuple(inputs) + tuple(outs) + tuple(scratch)
    values = pl.pallas_call(
        functools.partial(front_kernel, n_ctx, n_f, names),
        out_shape=tuple(outs.values()),
        in_specs=[anywhere if m in in_hbm else vmem for m in inputs],
        out_specs=tuple([anywhere if m in out_hbm else vmem for m in outs]),
        scratch_shapes=list(scratch.values()),
        compiler_params=pltpu.CompilerParams(
            collective_id=1, has_side_effects=True, vmem_limit_bytes=48 << 20
        ),
        name="front",
    )(*inputs.values())
    return dict(zip(outs, values, strict=True))


def tiles(total, wide, body):
    whole = total // wide

    @pl.loop(0, whole)
    def _(t):
        body(pl.multiple_of(t * wide, wide), wide)

    if total % wide:
        body(whole * wide, total % wide)


def rows_product_kernel(a_ref, b_ref, o_ref):
    o_ref[...] = contract_last(a_ref[...], b_ref[...]).astype(BF16)


def rows_product(a, b, tile):
    return pl.pallas_call(
        rows_product_kernel,
        out_shape=jax.ShapeDtypeStruct((a.shape[0], b.shape[0]), BF16),
        grid=(b.shape[0] // tile,),
        in_specs=[
            pl.BlockSpec(a.shape, lambda i: (0, 0)),
            pl.BlockSpec((tile, b.shape[1]), lambda i: (i, 0)),
        ],
        out_specs=pl.BlockSpec((a.shape[0], tile), lambda i: (0, i)),
        compiler_params=pltpu.CompilerParams(vmem_limit_bytes=32 << 20),
        name="rows_product",
    )(a, b)


def ffn_kernel(n_f, names, *refs):
    r = dict(zip(names, refs, strict=True))
    c_idx = lax.axis_index("ctx")
    f_idx = lax.axis_index("fsdp")
    moves = Sender()
    at_sem = [0]
    core, far = (c_idx, flip(f_idx, 1)), (c_idx, flip(f_idx, 2))
    beside = (flip(c_idx, 1), f_idx)
    y_idx = c_idx % 2

    def send(src, dst, peer):
        i = at_sem[0]
        at_sem[0] += 1
        return moves(src, dst, r["send_sem"].at[i], r["recv_sem"].at[i], peer)

    barrier = pltpu.get_barrier_semaphore()
    for peer in (core, far, (c_idx, flip(f_idx, 3)), beside):
        pl.semaphore_signal(barrier, inc=1, device_id=peer, device_id_type=MESH)
    pl.semaphore_wait(barrier, 4)

    tokens, width = r["normed"].shape
    mine = r["attn_group"].at[pl.ds(pl.multiple_of(f_idx * tokens, tokens), tokens)]
    own_attn = pltpu.make_async_copy(r["attn_cut"].at[f_idx], mine, r["load_sem"].at[3])
    own_attn.start()

    def send_attn(mask):
        return send(r["attn_cut"].at[flip(f_idx, mask)], mine, (c_idx, flip(f_idx, mask)))

    units = r["w_down"].shape[0]
    group, dz = r["group"], r["dz"]
    block = [slice(i * tokens, (i + 1) * tokens) for i in range(4)]

    def gather(buf):
        to_core = send(buf.at[block[0]], buf.at[block[1]], core)
        to_far = send(buf.at[block[0]], buf.at[block[2]], far)
        return to_core, to_far

    def gather_far(buf, to_far):
        to_far.wait_recv()
        send(buf.at[block[2]], buf.at[block[3]], core).wait_recv()

    group[block[0], :] = r["normed"][...]
    to_core, to_far = gather(group)
    loads = []
    for i, m in enumerate(("gate", "up", "down")):
        load = pltpu.make_async_copy(r["w_" + m], r["v_" + m], r["load_sem"].at[i])
        load.start()
        loads.append(load)
    loads[0].wait()
    loads[1].wait()

    def hidden_part(first):
        @pl.loop(0, 2)
        def _(i):
            hidden_block(pl.ds(pl.multiple_of(first + i * tokens, tokens), tokens))

    def hidden_block(rows):
        def one(start, wide):
            at = pl.ds(start, wide)
            both = jnp.concatenate([r["v_gate"][:, at], r["v_up"][:, at]], axis=1)
            out = jnp.dot(group[rows, :], both, preferred_element_type=F32)
            gate, up = out[:, :wide], out[:, wide:]
            r["gate"][rows, at] = gate.astype(BF16)
            r["up"][rows, at] = up.astype(BF16)
            r["hid"][rows, at] = (gate / (1.0 + jnp.exp(-gate)) * up).astype(BF16)

        tiles(units, 128, one)

    to_core.wait_recv()
    hidden_part(0)
    gather_far(group, to_far)
    attn_copies = [send_attn(1), send_attn(2)]
    hidden_part(2 * tokens)
    loads[2].wait()

    def down_block(i, dest):
        def one(start, wide):
            at = pl.ds(start, wide)
            dest[:, at] = jnp.dot(
                r["hid"][block[i], :], r["v_down"][:, at], preferred_element_type=F32
            ).astype(dest.dtype)

        tiles(width, 256, one)

    def back_block(i, dest):
        def one(start, wide):
            at = pl.ds(start, wide)
            dest[:, at] = (
                contract_last(r["gate"][block[i], :], r["v_gate"][at, :])
                + contract_last(r["up"][block[i], :], r["v_up"][at, :])
            ).astype(dest.dtype)

        tiles(width, 256, one)

    def add_rows(dest, one, two):
        def add(at):
            dest[at, :] = (one[at, :].astype(F32) + two[at, :].astype(F32)).astype(dest.dtype)

        row_loop(tokens, add)

    def far_sum(k, make):
        make(3, r["give"].at[2 * k])
        step = send(r["give"].at[2 * k], r["got"].at[2 * k], core)
        make(2, r["far_sum"])
        step.wait_recv()
        add_rows(r["far_give"].at[k], r["far_sum"], r["got"].at[2 * k])
        return send(r["far_give"].at[k], r["far_got"].at[k], far)

    def near_sum(k, make):
        make(1, r["give"].at[2 * k + 1])
        step = send(r["give"].at[2 * k + 1], r["got"].at[2 * k + 1], core)
        make(0, r["near_sum"])
        return step

    def near_end(k, step):
        step.wait_recv()
        add_rows(r["near_sum"], r["near_sum"], r["got"].at[2 * k + 1])

    far_step = far_sum(0, down_block)
    near_end(0, near_sum(0, down_block))
    far_step.wait_recv()
    r["sq"][...] = jnp.zeros_like(r["sq"])

    def loss_rows(at):
        value = r["resid"][at, :] + r["near_sum"][at, :] + r["far_got"][0, at, :].astype(F32)
        r["result"][at, :] = value.astype(BF16)
        diff = value - r["teacher"][at, :].astype(F32)
        squares = jnp.sum(diff * diff, axis=1, keepdims=True) * r["valid"][at, :]
        r["sq"][:1, :] += jnp.sum(squares, axis=0, keepdims=True)
        grad = diff * r["valid_scale"][at, :1]
        r["grad_resid"][at, :] = grad
        dz[at, :] = grad.astype(BF16)

    row_loop(tokens, loss_rows, step=16)
    to_core, to_far = gather(dz)

    def back_hidden(first):
        @pl.loop(0, 2)
        def _(i):
            back_hidden_block(pl.ds(pl.multiple_of(first + i * tokens, tokens), tokens))

    def back_hidden_block(rows):
        def one(start, wide):
            at = pl.ds(start, wide)
            grad = contract_last(dz[rows, :], r["v_down"][at, :])
            gate = r["gate"][rows, at].astype(F32)
            up = r["up"][rows, at].astype(F32)
            sigma = 1.0 / (1.0 + jnp.exp(-gate))
            r["gate"][rows, at] = (grad * up * sigma * (1.0 + gate * (1.0 - sigma))).astype(BF16)
            r["up"][rows, at] = (grad * (gate * sigma)).astype(BF16)

        tiles(units, 256, one)

    to_core.wait_recv()
    back_hidden(0)
    near_step = near_sum(1, back_block)
    gather_far(dz, to_far)
    saves = []

    def save(src, dst, i):
        copy = pltpu.make_async_copy(src, dst, r["save_sem"].at[i])
        copy.start()
        return copy

    def down_tile(start, wide):
        at = pl.ds(start, wide)
        spot = r["tile"].at[pl.ds(0, wide)]
        left = r["hid"][:, at].T

        def column(start, wide):
            to = pl.ds(start, wide)
            spot[:, to] = jnp.dot(left, dz[:, to], preferred_element_type=F32).astype(BF16)

        tiles(width, 512, column)
        save(spot, r["down_part"].at[at], 0).wait()

    tiles(units, 128, down_tile)
    half = units // 2
    give = pl.ds(pl.multiple_of((1 - y_idx) * half, half), half)
    down_step = send(r["down_part"].at[give], r["down_got"], beside)
    attn_copies.append(send_attn(3))
    back_hidden(2 * tokens)
    far_step = far_sum(1, back_block)
    near_end(1, near_step)

    def gate_tile(start, wide):
        at = pl.ds(start, wide)
        left = group[:, at].T
        for i, m in enumerate(("gate", "up")):
            spot = r["wide_tile"].at[i]

            def column(start, wide, m=m, spot=spot):
                to = pl.ds(start, wide)
                spot[:, to] = jnp.dot(left, r[m][:, to], preferred_element_type=F32).astype(BF16)

            tiles(units, 256, column)
            saves.append(save(spot, r[m + "_part"].at[at], 1 + i))
        saves.pop().wait()
        saves.pop().wait()

    tiles(width, 256, gate_tile)
    far_step.wait_recv()
    gain = r["gain_two"][...]
    r["gain_sum"][...] = jnp.zeros_like(r["gain_sum"])

    def norm_rows(at):
        grad = r["near_sum"][at, :] + r["far_got"][1, at, :].astype(F32)
        value = r["resid"][at, :]
        scale = lax.rsqrt(jnp.mean(value * value, axis=-1, keepdims=True) + NORM_EPS)
        r["gain_sum"][...] += jnp.sum(grad * value * scale, axis=0, keepdims=True)
        ge = gain * grad
        inner = jnp.mean(ge * value, axis=-1, keepdims=True)
        total = r["grad_resid"][at, :] + scale * ge - value * (scale * scale * scale) * inner
        r["grad_resid"][at, :] = total
        r["grad_branch"][at, :] = total.astype(BF16)

    row_loop(tokens, norm_rows, step=16)
    for copy in attn_copies + [down_step]:
        copy.wait_recv()
    own_attn.wait()
    moves.finish()


def feed_forward(n_f, inputs):
    tokens, width = inputs["normed"].shape
    units = inputs["w_down"].shape[0]
    shape = jax.ShapeDtypeStruct
    outs = {
        "result": shape((tokens, width), BF16),
        "grad_resid": shape((tokens, width), F32),
        "grad_branch": shape((tokens, width), BF16),
        "down_part": shape((units, width), BF16),
        "down_got": shape((units // 2, width), BF16),
        "gate_part": shape((width, units), BF16),
        "up_part": shape((width, units), BF16),
        "attn_group": shape((tokens * n_f, inputs["attn_cut"].shape[2]), BF16),
        "gain_sum": shape((1, width), F32),
        "sq": shape((8, 128), F32),
    }
    hbm = ("w_gate", "w_up", "w_down", "attn_cut", "attn_group")
    hbm += ("down_part", "down_got", "gate_part", "up_part")
    dma = pltpu.SemaphoreType.DMA
    many = tokens * n_f
    scratch = {
        "v_gate": pltpu.VMEM((width, units), BF16),
        "v_up": pltpu.VMEM((width, units), BF16),
        "v_down": pltpu.VMEM((units, width), BF16),
        "group": pltpu.VMEM((many, width), BF16),
        "dz": pltpu.VMEM((many, width), BF16),
        "gate": pltpu.VMEM((many, units), BF16),
        "up": pltpu.VMEM((many, units), BF16),
        "hid": pltpu.VMEM((many, units), BF16),
        "give": pltpu.VMEM((4, tokens, width), BF16),
        "got": pltpu.VMEM((4, tokens, width), BF16),
        "far_sum": pltpu.VMEM((tokens, width), F32),
        "near_sum": pltpu.VMEM((tokens, width), F32),
        "far_give": pltpu.VMEM((2, tokens, width), BF16),
        "far_got": pltpu.VMEM((2, tokens, width), BF16),
        "tile": pltpu.VMEM((128, width), BF16),
        "wide_tile": pltpu.VMEM((2, 256, units), BF16),
        "send_sem": dma((16,)),
        "recv_sem": dma((16,)),
        "load_sem": dma((4,)),
        "save_sem": dma((3,)),
    }
    vmem = pl.BlockSpec(memory_space=pltpu.VMEM)
    anywhere = pl.BlockSpec(memory_space=pl.ANY)
    names = tuple(inputs) + tuple(outs) + tuple(scratch)
    values = pl.pallas_call(
        functools.partial(ffn_kernel, n_f, names),
        out_shape=tuple(outs.values()),
        in_specs=[anywhere if m in hbm else vmem for m in inputs],
        out_specs=tuple([anywhere if m in hbm else vmem for m in outs]),
        scratch_shapes=list(scratch.values()),
        compiler_params=pltpu.CompilerParams(
            collective_id=2, has_side_effects=True, vmem_limit_bytes=60 << 20
        ),
        name="feed_forward",
    )(*inputs.values())
    return dict(zip(outs, values, strict=True))


def body(
    hidden_in,
    teacher,
    blocks,
    seq_ids,
    valid_mask,
    norm1_gain,
    q_down,
    q_gain,
    q_up,
    kv_weight,
    out_proj,
    norm2_gain,
    w_gate,
    w_up,
    w_down,
):
    row_count, model_width = hidden_in.shape
    head_size = kv_weight.shape[1] // 2
    heads_width = q_up.shape[1]
    head_count = heads_width // head_size
    half_dim = head_size // 2
    q_width = q_down.shape[1]
    n_ctx = lax.axis_size("ctx")
    n_f = lax.axis_size("fsdp")
    n_z = n_ctx // 2
    token_total = row_count * n_ctx * n_f
    seq_pieces = 2 * SEQ_BLOCKS
    c_idx = lax.axis_index("ctx")
    f_idx = lax.axis_index("fsdp")
    y_idx = c_idx % 2
    z_idx = c_idx // 2
    x_idx = f_idx // 2
    k_idx = f_idx % 2

    def by_f(values, mask):
        return lax.ppermute(values, "fsdp", [(i, i ^ mask) for i in range(n_f)])

    def by_c(values, mask):
        return lax.ppermute(values, "ctx", [(i, i ^ mask) for i in range(n_ctx)])

    def cut(values, start, size, axis):
        return lax.dynamic_slice_in_dim(values, start, size, axis)

    def ctx_split(grad):
        view = grad.reshape(n_z, 2, grad.shape[0] // n_ctx, grad.shape[1])
        give = lax.dynamic_index_in_dim(view, 1 - y_idx, 1, keepdims=False)
        keep = lax.dynamic_index_in_dim(view, y_idx, 1, keepdims=False)
        return give, keep

    def ctx_pair(keep, got):
        return (keep.astype(F32) + got.astype(F32)).astype(BF16)

    def ctx_spread(pair):
        return [pair] + [
            by_c(lax.dynamic_index_in_dim(pair, z_idx ^ r, 0, keepdims=False), 2 * r)
            for r in range(1, n_z)
        ]

    def ctx_total(parts):
        total = lax.dynamic_index_in_dim(parts[0], z_idx, 0, keepdims=False).astype(F32)
        for got in parts[1:]:
            total = total + got.astype(F32)
        return total

    def group_rows(values):
        return lax.all_gather(values, "fsdp", axis=0, tiled=True)

    valid_f = valid_mask.astype(F32)
    own_pieces = row_count // PIECE
    info = jnp.concatenate(
        [
            norm1_gain.astype(F32),
            q_gain.astype(F32),
            norm2_gain.astype(F32),
            jnp.full((128,), jnp.sum(valid_f)),
        ]
    )
    info = jnp.pad(info, (0, -info.shape[0] % 1024)).reshape(-1, 128)
    own_tags = jnp.stack([blocks.reshape(-1, PIECE)[:, 0], seq_ids.reshape(-1, PIECE)[:, 0]], 1)
    tag = jnp.pad(own_tags.astype(F32).reshape(1, -1), ((0, 7), (0, 128 - 2 * own_pieces)))
    own = jnp.concatenate([blocks.reshape(-1, PIECE)[:, 0], seq_ids[:1]])

    positions = blocks * PIECE + jnp.arange(row_count, dtype=jnp.int32) % PIECE
    freq_table = 10000.0 ** (-(jnp.arange(half_dim, dtype=F32) * 2.0 / head_size))
    angle_table = positions.astype(F32)[:, None] * freq_table[None, :]
    cosine = jnp.cos(angle_table)
    sine = jnp.sin(angle_table)
    fetched = front(
        n_ctx,
        n_f,
        {
            "q_down": q_down,
            "kv_weight": kv_weight,
            "q_up": q_up,
            "out_proj": out_proj,
            "w_gate": w_gate,
            "w_up": w_up,
            "hidden": hidden_in,
            "info": info,
            "tag": tag,
            "cos": cosine,
            "sin": sine,
        },
        head_size,
    )
    w_out = fetched["w_out"]
    all_kv, q_rot = fetched["all_kv"], fetched["q_rot"]
    normed, q_low, q_normed = fetched["normed"], fetched["q_low"], fetched["q_normed"]
    gain_one, gain_q, gain_two = fetched["gain_one"], fetched["gain_q"], fetched["gain_two"]
    tags = fetched["tags"][:, 0, : 2 * own_pieces].reshape(-1, 2).astype(jnp.int32)
    total_count = jnp.sum(fetched["tags"][:, 1, 0])
    hidden_f = hidden_in.astype(F32)
    scale_q = rms_scale(q_low)

    out_block = heads_width // (n_ctx * n_f)
    if out_block == 128:
        attn_heads, lse, attn_cut = attn_fwd(
            tags, own, q_rot, all_kv, head_size, seq_pieces, n_f, True
        )
    else:
        attn_heads, lse = attn_fwd(tags, own, q_rot, all_kv, head_size, seq_pieces, n_f, False)
        attn_cut = attn_heads.reshape(row_count, n_ctx, n_f, out_block).transpose(2, 0, 1, 3)
        attn_cut = attn_cut.reshape(n_f, row_count, n_ctx * out_block)
    resid = hidden_f + dot(attn_heads, w_out)
    scale_two = rms_scale(resid)
    normed_two = (resid * scale_two * gain_two).astype(BF16)

    wide_valid = jnp.broadcast_to(valid_f[:, None], (row_count, 128))
    ffn = feed_forward(
        n_f,
        {
            "normed": normed_two,
            "resid": resid,
            "teacher": teacher,
            "valid": wide_valid,
            "valid_scale": wide_valid * (token_total / total_count),
            "gain_two": gain_two,
            "w_gate": fetched["gate_full"],
            "w_up": fetched["up_full"],
            "w_down": w_down,
            "attn_cut": attn_cut,
        },
    )
    grad_resid, grad_branch = ffn["grad_resid"], ffn["grad_branch"]
    grad_gain_two = ffn["gain_sum"].reshape(-1)
    sq_local = ffn["sq"][0, 0]
    half_units = w_down.shape[0] // 2
    down_pair = ctx_pair(cut(ffn["down_part"], y_idx * half_units, half_units, 0), ffn["down_got"])
    down_parts = ctx_spread(down_pair.reshape(n_z, -1, model_width))
    gate_give, gate_keep = ctx_split(ffn["gate_part"])
    gate_got = by_c(gate_give, 1)
    early = n_z // 2
    up_blocks = ffn["up_part"].reshape(n_z, 2, model_width // n_ctx, -1)
    up_got = by_c(
        lax.dynamic_index_in_dim(up_blocks[:early], 1 - y_idx, 1, keepdims=False), 1
    )
    branch_group = group_rows(grad_branch)
    grad_attn = rows_product(grad_branch, w_out, 256)
    grad_qlin, grad_seq = attn_bwd(
        tags, own, q_rot, grad_attn, attn_heads, lse, cosine, sine, all_kv, head_size, seq_pieces
    )
    qlin_group = lax.all_to_all(grad_qlin, "fsdp", 1, 0, tiled=True)
    down_parts, gate_got, grad_seq = together(down_parts, gate_got, grad_seq)

    by_piece = grad_seq.reshape(seq_pieces, PIECE, 2 * head_size)
    piece_tag = tags[:, 0].reshape(n_z, 2, own_pieces)
    piece_own = (tags[:, 1] == seq_ids[0]).reshape(n_z, 2, own_pieces)

    def kv_half(bit):
        places = lax.dynamic_index_in_dim(piece_tag, bit, 1, keepdims=False).reshape(-1)
        picked = by_piece[places]
        if n_ctx * own_pieces != seq_pieces:
            mine = lax.dynamic_index_in_dim(piece_own, bit, 1, keepdims=False).reshape(-1)
            picked = jnp.where(mine[:, None, None], picked, jnp.zeros_like(picked))
        return picked.reshape(n_z, own_pieces * PIECE, 2 * head_size)

    kv_part = jnp.stack([kv_half(0), kv_half(1)], axis=1)
    q_cut, kv_cut = q_width // n_f, 2 * head_size // n_f
    qnorm_group = group_rows(q_normed)
    normed_group = group_rows(normed)

    grad_qnormed = dot_t(grad_qlin, fetched["w_qu"])
    grad_qlow_f, grad_gain_q = rms_back(q_low, scale_q, gain_q, grad_qnormed)
    grad_qlow = grad_qlow_f.astype(BF16)
    attn_group = ffn["attn_group"]
    da_q = dot_t(grad_qlow, fetched["w_qd"])
    gate_pair = ctx_pair(gate_keep, gate_got)
    out_part = dot_rows(attn_group, branch_group).astype(BF16)
    qup_part = dot_rows(qnorm_group, qlin_group).astype(BF16)

    def by_ctx(grad):
        return grad.reshape(n_z, 2, grad.shape[0] // n_ctx, grad.shape[1])

    order = [
        (c * n_f + f, f * n_ctx + c % 2 * n_z + c // 2) for c in range(n_ctx) for f in range(n_f)
    ]
    down_rows = ctx_total(down_parts).astype(BF16)
    down_sent = lax.ppermute(down_rows, ("ctx", "fsdp"), order)

    up_got, out_part, qup_part = together(up_got, out_part, qup_part)

    small = jnp.concatenate(
        [jnp.zeros((model_width,), F32), grad_gain_q, grad_gain_two, sq_local.reshape(1)]
    )
    entries = small.shape[0]
    small = jnp.pad(small, (0, -entries % 1024)).reshape(-1, 128)
    ends = tail_reduce(
        n_ctx,
        n_f,
        {
            "gate": gate_pair,
            "kv": kv_part,
            "up": up_blocks,
            "up_got": up_got,
            "out": by_ctx(out_part),
            "qup": by_ctx(qup_part),
            "dqa": grad_qlow,
            "cos": cosine,
            "sin": sine,
            "normed_group": normed_group,
            "w_kv": fetched["w_kv"],
            "da_q": da_q,
            "hidden": hidden_in,
            "gain_one": gain_one,
            "grad_resid": grad_resid,
            "small": small,
        },
        q_width,
    )
    small, down_sent = together(ends["small_out"], down_sent)
    small = small.reshape(-1)[:entries]
    grad_down = down_sent.astype(F32)

    device = c_idx * n_f + f_idx
    q1, q2 = model_width, model_width + q_width
    n_dev = n_ctx * n_f

    def own_part(values):
        size = values.shape[0] // n_dev
        return cut(values, device * size, size, 0)

    loss_now = small[-1] / (model_width * total_count)
    return (
        ffn["result"],
        loss_now,
        ends["grad_input"],
        own_part(small[:q1]),
        ends["out_qd"],
        own_part(small[q1:q2]),
        ends["out_qup"],
        ends["out_kvw"],
        ends["out_out"],
        own_part(small[q2 : q2 + model_width]),
        ends["out_gate"],
        ends["out_up"],
        grad_down,
    )


def solution(mesh):
    both = ("ctx", "fsdp")
    rows = P(both, None)
    flat = P(both)
    shard = P("fsdp", None)
    gain = P("fsdp")
    return jax.shard_map(
        body,
        mesh=mesh,
        in_specs=(
            rows,
            rows,
            flat,
            flat,
            flat,
            gain,
            shard,
            gain,
            shard,
            shard,
            shard,
            gain,
            shard,
            shard,
            shard,
        ),
        out_specs=(
            rows,
            P(),
            rows,
            flat,
            rows,
            flat,
            rows,
            rows,
            rows,
            flat,
            rows,
            rows,
            rows,
        ),
        check_vma=False,
    )
```

```python
import functools
import math

import jax
import jax.numpy as jnp
from jax import lax
from jax.experimental import pallas as pl
from jax.experimental.pallas import tpu as pltpu
from jax.sharding import PartitionSpec as P

PIECE = 128
SEQ_BLOCKS = 8
NORM_EPS = 1e-05
F32 = jnp.float32
BF16 = jnp.bfloat16
LOG2E = math.log2(math.e)
HEAD_GROUP = 16


def rms_scale(values):
    return lax.rsqrt(jnp.mean(values * values, axis=-1, keepdims=True) + NORM_EPS)


def rms_back(values, scale, gain, grad):
    grad_gain = jnp.sum(grad * values * scale, axis=0)
    ge = gain * grad
    inner = jnp.mean(ge * values, axis=-1, keepdims=True)
    return scale * ge - values * (scale * scale * scale) * inner, grad_gain


def rope_apply(values, cosine, sine):
    half_dim = values.shape[-1] // 2
    one = values[..., :half_dim]
    two = values[..., half_dim:]
    return jnp.concatenate([one * cosine - two * sine, two * cosine + one * sine], axis=-1)


def rope_back(grads, cosine, sine):
    half_dim = grads.shape[-1] // 2
    one = grads[..., :half_dim]
    two = grads[..., half_dim:]
    return jnp.concatenate([one * cosine + two * sine, two * cosine - one * sine], axis=-1)


def together(*values):
    return lax.optimization_barrier(values)


def dot(a, b):
    return jnp.dot(a, b, preferred_element_type=F32)


def dot_t(a, b):
    return lax.dot_general(a, b, (((1,), (1,)), ((), ())), preferred_element_type=F32)


def dot_rows(a, b):
    return lax.dot_general(a, b, (((0,), (0,)), ((), ())), preferred_element_type=F32)


def contract_last(a, b):
    return lax.dot_general(a, b, (((1,), (1,)), ((), ())), preferred_element_type=F32)

def find_pieces(tags_ref, own_ref, pick_ref, total):
    @pl.loop(0, total)
    def _(u):
        @pl.when(tags_ref[u, 1] == own_ref[2])
        def _():
            pick_ref[tags_ref[u, 0]] = u

def stack_heads(ref, hd):
    return jnp.concatenate([ref[:, h*hd:(h+1)*hd] for h in range(HEAD_GROUP)], axis=0)

def attn_fwd_kernel(n_f, tags_ref, own_ref, q_ref, kv_ref, o_ref, lse_ref, *rest):
    k_s, vt_s, acc_s, pick_s = rest[-4:]
    half = pl.program_id(0)
    hd = k_s.shape[1]
    pieces = k_s.shape[0] // PIECE
    total = kv_ref.shape[0] // PIECE
    wide = 2 * PIECE
    coef = hd ** -0.5 * LOG2E

    @pl.when((half == 0) & (pl.program_id(1) == 0))
    def _():
        find_pieces(tags_ref, own_ref, pick_s, total)
        for i in range(pieces):
            rows = pl.ds(pl.multiple_of(pick_s[i] * PIECE, PIECE), PIECE)
            k_s[i*PIECE:(i+1)*PIECE, :] = kv_ref[rows, :hd]
            vt_s[:, i*PIECE:(i+1)*PIECE] = kv_ref[rows, hd:].T

    q = stack_heads(q_ref, hd)
    acc_s[...] = jnp.zeros_like(acc_s)
    rows = q.shape[0]
    def step(i, carry):
        peak, total_p = carry
        at = pl.ds(pl.multiple_of(i * wide, wide), wide)
        raw = contract_last(k_s[at, :], q)
        top = jnp.maximum(peak, jnp.max(raw, axis=0, keepdims=True))
        fade = jnp.exp2((peak - top) * coef)
        p = jnp.exp2((raw - top) * coef)
        acc_s[...] = acc_s[...] * fade + jnp.dot(vt_s[:, at], p.astype(BF16), preferred_element_type=F32)
        return top, total_p * fade + jnp.sum(p, axis=0, keepdims=True)
    count = own_ref[half] // 2 + 1
    peak, total_p = lax.fori_loop(0, count, step, (jnp.full((1, rows), -1e30, F32), jnp.zeros((1, rows), F32)))
    out = (acc_s[...] / total_p).astype(BF16).T
    for h in range(HEAD_GROUP):
        o_ref[:, h*hd:(h+1)*hd] = out[h*PIECE:(h+1)*PIECE, :]
    if len(rest) > 4:
        for b in range(HEAD_GROUP * hd // 128):
            head, part = b * 128 // hd, b * 128 % hd
            rest[0][b % n_f, :, b // n_f * 128:(b // n_f + 1) * 128] = out[
                head*PIECE:(head+1)*PIECE, part:part+128
            ]
    lse_ref[0] = peak * coef + jnp.log2(total_p)

def attn_fwd(tags, own, q, kv, hd, pieces, n_f, cut):
    n_rows, width = q.shape
    groups = width // hd // HEAD_GROUP
    gw = HEAD_GROUP * hd
    halves = n_rows // PIECE
    rows = HEAD_GROUP * PIECE
    blk = pl.BlockSpec((PIECE, gw), lambda p, g, *_: (p, g))
    flops = 4 * n_rows * width * pieces * PIECE * 9 // 16
    shapes = [jax.ShapeDtypeStruct(q.shape, BF16), jax.ShapeDtypeStruct((halves*groups, 1, rows), F32)]
    specs = [blk, pl.BlockSpec((1, 1, rows), lambda p, g, *_: (p*groups+g, 0, 0))]
    if cut:
        shapes.append(jax.ShapeDtypeStruct((n_f, n_rows, width // n_f), BF16))
        specs.append(pl.BlockSpec((n_f, PIECE, gw // n_f), lambda p, g, *_: (0, p, g)))
    return pl.pallas_call(
        functools.partial(attn_fwd_kernel, n_f),
        out_shape=tuple(shapes),
        grid_spec=pltpu.PrefetchScalarGridSpec(
            num_scalar_prefetch=2, grid=(halves, groups),
            in_specs=[blk, pl.BlockSpec(kv.shape, lambda p, g, *_: (0, 0))],
            out_specs=tuple(specs),
            scratch_shapes=[pltpu.VMEM((pieces*PIECE, hd), BF16), pltpu.VMEM((hd, pieces*PIECE), BF16),
                            pltpu.VMEM((hd, rows), F32), pltpu.SMEM((pieces,), jnp.int32)]),
        compiler_params=pltpu.CompilerParams(vmem_limit_bytes=40 << 20),
        cost_estimate=pl.CostEstimate(flops=flops, transcendentals=flops//(4*hd), bytes_accessed=2*(2*q.size+kv.size)),
        name="attn_fwd",
    )(tags, own, q, kv)

def attn_bwd_kernel(tags_ref, own_ref, q_ref, do_ref, o_ref, lse_ref, cos_ref, sin_ref, kv_ref, dq_ref, dkv_ref,
                    k_s, kt_s, v_s, dq_s, dk_s, dv_s, pick_s):
    half = pl.program_id(0)
    group = pl.program_id(1)
    hd = k_s.shape[1]
    pieces = k_s.shape[0] // PIECE
    total = kv_ref.shape[0] // PIECE
    wide = 2 * PIECE
    coef = hd ** -0.5 * LOG2E
    scale = hd ** -0.5

    @pl.when((half == 0) & (group == 0))
    def _():
        find_pieces(tags_ref, own_ref, pick_s, total)
        for i in range(pieces):
            rows = pl.ds(pl.multiple_of(pick_s[i] * PIECE, PIECE), PIECE)
            keys = kv_ref[rows, :hd]
            k_s[i*PIECE:(i+1)*PIECE, :] = keys
            kt_s[:, i*PIECE:(i+1)*PIECE] = keys.T
            v_s[i*PIECE:(i+1)*PIECE, :] = kv_ref[rows, hd:]
        dk_s[...] = jnp.zeros_like(dk_s)
        dv_s[...] = jnp.zeros_like(dv_s)

    q = stack_heads(q_ref, hd)
    do = stack_heads(do_ref, hd)
    prod = do.astype(F32) * stack_heads(o_ref, hd).astype(F32)
    delta = lax.dot_general(jnp.ones((8, hd), F32), prod, (((1,), (1,)), ((), ())),
                            preferred_element_type=F32, precision=lax.Precision.HIGHEST)[:1]
    lse = lse_ref[0]
    dq_s[...] = jnp.zeros_like(dq_s)
    def step(i, carry):
        at = pl.ds(pl.multiple_of(i * wide, wide), wide)
        p = jnp.exp2(contract_last(k_s[at, :], q) * coef - lse)
        dp = contract_last(v_s[at, :], do)
        ds = (p * (dp - delta)).astype(BF16)
        dv_s[at, :] += jnp.dot(p.astype(BF16), do, preferred_element_type=F32)
        dk_s[at, :] += jnp.dot(ds, q, preferred_element_type=F32)
        dq_s[...] += jnp.dot(kt_s[:, at], ds, preferred_element_type=F32)
        return carry
    lax.fori_loop(0, own_ref[half] // 2 + 1, step, 0)
    dq = (dq_s[...] * scale).T
    cos, sin = cos_ref[...], sin_ref[...]
    mid = hd // 2
    for h in range(HEAD_GROUP):
        one = dq[h*PIECE:(h+1)*PIECE, :mid]
        two = dq[h*PIECE:(h+1)*PIECE, mid:]
        dq_ref[:, h*hd:h*hd+mid] = (one * cos + two * sin).astype(BF16)
        dq_ref[:, h*hd+mid:(h+1)*hd] = (two * cos - one * sin).astype(BF16)

    @pl.when((half == pl.num_programs(0) - 1) & (group == pl.num_programs(1) - 1))
    def _():
        dkv_ref[:, :hd] = (dk_s[...] * scale).astype(BF16)
        dkv_ref[:, hd:] = dv_s[...].astype(BF16)

def attn_bwd(tags, own, q, do, o, lse, cos, sin, kv, hd, pieces):
    n_rows, width = q.shape
    groups = width // hd // HEAD_GROUP
    gw = HEAD_GROUP * hd
    halves = n_rows // PIECE
    rows = HEAD_GROUP * PIECE
    blk = pl.BlockSpec((PIECE, gw), lambda p, g, *_: (p, g))
    trig = pl.BlockSpec((PIECE, hd // 2), lambda p, g, *_: (p, 0))
    keys = pieces * PIECE
    return pl.pallas_call(
        attn_bwd_kernel,
        out_shape=(jax.ShapeDtypeStruct(q.shape, BF16), jax.ShapeDtypeStruct((keys, 2*hd), BF16)),
        grid_spec=pltpu.PrefetchScalarGridSpec(
            num_scalar_prefetch=2, grid=(halves, groups),
            in_specs=[blk, blk, blk, pl.BlockSpec((1, 1, rows), lambda p, g, *_: (p*groups+g, 0, 0)), trig, trig,
                      pl.BlockSpec(kv.shape, lambda p, g, *_: (0, 0))],
            out_specs=[blk, pl.BlockSpec((keys, 2*hd), lambda p, g, *_: (0, 0))],
            scratch_shapes=[pltpu.VMEM((keys, hd), BF16), pltpu.VMEM((hd, keys), BF16), pltpu.VMEM((keys, hd), BF16),
                            pltpu.VMEM((hd, rows), F32), pltpu.VMEM((keys, hd), F32), pltpu.VMEM((keys, hd), F32),
                            pltpu.SMEM((pieces,), jnp.int32)]),
        compiler_params=pltpu.CompilerParams(vmem_limit_bytes=48 << 20),
        name="attn_bwd",
    )(tags, own, q, do, o, lse, cos, sin, kv)

MESH = pl.DeviceIdType.MESH


def flip(index, mask):
    out = 0
    bit = 1
    while bit <= mask:
        part = (index // bit) % 2
        out = out + bit * ((1 - part) if mask & bit else part)
        bit *= 2
    return out + (index // bit) * bit


def row_loop(rows, body, step=32):
    if rows % step:
        step = 16

    @pl.loop(0, rows // step)
    def _(i):
        body(pl.ds(pl.multiple_of(i * step, step), step))


class Sender:
    def __init__(self):
        self.open = []

    def make(self, src, dst, send_sem, recv_sem, peer):
        return pltpu.make_async_remote_copy(
            src_ref=src,
            dst_ref=dst,
            send_sem=send_sem,
            recv_sem=recv_sem,
            device_id=peer,
            device_id_type=MESH,
        )

    def __call__(self, *args):
        copy = self.make(*args)
        copy.start()
        self.open.append(copy)
        return copy

    def finish(self):
        for copy in self.open:
            copy.wait_send()


class LineSum:
    def __init__(self, own, got, send_sem, recv_sem, c_idx, f_idx, n_z, sender):
        self.own, self.got, self.send_sem, self.recv_sem = own, got, send_sem, recv_sem
        self.n_z, self.sender = n_z, sender
        self.z = c_idx // 2
        self.left = (c_idx - 2, f_idx)
        self.right = (c_idx + 2, f_idx)

    def copy(self, b, slot, peer):
        return self.sender.make(
            self.own.at[b], self.got.at[slot], self.send_sem.at[b], self.recv_sem.at[slot], peer
        )

    def take(self, b, slot):
        self.copy(b, slot, self.left).wait_recv()

        def add(at):
            self.own[b, at, :] = (
                self.own[b, at, :].astype(F32) + self.got[slot, at, :].astype(F32)
            ).astype(BF16)

        row_loop(self.own.shape[1], add)

    def go_right(self, b):
        z = self.z

        @pl.when(z < b)
        def _():
            @pl.when(z > 0)
            def _():
                self.take(b, b)

            self.copy(b, b, self.right).start()

    def go_left(self, b):
        z, n_z = self.z, self.n_z

        @pl.when(z > b)
        def _():
            @pl.when(z < n_z - 1)
            def _():
                self.take(b, b)

            @pl.when(z - 1 > b)
            def _():
                self.copy(b, b, self.left).start()

            @pl.when(z - 1 == b)
            def _():
                self.copy(b, n_z, self.left).start()

    def step(self, i):
        @pl.when(2 * self.z < self.n_z)
        def _():
            self.go_right(self.n_z - 1 - i)
            self.go_left(i)

        @pl.when(2 * self.z >= self.n_z)
        def _():
            self.go_left(i)
            self.go_right(self.n_z - 1 - i)

    def total(self, store):
        z, n_z = self.z, self.n_z

        @pl.when(z > 0)
        def _():
            self.copy(z, z, self.left).wait_recv()

        @pl.when(z < n_z - 1)
        def _():
            self.copy(z, n_z, self.left).wait_recv()

        rows = self.own.shape[1]

        @pl.when(z == 0)
        def _():
            row_loop(
                rows,
                lambda at: store(
                    at, self.own[z, at, :].astype(F32) + self.got[n_z, at, :].astype(F32)
                ),
            )

        @pl.when(z == n_z - 1)
        def _():
            row_loop(
                rows,
                lambda at: store(
                    at, self.own[z, at, :].astype(F32) + self.got[z, at, :].astype(F32)
                ),
            )

        @pl.when((z > 0) & (z < n_z - 1))
        def _():
            row_loop(
                rows,
                lambda at: store(
                    at,
                    self.own[z, at, :].astype(F32)
                    + self.got[z, at, :].astype(F32)
                    + self.got[n_z, at, :].astype(F32),
                ),
            )

    def finish(self):
        for b in range(self.n_z):

            @pl.when(self.z != b)
            def _(b=b):
                self.copy(b, b, self.left).wait_send()


WINDOW = 3
TAIL_NAMES = ("gate", "kv", "up", "out", "qup", "low")
TAIL_CUT = ("gate", "up", "qup", "low")
TAIL_SENT = ("kv", "up", "out", "qup", "low")


def tail_kernel(n_ctx, n_f, names_in, names_out, names_scratch, *refs):
    n_z = n_ctx // 2
    names = list(names_in) + list(names_out) + list(names_scratch)
    r = dict(zip(names, refs, strict=True))
    c_idx = lax.axis_index("ctx")
    f_idx = lax.axis_index("fsdp")
    y_idx = c_idx % 2
    z_idx = c_idx // 2
    send = Sender()

    def over_c(mask):
        return (flip(c_idx, mask), f_idx)

    def over_f(mask):
        return (c_idx, flip(f_idx, mask))

    barrier = pltpu.get_barrier_semaphore()
    for mask in range(1, n_f):
        pl.semaphore_signal(barrier, inc=1, device_id=over_f(mask), device_id_type=MESH)
    for mask in range(1, n_ctx):
        pl.semaphore_signal(barrier, inc=1, device_id=over_c(mask), device_id_type=MESH)
    pl.semaphore_wait(barrier, n_f - 1 + n_ctx - 1)

    lines = {
        m: LineSum(
            r["pair_" + m],
            r["z_" + m],
            r["z_send"].at[i],
            r["z_recv"].at[i],
            c_idx,
            f_idx,
            n_z,
            send,
        )
        for i, m in enumerate(TAIL_NAMES)
    }
    y_copies, keeps = {}, {}
    early = r["up_got"].shape[0]

    parts = {m: r[m] for m in ("kv", "up", "out", "qup")}
    parts["low"] = r["part_low"]
    queue = [
        (m, b) for m in TAIL_SENT for b in range(n_z) if m != "up" or b >= early
    ]
    owed = tuple(queue)

    def next_y():
        if queue:
            m, b = queue.pop(0)
            i = TAIL_SENT.index(m)
            y_copies[m, b] = send(
                parts[m].at[b, 1 - y_idx],
                r["y_" + m].at[b],
                r["y_send"].at[i, b],
                r["y_recv"].at[i, b],
                over_c(1),
            )
            take_own(m, b)

    def take_own(m, b):
        keep = pltpu.make_async_copy(
            parts[m].at[b, y_idx],
            r["pair_" + m].at[b],
            r["keep_sem"].at[TAIL_SENT.index(m), b],
        )
        keep.start()
        keeps[m, b] = keep

    def add_pair(m, b):
        y_copies[m, b].wait_recv()
        next_y()
        add_ready(m, b)

    def add_ready(m, b):
        keeps[m, b].wait()
        pair, got = r["pair_" + m], r["y_" + m]

        def add(at):
            pair[b, at, :] = (pair[b, at, :].astype(F32) + got[b, at, :].astype(F32)).astype(BF16)

        row_loop(pair.shape[1], add)

    def advance(pair, line):
        if pair == "up":
            here.wait()
            for b in range(early):
                add_ready(pair, b)
        for b in range(n_z):
            if pair is not None and (pair, b) in owed:
                add_pair(pair, b)
            if line is not None and b < n_z - 1:
                lines[line].step(b)

    f_copies = {}

    def finish_sum(m):
        lines[m].total(lambda at, value: store_total(m, at, value))
        if m in TAIL_CUT:
            i = TAIL_CUT.index(m)
            part = r["tot_" + m].shape[0] // n_f
            for s in range(1, n_f):
                at = pl.ds(pl.multiple_of(flip(f_idx, s) * part, part), part)
                f_copies[m, s] = send(
                    r["tot_" + m].at[at, :],
                    r["f_" + m].at[s - 1],
                    r["f_send"].at[i, s - 1],
                    r["f_recv"].at[i, s - 1],
                    over_f(s),
                )

    def store_total(m, at, value):
        if m in TAIL_CUT:
            r["tot_" + m][at, :] = value.astype(BF16)
        else:
            r["out_" + m][at, :] = value

    def put_out(m):
        total = r["tot_" + m]
        rows, width = total.shape
        part = rows // n_f
        cuts = {"out_" + m: (0, width)}
        if m == "low":
            split = r["qd_group"].shape[1]
            cuts = {"out_qd": (0, split), "out_kvw": (split, width - split)}
        for s in range(n_f):
            source = flip(f_idx, s)
            if s:
                f_copies[m, s].wait_recv()
                got = r["f_" + m].at[s - 1]
            else:
                got = total.at[pl.ds(pl.multiple_of(f_idx * part, part), part)]
            for name, (start, wide) in cuts.items():
                at = pl.ds(pl.multiple_of(source * wide, 128), wide)
                r[name][:, at] = got[:, start : start + wide].astype(F32)

    def cut_low(src, dst, width, index):
        rows = src.shape[0]
        mine = pl.ds(pl.multiple_of(f_idx * rows, rows), rows)
        copies = []
        for s in range(1, n_f):
            at = pl.ds(pl.multiple_of(flip(f_idx, s) * width, 128), width)
            copies.append(
                send(
                    src.at[:, at],
                    dst.at[mine, :],
                    r["low_send"].at[index, s - 1],
                    r["low_recv"].at[index, s - 1],
                    over_f(s),
                )
            )
        own = pl.ds(pl.multiple_of(f_idx * width, 128), width)
        dst[mine, :] = src[:, own]
        return copies

    for _ in range(WINDOW):
        next_y()
    q_copies = cut_low(r["dqa"], r["qd_group"], r["qd_group"].shape[1], 0)
    pair_in = pltpu.make_async_copy(r["gate"], r["pair_gate"], r["keep_sem"].at[0, n_z])
    pair_in.start()
    here = pltpu.make_async_copy(
        r["up_got"], r["y_up"].at[pl.ds(0, early)], r["keep_sem"].at[1, n_z]
    )
    here.start()
    for b in range(early):
        take_own("up", b)
    pair_in.wait()
    advance("kv", "gate")
    advance("up", "kv")
    finish_sum("gate")

    head = r["dkv"].shape[1] // 2
    mid = head // 2

    def store_kv(at, value):
        cos, sin = r["cos"][at, :], r["sin"][at, :]
        one, two = value[:, :mid], value[:, mid:head]
        r["dkv"][at, :mid] = (one * cos + two * sin).astype(BF16)
        r["dkv"][at, mid:head] = (two * cos - one * sin).astype(BF16)
        r["dkv"][at, head:] = value[:, head:].astype(BF16)

    lines["kv"].total(store_kv)
    kv_copies = cut_low(r["dkv"], r["kv_group"], r["kv_group"].shape[1], 1)

    def low_part(group, start):
        normed, part = r["normed_group"], r["part_low"]
        rows = part.shape[2]
        for c in range(n_ctx):
            part[c // 2, c % 2, :, start : start + group.shape[1]] = lax.dot_general(
                normed[:, c * rows : (c + 1) * rows],
                group[...],
                (((0,), (0,)), ((), ())),
                preferred_element_type=F32,
            ).astype(BF16)

    for copy in q_copies:
        copy.wait_recv()
    low_part(r["qd_group"], 0)
    advance("out", "up")
    for copy in kv_copies:
        copy.wait_recv()
    low_part(r["kv_group"], r["qd_group"].shape[1])

    grad_in, w_kv = r["grad_input"], r["w_kv"]
    width = grad_in.shape[1]
    tile = 256

    @pl.loop(0, width // tile)
    def _(t):
        at = pl.ds(pl.multiple_of(t * tile, tile), tile)
        grad_in[:, at] = r["da_q"][:, at] + lax.dot_general(
            r["dkv"][...],
            w_kv[at, :],
            (((1,), (1,)), ((), ())),
            preferred_element_type=F32,
        )

    r["gain_sum"][...] = jnp.zeros_like(r["gain_sum"])
    gain = r["gain_one"][...]

    def norm_rows(at):
        value = r["hidden"][at, :].astype(F32)
        grad = grad_in[at, :]
        scale = lax.rsqrt(jnp.mean(value * value, axis=-1, keepdims=True) + NORM_EPS)
        r["gain_sum"][...] += jnp.sum(grad * value * scale, axis=0, keepdims=True)
        ge = gain * grad
        inner = jnp.mean(ge * value, axis=-1, keepdims=True)
        grad_in[at, :] = (
            r["grad_resid"][at, :] + scale * ge - value * (scale * scale * scale) * inner
        )

    row_loop(grad_in.shape[0], norm_rows, step=16)

    small, small_got = r["small_out"], r["small_got"]
    small[...] = r["small"][...]
    for i in range(width // 128):
        small[i : i + 1, :] = r["gain_sum"][:, i * 128 : (i + 1) * 128]
    steps = [over_f(1), over_f(2), over_c(1)]
    mask = 2
    while mask < n_ctx:
        steps.append(over_c(mask))
        mask *= 2
    small_copies = {}

    def small_start(s):
        small_got[s, 0] = small[...]
        small_copies[s] = send(
            small_got.at[s, 0],
            small_got.at[s, 1],
            r["s_send"].at[s],
            r["s_recv"].at[s],
            steps[s],
        )

    def small_end(s):
        small_copies[s].wait_recv()
        small[...] = small[...] + small_got[s, 1]

    for s in range(2):
        small_start(s)
        small_end(s)
    small_start(2)

    put_out("gate")
    advance("qup", "out")
    finish_sum("up")
    advance("low", "qup")
    finish_sum("out")
    small_end(2)
    small_start(3)
    put_out("up")
    finish_sum("qup")
    advance(None, "low")
    for s in range(3, len(steps)):
        if s > 3:
            small_start(s)
        small_end(s)
    finish_sum("low")
    put_out("qup")
    put_out("low")
    send.finish()
    for m in TAIL_NAMES:
        lines[m].finish()


def tail_reduce(n_ctx, n_f, inputs, q_width):
    n_z = n_ctx // 2
    vmem = pl.BlockSpec(memory_space=pltpu.VMEM)
    anywhere = pl.BlockSpec(memory_space=pl.ANY)
    rows, width = inputs["hidden"].shape
    kv_width = inputs["w_kv"].shape[1]
    in_hbm = ("gate", "kv", "up", "up_got", "out", "qup")
    names_in = tuple(inputs)
    in_specs = [anywhere if m in in_hbm else vmem for m in names_in]
    block = {m: inputs[m].shape[-2:] for m in in_hbm}
    cut_q, cut_kv, high = q_width // n_f, kv_width // n_f, width // n_ctx
    block["low"] = (high, cut_q + cut_kv)
    outs = {
        "small_out": jax.ShapeDtypeStruct(inputs["small"].shape, F32),
        "grad_input": jax.ShapeDtypeStruct((rows, width), F32),
        "out_qd": jax.ShapeDtypeStruct((high // n_f, q_width), F32),
        "out_kvw": jax.ShapeDtypeStruct((high // n_f, kv_width), F32),
    }
    scratch = {}
    for m in TAIL_NAMES:
        high, wide = block[m]
        scratch["pair_" + m] = pltpu.VMEM((n_z, high, wide), BF16)
        scratch["z_" + m] = pltpu.VMEM((n_z + 1, high, wide), BF16)
        if m in TAIL_SENT:
            scratch["y_" + m] = pltpu.VMEM((n_z, high, wide), BF16)
        if m in TAIL_CUT:
            scratch["tot_" + m] = pltpu.VMEM((high, wide), BF16)
            scratch["f_" + m] = pltpu.VMEM((n_f - 1, high // n_f, wide), BF16)
            if m != "low":
                outs["out_" + m] = jax.ShapeDtypeStruct((high // n_f, wide * n_f), F32)
        elif m != "kv":
            outs["out_" + m] = jax.ShapeDtypeStruct((high, wide), F32)
    scratch["dkv"] = pltpu.VMEM((rows, kv_width), BF16)
    scratch["qd_group"] = pltpu.VMEM((rows * n_f, q_width // n_f), BF16)
    scratch["kv_group"] = pltpu.VMEM((rows * n_f, kv_width // n_f), BF16)
    scratch["part_low"] = pltpu.VMEM((n_z, 2) + block["low"], BF16)
    scratch["gain_sum"] = pltpu.VMEM((1, width), F32)
    steps = 2 + (n_ctx.bit_length() - 1)
    scratch["small_got"] = pltpu.VMEM((steps, 2) + inputs["small"].shape, F32)
    dma = pltpu.SemaphoreType.DMA
    sent, cut = len(TAIL_SENT), len(TAIL_CUT)
    scratch["s_send"] = dma((steps,))
    scratch["s_recv"] = dma((steps,))
    scratch["y_send"] = dma((sent, n_z))
    scratch["y_recv"] = dma((sent, n_z))
    scratch["keep_sem"] = dma((sent, n_z + 1))
    scratch["z_send"] = dma((len(TAIL_NAMES), n_z))
    scratch["z_recv"] = dma((len(TAIL_NAMES), n_z + 1))
    scratch["f_send"] = dma((cut, n_f - 1))
    scratch["f_recv"] = dma((cut, n_f - 1))
    scratch["low_send"] = dma((2, n_f - 1))
    scratch["low_recv"] = dma((2, n_f - 1))
    values = pl.pallas_call(
        functools.partial(tail_kernel, n_ctx, n_f, names_in, tuple(outs), tuple(scratch)),
        out_shape=tuple(outs.values()),
        in_specs=in_specs,
        out_specs=tuple([vmem] * len(outs)),
        scratch_shapes=list(scratch.values()),
        compiler_params=pltpu.CompilerParams(
            collective_id=0, has_side_effects=True, vmem_limit_bytes=60 << 20
        ),
        name="tail_reduce",
    )(*inputs.values())
    return dict(zip(outs, values, strict=True))


def split_columns(width):
    return slice(0, width // 2), slice(width // 2, width)


def front_kernel(n_ctx, n_f, names, *refs):
    r = dict(zip(names, refs, strict=True))
    n_z = n_ctx // 2
    c_idx = lax.axis_index("ctx")
    f_idx = lax.axis_index("fsdp")
    y_idx = c_idx % 2
    z_bit = (c_idx // 2) % 2
    x_idx = f_idx // 2
    k_idx = f_idx % 2
    far_idx = flip(f_idx, 2)
    moves = Sender()
    local = []
    at_sem = [0]

    def over_c(mask):
        return (flip(c_idx, mask), f_idx)

    def over_f(mask):
        return (c_idx, flip(f_idx, mask))

    def send(src, dst, peer):
        i = at_sem[0]
        at_sem[0] += 1
        return moves(src, dst, r["send_sem"].at[i], r["recv_sem"].at[i], peer)

    def keep(src, dst):
        copy = pltpu.make_async_copy(src, dst, r["local_sem"].at[len(local)])
        copy.start()
        local.append(copy)
        return copy

    def rows(start, size):
        return pl.ds(pl.multiple_of(start, size), size)

    barrier = pltpu.get_barrier_semaphore()
    for mask in range(1, n_f):
        pl.semaphore_signal(barrier, inc=1, device_id=over_f(mask), device_id_type=MESH)
    for mask in range(1, n_ctx):
        pl.semaphore_signal(barrier, inc=1, device_id=over_c(mask), device_id_type=MESH)
    pl.semaphore_wait(barrier, n_f - 1 + n_ctx - 1)

    infos, tags = r["infos"], r["tags"]
    infos[f_idx] = r["info"][...]
    info_copies = [
        send(infos.at[f_idx], infos.at[f_idx], over_f(mask)) for mask in range(1, n_f)
    ]

    class Rows:
        def __init__(self, shard, dest, bit, hop, chunks):
            self.dest, self.bit, self.hop = dest, bit, hop
            self.shard = shard
            self.size = shard.shape[0]
            self.half = self.size // 2
            self.step = self.half // chunks
            self.chunks = chunks
            self.far, self.next, self.cross = [], [], []

        def start(self, spare=None):
            mine = self.dest.at[rows(f_idx * self.size, self.size)]
            if spare is None:
                self.kept = keep(self.shard, mine)
            else:
                self.spare, self.kept = spare, keep(self.shard, spare)
            self.cross.append(send(self.shard, mine, over_f(1)))

        def settle(self):
            self.kept.wait()
            keep(self.spare, self.dest.at[rows(f_idx * self.size, self.size)])

        def reach(self, i):
            part = self.bit * self.half + i * self.step
            self.far.append(
                send(
                    self.shard.at[rows(part, self.step)],
                    self.dest.at[rows(f_idx * self.size + part, self.step)],
                    over_f(2),
                )
            )

        def place(self, bit, i):
            return self.dest.at[rows(far_idx * self.size + bit * self.half + i * self.step, self.step)]

        def hop_on(self, i):
            self.far[i].wait_recv()
            reach_next()
            here = self.place(self.bit, i)
            self.next.append(send(here, here, over_c(self.hop)))
            self.cross.append(send(here, here, over_f(1)))

        def pass_on(self, i):
            self.next[i].wait_recv()
            here = self.place(1 - self.bit, i)
            self.cross.append(send(here, here, over_f(1)))

        def end(self):
            for copy in self.cross:
                copy.wait_recv()

    class Columns:
        def __init__(self, shard, dest, box, bits, hops):
            self.shard, self.dest, self.box = shard, dest, box
            self.bits, self.hops = bits, hops
            self.size = shard.shape[0]
            self.width = dest.shape[1]
            self.quarter = self.size // 4

        def columns(self, start, count=1):
            return pl.ds(pl.multiple_of(start * self.width, 128), count * self.width)

        def start(self, spare):
            mine = self.dest.at[rows(f_idx * self.size, self.size)]
            self.spare, self.kept = spare, keep(self.shard.at[:, self.columns(f_idx)], spare)
            self.cross = [send(self.shard.at[:, self.columns(flip(f_idx, 1))], mine, over_f(1))]

        def settle(self):
            self.kept.wait()
            keep(self.spare, self.dest.at[rows(f_idx * self.size, self.size)])

        def reach(self, i):
            one, two = self.bits
            at = rows((two * 2 + one) * self.quarter, self.quarter)
            self.far = send(
                self.shard.at[at, self.columns((1 - x_idx) * 2, 2)], self.box.at[at], over_f(2)
            )

        def piece(self, one, two):
            return self.box.at[rows((two * 2 + one) * self.quarter, self.quarter)]

        def first(self):
            one, two = self.bits
            self.far.wait_recv()
            reach_next()
            here = self.piece(one, two)
            self.step = send(here, here, over_c(self.hops[0]))
            self.last = [send(here, here, over_c(self.hops[1]))]

        def second(self):
            one, two = self.bits
            self.step.wait_recv()
            here = self.piece(1 - one, two)
            self.last.append(send(here, here, over_c(self.hops[1])))

        def part(self):
            for copy in self.last:
                copy.wait_recv()
            there = self.dest.at[rows(far_idx * self.size, self.size)]
            self.cross.append(send(self.box.at[:, self.columns(1 - k_idx)], there, over_f(1)))
            keep(self.box.at[:, self.columns(k_idx)], there)

        def end(self):
            for copy in self.cross:
                copy.wait_recv()

    kv = Rows(r["kv_weight"], r["kv_full"], y_idx, 1, 1)
    qd = Rows(r["q_down"], r["qd_full"], y_idx, 1, 1)
    qu = Rows(r["q_up"], r["qu_full"], z_bit, 2, 2)
    left, right = split_columns(r["out_proj"].shape[1])
    outs = [
        Rows(r["out_proj"].at[:, left], r["w_out"].at[:, left], y_idx, 1, 2),
        Rows(r["out_proj"].at[:, right], r["w_out"].at[:, right], z_bit, 2, 2),
    ]
    gate = Columns(r["w_gate"], r["gate_full"], r["gate_box"], (y_idx, z_bit), (1, 2))
    up = Columns(r["w_up"], r["up_full"], r["up_box"], (z_bit, y_idx), (2, 1))
    queue = [(kv, 0), (qd, 0), (qu, 0), (qu, 1), (gate, 0), (up, 0)]
    queue += [(out, i) for i in range(2) for out in outs]

    def reach_next():
        if queue:
            part, i = queue.pop(0)
            part.reach(i)

    reach_next()
    reach_next()
    reach_next()
    kv.start()
    qd.start()

    for copy in info_copies:
        copy.wait_recv()
    d1 = r["gain_one"].shape[1] // n_f // 128
    d2 = r["gain_q"].shape[1] // n_f // 128
    count = infos[0, 2 * d1 + d2 : 2 * d1 + d2 + 1, :]
    for f in range(n_f):
        for i in range(d1):
            col = slice((f * d1 + i) * 128, (f * d1 + i + 1) * 128)
            r["gain_one"][:, col] = infos[f, i : i + 1, :]
            r["gain_two"][:, col] = infos[f, d1 + d2 + i : d1 + d2 + i + 1, :]
        for i in range(d2):
            col = slice((f * d2 + i) * 128, (f * d2 + i + 1) * 128)
            r["gain_q"][:, col] = infos[f, d1 + i : d1 + i + 1, :]
        if f:
            count = count + infos[f, 2 * d1 + d2 : 2 * d1 + d2 + 1, :]
    tags[c_idx] = r["tag"][...]
    tags[c_idx, 1:2, :] = count
    tag_copies = [send(tags.at[c_idx], tags.at[c_idx], over_c(mask)) for mask in range(1, n_ctx)]

    normed = r["normed"]
    gain_one = r["gain_one"][...]

    def norm_rows(at):
        value = r["hidden"][at, :].astype(F32)
        scale = lax.rsqrt(jnp.mean(value * value, axis=-1, keepdims=True) + NORM_EPS)
        normed[at, :] = (value * scale * gain_one).astype(BF16)

    row_loop(normed.shape[0], norm_rows, step=16)

    kv.hop_on(0)
    qd.hop_on(0)
    qu.start()
    kv.pass_on(0)
    qd.pass_on(0)
    kv.end()
    kv.kept.wait()
    head = r["kv_full"].shape[1] // 2
    mid = head // 2
    cos, sin = r["cos"], r["sin"]
    kv_rows = r["kv_rows"]
    keys = jnp.dot(normed[...], r["kv_full"][:, :head], preferred_element_type=F32)
    one, two = keys[:, :mid], keys[:, mid:]
    kv_rows[:, :mid] = (one * cos[...] - two * sin[...]).astype(BF16)
    kv_rows[:, mid:head] = (two * cos[...] + one * sin[...]).astype(BF16)
    kv_rows[:, head:] = jnp.dot(
        normed[...], r["kv_full"][:, head:], preferred_element_type=F32
    ).astype(BF16)
    all_kv = r["all_kv"]
    tokens = normed.shape[0]

    def kv_place(c):
        return all_kv.at[rows(c * tokens, tokens)]

    kv_z = [send(kv_rows, kv_place(c_idx), over_c(2 * s)) for s in range(1, n_z)]
    kv_y = [send(kv_rows, kv_place(c_idx), over_c(1))]
    keep(kv_rows, kv_place(c_idx))
    qu.hop_on(0)
    qd.end()
    qd.kept.wait()

    @pl.loop(0, r["q_low"].shape[1] // 256)
    def _(t):
        at = pl.ds(pl.multiple_of(t * 256, 256), 256)
        r["q_low"][:, at] = jnp.dot(
            normed[...], r["qd_full"][:, at], preferred_element_type=F32
        )

    gain_q = r["gain_q"][...]

    def norm_low(at):
        value = r["q_low"][at, :]
        scale = lax.rsqrt(jnp.mean(value * value, axis=-1, keepdims=True) + NORM_EPS)
        r["q_normed"][at, :] = (value * scale * gain_q).astype(BF16)

    row_loop(tokens, norm_low, step=16)
    qu.hop_on(1)
    gate.first()
    for s in range(1, n_z):
        kv_z[s - 1].wait_recv()
        here = kv_place(flip(c_idx, 2 * s))
        kv_y.append(send(here, here, over_c(1)))
    qu.pass_on(0)
    qu.pass_on(1)
    up.first()
    qu.end()
    gate.start(r["gate_spare"])
    up.start(r["up_spare"])
    outs[0].start(r["out_spare"].at[:, left])
    outs[1].start(r["out_spare"].at[:, right])
    qu.kept.wait()

    @pl.loop(0, r["q_rot"].shape[1] // head)
    def _(h):
        start = pl.multiple_of(h * head, head)
        value = jnp.dot(
            r["q_normed"][...],
            r["qu_full"][:, pl.ds(start, head)],
            preferred_element_type=F32,
        )
        one, two = value[:, :mid], value[:, mid:]
        r["q_rot"][:, pl.ds(start, mid)] = (one * cos[...] - two * sin[...]).astype(BF16)
        late = pl.multiple_of(h * head + mid, mid)
        r["q_rot"][:, pl.ds(late, mid)] = (two * cos[...] + one * sin[...]).astype(BF16)

    for part in [gate, up] + outs:
        part.settle()
    for m in ("kv", "qd", "qu"):
        keep(r[m + "_full"], r["w_" + m])
    gate.second()
    for out in outs:
        out.hop_on(0)
    up.second()
    for out in outs:
        out.hop_on(1)
    gate.part()
    for i in range(2):
        for out in outs:
            out.pass_on(i)
    up.part()
    for copy in kv_y + tag_copies:
        copy.wait_recv()
    for part in [gate, up] + outs:
        part.end()
    for copy in local:
        if not any(copy is part.kept for part in [kv, qd, qu, gate, up] + outs):
            copy.wait()
    moves.finish()


def front(n_ctx, n_f, inputs, head_size):
    tokens, width = inputs["hidden"].shape
    shape = jax.ShapeDtypeStruct
    q_width = inputs["q_down"].shape[1]
    heads_width = inputs["q_up"].shape[1]
    part = inputs["w_gate"].shape[1] // n_f

    def whole(m):
        return (inputs[m].shape[0] * n_f, inputs[m].shape[1])

    in_hbm = ("q_down", "kv_weight", "q_up", "out_proj", "w_gate", "w_up")
    outs = {
        "w_qd": shape(whole("q_down"), BF16),
        "w_kv": shape(whole("kv_weight"), BF16),
        "w_qu": shape(whole("q_up"), BF16),
        "w_out": shape(whole("out_proj"), BF16),
        "gate_full": shape((width, part), BF16),
        "up_full": shape((width, part), BF16),
        "all_kv": shape((tokens * n_ctx, 2 * head_size), BF16),
        "normed": shape((tokens, width), BF16),
        "q_low": shape((tokens, q_width), F32),
        "q_normed": shape((tokens, q_width), BF16),
        "q_rot": shape((tokens, heads_width), BF16),
        "gain_one": shape((1, width), F32),
        "gain_q": shape((1, q_width), F32),
        "gain_two": shape((1, width), F32),
        "tags": shape((n_ctx, 8, 128), F32),
    }
    out_hbm = ("w_qd", "w_kv", "w_qu", "w_out", "gate_full", "up_full", "all_kv")
    box = (inputs["w_gate"].shape[0], 2 * part)
    dma = pltpu.SemaphoreType.DMA
    scratch = {
        "infos": pltpu.VMEM((n_f,) + inputs["info"].shape, F32),
        "qd_full": pltpu.VMEM(whole("q_down"), BF16),
        "kv_full": pltpu.VMEM(whole("kv_weight"), BF16),
        "qu_full": pltpu.VMEM(whole("q_up"), BF16),
        "gate_box": pltpu.VMEM(box, BF16),
        "up_box": pltpu.VMEM(box, BF16),
        "gate_spare": pltpu.VMEM((box[0], part), BF16),
        "up_spare": pltpu.VMEM((box[0], part), BF16),
        "out_spare": pltpu.VMEM(inputs["out_proj"].shape, BF16),
        "kv_rows": pltpu.VMEM((tokens, 2 * head_size), BF16),
        "send_sem": dma((64 + 2 * n_ctx,)),
        "recv_sem": dma((64 + 2 * n_ctx,)),
        "local_sem": dma((24,)),
    }
    vmem = pl.BlockSpec(memory_space=pltpu.VMEM)
    anywhere = pl.BlockSpec(memory_space=pl.ANY)
    names = tuple(inputs) + tuple(outs) + tuple(scratch)
    values = pl.pallas_call(
        functools.partial(front_kernel, n_ctx, n_f, names),
        out_shape=tuple(outs.values()),
        in_specs=[anywhere if m in in_hbm else vmem for m in inputs],
        out_specs=tuple([anywhere if m in out_hbm else vmem for m in outs]),
        scratch_shapes=list(scratch.values()),
        compiler_params=pltpu.CompilerParams(
            collective_id=1, has_side_effects=True, vmem_limit_bytes=48 << 20
        ),
        name="front",
    )(*inputs.values())
    return dict(zip(outs, values, strict=True))


def tiles(total, wide, body):
    whole = total // wide

    @pl.loop(0, whole)
    def _(t):
        body(pl.multiple_of(t * wide, wide), wide)

    if total % wide:
        body(whole * wide, total % wide)


def contract_first(a, b):
    return jnp.dot(a.T, b, preferred_element_type=F32)


def rows_product_kernel(a_ref, b_ref, o_ref):
    o_ref[...] = contract_last(a_ref[...], b_ref[...]).astype(BF16)


def rows_product(a, b, tile):
    return pl.pallas_call(
        rows_product_kernel,
        out_shape=jax.ShapeDtypeStruct((a.shape[0], b.shape[0]), BF16),
        grid=(b.shape[0] // tile,),
        in_specs=[
            pl.BlockSpec(a.shape, lambda i: (0, 0)),
            pl.BlockSpec((tile, b.shape[1]), lambda i: (i, 0)),
        ],
        out_specs=pl.BlockSpec((a.shape[0], tile), lambda i: (0, i)),
        compiler_params=pltpu.CompilerParams(vmem_limit_bytes=58 << 20),
        name="rows_product",
    )(a, b)


def ffn_kernel(n_f, names, *refs):
    r = dict(zip(names, refs, strict=True))
    c_idx = lax.axis_index("ctx")
    f_idx = lax.axis_index("fsdp")
    moves = Sender()
    at_sem = [0]
    core, far = (c_idx, flip(f_idx, 1)), (c_idx, flip(f_idx, 2))
    beside = (flip(c_idx, 1), f_idx)
    y_idx = c_idx % 2

    def send(src, dst, peer):
        i = at_sem[0]
        at_sem[0] += 1
        return moves(src, dst, r["send_sem"].at[i], r["recv_sem"].at[i], peer)

    barrier = pltpu.get_barrier_semaphore()
    for peer in (core, far, (c_idx, flip(f_idx, 3)), beside):
        pl.semaphore_signal(barrier, inc=1, device_id=peer, device_id_type=MESH)
    pl.semaphore_wait(barrier, 4)

    tokens, width = r["normed"].shape
    mine = r["attn_group"].at[pl.ds(pl.multiple_of(f_idx * tokens, tokens), tokens)]
    own_attn = pltpu.make_async_copy(r["attn_cut"].at[f_idx], mine, r["load_sem"].at[3])
    own_attn.start()

    def send_attn(mask):
        return send(r["attn_cut"].at[flip(f_idx, mask)], mine, (c_idx, flip(f_idx, mask)))

    units = r["w_down"].shape[0]
    group, dz = r["group"], r["dz"]
    block = [slice(i * tokens, (i + 1) * tokens) for i in range(4)]
    pair = [slice(0, 2 * tokens), slice(2 * tokens, 4 * tokens)]

    def gather(buf):
        to_core = send(buf.at[block[0]], buf.at[block[1]], core)
        to_far = send(buf.at[block[0]], buf.at[block[2]], far)
        return to_core, to_far

    def gather_far(buf, to_far):
        to_far.wait_recv()
        send(buf.at[block[2]], buf.at[block[3]], core).wait_recv()

    group[block[0], :] = r["normed"][...]
    to_core, to_far = gather(group)
    loads = []
    for i, m in enumerate(("gate", "up", "down")):
        load = pltpu.make_async_copy(r["w_" + m], r["v_" + m], r["load_sem"].at[i])
        load.start()
        loads.append(load)
    loads[0].wait()
    loads[1].wait()

    def hidden_part(rows):
        def one(start, wide):
            at = pl.ds(start, wide)
            both = jnp.concatenate([r["v_gate"][:, at], r["v_up"][:, at]], axis=1)
            out = jnp.dot(group[rows, :], both, preferred_element_type=F32)
            gate, up = out[:, :wide], out[:, wide:]
            r["gate"][rows, at] = gate.astype(BF16)
            r["up"][rows, at] = up.astype(BF16)
            r["hid"][rows, at] = (gate / (1.0 + jnp.exp(-gate)) * up).astype(BF16)

        tiles(units, 128, one)

    to_core.wait_recv()
    hidden_part(pair[0])
    gather_far(group, to_far)
    attn_copies = [send_attn(1), send_attn(2)]
    hidden_part(pair[1])
    loads[2].wait()

    def down_block(i, dest):
        def one(start, wide):
            at = pl.ds(start, wide)
            dest[:, at] = jnp.dot(
                r["hid"][block[i], :], r["v_down"][:, at], preferred_element_type=F32
            ).astype(dest.dtype)

        tiles(width, 256, one)

    def back_block(i, dest):
        def one(start, wide):
            at = pl.ds(start, wide)
            dest[:, at] = (
                contract_last(r["gate"][block[i], :], r["v_gate"][at, :])
                + contract_last(r["up"][block[i], :], r["v_up"][at, :])
            ).astype(dest.dtype)

        tiles(width, 256, one)

    def add_rows(dest, one, two):
        def add(at):
            dest[at, :] = (one[at, :].astype(F32) + two[at, :].astype(F32)).astype(dest.dtype)

        row_loop(tokens, add)

    def far_sum(k, make):
        make(3, r["give"].at[2 * k])
        step = send(r["give"].at[2 * k], r["got"].at[2 * k], core)
        make(2, r["far_sum"])
        step.wait_recv()
        add_rows(r["far_give"].at[k], r["far_sum"], r["got"].at[2 * k])
        return send(r["far_give"].at[k], r["far_got"].at[k], far)

    def near_sum(k, make):
        make(1, r["give"].at[2 * k + 1])
        step = send(r["give"].at[2 * k + 1], r["got"].at[2 * k + 1], core)
        make(0, r["near_sum"])
        return step

    def near_end(k, step):
        step.wait_recv()
        add_rows(r["near_sum"], r["near_sum"], r["got"].at[2 * k + 1])

    far_step = far_sum(0, down_block)
    near_end(0, near_sum(0, down_block))
    far_step.wait_recv()
    r["sq"][...] = jnp.zeros_like(r["sq"])

    def loss_rows(at):
        value = r["resid"][at, :] + r["near_sum"][at, :] + r["far_got"][0, at, :].astype(F32)
        r["result"][at, :] = value.astype(BF16)
        diff = value - r["teacher"][at, :].astype(F32)
        squares = jnp.sum(diff * diff, axis=1, keepdims=True) * r["valid"][at, :]
        r["sq"][:1, :] += jnp.sum(squares, axis=0, keepdims=True)
        grad = diff * r["valid_scale"][at, :1]
        r["grad_resid"][at, :] = grad
        dz[at, :] = grad.astype(BF16)

    row_loop(tokens, loss_rows, step=16)
    to_core, to_far = gather(dz)

    def back_hidden(rows):
        def one(start, wide):
            at = pl.ds(start, wide)
            grad = contract_last(dz[rows, :], r["v_down"][at, :])
            gate = r["gate"][rows, at].astype(F32)
            up = r["up"][rows, at].astype(F32)
            sigma = 1.0 / (1.0 + jnp.exp(-gate))
            r["gate"][rows, at] = (grad * up * sigma * (1.0 + gate * (1.0 - sigma))).astype(BF16)
            r["up"][rows, at] = (grad * (gate * sigma)).astype(BF16)

        tiles(units, 256, one)

    to_core.wait_recv()
    back_hidden(pair[0])
    near_step = near_sum(1, back_block)
    gather_far(dz, to_far)
    saves = []

    def save(src, dst, i):
        copy = pltpu.make_async_copy(src, dst, r["save_sem"].at[i])
        copy.start()
        return copy

    def down_tile(start, wide):
        at = pl.ds(start, wide)
        spot = r["tile"].at[pl.ds(0, wide)]
        spot[...] = contract_first(r["hid"][:, at], dz[...]).astype(BF16)
        save(spot, r["down_part"].at[at], 0).wait()

    count = units // 128
    first = (count + 1) // 2

    @pl.loop(0, first)
    def _(t):
        down_tile(pl.multiple_of(((count - first) * (1 - y_idx) + t) * 128, 128), 128)

    half = units // 2
    give = pl.ds(pl.multiple_of((1 - y_idx) * half, half), half)
    down_step = send(r["down_part"].at[give], r["down_got"], beside)
    attn_copies.append(send_attn(3))
    back_hidden(pair[1])
    far_step = far_sum(1, back_block)
    near_end(1, near_step)

    @pl.loop(0, count - first)
    def _(t):
        down_tile(pl.multiple_of((first * y_idx + t) * 128, 128), 128)

    def gate_tile(start, wide):
        at = pl.ds(start, wide)
        left = group[:, at].T
        for i, m in enumerate(("gate", "up")):
            spot = r["wide_tile"].at[i]
            spot[...] = jnp.dot(left, r[m][...], preferred_element_type=F32).astype(BF16)
            saves.append(save(spot, r[m + "_part"].at[at], 1 + i))
        saves.pop().wait()
        saves.pop().wait()

    tiles(width, 256, gate_tile)
    far_step.wait_recv()
    gain = r["gain_two"][...]
    r["gain_sum"][...] = jnp.zeros_like(r["gain_sum"])

    def norm_rows(at):
        grad = r["near_sum"][at, :] + r["far_got"][1, at, :].astype(F32)
        value = r["resid"][at, :]
        scale = lax.rsqrt(jnp.mean(value * value, axis=-1, keepdims=True) + NORM_EPS)
        r["gain_sum"][...] += jnp.sum(grad * value * scale, axis=0, keepdims=True)
        ge = gain * grad
        inner = jnp.mean(ge * value, axis=-1, keepdims=True)
        total = r["grad_resid"][at, :] + scale * ge - value * (scale * scale * scale) * inner
        r["grad_resid"][at, :] = total
        r["grad_branch"][at, :] = total.astype(BF16)

    row_loop(tokens, norm_rows, step=16)
    for copy in attn_copies + [down_step]:
        copy.wait_recv()
    own_attn.wait()
    moves.finish()


def feed_forward(n_f, inputs):
    tokens, width = inputs["normed"].shape
    units = inputs["w_down"].shape[0]
    shape = jax.ShapeDtypeStruct
    outs = {
        "result": shape((tokens, width), BF16),
        "grad_resid": shape((tokens, width), F32),
        "grad_branch": shape((tokens, width), BF16),
        "down_part": shape((units, width), BF16),
        "down_got": shape((units // 2, width), BF16),
        "gate_part": shape((width, units), BF16),
        "up_part": shape((width, units), BF16),
        "attn_group": shape((tokens * n_f, inputs["attn_cut"].shape[2]), BF16),
        "gain_sum": shape((1, width), F32),
        "sq": shape((8, 128), F32),
    }
    hbm = ("w_gate", "w_up", "w_down", "attn_cut", "attn_group")
    hbm += ("down_part", "down_got", "gate_part", "up_part")
    dma = pltpu.SemaphoreType.DMA
    many = tokens * n_f
    scratch = {
        "v_gate": pltpu.VMEM((width, units), BF16),
        "v_up": pltpu.VMEM((width, units), BF16),
        "v_down": pltpu.VMEM((units, width), BF16),
        "group": pltpu.VMEM((many, width), BF16),
        "dz": pltpu.VMEM((many, width), BF16),
        "gate": pltpu.VMEM((many, units), BF16),
        "up": pltpu.VMEM((many, units), BF16),
        "hid": pltpu.VMEM((many, units), BF16),
        "give": pltpu.VMEM((4, tokens, width), BF16),
        "got": pltpu.VMEM((4, tokens, width), BF16),
        "far_sum": pltpu.VMEM((tokens, width), F32),
        "near_sum": pltpu.VMEM((tokens, width), F32),
        "far_give": pltpu.VMEM((2, tokens, width), BF16),
        "far_got": pltpu.VMEM((2, tokens, width), BF16),
        "tile": pltpu.VMEM((128, width), BF16),
        "wide_tile": pltpu.VMEM((2, 256, units), BF16),
        "send_sem": dma((16,)),
        "recv_sem": dma((16,)),
        "load_sem": dma((4,)),
        "save_sem": dma((3,)),
    }
    vmem = pl.BlockSpec(memory_space=pltpu.VMEM)
    anywhere = pl.BlockSpec(memory_space=pl.ANY)
    names = tuple(inputs) + tuple(outs) + tuple(scratch)
    values = pl.pallas_call(
        functools.partial(ffn_kernel, n_f, names),
        out_shape=tuple(outs.values()),
        in_specs=[anywhere if m in hbm else vmem for m in inputs],
        out_specs=tuple([anywhere if m in hbm else vmem for m in outs]),
        scratch_shapes=list(scratch.values()),
        compiler_params=pltpu.CompilerParams(
            collective_id=2, has_side_effects=True, vmem_limit_bytes=60 << 20
        ),
        name="feed_forward",
    )(*inputs.values())
    return dict(zip(outs, values, strict=True))


def body(
    hidden_in,
    teacher,
    blocks,
    seq_ids,
    valid_mask,
    norm1_gain,
    q_down,
    q_gain,
    q_up,
    kv_weight,
    out_proj,
    norm2_gain,
    w_gate,
    w_up,
    w_down,
):
    row_count, model_width = hidden_in.shape
    head_size = kv_weight.shape[1] // 2
    heads_width = q_up.shape[1]
    head_count = heads_width // head_size
    half_dim = head_size // 2
    q_width = q_down.shape[1]
    n_ctx = lax.axis_size("ctx")
    n_f = lax.axis_size("fsdp")
    n_z = n_ctx // 2
    token_total = row_count * n_ctx * n_f
    seq_pieces = 2 * SEQ_BLOCKS
    c_idx = lax.axis_index("ctx")
    f_idx = lax.axis_index("fsdp")
    y_idx = c_idx % 2
    z_idx = c_idx // 2
    x_idx = f_idx // 2
    k_idx = f_idx % 2

    def by_f(values, mask):
        return lax.ppermute(values, "fsdp", [(i, i ^ mask) for i in range(n_f)])

    def by_c(values, mask):
        return lax.ppermute(values, "ctx", [(i, i ^ mask) for i in range(n_ctx)])

    def cut(values, start, size, axis):
        return lax.dynamic_slice_in_dim(values, start, size, axis)

    def ctx_split(grad):
        view = grad.reshape(n_z, 2, grad.shape[0] // n_ctx, grad.shape[1])
        give = lax.dynamic_index_in_dim(view, 1 - y_idx, 1, keepdims=False)
        keep = lax.dynamic_index_in_dim(view, y_idx, 1, keepdims=False)
        return give, keep

    def ctx_pair(keep, got):
        return (keep.astype(F32) + got.astype(F32)).astype(BF16)

    def ctx_spread(pair):
        return [pair] + [
            by_c(lax.dynamic_index_in_dim(pair, z_idx ^ r, 0, keepdims=False), 2 * r)
            for r in range(1, n_z)
        ]

    def ctx_total(parts):
        total = lax.dynamic_index_in_dim(parts[0], z_idx, 0, keepdims=False).astype(F32)
        for got in parts[1:]:
            total = total + got.astype(F32)
        return total

    def group_rows(values):
        return lax.all_gather(values, "fsdp", axis=0, tiled=True)

    valid_f = valid_mask.astype(F32)
    own_pieces = row_count // PIECE
    info = jnp.concatenate(
        [
            norm1_gain.astype(F32),
            q_gain.astype(F32),
            norm2_gain.astype(F32),
            jnp.full((128,), jnp.sum(valid_f)),
        ]
    )
    info = jnp.pad(info, (0, -info.shape[0] % 1024)).reshape(-1, 128)
    own_tags = jnp.stack([blocks.reshape(-1, PIECE)[:, 0], seq_ids.reshape(-1, PIECE)[:, 0]], 1)
    tag = jnp.pad(own_tags.astype(F32).reshape(1, -1), ((0, 7), (0, 128 - 2 * own_pieces)))
    own = jnp.concatenate([blocks.reshape(-1, PIECE)[:, 0], seq_ids[:1]])

    positions = blocks * PIECE + jnp.arange(row_count, dtype=jnp.int32) % PIECE
    freq_table = 10000.0 ** (-(jnp.arange(half_dim, dtype=F32) * 2.0 / head_size))
    angle_table = positions.astype(F32)[:, None] * freq_table[None, :]
    cosine = jnp.cos(angle_table)
    sine = jnp.sin(angle_table)
    fetched = front(
        n_ctx,
        n_f,
        {
            "q_down": q_down,
            "kv_weight": kv_weight,
            "q_up": q_up,
            "out_proj": out_proj,
            "w_gate": w_gate,
            "w_up": w_up,
            "hidden": hidden_in,
            "info": info,
            "tag": tag,
            "cos": cosine,
            "sin": sine,
        },
        head_size,
    )
    w_out = fetched["w_out"]
    all_kv, q_rot = fetched["all_kv"], fetched["q_rot"]
    normed, q_low, q_normed = fetched["normed"], fetched["q_low"], fetched["q_normed"]
    gain_one, gain_q, gain_two = fetched["gain_one"], fetched["gain_q"], fetched["gain_two"]
    tags = fetched["tags"][:, 0, : 2 * own_pieces].reshape(-1, 2).astype(jnp.int32)
    total_count = jnp.sum(fetched["tags"][:, 1, 0])
    hidden_f = hidden_in.astype(F32)
    scale_q = rms_scale(q_low)

    out_block = heads_width // (n_ctx * n_f)
    if out_block == 128:
        attn_heads, lse, attn_cut = attn_fwd(
            tags, own, q_rot, all_kv, head_size, seq_pieces, n_f, True
        )
    else:
        attn_heads, lse = attn_fwd(tags, own, q_rot, all_kv, head_size, seq_pieces, n_f, False)
        attn_cut = attn_heads.reshape(row_count, n_ctx, n_f, out_block).transpose(2, 0, 1, 3)
        attn_cut = attn_cut.reshape(n_f, row_count, n_ctx * out_block)
    resid = hidden_f + dot(attn_heads, w_out)
    scale_two = rms_scale(resid)
    normed_two = (resid * scale_two * gain_two).astype(BF16)

    wide_valid = jnp.broadcast_to(valid_f[:, None], (row_count, 128))
    ffn = feed_forward(
        n_f,
        {
            "normed": normed_two,
            "resid": resid,
            "teacher": teacher,
            "valid": wide_valid,
            "valid_scale": wide_valid * (token_total / total_count),
            "gain_two": gain_two,
            "w_gate": fetched["gate_full"],
            "w_up": fetched["up_full"],
            "w_down": w_down,
            "attn_cut": attn_cut,
        },
    )
    grad_resid, grad_branch = ffn["grad_resid"], ffn["grad_branch"]
    grad_gain_two = ffn["gain_sum"].reshape(-1)
    sq_local = ffn["sq"][0, 0]
    half_units = w_down.shape[0] // 2
    down_pair = ctx_pair(cut(ffn["down_part"], y_idx * half_units, half_units, 0), ffn["down_got"])
    down_parts = ctx_spread(down_pair.reshape(n_z, -1, model_width))
    gate_give, gate_keep = ctx_split(ffn["gate_part"])
    gate_got = by_c(gate_give, 1)
    early = n_z // 2
    up_blocks = ffn["up_part"].reshape(n_z, 2, model_width // n_ctx, -1)
    up_got = by_c(
        lax.dynamic_index_in_dim(up_blocks[:early], 1 - y_idx, 1, keepdims=False), 1
    )
    branch_group = group_rows(grad_branch)
    grad_attn = rows_product(grad_branch, w_out, 512)
    grad_qlin, grad_seq = attn_bwd(
        tags, own, q_rot, grad_attn, attn_heads, lse, cosine, sine, all_kv, head_size, seq_pieces
    )
    qlin_group = lax.all_to_all(grad_qlin, "fsdp", 1, 0, tiled=True)
    down_parts, gate_got, grad_seq = together(down_parts, gate_got, grad_seq)

    by_piece = grad_seq.reshape(seq_pieces, PIECE, 2 * head_size)
    piece_tag = tags[:, 0].reshape(n_z, 2, own_pieces)
    piece_own = (tags[:, 1] == seq_ids[0]).reshape(n_z, 2, own_pieces)

    def kv_half(bit):
        places = lax.dynamic_index_in_dim(piece_tag, bit, 1, keepdims=False).reshape(-1)
        picked = by_piece[places]
        if n_ctx * own_pieces != seq_pieces:
            mine = lax.dynamic_index_in_dim(piece_own, bit, 1, keepdims=False).reshape(-1)
            picked = jnp.where(mine[:, None, None], picked, jnp.zeros_like(picked))
        return picked.reshape(n_z, own_pieces * PIECE, 2 * head_size)

    kv_part = jnp.stack([kv_half(0), kv_half(1)], axis=1)
    q_cut, kv_cut = q_width // n_f, 2 * head_size // n_f
    qnorm_group = group_rows(q_normed)
    normed_group = group_rows(normed)

    grad_qnormed = dot_t(grad_qlin, fetched["w_qu"])
    grad_qlow_f, grad_gain_q = rms_back(q_low, scale_q, gain_q, grad_qnormed)
    grad_qlow = grad_qlow_f.astype(BF16)
    attn_group = ffn["attn_group"]
    da_q = dot_t(grad_qlow, fetched["w_qd"])
    gate_pair = ctx_pair(gate_keep, gate_got)
    out_part = dot_rows(attn_group, branch_group).astype(BF16)
    qup_part = dot_rows(qnorm_group, qlin_group).astype(BF16)

    def by_ctx(grad):
        return grad.reshape(n_z, 2, grad.shape[0] // n_ctx, grad.shape[1])

    order = [
        (c * n_f + f, f * n_ctx + c % 2 * n_z + c // 2) for c in range(n_ctx) for f in range(n_f)
    ]
    down_rows = ctx_total(down_parts).astype(BF16)
    down_sent = lax.ppermute(down_rows, ("ctx", "fsdp"), order)

    up_got, out_part, qup_part = together(up_got, out_part, qup_part)

    small = jnp.concatenate(
        [jnp.zeros((model_width,), F32), grad_gain_q, grad_gain_two, sq_local.reshape(1)]
    )
    entries = small.shape[0]
    small = jnp.pad(small, (0, -entries % 1024)).reshape(-1, 128)
    ends = tail_reduce(
        n_ctx,
        n_f,
        {
            "gate": gate_pair,
            "kv": kv_part,
            "up": up_blocks,
            "up_got": up_got,
            "out": by_ctx(out_part),
            "qup": by_ctx(qup_part),
            "dqa": grad_qlow,
            "cos": cosine,
            "sin": sine,
            "normed_group": normed_group,
            "w_kv": fetched["w_kv"],
            "da_q": da_q,
            "hidden": hidden_in,
            "gain_one": gain_one,
            "grad_resid": grad_resid,
            "small": small,
        },
        q_width,
    )
    small, down_sent = together(ends["small_out"], down_sent)
    small = small.reshape(-1)[:entries]
    grad_down = down_sent.astype(F32)

    device = c_idx * n_f + f_idx
    q1, q2 = model_width, model_width + q_width
    n_dev = n_ctx * n_f

    def own_part(values):
        size = values.shape[0] // n_dev
        return cut(values, device * size, size, 0)

    loss_now = small[-1] / (model_width * total_count)
    return (
        ffn["result"],
        loss_now,
        ends["grad_input"],
        own_part(small[:q1]),
        ends["out_qd"],
        own_part(small[q1:q2]),
        ends["out_qup"],
        ends["out_kvw"],
        ends["out_out"],
        own_part(small[q2 : q2 + model_width]),
        ends["out_gate"],
        ends["out_up"],
        grad_down,
    )


def solution(mesh):
    both = ("ctx", "fsdp")
    rows = P(both, None)
    flat = P(both)
    shard = P("fsdp", None)
    gain = P("fsdp")
    return jax.shard_map(
        body,
        mesh=mesh,
        in_specs=(
            rows,
            rows,
            flat,
            flat,
            flat,
            gain,
            shard,
            gain,
            shard,
            shard,
            shard,
            gain,
            shard,
            shard,
            shard,
        ),
        out_specs=(
            rows,
            P(),
            rows,
            flat,
            rows,
            flat,
            rows,
            rows,
            rows,
            flat,
            rows,
            rows,
            rows,
        ),
        check_vma=False,
    )
```

```python
import functools
import math

import jax
import jax.numpy as jnp
from jax import lax
from jax.experimental import pallas as pl
from jax.experimental.pallas import tpu as pltpu
from jax.sharding import PartitionSpec as P

PIECE = 128
SEQ_BLOCKS = 8
NORM_EPS = 1e-05
F32 = jnp.float32
BF16 = jnp.bfloat16
LOG2E = math.log2(math.e)
HEAD_GROUP = 16


def rms_scale(values):
    return lax.rsqrt(jnp.mean(values * values, axis=-1, keepdims=True) + NORM_EPS)


def rms_back(values, scale, gain, grad):
    grad_gain = jnp.sum(grad * values * scale, axis=0)
    ge = gain * grad
    inner = jnp.mean(ge * values, axis=-1, keepdims=True)
    return scale * ge - values * (scale * scale * scale) * inner, grad_gain


def rope_apply(values, cosine, sine):
    half_dim = values.shape[-1] // 2
    one = values[..., :half_dim]
    two = values[..., half_dim:]
    return jnp.concatenate([one * cosine - two * sine, two * cosine + one * sine], axis=-1)


def rope_back(grads, cosine, sine):
    half_dim = grads.shape[-1] // 2
    one = grads[..., :half_dim]
    two = grads[..., half_dim:]
    return jnp.concatenate([one * cosine + two * sine, two * cosine - one * sine], axis=-1)


def together(*values):
    return lax.optimization_barrier(values)


def dot(a, b):
    return jnp.dot(a, b, preferred_element_type=F32)


def dot_t(a, b):
    return lax.dot_general(a, b, (((1,), (1,)), ((), ())), preferred_element_type=F32)


def dot_rows(a, b):
    return lax.dot_general(a, b, (((0,), (0,)), ((), ())), preferred_element_type=F32)


def contract_last(a, b):
    return lax.dot_general(a, b, (((1,), (1,)), ((), ())), preferred_element_type=F32)

def find_pieces(tags_ref, own_ref, pick_ref, total):
    @pl.loop(0, total)
    def _(u):
        @pl.when(tags_ref[u, 1] == own_ref[2])
        def _():
            pick_ref[tags_ref[u, 0]] = u

def stack_heads(ref, hd):
    return jnp.concatenate([ref[:, h*hd:(h+1)*hd] for h in range(HEAD_GROUP)], axis=0)

def attn_fwd_kernel(n_f, tags_ref, own_ref, q_ref, kv_ref, o_ref, lse_ref, *rest):
    k_s, vt_s, acc_s, pick_s = rest[-4:]
    half = pl.program_id(0)
    hd = k_s.shape[1]
    pieces = k_s.shape[0] // PIECE
    total = kv_ref.shape[0] // PIECE
    wide = 2 * PIECE
    coef = hd ** -0.5 * LOG2E

    @pl.when((half == 0) & (pl.program_id(1) == 0))
    def _():
        find_pieces(tags_ref, own_ref, pick_s, total)
        for i in range(pieces):
            rows = pl.ds(pl.multiple_of(pick_s[i] * PIECE, PIECE), PIECE)
            k_s[i*PIECE:(i+1)*PIECE, :] = kv_ref[rows, :hd]
            vt_s[:, i*PIECE:(i+1)*PIECE] = kv_ref[rows, hd:].T

    q = stack_heads(q_ref, hd)
    acc_s[...] = jnp.zeros_like(acc_s)
    rows = q.shape[0]
    def step(i, carry):
        peak, total_p = carry
        at = pl.ds(pl.multiple_of(i * wide, wide), wide)
        raw = contract_last(k_s[at, :], q)
        top = jnp.maximum(peak, jnp.max(raw, axis=0, keepdims=True))
        fade = jnp.exp2((peak - top) * coef)
        p = jnp.exp2((raw - top) * coef)
        acc_s[...] = acc_s[...] * fade + jnp.dot(vt_s[:, at], p.astype(BF16), preferred_element_type=F32)
        return top, total_p * fade + jnp.sum(p, axis=0, keepdims=True)
    count = own_ref[half] // 2 + 1
    peak, total_p = lax.fori_loop(0, count, step, (jnp.full((1, rows), -1e30, F32), jnp.zeros((1, rows), F32)))
    out = (acc_s[...] / total_p).astype(BF16).T
    for h in range(HEAD_GROUP):
        o_ref[:, h*hd:(h+1)*hd] = out[h*PIECE:(h+1)*PIECE, :]
    if len(rest) > 4:
        for b in range(HEAD_GROUP * hd // 128):
            head, part = b * 128 // hd, b * 128 % hd
            rest[0][b % n_f, :, b // n_f * 128:(b // n_f + 1) * 128] = out[
                head*PIECE:(head+1)*PIECE, part:part+128
            ]
    lse_ref[0] = peak * coef + jnp.log2(total_p)

def attn_fwd(tags, own, q, kv, hd, pieces, n_f, cut):
    n_rows, width = q.shape
    groups = width // hd // HEAD_GROUP
    gw = HEAD_GROUP * hd
    halves = n_rows // PIECE
    rows = HEAD_GROUP * PIECE
    blk = pl.BlockSpec((PIECE, gw), lambda p, g, *_: (p, g))
    flops = 4 * n_rows * width * pieces * PIECE * 9 // 16
    shapes = [jax.ShapeDtypeStruct(q.shape, BF16), jax.ShapeDtypeStruct((halves*groups, 1, rows), F32)]
    specs = [blk, pl.BlockSpec((1, 1, rows), lambda p, g, *_: (p*groups+g, 0, 0))]
    if cut:
        shapes.append(jax.ShapeDtypeStruct((n_f, n_rows, width // n_f), BF16))
        specs.append(pl.BlockSpec((n_f, PIECE, gw // n_f), lambda p, g, *_: (0, p, g)))
    return pl.pallas_call(
        functools.partial(attn_fwd_kernel, n_f),
        out_shape=tuple(shapes),
        grid_spec=pltpu.PrefetchScalarGridSpec(
            num_scalar_prefetch=2, grid=(halves, groups),
            in_specs=[blk, pl.BlockSpec(kv.shape, lambda p, g, *_: (0, 0))],
            out_specs=tuple(specs),
            scratch_shapes=[pltpu.VMEM((pieces*PIECE, hd), BF16), pltpu.VMEM((hd, pieces*PIECE), BF16),
                            pltpu.VMEM((hd, rows), F32), pltpu.SMEM((pieces,), jnp.int32)]),
        compiler_params=pltpu.CompilerParams(vmem_limit_bytes=40 << 20),
        cost_estimate=pl.CostEstimate(flops=flops, transcendentals=flops//(4*hd), bytes_accessed=2*(2*q.size+kv.size)),
        name="attn_fwd",
    )(tags, own, q, kv)

def attn_bwd_kernel(tags_ref, own_ref, q_ref, do_ref, o_ref, lse_ref, cos_ref, sin_ref, kv_ref, dq_ref, dkv_ref,
                    k_s, kt_s, v_s, dq_s, dk_s, dv_s, pick_s):
    half = pl.program_id(0)
    group = pl.program_id(1)
    hd = k_s.shape[1]
    pieces = k_s.shape[0] // PIECE
    total = kv_ref.shape[0] // PIECE
    wide = 2 * PIECE
    coef = hd ** -0.5 * LOG2E
    scale = hd ** -0.5

    @pl.when((half == 0) & (group == 0))
    def _():
        find_pieces(tags_ref, own_ref, pick_s, total)
        for i in range(pieces):
            rows = pl.ds(pl.multiple_of(pick_s[i] * PIECE, PIECE), PIECE)
            keys = kv_ref[rows, :hd]
            k_s[i*PIECE:(i+1)*PIECE, :] = keys
            kt_s[:, i*PIECE:(i+1)*PIECE] = keys.T
            v_s[i*PIECE:(i+1)*PIECE, :] = kv_ref[rows, hd:]
        dk_s[...] = jnp.zeros_like(dk_s)
        dv_s[...] = jnp.zeros_like(dv_s)

    q = stack_heads(q_ref, hd)
    do = stack_heads(do_ref, hd)
    prod = do.astype(F32) * stack_heads(o_ref, hd).astype(F32)
    delta = lax.dot_general(jnp.ones((8, hd), F32), prod, (((1,), (1,)), ((), ())),
                            preferred_element_type=F32, precision=lax.Precision.HIGHEST)[:1]
    lse = lse_ref[0]
    dq_s[...] = jnp.zeros_like(dq_s)
    def step(i, carry):
        at = pl.ds(pl.multiple_of(i * wide, wide), wide)
        p = jnp.exp2(contract_last(k_s[at, :], q) * coef - lse)
        dp = contract_last(v_s[at, :], do)
        ds = (p * (dp - delta)).astype(BF16)
        dv_s[at, :] += jnp.dot(p.astype(BF16), do, preferred_element_type=F32)
        dk_s[at, :] += jnp.dot(ds, q, preferred_element_type=F32)
        dq_s[...] += jnp.dot(kt_s[:, at], ds, preferred_element_type=F32)
        return carry
    lax.fori_loop(0, own_ref[half] // 2 + 1, step, 0)
    dq = (dq_s[...] * scale).T
    cos, sin = cos_ref[...], sin_ref[...]
    mid = hd // 2
    for h in range(HEAD_GROUP):
        one = dq[h*PIECE:(h+1)*PIECE, :mid]
        two = dq[h*PIECE:(h+1)*PIECE, mid:]
        dq_ref[:, h*hd:h*hd+mid] = (one * cos + two * sin).astype(BF16)
        dq_ref[:, h*hd+mid:(h+1)*hd] = (two * cos - one * sin).astype(BF16)

    @pl.when((half == pl.num_programs(0) - 1) & (group == pl.num_programs(1) - 1))
    def _():
        dkv_ref[:, :hd] = (dk_s[...] * scale).astype(BF16)
        dkv_ref[:, hd:] = dv_s[...].astype(BF16)

def attn_bwd(tags, own, q, do, o, lse, cos, sin, kv, hd, pieces):
    n_rows, width = q.shape
    groups = width // hd // HEAD_GROUP
    gw = HEAD_GROUP * hd
    halves = n_rows // PIECE
    rows = HEAD_GROUP * PIECE
    blk = pl.BlockSpec((PIECE, gw), lambda p, g, *_: (p, g))
    trig = pl.BlockSpec((PIECE, hd // 2), lambda p, g, *_: (p, 0))
    keys = pieces * PIECE
    return pl.pallas_call(
        attn_bwd_kernel,
        out_shape=(jax.ShapeDtypeStruct(q.shape, BF16), jax.ShapeDtypeStruct((keys, 2*hd), BF16)),
        grid_spec=pltpu.PrefetchScalarGridSpec(
            num_scalar_prefetch=2, grid=(halves, groups),
            in_specs=[blk, blk, blk, pl.BlockSpec((1, 1, rows), lambda p, g, *_: (p*groups+g, 0, 0)), trig, trig,
                      pl.BlockSpec(kv.shape, lambda p, g, *_: (0, 0))],
            out_specs=[blk, pl.BlockSpec((keys, 2*hd), lambda p, g, *_: (0, 0))],
            scratch_shapes=[pltpu.VMEM((keys, hd), BF16), pltpu.VMEM((hd, keys), BF16), pltpu.VMEM((keys, hd), BF16),
                            pltpu.VMEM((hd, rows), F32), pltpu.VMEM((keys, hd), F32), pltpu.VMEM((keys, hd), F32),
                            pltpu.SMEM((pieces,), jnp.int32)]),
        compiler_params=pltpu.CompilerParams(vmem_limit_bytes=48 << 20),
        name="attn_bwd",
    )(tags, own, q, do, o, lse, cos, sin, kv)

MESH = pl.DeviceIdType.MESH


def flip(index, mask):
    out = 0
    bit = 1
    while bit <= mask:
        part = (index // bit) % 2
        out = out + bit * ((1 - part) if mask & bit else part)
        bit *= 2
    return out + (index // bit) * bit


def row_loop(rows, body, step=32):
    if rows % step:
        step = 16

    @pl.loop(0, rows // step)
    def _(i):
        body(pl.ds(pl.multiple_of(i * step, step), step))


class Sender:
    def __init__(self):
        self.open = []

    def make(self, src, dst, send_sem, recv_sem, peer):
        return pltpu.make_async_remote_copy(
            src_ref=src,
            dst_ref=dst,
            send_sem=send_sem,
            recv_sem=recv_sem,
            device_id=peer,
            device_id_type=MESH,
        )

    def __call__(self, *args):
        copy = self.make(*args)
        copy.start()
        self.open.append(copy)
        return copy

    def finish(self):
        for copy in self.open:
            copy.wait_send()


class LineSum:
    def __init__(self, own, got, send_sem, recv_sem, c_idx, f_idx, n_z, sender):
        self.own, self.got, self.send_sem, self.recv_sem = own, got, send_sem, recv_sem
        self.n_z, self.sender = n_z, sender
        self.z = c_idx // 2
        self.left = (c_idx - 2, f_idx)
        self.right = (c_idx + 2, f_idx)

    def copy(self, b, slot, peer):
        return self.sender.make(
            self.own.at[b], self.got.at[slot], self.send_sem.at[b], self.recv_sem.at[slot], peer
        )

    def take(self, b, slot):
        self.copy(b, slot, self.left).wait_recv()

        def add(at):
            self.own[b, at, :] = (
                self.own[b, at, :].astype(F32) + self.got[slot, at, :].astype(F32)
            ).astype(BF16)

        row_loop(self.own.shape[1], add)

    def go_right(self, b):
        z = self.z

        @pl.when(z < b)
        def _():
            @pl.when(z > 0)
            def _():
                self.take(b, b)

            self.copy(b, b, self.right).start()

    def go_left(self, b):
        z, n_z = self.z, self.n_z

        @pl.when(z > b)
        def _():
            @pl.when(z < n_z - 1)
            def _():
                self.take(b, b)

            @pl.when(z - 1 > b)
            def _():
                self.copy(b, b, self.left).start()

            @pl.when(z - 1 == b)
            def _():
                self.copy(b, n_z, self.left).start()

    def step(self, i):
        @pl.when(2 * self.z < self.n_z)
        def _():
            self.go_right(self.n_z - 1 - i)
            self.go_left(i)

        @pl.when(2 * self.z >= self.n_z)
        def _():
            self.go_left(i)
            self.go_right(self.n_z - 1 - i)

    def total(self, store):
        z, n_z = self.z, self.n_z

        @pl.when(z > 0)
        def _():
            self.copy(z, z, self.left).wait_recv()

        @pl.when(z < n_z - 1)
        def _():
            self.copy(z, n_z, self.left).wait_recv()

        rows = self.own.shape[1]

        @pl.when(z == 0)
        def _():
            row_loop(
                rows,
                lambda at: store(
                    at, self.own[z, at, :].astype(F32) + self.got[n_z, at, :].astype(F32)
                ),
            )

        @pl.when(z == n_z - 1)
        def _():
            row_loop(
                rows,
                lambda at: store(
                    at, self.own[z, at, :].astype(F32) + self.got[z, at, :].astype(F32)
                ),
            )

        @pl.when((z > 0) & (z < n_z - 1))
        def _():
            row_loop(
                rows,
                lambda at: store(
                    at,
                    self.own[z, at, :].astype(F32)
                    + self.got[z, at, :].astype(F32)
                    + self.got[n_z, at, :].astype(F32),
                ),
            )

    def finish(self):
        for b in range(self.n_z):

            @pl.when(self.z != b)
            def _(b=b):
                self.copy(b, b, self.left).wait_send()


WINDOW = 3
TAIL_NAMES = ("gate", "kv", "up", "out", "qup", "low")
TAIL_CUT = ("gate", "up", "qup", "low")
TAIL_SENT = ("kv", "up", "out", "qup", "low")


def tail_kernel(n_ctx, n_f, names_in, names_out, names_scratch, *refs):
    n_z = n_ctx // 2
    names = list(names_in) + list(names_out) + list(names_scratch)
    r = dict(zip(names, refs, strict=True))
    c_idx = lax.axis_index("ctx")
    f_idx = lax.axis_index("fsdp")
    y_idx = c_idx % 2
    z_idx = c_idx // 2
    send = Sender()

    def over_c(mask):
        return (flip(c_idx, mask), f_idx)

    def over_f(mask):
        return (c_idx, flip(f_idx, mask))

    barrier = pltpu.get_barrier_semaphore()
    for mask in range(1, n_f):
        pl.semaphore_signal(barrier, inc=1, device_id=over_f(mask), device_id_type=MESH)
    for mask in range(1, n_ctx):
        pl.semaphore_signal(barrier, inc=1, device_id=over_c(mask), device_id_type=MESH)
    pl.semaphore_wait(barrier, n_f - 1 + n_ctx - 1)

    lines = {
        m: LineSum(
            r["pair_" + m],
            r["z_" + m],
            r["z_send"].at[i],
            r["z_recv"].at[i],
            c_idx,
            f_idx,
            n_z,
            send,
        )
        for i, m in enumerate(TAIL_NAMES)
    }
    y_copies, keeps = {}, {}
    early = r["up_got"].shape[0]

    parts = {m: r[m] for m in ("kv", "up", "out", "qup")}
    parts["low"] = r["part_low"]
    queue = [
        (m, b) for m in TAIL_SENT for b in range(n_z) if m != "up" or b >= early
    ]
    owed = tuple(queue)

    def next_y():
        if queue:
            m, b = queue.pop(0)
            i = TAIL_SENT.index(m)
            y_copies[m, b] = send(
                parts[m].at[b, 1 - y_idx],
                r["y_" + m].at[b],
                r["y_send"].at[i, b],
                r["y_recv"].at[i, b],
                over_c(1),
            )
            take_own(m, b)

    def take_own(m, b):
        keep = pltpu.make_async_copy(
            parts[m].at[b, y_idx],
            r["pair_" + m].at[b],
            r["keep_sem"].at[TAIL_SENT.index(m), b],
        )
        keep.start()
        keeps[m, b] = keep

    def add_pair(m, b):
        y_copies[m, b].wait_recv()
        next_y()
        add_ready(m, b)

    def add_ready(m, b):
        keeps[m, b].wait()
        pair, got = r["pair_" + m], r["y_" + m]

        def add(at):
            pair[b, at, :] = (pair[b, at, :].astype(F32) + got[b, at, :].astype(F32)).astype(BF16)

        row_loop(pair.shape[1], add)

    def advance(pair, line, work=()):
        if pair == "up":
            here.wait()
            for b in range(early):
                add_ready(pair, b)
        for b in range(n_z):
            if pair is not None and (pair, b) in owed:
                add_pair(pair, b)
            if line is not None and b < n_z - 1:
                lines[line].step(b)
            if b < len(work):
                work[b]()

    f_copies = {}

    def finish_sum(m):
        lines[m].total(lambda at, value: store_total(m, at, value))
        if m in TAIL_CUT:
            i = TAIL_CUT.index(m)
            part = r["tot_" + m].shape[0] // n_f
            for s in range(1, n_f):
                at = pl.ds(pl.multiple_of(flip(f_idx, s) * part, part), part)
                f_copies[m, s] = send(
                    r["tot_" + m].at[at, :],
                    r["f_" + m].at[s - 1],
                    r["f_send"].at[i, s - 1],
                    r["f_recv"].at[i, s - 1],
                    over_f(s),
                )

    def store_total(m, at, value):
        if m in TAIL_CUT:
            r["tot_" + m][at, :] = value.astype(BF16)
        else:
            r["out_" + m][at, :] = value

    def put_out(m):
        total = r["tot_" + m]
        rows, width = total.shape
        part = rows // n_f
        cuts = {"out_" + m: (0, width)}
        if m == "low":
            split = r["qd_group"].shape[1]
            cuts = {"out_qd": (0, split), "out_kvw": (split, width - split)}
        for s in range(n_f):
            source = flip(f_idx, s)
            if s:
                f_copies[m, s].wait_recv()
                got = r["f_" + m].at[s - 1]
            else:
                got = total.at[pl.ds(pl.multiple_of(f_idx * part, part), part)]
            for name, (start, wide) in cuts.items():
                at = pl.ds(pl.multiple_of(source * wide, 128), wide)
                r[name][:, at] = got[:, start : start + wide].astype(F32)

    def cut_low(src, dst, width, index):
        rows = src.shape[0]
        mine = pl.ds(pl.multiple_of(f_idx * rows, rows), rows)
        copies = []
        for s in range(1, n_f):
            at = pl.ds(pl.multiple_of(flip(f_idx, s) * width, 128), width)
            copies.append(
                send(
                    src.at[:, at],
                    dst.at[mine, :],
                    r["low_send"].at[index, s - 1],
                    r["low_recv"].at[index, s - 1],
                    over_f(s),
                )
            )
        own = pl.ds(pl.multiple_of(f_idx * width, 128), width)
        dst[mine, :] = src[:, own]
        return copies

    for _ in range(WINDOW):
        next_y()
    q_copies = cut_low(r["dqa"], r["qd_group"], r["qd_group"].shape[1], 0)
    pair_in = pltpu.make_async_copy(r["gate"], r["pair_gate"], r["keep_sem"].at[0, n_z])
    pair_in.start()
    here = pltpu.make_async_copy(
        r["up_got"], r["y_up"].at[pl.ds(0, early)], r["keep_sem"].at[1, n_z]
    )
    here.start()
    for b in range(early):
        take_own("up", b)
    pair_in.wait()
    def low_part(group, start):
        normed, part = r["normed_group"], r["part_low"]
        rows = part.shape[2]
        for c in range(n_ctx):
            part[c // 2, c % 2, :, start : start + group.shape[1]] = lax.dot_general(
                normed[:, c * rows : (c + 1) * rows],
                group[...],
                (((0,), (0,)), ((), ())),
                preferred_element_type=F32,
            ).astype(BF16)

    def low_queries():
        for copy in q_copies:
            copy.wait_recv()
        low_part(r["qd_group"], 0)

    advance("kv", "gate", (low_queries,))
    advance("up", "kv")
    finish_sum("gate")

    head = r["dkv"].shape[1] // 2
    mid = head // 2

    def store_kv(at, value):
        cos, sin = r["cos"][at, :], r["sin"][at, :]
        one, two = value[:, :mid], value[:, mid:head]
        r["dkv"][at, :mid] = (one * cos + two * sin).astype(BF16)
        r["dkv"][at, mid:head] = (two * cos - one * sin).astype(BF16)
        r["dkv"][at, head:] = value[:, head:].astype(BF16)

    lines["kv"].total(store_kv)
    kv_copies = cut_low(r["dkv"], r["kv_group"], r["kv_group"].shape[1], 1)

    def low_keys():
        for copy in kv_copies:
            copy.wait_recv()
        low_part(r["kv_group"], r["qd_group"].shape[1])

    grad_in, w_kv = r["grad_input"], r["w_kv"]
    width = grad_in.shape[1]
    tile = 256

    def input_products():
        @pl.loop(0, width // tile)
        def _(t):
            at = pl.ds(pl.multiple_of(t * tile, tile), tile)
            grad_in[:, at] = r["da_q"][:, at] + lax.dot_general(
                r["dkv"][...],
                w_kv[at, :],
                (((1,), (1,)), ((), ())),
                preferred_element_type=F32,
            )

    gain = r["gain_one"][...]

    def norm_rows(at):
        value = r["hidden"][at, :].astype(F32)
        grad = grad_in[at, :]
        scale = lax.rsqrt(jnp.mean(value * value, axis=-1, keepdims=True) + NORM_EPS)
        r["gain_sum"][...] += jnp.sum(grad * value * scale, axis=0, keepdims=True)
        ge = gain * grad
        inner = jnp.mean(ge * value, axis=-1, keepdims=True)
        grad_in[at, :] = (
            r["grad_resid"][at, :] + scale * ge - value * (scale * scale * scale) * inner
        )

    def input_norm():
        r["gain_sum"][...] = jnp.zeros_like(r["gain_sum"])
        row_loop(grad_in.shape[0], norm_rows, step=16)


    small, small_got = r["small_out"], r["small_got"]
    steps = [over_f(1), over_f(2), over_c(1)]
    mask = 2
    while mask < n_ctx:
        steps.append(over_c(mask))
        mask *= 2
    small_copies = {}

    def small_start(s):
        small_got[s, 0] = small[...]
        small_copies[s] = send(
            small_got.at[s, 0],
            small_got.at[s, 1],
            r["s_send"].at[s],
            r["s_recv"].at[s],
            steps[s],
        )

    def small_end(s):
        small_copies[s].wait_recv()
        small[...] = small[...] + small_got[s, 1]

    def small_first():
        small[...] = r["small"][...]
        for i in range(width // 128):
            small[i : i + 1, :] = r["gain_sum"][:, i * 128 : (i + 1) * 128]
        for s in range(2):
            small_start(s)
            small_end(s)
        small_start(2)

    advance("out", "up", (low_keys, input_products, input_norm, small_first))
    put_out("gate")
    advance("qup", "out")
    finish_sum("up")
    advance("low", "qup")
    finish_sum("out")
    small_end(2)
    small_start(3)
    put_out("up")
    finish_sum("qup")
    advance(None, "low")
    for s in range(3, len(steps)):
        if s > 3:
            small_start(s)
        small_end(s)
    finish_sum("low")
    put_out("qup")
    put_out("low")
    send.finish()
    for m in TAIL_NAMES:
        lines[m].finish()


def tail_reduce(n_ctx, n_f, inputs, q_width):
    n_z = n_ctx // 2
    vmem = pl.BlockSpec(memory_space=pltpu.VMEM)
    anywhere = pl.BlockSpec(memory_space=pl.ANY)
    rows, width = inputs["hidden"].shape
    kv_width = inputs["w_kv"].shape[1]
    in_hbm = ("gate", "kv", "up", "up_got", "out", "qup")
    names_in = tuple(inputs)
    in_specs = [anywhere if m in in_hbm else vmem for m in names_in]
    block = {m: inputs[m].shape[-2:] for m in in_hbm}
    cut_q, cut_kv, high = q_width // n_f, kv_width // n_f, width // n_ctx
    block["low"] = (high, cut_q + cut_kv)
    outs = {
        "small_out": jax.ShapeDtypeStruct(inputs["small"].shape, F32),
        "grad_input": jax.ShapeDtypeStruct((rows, width), F32),
        "out_qd": jax.ShapeDtypeStruct((high // n_f, q_width), F32),
        "out_kvw": jax.ShapeDtypeStruct((high // n_f, kv_width), F32),
    }
    scratch = {}
    for m in TAIL_NAMES:
        high, wide = block[m]
        scratch["pair_" + m] = pltpu.VMEM((n_z, high, wide), BF16)
        scratch["z_" + m] = pltpu.VMEM((n_z + 1, high, wide), BF16)
        if m in TAIL_SENT:
            scratch["y_" + m] = pltpu.VMEM((n_z, high, wide), BF16)
        if m in TAIL_CUT:
            scratch["tot_" + m] = pltpu.VMEM((high, wide), BF16)
            scratch["f_" + m] = pltpu.VMEM((n_f - 1, high // n_f, wide), BF16)
            if m != "low":
                outs["out_" + m] = jax.ShapeDtypeStruct((high // n_f, wide * n_f), F32)
        elif m != "kv":
            outs["out_" + m] = jax.ShapeDtypeStruct((high, wide), F32)
    scratch["dkv"] = pltpu.VMEM((rows, kv_width), BF16)
    scratch["qd_group"] = pltpu.VMEM((rows * n_f, q_width // n_f), BF16)
    scratch["kv_group"] = pltpu.VMEM((rows * n_f, kv_width // n_f), BF16)
    scratch["part_low"] = pltpu.VMEM((n_z, 2) + block["low"], BF16)
    scratch["gain_sum"] = pltpu.VMEM((1, width), F32)
    steps = 2 + (n_ctx.bit_length() - 1)
    scratch["small_got"] = pltpu.VMEM((steps, 2) + inputs["small"].shape, F32)
    dma = pltpu.SemaphoreType.DMA
    sent, cut = len(TAIL_SENT), len(TAIL_CUT)
    scratch["s_send"] = dma((steps,))
    scratch["s_recv"] = dma((steps,))
    scratch["y_send"] = dma((sent, n_z))
    scratch["y_recv"] = dma((sent, n_z))
    scratch["keep_sem"] = dma((sent, n_z + 1))
    scratch["z_send"] = dma((len(TAIL_NAMES), n_z))
    scratch["z_recv"] = dma((len(TAIL_NAMES), n_z + 1))
    scratch["f_send"] = dma((cut, n_f - 1))
    scratch["f_recv"] = dma((cut, n_f - 1))
    scratch["low_send"] = dma((2, n_f - 1))
    scratch["low_recv"] = dma((2, n_f - 1))
    values = pl.pallas_call(
        functools.partial(tail_kernel, n_ctx, n_f, names_in, tuple(outs), tuple(scratch)),
        out_shape=tuple(outs.values()),
        in_specs=in_specs,
        out_specs=tuple([vmem] * len(outs)),
        scratch_shapes=list(scratch.values()),
        compiler_params=pltpu.CompilerParams(
            collective_id=0, has_side_effects=True, vmem_limit_bytes=60 << 20
        ),
        name="tail_reduce",
    )(*inputs.values())
    return dict(zip(outs, values, strict=True))


def split_columns(width):
    return slice(0, width // 2), slice(width // 2, width)


def front_kernel(n_ctx, n_f, names, *refs):
    r = dict(zip(names, refs, strict=True))
    n_z = n_ctx // 2
    c_idx = lax.axis_index("ctx")
    f_idx = lax.axis_index("fsdp")
    y_idx = c_idx % 2
    z_bit = (c_idx // 2) % 2
    x_idx = f_idx // 2
    k_idx = f_idx % 2
    far_idx = flip(f_idx, 2)
    moves = Sender()
    local = []
    at_sem = [0]

    def over_c(mask):
        return (flip(c_idx, mask), f_idx)

    def over_f(mask):
        return (c_idx, flip(f_idx, mask))

    def send(src, dst, peer):
        i = at_sem[0]
        at_sem[0] += 1
        return moves(src, dst, r["send_sem"].at[i], r["recv_sem"].at[i], peer)

    def keep(src, dst):
        copy = pltpu.make_async_copy(src, dst, r["local_sem"].at[len(local)])
        copy.start()
        local.append(copy)
        return copy

    def rows(start, size):
        return pl.ds(pl.multiple_of(start, size), size)

    barrier = pltpu.get_barrier_semaphore()
    for mask in range(1, n_f):
        pl.semaphore_signal(barrier, inc=1, device_id=over_f(mask), device_id_type=MESH)
    for mask in range(1, n_ctx):
        pl.semaphore_signal(barrier, inc=1, device_id=over_c(mask), device_id_type=MESH)
    pl.semaphore_wait(barrier, n_f - 1 + n_ctx - 1)

    infos, tags = r["infos"], r["tags"]
    infos[f_idx] = r["info"][...]
    info_copies = [
        send(infos.at[f_idx], infos.at[f_idx], over_f(mask)) for mask in range(1, n_f)
    ]

    class Rows:
        def __init__(self, shard, dest, bit, hop, chunks):
            self.dest, self.bit, self.hop = dest, bit, hop
            self.shard = shard
            self.size = shard.shape[0]
            self.half = self.size // 2
            self.step = self.half // chunks
            self.chunks = chunks
            self.far, self.next, self.cross = [], [], []

        def start(self, spare=None):
            mine = self.dest.at[rows(f_idx * self.size, self.size)]
            if spare is None:
                self.kept = keep(self.shard, mine)
            else:
                self.spare, self.kept = spare, keep(self.shard, spare)
            self.cross.append(send(self.shard, mine, over_f(1)))

        def settle(self):
            self.kept.wait()
            keep(self.spare, self.dest.at[rows(f_idx * self.size, self.size)])

        def reach(self, i):
            part = self.bit * self.half + i * self.step
            self.far.append(
                send(
                    self.shard.at[rows(part, self.step)],
                    self.dest.at[rows(f_idx * self.size + part, self.step)],
                    over_f(2),
                )
            )

        def place(self, bit, i):
            return self.dest.at[rows(far_idx * self.size + bit * self.half + i * self.step, self.step)]

        def hop_on(self, i):
            self.far[i].wait_recv()
            reach_next()
            here = self.place(self.bit, i)
            self.next.append(send(here, here, over_c(self.hop)))
            self.cross.append(send(here, here, over_f(1)))

        def pass_on(self, i):
            self.next[i].wait_recv()
            here = self.place(1 - self.bit, i)
            self.cross.append(send(here, here, over_f(1)))

        def end(self):
            for copy in self.cross:
                copy.wait_recv()

    class Columns:
        def __init__(self, shard, dest, box, bits, hops):
            self.shard, self.dest, self.box = shard, dest, box
            self.bits, self.hops = bits, hops
            self.size = shard.shape[0]
            self.width = dest.shape[1]
            self.quarter = self.size // 4

        def columns(self, start, count=1):
            return pl.ds(pl.multiple_of(start * self.width, 128), count * self.width)

        def start(self, spare):
            mine = self.dest.at[rows(f_idx * self.size, self.size)]
            self.spare, self.kept = spare, keep(self.shard.at[:, self.columns(f_idx)], spare)
            self.cross = [send(self.shard.at[:, self.columns(flip(f_idx, 1))], mine, over_f(1))]

        def settle(self):
            self.kept.wait()
            keep(self.spare, self.dest.at[rows(f_idx * self.size, self.size)])

        def reach(self, i):
            one, two = self.bits
            at = rows((two * 2 + one) * self.quarter, self.quarter)
            self.far = send(
                self.shard.at[at, self.columns((1 - x_idx) * 2, 2)], self.box.at[at], over_f(2)
            )

        def piece(self, one, two):
            return self.box.at[rows((two * 2 + one) * self.quarter, self.quarter)]

        def first(self):
            one, two = self.bits
            self.far.wait_recv()
            reach_next()
            here = self.piece(one, two)
            self.step = send(here, here, over_c(self.hops[0]))
            self.last = [send(here, here, over_c(self.hops[1]))]

        def second(self):
            one, two = self.bits
            self.step.wait_recv()
            here = self.piece(1 - one, two)
            self.last.append(send(here, here, over_c(self.hops[1])))

        def part(self):
            for copy in self.last:
                copy.wait_recv()
            there = self.dest.at[rows(far_idx * self.size, self.size)]
            self.cross.append(send(self.box.at[:, self.columns(1 - k_idx)], there, over_f(1)))
            keep(self.box.at[:, self.columns(k_idx)], there)

        def end(self):
            for copy in self.cross:
                copy.wait_recv()

    kv = Rows(r["kv_weight"], r["kv_full"], y_idx, 1, 1)
    qd = Rows(r["q_down"], r["qd_full"], y_idx, 1, 1)
    qu = Rows(r["q_up"], r["qu_full"], z_bit, 2, 2)
    left, right = split_columns(r["out_proj"].shape[1])
    outs = [
        Rows(r["out_proj"].at[:, left], r["w_out"].at[:, left], y_idx, 1, 2),
        Rows(r["out_proj"].at[:, right], r["w_out"].at[:, right], z_bit, 2, 2),
    ]
    gate = Columns(r["w_gate"], r["gate_full"], r["gate_box"], (y_idx, z_bit), (1, 2))
    up = Columns(r["w_up"], r["up_full"], r["up_box"], (z_bit, y_idx), (2, 1))
    queue = [(kv, 0), (qd, 0), (qu, 0), (qu, 1), (gate, 0), (up, 0)]
    queue += [(out, i) for i in range(2) for out in outs]

    def reach_next():
        if queue:
            part, i = queue.pop(0)
            part.reach(i)

    reach_next()
    reach_next()
    reach_next()
    kv.start()
    qd.start()

    for copy in info_copies:
        copy.wait_recv()
    d1 = r["gain_one"].shape[1] // n_f // 128
    d2 = r["gain_q"].shape[1] // n_f // 128
    count = infos[0, 2 * d1 + d2 : 2 * d1 + d2 + 1, :]
    for f in range(n_f):
        for i in range(d1):
            col = slice((f * d1 + i) * 128, (f * d1 + i + 1) * 128)
            r["gain_one"][:, col] = infos[f, i : i + 1, :]
            r["gain_two"][:, col] = infos[f, d1 + d2 + i : d1 + d2 + i + 1, :]
        for i in range(d2):
            col = slice((f * d2 + i) * 128, (f * d2 + i + 1) * 128)
            r["gain_q"][:, col] = infos[f, d1 + i : d1 + i + 1, :]
        if f:
            count = count + infos[f, 2 * d1 + d2 : 2 * d1 + d2 + 1, :]
    tags[c_idx] = r["tag"][...]
    tags[c_idx, 1:2, :] = count
    tag_copies = [send(tags.at[c_idx], tags.at[c_idx], over_c(mask)) for mask in range(1, n_ctx)]

    normed = r["normed"]
    gain_one = r["gain_one"][...]

    def norm_rows(at):
        value = r["hidden"][at, :].astype(F32)
        scale = lax.rsqrt(jnp.mean(value * value, axis=-1, keepdims=True) + NORM_EPS)
        normed[at, :] = (value * scale * gain_one).astype(BF16)

    row_loop(normed.shape[0], norm_rows, step=16)

    kv.hop_on(0)
    qd.hop_on(0)
    qu.start()
    kv.pass_on(0)
    qd.pass_on(0)
    kv.end()
    kv.kept.wait()
    head = r["kv_full"].shape[1] // 2
    mid = head // 2
    cos, sin = r["cos"], r["sin"]
    kv_rows = r["kv_rows"]
    keys = jnp.dot(normed[...], r["kv_full"][:, :head], preferred_element_type=F32)
    one, two = keys[:, :mid], keys[:, mid:]
    kv_rows[:, :mid] = (one * cos[...] - two * sin[...]).astype(BF16)
    kv_rows[:, mid:head] = (two * cos[...] + one * sin[...]).astype(BF16)
    kv_rows[:, head:] = jnp.dot(
        normed[...], r["kv_full"][:, head:], preferred_element_type=F32
    ).astype(BF16)
    all_kv = r["all_kv"]
    tokens = normed.shape[0]

    def kv_place(c):
        return all_kv.at[rows(c * tokens, tokens)]

    kv_z = [send(kv_rows, kv_place(c_idx), over_c(2 * s)) for s in range(1, n_z)]
    kv_y = [send(kv_rows, kv_place(c_idx), over_c(1))]
    keep(kv_rows, kv_place(c_idx))
    qu.hop_on(0)
    qd.end()
    qd.kept.wait()

    @pl.loop(0, r["q_low"].shape[1] // 256)
    def _(t):
        at = pl.ds(pl.multiple_of(t * 256, 256), 256)
        r["q_low"][:, at] = jnp.dot(
            normed[...], r["qd_full"][:, at], preferred_element_type=F32
        )

    gain_q = r["gain_q"][...]

    def norm_low(at):
        value = r["q_low"][at, :]
        scale = lax.rsqrt(jnp.mean(value * value, axis=-1, keepdims=True) + NORM_EPS)
        r["q_normed"][at, :] = (value * scale * gain_q).astype(BF16)

    row_loop(tokens, norm_low, step=16)
    qu.hop_on(1)
    gate.first()
    for s in range(1, n_z):
        kv_z[s - 1].wait_recv()
        here = kv_place(flip(c_idx, 2 * s))
        kv_y.append(send(here, here, over_c(1)))
    qu.pass_on(0)
    qu.pass_on(1)
    up.first()
    qu.end()
    gate.start(r["gate_spare"])
    up.start(r["up_spare"])
    outs[0].start(r["out_spare"].at[:, left])
    outs[1].start(r["out_spare"].at[:, right])
    qu.kept.wait()

    @pl.loop(0, r["q_rot"].shape[1] // head)
    def _(h):
        start = pl.multiple_of(h * head, head)
        value = jnp.dot(
            r["q_normed"][...],
            r["qu_full"][:, pl.ds(start, head)],
            preferred_element_type=F32,
        )
        one, two = value[:, :mid], value[:, mid:]
        r["q_rot"][:, pl.ds(start, mid)] = (one * cos[...] - two * sin[...]).astype(BF16)
        late = pl.multiple_of(h * head + mid, mid)
        r["q_rot"][:, pl.ds(late, mid)] = (two * cos[...] + one * sin[...]).astype(BF16)

    for part in [gate, up] + outs:
        part.settle()
    for m in ("kv", "qd", "qu"):
        keep(r[m + "_full"], r["w_" + m])
    gate.second()
    for out in outs:
        out.hop_on(0)
    up.second()
    for out in outs:
        out.hop_on(1)
    gate.part()
    for i in range(2):
        for out in outs:
            out.pass_on(i)
    up.part()
    for copy in kv_y + tag_copies:
        copy.wait_recv()
    for part in [gate, up] + outs:
        part.end()
    for copy in local:
        if not any(copy is part.kept for part in [kv, qd, qu, gate, up] + outs):
            copy.wait()
    moves.finish()


def front(n_ctx, n_f, inputs, head_size):
    tokens, width = inputs["hidden"].shape
    shape = jax.ShapeDtypeStruct
    q_width = inputs["q_down"].shape[1]
    heads_width = inputs["q_up"].shape[1]
    part = inputs["w_gate"].shape[1] // n_f

    def whole(m):
        return (inputs[m].shape[0] * n_f, inputs[m].shape[1])

    in_hbm = ("q_down", "kv_weight", "q_up", "out_proj", "w_gate", "w_up")
    outs = {
        "w_qd": shape(whole("q_down"), BF16),
        "w_kv": shape(whole("kv_weight"), BF16),
        "w_qu": shape(whole("q_up"), BF16),
        "w_out": shape(whole("out_proj"), BF16),
        "gate_full": shape((width, part), BF16),
        "up_full": shape((width, part), BF16),
        "all_kv": shape((tokens * n_ctx, 2 * head_size), BF16),
        "normed": shape((tokens, width), BF16),
        "q_low": shape((tokens, q_width), F32),
        "q_normed": shape((tokens, q_width), BF16),
        "q_rot": shape((tokens, heads_width), BF16),
        "gain_one": shape((1, width), F32),
        "gain_q": shape((1, q_width), F32),
        "gain_two": shape((1, width), F32),
        "tags": shape((n_ctx, 8, 128), F32),
    }
    out_hbm = ("w_qd", "w_kv", "w_qu", "w_out", "gate_full", "up_full", "all_kv")
    box = (inputs["w_gate"].shape[0], 2 * part)
    dma = pltpu.SemaphoreType.DMA
    scratch = {
        "infos": pltpu.VMEM((n_f,) + inputs["info"].shape, F32),
        "qd_full": pltpu.VMEM(whole("q_down"), BF16),
        "kv_full": pltpu.VMEM(whole("kv_weight"), BF16),
        "qu_full": pltpu.VMEM(whole("q_up"), BF16),
        "gate_box": pltpu.VMEM(box, BF16),
        "up_box": pltpu.VMEM(box, BF16),
        "gate_spare": pltpu.VMEM((box[0], part), BF16),
        "up_spare": pltpu.VMEM((box[0], part), BF16),
        "out_spare": pltpu.VMEM(inputs["out_proj"].shape, BF16),
        "kv_rows": pltpu.VMEM((tokens, 2 * head_size), BF16),
        "send_sem": dma((64 + 2 * n_ctx,)),
        "recv_sem": dma((64 + 2 * n_ctx,)),
        "local_sem": dma((24,)),
    }
    vmem = pl.BlockSpec(memory_space=pltpu.VMEM)
    anywhere = pl.BlockSpec(memory_space=pl.ANY)
    names = tuple(inputs) + tuple(outs) + tuple(scratch)
    values = pl.pallas_call(
        functools.partial(front_kernel, n_ctx, n_f, names),
        out_shape=tuple(outs.values()),
        in_specs=[anywhere if m in in_hbm else vmem for m in inputs],
        out_specs=tuple([anywhere if m in out_hbm else vmem for m in outs]),
        scratch_shapes=list(scratch.values()),
        compiler_params=pltpu.CompilerParams(
            collective_id=1, has_side_effects=True, vmem_limit_bytes=48 << 20
        ),
        name="front",
    )(*inputs.values())
    return dict(zip(outs, values, strict=True))


def tiles(total, wide, body):
    whole = total // wide

    @pl.loop(0, whole)
    def _(t):
        body(pl.multiple_of(t * wide, wide), wide)

    if total % wide:
        body(whole * wide, total % wide)


def contract_first(a, b):
    return jnp.dot(a.T, b, preferred_element_type=F32)


def rows_product_kernel(a_ref, b_ref, o_ref):
    o_ref[...] = contract_last(a_ref[...], b_ref[...]).astype(BF16)


def rows_product(a, b, tile):
    return pl.pallas_call(
        rows_product_kernel,
        out_shape=jax.ShapeDtypeStruct((a.shape[0], b.shape[0]), BF16),
        grid=(b.shape[0] // tile,),
        in_specs=[
            pl.BlockSpec(a.shape, lambda i: (0, 0)),
            pl.BlockSpec((tile, b.shape[1]), lambda i: (i, 0)),
        ],
        out_specs=pl.BlockSpec((a.shape[0], tile), lambda i: (0, i)),
        compiler_params=pltpu.CompilerParams(vmem_limit_bytes=58 << 20),
        name="rows_product",
    )(a, b)


def ffn_kernel(n_f, names, *refs):
    r = dict(zip(names, refs, strict=True))
    c_idx = lax.axis_index("ctx")
    f_idx = lax.axis_index("fsdp")
    moves = Sender()
    at_sem = [0]
    core, far = (c_idx, flip(f_idx, 1)), (c_idx, flip(f_idx, 2))
    beside = (flip(c_idx, 1), f_idx)
    y_idx = c_idx % 2

    def send(src, dst, peer):
        i = at_sem[0]
        at_sem[0] += 1
        return moves(src, dst, r["send_sem"].at[i], r["recv_sem"].at[i], peer)

    barrier = pltpu.get_barrier_semaphore()
    for peer in (core, far, (c_idx, flip(f_idx, 3)), beside):
        pl.semaphore_signal(barrier, inc=1, device_id=peer, device_id_type=MESH)
    pl.semaphore_wait(barrier, 4)

    tokens, width = r["normed"].shape
    mine = r["attn_group"].at[pl.ds(pl.multiple_of(f_idx * tokens, tokens), tokens)]
    own_attn = pltpu.make_async_copy(r["attn_cut"].at[f_idx], mine, r["load_sem"].at[3])
    own_attn.start()

    def send_attn(mask):
        return send(r["attn_cut"].at[flip(f_idx, mask)], mine, (c_idx, flip(f_idx, mask)))

    units = r["w_down"].shape[0]
    group, dz = r["group"], r["dz"]
    block = [slice(i * tokens, (i + 1) * tokens) for i in range(4)]
    pair = [slice(0, 2 * tokens), slice(2 * tokens, 4 * tokens)]

    def gather(buf):
        to_core = send(buf.at[block[0]], buf.at[block[1]], core)
        to_far = send(buf.at[block[0]], buf.at[block[2]], far)
        return to_core, to_far

    def gather_far(buf, to_far):
        to_far.wait_recv()
        send(buf.at[block[2]], buf.at[block[3]], core).wait_recv()

    group[block[0], :] = r["normed"][...]
    to_core, to_far = gather(group)
    loads = []
    for i, m in enumerate(("gate", "up", "down")):
        load = pltpu.make_async_copy(r["w_" + m], r["v_" + m], r["load_sem"].at[i])
        load.start()
        loads.append(load)
    loads[0].wait()
    loads[1].wait()

    def hidden_part(rows):
        def one(start, wide):
            at = pl.ds(start, wide)
            both = jnp.concatenate([r["v_gate"][:, at], r["v_up"][:, at]], axis=1)
            out = jnp.dot(group[rows, :], both, preferred_element_type=F32)
            gate, up = out[:, :wide], out[:, wide:]
            r["gate"][rows, at] = gate.astype(BF16)
            r["up"][rows, at] = up.astype(BF16)
            r["hid"][rows, at] = (gate / (1.0 + jnp.exp(-gate)) * up).astype(BF16)

        tiles(units, 128, one)

    to_core.wait_recv()
    hidden_part(pair[0])
    gather_far(group, to_far)
    attn_copies = [send_attn(1), send_attn(2)]
    hidden_part(pair[1])
    loads[2].wait()

    def down_block(i, dest):
        def one(start, wide):
            at = pl.ds(start, wide)
            dest[:, at] = jnp.dot(
                r["hid"][block[i], :], r["v_down"][:, at], preferred_element_type=F32
            ).astype(dest.dtype)

        tiles(width, 256, one)

    def back_block(i, dest):
        def one(start, wide):
            at = pl.ds(start, wide)
            dest[:, at] = (
                contract_last(r["gate"][block[i], :], r["v_gate"][at, :])
                + contract_last(r["up"][block[i], :], r["v_up"][at, :])
            ).astype(dest.dtype)

        tiles(width, 256, one)

    def add_rows(dest, one, two):
        def add(at):
            dest[at, :] = (one[at, :].astype(F32) + two[at, :].astype(F32)).astype(dest.dtype)

        row_loop(tokens, add)

    def far_sum(k, make):
        make(3, r["give"].at[2 * k])
        step = send(r["give"].at[2 * k], r["got"].at[2 * k], core)
        make(2, r["far_sum"])
        step.wait_recv()
        add_rows(r["far_give"].at[k], r["far_sum"], r["got"].at[2 * k])
        return send(r["far_give"].at[k], r["far_got"].at[k], far)

    def near_sum(k, make):
        make(1, r["give"].at[2 * k + 1])
        step = send(r["give"].at[2 * k + 1], r["got"].at[2 * k + 1], core)
        make(0, r["near_sum"])
        return step

    def near_end(k, step):
        step.wait_recv()
        add_rows(r["near_sum"], r["near_sum"], r["got"].at[2 * k + 1])

    far_step = far_sum(0, down_block)
    near_end(0, near_sum(0, down_block))
    far_step.wait_recv()
    r["sq"][...] = jnp.zeros_like(r["sq"])

    def loss_rows(at):
        value = r["resid"][at, :] + r["near_sum"][at, :] + r["far_got"][0, at, :].astype(F32)
        r["result"][at, :] = value.astype(BF16)
        diff = value - r["teacher"][at, :].astype(F32)
        squares = jnp.sum(diff * diff, axis=1, keepdims=True) * r["valid"][at, :]
        r["sq"][:1, :] += jnp.sum(squares, axis=0, keepdims=True)
        grad = diff * r["valid_scale"][at, :1]
        r["grad_resid"][at, :] = grad
        dz[at, :] = grad.astype(BF16)

    row_loop(tokens, loss_rows, step=16)
    to_core, to_far = gather(dz)

    def back_hidden(rows):
        def one(start, wide):
            at = pl.ds(start, wide)
            grad = contract_last(dz[rows, :], r["v_down"][at, :])
            gate = r["gate"][rows, at].astype(F32)
            up = r["up"][rows, at].astype(F32)
            sigma = 1.0 / (1.0 + jnp.exp(-gate))
            r["gate"][rows, at] = (grad * up * sigma * (1.0 + gate * (1.0 - sigma))).astype(BF16)
            r["up"][rows, at] = (grad * (gate * sigma)).astype(BF16)

        tiles(units, 256, one)

    to_core.wait_recv()
    back_hidden(pair[0])
    near_step = near_sum(1, back_block)
    gather_far(dz, to_far)
    saves = []

    def save(src, dst, i):
        copy = pltpu.make_async_copy(src, dst, r["save_sem"].at[i])
        copy.start()
        return copy

    def down_tile(start, wide):
        at = pl.ds(start, wide)
        spot = r["tile"].at[pl.ds(0, wide)]
        spot[...] = contract_first(r["hid"][:, at], dz[...]).astype(BF16)
        save(spot, r["down_part"].at[at], 0).wait()

    count = units // 128
    first = (count + 1) // 2

    @pl.loop(0, first)
    def _(t):
        down_tile(pl.multiple_of(((count - first) * (1 - y_idx) + t) * 128, 128), 128)

    half = units // 2
    give = pl.ds(pl.multiple_of((1 - y_idx) * half, half), half)
    down_step = send(r["down_part"].at[give], r["down_got"], beside)
    attn_copies.append(send_attn(3))
    back_hidden(pair[1])
    far_step = far_sum(1, back_block)
    near_end(1, near_step)

    @pl.loop(0, count - first)
    def _(t):
        down_tile(pl.multiple_of((first * y_idx + t) * 128, 128), 128)

    def gate_tile(start, wide):
        at = pl.ds(start, wide)
        left = group[:, at].T
        for i, m in enumerate(("gate", "up")):
            spot = r["wide_tile"].at[i]
            spot[...] = jnp.dot(left, r[m][...], preferred_element_type=F32).astype(BF16)
            saves.append(save(spot, r[m + "_part"].at[at], 1 + i))
        saves.pop().wait()
        saves.pop().wait()

    tiles(width, 256, gate_tile)
    far_step.wait_recv()
    gain = r["gain_two"][...]
    r["gain_sum"][...] = jnp.zeros_like(r["gain_sum"])

    def norm_rows(at):
        grad = r["near_sum"][at, :] + r["far_got"][1, at, :].astype(F32)
        value = r["resid"][at, :]
        scale = lax.rsqrt(jnp.mean(value * value, axis=-1, keepdims=True) + NORM_EPS)
        r["gain_sum"][...] += jnp.sum(grad * value * scale, axis=0, keepdims=True)
        ge = gain * grad
        inner = jnp.mean(ge * value, axis=-1, keepdims=True)
        total = r["grad_resid"][at, :] + scale * ge - value * (scale * scale * scale) * inner
        r["grad_resid"][at, :] = total
        r["grad_branch"][at, :] = total.astype(BF16)

    row_loop(tokens, norm_rows, step=16)
    for copy in attn_copies + [down_step]:
        copy.wait_recv()
    own_attn.wait()
    moves.finish()


def feed_forward(n_f, inputs):
    tokens, width = inputs["normed"].shape
    units = inputs["w_down"].shape[0]
    shape = jax.ShapeDtypeStruct
    outs = {
        "result": shape((tokens, width), BF16),
        "grad_resid": shape((tokens, width), F32),
        "grad_branch": shape((tokens, width), BF16),
        "down_part": shape((units, width), BF16),
        "down_got": shape((units // 2, width), BF16),
        "gate_part": shape((width, units), BF16),
        "up_part": shape((width, units), BF16),
        "attn_group": shape((tokens * n_f, inputs["attn_cut"].shape[2]), BF16),
        "gain_sum": shape((1, width), F32),
        "sq": shape((8, 128), F32),
    }
    hbm = ("w_gate", "w_up", "w_down", "attn_cut", "attn_group")
    hbm += ("down_part", "down_got", "gate_part", "up_part")
    dma = pltpu.SemaphoreType.DMA
    many = tokens * n_f
    scratch = {
        "v_gate": pltpu.VMEM((width, units), BF16),
        "v_up": pltpu.VMEM((width, units), BF16),
        "v_down": pltpu.VMEM((units, width), BF16),
        "group": pltpu.VMEM((many, width), BF16),
        "dz": pltpu.VMEM((many, width), BF16),
        "gate": pltpu.VMEM((many, units), BF16),
        "up": pltpu.VMEM((many, units), BF16),
        "hid": pltpu.VMEM((many, units), BF16),
        "give": pltpu.VMEM((4, tokens, width), BF16),
        "got": pltpu.VMEM((4, tokens, width), BF16),
        "far_sum": pltpu.VMEM((tokens, width), F32),
        "near_sum": pltpu.VMEM((tokens, width), F32),
        "far_give": pltpu.VMEM((2, tokens, width), BF16),
        "far_got": pltpu.VMEM((2, tokens, width), BF16),
        "tile": pltpu.VMEM((128, width), BF16),
        "wide_tile": pltpu.VMEM((2, 256, units), BF16),
        "send_sem": dma((16,)),
        "recv_sem": dma((16,)),
        "load_sem": dma((4,)),
        "save_sem": dma((3,)),
    }
    vmem = pl.BlockSpec(memory_space=pltpu.VMEM)
    anywhere = pl.BlockSpec(memory_space=pl.ANY)
    names = tuple(inputs) + tuple(outs) + tuple(scratch)
    values = pl.pallas_call(
        functools.partial(ffn_kernel, n_f, names),
        out_shape=tuple(outs.values()),
        in_specs=[anywhere if m in hbm else vmem for m in inputs],
        out_specs=tuple([anywhere if m in hbm else vmem for m in outs]),
        scratch_shapes=list(scratch.values()),
        compiler_params=pltpu.CompilerParams(
            collective_id=2, has_side_effects=True, vmem_limit_bytes=60 << 20
        ),
        name="feed_forward",
    )(*inputs.values())
    return dict(zip(outs, values, strict=True))


def body(
    hidden_in,
    teacher,
    blocks,
    seq_ids,
    valid_mask,
    norm1_gain,
    q_down,
    q_gain,
    q_up,
    kv_weight,
    out_proj,
    norm2_gain,
    w_gate,
    w_up,
    w_down,
):
    row_count, model_width = hidden_in.shape
    head_size = kv_weight.shape[1] // 2
    heads_width = q_up.shape[1]
    head_count = heads_width // head_size
    half_dim = head_size // 2
    q_width = q_down.shape[1]
    n_ctx = lax.axis_size("ctx")
    n_f = lax.axis_size("fsdp")
    n_z = n_ctx // 2
    token_total = row_count * n_ctx * n_f
    seq_pieces = 2 * SEQ_BLOCKS
    c_idx = lax.axis_index("ctx")
    f_idx = lax.axis_index("fsdp")
    y_idx = c_idx % 2
    z_idx = c_idx // 2
    x_idx = f_idx // 2
    k_idx = f_idx % 2

    def by_f(values, mask):
        return lax.ppermute(values, "fsdp", [(i, i ^ mask) for i in range(n_f)])

    def by_c(values, mask):
        return lax.ppermute(values, "ctx", [(i, i ^ mask) for i in range(n_ctx)])

    def cut(values, start, size, axis):
        return lax.dynamic_slice_in_dim(values, start, size, axis)

    def ctx_split(grad):
        view = grad.reshape(n_z, 2, grad.shape[0] // n_ctx, grad.shape[1])
        give = lax.dynamic_index_in_dim(view, 1 - y_idx, 1, keepdims=False)
        keep = lax.dynamic_index_in_dim(view, y_idx, 1, keepdims=False)
        return give, keep

    def ctx_pair(keep, got):
        return (keep.astype(F32) + got.astype(F32)).astype(BF16)

    def ctx_spread(pair):
        return [pair] + [
            by_c(lax.dynamic_index_in_dim(pair, z_idx ^ r, 0, keepdims=False), 2 * r)
            for r in range(1, n_z)
        ]

    def ctx_total(parts):
        total = lax.dynamic_index_in_dim(parts[0], z_idx, 0, keepdims=False).astype(F32)
        for got in parts[1:]:
            total = total + got.astype(F32)
        return total

    def group_rows(values):
        return lax.all_gather(values, "fsdp", axis=0, tiled=True)

    valid_f = valid_mask.astype(F32)
    own_pieces = row_count // PIECE
    info = jnp.concatenate(
        [
            norm1_gain.astype(F32),
            q_gain.astype(F32),
            norm2_gain.astype(F32),
            jnp.full((128,), jnp.sum(valid_f)),
        ]
    )
    info = jnp.pad(info, (0, -info.shape[0] % 1024)).reshape(-1, 128)
    own_tags = jnp.stack([blocks.reshape(-1, PIECE)[:, 0], seq_ids.reshape(-1, PIECE)[:, 0]], 1)
    tag = jnp.pad(own_tags.astype(F32).reshape(1, -1), ((0, 7), (0, 128 - 2 * own_pieces)))
    own = jnp.concatenate([blocks.reshape(-1, PIECE)[:, 0], seq_ids[:1]])

    positions = blocks * PIECE + jnp.arange(row_count, dtype=jnp.int32) % PIECE
    freq_table = 10000.0 ** (-(jnp.arange(half_dim, dtype=F32) * 2.0 / head_size))
    angle_table = positions.astype(F32)[:, None] * freq_table[None, :]
    cosine = jnp.cos(angle_table)
    sine = jnp.sin(angle_table)
    fetched = front(
        n_ctx,
        n_f,
        {
            "q_down": q_down,
            "kv_weight": kv_weight,
            "q_up": q_up,
            "out_proj": out_proj,
            "w_gate": w_gate,
            "w_up": w_up,
            "hidden": hidden_in,
            "info": info,
            "tag": tag,
            "cos": cosine,
            "sin": sine,
        },
        head_size,
    )
    w_out = fetched["w_out"]
    all_kv, q_rot = fetched["all_kv"], fetched["q_rot"]
    normed, q_low, q_normed = fetched["normed"], fetched["q_low"], fetched["q_normed"]
    gain_one, gain_q, gain_two = fetched["gain_one"], fetched["gain_q"], fetched["gain_two"]
    tags = fetched["tags"][:, 0, : 2 * own_pieces].reshape(-1, 2).astype(jnp.int32)
    total_count = jnp.sum(fetched["tags"][:, 1, 0])
    hidden_f = hidden_in.astype(F32)
    scale_q = rms_scale(q_low)

    out_block = heads_width // (n_ctx * n_f)
    if out_block == 128:
        attn_heads, lse, attn_cut = attn_fwd(
            tags, own, q_rot, all_kv, head_size, seq_pieces, n_f, True
        )
    else:
        attn_heads, lse = attn_fwd(tags, own, q_rot, all_kv, head_size, seq_pieces, n_f, False)
        attn_cut = attn_heads.reshape(row_count, n_ctx, n_f, out_block).transpose(2, 0, 1, 3)
        attn_cut = attn_cut.reshape(n_f, row_count, n_ctx * out_block)
    resid = hidden_f + dot(attn_heads, w_out)
    scale_two = rms_scale(resid)
    normed_two = (resid * scale_two * gain_two).astype(BF16)

    wide_valid = jnp.broadcast_to(valid_f[:, None], (row_count, 128))
    ffn = feed_forward(
        n_f,
        {
            "normed": normed_two,
            "resid": resid,
            "teacher": teacher,
            "valid": wide_valid,
            "valid_scale": wide_valid * (token_total / total_count),
            "gain_two": gain_two,
            "w_gate": fetched["gate_full"],
            "w_up": fetched["up_full"],
            "w_down": w_down,
            "attn_cut": attn_cut,
        },
    )
    grad_resid, grad_branch = ffn["grad_resid"], ffn["grad_branch"]
    grad_gain_two = ffn["gain_sum"].reshape(-1)
    sq_local = ffn["sq"][0, 0]
    half_units = w_down.shape[0] // 2
    down_pair = ctx_pair(cut(ffn["down_part"], y_idx * half_units, half_units, 0), ffn["down_got"])
    down_parts = ctx_spread(down_pair.reshape(n_z, -1, model_width))
    gate_give, gate_keep = ctx_split(ffn["gate_part"])
    gate_got = by_c(gate_give, 1)
    early = n_z // 2
    up_blocks = ffn["up_part"].reshape(n_z, 2, model_width // n_ctx, -1)
    up_got = by_c(
        lax.dynamic_index_in_dim(up_blocks[:early], 1 - y_idx, 1, keepdims=False), 1
    )
    branch_group = group_rows(grad_branch)
    grad_attn = rows_product(grad_branch, w_out, 512)
    grad_qlin, grad_seq = attn_bwd(
        tags, own, q_rot, grad_attn, attn_heads, lse, cosine, sine, all_kv, head_size, seq_pieces
    )
    qlin_group = lax.all_to_all(grad_qlin, "fsdp", 1, 0, tiled=True)
    down_parts, gate_got, grad_seq = together(down_parts, gate_got, grad_seq)

    by_piece = grad_seq.reshape(seq_pieces, PIECE, 2 * head_size)
    piece_tag = tags[:, 0].reshape(n_z, 2, own_pieces)
    piece_own = (tags[:, 1] == seq_ids[0]).reshape(n_z, 2, own_pieces)

    def kv_half(bit):
        places = lax.dynamic_index_in_dim(piece_tag, bit, 1, keepdims=False).reshape(-1)
        picked = by_piece[places]
        if n_ctx * own_pieces != seq_pieces:
            mine = lax.dynamic_index_in_dim(piece_own, bit, 1, keepdims=False).reshape(-1)
            picked = jnp.where(mine[:, None, None], picked, jnp.zeros_like(picked))
        return picked.reshape(n_z, own_pieces * PIECE, 2 * head_size)

    kv_part = jnp.stack([kv_half(0), kv_half(1)], axis=1)
    q_cut, kv_cut = q_width // n_f, 2 * head_size // n_f
    qnorm_group = group_rows(q_normed)
    normed_group = group_rows(normed)

    grad_qnormed = dot_t(grad_qlin, fetched["w_qu"])
    grad_qlow_f, grad_gain_q = rms_back(q_low, scale_q, gain_q, grad_qnormed)
    grad_qlow = grad_qlow_f.astype(BF16)
    attn_group = ffn["attn_group"]
    da_q = dot_t(grad_qlow, fetched["w_qd"])
    gate_pair = ctx_pair(gate_keep, gate_got)
    out_part = dot_rows(attn_group, branch_group).astype(BF16)
    qup_part = dot_rows(qnorm_group, qlin_group).astype(BF16)

    def by_ctx(grad):
        return grad.reshape(n_z, 2, grad.shape[0] // n_ctx, grad.shape[1])

    order = [
        (c * n_f + f, f * n_ctx + c % 2 * n_z + c // 2) for c in range(n_ctx) for f in range(n_f)
    ]
    down_rows = ctx_total(down_parts).astype(BF16)
    down_sent = lax.ppermute(down_rows, ("ctx", "fsdp"), order)

    up_got, out_part, qup_part = together(up_got, out_part, qup_part)

    small = jnp.concatenate(
        [jnp.zeros((model_width,), F32), grad_gain_q, grad_gain_two, sq_local.reshape(1)]
    )
    entries = small.shape[0]
    small = jnp.pad(small, (0, -entries % 1024)).reshape(-1, 128)
    ends = tail_reduce(
        n_ctx,
        n_f,
        {
            "gate": gate_pair,
            "kv": kv_part,
            "up": up_blocks,
            "up_got": up_got,
            "out": by_ctx(out_part),
            "qup": by_ctx(qup_part),
            "dqa": grad_qlow,
            "cos": cosine,
            "sin": sine,
            "normed_group": normed_group,
            "w_kv": fetched["w_kv"],
            "da_q": da_q,
            "hidden": hidden_in,
            "gain_one": gain_one,
            "grad_resid": grad_resid,
            "small": small,
        },
        q_width,
    )
    small, down_sent = together(ends["small_out"], down_sent)
    small = small.reshape(-1)[:entries]
    grad_down = down_sent.astype(F32)

    device = c_idx * n_f + f_idx
    q1, q2 = model_width, model_width + q_width
    n_dev = n_ctx * n_f

    def own_part(values):
        size = values.shape[0] // n_dev
        return cut(values, device * size, size, 0)

    loss_now = small[-1] / (model_width * total_count)
    return (
        ffn["result"],
        loss_now,
        ends["grad_input"],
        own_part(small[:q1]),
        ends["out_qd"],
        own_part(small[q1:q2]),
        ends["out_qup"],
        ends["out_kvw"],
        ends["out_out"],
        own_part(small[q2 : q2 + model_width]),
        ends["out_gate"],
        ends["out_up"],
        grad_down,
    )


def solution(mesh):
    both = ("ctx", "fsdp")
    rows = P(both, None)
    flat = P(both)
    shard = P("fsdp", None)
    gain = P("fsdp")
    return jax.shard_map(
        body,
        mesh=mesh,
        in_specs=(
            rows,
            rows,
            flat,
            flat,
            flat,
            gain,
            shard,
            gain,
            shard,
            shard,
            shard,
            gain,
            shard,
            shard,
            shard,
        ),
        out_specs=(
            rows,
            P(),
            rows,
            flat,
            rows,
            flat,
            rows,
            rows,
            rows,
            flat,
            rows,
            rows,
            rows,
        ),
        check_vma=False,
    )
```

```python
import functools
import math

import jax
import jax.numpy as jnp
from jax import lax
from jax.experimental import pallas as pl
from jax.experimental.pallas import tpu as pltpu
from jax.sharding import PartitionSpec as P

PIECE = 128
SEQ_BLOCKS = 8
NORM_EPS = 1e-05
F32 = jnp.float32
BF16 = jnp.bfloat16
LOG2E = math.log2(math.e)
HEAD_GROUP = 16


def rms_scale(values):
    return lax.rsqrt(jnp.mean(values * values, axis=-1, keepdims=True) + NORM_EPS)


def rms_back(values, scale, gain, grad):
    grad_gain = jnp.sum(grad * values * scale, axis=0)
    ge = gain * grad
    inner = jnp.mean(ge * values, axis=-1, keepdims=True)
    return scale * ge - values * (scale * scale * scale) * inner, grad_gain


def rope_apply(values, cosine, sine):
    half_dim = values.shape[-1] // 2
    one = values[..., :half_dim]
    two = values[..., half_dim:]
    return jnp.concatenate([one * cosine - two * sine, two * cosine + one * sine], axis=-1)


def rope_back(grads, cosine, sine):
    half_dim = grads.shape[-1] // 2
    one = grads[..., :half_dim]
    two = grads[..., half_dim:]
    return jnp.concatenate([one * cosine + two * sine, two * cosine - one * sine], axis=-1)


def together(*values):
    return lax.optimization_barrier(values)


def dot(a, b):
    return jnp.dot(a, b, preferred_element_type=F32)


def dot_t(a, b):
    return lax.dot_general(a, b, (((1,), (1,)), ((), ())), preferred_element_type=F32)


def dot_rows(a, b):
    return lax.dot_general(a, b, (((0,), (0,)), ((), ())), preferred_element_type=F32)


def contract_last(a, b):
    return lax.dot_general(a, b, (((1,), (1,)), ((), ())), preferred_element_type=F32)

def find_pieces(tags_ref, own_ref, pick_ref, total):
    @pl.loop(0, total)
    def _(u):
        @pl.when(tags_ref[u, 1] == own_ref[2])
        def _():
            pick_ref[tags_ref[u, 0]] = u

def stack_heads(ref, hd):
    return jnp.concatenate([ref[:, h*hd:(h+1)*hd] for h in range(HEAD_GROUP)], axis=0)

def attn_fwd_kernel(n_f, tags_ref, own_ref, q_ref, kv_ref, o_ref, lse_ref, *rest):
    k_s, vt_s, acc_s, pick_s = rest[-4:]
    half = pl.program_id(0)
    hd = k_s.shape[1]
    pieces = k_s.shape[0] // PIECE
    total = kv_ref.shape[0] // PIECE
    wide = 2 * PIECE
    coef = hd ** -0.5 * LOG2E

    @pl.when((half == 0) & (pl.program_id(1) == 0))
    def _():
        find_pieces(tags_ref, own_ref, pick_s, total)
        for i in range(pieces):
            rows = pl.ds(pl.multiple_of(pick_s[i] * PIECE, PIECE), PIECE)
            k_s[i*PIECE:(i+1)*PIECE, :] = kv_ref[rows, :hd]
            vt_s[:, i*PIECE:(i+1)*PIECE] = kv_ref[rows, hd:].T

    q = stack_heads(q_ref, hd)
    acc_s[...] = jnp.zeros_like(acc_s)
    rows = q.shape[0]
    def step(i, carry):
        peak, total_p = carry
        at = pl.ds(pl.multiple_of(i * wide, wide), wide)
        raw = contract_last(k_s[at, :], q)
        top = jnp.maximum(peak, jnp.max(raw, axis=0, keepdims=True))
        fade = jnp.exp2((peak - top) * coef)
        p = jnp.exp2((raw - top) * coef)
        acc_s[...] = acc_s[...] * fade + jnp.dot(vt_s[:, at], p.astype(BF16), preferred_element_type=F32)
        return top, total_p * fade + jnp.sum(p, axis=0, keepdims=True)
    count = own_ref[half] // 2 + 1
    peak, total_p = lax.fori_loop(0, count, step, (jnp.full((1, rows), -1e30, F32), jnp.zeros((1, rows), F32)))
    out = (acc_s[...] / total_p).astype(BF16).T
    for h in range(HEAD_GROUP):
        o_ref[:, h*hd:(h+1)*hd] = out[h*PIECE:(h+1)*PIECE, :]
    if len(rest) > 4:
        for b in range(HEAD_GROUP * hd // 128):
            head, part = b * 128 // hd, b * 128 % hd
            rest[0][b % n_f, :, b // n_f * 128:(b // n_f + 1) * 128] = out[
                head*PIECE:(head+1)*PIECE, part:part+128
            ]
    lse_ref[0] = peak * coef + jnp.log2(total_p)

def attn_fwd(tags, own, q, kv, hd, pieces, n_f, cut):
    n_rows, width = q.shape
    groups = width // hd // HEAD_GROUP
    gw = HEAD_GROUP * hd
    halves = n_rows // PIECE
    rows = HEAD_GROUP * PIECE
    blk = pl.BlockSpec((PIECE, gw), lambda p, g, *_: (p, g))
    flops = 4 * n_rows * width * pieces * PIECE * 9 // 16
    shapes = [jax.ShapeDtypeStruct(q.shape, BF16), jax.ShapeDtypeStruct((halves*groups, 1, rows), F32)]
    specs = [blk, pl.BlockSpec((1, 1, rows), lambda p, g, *_: (p*groups+g, 0, 0))]
    if cut:
        shapes.append(jax.ShapeDtypeStruct((n_f, n_rows, width // n_f), BF16))
        specs.append(pl.BlockSpec((n_f, PIECE, gw // n_f), lambda p, g, *_: (0, p, g)))
    return pl.pallas_call(
        functools.partial(attn_fwd_kernel, n_f),
        out_shape=tuple(shapes),
        grid_spec=pltpu.PrefetchScalarGridSpec(
            num_scalar_prefetch=2, grid=(halves, groups),
            in_specs=[blk, pl.BlockSpec(kv.shape, lambda p, g, *_: (0, 0))],
            out_specs=tuple(specs),
            scratch_shapes=[pltpu.VMEM((pieces*PIECE, hd), BF16), pltpu.VMEM((hd, pieces*PIECE), BF16),
                            pltpu.VMEM((hd, rows), F32), pltpu.SMEM((pieces,), jnp.int32)]),
        compiler_params=pltpu.CompilerParams(vmem_limit_bytes=40 << 20),
        cost_estimate=pl.CostEstimate(flops=flops, transcendentals=flops//(4*hd), bytes_accessed=2*(2*q.size+kv.size)),
        name="attn_fwd",
    )(tags, own, q, kv)

def attn_bwd_kernel(tags_ref, own_ref, q_ref, do_ref, o_ref, lse_ref, cos_ref, sin_ref, kv_ref, dq_ref, dkv_ref,
                    k_s, kt_s, v_s, dq_s, dk_s, dv_s, pick_s):
    half = pl.program_id(0)
    group = pl.program_id(1)
    hd = k_s.shape[1]
    pieces = k_s.shape[0] // PIECE
    total = kv_ref.shape[0] // PIECE
    wide = 2 * PIECE
    coef = hd ** -0.5 * LOG2E
    scale = hd ** -0.5

    @pl.when((half == 0) & (group == 0))
    def _():
        find_pieces(tags_ref, own_ref, pick_s, total)
        for i in range(pieces):
            rows = pl.ds(pl.multiple_of(pick_s[i] * PIECE, PIECE), PIECE)
            keys = kv_ref[rows, :hd]
            k_s[i*PIECE:(i+1)*PIECE, :] = keys
            kt_s[:, i*PIECE:(i+1)*PIECE] = keys.T
            v_s[i*PIECE:(i+1)*PIECE, :] = kv_ref[rows, hd:]
        dk_s[...] = jnp.zeros_like(dk_s)
        dv_s[...] = jnp.zeros_like(dv_s)

    q = stack_heads(q_ref, hd)
    do = stack_heads(do_ref, hd)
    prod = do.astype(F32) * stack_heads(o_ref, hd).astype(F32)
    delta = lax.dot_general(jnp.ones((8, hd), F32), prod, (((1,), (1,)), ((), ())),
                            preferred_element_type=F32, precision=lax.Precision.HIGHEST)[:1]
    lse = lse_ref[0]
    dq_s[...] = jnp.zeros_like(dq_s)
    def step(i, carry):
        at = pl.ds(pl.multiple_of(i * wide, wide), wide)
        p = jnp.exp2(contract_last(k_s[at, :], q) * coef - lse)
        dp = contract_last(v_s[at, :], do)
        ds = (p * (dp - delta)).astype(BF16)
        dv_s[at, :] += jnp.dot(p.astype(BF16), do, preferred_element_type=F32)
        dk_s[at, :] += jnp.dot(ds, q, preferred_element_type=F32)
        dq_s[...] += jnp.dot(kt_s[:, at], ds, preferred_element_type=F32)
        return carry
    lax.fori_loop(0, own_ref[half] // 2 + 1, step, 0)
    dq = (dq_s[...] * scale).T
    cos, sin = cos_ref[...], sin_ref[...]
    mid = hd // 2
    for h in range(HEAD_GROUP):
        one = dq[h*PIECE:(h+1)*PIECE, :mid]
        two = dq[h*PIECE:(h+1)*PIECE, mid:]
        dq_ref[:, h*hd:h*hd+mid] = (one * cos + two * sin).astype(BF16)
        dq_ref[:, h*hd+mid:(h+1)*hd] = (two * cos - one * sin).astype(BF16)

    @pl.when((half == pl.num_programs(0) - 1) & (group == pl.num_programs(1) - 1))
    def _():
        for i in range(pieces):
            at = slice(i*PIECE, (i+1)*PIECE)
            rows = at if total != pieces else pl.ds(pl.multiple_of(pick_s[i] * PIECE, PIECE), PIECE)
            dkv_ref[rows, :hd] = (dk_s[at, :] * scale).astype(BF16)
            dkv_ref[rows, hd:] = dv_s[at, :].astype(BF16)

def attn_bwd(tags, own, q, do, o, lse, cos, sin, kv, hd, pieces):
    n_rows, width = q.shape
    groups = width // hd // HEAD_GROUP
    gw = HEAD_GROUP * hd
    halves = n_rows // PIECE
    rows = HEAD_GROUP * PIECE
    blk = pl.BlockSpec((PIECE, gw), lambda p, g, *_: (p, g))
    trig = pl.BlockSpec((PIECE, hd // 2), lambda p, g, *_: (p, 0))
    keys = pieces * PIECE
    return pl.pallas_call(
        attn_bwd_kernel,
        out_shape=(jax.ShapeDtypeStruct(q.shape, BF16), jax.ShapeDtypeStruct((keys, 2*hd), BF16)),
        grid_spec=pltpu.PrefetchScalarGridSpec(
            num_scalar_prefetch=2, grid=(halves, groups),
            in_specs=[blk, blk, blk, pl.BlockSpec((1, 1, rows), lambda p, g, *_: (p*groups+g, 0, 0)), trig, trig,
                      pl.BlockSpec(kv.shape, lambda p, g, *_: (0, 0))],
            out_specs=[blk, pl.BlockSpec((keys, 2*hd), lambda p, g, *_: (0, 0))],
            scratch_shapes=[pltpu.VMEM((keys, hd), BF16), pltpu.VMEM((hd, keys), BF16), pltpu.VMEM((keys, hd), BF16),
                            pltpu.VMEM((hd, rows), F32), pltpu.VMEM((keys, hd), F32), pltpu.VMEM((keys, hd), F32),
                            pltpu.SMEM((pieces,), jnp.int32)]),
        compiler_params=pltpu.CompilerParams(vmem_limit_bytes=48 << 20),
        name="attn_bwd",
    )(tags, own, q, do, o, lse, cos, sin, kv)

MESH = pl.DeviceIdType.MESH


def flip(index, mask):
    out = 0
    bit = 1
    while bit <= mask:
        part = (index // bit) % 2
        out = out + bit * ((1 - part) if mask & bit else part)
        bit *= 2
    return out + (index // bit) * bit


def row_loop(rows, body, step=32):
    if rows % step:
        step = 16

    @pl.loop(0, rows // step)
    def _(i):
        body(pl.ds(pl.multiple_of(i * step, step), step))


class Sender:
    def __init__(self):
        self.open = []

    def make(self, src, dst, send_sem, recv_sem, peer):
        return pltpu.make_async_remote_copy(
            src_ref=src,
            dst_ref=dst,
            send_sem=send_sem,
            recv_sem=recv_sem,
            device_id=peer,
            device_id_type=MESH,
        )

    def __call__(self, *args):
        copy = self.make(*args)
        copy.start()
        self.open.append(copy)
        return copy

    def finish(self):
        for copy in self.open:
            copy.wait_send()


class LineSum:
    def __init__(self, own, got, send_sem, recv_sem, c_idx, f_idx, n_z, sender):
        self.own, self.got, self.send_sem, self.recv_sem = own, got, send_sem, recv_sem
        self.n_z, self.sender = n_z, sender
        self.z = c_idx // 2
        self.left = (c_idx - 2, f_idx)
        self.right = (c_idx + 2, f_idx)

    def copy(self, b, slot, peer):
        return self.sender.make(
            self.own.at[b], self.got.at[slot], self.send_sem.at[b], self.recv_sem.at[slot], peer
        )

    def take(self, b, slot):
        self.copy(b, slot, self.left).wait_recv()

        def add(at):
            self.own[b, at, :] = (
                self.own[b, at, :].astype(F32) + self.got[slot, at, :].astype(F32)
            ).astype(BF16)

        row_loop(self.own.shape[1], add)

    def go_right(self, b):
        z = self.z

        @pl.when(z < b)
        def _():
            @pl.when(z > 0)
            def _():
                self.take(b, b)

            self.copy(b, b, self.right).start()

    def go_left(self, b):
        z, n_z = self.z, self.n_z

        @pl.when(z > b)
        def _():
            @pl.when(z < n_z - 1)
            def _():
                self.take(b, b)

            @pl.when(z - 1 > b)
            def _():
                self.copy(b, b, self.left).start()

            @pl.when(z - 1 == b)
            def _():
                self.copy(b, n_z, self.left).start()

    def step(self, i):
        @pl.when(2 * self.z < self.n_z)
        def _():
            self.go_right(self.n_z - 1 - i)
            self.go_left(i)

        @pl.when(2 * self.z >= self.n_z)
        def _():
            self.go_left(i)
            self.go_right(self.n_z - 1 - i)

    def total(self, store):
        z, n_z = self.z, self.n_z

        @pl.when(z > 0)
        def _():
            self.copy(z, z, self.left).wait_recv()

        @pl.when(z < n_z - 1)
        def _():
            self.copy(z, n_z, self.left).wait_recv()

        rows = self.own.shape[1]

        @pl.when(z == 0)
        def _():
            row_loop(
                rows,
                lambda at: store(
                    at, self.own[z, at, :].astype(F32) + self.got[n_z, at, :].astype(F32)
                ),
            )

        @pl.when(z == n_z - 1)
        def _():
            row_loop(
                rows,
                lambda at: store(
                    at, self.own[z, at, :].astype(F32) + self.got[z, at, :].astype(F32)
                ),
            )

        @pl.when((z > 0) & (z < n_z - 1))
        def _():
            row_loop(
                rows,
                lambda at: store(
                    at,
                    self.own[z, at, :].astype(F32)
                    + self.got[z, at, :].astype(F32)
                    + self.got[n_z, at, :].astype(F32),
                ),
            )

    def finish(self):
        for b in range(self.n_z):

            @pl.when(self.z != b)
            def _(b=b):
                self.copy(b, b, self.left).wait_send()


WINDOW = 3
TAIL_NAMES = ("gate", "kv", "up", "out", "qup", "low")
TAIL_CUT = ("gate", "up", "qup", "low")
TAIL_SENT = ("kv", "up", "out", "qup", "low")


def tail_kernel(n_ctx, n_f, names_in, names_out, names_scratch, *refs):
    n_z = n_ctx // 2
    names = list(names_in) + list(names_out) + list(names_scratch)
    r = dict(zip(names, refs, strict=True))
    c_idx = lax.axis_index("ctx")
    f_idx = lax.axis_index("fsdp")
    y_idx = c_idx % 2
    z_idx = c_idx // 2
    send = Sender()

    def over_c(mask):
        return (flip(c_idx, mask), f_idx)

    def over_f(mask):
        return (c_idx, flip(f_idx, mask))

    barrier = pltpu.get_barrier_semaphore()
    for mask in range(1, n_f):
        pl.semaphore_signal(barrier, inc=1, device_id=over_f(mask), device_id_type=MESH)
    for mask in range(1, n_ctx):
        pl.semaphore_signal(barrier, inc=1, device_id=over_c(mask), device_id_type=MESH)
    pl.semaphore_wait(barrier, n_f - 1 + n_ctx - 1)

    lines = {
        m: LineSum(
            r["pair_" + m],
            r["z_" + m],
            r["z_send"].at[i],
            r["z_recv"].at[i],
            c_idx,
            f_idx,
            n_z,
            send,
        )
        for i, m in enumerate(TAIL_NAMES)
    }
    y_copies, keeps = {}, {}
    early = r["up_got"].shape[0]

    parts = {m: r[m] for m in ("kv", "up", "out", "qup")}
    parts["low"] = r["part_low"]
    queue = [
        (m, b) for m in TAIL_SENT for b in range(n_z) if m != "up" or b >= early
    ]
    owed = tuple(queue)

    def next_y():
        if queue:
            m, b = queue.pop(0)
            i = TAIL_SENT.index(m)
            y_copies[m, b] = send(
                parts[m].at[b, 1 - y_idx],
                r["y_" + m].at[b],
                r["y_send"].at[i, b],
                r["y_recv"].at[i, b],
                over_c(1),
            )
            take_own(m, b)

    def take_own(m, b):
        keep = pltpu.make_async_copy(
            parts[m].at[b, y_idx],
            r["pair_" + m].at[b],
            r["keep_sem"].at[TAIL_SENT.index(m), b],
        )
        keep.start()
        keeps[m, b] = keep

    def add_pair(m, b):
        y_copies[m, b].wait_recv()
        next_y()
        add_ready(m, b)

    def add_ready(m, b):
        keeps[m, b].wait()
        pair, got = r["pair_" + m], r["y_" + m]

        def add(at):
            pair[b, at, :] = (pair[b, at, :].astype(F32) + got[b, at, :].astype(F32)).astype(BF16)

        row_loop(pair.shape[1], add)

    def advance(pair, line, work=()):
        if pair == "up":
            here.wait()
            for b in range(early):
                add_ready(pair, b)
        for b in range(n_z):
            if pair is not None and (pair, b) in owed:
                add_pair(pair, b)
            if line is not None and b < n_z - 1:
                lines[line].step(b)
            if b < len(work):
                work[b]()

    f_copies = {}

    def finish_sum(m):
        lines[m].total(lambda at, value: store_total(m, at, value))
        if m in TAIL_CUT:
            i = TAIL_CUT.index(m)
            part = r["tot_" + m].shape[0] // n_f
            for s in range(1, n_f):
                at = pl.ds(pl.multiple_of(flip(f_idx, s) * part, part), part)
                f_copies[m, s] = send(
                    r["tot_" + m].at[at, :],
                    r["f_" + m].at[s - 1],
                    r["f_send"].at[i, s - 1],
                    r["f_recv"].at[i, s - 1],
                    over_f(s),
                )

    def store_total(m, at, value):
        if m in TAIL_CUT:
            r["tot_" + m][at, :] = value.astype(BF16)
        else:
            r["out_" + m][at, :] = value

    def put_out(m):
        total = r["tot_" + m]
        rows, width = total.shape
        part = rows // n_f
        cuts = {"out_" + m: (0, width)}
        if m == "low":
            split = r["qd_group"].shape[1]
            cuts = {"out_qd": (0, split), "out_kvw": (split, width - split)}
        for s in range(n_f):
            source = flip(f_idx, s)
            if s:
                f_copies[m, s].wait_recv()
                got = r["f_" + m].at[s - 1]
            else:
                got = total.at[pl.ds(pl.multiple_of(f_idx * part, part), part)]
            for name, (start, wide) in cuts.items():
                at = pl.ds(pl.multiple_of(source * wide, 128), wide)
                r[name][:, at] = got[:, start : start + wide].astype(F32)

    def cut_low(src, dst, width, index):
        rows = src.shape[0]
        mine = pl.ds(pl.multiple_of(f_idx * rows, rows), rows)
        copies = []
        for s in range(1, n_f):
            at = pl.ds(pl.multiple_of(flip(f_idx, s) * width, 128), width)
            copies.append(
                send(
                    src.at[:, at],
                    dst.at[mine, :],
                    r["low_send"].at[index, s - 1],
                    r["low_recv"].at[index, s - 1],
                    over_f(s),
                )
            )
        own = pl.ds(pl.multiple_of(f_idx * width, 128), width)
        dst[mine, :] = src[:, own]
        return copies

    for _ in range(WINDOW):
        next_y()
    q_copies = cut_low(r["dqa"], r["qd_group"], r["qd_group"].shape[1], 0)
    pair_in = pltpu.make_async_copy(r["gate"], r["pair_gate"], r["keep_sem"].at[0, n_z])
    pair_in.start()
    here = pltpu.make_async_copy(
        r["up_got"], r["y_up"].at[pl.ds(0, early)], r["keep_sem"].at[1, n_z]
    )
    here.start()
    for b in range(early):
        take_own("up", b)
    pair_in.wait()
    def low_part(group, start):
        normed, part = r["normed_group"], r["part_low"]
        rows = part.shape[2]
        for c in range(n_ctx):
            part[c // 2, c % 2, :, start : start + group.shape[1]] = lax.dot_general(
                normed[:, c * rows : (c + 1) * rows],
                group[...],
                (((0,), (0,)), ((), ())),
                preferred_element_type=F32,
            ).astype(BF16)

    def low_queries():
        for copy in q_copies:
            copy.wait_recv()
        low_part(r["qd_group"], 0)

    advance("kv", "gate", (low_queries,))
    advance("up", "kv")
    finish_sum("gate")

    head = r["dkv"].shape[1] // 2
    mid = head // 2

    def store_kv(at, value):
        cos, sin = r["cos"][at, :], r["sin"][at, :]
        one, two = value[:, :mid], value[:, mid:head]
        r["dkv"][at, :mid] = (one * cos + two * sin).astype(BF16)
        r["dkv"][at, mid:head] = (two * cos - one * sin).astype(BF16)
        r["dkv"][at, head:] = value[:, head:].astype(BF16)

    lines["kv"].total(store_kv)
    kv_copies = cut_low(r["dkv"], r["kv_group"], r["kv_group"].shape[1], 1)

    def low_keys():
        for copy in kv_copies:
            copy.wait_recv()
        low_part(r["kv_group"], r["qd_group"].shape[1])

    grad_in, w_kv = r["grad_input"], r["w_kv"]
    width = grad_in.shape[1]
    tile = 256

    def input_products():
        @pl.loop(0, width // tile)
        def _(t):
            at = pl.ds(pl.multiple_of(t * tile, tile), tile)
            grad_in[:, at] = r["da_q"][:, at] + lax.dot_general(
                r["dkv"][...],
                w_kv[at, :],
                (((1,), (1,)), ((), ())),
                preferred_element_type=F32,
            )

    gain = r["gain_one"][...]

    def norm_rows(at):
        value = r["hidden"][at, :].astype(F32)
        grad = grad_in[at, :]
        scale = lax.rsqrt(jnp.mean(value * value, axis=-1, keepdims=True) + NORM_EPS)
        r["gain_sum"][...] += jnp.sum(grad * value * scale, axis=0, keepdims=True)
        ge = gain * grad
        inner = jnp.mean(ge * value, axis=-1, keepdims=True)
        grad_in[at, :] = (
            r["grad_resid"][at, :] + scale * ge - value * (scale * scale * scale) * inner
        )

    def input_norm():
        r["gain_sum"][...] = jnp.zeros_like(r["gain_sum"])
        row_loop(grad_in.shape[0], norm_rows, step=16)


    small, small_got = r["small_out"], r["small_got"]
    steps = [over_f(1), over_f(2), over_c(1)]
    mask = 2
    while mask < n_ctx:
        steps.append(over_c(mask))
        mask *= 2
    small_copies = {}

    def small_start(s):
        small_got[s, 0] = small[...]
        small_copies[s] = send(
            small_got.at[s, 0],
            small_got.at[s, 1],
            r["s_send"].at[s],
            r["s_recv"].at[s],
            steps[s],
        )

    def small_end(s):
        small_copies[s].wait_recv()
        small[...] = small[...] + small_got[s, 1]

    def small_first():
        small[...] = r["small"][...]
        for i in range(width // 128):
            small[i : i + 1, :] = r["gain_sum"][:, i * 128 : (i + 1) * 128]
        for s in range(2):
            small_start(s)
            small_end(s)
        small_start(2)

    advance("out", "up", (low_keys, input_products, input_norm, small_first))
    put_out("gate")
    advance("qup", "out")
    finish_sum("up")
    advance("low", "qup")
    finish_sum("out")
    small_end(2)
    small_start(3)
    put_out("up")
    finish_sum("qup")
    advance(None, "low")
    for s in range(3, len(steps)):
        if s > 3:
            small_start(s)
        small_end(s)
    finish_sum("low")
    put_out("qup")
    put_out("low")
    send.finish()
    for m in TAIL_NAMES:
        lines[m].finish()


def tail_reduce(n_ctx, n_f, inputs, q_width):
    n_z = n_ctx // 2
    vmem = pl.BlockSpec(memory_space=pltpu.VMEM)
    anywhere = pl.BlockSpec(memory_space=pl.ANY)
    rows, width = inputs["hidden"].shape
    kv_width = inputs["w_kv"].shape[1]
    in_hbm = ("gate", "kv", "up", "up_got", "out", "qup")
    names_in = tuple(inputs)
    in_specs = [anywhere if m in in_hbm else vmem for m in names_in]
    block = {m: inputs[m].shape[-2:] for m in in_hbm}
    cut_q, cut_kv, high = q_width // n_f, kv_width // n_f, width // n_ctx
    block["low"] = (high, cut_q + cut_kv)
    outs = {
        "small_out": jax.ShapeDtypeStruct(inputs["small"].shape, F32),
        "grad_input": jax.ShapeDtypeStruct((rows, width), F32),
        "out_qd": jax.ShapeDtypeStruct((high // n_f, q_width), F32),
        "out_kvw": jax.ShapeDtypeStruct((high // n_f, kv_width), F32),
    }
    scratch = {}
    for m in TAIL_NAMES:
        high, wide = block[m]
        scratch["pair_" + m] = pltpu.VMEM((n_z, high, wide), BF16)
        scratch["z_" + m] = pltpu.VMEM((n_z + 1, high, wide), BF16)
        if m in TAIL_SENT:
            scratch["y_" + m] = pltpu.VMEM((n_z, high, wide), BF16)
        if m in TAIL_CUT:
            scratch["tot_" + m] = pltpu.VMEM((high, wide), BF16)
            scratch["f_" + m] = pltpu.VMEM((n_f - 1, high // n_f, wide), BF16)
            if m != "low":
                outs["out_" + m] = jax.ShapeDtypeStruct((high // n_f, wide * n_f), F32)
        elif m != "kv":
            outs["out_" + m] = jax.ShapeDtypeStruct((high, wide), F32)
    scratch["dkv"] = pltpu.VMEM((rows, kv_width), BF16)
    scratch["qd_group"] = pltpu.VMEM((rows * n_f, q_width // n_f), BF16)
    scratch["kv_group"] = pltpu.VMEM((rows * n_f, kv_width // n_f), BF16)
    scratch["part_low"] = pltpu.VMEM((n_z, 2) + block["low"], BF16)
    scratch["gain_sum"] = pltpu.VMEM((1, width), F32)
    steps = 2 + (n_ctx.bit_length() - 1)
    scratch["small_got"] = pltpu.VMEM((steps, 2) + inputs["small"].shape, F32)
    dma = pltpu.SemaphoreType.DMA
    sent, cut = len(TAIL_SENT), len(TAIL_CUT)
    scratch["s_send"] = dma((steps,))
    scratch["s_recv"] = dma((steps,))
    scratch["y_send"] = dma((sent, n_z))
    scratch["y_recv"] = dma((sent, n_z))
    scratch["keep_sem"] = dma((sent, n_z + 1))
    scratch["z_send"] = dma((len(TAIL_NAMES), n_z))
    scratch["z_recv"] = dma((len(TAIL_NAMES), n_z + 1))
    scratch["f_send"] = dma((cut, n_f - 1))
    scratch["f_recv"] = dma((cut, n_f - 1))
    scratch["low_send"] = dma((2, n_f - 1))
    scratch["low_recv"] = dma((2, n_f - 1))
    values = pl.pallas_call(
        functools.partial(tail_kernel, n_ctx, n_f, names_in, tuple(outs), tuple(scratch)),
        out_shape=tuple(outs.values()),
        in_specs=in_specs,
        out_specs=tuple([vmem] * len(outs)),
        scratch_shapes=list(scratch.values()),
        compiler_params=pltpu.CompilerParams(
            collective_id=0, has_side_effects=True, vmem_limit_bytes=60 << 20
        ),
        name="tail_reduce",
    )(*inputs.values())
    return dict(zip(outs, values, strict=True))


def split_columns(width):
    return slice(0, width // 2), slice(width // 2, width)


def front_kernel(n_ctx, n_f, names, *refs):
    r = dict(zip(names, refs, strict=True))
    n_z = n_ctx // 2
    c_idx = lax.axis_index("ctx")
    f_idx = lax.axis_index("fsdp")
    y_idx = c_idx % 2
    z_bit = (c_idx // 2) % 2
    x_idx = f_idx // 2
    k_idx = f_idx % 2
    far_idx = flip(f_idx, 2)
    moves = Sender()
    local = []
    at_sem = [0]

    def over_c(mask):
        return (flip(c_idx, mask), f_idx)

    def over_f(mask):
        return (c_idx, flip(f_idx, mask))

    def send(src, dst, peer):
        i = at_sem[0]
        at_sem[0] += 1
        return moves(src, dst, r["send_sem"].at[i], r["recv_sem"].at[i], peer)

    def keep(src, dst):
        copy = pltpu.make_async_copy(src, dst, r["local_sem"].at[len(local)])
        copy.start()
        local.append(copy)
        return copy

    def rows(start, size):
        return pl.ds(pl.multiple_of(start, size), size)

    barrier = pltpu.get_barrier_semaphore()
    for mask in range(1, n_f):
        pl.semaphore_signal(barrier, inc=1, device_id=over_f(mask), device_id_type=MESH)
    for mask in range(1, n_ctx):
        pl.semaphore_signal(barrier, inc=1, device_id=over_c(mask), device_id_type=MESH)
    pl.semaphore_wait(barrier, n_f - 1 + n_ctx - 1)

    infos, tags = r["infos"], r["tags"]
    infos[f_idx] = r["info"][...]
    info_copies = [
        send(infos.at[f_idx], infos.at[f_idx], over_f(mask)) for mask in range(1, n_f)
    ]

    class Rows:
        def __init__(self, shard, dest, bit, hop, chunks):
            self.dest, self.bit, self.hop = dest, bit, hop
            self.shard = shard
            self.size = shard.shape[0]
            self.half = self.size // 2
            self.step = self.half // chunks
            self.chunks = chunks
            self.far, self.next, self.cross = [], [], []

        def start(self, spare=None):
            mine = self.dest.at[rows(f_idx * self.size, self.size)]
            if spare is None:
                self.kept = keep(self.shard, mine)
            else:
                self.spare, self.kept = spare, keep(self.shard, spare)
            self.cross.append(send(self.shard, mine, over_f(1)))

        def settle(self):
            self.kept.wait()
            keep(self.spare, self.dest.at[rows(f_idx * self.size, self.size)])

        def reach(self, i):
            part = self.bit * self.half + i * self.step
            self.far.append(
                send(
                    self.shard.at[rows(part, self.step)],
                    self.dest.at[rows(f_idx * self.size + part, self.step)],
                    over_f(2),
                )
            )

        def place(self, bit, i):
            return self.dest.at[rows(far_idx * self.size + bit * self.half + i * self.step, self.step)]

        def hop_on(self, i):
            self.far[i].wait_recv()
            reach_next()
            here = self.place(self.bit, i)
            self.next.append(send(here, here, over_c(self.hop)))
            self.cross.append(send(here, here, over_f(1)))

        def pass_on(self, i):
            self.next[i].wait_recv()
            here = self.place(1 - self.bit, i)
            self.cross.append(send(here, here, over_f(1)))

        def end(self):
            for copy in self.cross:
                copy.wait_recv()

    class Columns:
        def __init__(self, shard, dest, box, bits, hops):
            self.shard, self.dest, self.box = shard, dest, box
            self.bits, self.hops = bits, hops
            self.size = shard.shape[0]
            self.width = dest.shape[1]
            self.quarter = self.size // 4

        def columns(self, start, count=1):
            return pl.ds(pl.multiple_of(start * self.width, 128), count * self.width)

        def start(self, spare):
            mine = self.dest.at[rows(f_idx * self.size, self.size)]
            self.spare, self.kept = spare, keep(self.shard.at[:, self.columns(f_idx)], spare)
            self.cross = [send(self.shard.at[:, self.columns(flip(f_idx, 1))], mine, over_f(1))]

        def settle(self):
            self.kept.wait()
            keep(self.spare, self.dest.at[rows(f_idx * self.size, self.size)])

        def reach(self, i):
            one, two = self.bits
            at = rows((two * 2 + one) * self.quarter, self.quarter)
            self.far = send(
                self.shard.at[at, self.columns((1 - x_idx) * 2, 2)], self.box.at[at], over_f(2)
            )

        def piece(self, one, two):
            return self.box.at[rows((two * 2 + one) * self.quarter, self.quarter)]

        def first(self):
            one, two = self.bits
            self.far.wait_recv()
            reach_next()
            here = self.piece(one, two)
            self.step = send(here, here, over_c(self.hops[0]))
            self.last = [send(here, here, over_c(self.hops[1]))]

        def second(self):
            one, two = self.bits
            self.step.wait_recv()
            here = self.piece(1 - one, two)
            self.last.append(send(here, here, over_c(self.hops[1])))

        def part(self):
            for copy in self.last:
                copy.wait_recv()
            there = self.dest.at[rows(far_idx * self.size, self.size)]
            self.cross.append(send(self.box.at[:, self.columns(1 - k_idx)], there, over_f(1)))
            keep(self.box.at[:, self.columns(k_idx)], there)

        def end(self):
            for copy in self.cross:
                copy.wait_recv()

    kv = Rows(r["kv_weight"], r["kv_full"], y_idx, 1, 1)
    qd = Rows(r["q_down"], r["qd_full"], y_idx, 1, 1)
    qu = Rows(r["q_up"], r["qu_full"], z_bit, 2, 2)
    left, right = split_columns(r["out_proj"].shape[1])
    outs = [
        Rows(r["out_proj"].at[:, left], r["w_out"].at[:, left], y_idx, 1, 2),
        Rows(r["out_proj"].at[:, right], r["w_out"].at[:, right], z_bit, 2, 2),
    ]
    gate = Columns(r["w_gate"], r["gate_full"], r["gate_box"], (y_idx, z_bit), (1, 2))
    up = Columns(r["w_up"], r["up_full"], r["up_box"], (z_bit, y_idx), (2, 1))
    queue = [(kv, 0), (qd, 0), (qu, 0), (qu, 1), (gate, 0), (up, 0)]
    queue += [(out, i) for i in range(2) for out in outs]

    def reach_next():
        if queue:
            part, i = queue.pop(0)
            part.reach(i)

    reach_next()
    reach_next()
    reach_next()
    kv.start()
    qd.start()

    for copy in info_copies:
        copy.wait_recv()
    d1 = r["gain_one"].shape[1] // n_f // 128
    d2 = r["gain_q"].shape[1] // n_f // 128
    count = infos[0, 2 * d1 + d2 : 2 * d1 + d2 + 1, :]
    for f in range(n_f):
        for i in range(d1):
            col = slice((f * d1 + i) * 128, (f * d1 + i + 1) * 128)
            r["gain_one"][:, col] = infos[f, i : i + 1, :]
            r["gain_two"][:, col] = infos[f, d1 + d2 + i : d1 + d2 + i + 1, :]
        for i in range(d2):
            col = slice((f * d2 + i) * 128, (f * d2 + i + 1) * 128)
            r["gain_q"][:, col] = infos[f, d1 + i : d1 + i + 1, :]
        if f:
            count = count + infos[f, 2 * d1 + d2 : 2 * d1 + d2 + 1, :]
    tags[c_idx] = r["tag"][...]
    tags[c_idx, 1:2, :] = count
    tag_copies = [send(tags.at[c_idx], tags.at[c_idx], over_c(mask)) for mask in range(1, n_ctx)]

    normed = r["normed"]
    gain_one = r["gain_one"][...]

    def norm_rows(at):
        value = r["hidden"][at, :].astype(F32)
        scale = lax.rsqrt(jnp.mean(value * value, axis=-1, keepdims=True) + NORM_EPS)
        normed[at, :] = (value * scale * gain_one).astype(BF16)

    row_loop(normed.shape[0], norm_rows, step=16)

    kv.hop_on(0)
    qd.hop_on(0)
    qu.start()
    kv.pass_on(0)
    qd.pass_on(0)
    kv.end()
    kv.kept.wait()
    head = r["kv_full"].shape[1] // 2
    mid = head // 2
    cos, sin = r["cos"], r["sin"]
    kv_rows = r["kv_rows"]
    keys = jnp.dot(normed[...], r["kv_full"][:, :head], preferred_element_type=F32)
    one, two = keys[:, :mid], keys[:, mid:]
    kv_rows[:, :mid] = (one * cos[...] - two * sin[...]).astype(BF16)
    kv_rows[:, mid:head] = (two * cos[...] + one * sin[...]).astype(BF16)
    kv_rows[:, head:] = jnp.dot(
        normed[...], r["kv_full"][:, head:], preferred_element_type=F32
    ).astype(BF16)
    all_kv = r["all_kv"]
    tokens = normed.shape[0]

    def kv_place(c):
        return all_kv.at[rows(c * tokens, tokens)]

    kv_z = [send(kv_rows, kv_place(c_idx), over_c(2 * s)) for s in range(1, n_z)]
    kv_y = [send(kv_rows, kv_place(c_idx), over_c(1))]
    keep(kv_rows, kv_place(c_idx))
    qu.hop_on(0)
    qd.end()
    qd.kept.wait()

    @pl.loop(0, r["q_low"].shape[1] // 256)
    def _(t):
        at = pl.ds(pl.multiple_of(t * 256, 256), 256)
        r["q_low"][:, at] = jnp.dot(
            normed[...], r["qd_full"][:, at], preferred_element_type=F32
        )

    gain_q = r["gain_q"][...]

    def norm_low(at):
        value = r["q_low"][at, :]
        scale = lax.rsqrt(jnp.mean(value * value, axis=-1, keepdims=True) + NORM_EPS)
        r["q_normed"][at, :] = (value * scale * gain_q).astype(BF16)

    row_loop(tokens, norm_low, step=16)
    qu.hop_on(1)
    gate.first()
    for s in range(1, n_z):
        kv_z[s - 1].wait_recv()
        here = kv_place(flip(c_idx, 2 * s))
        kv_y.append(send(here, here, over_c(1)))
    qu.pass_on(0)
    qu.pass_on(1)
    up.first()
    qu.end()
    gate.start(r["gate_spare"])
    up.start(r["up_spare"])
    outs[0].start(r["out_spare"].at[:, left])
    outs[1].start(r["out_spare"].at[:, right])
    qu.kept.wait()

    @pl.loop(0, r["q_rot"].shape[1] // head)
    def _(h):
        start = pl.multiple_of(h * head, head)
        value = jnp.dot(
            r["q_normed"][...],
            r["qu_full"][:, pl.ds(start, head)],
            preferred_element_type=F32,
        )
        one, two = value[:, :mid], value[:, mid:]
        r["q_rot"][:, pl.ds(start, mid)] = (one * cos[...] - two * sin[...]).astype(BF16)
        late = pl.multiple_of(h * head + mid, mid)
        r["q_rot"][:, pl.ds(late, mid)] = (two * cos[...] + one * sin[...]).astype(BF16)

    for part in [gate, up] + outs:
        part.settle()
    for m in ("kv", "qd", "qu"):
        keep(r[m + "_full"], r["w_" + m])
    gate.second()
    for out in outs:
        out.hop_on(0)
    up.second()
    for out in outs:
        out.hop_on(1)
    gate.part()
    for i in range(2):
        for out in outs:
            out.pass_on(i)
    up.part()
    for copy in kv_y + tag_copies:
        copy.wait_recv()
    for part in [gate, up] + outs:
        part.end()
    for copy in local:
        if not any(copy is part.kept for part in [kv, qd, qu, gate, up] + outs):
            copy.wait()
    moves.finish()


def front(n_ctx, n_f, inputs, head_size):
    tokens, width = inputs["hidden"].shape
    shape = jax.ShapeDtypeStruct
    q_width = inputs["q_down"].shape[1]
    heads_width = inputs["q_up"].shape[1]
    part = inputs["w_gate"].shape[1] // n_f

    def whole(m):
        return (inputs[m].shape[0] * n_f, inputs[m].shape[1])

    in_hbm = ("q_down", "kv_weight", "q_up", "out_proj", "w_gate", "w_up")
    outs = {
        "w_qd": shape(whole("q_down"), BF16),
        "w_kv": shape(whole("kv_weight"), BF16),
        "w_qu": shape(whole("q_up"), BF16),
        "w_out": shape(whole("out_proj"), BF16),
        "gate_full": shape((width, part), BF16),
        "up_full": shape((width, part), BF16),
        "all_kv": shape((tokens * n_ctx, 2 * head_size), BF16),
        "normed": shape((tokens, width), BF16),
        "q_low": shape((tokens, q_width), F32),
        "q_normed": shape((tokens, q_width), BF16),
        "q_rot": shape((tokens, heads_width), BF16),
        "gain_one": shape((1, width), F32),
        "gain_q": shape((1, q_width), F32),
        "gain_two": shape((1, width), F32),
        "tags": shape((n_ctx, 8, 128), F32),
    }
    out_hbm = ("w_qd", "w_kv", "w_qu", "w_out", "gate_full", "up_full", "all_kv")
    box = (inputs["w_gate"].shape[0], 2 * part)
    dma = pltpu.SemaphoreType.DMA
    scratch = {
        "infos": pltpu.VMEM((n_f,) + inputs["info"].shape, F32),
        "qd_full": pltpu.VMEM(whole("q_down"), BF16),
        "kv_full": pltpu.VMEM(whole("kv_weight"), BF16),
        "qu_full": pltpu.VMEM(whole("q_up"), BF16),
        "gate_box": pltpu.VMEM(box, BF16),
        "up_box": pltpu.VMEM(box, BF16),
        "gate_spare": pltpu.VMEM((box[0], part), BF16),
        "up_spare": pltpu.VMEM((box[0], part), BF16),
        "out_spare": pltpu.VMEM(inputs["out_proj"].shape, BF16),
        "kv_rows": pltpu.VMEM((tokens, 2 * head_size), BF16),
        "send_sem": dma((64 + 2 * n_ctx,)),
        "recv_sem": dma((64 + 2 * n_ctx,)),
        "local_sem": dma((24,)),
    }
    vmem = pl.BlockSpec(memory_space=pltpu.VMEM)
    anywhere = pl.BlockSpec(memory_space=pl.ANY)
    names = tuple(inputs) + tuple(outs) + tuple(scratch)
    values = pl.pallas_call(
        functools.partial(front_kernel, n_ctx, n_f, names),
        out_shape=tuple(outs.values()),
        in_specs=[anywhere if m in in_hbm else vmem for m in inputs],
        out_specs=tuple([anywhere if m in out_hbm else vmem for m in outs]),
        scratch_shapes=list(scratch.values()),
        compiler_params=pltpu.CompilerParams(
            collective_id=1, has_side_effects=True, vmem_limit_bytes=48 << 20
        ),
        name="front",
    )(*inputs.values())
    return dict(zip(outs, values, strict=True))


def tiles(total, wide, body):
    whole = total // wide

    @pl.loop(0, whole)
    def _(t):
        body(pl.multiple_of(t * wide, wide), wide)

    if total % wide:
        body(whole * wide, total % wide)


def contract_first(a, b):
    return jnp.dot(a.T, b, preferred_element_type=F32)


def rows_product_kernel(a_ref, b_ref, o_ref):
    o_ref[...] = contract_last(a_ref[...], b_ref[...]).astype(BF16)


def rows_product(a, b, tile):
    return pl.pallas_call(
        rows_product_kernel,
        out_shape=jax.ShapeDtypeStruct((a.shape[0], b.shape[0]), BF16),
        grid=(b.shape[0] // tile,),
        in_specs=[
            pl.BlockSpec(a.shape, lambda i: (0, 0)),
            pl.BlockSpec((tile, b.shape[1]), lambda i: (i, 0)),
        ],
        out_specs=pl.BlockSpec((a.shape[0], tile), lambda i: (0, i)),
        compiler_params=pltpu.CompilerParams(vmem_limit_bytes=58 << 20),
        name="rows_product",
    )(a, b)


def ffn_kernel(n_f, names, *refs):
    r = dict(zip(names, refs, strict=True))
    c_idx = lax.axis_index("ctx")
    f_idx = lax.axis_index("fsdp")
    moves = Sender()
    at_sem = [0]
    core, far = (c_idx, flip(f_idx, 1)), (c_idx, flip(f_idx, 2))
    beside = (flip(c_idx, 1), f_idx)
    y_idx = c_idx % 2

    def send(src, dst, peer):
        i = at_sem[0]
        at_sem[0] += 1
        return moves(src, dst, r["send_sem"].at[i], r["recv_sem"].at[i], peer)

    barrier = pltpu.get_barrier_semaphore()
    for peer in (core, far, (c_idx, flip(f_idx, 3)), beside):
        pl.semaphore_signal(barrier, inc=1, device_id=peer, device_id_type=MESH)
    pl.semaphore_wait(barrier, 4)

    tokens, width = r["normed"].shape
    mine = r["attn_group"].at[pl.ds(pl.multiple_of(f_idx * tokens, tokens), tokens)]
    own_attn = pltpu.make_async_copy(r["attn_cut"].at[f_idx], mine, r["load_sem"].at[3])
    own_attn.start()

    def send_attn(mask):
        return send(r["attn_cut"].at[flip(f_idx, mask)], mine, (c_idx, flip(f_idx, mask)))

    units = r["w_down"].shape[0]
    group, dz = r["group"], r["dz"]
    block = [slice(i * tokens, (i + 1) * tokens) for i in range(4)]
    pair = [slice(0, 2 * tokens), slice(2 * tokens, 4 * tokens)]

    def gather(buf):
        to_core = send(buf.at[block[0]], buf.at[block[1]], core)
        to_far = send(buf.at[block[0]], buf.at[block[2]], far)
        return to_core, to_far

    def gather_far(buf, to_far):
        to_far.wait_recv()
        send(buf.at[block[2]], buf.at[block[3]], core).wait_recv()

    group[block[0], :] = r["normed"][...]
    to_core, to_far = gather(group)
    loads = []
    for i, m in enumerate(("gate", "up", "down")):
        load = pltpu.make_async_copy(r["w_" + m], r["v_" + m], r["load_sem"].at[i])
        load.start()
        loads.append(load)
    loads[0].wait()
    loads[1].wait()

    def hidden_part(rows):
        def one(start, wide):
            at = pl.ds(start, wide)
            both = jnp.concatenate([r["v_gate"][:, at], r["v_up"][:, at]], axis=1)
            out = jnp.dot(group[rows, :], both, preferred_element_type=F32)
            gate, up = out[:, :wide], out[:, wide:]
            r["gate"][rows, at] = gate.astype(BF16)
            r["up"][rows, at] = up.astype(BF16)
            r["hid"][rows, at] = (gate / (1.0 + jnp.exp(-gate)) * up).astype(BF16)

        tiles(units, 128, one)

    to_core.wait_recv()
    hidden_part(pair[0])
    gather_far(group, to_far)
    attn_copies = [send_attn(1), send_attn(2)]
    hidden_part(pair[1])
    loads[2].wait()

    def down_block(i, dest):
        def one(start, wide):
            at = pl.ds(start, wide)
            dest[:, at] = jnp.dot(
                r["hid"][block[i], :], r["v_down"][:, at], preferred_element_type=F32
            ).astype(dest.dtype)

        tiles(width, 256, one)

    def back_block(i, dest):
        def one(start, wide):
            at = pl.ds(start, wide)
            dest[:, at] = (
                contract_last(r["gate"][block[i], :], r["v_gate"][at, :])
                + contract_last(r["up"][block[i], :], r["v_up"][at, :])
            ).astype(dest.dtype)

        tiles(width, 256, one)

    def add_rows(dest, one, two):
        def add(at):
            dest[at, :] = (one[at, :].astype(F32) + two[at, :].astype(F32)).astype(dest.dtype)

        row_loop(tokens, add)

    def far_sum(k, make):
        make(3, r["give"].at[2 * k])
        step = send(r["give"].at[2 * k], r["got"].at[2 * k], core)
        make(2, r["far_sum"])
        step.wait_recv()
        add_rows(r["far_give"].at[k], r["far_sum"], r["got"].at[2 * k])
        return send(r["far_give"].at[k], r["far_got"].at[k], far)

    def near_sum(k, make):
        make(1, r["give"].at[2 * k + 1])
        step = send(r["give"].at[2 * k + 1], r["got"].at[2 * k + 1], core)
        make(0, r["near_sum"])
        return step

    def near_end(k, step):
        step.wait_recv()
        add_rows(r["near_sum"], r["near_sum"], r["got"].at[2 * k + 1])

    far_step = far_sum(0, down_block)
    near_end(0, near_sum(0, down_block))
    far_step.wait_recv()
    r["sq"][...] = jnp.zeros_like(r["sq"])

    def loss_rows(at):
        value = r["resid"][at, :] + r["near_sum"][at, :] + r["far_got"][0, at, :].astype(F32)
        r["result"][at, :] = value.astype(BF16)
        diff = value - r["teacher"][at, :].astype(F32)
        squares = jnp.sum(diff * diff, axis=1, keepdims=True) * r["valid"][at, :]
        r["sq"][:1, :] += jnp.sum(squares, axis=0, keepdims=True)
        grad = diff * r["valid_scale"][at, :1]
        r["grad_resid"][at, :] = grad
        dz[at, :] = grad.astype(BF16)

    row_loop(tokens, loss_rows, step=16)
    to_core, to_far = gather(dz)

    def back_hidden(rows):
        def one(start, wide):
            at = pl.ds(start, wide)
            grad = contract_last(dz[rows, :], r["v_down"][at, :])
            gate = r["gate"][rows, at].astype(F32)
            up = r["up"][rows, at].astype(F32)
            sigma = 1.0 / (1.0 + jnp.exp(-gate))
            r["gate"][rows, at] = (grad * up * sigma * (1.0 + gate * (1.0 - sigma))).astype(BF16)
            r["up"][rows, at] = (grad * (gate * sigma)).astype(BF16)

        tiles(units, 256, one)

    to_core.wait_recv()
    back_hidden(pair[0])
    near_step = near_sum(1, back_block)
    gather_far(dz, to_far)
    saves = []

    def save(src, dst, i):
        copy = pltpu.make_async_copy(src, dst, r["save_sem"].at[i])
        copy.start()
        return copy

    def down_tile(start, wide):
        at = pl.ds(start, wide)
        spot = r["tile"].at[pl.ds(0, wide)]
        spot[...] = contract_first(r["hid"][:, at], dz[...]).astype(BF16)
        save(spot, r["down_part"].at[at], 0).wait()

    count = units // 128
    first = (count + 1) // 2

    @pl.loop(0, first)
    def _(t):
        down_tile(pl.multiple_of(((count - first) * (1 - y_idx) + t) * 128, 128), 128)

    half = units // 2
    give = pl.ds(pl.multiple_of((1 - y_idx) * half, half), half)
    down_step = send(r["down_part"].at[give], r["down_got"], beside)
    attn_copies.append(send_attn(3))
    back_hidden(pair[1])
    far_step = far_sum(1, back_block)
    near_end(1, near_step)

    @pl.loop(0, count - first)
    def _(t):
        down_tile(pl.multiple_of((first * y_idx + t) * 128, 128), 128)

    def gate_tile(start, wide):
        at = pl.ds(start, wide)
        left = group[:, at].T
        for i, m in enumerate(("gate", "up")):
            spot = r["wide_tile"].at[i]
            spot[...] = jnp.dot(left, r[m][...], preferred_element_type=F32).astype(BF16)
            saves.append(save(spot, r[m + "_part"].at[at], 1 + i))
        saves.pop().wait()
        saves.pop().wait()

    tiles(width, 256, gate_tile)
    far_step.wait_recv()
    gain = r["gain_two"][...]
    r["gain_sum"][...] = jnp.zeros_like(r["gain_sum"])

    def norm_rows(at):
        grad = r["near_sum"][at, :] + r["far_got"][1, at, :].astype(F32)
        value = r["resid"][at, :]
        scale = lax.rsqrt(jnp.mean(value * value, axis=-1, keepdims=True) + NORM_EPS)
        r["gain_sum"][...] += jnp.sum(grad * value * scale, axis=0, keepdims=True)
        ge = gain * grad
        inner = jnp.mean(ge * value, axis=-1, keepdims=True)
        total = r["grad_resid"][at, :] + scale * ge - value * (scale * scale * scale) * inner
        r["grad_resid"][at, :] = total
        r["grad_branch"][at, :] = total.astype(BF16)

    row_loop(tokens, norm_rows, step=16)
    for copy in attn_copies + [down_step]:
        copy.wait_recv()
    own_attn.wait()
    moves.finish()


def feed_forward(n_f, inputs):
    tokens, width = inputs["normed"].shape
    units = inputs["w_down"].shape[0]
    shape = jax.ShapeDtypeStruct
    outs = {
        "result": shape((tokens, width), BF16),
        "grad_resid": shape((tokens, width), F32),
        "grad_branch": shape((tokens, width), BF16),
        "down_part": shape((units, width), BF16),
        "down_got": shape((units // 2, width), BF16),
        "gate_part": shape((width, units), BF16),
        "up_part": shape((width, units), BF16),
        "attn_group": shape((tokens * n_f, inputs["attn_cut"].shape[2]), BF16),
        "gain_sum": shape((1, width), F32),
        "sq": shape((8, 128), F32),
    }
    hbm = ("w_gate", "w_up", "w_down", "attn_cut", "attn_group")
    hbm += ("down_part", "down_got", "gate_part", "up_part")
    dma = pltpu.SemaphoreType.DMA
    many = tokens * n_f
    scratch = {
        "v_gate": pltpu.VMEM((width, units), BF16),
        "v_up": pltpu.VMEM((width, units), BF16),
        "v_down": pltpu.VMEM((units, width), BF16),
        "group": pltpu.VMEM((many, width), BF16),
        "dz": pltpu.VMEM((many, width), BF16),
        "gate": pltpu.VMEM((many, units), BF16),
        "up": pltpu.VMEM((many, units), BF16),
        "hid": pltpu.VMEM((many, units), BF16),
        "give": pltpu.VMEM((4, tokens, width), BF16),
        "got": pltpu.VMEM((4, tokens, width), BF16),
        "far_sum": pltpu.VMEM((tokens, width), F32),
        "near_sum": pltpu.VMEM((tokens, width), F32),
        "far_give": pltpu.VMEM((2, tokens, width), BF16),
        "far_got": pltpu.VMEM((2, tokens, width), BF16),
        "tile": pltpu.VMEM((128, width), BF16),
        "wide_tile": pltpu.VMEM((2, 256, units), BF16),
        "send_sem": dma((16,)),
        "recv_sem": dma((16,)),
        "load_sem": dma((4,)),
        "save_sem": dma((3,)),
    }
    vmem = pl.BlockSpec(memory_space=pltpu.VMEM)
    anywhere = pl.BlockSpec(memory_space=pl.ANY)
    names = tuple(inputs) + tuple(outs) + tuple(scratch)
    values = pl.pallas_call(
        functools.partial(ffn_kernel, n_f, names),
        out_shape=tuple(outs.values()),
        in_specs=[anywhere if m in hbm else vmem for m in inputs],
        out_specs=tuple([anywhere if m in hbm else vmem for m in outs]),
        scratch_shapes=list(scratch.values()),
        compiler_params=pltpu.CompilerParams(
            collective_id=2, has_side_effects=True, vmem_limit_bytes=60 << 20
        ),
        name="feed_forward",
    )(*inputs.values())
    return dict(zip(outs, values, strict=True))


def body(
    hidden_in,
    teacher,
    blocks,
    seq_ids,
    valid_mask,
    norm1_gain,
    q_down,
    q_gain,
    q_up,
    kv_weight,
    out_proj,
    norm2_gain,
    w_gate,
    w_up,
    w_down,
):
    row_count, model_width = hidden_in.shape
    head_size = kv_weight.shape[1] // 2
    heads_width = q_up.shape[1]
    head_count = heads_width // head_size
    half_dim = head_size // 2
    q_width = q_down.shape[1]
    n_ctx = lax.axis_size("ctx")
    n_f = lax.axis_size("fsdp")
    n_z = n_ctx // 2
    token_total = row_count * n_ctx * n_f
    seq_pieces = 2 * SEQ_BLOCKS
    c_idx = lax.axis_index("ctx")
    f_idx = lax.axis_index("fsdp")
    y_idx = c_idx % 2
    z_idx = c_idx // 2
    x_idx = f_idx // 2
    k_idx = f_idx % 2

    def by_f(values, mask):
        return lax.ppermute(values, "fsdp", [(i, i ^ mask) for i in range(n_f)])

    def by_c(values, mask):
        return lax.ppermute(values, "ctx", [(i, i ^ mask) for i in range(n_ctx)])

    def cut(values, start, size, axis):
        return lax.dynamic_slice_in_dim(values, start, size, axis)

    def ctx_split(grad):
        view = grad.reshape(n_z, 2, grad.shape[0] // n_ctx, grad.shape[1])
        give = lax.dynamic_index_in_dim(view, 1 - y_idx, 1, keepdims=False)
        keep = lax.dynamic_index_in_dim(view, y_idx, 1, keepdims=False)
        return give, keep

    def ctx_pair(keep, got):
        return (keep.astype(F32) + got.astype(F32)).astype(BF16)

    def ctx_spread(pair):
        return [pair] + [
            by_c(lax.dynamic_index_in_dim(pair, z_idx ^ r, 0, keepdims=False), 2 * r)
            for r in range(1, n_z)
        ]

    def ctx_total(parts):
        total = lax.dynamic_index_in_dim(parts[0], z_idx, 0, keepdims=False).astype(F32)
        for got in parts[1:]:
            total = total + got.astype(F32)
        return total

    def group_rows(values):
        return lax.all_gather(values, "fsdp", axis=0, tiled=True)

    valid_f = valid_mask.astype(F32)
    own_pieces = row_count // PIECE
    info = jnp.concatenate(
        [
            norm1_gain.astype(F32),
            q_gain.astype(F32),
            norm2_gain.astype(F32),
            jnp.full((128,), jnp.sum(valid_f)),
        ]
    )
    info = jnp.pad(info, (0, -info.shape[0] % 1024)).reshape(-1, 128)
    own_tags = jnp.stack([blocks.reshape(-1, PIECE)[:, 0], seq_ids.reshape(-1, PIECE)[:, 0]], 1)
    tag = jnp.pad(own_tags.astype(F32).reshape(1, -1), ((0, 7), (0, 128 - 2 * own_pieces)))
    own = jnp.concatenate([blocks.reshape(-1, PIECE)[:, 0], seq_ids[:1]])

    positions = blocks * PIECE + jnp.arange(row_count, dtype=jnp.int32) % PIECE
    freq_table = 10000.0 ** (-(jnp.arange(half_dim, dtype=F32) * 2.0 / head_size))
    angle_table = positions.astype(F32)[:, None] * freq_table[None, :]
    cosine = jnp.cos(angle_table)
    sine = jnp.sin(angle_table)
    fetched = front(
        n_ctx,
        n_f,
        {
            "q_down": q_down,
            "kv_weight": kv_weight,
            "q_up": q_up,
            "out_proj": out_proj,
            "w_gate": w_gate,
            "w_up": w_up,
            "hidden": hidden_in,
            "info": info,
            "tag": tag,
            "cos": cosine,
            "sin": sine,
        },
        head_size,
    )
    w_out = fetched["w_out"]
    all_kv, q_rot = fetched["all_kv"], fetched["q_rot"]
    normed, q_low, q_normed = fetched["normed"], fetched["q_low"], fetched["q_normed"]
    gain_one, gain_q, gain_two = fetched["gain_one"], fetched["gain_q"], fetched["gain_two"]
    tags = fetched["tags"][:, 0, : 2 * own_pieces].reshape(-1, 2).astype(jnp.int32)
    total_count = jnp.sum(fetched["tags"][:, 1, 0])
    hidden_f = hidden_in.astype(F32)
    scale_q = rms_scale(q_low)

    out_block = heads_width // (n_ctx * n_f)
    if out_block == 128:
        attn_heads, lse, attn_cut = attn_fwd(
            tags, own, q_rot, all_kv, head_size, seq_pieces, n_f, True
        )
    else:
        attn_heads, lse = attn_fwd(tags, own, q_rot, all_kv, head_size, seq_pieces, n_f, False)
        attn_cut = attn_heads.reshape(row_count, n_ctx, n_f, out_block).transpose(2, 0, 1, 3)
        attn_cut = attn_cut.reshape(n_f, row_count, n_ctx * out_block)
    resid = hidden_f + dot(attn_heads, w_out)
    scale_two = rms_scale(resid)
    normed_two = (resid * scale_two * gain_two).astype(BF16)

    wide_valid = jnp.broadcast_to(valid_f[:, None], (row_count, 128))
    ffn = feed_forward(
        n_f,
        {
            "normed": normed_two,
            "resid": resid,
            "teacher": teacher,
            "valid": wide_valid,
            "valid_scale": wide_valid * (token_total / total_count),
            "gain_two": gain_two,
            "w_gate": fetched["gate_full"],
            "w_up": fetched["up_full"],
            "w_down": w_down,
            "attn_cut": attn_cut,
        },
    )
    grad_resid, grad_branch = ffn["grad_resid"], ffn["grad_branch"]
    grad_gain_two = ffn["gain_sum"].reshape(-1)
    sq_local = ffn["sq"][0, 0]
    half_units = w_down.shape[0] // 2
    down_pair = ctx_pair(cut(ffn["down_part"], y_idx * half_units, half_units, 0), ffn["down_got"])
    down_parts = ctx_spread(down_pair.reshape(n_z, -1, model_width))
    gate_give, gate_keep = ctx_split(ffn["gate_part"])
    gate_got = by_c(gate_give, 1)
    early = n_z // 2
    up_blocks = ffn["up_part"].reshape(n_z, 2, model_width // n_ctx, -1)
    up_got = by_c(
        lax.dynamic_index_in_dim(up_blocks[:early], 1 - y_idx, 1, keepdims=False), 1
    )
    branch_group = group_rows(grad_branch)
    grad_attn = rows_product(grad_branch, w_out, 512)
    grad_qlin, grad_seq = attn_bwd(
        tags, own, q_rot, grad_attn, attn_heads, lse, cosine, sine, all_kv, head_size, seq_pieces
    )
    qlin_group = lax.all_to_all(grad_qlin, "fsdp", 1, 0, tiled=True)
    down_parts, gate_got, grad_seq = together(down_parts, gate_got, grad_seq)

    by_piece = grad_seq.reshape(seq_pieces, PIECE, 2 * head_size)
    piece_tag = tags[:, 0].reshape(n_z, 2, own_pieces)
    piece_own = (tags[:, 1] == seq_ids[0]).reshape(n_z, 2, own_pieces)

    def kv_half(bit):
        places = lax.dynamic_index_in_dim(piece_tag, bit, 1, keepdims=False).reshape(-1)
        picked = by_piece[places]
        if n_ctx * own_pieces != seq_pieces:
            mine = lax.dynamic_index_in_dim(piece_own, bit, 1, keepdims=False).reshape(-1)
            picked = jnp.where(mine[:, None, None], picked, jnp.zeros_like(picked))
        return picked.reshape(n_z, own_pieces * PIECE, 2 * head_size)

    if n_ctx * own_pieces == seq_pieces:
        kv_part = grad_seq.reshape(n_z, 2, row_count, 2 * head_size)
    else:
        kv_part = jnp.stack([kv_half(0), kv_half(1)], axis=1)
    q_cut, kv_cut = q_width // n_f, 2 * head_size // n_f
    qnorm_group = group_rows(q_normed)
    normed_group = group_rows(normed)

    grad_qnormed = dot_t(grad_qlin, fetched["w_qu"])
    grad_qlow_f, grad_gain_q = rms_back(q_low, scale_q, gain_q, grad_qnormed)
    grad_qlow = grad_qlow_f.astype(BF16)
    attn_group = ffn["attn_group"]
    da_q = dot_t(grad_qlow, fetched["w_qd"])
    gate_pair = ctx_pair(gate_keep, gate_got)
    out_part = dot_rows(attn_group, branch_group).astype(BF16)
    qup_part = dot_rows(qnorm_group, qlin_group).astype(BF16)

    def by_ctx(grad):
        return grad.reshape(n_z, 2, grad.shape[0] // n_ctx, grad.shape[1])

    order = [
        (c * n_f + f, f * n_ctx + c % 2 * n_z + c // 2) for c in range(n_ctx) for f in range(n_f)
    ]
    down_rows = ctx_total(down_parts).astype(BF16)
    down_sent = lax.ppermute(down_rows, ("ctx", "fsdp"), order)

    up_got, out_part, qup_part = together(up_got, out_part, qup_part)

    small = jnp.concatenate(
        [jnp.zeros((model_width,), F32), grad_gain_q, grad_gain_two, sq_local.reshape(1)]
    )
    entries = small.shape[0]
    small = jnp.pad(small, (0, -entries % 1024)).reshape(-1, 128)
    ends = tail_reduce(
        n_ctx,
        n_f,
        {
            "gate": gate_pair,
            "kv": kv_part,
            "up": up_blocks,
            "up_got": up_got,
            "out": by_ctx(out_part),
            "qup": by_ctx(qup_part),
            "dqa": grad_qlow,
            "cos": cosine,
            "sin": sine,
            "normed_group": normed_group,
            "w_kv": fetched["w_kv"],
            "da_q": da_q,
            "hidden": hidden_in,
            "gain_one": gain_one,
            "grad_resid": grad_resid,
            "small": small,
        },
        q_width,
    )
    small, down_sent = together(ends["small_out"], down_sent)
    small = small.reshape(-1)[:entries]
    grad_down = down_sent.astype(F32)

    device = c_idx * n_f + f_idx
    q1, q2 = model_width, model_width + q_width
    n_dev = n_ctx * n_f

    def own_part(values):
        size = values.shape[0] // n_dev
        return cut(values, device * size, size, 0)

    loss_now = small[-1] / (model_width * total_count)
    return (
        ffn["result"],
        loss_now,
        ends["grad_input"],
        own_part(small[:q1]),
        ends["out_qd"],
        own_part(small[q1:q2]),
        ends["out_qup"],
        ends["out_kvw"],
        ends["out_out"],
        own_part(small[q2 : q2 + model_width]),
        ends["out_gate"],
        ends["out_up"],
        grad_down,
    )


def solution(mesh):
    both = ("ctx", "fsdp")
    rows = P(both, None)
    flat = P(both)
    shard = P("fsdp", None)
    gain = P("fsdp")
    return jax.shard_map(
        body,
        mesh=mesh,
        in_specs=(
            rows,
            rows,
            flat,
            flat,
            flat,
            gain,
            shard,
            gain,
            shard,
            shard,
            shard,
            gain,
            shard,
            shard,
            shard,
        ),
        out_specs=(
            rows,
            P(),
            rows,
            flat,
            rows,
            flat,
            rows,
            rows,
            rows,
            flat,
            rows,
            rows,
            rows,
        ),
        check_vma=False,
    )
```
